32 devices in a mesh: group: 2 (over x), shard: 16 (over z, y, core).
Axes of the slice: x: 2, y: 2, z: 4, core: 2. Of those that a mesh axis runs over, the one named last changes fastest.
Arguments:
- tokens_in: bfloat16 [16384, 1024], P(('group', 'shard')), may hold values from -6 to 6
- out_grad: bfloat16 [16384, 1024], P(('group', 'shard')), may hold values from -6 to 6
- deal_order: int32 [32, 512], P(('group', 'shard')), may hold values from 0 to 511, each once within a row
- seq_lengths: int32 [2, 3], P('group'), may hold values from 1024 to 4096, as said below
- value_routes: int32 [16384, 4, 2], P(('group', 'shard')), may hold values from 0 to 4, all different within a row
- output_routes: int32 [16384, 4, 2], P(('group', 'shard')), may hold values from 0 to 4, all different within a row
- ffn_routes: int32 [16384, 16], P(('group', 'shard')), may hold values from 0 to 63, all different within a row; in each aligned block of 512 rows (0 to 511, 512 to 1023, ...) at most 192 rows name the same one
- norm1_gain: bfloat16 [1024], P(('group', 'shard')), may hold values from 0.5 to 1.5
- norm1_bias: bfloat16 [1024], P(('group', 'shard')), may hold values from -0.59765625 to 0.59765625
- norm2_gain: bfloat16 [1024], P(('group', 'shard')), may hold values from 0.5 to 1.5
- norm2_bias: bfloat16 [1024], P(('group', 'shard')), may hold values from -0.59765625 to 0.59765625
- query_weight: bfloat16 [1024, 512], P(('group', 'shard')), may hold values from -0.1875 to 0.1875
- key_weight: bfloat16 [1024, 512], P(('group', 'shard')), may hold values from -0.1875 to 0.1875
- value_weight: bfloat16 [1024, 2560], P(('group', 'shard')), may hold values from -0.1875 to 0.1875
- output_weight: bfloat16 [1024, 2560], P(('group', 'shard')), may hold values from -4 to 4
- value_router: bfloat16 [1024, 20], P(('group', 'shard')), may hold values from -0.125 to 0.125
- output_router: bfloat16 [1024, 20], P(('group', 'shard')), may hold values from -0.125 to 0.125
- ffn_router: bfloat16 [1024, 64], P(('group', 'shard')), may hold values from -0.09375 to 0.09375
- ffn_in: bfloat16 [1024, 8192], P('group', 'shard'), may hold values from -0.1875 to 0.1875
- ffn_out: bfloat16 [1024, 8192], P('group', 'shard'), may hold values from -0.5 to 0.5
Outputs:
- layer_out: bfloat16 [16384, 1024], P(('group', 'shard'))
- input_grad: float32 [16384, 1024], P(('group', 'shard'))
- norm1_gain_grad: float32 [1024], P(('group', 'shard'))
- norm1_bias_grad: float32 [1024], P(('group', 'shard'))
- norm2_gain_grad: float32 [1024], P(('group', 'shard'))
- norm2_bias_grad: float32 [1024], P(('group', 'shard'))
- query_weight_grad: float32 [1024, 512], P(('group', 'shard'))
- key_weight_grad: float32 [1024, 512], P(('group', 'shard'))
- value_weight_grad: float32 [1024, 2560], P(('group', 'shard'))
- output_weight_grad: float32 [1024, 2560], P(('group', 'shard'))
- value_router_grad: float32 [1024, 20], P(('group', 'shard'))
- output_router_grad: float32 [1024, 20], P(('group', 'shard'))
- ffn_router_grad: float32 [1024, 64], P(('group', 'shard'))
- ffn_in_grad: float32 [1024, 8192], P('group', 'shard')
- ffn_out_grad: float32 [1024, 8192], P('group', 'shard')
The draws below stay inside these ranges and needn't reach their ends.
Inputs may be any that keep to these rules, and one draw needn't show every extreme that they name: `deal_order`: each row is a permutation of 0 to 511. `seq_lengths`: each group's lengths add up to its tokens, 512 on each of its devices. `value_routes`: the two entries of a token and head differ. `output_routes`: the two entries of a token and head differ. `ffn_routes`: a token's 16 entries differ; within the rows of one device no expert is named by more than 192 rows.
All inputs are finite; a program needn't handle non-finite values.
Results may differ from the reference program's by a relative error of at most 0.015.
Values may be sent and summed in bfloat16 or wider, within the bound.
A program may use at most 576 MiB of HBM per device.

```python
import math
import jax
import jax.numpy as jnp
import numpy as np
from jax import lax

D = 1024
HEADS = 4
DH = 128
VEXP = 5
FH = 128
FTOP = 16
LMAX = 4096
LMIN = 1024
TOK_DEV = 512
FEXP = 64
TOKENS = 16384
NSEQ = 3
REACH = 8
FCAP = 192
N_GROUP = 2
N_SHARD = 16


def draw_seq_lengths(key, part):
    pair_count = NSEQ // 2
    spread = jax.random.randint(jax.random.fold_in(key, 11), (N_GROUP, pair_count), 0, LMAX - 2 * LMIN + 1, dtype=jnp.int32)
    first_half = LMIN + spread
    second_half = LMAX - first_half
    longest = jnp.full((N_GROUP, 1), LMAX, jnp.int32)
    lengths = jnp.concatenate([longest, first_half, second_half], axis=1)
    shuffles = jax.vmap(lambda sub_key: jax.random.permutation(sub_key, NSEQ))(jax.random.split(jax.random.fold_in(key, 12), N_GROUP))
    return jnp.take_along_axis(lengths, shuffles.astype(jnp.int32), axis=1)


def block_levels(own_key, dims, shards, low, top_value):
    level = 1.0
    for axis_at, blocks in shards:
        draws = jax.random.uniform(jax.random.fold_in(jax.random.fold_in(own_key, 6), axis_at), (blocks,), jnp.float32, low / len(shards), top_value / len(shards))
        level = level * jnp.repeat(jnp.exp(draws), dims[axis_at] // blocks).reshape((-1,) + (1,) * (len(dims) - 1 - axis_at))
    return level


def picks_of(stream_key, rows, count, top, lift):
    order = jax.random.permutation(jax.random.fold_in(stream_key, 1), count)
    pull = order
    for power in range(3):
        pull = pull * pull // count
    pull = pull * lift // count
    tickets = jax.random.randint(jax.random.fold_in(stream_key, 2), (rows, count), 0, 4096) + pull
    sure = jax.random.permutation(jax.random.fold_in(stream_key, 3), rows)[jnp.arange(count) % rows]
    tickets = jnp.where(jnp.arange(rows)[:, None] == sure[None, :], 1 << 14, tickets)
    score = tickets * count + jnp.arange(count)
    return lax.top_k(score.astype(jnp.int32), top)[1].astype(jnp.int32)


def shared_out(key, own, number, rows, number_of, top, most, skew):
    sequence = jax.random.permutation(key, number_of)
    heavy_load, common = shares(number_of, rows * top, most, skew, True), shares(number_of, rows * top, most, skew, False)
    places = jnp.arange(number_of)

    def named(sizes, rotation):
        used = int((sizes > 0).sum())
        fixed = max(1, used // 4)
        moved = fixed + (places - fixed + rotation * (used - fixed)) % max(1, number_of - fixed)
        return jnp.zeros((number_of,), jnp.int32).at[sequence[jnp.where(places < fixed, places, moved)]].set(jnp.asarray(sizes, jnp.int32))

    sizes = jnp.where(number % 4 == 0, named(heavy_load, number // 4), named(common, number - number // 4 - 1))
    mixed = jax.random.permutation(jax.random.fold_in(own, 3), number_of)
    donor, taker = mixed[0:number_of // 2 * 2:2], mixed[1:number_of // 2 * 2:2]
    room = jnp.minimum(sizes[donor] - 1, most - sizes[taker]) // 2
    room = jnp.where((donor == sequence[0]) | (taker == sequence[0]) | (sizes[taker] == 0), 0, jnp.maximum(room, 0))
    moved = jax.random.randint(jax.random.fold_in(own, 4), (number_of // 2,), 0, 1 << 20) % (room + 1)
    sizes = sizes.at[donor].add(-moved).at[taker].add(moved)
    items = jnp.searchsorted(jnp.cumsum(sizes), jnp.arange(rows * top), side="right").astype(jnp.int32)
    listing = items.reshape(top, rows).T
    listing = listing[jax.random.permutation(jax.random.fold_in(own, 1), rows)]
    rotation = jax.random.randint(jax.random.fold_in(own, 2), (rows, 1), 0, top)
    return jnp.take_along_axis(listing, (jnp.arange(top)[None, :] + rotation) % top, axis=1)


def shares(count, total, reach, skew, full):
    weights = [(1 << 20) // math.isqrt(standing ** skew) + 1 for standing in range(1, count + 1)]
    largest = reach if full else min(reach, max(-(-total // count), total * weights[0] // sum(weights)))
    least = 1 if total - largest >= count - 1 else 0
    counts, rest = [largest] + [least] * (count - 1), total - largest - least * (count - 1)
    while rest > 0:
        candidates = [i for i in range(1, count) if counts[i] < largest] or [i for i in range(1, count) if counts[i] < reach]
        whole, remaining = sum([weights[i] for i in candidates]), rest
        for i in candidates:
            addition = min(reach - counts[i], max(1, remaining * weights[i] // whole), rest)
            counts[i] = counts[i] + addition
            rest = rest - addition
    return np.array(counts)


def normal_values(rng, shape, scale, most, cuts=(), held_as=jnp.bfloat16):
    values = jax.random.normal(rng, shape, jnp.float32) * scale
    if len(cuts) > 0:
        values = block_levels(rng, shape, cuts, -0.22, 0.18) * values
    return jnp.clip(values, min=-most, max=most).astype(held_as)


def setup_inputs(seed: int = 0) -> dict:
    seeds = jax.random.split(jax.random.key(seed), 21)
    tokens_in = normal_values(seeds[0], (TOKENS, D), 1.0, 6.0, ((0, 32),))
    out_grad = normal_values(seeds[1], (TOKENS, D), 1.0, 6.0, ((0, 32),))
    deal_order = jax.vmap(lambda own: jax.random.permutation(own, TOK_DEV))(jax.random.split(seeds[2], (N_GROUP * N_SHARD))).reshape((N_GROUP * N_SHARD, TOK_DEV)).astype(jnp.int32)
    seq_lengths = draw_seq_lengths(jax.random.fold_in(seeds[20], 71), 0)
    value_routes = picks_of(seeds[4], TOKENS * HEADS, VEXP, 2, 0).reshape((TOKENS, HEADS, 2))
    output_routes = picks_of(seeds[5], TOKENS * HEADS, VEXP, 2, 3276).reshape((TOKENS, HEADS, 2))
    ffn_routes_keys = jax.random.split(jax.random.fold_in(seeds[6], 1), TOKENS // TOK_DEV)
    ffn_routes_turns = jax.random.permutation(jax.random.fold_in(seeds[6], 3), TOKENS // TOK_DEV)
    ffn_routes = jax.vmap(lambda own, number: shared_out(jax.random.fold_in(seeds[6], 2), own, number, TOK_DEV, FEXP, FTOP, FCAP, 1))(ffn_routes_keys, ffn_routes_turns).reshape((TOKENS, FTOP))
    norm1_gain = jnp.clip(1.0 + 0.1 * jax.random.normal(seeds[7], (D,), jnp.float32), 0.5, 1.5).astype(jnp.bfloat16)
    norm1_bias = normal_values(seeds[8], (D,), 0.1, 0.59765625, ((0, 32),))
    norm2_gain = jnp.clip(1.0 + 0.1 * jax.random.normal(seeds[9], (D,), jnp.float32), 0.5, 1.5).astype(jnp.bfloat16)
    norm2_bias = normal_values(seeds[10], (D,), 0.1, 0.59765625, ((0, 32),))
    query_weight = normal_values(seeds[11], (D, HEADS * DH), D ** -0.5, 0.1875, ((0, 32),))
    key_weight = normal_values(seeds[12], (D, HEADS * DH), D ** -0.5, 0.1875, ((0, 32),))
    value_weight = normal_values(seeds[13], (D, HEADS * VEXP * DH), D ** -0.5, 0.1875, ((0, 32),))
    output_weight = normal_values(seeds[14], (D, HEADS * VEXP * DH), 2 ** -0.5, 4.0, ((0, 32),))
    value_router = normal_values(seeds[15], (D, HEADS * VEXP), (2 * D) ** -0.5, 0.125, ((0, 32),))
    output_router = normal_values(seeds[16], (D, HEADS * VEXP), (2 * D) ** -0.5, 0.125, ((0, 32),))
    ffn_router = normal_values(seeds[17], (D, FEXP), (4 * D) ** -0.5, 0.09375, ((0, 32),))
    ffn_in = normal_values(seeds[18], (D, FEXP * FH), D ** -0.5, 0.1875, ((0, 2), (1, 16)))
    ffn_out = normal_values(seeds[19], (D, FEXP * FH), (FTOP * FH // 16) ** -0.5, 0.5, ((0, 2), (1, 16)))
    return dict(tokens_in=tokens_in, out_grad=out_grad, deal_order=deal_order, seq_lengths=seq_lengths, value_routes=value_routes, output_routes=output_routes, ffn_routes=ffn_routes, norm1_gain=norm1_gain, norm1_bias=norm1_bias, norm2_gain=norm2_gain, norm2_bias=norm2_bias, query_weight=query_weight, key_weight=key_weight, value_weight=value_weight, output_weight=output_weight, value_router=value_router, output_router=output_router, ffn_router=ffn_router, ffn_in=ffn_in, ffn_out=ffn_out)


@jax.custom_vjp
def low(v):
    return lax.optimization_barrier(v.astype(jnp.bfloat16)).astype(jnp.float32)

@jax.custom_vjp
def low_back(v):
    return v

def low_keep(v):
    return (low(v), None)

def low_pass(kept, grad):
    return (grad,)

def back_keep(v):
    return (v, None)

def back_low(kept, grad):
    return (low(grad),)
low.defvjp(low_keep, low_pass)
low_back.defvjp(back_keep, back_low)

def matmul(left_side, right_side):
    return jnp.dot(left_side, right_side, precision=lax.Precision.HIGHEST, preferred_element_type=jnp.float32)

def layer_norm(inputs, gain_vec, bias_vec):
    centred = inputs - lax.optimization_barrier(jnp.mean(inputs, axis=-1, keepdims=True))
    scaled = centred * lax.rsqrt(lax.optimization_barrier(jnp.mean(centred * centred, axis=-1, keepdims=True)) + 1e-05)
    return scaled * gain_vec + bias_vec

def choose(routes, options):
    return lax.optimization_barrier(jnp.sum((routes[..., None] == jnp.arange(options, dtype=jnp.int32)).astype(jnp.float32), axis=-2))

def segment_of(seq_ends, positions):
    return lax.optimization_barrier(jnp.sum((seq_ends[None, :] <= positions[:, None]).astype(jnp.int32), axis=1))

@jax.checkpoint
def attend_block(queries, key_rows, values, seg_query, pos_query, seg_key, pos_key):
    scores = jnp.einsum('qhd,khd->hqk', queries, key_rows, precision=lax.Precision.HIGHEST) * DH ** (-0.5)
    scores = low_back(scores)
    visible = (seg_key[None, :] == seg_query[:, None]) & (pos_key[None, :] <= pos_query[:, None]) & (pos_key[None, :] >= 0)
    scores = jnp.where(visible[None], scores, -1e+30)
    soft = jax.nn.softmax(scores, axis=-1)
    return jnp.einsum('hqk,khd->qhd', low(soft), values, precision=lax.Precision.HIGHEST)

def attention(queries, key_rows, values, seq_ends):
    key_span = (REACH + 1) * TOK_DEV
    block_rows = min(512, TOK_DEV)
    per_group = TOK_DEV * N_SHARD
    per_count = per_group // block_rows
    query_four = queries.reshape(N_GROUP, per_group, HEADS, DH)
    padding = ((0, 0), (REACH * TOK_DEV, 0), (0, 0), (0, 0))
    key_four = jnp.pad(key_rows.reshape(N_GROUP, per_group, HEADS, DH), padding)
    value_four = jnp.pad(values.reshape(N_GROUP, per_group, HEADS, DH), padding)

    def one_block(position):
        group_id = (position // per_count).astype(jnp.int32)
        start = (position % per_count * block_rows).astype(jnp.int32)
        first_key = (start // TOK_DEV * TOK_DEV).astype(jnp.int32)
        zero = jnp.zeros((), jnp.int32)
        query_block = lax.dynamic_slice(query_four, (group_id, start, zero, zero), (1, block_rows, HEADS, DH))[0]
        key_block = lax.dynamic_slice(key_four, (group_id, first_key, zero, zero), (1, key_span, HEADS, DH))[0]
        value_block = lax.dynamic_slice(value_four, (group_id, first_key, zero, zero), (1, key_span, HEADS, DH))[0]
        limits = lax.dynamic_slice(seq_ends, (group_id, zero), (1, NSEQ))[0]
        pos_query = start + jnp.arange(block_rows, dtype=jnp.int32)
        pos_key = first_key - REACH * TOK_DEV + jnp.arange(key_span, dtype=jnp.int32)
        return attend_block(query_block, key_block, value_block, segment_of(limits, pos_query), pos_query, segment_of(limits, pos_key), pos_key)
    result = lax.map(one_block, jnp.arange(N_GROUP * per_count, dtype=jnp.int32))
    return result.reshape(TOKENS, HEADS, DH)

@jax.checkpoint
def expert_block(hidden_in, gate_rows, ffn_in, ffn_out):
    pre_act = low_back(matmul(hidden_in, ffn_in))
    active = low(jax.nn.silu(pre_act) * jnp.repeat(gate_rows, FH, axis=1))
    return lax.dot_general(active, ffn_out, (((1,), (1,)), ((), ())), precision=lax.Precision.HIGHEST, preferred_element_type=jnp.float32)

def reference(tokens_in, out_grad, deal_order, seq_lengths, value_routes, output_routes, ffn_routes, norm1_gain, norm1_bias, norm2_gain, norm2_bias, query_weight, key_weight, value_weight, output_weight, value_router, output_router, ffn_router, ffn_in, ffn_out):
    per_peer = TOK_DEV // N_SHARD
    worker_row = jnp.arange(TOKENS, dtype=jnp.int32)
    device = worker_row // TOK_DEV
    group_id = device // N_SHARD
    worker = device % N_SHARD
    slot_ids = deal_order.reshape(-1).astype(jnp.int32)
    source = slot_ids // per_peer
    dealt_row = ((group_id * N_SHARD + source) * TOK_DEV + worker * per_peer + slot_ids % per_peer).astype(jnp.int32)
    seq_ends = jnp.cumsum(seq_lengths, axis=1).astype(jnp.int32)
    value_mask = choose(value_routes, VEXP)
    output_mask = choose(output_routes, VEXP)
    ffn_mask = choose(ffn_routes, FEXP)
    params = (norm1_gain.astype(jnp.float32), norm1_bias.astype(jnp.float32), norm2_gain.astype(jnp.float32), norm2_bias.astype(jnp.float32), query_weight.astype(jnp.float32), key_weight.astype(jnp.float32), value_weight.astype(jnp.float32), output_weight.astype(jnp.float32), value_router.astype(jnp.float32), output_router.astype(jnp.float32), ffn_router.astype(jnp.float32), ffn_in.astype(jnp.float32), ffn_out.astype(jnp.float32))

    def forward(inputs, weights):
        gain_one, bias_one, gain_two, bias_two, w_query, w_key, w_value, w_output, r_value, r_output, r_ffn, w_in, w_out = weights
        worker_in = inputs[dealt_row]
        normed_one = low(layer_norm(worker_in, gain_one, bias_one))
        queries = low_back(low(matmul(normed_one, w_query)))
        key_rows = low_back(low(matmul(normed_one, w_key)))
        projected = low_back(matmul(worker_in, w_value)).reshape(TOKENS, HEADS, VEXP, DH)
        value_gate = jax.nn.sigmoid(low_back(matmul(normed_one, r_value))).reshape(TOKENS, HEADS, VEXP) * value_mask
        values = low(lax.optimization_barrier(jnp.sum(value_gate[..., None] * projected, axis=2)))
        attended = low_back(attention(queries.reshape(TOKENS, HEADS, DH), key_rows.reshape(TOKENS, HEADS, DH), values, seq_ends))
        out_gate = jax.nn.sigmoid(low_back(matmul(normed_one, r_output))).reshape(TOKENS, HEADS, VEXP) * output_mask
        mixed_rows = low((out_gate[..., None] * attended[:, :, None, :]).reshape(TOKENS, HEADS * VEXP * DH))
        branch = low_back(low(lax.dot_general(mixed_rows, w_output, (((1,), (1,)), ((), ())), precision=lax.Precision.HIGHEST, preferred_element_type=jnp.float32)))
        home = jnp.zeros_like(inputs).at[dealt_row].set(branch)
        middle = inputs + home
        normed_two = low(layer_norm(middle, gain_two, bias_two))
        ffn_gate = jax.nn.sigmoid(low_back(matmul(normed_two, r_ffn))) * ffn_mask
        hidden_in = low(middle)
        feed = lax.map(lambda pair_rows: expert_block(pair_rows[0], pair_rows[1], w_in, w_out), (hidden_in.reshape(TOKENS // TOK_DEV, TOK_DEV, D), ffn_gate.reshape(TOKENS // TOK_DEV, TOK_DEV, FEXP)))
        return middle + feed.reshape(TOKENS, D)
    layer_value, pullback = jax.vjp(forward, tokens_in.astype(jnp.float32), params)
    input_grad, weight_grads = pullback(out_grad.astype(jnp.float32))
    grad_gain_one, grad_bias_one, grad_gain_two, grad_bias_two, grad_query, grad_key, grad_value, grad_output, grad_r_value, grad_r_output, grad_r_ffn, grad_in, grad_out = weight_grads
    return (layer_value.astype(jnp.bfloat16), input_grad, grad_gain_one, grad_bias_one, grad_gain_two, grad_bias_two, grad_query, grad_key, grad_value, grad_output, grad_r_value, grad_r_output, grad_r_ffn, grad_in, grad_out)
```

```python
import functools

import jax
import jax.numpy as jnp
from jax import lax
from jax.experimental import pallas as pl
from jax.experimental.pallas import tpu as pltpu
from jax.sharding import Mesh, PartitionSpec as P

HEADS = 4
DH = 128
VEXP = 5
FH = 128
LMAX = 4096

TOK = ("group", "level", "head")


def matmul(left_side, right_side):
    return jnp.dot(left_side, right_side, preferred_element_type=jnp.float32)


def transposed(left_side, right_side):
    return lax.dot_general(
        left_side, right_side, (((1,), (1,)), ((), ())), preferred_element_type=jnp.float32
    )


def contract_rows(left_side, right_side):
    return lax.dot_general(
        left_side, right_side, (((0,), (0,)), ((), ())), preferred_element_type=jnp.float32
    )


def low(value):
    return value.astype(jnp.bfloat16)


def layer_norm(inputs, gain_vec, bias_vec):
    centred = inputs - jnp.mean(inputs, axis=-1, keepdims=True)
    inverse = lax.rsqrt(jnp.mean(centred * centred, axis=-1, keepdims=True) + 1e-05)
    scaled = centred * inverse
    return (scaled * gain_vec + bias_vec, scaled, inverse)


def norm_back(grad_normed, gain_vec, scaled, inverse):
    inner_grad = grad_normed * gain_vec
    return inverse * (
        inner_grad
        - jnp.mean(inner_grad, axis=-1, keepdims=True)
        - scaled * jnp.mean(inner_grad * scaled, axis=-1, keepdims=True)
    )


def silu_slope(pre_act, sig):
    return sig * (1.0 + pre_act * (1.0 - sig))


def to_workers(rows):
    levels = lax.axis_size("level")
    count = rows.shape[0]
    came = lax.all_to_all(
        rows.reshape(levels, count // levels, -1), "level", split_axis=0, concat_axis=0, tiled=True
    )
    came = came.reshape(levels, HEADS, count // levels // HEADS, -1)
    return came.transpose(1, 0, 2, 3).reshape(count, -1)


def to_home(rows):
    levels = lax.axis_size("level")
    count = rows.shape[0]
    out = rows.reshape(HEADS, levels, count // levels // HEADS, -1).transpose(1, 0, 2, 3)
    back = lax.all_to_all(
        out.reshape(levels, count // levels, -1), "level", split_axis=0, concat_axis=0, tiled=True
    )
    return back.reshape(count, -1)


MESH = pl.DeviceIdType.MESH


def partners(head):
    near = head + 1 - 2 * lax.rem(head, 2)
    far = lax.rem(head + 2, HEADS)
    return near, far


def greet(near, far):
    barrier = pltpu.get_barrier_semaphore()
    for peer in (near, far):
        pl.semaphore_signal(barrier, inc=1, device_id={"head": peer}, device_id_type=MESH)
    pl.semaphore_wait(barrier, 2)


def gather_kernel(own, out, local_sem, near_send, near_recv, far_send, far_recv, pass_send, pass_recv):
    head = lax.axis_index("head")
    near, far = partners(head)
    greet(near, far)

    def remote(src, dst, send, recv, peer):
        return pltpu.make_async_remote_copy(
            src_ref=src,
            dst_ref=dst,
            send_sem=send,
            recv_sem=recv,
            device_id={"head": peer},
            device_id_type=MESH,
        )

    to_far = [
        remote(own.at[i], out.at[i, head], far_send.at[i], far_recv.at[i], far)
        for i in range(HEADS)
    ]
    to_near = [
        remote(own.at[i], out.at[i, head], near_send.at[i], near_recv.at[i], near)
        for i in range(HEADS)
    ]
    passed = [
        remote(out.at[i, far], out.at[i, far], pass_send.at[i], pass_recv.at[i], near)
        for i in range(HEADS)
    ]
    kept = [
        pltpu.make_async_copy(own.at[i], out.at[i, head], local_sem.at[i]) for i in range(HEADS)
    ]
    for copy in to_far + to_near + kept:
        copy.start()
    for i in range(HEADS):
        to_far[i].wait_recv()
        passed[i].start()
    for i in range(HEADS):
        to_near[i].wait_recv()
        passed[i].wait_recv()
        kept[i].wait()
        to_far[i].wait_send()
        to_near[i].wait_send()
        passed[i].wait_send()


def level_gather(rows, collective_id):
    count, width = rows.shape
    sems = [pltpu.SemaphoreType.DMA((HEADS,))] * 7
    whole = pl.pallas_call(
        gather_kernel,
        out_shape=jax.ShapeDtypeStruct((HEADS, HEADS, count // HEADS, width), rows.dtype),
        in_specs=[pl.BlockSpec(memory_space=pl.ANY)],
        out_specs=pl.BlockSpec(memory_space=pl.ANY),
        scratch_shapes=sems,
        compiler_params=pltpu.CompilerParams(collective_id=collective_id, has_side_effects=True),
        name="level_gather",
    )(rows.reshape(HEADS, count // HEADS, width))
    return whole.reshape(HEADS * count, width)


def scatter_kernel(part, out, near_buf, send_buf, far_buf, near_send, near_recv, far_send, far_recv):
    head = lax.axis_index("head")
    near, far = partners(head)
    greet(near, far)
    across = HEADS - 1 - head

    def to_near(slot, i, dest):
        return pltpu.make_async_remote_copy(
            src_ref=part.at[i, dest],
            dst_ref=near_buf.at[slot, i],
            send_sem=near_send.at[slot, i],
            recv_sem=near_recv.at[slot, i],
            device_id={"head": near},
            device_id_type=MESH,
        )

    first = [to_near(0, i, across) for i in range(HEADS)]
    second = [to_near(1, i, near) for i in range(HEADS)]
    onward = [
        pltpu.make_async_remote_copy(
            src_ref=send_buf.at[i],
            dst_ref=far_buf.at[i],
            send_sem=far_send.at[i],
            recv_sem=far_recv.at[i],
            device_id={"head": far},
            device_id_type=MESH,
        )
        for i in range(HEADS)
    ]
    for copy in first + second:
        copy.start()
    for i in range(HEADS):
        first[i].wait_recv()
        both = part[i, far].astype(jnp.float32) + near_buf[0, i].astype(jnp.float32)
        send_buf[i] = both.astype(jnp.bfloat16)
        onward[i].start()
    for i in range(HEADS):
        second[i].wait_recv()
        out[i] = part[i, head].astype(jnp.float32) + near_buf[1, i].astype(jnp.float32)
    for i in range(HEADS):
        onward[i].wait_recv()
        out[i] = out[i] + far_buf[i].astype(jnp.float32)
    for i in range(HEADS):
        first[i].wait_send()
        second[i].wait_send()
        onward[i].wait_send()


def level_scatter(rows, collective_id):
    total, width = rows.shape
    piece = total // (HEADS * HEADS)
    low_type = jnp.bfloat16
    mine = pl.pallas_call(
        scatter_kernel,
        out_shape=jax.ShapeDtypeStruct((HEADS, piece, width), jnp.float32),
        in_specs=[pl.BlockSpec(memory_space=pltpu.VMEM)],
        out_specs=pl.BlockSpec(memory_space=pltpu.VMEM),
        scratch_shapes=[
            pltpu.VMEM((2, HEADS, piece, width), low_type),
            pltpu.VMEM((HEADS, piece, width), low_type),
            pltpu.VMEM((HEADS, piece, width), low_type),
            pltpu.SemaphoreType.DMA((2, HEADS)),
            pltpu.SemaphoreType.DMA((2, HEADS)),
            pltpu.SemaphoreType.DMA((HEADS,)),
            pltpu.SemaphoreType.DMA((HEADS,)),
        ],
        compiler_params=pltpu.CompilerParams(
            collective_id=collective_id, has_side_effects=True, vmem_limit_bytes=32 * 2**20
        ),
        name="level_scatter",
    )(rows.reshape(HEADS, HEADS, piece, width))
    return mine.reshape(HEADS * piece, width)


BLOCK = 512
LOG2E = 1.4426950408889634


def dot(left_side, right_side, left_dim, right_dim):
    return lax.dot_general(
        left_side,
        right_side,
        (((left_dim,), (right_dim,)), ((), ())),
        preferred_element_type=jnp.float32,
    )


def attend_kernel(first, last, q, k, v, pos_q, start_q, pos_k, out, lse, top, total, acc):
    at = pl.program_id(0)
    rate = LOG2E * DH ** (-0.5)
    top[...] = jnp.full_like(top, -1e30)
    total[...] = jnp.zeros_like(total)
    acc[...] = jnp.zeros_like(acc)
    query = q[...]
    row_at, row_from = pos_q[...], start_q[...]

    def step(block, carry):
        rows = pl.ds(pl.multiple_of(block * BLOCK, BLOCK), BLOCK)
        scores = dot(query, k[rows, :], 1, 1)
        key_at = pos_k[block]
        scores = jnp.where((key_at >= row_from) & (key_at <= row_at), scores, -1e30)
        old = top[...]
        new = jnp.maximum(old, jnp.max(scores, axis=1, keepdims=True))
        shrink = jnp.exp2((old - new) * rate)
        weight = jnp.exp2((scores - new) * rate)
        total[...] = total[...] * shrink + jnp.sum(weight, axis=1, keepdims=True)
        acc[...] = acc[...] * shrink + dot(weight.astype(jnp.bfloat16), v[rows, :], 1, 0)
        top[...] = new
        return carry

    lax.fori_loop(first[at], last[at] + 1, step, 0)
    out[...] = acc[...] / total[...]
    lse[...] = top[...] * rate + jnp.log2(total[...])


def attend(first, last, queries, window, pos_q, start_q, pos_k):
    rows = queries.shape[0]
    span = window.shape[0]
    column = pl.BlockSpec((BLOCK, 1), lambda i, *_: (i, 0))
    grid_spec = pltpu.PrefetchScalarGridSpec(
        num_scalar_prefetch=2,
        grid=(rows // BLOCK,),
        in_specs=[
            pl.BlockSpec((BLOCK, DH), lambda i, *_: (i, 0)),
            pl.BlockSpec((span, DH), lambda i, *_: (0, 0)),
            pl.BlockSpec((span, DH), lambda i, *_: (0, 1)),
            column,
            column,
            pl.BlockSpec((span // BLOCK, 1, BLOCK), lambda i, *_: (0, 0, 0)),
        ],
        out_specs=[pl.BlockSpec((BLOCK, DH), lambda i, *_: (i, 0)), column],
        scratch_shapes=[
            pltpu.VMEM((BLOCK, 1), jnp.float32),
            pltpu.VMEM((BLOCK, 1), jnp.float32),
            pltpu.VMEM((BLOCK, DH), jnp.float32),
        ],
    )
    return pl.pallas_call(
        attend_kernel,
        grid_spec=grid_spec,
        out_shape=[
            jax.ShapeDtypeStruct((rows, DH), jnp.float32),
            jax.ShapeDtypeStruct((rows, 1), jnp.float32),
        ],
        compiler_params=pltpu.CompilerParams(vmem_limit_bytes=48 * 2**20),
        name="attend",
    )(first, last, queries, window, window, pos_q, start_q, pos_k)


def attend_back_kernel(
    first, last, q, k, v, grad, pos_q, start_q, lse, inner, pos_k, grad_q, grad_k, grad_v, acc
):
    at = pl.program_id(0)
    rate = LOG2E * DH ** (-0.5)

    @pl.when(at == 0)
    def _():
        grad_k[...] = jnp.zeros_like(grad_k)
        grad_v[...] = jnp.zeros_like(grad_v)

    acc[...] = jnp.zeros_like(acc)
    query, grad_out = q[...], grad[...]
    row_at, row_from, row_lse, row_inner = pos_q[0], start_q[0], lse[0], inner[0]

    def step(block, carry):
        rows = pl.ds(pl.multiple_of(block * BLOCK, BLOCK), BLOCK)
        key, value = k[rows, :], v[rows, :]
        scores = dot(key, query, 1, 1)
        key_at = pos_k[rows, :]
        seen = (key_at >= row_from) & (key_at <= row_at)
        soft = jnp.where(seen, jnp.exp2(scores * rate - row_lse), 0.0)
        grad_soft = dot(value, grad_out, 1, 1)
        grad_scores = (soft * (grad_soft - row_inner)).astype(jnp.bfloat16)
        grad_v[rows, :] += dot(soft.astype(jnp.bfloat16), grad_out, 1, 0)
        grad_k[rows, :] += dot(grad_scores, query, 1, 0)
        acc[...] += dot(grad_scores, key, 0, 0)
        return carry

    lax.fori_loop(first[at], last[at] + 1, step, 0)
    grad_q[...] = (acc[...] * DH ** (-0.5)).astype(jnp.bfloat16)


def attend_back(first, last, queries, window, grads, pos_q, start_q, lse, inner, pos_k):
    rows = queries.shape[0]
    span = window.shape[0]
    block = pl.BlockSpec((BLOCK, DH), lambda i, *_: (i, 0))
    line = pl.BlockSpec((1, 1, BLOCK), lambda i, *_: (i, 0, 0))
    grid_spec = pltpu.PrefetchScalarGridSpec(
        num_scalar_prefetch=2,
        grid=(rows // BLOCK,),
        in_specs=[
            block,
            pl.BlockSpec((span, DH), lambda i, *_: (0, 0)),
            pl.BlockSpec((span, DH), lambda i, *_: (0, 1)),
            block,
            line,
            line,
            line,
            line,
            pl.BlockSpec((span, 1), lambda i, *_: (0, 0)),
        ],
        out_specs=[
            block,
            pl.BlockSpec((span, DH), lambda i, *_: (0, 0)),
            pl.BlockSpec((span, DH), lambda i, *_: (0, 0)),
        ],
        scratch_shapes=[pltpu.VMEM((BLOCK, DH), jnp.float32)],
    )
    return pl.pallas_call(
        attend_back_kernel,
        grid_spec=grid_spec,
        out_shape=[
            jax.ShapeDtypeStruct((rows, DH), jnp.bfloat16),
            jax.ShapeDtypeStruct((span, DH), jnp.float32),
            jax.ShapeDtypeStruct((span, DH), jnp.float32),
        ],
        compiler_params=pltpu.CompilerParams(vmem_limit_bytes=48 * 2**20),
        name="attend_back",
    )(first, last, queries, window, window, grads, pos_q, start_q, lse, inner, pos_k)


def chosen(routes, options):
    return jnp.sum(
        (routes[..., None] == jnp.arange(options, dtype=jnp.int32)).astype(jnp.float32), axis=-2
    )


def shift(value, axis, by):
    count = lax.axis_size(axis)
    pairs = [(i, i + by) for i in range(count) if 0 <= i + by < count]
    return lax.ppermute(value, axis, pairs)


def body(
    tokens_in,
    out_grad,
    deal_order,
    seq_lengths,
    value_routes,
    output_routes,
    ffn_routes,
    norm1_gain,
    norm1_bias,
    norm2_gain,
    norm2_bias,
    query_weight,
    key_weight,
    value_weight,
    output_weight,
    value_router,
    output_router,
    ffn_router,
    ffn_in,
    ffn_out,
):
    groups = lax.axis_size("group")
    levels = lax.axis_size("level")
    level = lax.axis_index("level")
    head = lax.axis_index("head")
    count, width = tokens_in.shape
    piece = count // (levels * HEADS)
    wrows = query_weight.shape[0]
    experts = ffn_router.shape[1]
    local_experts = ffn_in.shape[1] // FH

    small = jnp.concatenate(
        [
            ffn_router,
            norm1_gain[:, None],
            norm1_bias[:, None],
            norm2_gain[:, None],
            norm2_bias[:, None],
        ],
        axis=1,
    )
    shared = small.shape[1]
    pad = -(shared + 2 * VEXP) % 128
    packed = jnp.concatenate(
        [
            query_weight.reshape(wrows, HEADS, DH),
            key_weight.reshape(wrows, HEADS, DH),
            value_weight.reshape(wrows, HEADS, VEXP * DH),
            output_weight.reshape(wrows, HEADS, VEXP * DH),
            value_router.reshape(wrows, HEADS, VEXP),
            output_router.reshape(wrows, HEADS, VEXP),
            jnp.broadcast_to(small[:, None, :], (wrows, HEADS, shared)),
            jnp.zeros((wrows, HEADS, pad), jnp.bfloat16),
        ],
        axis=2,
    )
    cols = packed.shape[2]
    mine = lax.all_to_all(
        packed.transpose(1, 0, 2), "head", split_axis=0, concat_axis=0, tiled=True
    ).reshape(HEADS * wrows, cols)
    full = lax.all_gather(mine, ("group", "level"), axis=0, tiled=True)
    base = 2 * DH + 2 * VEXP * DH
    w_query = full[:, :DH]
    w_key = full[:, DH : 2 * DH]
    w_value = full[:, 2 * DH : 2 * DH + VEXP * DH]
    w_output = full[:, 2 * DH + VEXP * DH : base]
    r_value = full[:, base : base + VEXP]
    r_output = full[:, base + VEXP : base + 2 * VEXP]
    at = base + 2 * VEXP
    r_ffn = full[:, at : at + experts]
    gain_one, bias_one, gain_two, bias_two = (
        full[:, at + experts + i].astype(jnp.float32) for i in range(4)
    )

    def gather_ffn(weight):
        whole = lax.all_gather(weight, "level", axis=0)
        return lax.all_gather(whole, "group", axis=1, tiled=True)

    w_in = gather_ffn(ffn_in)
    w_out = gather_ffn(ffn_out)

    own_tokens = to_workers(tokens_in)
    own_grads = to_workers(out_grad)
    own_routes = to_workers(ffn_routes)
    worker_in = level_gather(own_tokens, 1)

    shards = levels * HEADS
    orders = lax.all_gather(deal_order, ("level", "head"), axis=0, tiled=True)
    ramp = jnp.arange(count, dtype=jnp.int32)
    place = orders[:, None, :] == ramp[None, :, None]
    inverse = jnp.sum(place * ramp[None, None, :], axis=2)
    rows = HEADS * count
    spots = jnp.arange(shards, dtype=jnp.int32)[:, None] * count + inverse
    spots = jnp.swapaxes(spots.reshape(shards, levels, HEADS, piece), 1, 2).reshape(levels, rows)
    reach = -(-LMAX // rows)
    spots = jnp.concatenate([jnp.full((reach, rows), -1, jnp.int32), spots], axis=0)
    pos_all = lax.dynamic_slice_in_dim(spots, level, reach + 1, 0).reshape(-1)
    positions = pos_all[reach * rows :]
    tables = jnp.concatenate(
        [value_routes.reshape(count, -1), output_routes.reshape(count, -1)], axis=1
    )
    tables = lax.all_gather(tables, "head", axis=0)

    def routes_of(first):
        part = tables[:, :, first : first + 2 * HEADS].reshape(HEADS, count, HEADS, 2)
        return lax.dynamic_index_in_dim(part, head, 2, keepdims=False)

    masks = jnp.concatenate(
        [chosen(routes_of(0), VEXP), chosen(routes_of(2 * HEADS), VEXP)], axis=-1
    )
    here = lax.dynamic_slice_in_dim(place, level * HEADS, HEADS, 0)
    masks = jnp.einsum("ktr,kre->kte", low(here), low(masks), preferred_element_type=jnp.float32)
    masks = jnp.swapaxes(masks.reshape(HEADS, levels, HEADS, piece, 2 * VEXP), 1, 2)
    masks = masks.reshape(rows, 2 * VEXP)
    value_mask, out_mask = masks[:, :VEXP], masks[:, VEXP:]

    normed, scaled_one, inverse_one = layer_norm(worker_in.astype(jnp.float32), gain_one, bias_one)
    normed_one = low(normed)
    queries = low(matmul(normed_one, w_query))
    keys = low(matmul(normed_one, w_key))
    projected = matmul(worker_in, w_value).reshape(rows, VEXP, DH)
    value_sig = jax.nn.sigmoid(matmul(normed_one, r_value))
    value_gate = value_sig * value_mask
    values = low(jnp.sum(value_gate[..., None] * projected, axis=1))
    span = (reach + 1) * rows
    window = [jnp.concatenate([keys, values], axis=1)]
    for _ in range(reach):
        window.insert(0, shift(window[0], "level", 1))
    window = jnp.concatenate(window, axis=0)
    seq_ends = jnp.cumsum(seq_lengths[0])

    def starts_of(places):
        return jnp.max(jnp.where(seq_ends <= places[:, None], seq_ends, 0), axis=1)

    starts = starts_of(positions)
    blocks = rows // BLOCK
    base_block = (level - reach) * blocks
    first_block = starts_of(level * rows + jnp.arange(blocks, dtype=jnp.int32) * BLOCK) // BLOCK
    first_block = jnp.maximum(first_block - base_block, 0)
    last_block = reach * blocks + jnp.arange(blocks, dtype=jnp.int32)
    scale = DH ** (-0.5)
    attended, log_total = attend(
        first_block,
        last_block,
        queries,
        window,
        positions[:, None],
        starts[:, None],
        pos_all.reshape(span // BLOCK, 1, BLOCK),
    )

    out_sig = jax.nn.sigmoid(matmul(normed_one, r_output))
    out_gate = out_sig * out_mask
    mixed = low((out_gate[..., None] * attended[:, None, :]).reshape(rows, VEXP * DH))
    branch = low(level_scatter(low(transposed(mixed, w_output)), 2))
    middle = own_tokens.astype(jnp.float32) + branch.astype(jnp.float32)

    normed_mid, scaled_two, inverse_two = layer_norm(middle, gain_two, bias_two)
    normed_two = low(normed_mid)
    ffn_sig = jax.nn.sigmoid(matmul(normed_two, r_ffn))
    member = chosen(own_routes, experts)
    shares = (ffn_sig * member).reshape(count, levels, HEADS, local_experts)
    shares = jnp.swapaxes(shares, 1, 2).reshape(count, experts)
    spare = -experts % 128
    hidden = level_gather(jnp.pad(low(jnp.concatenate([middle, shares], axis=1)), ((0, 0), (0, spare))), 3)
    mine = levels * local_experts
    gates = lax.dynamic_slice_in_dim(hidden, width + head * mine, mine, 1)
    gates = jnp.repeat(gates.astype(jnp.float32), FH, axis=1).reshape(rows, levels, -1)
    hidden = hidden[:, :width]
    cotangent = level_gather(own_grads, 1)
    actives, grad_pres, gate_grads = [], [], []
    for i in range(levels):
        pre_act = matmul(hidden, w_in[i])
        sig = jax.nn.sigmoid(pre_act)
        act_pre = pre_act * sig
        actives.append(low(act_pre * gates[:, i]))
        grad_active = matmul(cotangent, w_out[i])
        gate_grads.append(
            jnp.sum((grad_active * act_pre).reshape(rows, local_experts, FH), axis=-1)
        )
        grad_pres.append(low(grad_active * gates[:, i] * silu_slope(pre_act, sig)))
    feed = sum(transposed(actives[i], w_out[i]) for i in range(levels))
    grad_rows = sum(transposed(grad_pres[i], w_in[i]) for i in range(levels))
    grad_in = jnp.stack([low(contract_rows(hidden, grad_pres[i])) for i in range(levels)])
    grad_out = jnp.stack([low(contract_rows(cotangent, actives[i])) for i in range(levels)])

    def scatter_ffn(grad):
        part = lax.psum_scatter(grad, "level", scatter_dimension=0)
        return lax.psum_scatter(part, "group", scatter_dimension=0, tiled=True).astype(jnp.float32)

    ffn_in_grad = scatter_ffn(grad_in)
    ffn_out_grad = scatter_ffn(grad_out)
    layer_out = to_home(low(middle + level_scatter(low(feed), 2)))
    gate_grads = jnp.concatenate(gate_grads, axis=1)
    wide = jnp.zeros((rows, experts + spare), jnp.float32)
    wide = lax.dynamic_update_slice_in_dim(wide, gate_grads, head * mine, 1)
    summed = level_scatter(low(jnp.concatenate([grad_rows, wide], axis=1)), 4)
    gate_grads = summed[:, width : width + experts].reshape(count, HEADS, levels, local_experts)
    gate_grads = jnp.swapaxes(gate_grads, 1, 2).reshape(count, experts)
    grad_logit = low(gate_grads * ffn_sig * (1.0 - ffn_sig) * member)
    grad_second = transposed(grad_logit, r_ffn)
    grad_r_ffn = contract_rows(normed_two, grad_logit)
    grad_gain_two = jnp.sum(grad_second * scaled_two, axis=0)
    grad_bias_two = jnp.sum(grad_second, axis=0)
    grad_middle = (
        own_grads.astype(jnp.float32)
        + summed[:, :width]
        + norm_back(grad_second, gain_two, scaled_two, inverse_two)
    )

    grad_branch = level_gather(low(grad_middle), 1)
    grad_mixed = matmul(grad_branch, w_output).reshape(rows, VEXP, DH)
    grad_w_output = contract_rows(grad_branch, mixed)
    grad_out_gate = jnp.sum(grad_mixed * attended[:, None, :], axis=-1)
    grad_attended = low(jnp.sum(grad_mixed * out_gate[..., None], axis=1))
    grad_out_logit = low(grad_out_gate * out_sig * (1.0 - out_sig) * out_mask)
    row_inner = jnp.sum(grad_attended.astype(jnp.float32) * attended, axis=-1)

    def lines(values):
        return values.reshape(blocks, 1, BLOCK)

    grad_queries, key_window, value_window = attend_back(
        first_block,
        last_block,
        queries,
        window,
        grad_attended,
        lines(positions),
        lines(starts),
        lines(log_total),
        lines(row_inner),
        pos_all[:, None],
    )
    grad_window = jnp.concatenate([key_window * scale, value_window], axis=1)
    grad_window = grad_window.reshape(reach + 1, rows, 2 * DH)
    grad_both = grad_window[0]
    for i in range(reach):
        grad_both = grad_window[i + 1] + shift(low(grad_both), "level", -1).astype(jnp.float32)
    grad_keys, grad_values = low(grad_both[:, :DH]), grad_both[:, DH:]
    grad_projected = low((value_gate[..., None] * grad_values[:, None, :]).reshape(rows, VEXP * DH))
    grad_value_gate = jnp.sum(grad_values[:, None, :] * projected, axis=-1)
    grad_value_logit = low(grad_value_gate * value_sig * (1.0 - value_sig) * value_mask)
    grad_first = (
        transposed(grad_queries, w_query)
        + transposed(grad_keys, w_key)
        + transposed(grad_value_logit, r_value)
        + transposed(grad_out_logit, r_output)
    )
    grad_inputs = norm_back(grad_first, gain_one, scaled_one, inverse_one) + transposed(
        grad_projected, w_value
    )
    input_grad = to_home(low(grad_middle + level_scatter(low(grad_inputs), 2))).astype(jnp.float32)

    grads = jnp.concatenate(
        [
            contract_rows(normed_one, grad_queries),
            contract_rows(normed_one, grad_keys),
            contract_rows(worker_in, grad_projected),
            grad_w_output,
            contract_rows(normed_one, grad_value_logit),
            contract_rows(normed_one, grad_out_logit),
            grad_r_ffn,
            jnp.sum(grad_first * scaled_one, axis=0)[:, None],
            jnp.sum(grad_first, axis=0)[:, None],
            grad_gain_two[:, None],
            grad_bias_two[:, None],
            jnp.zeros((width, pad), jnp.float32),
        ],
        axis=1,
    )
    part = low(grads).reshape(groups, width // groups, cols)
    part = lax.all_to_all(part, "group", split_axis=0, concat_axis=0)
    part = jnp.sum(part.astype(jnp.float32), axis=0)
    part = low(part).reshape(levels, HEADS * wrows, cols)
    part = lax.all_to_all(part, "level", split_axis=0, concat_axis=0)
    part = jnp.sum(part.astype(jnp.float32), axis=0)
    part = lax.all_to_all(
        part.reshape(HEADS, wrows, cols), "head", split_axis=0, concat_axis=0, tiled=True
    )

    def columns(first, size):
        return part[:, :, first : first + size].transpose(1, 0, 2).reshape(wrows, HEADS * size)

    common = jnp.sum(part[:, :, at:], axis=0)
    return (
        layer_out,
        input_grad,
        common[:, experts],
        common[:, experts + 1],
        common[:, experts + 2],
        common[:, experts + 3],
        columns(0, DH),
        columns(DH, DH),
        columns(2 * DH, VEXP * DH),
        columns(2 * DH + VEXP * DH, VEXP * DH),
        columns(base, VEXP),
        columns(base + VEXP, VEXP),
        common[:, :experts],
        ffn_in_grad,
        ffn_out_grad,
    )


def solution(mesh):
    groups, shards = mesh.devices.shape
    fine = Mesh(mesh.devices.reshape(groups, shards // HEADS, HEADS), TOK)
    two, one, three = P(TOK, None), P(TOK), P(TOK, None, None)
    ffn = P("group", ("level", "head"))
    return jax.shard_map(
        body,
        mesh=fine,
        in_specs=(two, two, two, P("group", None), three, three, two, one, one, one, one)
        + (two,) * 7
        + (ffn, ffn),
        out_specs=(two, two, one, one, one, one) + (two,) * 7 + (ffn, ffn),
        check_vma=False,
    )
```

```python
import functools

import jax
import jax.numpy as jnp
from jax import lax
from jax.experimental import pallas as pl
from jax.experimental.pallas import tpu as pltpu
from jax.sharding import Mesh, PartitionSpec as P

HEADS = 4
DH = 128
VEXP = 5
FH = 128
LMAX = 4096

TOK = ("group", "level", "head")


def matmul(left_side, right_side):
    return jnp.dot(left_side, right_side, preferred_element_type=jnp.float32)


def transposed(left_side, right_side):
    return lax.dot_general(
        left_side, right_side, (((1,), (1,)), ((), ())), preferred_element_type=jnp.float32
    )


def contract_rows(left_side, right_side):
    return lax.dot_general(
        left_side, right_side, (((0,), (0,)), ((), ())), preferred_element_type=jnp.float32
    )


def low(value):
    return value.astype(jnp.bfloat16)


def layer_norm(inputs, gain_vec, bias_vec):
    centred = inputs - jnp.mean(inputs, axis=-1, keepdims=True)
    inverse = lax.rsqrt(jnp.mean(centred * centred, axis=-1, keepdims=True) + 1e-05)
    scaled = centred * inverse
    return (scaled * gain_vec + bias_vec, scaled, inverse)


def norm_back(grad_normed, gain_vec, scaled, inverse):
    inner_grad = grad_normed * gain_vec
    return inverse * (
        inner_grad
        - jnp.mean(inner_grad, axis=-1, keepdims=True)
        - scaled * jnp.mean(inner_grad * scaled, axis=-1, keepdims=True)
    )


def to_workers(rows):
    levels = lax.axis_size("level")
    count = rows.shape[0]
    came = lax.all_to_all(
        rows.reshape(levels, count // levels, -1), "level", split_axis=0, concat_axis=0, tiled=True
    )
    came = came.reshape(levels, HEADS, count // levels // HEADS, -1)
    return came.transpose(1, 0, 2, 3).reshape(count, -1)


MESH = pl.DeviceIdType.MESH


def partners(head):
    near = head + 1 - 2 * lax.rem(head, 2)
    far = lax.rem(head + 2, HEADS)
    return near, far


def greet(near, far):
    barrier = pltpu.get_barrier_semaphore()
    for peer in (near, far):
        pl.semaphore_signal(barrier, inc=1, device_id={"head": peer}, device_id_type=MESH)
    pl.semaphore_wait(barrier, 2)


def remote(src, dst, send, recv, peer):
    return pltpu.make_async_remote_copy(
        src_ref=src,
        dst_ref=dst,
        send_sem=send,
        recv_sem=recv,
        device_id={"head": peer},
        device_id_type=MESH,
    )


def cost(flops, moved):
    return pl.CostEstimate(flops=int(flops), bytes_accessed=int(moved), transcendentals=0)


def gather_kernel(
    by_source, own, out, local_sem, near_send, near_recv, far_send, far_recv, pass_send, pass_recv
):
    head = lax.axis_index("head")
    near, far = partners(head)
    greet(near, far)

    def spot(i, source):
        return out.at[source, i] if by_source else out.at[i, source]

    pieces = range(HEADS)
    to_far = [remote(own.at[i], spot(i, head), far_send.at[i], far_recv.at[i], far) for i in pieces]
    to_near = [
        remote(own.at[i], spot(i, head), near_send.at[i], near_recv.at[i], near) for i in pieces
    ]
    passed = [
        remote(spot(i, far), spot(i, far), pass_send.at[i], pass_recv.at[i], near) for i in pieces
    ]
    kept = [pltpu.make_async_copy(own.at[i], spot(i, head), local_sem.at[i]) for i in pieces]
    for copy in to_far + to_near + kept:
        copy.start()
    for i in pieces:
        to_far[i].wait_recv()
        passed[i].start()
    for i in pieces:
        to_near[i].wait_recv()
        passed[i].wait_recv()
        kept[i].wait()
        to_far[i].wait_send()
        to_near[i].wait_send()
        passed[i].wait_send()


def level_gather(rows, collective_id, by_source=False):
    count, width = rows.shape
    whole = pl.pallas_call(
        functools.partial(gather_kernel, by_source),
        out_shape=jax.ShapeDtypeStruct((HEADS, HEADS, count // HEADS, width), rows.dtype),
        in_specs=[pl.BlockSpec(memory_space=pltpu.VMEM)],
        out_specs=pl.BlockSpec(memory_space=pl.ANY),
        scratch_shapes=[pltpu.SemaphoreType.DMA((HEADS,))] * 7,
        compiler_params=pltpu.CompilerParams(collective_id=collective_id, has_side_effects=True),
        cost_estimate=cost(0, 90e6),
        name="level_gather",
    )(rows.reshape(HEADS, count // HEADS, width))
    return whole.reshape(HEADS * count, width)


def scatter_kernel(
    by_source, part, out, near_buf, send_buf, far_buf, near_send, near_recv, far_send, far_recv
):
    head = lax.axis_index("head")
    near, far = partners(head)
    greet(near, far)
    across = HEADS - 1 - head
    pieces = range(HEADS)

    def spot(i, dest):
        return (dest, i) if by_source else (i, dest)

    def to_near(slot, i, dest):
        return remote(
            part.at[spot(i, dest)],
            near_buf.at[slot, i],
            near_send.at[slot, i],
            near_recv.at[slot, i],
            near,
        )

    first = [to_near(0, i, across) for i in pieces]
    second = [to_near(1, i, near) for i in pieces]
    onward = [
        remote(send_buf.at[i], far_buf.at[i], far_send.at[i], far_recv.at[i], far) for i in pieces
    ]
    for copy in first + second:
        copy.start()
    for i in pieces:
        first[i].wait_recv()
        both = part[spot(i, far)].astype(jnp.float32) + near_buf[0, i].astype(jnp.float32)
        send_buf[i] = both.astype(jnp.bfloat16)
        onward[i].start()
    for i in pieces:
        second[i].wait_recv()
        out[i] = part[spot(i, head)].astype(jnp.float32) + near_buf[1, i].astype(jnp.float32)
    for i in pieces:
        onward[i].wait_recv()
        out[i] = out[i] + far_buf[i].astype(jnp.float32)
    for i in pieces:
        first[i].wait_send()
        second[i].wait_send()
        onward[i].wait_send()


def level_scatter(rows, collective_id, by_source=False):
    total, width = rows.shape
    piece = total // (HEADS * HEADS)
    low_type = jnp.bfloat16
    mine = pl.pallas_call(
        functools.partial(scatter_kernel, by_source),
        out_shape=jax.ShapeDtypeStruct((HEADS, piece, width), jnp.float32),
        in_specs=[pl.BlockSpec(memory_space=pltpu.VMEM)],
        out_specs=pl.BlockSpec(memory_space=pltpu.VMEM),
        scratch_shapes=[
            pltpu.VMEM((2, HEADS, piece, width), low_type),
            pltpu.VMEM((HEADS, piece, width), low_type),
            pltpu.VMEM((HEADS, piece, width), low_type),
            pltpu.SemaphoreType.DMA((2, HEADS)),
            pltpu.SemaphoreType.DMA((2, HEADS)),
            pltpu.SemaphoreType.DMA((HEADS,)),
            pltpu.SemaphoreType.DMA((HEADS,)),
        ],
        compiler_params=pltpu.CompilerParams(
            collective_id=collective_id, has_side_effects=True, vmem_limit_bytes=32 * 2**20
        ),
        cost_estimate=cost(0, 80e6),
        name="level_scatter",
    )(rows.reshape(HEADS, HEADS, piece, width))
    return mine.reshape(HEADS * piece, width)


def meet(near):
    barrier = pltpu.get_barrier_semaphore()
    pl.semaphore_signal(barrier, inc=1, device_id={"head": near}, device_id_type=MESH)
    pl.semaphore_wait(barrier, 1)


def pair_scatter_kernel(by_source, part, out, out_far, near_buf, send, recv):
    head = lax.axis_index("head")
    near, far = partners(head)
    meet(near)
    across = HEADS - 1 - head
    pieces = range(HEADS)

    def spot(i, dest):
        return (dest, i) if by_source else (i, dest)

    def to_near(slot, i, dest):
        return remote(
            part.at[spot(i, dest)], near_buf.at[slot, i], send.at[slot, i], recv.at[slot, i], near
        )

    first = [to_near(0, i, across) for i in pieces]
    second = [to_near(1, i, near) for i in pieces]
    for copy in first + second:
        copy.start()
    for i in pieces:
        first[i].wait_recv()
        both = part[spot(i, far)].astype(jnp.float32) + near_buf[0, i].astype(jnp.float32)
        out_far[i] = both.astype(jnp.bfloat16)
    for i in pieces:
        second[i].wait_recv()
        out[i] = part[spot(i, head)].astype(jnp.float32) + near_buf[1, i].astype(jnp.float32)
    for i in pieces:
        first[i].wait_send()
        second[i].wait_send()


def pair_scatter(rows, collective_id, by_source=False):
    total, width = rows.shape
    piece = total // (HEADS * HEADS)
    mine, other = pl.pallas_call(
        functools.partial(pair_scatter_kernel, by_source),
        out_shape=[
            jax.ShapeDtypeStruct((HEADS, piece, width), jnp.float32),
            jax.ShapeDtypeStruct((HEADS, piece, width), jnp.bfloat16),
        ],
        in_specs=[pl.BlockSpec(memory_space=pltpu.VMEM)],
        out_specs=[pl.BlockSpec(memory_space=pltpu.VMEM)] * 2,
        scratch_shapes=[
            pltpu.VMEM((2, HEADS, piece, width), jnp.bfloat16),
            pltpu.SemaphoreType.DMA((2, HEADS)),
            pltpu.SemaphoreType.DMA((2, HEADS)),
        ],
        compiler_params=pltpu.CompilerParams(
            collective_id=collective_id, has_side_effects=True, vmem_limit_bytes=32 * 2**20
        ),
        cost_estimate=cost(0, 25e6),
        name="pair_scatter",
    )(rows.reshape(HEADS, HEADS, piece, width))
    return mine.reshape(HEADS * piece, width), other.reshape(HEADS * piece, width)


def pair_gather_kernel(by_source, own, other, out, local_sem, send, recv):
    head = lax.axis_index("head")
    near, far = partners(head)
    meet(near)
    copies, kept = [], []
    for i in range(HEADS):
        for slot, (block, source) in enumerate(((own, head), (other, far))):
            place = out.at[source, i] if by_source else out.at[i, source]
            copies.append(
                remote(block.at[i], place, send.at[slot, i], recv.at[slot, i], near)
            )
            kept.append(pltpu.make_async_copy(block.at[i], place, local_sem.at[slot, i]))
    for copy in copies + kept:
        copy.start()
    for copy in copies + kept:
        copy.wait()


def pair_gather(own, other, collective_id, by_source=False):
    count, width = own.shape
    split = (HEADS, count // HEADS, width)
    whole = pl.pallas_call(
        functools.partial(pair_gather_kernel, by_source),
        out_shape=jax.ShapeDtypeStruct((HEADS,) + split, own.dtype),
        in_specs=[pl.BlockSpec(memory_space=pltpu.VMEM)] * 2,
        out_specs=pl.BlockSpec(memory_space=pl.ANY),
        scratch_shapes=[pltpu.SemaphoreType.DMA((2, HEADS))] * 3,
        compiler_params=pltpu.CompilerParams(collective_id=collective_id, has_side_effects=True),
        cost_estimate=cost(0, 25e6),
        name="pair_gather",
    )(own.reshape(split), other.reshape(split))
    return whole.reshape(HEADS * count, width)


def to_far(rows):
    return lax.ppermute(rows, "head", [(i, (i + 2) % HEADS) for i in range(HEADS)])


def after(value, *others):
    return lax.optimization_barrier((value,) + others)[0]


def ring(axis):
    me, size = lax.axis_index(axis), lax.axis_size(axis)
    ahead = [lax.rem(me + k, size) for k in range(1, size)]
    behind = [lax.rem(me + size - k, size) for k in range(1, size)]
    return me, ahead, behind


def reach_out(src, dst, send, recv, peer):
    return pltpu.make_async_remote_copy(
        src_ref=src, dst_ref=dst, send_sem=send, recv_sem=recv, device_id=peer, device_id_type=MESH
    )


def greet_all(peers):
    barrier = pltpu.get_barrier_semaphore()
    for peer in peers:
        pl.semaphore_signal(barrier, inc=1, device_id=peer, device_id_type=MESH)
    pl.semaphore_wait(barrier, len(peers))


def start_kernel(
    tokens, weights, tables, picks, order, rows, full, routes, chosen_rows, orders, own_sem, *sems
):
    sems = iter(sems)

    def pair():
        return next(sems), next(sems)

    group, groups_ahead, _ = ring("group")
    level, levels_ahead, levels_behind = ring("level")
    head = lax.axis_index("head")
    near, far = partners(head)
    mates = [near, far, HEADS - 1 - head]
    greet_all(
        [{"head": m} for m in mates]
        + [{"level": n} for n in levels_ahead]
        + [{"group": n} for n in groups_ahead]
    )
    started = []

    def send(src, dst, send_sem, recv_sem, peer):
        copy = reach_out(src, dst, send_sem, recv_sem, peer)
        copy.start()
        started.append(copy)
        return copy

    out_s, out_r = pair()
    pick_s, pick_r = pair()
    crossing, picking = [], []
    for k, to in enumerate(levels_ahead):
        peer = {"level": to}
        crossing.append(send(tokens.at[to], rows.at[:, head, level], out_s.at[k], out_r.at[k], peer))
    mate_s, mate_r = pair()
    table_s, table_r = pair()
    order_s, order_r = pair()
    to_mates, order_mates, table_mates = [], [], []
    for k, to in enumerate(mates):
        peer = {"head": to}
        to_mates.append(
            send(weights.at[to], full.at[group, level, head], mate_s.at[k], mate_r.at[k], peer)
        )
        order_mates.append(
            send(order, orders.at[level, head], order_s.at[k], order_r.at[k], peer)
        )
    own = [
        (tokens.at[level], rows.at[:, head, level]),
        (weights.at[head], full.at[group, level, head]),
        (tables.at[head], routes.at[head]),
        (picks.at[level], chosen_rows.at[level]),
        (order, orders.at[level, head]),
    ]
    own = [pltpu.make_async_copy(src, dst, own_sem.at[i]) for i, (src, dst) in enumerate(own)]
    for copy in own:
        copy.start()
    far_s, far_r = pair()
    near_s, near_r = pair()
    pass_s, pass_r = pair()
    to_far, to_near = [], []

    def share(k, src, source):
        place = rows.at[:, head, source]
        to_far.append(send(src, place, far_s.at[k], far_r.at[k], {"head": far}))
        to_near.append(send(src, place, near_s.at[k], near_r.at[k], {"head": near}))

    share(0, tokens.at[level], level)
    block_s, block_r = pair()
    group_s, group_r = pair()
    orders_s, orders_r = pair()
    for copy in to_mates:
        copy.wait_recv()
    own[1].wait()
    blocks, grouped, ordered = [], [], []

    def to_groups(j, source):
        for k, to in enumerate(groups_ahead):
            block = full.at[group, source]
            grouped.append(
                send(block, block, group_s.at[k, j], group_r.at[k, j], {"group": to})
            )

    for k, to in enumerate(levels_ahead):
        block = full.at[group, level]
        blocks.append(send(block, block, block_s.at[k], block_r.at[k], {"level": to}))
    to_groups(0, level)
    for k, to in enumerate(mates):
        table_mates.append(
            send(tables.at[to], routes.at[head], table_s.at[k], table_r.at[k], {"head": to})
        )
    for k, to in enumerate(levels_ahead):
        picking.append(
            send(picks.at[to], chosen_rows.at[level], pick_s.at[k], pick_r.at[k], {"level": to})
        )
    for copy in order_mates:
        copy.wait_recv()
    own[4].wait()
    for k, to in enumerate(levels_ahead):
        block = orders.at[level]
        ordered.append(send(block, block, orders_s.at[k], orders_r.at[k], {"level": to}))
    for k, source in enumerate(levels_behind):
        crossing[k].wait_recv()
        share(k + 1, rows.at[:, head, source], source)
    for k, source in enumerate(levels_behind):
        blocks[k].wait_recv()
        to_groups(k + 1, source)
    passed = []
    for k, source in enumerate([level] + levels_behind):
        to_far[k].wait_recv()
        place = rows.at[:, far, source]
        passed.append(send(place, place, pass_s.at[k], pass_r.at[k], {"head": near}))
    for copy in to_near + passed + grouped + table_mates + picking + ordered:
        copy.wait_recv()
    for copy in started:
        copy.wait_send()
    for i in (0, 2, 3):
        own[i].wait()


def start(tokens, weights, tables, picks, order):
    groups, levels = lax.axis_size("group"), lax.axis_size("level")
    _, _, piece, width = tokens.shape
    shapes = [
        jax.ShapeDtypeStruct((HEADS, HEADS, levels, piece, width), tokens.dtype),
        jax.ShapeDtypeStruct((groups, levels) + weights.shape, weights.dtype),
        jax.ShapeDtypeStruct(tables.shape, tables.dtype),
        jax.ShapeDtypeStruct(picks.shape, picks.dtype),
        jax.ShapeDtypeStruct((levels, HEADS) + order.shape, order.dtype),
    ]
    dma = pltpu.SemaphoreType.DMA
    others, mates = (levels - 1,), (HEADS - 1,)
    counts = [others] * 2 + [mates] * 3 + [(levels,)] * 3 + [others, (groups - 1, levels), others]
    return pl.pallas_call(
        start_kernel,
        out_shape=shapes,
        in_specs=[pl.BlockSpec(memory_space=pltpu.VMEM)] * 5,
        out_specs=[pl.BlockSpec(memory_space=pl.ANY)] * 5,
        scratch_shapes=[dma((5,))] + [dma(c) for c in counts for _ in range(2)],
        compiler_params=pltpu.CompilerParams(collective_id=9, has_side_effects=True),
        cost_estimate=cost(0, 200e6),
        name="start",
    )(tokens, weights, tables, picks, order)


def finish_kernel(
    part,
    middle,
    done,
    grads,
    home_grad,
    home_out,
    owned,
    near_buf,
    send_buf,
    far_buf,
    total,
    back_buf,
    came_buf,
    group_buf,
    level_send,
    level_buf,
    head_send,
    own_sem,
    *sems,
):
    sems = iter(sems)

    def pair():
        return next(sems), next(sems)

    group, groups_ahead, _ = ring("group")
    level, levels_ahead, levels_behind = ring("level")
    head = lax.axis_index("head")
    near, far = partners(head)
    across = HEADS - 1 - head
    mates = [near, far, across]
    greet_all(
        [{"head": m} for m in mates]
        + [{"level": n} for n in levels_ahead]
        + [{"group": n} for n in groups_ahead]
    )
    started = []

    def send(src, dst, send_sem, recv_sem, peer):
        copy = reach_out(src, dst, send_sem, recv_sem, peer)
        copy.start()
        started.append(copy)
        return copy

    pieces = range(HEADS)
    near_s, near_r = pair()
    far_s, far_r = pair()
    group_s, group_r = pair()
    done_s, done_r = pair()
    back_s, back_r = pair()
    level_s, level_r = pair()
    mate_s, mate_r = pair()
    first, second, onward = [], [], []
    for slot, (dest, copies) in enumerate(((across, first), (near, second))):
        for i in pieces:
            copies.append(
                send(
                    part.at[i, dest],
                    near_buf.at[slot, i],
                    near_s.at[slot, i],
                    near_r.at[slot, i],
                    {"head": near},
                )
            )
    order = levels_ahead + [level]
    grouped = []
    for j, dest in enumerate(order):
        grouped.append(
            [
                send(
                    grads.at[to, dest],
                    group_buf.at[k, j],
                    group_s.at[k, j],
                    group_r.at[k, j],
                    {"group": to},
                )
                for k, to in enumerate(groups_ahead)
            ]
        )
    out_own = pltpu.make_async_copy(done.at[:, level], home_out.at[level], own_sem)
    out_own.start()
    homing = [
        send(done.at[:, to], home_out.at[level], done_s.at[k], done_r.at[k], {"level": to})
        for k, to in enumerate(levels_ahead)
    ]
    for i in pieces:
        first[i].wait_recv()
        both = part[i, far].astype(jnp.float32) + near_buf[0, i].astype(jnp.float32)
        send_buf[i] = both.astype(jnp.bfloat16)
        onward.append(send(send_buf.at[i], far_buf.at[i], far_s.at[i], far_r.at[i], {"head": far}))
    for i in pieces:
        second[i].wait_recv()
        both = part[i, head].astype(jnp.float32) + near_buf[1, i].astype(jnp.float32)
        total[i] = both + middle[i]
    leveled = []
    for j, dest in enumerate(order):
        amount = grads[group, dest].astype(jnp.float32)
        for k, copy in enumerate(grouped[j]):
            copy.wait_recv()
            amount = amount + group_buf[k, j].astype(jnp.float32)
        level_send[j] = amount.astype(jnp.bfloat16)
        if j < len(levels_ahead):
            leveled.append(
                send(level_send.at[j], level_buf.at[j], level_s.at[j], level_r.at[j], {"level": dest})
            )
    for i in pieces:
        onward[i].wait_recv()
        both = total[i] + far_buf[i].astype(jnp.float32)
        back_buf[i] = both.astype(jnp.bfloat16).reshape(back_buf.shape[1:])
    backs = [
        send(back_buf.at[:, to], came_buf.at[level], back_s.at[k], back_r.at[k], {"level": to})
        for k, to in enumerate(levels_ahead)
    ]
    amount = level_send[len(levels_ahead)].astype(jnp.float32)
    for j, copy in enumerate(leveled):
        copy.wait_recv()
        amount = amount + level_buf[j].astype(jnp.float32)
    head_send[...] = amount.astype(jnp.bfloat16)
    sharing = [
        send(head_send.at[to], owned.at[head], mate_s.at[k], mate_r.at[k], {"head": to})
        for k, to in enumerate(mates)
    ]
    owned[head] = head_send[head]
    home_grad[level] = back_buf[:, level].astype(jnp.float32)
    for k, source in enumerate(levels_behind):
        backs[k].wait_recv()
        home_grad[source] = came_buf[source].astype(jnp.float32)
    for copy in homing + sharing:
        copy.wait_recv()
    for copy in started:
        copy.wait_send()
    out_own.wait()


def finish(part, middle, done, grads):
    groups, levels = lax.axis_size("group"), lax.axis_size("level")
    _, _, piece, width = done.shape
    low_type = jnp.bfloat16
    count = levels * piece
    block = grads.shape[2:]
    dma = pltpu.SemaphoreType.DMA
    others = (levels - 1,)
    counts = [(2, HEADS), (HEADS,), (groups - 1, levels), others, others, others, (HEADS - 1,)]
    vmem = pl.BlockSpec(memory_space=pltpu.VMEM)
    return pl.pallas_call(
        finish_kernel,
        out_shape=[
            jax.ShapeDtypeStruct((levels, HEADS, piece, width), jnp.float32),
            jax.ShapeDtypeStruct((levels, HEADS, piece, width), low_type),
            jax.ShapeDtypeStruct(block, low_type),
        ],
        in_specs=[vmem] * 4,
        out_specs=[vmem] * 3,
        scratch_shapes=[
            pltpu.VMEM((2, HEADS, count, width), low_type),
            pltpu.VMEM((HEADS, count, width), low_type),
            pltpu.VMEM((HEADS, count, width), low_type),
            pltpu.VMEM((HEADS, count, width), jnp.float32),
            pltpu.VMEM((HEADS, levels, piece, width), low_type),
            pltpu.VMEM((levels, HEADS, piece, width), low_type),
            pltpu.VMEM((groups - 1, levels) + block, low_type),
            pltpu.VMEM((levels,) + block, low_type),
            pltpu.VMEM((levels - 1,) + block, low_type),
            pltpu.VMEM(block, low_type),
            dma,
        ]
        + [dma(c) for c in counts for _ in range(2)],
        compiler_params=pltpu.CompilerParams(
            collective_id=10, has_side_effects=True, vmem_limit_bytes=56 * 2**20
        ),
        cost_estimate=cost(0, 200e6),
        name="finish",
    )(part, middle, done, grads)


BLOCK = 512
LOG2E = 1.4426950408889634


def dot(left_side, right_side, left_dim, right_dim):
    return lax.dot_general(
        left_side,
        right_side,
        (((left_dim,), (right_dim,)), ((), ())),
        preferred_element_type=jnp.float32,
    )


def attend_kernel(parts, first, q, *refs):
    keys, values = refs[:parts], refs[parts : 2 * parts]
    pos_q, start_q, pos_k, out, lse, top, total, acc = refs[2 * parts :]
    at = pl.program_id(0)
    blocks = pl.num_programs(0)
    rate = LOG2E * DH ** (-0.5)
    top[...] = jnp.full_like(top, -1e30)
    total[...] = jnp.zeros_like(total)
    acc[...] = jnp.zeros_like(acc)
    query = q[...]
    row_at, row_from = pos_q[0], start_q[0]

    for part in range(parts):

        def step(block, carry, k=keys[part], v=values[part], part=part):
            rows = pl.ds(pl.multiple_of(block * BLOCK, BLOCK), BLOCK)
            spot = pl.ds(pl.multiple_of((part * blocks + block) * BLOCK, BLOCK), BLOCK)
            scores = dot(k[rows, :], query, 1, 1)
            key_at = pos_k[spot, :]
            scores = jnp.where((key_at >= row_from) & (key_at <= row_at), scores, -1e30)
            old = top[...]
            new = jnp.maximum(old, jnp.max(scores, axis=0, keepdims=True))
            shrink = jnp.exp2((old - new) * rate)
            weight = jnp.exp2((scores - new) * rate)
            total[...] = total[...] * shrink + jnp.sum(weight, axis=0, keepdims=True)
            acc[...] = acc[...] * shrink + dot(v[rows, :], weight.astype(jnp.bfloat16), 0, 0)
            top[...] = new
            return carry

        begin = jnp.maximum(first[at] - part * blocks, 0)
        end = at + 1 if part == parts - 1 else blocks
        lax.fori_loop(begin, end, step, 0)
    out[...] = (acc[...] / total[...]).T
    lse[0] = top[...] * rate + jnp.log2(total[...])


def attend(first, queries, window, pos_q, start_q, pos_k):
    rows = queries.shape[0]
    parts = len(window)
    line = pl.BlockSpec((1, 1, BLOCK), lambda i, *_: (i, 0, 0))
    grid_spec = pltpu.PrefetchScalarGridSpec(
        num_scalar_prefetch=1,
        grid=(rows // BLOCK,),
        in_specs=[pl.BlockSpec((BLOCK, DH), lambda i, *_: (i, 0))]
        + [pl.BlockSpec((rows, DH), lambda i, *_: (0, 0))] * parts
        + [pl.BlockSpec((rows, DH), lambda i, *_: (0, 1))] * parts
        + [line, line, pl.BlockSpec((parts * rows, 1), lambda i, *_: (0, 0))],
        out_specs=[pl.BlockSpec((BLOCK, DH), lambda i, *_: (i, 0)), line],
        scratch_shapes=[
            pltpu.VMEM((1, BLOCK), jnp.float32),
            pltpu.VMEM((1, BLOCK), jnp.float32),
            pltpu.VMEM((DH, BLOCK), jnp.float32),
        ],
    )
    return pl.pallas_call(
        functools.partial(attend_kernel, parts),
        grid_spec=grid_spec,
        out_shape=[
            jax.ShapeDtypeStruct((rows, DH), jnp.float32),
            jax.ShapeDtypeStruct((rows // BLOCK, 1, BLOCK), jnp.float32),
        ],
        compiler_params=pltpu.CompilerParams(vmem_limit_bytes=48 * 2**20),
        cost_estimate=cost(2e10, 1e7),
        name="attend",
    )(first, queries, *window, *window, pos_q, start_q, pos_k)


def attend_back_kernel(parts, first, q, *refs):
    keys, values = refs[:parts], refs[parts : 2 * parts]
    grad, pos_q, start_q, lse, inner, pos_k, grad_q = refs[2 * parts : 2 * parts + 7]
    grads = refs[2 * parts + 7 : 3 * parts + 7]
    sum_k, sum_v, acc = refs[3 * parts + 7 :]
    at = pl.program_id(0)
    blocks = pl.num_programs(0)
    rate = LOG2E * DH ** (-0.5)
    scale = DH ** (-0.5)

    @pl.when(at == 0)
    def _():
        sum_k[...] = jnp.zeros_like(sum_k)
        sum_v[...] = jnp.zeros_like(sum_v)

    acc[...] = jnp.zeros_like(acc)
    query, grad_out = q[...], grad[...]
    row_at, row_from, row_lse, row_inner = pos_q[0], start_q[0], lse[0], inner[0]

    for part in range(parts):

        def step(block, carry, k=keys[part], v=values[part], part=part):
            rows = pl.ds(pl.multiple_of(block * BLOCK, BLOCK), BLOCK)
            spot = pl.ds(pl.multiple_of((part * blocks + block) * BLOCK, BLOCK), BLOCK)
            key, value = k[rows, :], v[rows, :]
            scores = dot(key, query, 1, 1)
            key_at = pos_k[spot, :]
            seen = (key_at >= row_from) & (key_at <= row_at)
            soft = jnp.where(seen, jnp.exp2(scores * rate - row_lse), 0.0)
            grad_soft = dot(value, grad_out, 1, 1)
            grad_scores = (soft * (grad_soft - row_inner)).astype(jnp.bfloat16)
            sum_v[spot, :] += dot(soft.astype(jnp.bfloat16), grad_out, 1, 0)
            sum_k[spot, :] += dot(grad_scores, query, 1, 0)
            acc[...] += dot(grad_scores, key, 0, 0)
            return carry

        begin = jnp.maximum(first[at] - part * blocks, 0)
        end = at + 1 if part == parts - 1 else blocks
        lax.fori_loop(begin, end, step, 0)
    grad_q[...] = (acc[...] * scale).astype(jnp.bfloat16)

    @pl.when(at == blocks - 1)
    def _():
        size = grads[0].shape[0]
        for part in range(parts):
            spot = slice(part * size, (part + 1) * size)
            grads[part][:, :DH] = (sum_k[spot, :] * scale).astype(grads[part].dtype)
            grads[part][:, DH:] = sum_v[spot, :].astype(grads[part].dtype)


def attend_back(first, queries, window, grads, pos_q, start_q, lse, inner, pos_k):
    rows = queries.shape[0]
    parts = len(window)
    block = pl.BlockSpec((BLOCK, DH), lambda i, *_: (i, 0))
    line = pl.BlockSpec((1, 1, BLOCK), lambda i, *_: (i, 0, 0))
    grid_spec = pltpu.PrefetchScalarGridSpec(
        num_scalar_prefetch=1,
        grid=(rows // BLOCK,),
        in_specs=[block]
        + [pl.BlockSpec((rows, DH), lambda i, *_: (0, 0))] * parts
        + [pl.BlockSpec((rows, DH), lambda i, *_: (0, 1))] * parts
        + [block, line, line, line, line]
        + [pl.BlockSpec((parts * rows, 1), lambda i, *_: (0, 0))],
        out_specs=[block] + [pl.BlockSpec((rows, 2 * DH), lambda i, *_: (0, 0))] * parts,
        scratch_shapes=[
            pltpu.VMEM((parts * rows, DH), jnp.float32),
            pltpu.VMEM((parts * rows, DH), jnp.float32),
            pltpu.VMEM((BLOCK, DH), jnp.float32),
        ],
    )
    kinds = [jnp.bfloat16] * (parts - 1) + [jnp.float32]
    return pl.pallas_call(
        functools.partial(attend_back_kernel, parts),
        grid_spec=grid_spec,
        out_shape=[jax.ShapeDtypeStruct((rows, DH), jnp.bfloat16)]
        + [jax.ShapeDtypeStruct((rows, 2 * DH), kind) for kind in kinds],
        compiler_params=pltpu.CompilerParams(vmem_limit_bytes=48 * 2**20),
        cost_estimate=cost(2e10, 1e7),
        name="attend_back",
    )(first, queries, *window, *window, grads, pos_q, start_q, lse, inner, pos_k)


def front_kernel(local, head, hidden, grads, weights, gates, active, grad_pre, rows_out, acc):
    groups, levels, _, depth, width = weights.shape
    tile = hidden.shape[0]
    model = groups * depth
    acc[...] = jnp.zeros_like(acc)
    gate_grads = []
    for level in range(levels):
        pre_act = jnp.zeros((tile, width), jnp.float32)
        grad_active = jnp.zeros((tile, width), jnp.float32)
        for group in range(groups):
            part = slice(group * depth, (group + 1) * depth)
            pre_act += dot(hidden[:, part], weights[group, level, 0], 1, 0)
            grad_active += dot(grads[:, part], weights[group, level, 1], 1, 0)
        first = level * local
        gate = jnp.concatenate(
            [jnp.broadcast_to(gates[:, first + e : first + e + 1], (tile, FH)) for e in range(local)],
            axis=1,
        )
        sig = 1.0 / (1.0 + jnp.exp2(-LOG2E * pre_act))
        act_pre = pre_act * sig
        columns = slice(level * width, (level + 1) * width)
        active[:, columns] = (act_pre * gate).astype(jnp.bfloat16)
        product = grad_active * act_pre
        for e in range(local):
            gate_grads.append(
                jnp.sum(product[:, e * FH : (e + 1) * FH], axis=1, keepdims=True)
            )
        slope = sig * (1.0 + pre_act * (1.0 - sig))
        low_pre = (grad_active * gate * slope).astype(jnp.bfloat16)
        grad_pre[:, columns] = low_pre
        for group in range(groups):
            part = slice(group * depth, (group + 1) * depth)
            acc[:, part] += dot(low_pre, weights[group, level, 0], 1, 1)
    rows_out[:, :model] = acc[...].astype(jnp.bfloat16)
    spare = rows_out.shape[1] - model
    lane = lax.broadcasted_iota(jnp.int32, (tile, spare), 1) - head[0] * (levels * local)
    spread = jnp.zeros((tile, spare), jnp.float32)
    for e, column in enumerate(gate_grads):
        spread = jnp.where(lane == e, column, spread)
    rows_out[:, model:] = spread.astype(jnp.bfloat16)


def ffn_front(head, hidden, grads, weights, gates, local):
    rows, wide = hidden.shape
    groups, levels, _, depth, width = weights.shape
    tile = 512

    def by_row(columns):
        return pl.BlockSpec((tile, columns), lambda i, *_: (i, 0))

    grid_spec = pltpu.PrefetchScalarGridSpec(
        num_scalar_prefetch=1,
        grid=(rows // tile,),
        in_specs=[
            by_row(wide),
            by_row(groups * depth),
            pl.BlockSpec(
                weights.shape, lambda i, *_: (0, 0, 0, 0, 0), pipeline_mode=pl.Buffered(1)
            ),
            by_row(gates.shape[1]),
        ],
        out_specs=[by_row(levels * width), by_row(levels * width), by_row(wide)],
        scratch_shapes=[pltpu.VMEM((tile, groups * depth), jnp.float32)],
    )
    hidden_units = jax.ShapeDtypeStruct((rows, levels * width), jnp.bfloat16)
    return pl.pallas_call(
        functools.partial(front_kernel, local),
        grid_spec=grid_spec,
        out_shape=[hidden_units, hidden_units, jax.ShapeDtypeStruct((rows, wide), jnp.bfloat16)],
        compiler_params=pltpu.CompilerParams(vmem_limit_bytes=58 * 2**20),
        cost_estimate=cost(6 * rows * groups * depth * levels * width, 3e7),
        name="ffn_front",
    )(head, hidden, grads, weights, gates)


def rear_kernel(rows_in, hidden_units, weight_grads):
    groups, _, depth, _ = weight_grads.shape
    units = hidden_units[...]
    for group in range(groups):
        part = slice(group * depth, (group + 1) * depth)
        weight_grads[group, 0] = dot(rows_in[:, part], units, 0, 0).astype(jnp.bfloat16)


def feed_kernel(rows_in, low_pre, active, weights, weight_grads, feed, acc):
    groups, _, _, depth, _ = weights.shape
    level = pl.program_id(0)
    units, act = low_pre[...], active[...]
    for group in range(groups):
        part = slice(group * depth, (group + 1) * depth)
        weight_grads[group, 0] = dot(rows_in[:, part], units, 0, 0).astype(jnp.bfloat16)
        fed = dot(act, weights[group, 0, 0], 1, 1)

        @pl.when(level == 0)
        def _():
            acc[:, part] = fed

        @pl.when(level > 0)
        def _():
            acc[:, part] += fed

    @pl.when(level == pl.num_programs(0) - 1)
    def _():
        feed[...] = acc[...].astype(jnp.bfloat16)


def whole_rows(rows, columns):
    return pl.BlockSpec((rows, columns), lambda i: (0, 0), pipeline_mode=pl.Buffered(1))


def ffn_feed(hidden, grad_pre, active, weights):
    rows, wide = hidden.shape
    groups, levels, _, depth, width = weights.shape
    by_level = pl.BlockSpec((rows, width), lambda i: (0, i))
    grads_spec = pl.BlockSpec((groups, 1, depth, width), lambda i: (0, i, 0, 0))
    return pl.pallas_call(
        feed_kernel,
        grid=(levels,),
        in_specs=[
            whole_rows(rows, wide),
            by_level,
            by_level,
            pl.BlockSpec((groups, 1, 1, depth, width), lambda i: (0, i, 1, 0, 0)),
        ],
        out_specs=[grads_spec, whole_rows(rows, groups * depth)],
        out_shape=[
            jax.ShapeDtypeStruct((groups, levels, depth, width), jnp.bfloat16),
            jax.ShapeDtypeStruct((rows, groups * depth), jnp.bfloat16),
        ],
        scratch_shapes=[pltpu.VMEM((rows, groups * depth), jnp.float32)],
        compiler_params=pltpu.CompilerParams(vmem_limit_bytes=58 * 2**20),
        cost_estimate=cost(6 * rows * groups * depth * levels * width, 3e7),
        name="ffn_feed",
    )(hidden, grad_pre, active, weights)


def ffn_rear(rows_in, units, groups, levels):
    rows, wide = rows_in.shape
    width = units.shape[1] // levels
    depth = wide // groups
    return pl.pallas_call(
        rear_kernel,
        grid=(levels,),
        in_specs=[whole_rows(rows, wide), pl.BlockSpec((rows, width), lambda i: (0, i))],
        out_specs=pl.BlockSpec((groups, 1, depth, width), lambda i: (0, i, 0, 0)),
        out_shape=jax.ShapeDtypeStruct((groups, levels, depth, width), jnp.bfloat16),
        compiler_params=pltpu.CompilerParams(vmem_limit_bytes=58 * 2**20),
        cost_estimate=cost(4 * rows * groups * depth * levels * width, 3e7),
        name="ffn_rear",
    )(rows_in, units)


def chosen(routes, options):
    return jnp.sum(
        (routes[..., None] == jnp.arange(options, dtype=jnp.int32)).astype(jnp.float32), axis=-2
    )


def shift(value, axis, by):
    count = lax.axis_size(axis)
    pairs = [(i, i + by) for i in range(count) if 0 <= i + by < count]
    return lax.ppermute(value, axis, pairs)


def body(
    tokens_in,
    out_grad,
    deal_order,
    seq_lengths,
    value_routes,
    output_routes,
    ffn_routes,
    norm1_gain,
    norm1_bias,
    norm2_gain,
    norm2_bias,
    query_weight,
    key_weight,
    value_weight,
    output_weight,
    value_router,
    output_router,
    ffn_router,
    ffn_in,
    ffn_out,
):
    groups = lax.axis_size("group")
    levels = lax.axis_size("level")
    level = lax.axis_index("level")
    head = lax.axis_index("head")
    count, width = tokens_in.shape
    piece = count // (levels * HEADS)
    wrows = query_weight.shape[0]
    experts = ffn_router.shape[1]
    local_experts = ffn_in.shape[1] // FH

    small = jnp.concatenate(
        [
            ffn_router,
            norm1_gain[:, None],
            norm1_bias[:, None],
            norm2_gain[:, None],
            norm2_bias[:, None],
        ],
        axis=1,
    )
    shared = small.shape[1]
    pad = -(shared + 2 * VEXP) % 128
    packed = jnp.concatenate(
        [
            query_weight.reshape(wrows, HEADS, DH),
            key_weight.reshape(wrows, HEADS, DH),
            value_weight.reshape(wrows, HEADS, VEXP * DH),
            output_weight.reshape(wrows, HEADS, VEXP * DH),
            value_router.reshape(wrows, HEADS, VEXP),
            output_router.reshape(wrows, HEADS, VEXP),
            jnp.broadcast_to(small[:, None, :], (wrows, HEADS, shared)),
            jnp.zeros((wrows, HEADS, pad), jnp.bfloat16),
        ],
        axis=2,
    )
    cols = packed.shape[2]
    tables = jnp.concatenate(
        [value_routes.transpose(1, 2, 0), output_routes.transpose(1, 2, 0)], axis=1
    )
    picks = ffn_routes.reshape(levels, HEADS * piece, -1).transpose(0, 2, 1)
    arrived, full, tables, picks, orders = start(
        tokens_in.reshape(levels, HEADS, piece, width),
        packed.transpose(1, 0, 2),
        tables,
        picks,
        deal_order,
    )
    worker_in = arrived.reshape(HEADS * count, width)
    own_tokens = lax.dynamic_index_in_dim(arrived, head, 1, keepdims=False).reshape(count, width)
    full = full.reshape(width, cols)

    both = after(jnp.stack([ffn_in, ffn_out]), full)
    both = lax.all_gather(both, ("group", "level"), axis=0)
    both = both.reshape((groups, levels) + both.shape[1:])

    base = 2 * DH + 2 * VEXP * DH
    w_query = full[:, :DH]
    w_key = full[:, DH : 2 * DH]
    w_value = full[:, 2 * DH : 2 * DH + VEXP * DH]
    w_output = full[:, 2 * DH + VEXP * DH : base]
    r_value = full[:, base : base + VEXP]
    r_output = full[:, base + VEXP : base + 2 * VEXP]
    at = base + 2 * VEXP
    r_ffn = full[:, at : at + experts]
    gain_one, bias_one, gain_two, bias_two = (
        full[:, at + experts + i].astype(jnp.float32) for i in range(4)
    )

    own_grads = to_workers(after(out_grad, worker_in))

    ramp = jnp.arange(count, dtype=jnp.int32)
    rows = HEADS * count

    def arrival(values):
        lead, shape = values.shape[:-3], values.shape[-1:]
        four = values.reshape(lead + (HEADS, levels, HEADS, piece) + shape)
        return jnp.swapaxes(four, -4, -3).reshape(lead + (rows,) + shape)

    reach = -(-LMAX // rows)
    orders = orders.reshape(levels, HEADS, count)
    orders = jnp.concatenate([jnp.zeros((reach, HEADS, count), jnp.int32), orders], axis=0)
    orders = lax.dynamic_slice_in_dim(orders, level, reach + 1, 0)
    here = orders[:, :, None, :] == ramp[None, None, :, None]
    inverse = jnp.sum(here * ramp, axis=3)
    shard = (level - reach + jnp.arange(reach + 1, dtype=jnp.int32))[:, None] * HEADS
    shard = shard + jnp.arange(HEADS, dtype=jnp.int32)[None, :]
    pos_all = jnp.where(shard[:, :, None] < 0, -1, shard[:, :, None] * count + inverse)
    pos_all = arrival(pos_all[..., None]).reshape(-1)
    positions = pos_all[reach * rows :]
    options = jnp.arange(VEXP, dtype=jnp.int32)[None, :, None]

    def mask_of(which):
        one, two = tables[:, which, None, :], tables[:, which + 1, None, :]
        return (one == options).astype(jnp.bfloat16) + (two == options).astype(jnp.bfloat16)

    masks = jnp.concatenate([mask_of(0), mask_of(2)], axis=1)
    masks = jnp.einsum(
        "ktr,ker->kte", low(here[reach]), masks, preferred_element_type=jnp.float32
    )
    masks = arrival(masks)
    value_mask, out_mask = masks[:, :VEXP], masks[:, VEXP:]
    own_routes = picks.reshape(levels, -1, HEADS, piece).transpose(2, 0, 3, 1).reshape(count, -1)

    normed, scaled_one, inverse_one = layer_norm(worker_in.astype(jnp.float32), gain_one, bias_one)
    normed_one = low(normed)
    queries = low(matmul(normed_one, w_query))
    keys = low(matmul(normed_one, w_key))
    projected = matmul(worker_in, w_value).reshape(rows, VEXP, DH)
    value_sig = jax.nn.sigmoid(matmul(normed_one, r_value))
    value_gate = value_sig * value_mask
    values = low(jnp.sum(value_gate[..., None] * projected, axis=1))
    span = (reach + 1) * rows
    window = [jnp.concatenate([keys, values], axis=1)]
    for _ in range(reach):
        window.insert(0, shift(window[0], "level", 1))
    seq_ends = jnp.cumsum(seq_lengths[0])

    def starts_of(places):
        return jnp.max(jnp.where(seq_ends <= places[:, None], seq_ends, 0), axis=1)

    starts = starts_of(positions)
    blocks = rows // BLOCK
    base_block = (level - reach) * blocks
    first_block = starts_of(level * rows + jnp.arange(blocks, dtype=jnp.int32) * BLOCK) // BLOCK
    first_block = jnp.maximum(first_block - base_block, 0)

    def lines(values):
        return values.reshape(blocks, 1, BLOCK)

    attended, log_total = attend(
        first_block,
        queries,
        window,
        lines(positions),
        lines(starts),
        pos_all[:, None],
    )

    out_sig = jax.nn.sigmoid(matmul(normed_one, r_output))
    out_gate = out_sig * out_mask
    mixed = low((out_gate[..., None] * attended[:, None, :]).reshape(rows, VEXP * DH))
    branch = low(level_scatter(low(transposed(mixed, w_output)), 2))
    middle = own_tokens.astype(jnp.float32) + branch.astype(jnp.float32)

    normed_mid, scaled_two, inverse_two = layer_norm(middle, gain_two, bias_two)
    normed_two = low(normed_mid)
    ffn_sig = jax.nn.sigmoid(matmul(normed_two, r_ffn))
    member = chosen(own_routes, experts)
    shares = (ffn_sig * member).reshape(count, levels, HEADS, local_experts)
    shares = jnp.swapaxes(shares, 1, 2).reshape(count, experts)
    spare = -experts % 128
    extended = jnp.concatenate([middle, shares], axis=1)
    hidden = level_gather(jnp.pad(low(extended), ((0, 0), (0, spare))), 3, True)
    mine = levels * local_experts
    gates = lax.dynamic_slice_in_dim(hidden, width + head * mine, mine, 1).astype(jnp.float32)
    cotangent = level_gather(own_grads, 5, True)
    active, grad_pre, grad_rows = ffn_front(
        head[None], hidden, cotangent, both, gates, local_experts
    )
    summed, beyond = pair_scatter(grad_rows, 4, True)
    came = to_far(beyond)
    grad_in, feed = ffn_feed(after(hidden, beyond), grad_pre, active, both)
    summed = summed + after(came, feed).astype(jnp.float32)

    gate_grads = summed[:, width : width + experts].reshape(count, HEADS, levels, local_experts)
    gate_grads = jnp.swapaxes(gate_grads, 1, 2).reshape(count, experts)
    grad_logit = low(gate_grads * ffn_sig * (1.0 - ffn_sig) * member)
    grad_second = transposed(grad_logit, r_ffn)
    grad_r_ffn = contract_rows(normed_two, grad_logit)
    grad_gain_two = jnp.sum(grad_second * scaled_two, axis=0)
    grad_bias_two = jnp.sum(grad_second, axis=0)
    grad_middle = (
        own_grads.astype(jnp.float32)
        + summed[:, :width]
        + norm_back(grad_second, gain_two, scaled_two, inverse_two)
    )

    own_branch = low(grad_middle)
    came = to_far(own_branch)
    grad_out = ffn_rear(after(cotangent, own_branch), active, groups, levels)
    grad_branch = pair_gather(own_branch, after(came, grad_out), 7)
    grad_ffn = [
        lax.psum_scatter(
            g.reshape((groups * levels,) + g.shape[2:]), ("group", "level"), scatter_dimension=0
        ).astype(jnp.float32)
        for g in (grad_in, grad_out)
    ]
    grad_mixed = matmul(grad_branch, w_output).reshape(rows, VEXP, DH)
    grad_out_gate = jnp.sum(grad_mixed * attended[:, None, :], axis=-1)
    grad_attended = low(jnp.sum(grad_mixed * out_gate[..., None], axis=1))
    grad_out_logit = low(grad_out_gate * out_sig * (1.0 - out_sig) * out_mask)
    row_inner = jnp.sum(grad_attended.astype(jnp.float32) * attended, axis=-1)
    grad_queries, *grad_window = attend_back(
        first_block,
        queries,
        window,
        grad_attended,
        lines(positions),
        lines(starts),
        log_total,
        lines(row_inner),
        pos_all[:, None],
    )
    came = shift(grad_window[0], "level", -1)
    fed, beyond = pair_scatter(after(feed, grad_queries), 6, True)
    grad_w_output = contract_rows(after(grad_branch, fed), mixed)
    for i in range(1, reach + 1):
        grad_both = grad_window[i].astype(jnp.float32) + came.astype(jnp.float32)
        if i < reach:
            came = shift(low(grad_both), "level", -1)
    fed_far = to_far(after(beyond, grad_both))
    done = low(middle + fed + fed_far.astype(jnp.float32))
    grad_keys, grad_values = low(grad_both[:, :DH]), grad_both[:, DH:]
    grad_projected = low((value_gate[..., None] * grad_values[:, None, :]).reshape(rows, VEXP * DH))
    grad_value_gate = jnp.sum(grad_values[:, None, :] * projected, axis=-1)
    grad_value_logit = low(grad_value_gate * value_sig * (1.0 - value_sig) * value_mask)
    grad_first = (
        transposed(grad_queries, w_query)
        + transposed(grad_keys, w_key)
        + transposed(grad_value_logit, r_value)
        + transposed(grad_out_logit, r_output)
    )
    grad_inputs = norm_back(grad_first, gain_one, scaled_one, inverse_one) + transposed(
        grad_projected, w_value
    )
    weight_grads = jnp.concatenate(
        [
            low(grad_w_output),
            low(contract_rows(normed_one, grad_queries)),
            low(contract_rows(normed_one, grad_keys)),
            low(contract_rows(worker_in, grad_projected)),
            low(contract_rows(normed_one, grad_value_logit)),
            low(contract_rows(normed_one, grad_out_logit)),
            low(grad_r_ffn),
            low(grad_gain_two)[:, None],
            low(grad_bias_two)[:, None],
            low(jnp.sum(grad_first * scaled_one, axis=0))[:, None],
            low(jnp.sum(grad_first, axis=0))[:, None],
            jnp.zeros((width, pad), jnp.bfloat16),
        ],
        axis=1,
    )
    input_grad, layer_out, owned = finish(
        low(grad_inputs).reshape(HEADS, HEADS, levels * piece, width),
        grad_middle.reshape(HEADS, levels * piece, width),
        done.reshape(HEADS, levels, piece, width),
        weight_grads.reshape(groups, levels, HEADS, wrows, cols),
    )
    owned = owned.astype(jnp.float32)

    def columns(first, size):
        return owned[:, :, first : first + size].transpose(1, 0, 2).reshape(wrows, HEADS * size)

    at = VEXP * DH
    common = jnp.sum(owned[:, :, base + 2 * VEXP :], axis=0)
    return (
        layer_out.reshape(count, width),
        input_grad.reshape(count, width),
        common[:, experts + 2],
        common[:, experts + 3],
        common[:, experts],
        common[:, experts + 1],
        columns(at, DH),
        columns(at + DH, DH),
        columns(at + 2 * DH, VEXP * DH),
        columns(0, VEXP * DH),
        columns(base, VEXP),
        columns(base + VEXP, VEXP),
        common[:, :experts],
        grad_ffn[0],
        grad_ffn[1],
    )


def solution(mesh):
    groups, shards = mesh.devices.shape
    fine = Mesh(mesh.devices.reshape(groups, shards // HEADS, HEADS), TOK)
    two, one, three = P(TOK, None), P(TOK), P(TOK, None, None)
    ffn = P("group", ("level", "head"))
    return jax.shard_map(
        body,
        mesh=fine,
        in_specs=(two, two, two, P("group", None), three, three, two, one, one, one, one)
        + (two,) * 7
        + (ffn, ffn),
        out_specs=(two, two, one, one, one, one) + (two,) * 7 + (ffn, ffn),
        check_vma=False,
    )
```

```python
import functools

import jax
import jax.numpy as jnp
from jax import lax
from jax.experimental import pallas as pl
from jax.experimental.pallas import tpu as pltpu
from jax.sharding import Mesh, PartitionSpec as P

HEADS = 4
DH = 128
VEXP = 5
FH = 128
LMAX = 4096

TOK = ("group", "level", "head")


def matmul(left_side, right_side):
    return jnp.dot(left_side, right_side, preferred_element_type=jnp.float32)


def transposed(left_side, right_side):
    return lax.dot_general(
        left_side, right_side, (((1,), (1,)), ((), ())), preferred_element_type=jnp.float32
    )


def contract_rows(left_side, right_side):
    return lax.dot_general(
        left_side, right_side, (((0,), (0,)), ((), ())), preferred_element_type=jnp.float32
    )


def low(value):
    return value.astype(jnp.bfloat16)


def layer_norm(inputs, gain_vec, bias_vec):
    centred = inputs - jnp.mean(inputs, axis=-1, keepdims=True)
    inverse = lax.rsqrt(jnp.mean(centred * centred, axis=-1, keepdims=True) + 1e-05)
    scaled = centred * inverse
    return (scaled * gain_vec + bias_vec, scaled, inverse)


def norm_back(grad_normed, gain_vec, scaled, inverse):
    inner_grad = grad_normed * gain_vec
    return inverse * (
        inner_grad
        - jnp.mean(inner_grad, axis=-1, keepdims=True)
        - scaled * jnp.mean(inner_grad * scaled, axis=-1, keepdims=True)
    )


def to_workers(rows):
    levels = lax.axis_size("level")
    count = rows.shape[0]
    came = lax.all_to_all(
        rows.reshape(levels, count // levels, -1), "level", split_axis=0, concat_axis=0, tiled=True
    )
    came = came.reshape(levels, HEADS, count // levels // HEADS, -1)
    return came.transpose(1, 0, 2, 3).reshape(count, -1)


def to_home(rows):
    levels = lax.axis_size("level")
    count = rows.shape[0]
    out = rows.reshape(HEADS, levels, count // levels // HEADS, -1).transpose(1, 0, 2, 3)
    back = lax.all_to_all(
        out.reshape(levels, count // levels, -1), "level", split_axis=0, concat_axis=0, tiled=True
    )
    return back.reshape(count, -1)


MESH = pl.DeviceIdType.MESH


def partners(head):
    near = head + 1 - 2 * lax.rem(head, 2)
    far = lax.rem(head + 2, HEADS)
    return near, far


def greet(near, far):
    barrier = pltpu.get_barrier_semaphore()
    for peer in (near, far):
        pl.semaphore_signal(barrier, inc=1, device_id={"head": peer}, device_id_type=MESH)
    pl.semaphore_wait(barrier, 2)


def remote(src, dst, send, recv, peer):
    return pltpu.make_async_remote_copy(
        src_ref=src,
        dst_ref=dst,
        send_sem=send,
        recv_sem=recv,
        device_id={"head": peer},
        device_id_type=MESH,
    )


def cost(flops, moved):
    return pl.CostEstimate(flops=int(flops), bytes_accessed=int(moved), transcendentals=0)


def gather_kernel(
    by_source, own, out, local_sem, near_send, near_recv, far_send, far_recv, pass_send, pass_recv
):
    head = lax.axis_index("head")
    near, far = partners(head)
    greet(near, far)

    def spot(i, source):
        return out.at[source, i] if by_source else out.at[i, source]

    pieces = range(HEADS)
    to_far = [remote(own.at[i], spot(i, head), far_send.at[i], far_recv.at[i], far) for i in pieces]
    to_near = [
        remote(own.at[i], spot(i, head), near_send.at[i], near_recv.at[i], near) for i in pieces
    ]
    passed = [
        remote(spot(i, far), spot(i, far), pass_send.at[i], pass_recv.at[i], near) for i in pieces
    ]
    kept = [pltpu.make_async_copy(own.at[i], spot(i, head), local_sem.at[i]) for i in pieces]
    for copy in to_far + to_near + kept:
        copy.start()
    for i in pieces:
        to_far[i].wait_recv()
        passed[i].start()
    for i in pieces:
        to_near[i].wait_recv()
        passed[i].wait_recv()
        kept[i].wait()
        to_far[i].wait_send()
        to_near[i].wait_send()
        passed[i].wait_send()


def level_gather(rows, collective_id, by_source=False):
    count, width = rows.shape
    whole = pl.pallas_call(
        functools.partial(gather_kernel, by_source),
        out_shape=jax.ShapeDtypeStruct((HEADS, HEADS, count // HEADS, width), rows.dtype),
        in_specs=[pl.BlockSpec(memory_space=pltpu.VMEM)],
        out_specs=pl.BlockSpec(memory_space=pl.ANY),
        scratch_shapes=[pltpu.SemaphoreType.DMA((HEADS,))] * 7,
        compiler_params=pltpu.CompilerParams(collective_id=collective_id, has_side_effects=True),
        cost_estimate=cost(0, 90e6),
        name="level_gather",
    )(rows.reshape(HEADS, count // HEADS, width))
    return whole.reshape(HEADS * count, width)


def scatter_kernel(
    by_source, part, out, near_buf, send_buf, far_buf, near_send, near_recv, far_send, far_recv
):
    head = lax.axis_index("head")
    near, far = partners(head)
    greet(near, far)
    across = HEADS - 1 - head
    pieces = range(HEADS)

    def spot(i, dest):
        return (dest, i) if by_source else (i, dest)

    def to_near(slot, i, dest):
        return remote(
            part.at[spot(i, dest)],
            near_buf.at[slot, i],
            near_send.at[slot, i],
            near_recv.at[slot, i],
            near,
        )

    first = [to_near(0, i, across) for i in pieces]
    second = [to_near(1, i, near) for i in pieces]
    onward = [
        remote(send_buf.at[i], far_buf.at[i], far_send.at[i], far_recv.at[i], far) for i in pieces
    ]
    for copy in first + second:
        copy.start()
    for i in pieces:
        first[i].wait_recv()
        both = part[spot(i, far)].astype(jnp.float32) + near_buf[0, i].astype(jnp.float32)
        send_buf[i] = both.astype(jnp.bfloat16)
        onward[i].start()
    for i in pieces:
        second[i].wait_recv()
        out[i] = part[spot(i, head)].astype(jnp.float32) + near_buf[1, i].astype(jnp.float32)
    for i in pieces:
        onward[i].wait_recv()
        out[i] = out[i] + far_buf[i].astype(jnp.float32)
    for i in pieces:
        first[i].wait_send()
        second[i].wait_send()
        onward[i].wait_send()


def level_scatter(rows, collective_id, by_source=False):
    total, width = rows.shape
    piece = total // (HEADS * HEADS)
    low_type = jnp.bfloat16
    mine = pl.pallas_call(
        functools.partial(scatter_kernel, by_source),
        out_shape=jax.ShapeDtypeStruct((HEADS, piece, width), jnp.float32),
        in_specs=[pl.BlockSpec(memory_space=pltpu.VMEM)],
        out_specs=pl.BlockSpec(memory_space=pltpu.VMEM),
        scratch_shapes=[
            pltpu.VMEM((2, HEADS, piece, width), low_type),
            pltpu.VMEM((HEADS, piece, width), low_type),
            pltpu.VMEM((HEADS, piece, width), low_type),
            pltpu.SemaphoreType.DMA((2, HEADS)),
            pltpu.SemaphoreType.DMA((2, HEADS)),
            pltpu.SemaphoreType.DMA((HEADS,)),
            pltpu.SemaphoreType.DMA((HEADS,)),
        ],
        compiler_params=pltpu.CompilerParams(
            collective_id=collective_id, has_side_effects=True, vmem_limit_bytes=32 * 2**20
        ),
        cost_estimate=cost(0, 80e6),
        name="level_scatter",
    )(rows.reshape(HEADS, HEADS, piece, width))
    return mine.reshape(HEADS * piece, width)


def meet(near):
    barrier = pltpu.get_barrier_semaphore()
    pl.semaphore_signal(barrier, inc=1, device_id={"head": near}, device_id_type=MESH)
    pl.semaphore_wait(barrier, 1)


def pair_scatter_kernel(by_source, part, out, out_far, near_buf, send, recv):
    head = lax.axis_index("head")
    near, far = partners(head)
    meet(near)
    across = HEADS - 1 - head
    pieces = range(HEADS)

    def spot(i, dest):
        return (dest, i) if by_source else (i, dest)

    def to_near(slot, i, dest):
        return remote(
            part.at[spot(i, dest)], near_buf.at[slot, i], send.at[slot, i], recv.at[slot, i], near
        )

    first = [to_near(0, i, across) for i in pieces]
    second = [to_near(1, i, near) for i in pieces]
    for copy in first + second:
        copy.start()
    for i in pieces:
        first[i].wait_recv()
        both = part[spot(i, far)].astype(jnp.float32) + near_buf[0, i].astype(jnp.float32)
        out_far[i] = both.astype(jnp.bfloat16)
    for i in pieces:
        second[i].wait_recv()
        out[i] = part[spot(i, head)].astype(jnp.float32) + near_buf[1, i].astype(jnp.float32)
    for i in pieces:
        first[i].wait_send()
        second[i].wait_send()


def pair_scatter(rows, collective_id, by_source=False):
    total, width = rows.shape
    piece = total // (HEADS * HEADS)
    mine, other = pl.pallas_call(
        functools.partial(pair_scatter_kernel, by_source),
        out_shape=[
            jax.ShapeDtypeStruct((HEADS, piece, width), jnp.float32),
            jax.ShapeDtypeStruct((HEADS, piece, width), jnp.bfloat16),
        ],
        in_specs=[pl.BlockSpec(memory_space=pltpu.VMEM)],
        out_specs=[pl.BlockSpec(memory_space=pltpu.VMEM)] * 2,
        scratch_shapes=[
            pltpu.VMEM((2, HEADS, piece, width), jnp.bfloat16),
            pltpu.SemaphoreType.DMA((2, HEADS)),
            pltpu.SemaphoreType.DMA((2, HEADS)),
        ],
        compiler_params=pltpu.CompilerParams(
            collective_id=collective_id, has_side_effects=True, vmem_limit_bytes=32 * 2**20
        ),
        cost_estimate=cost(0, 25e6),
        name="pair_scatter",
    )(rows.reshape(HEADS, HEADS, piece, width))
    return mine.reshape(HEADS * piece, width), other.reshape(HEADS * piece, width)


def pair_gather_kernel(by_source, own, other, out, local_sem, send, recv):
    head = lax.axis_index("head")
    near, far = partners(head)
    meet(near)
    copies, kept = [], []
    for i in range(HEADS):
        for slot, (block, source) in enumerate(((own, head), (other, far))):
            place = out.at[source, i] if by_source else out.at[i, source]
            copies.append(
                remote(block.at[i], place, send.at[slot, i], recv.at[slot, i], near)
            )
            kept.append(pltpu.make_async_copy(block.at[i], place, local_sem.at[slot, i]))
    for copy in copies + kept:
        copy.start()
    for copy in copies + kept:
        copy.wait()


def pair_gather(own, other, collective_id, by_source=False):
    count, width = own.shape
    split = (HEADS, count // HEADS, width)
    whole = pl.pallas_call(
        functools.partial(pair_gather_kernel, by_source),
        out_shape=jax.ShapeDtypeStruct((HEADS,) + split, own.dtype),
        in_specs=[pl.BlockSpec(memory_space=pltpu.VMEM)] * 2,
        out_specs=pl.BlockSpec(memory_space=pl.ANY),
        scratch_shapes=[pltpu.SemaphoreType.DMA((2, HEADS))] * 3,
        compiler_params=pltpu.CompilerParams(collective_id=collective_id, has_side_effects=True),
        cost_estimate=cost(0, 25e6),
        name="pair_gather",
    )(own.reshape(split), other.reshape(split))
    return whole.reshape(HEADS * count, width)


def to_far(rows):
    return lax.ppermute(rows, "head", [(i, (i + 2) % HEADS) for i in range(HEADS)])


def after(value, *others):
    return lax.optimization_barrier((value,) + others)[0]


def ring(axis):
    me, size = lax.axis_index(axis), lax.axis_size(axis)
    ahead = [lax.rem(me + k, size) for k in range(1, size)]
    behind = [lax.rem(me + size - k, size) for k in range(1, size)]
    return me, ahead, behind


def reach_out(src, dst, send, recv, peer):
    return pltpu.make_async_remote_copy(
        src_ref=src, dst_ref=dst, send_sem=send, recv_sem=recv, device_id=peer, device_id_type=MESH
    )


def greet_all(peers):
    barrier = pltpu.get_barrier_semaphore()
    for peer in peers:
        pl.semaphore_signal(barrier, inc=1, device_id=peer, device_id_type=MESH)
    pl.semaphore_wait(barrier, len(peers))


def start_kernel(
    tokens, weights, tables, picks, order, rows, full, routes, chosen_rows, orders, own_sem, *sems
):
    sems = iter(sems)

    def pair():
        return next(sems), next(sems)

    group, groups_ahead, _ = ring("group")
    level, levels_ahead, levels_behind = ring("level")
    head = lax.axis_index("head")
    near, far = partners(head)
    mates = [near, far, HEADS - 1 - head]
    greet_all(
        [{"head": m} for m in mates]
        + [{"level": n} for n in levels_ahead]
        + [{"group": n} for n in groups_ahead]
    )
    started = []

    def send(src, dst, send_sem, recv_sem, peer):
        copy = reach_out(src, dst, send_sem, recv_sem, peer)
        copy.start()
        started.append(copy)
        return copy

    out_s, out_r = pair()
    pick_s, pick_r = pair()
    crossing, picking = [], []
    for k, to in enumerate(levels_ahead):
        peer = {"level": to}
        crossing.append(send(tokens.at[to], rows.at[:, head, level], out_s.at[k], out_r.at[k], peer))
    mate_s, mate_r = pair()
    table_s, table_r = pair()
    order_s, order_r = pair()
    to_mates, order_mates, table_mates = [], [], []
    for k, to in enumerate(mates):
        peer = {"head": to}
        to_mates.append(
            send(weights.at[to], full.at[group, level, head], mate_s.at[k], mate_r.at[k], peer)
        )
        order_mates.append(
            send(order, orders.at[level, head], order_s.at[k], order_r.at[k], peer)
        )
    own = [
        (tokens.at[level], rows.at[:, head, level]),
        (weights.at[head], full.at[group, level, head]),
        (tables.at[head], routes.at[head]),
        (picks.at[level], chosen_rows.at[level]),
        (order, orders.at[level, head]),
    ]
    own = [pltpu.make_async_copy(src, dst, own_sem.at[i]) for i, (src, dst) in enumerate(own)]
    for copy in own:
        copy.start()
    far_s, far_r = pair()
    near_s, near_r = pair()
    pass_s, pass_r = pair()
    to_far, to_near = [], []

    def share(k, src, source):
        place = rows.at[:, head, source]
        to_far.append(send(src, place, far_s.at[k], far_r.at[k], {"head": far}))
        to_near.append(send(src, place, near_s.at[k], near_r.at[k], {"head": near}))

    share(0, tokens.at[level], level)
    block_s, block_r = pair()
    group_s, group_r = pair()
    orders_s, orders_r = pair()
    for copy in to_mates:
        copy.wait_recv()
    own[1].wait()
    blocks, grouped, ordered = [], [], []

    def to_groups(j, source):
        for k, to in enumerate(groups_ahead):
            block = full.at[group, source]
            grouped.append(
                send(block, block, group_s.at[k, j], group_r.at[k, j], {"group": to})
            )

    for k, to in enumerate(levels_ahead):
        block = full.at[group, level]
        blocks.append(send(block, block, block_s.at[k], block_r.at[k], {"level": to}))
    to_groups(0, level)
    for k, to in enumerate(mates):
        table_mates.append(
            send(tables.at[to], routes.at[head], table_s.at[k], table_r.at[k], {"head": to})
        )
    for k, to in enumerate(levels_ahead):
        picking.append(
            send(picks.at[to], chosen_rows.at[level], pick_s.at[k], pick_r.at[k], {"level": to})
        )
    for copy in order_mates:
        copy.wait_recv()
    own[4].wait()
    for k, to in enumerate(levels_ahead):
        block = orders.at[level]
        ordered.append(send(block, block, orders_s.at[k], orders_r.at[k], {"level": to}))
    for k, source in enumerate(levels_behind):
        crossing[k].wait_recv()
        share(k + 1, rows.at[:, head, source], source)
    for k, source in enumerate(levels_behind):
        blocks[k].wait_recv()
        to_groups(k + 1, source)
    passed = []
    for k, source in enumerate([level] + levels_behind):
        to_far[k].wait_recv()
        place = rows.at[:, far, source]
        passed.append(send(place, place, pass_s.at[k], pass_r.at[k], {"head": near}))
    for copy in to_near + passed + grouped + table_mates + picking + ordered:
        copy.wait_recv()
    for copy in started:
        copy.wait_send()
    for i in (0, 2, 3):
        own[i].wait()


def start(tokens, weights, tables, picks, order):
    groups, levels = lax.axis_size("group"), lax.axis_size("level")
    _, _, piece, width = tokens.shape
    shapes = [
        jax.ShapeDtypeStruct((HEADS, HEADS, levels, piece, width), tokens.dtype),
        jax.ShapeDtypeStruct((groups, levels) + weights.shape, weights.dtype),
        jax.ShapeDtypeStruct(tables.shape, tables.dtype),
        jax.ShapeDtypeStruct(picks.shape, picks.dtype),
        jax.ShapeDtypeStruct((levels, HEADS) + order.shape, order.dtype),
    ]
    dma = pltpu.SemaphoreType.DMA
    others, mates = (levels - 1,), (HEADS - 1,)
    counts = [others] * 2 + [mates] * 3 + [(levels,)] * 3 + [others, (groups - 1, levels), others]
    return pl.pallas_call(
        start_kernel,
        out_shape=shapes,
        in_specs=[pl.BlockSpec(memory_space=pltpu.VMEM)] * 5,
        out_specs=[pl.BlockSpec(memory_space=pl.ANY)] * 5,
        scratch_shapes=[dma((5,))] + [dma(c) for c in counts for _ in range(2)],
        compiler_params=pltpu.CompilerParams(collective_id=9, has_side_effects=True),
        cost_estimate=cost(0, 200e6),
        name="start",
    )(tokens, weights, tables, picks, order)


def finish_kernel(
    part,
    middle,
    grads,
    home_grad,
    owned,
    near_buf,
    send_buf,
    far_buf,
    total,
    back_buf,
    came_buf,
    group_buf,
    level_send,
    level_buf,
    head_send,
    *sems,
):
    sems = iter(sems)

    def pair():
        return next(sems), next(sems)

    group, groups_ahead, _ = ring("group")
    level, levels_ahead, levels_behind = ring("level")
    head = lax.axis_index("head")
    near, far = partners(head)
    across = HEADS - 1 - head
    mates = [near, far, across]
    greet_all(
        [{"head": m} for m in mates]
        + [{"level": n} for n in levels_ahead]
        + [{"group": n} for n in groups_ahead]
    )
    started = []

    def send(src, dst, send_sem, recv_sem, peer):
        copy = reach_out(src, dst, send_sem, recv_sem, peer)
        copy.start()
        started.append(copy)
        return copy

    pieces = range(HEADS)
    near_s, near_r = pair()
    far_s, far_r = pair()
    group_s, group_r = pair()
    back_s, back_r = pair()
    level_s, level_r = pair()
    mate_s, mate_r = pair()
    first, second, onward = [], [], []
    for slot, (dest, copies) in enumerate(((across, first), (near, second))):
        for i in pieces:
            copies.append(
                send(
                    part.at[i, dest],
                    near_buf.at[slot, i],
                    near_s.at[slot, i],
                    near_r.at[slot, i],
                    {"head": near},
                )
            )
    order = levels_ahead + [level]
    grouped = []
    for j, dest in enumerate(order):
        grouped.append(
            [
                send(
                    grads.at[to, dest],
                    group_buf.at[k, j],
                    group_s.at[k, j],
                    group_r.at[k, j],
                    {"group": to},
                )
                for k, to in enumerate(groups_ahead)
            ]
        )
    for i in pieces:
        first[i].wait_recv()
        both = part[i, far].astype(jnp.float32) + near_buf[0, i].astype(jnp.float32)
        send_buf[i] = both.astype(jnp.bfloat16)
        onward.append(send(send_buf.at[i], far_buf.at[i], far_s.at[i], far_r.at[i], {"head": far}))
    for i in pieces:
        second[i].wait_recv()
        both = part[i, head].astype(jnp.float32) + near_buf[1, i].astype(jnp.float32)
        total[i] = both + middle[i]
    leveled = []
    for j, dest in enumerate(order):
        amount = grads[group, dest].astype(jnp.float32)
        for k, copy in enumerate(grouped[j]):
            copy.wait_recv()
            amount = amount + group_buf[k, j].astype(jnp.float32)
        level_send[j] = amount.astype(jnp.bfloat16)
        if j < len(levels_ahead):
            leveled.append(
                send(level_send.at[j], level_buf.at[j], level_s.at[j], level_r.at[j], {"level": dest})
            )
    for i in pieces:
        onward[i].wait_recv()
        both = total[i] + far_buf[i].astype(jnp.float32)
        back_buf[i] = both.astype(jnp.bfloat16).reshape(back_buf.shape[1:])
    backs = [
        send(back_buf.at[:, to], came_buf.at[level], back_s.at[k], back_r.at[k], {"level": to})
        for k, to in enumerate(levels_ahead)
    ]
    amount = level_send[len(levels_ahead)].astype(jnp.float32)
    for j, copy in enumerate(leveled):
        copy.wait_recv()
        amount = amount + level_buf[j].astype(jnp.float32)
    head_send[...] = amount.astype(jnp.bfloat16)
    sharing = [
        send(head_send.at[to], owned.at[head], mate_s.at[k], mate_r.at[k], {"head": to})
        for k, to in enumerate(mates)
    ]
    owned[head] = head_send[head]
    home_grad[level] = back_buf[:, level].astype(jnp.float32)
    for k, source in enumerate(levels_behind):
        backs[k].wait_recv()
        home_grad[source] = came_buf[source].astype(jnp.float32)
    for copy in sharing:
        copy.wait_recv()
    for copy in started:
        copy.wait_send()


def finish(part, middle, grads):
    groups, levels = lax.axis_size("group"), lax.axis_size("level")
    _, count, width = middle.shape
    piece = count // levels
    low_type = jnp.bfloat16
    block = grads.shape[2:]
    dma = pltpu.SemaphoreType.DMA
    others = (levels - 1,)
    counts = [(2, HEADS), (HEADS,), (groups - 1, levels), others, others, (HEADS - 1,)]
    vmem = pl.BlockSpec(memory_space=pltpu.VMEM)
    return pl.pallas_call(
        finish_kernel,
        out_shape=[
            jax.ShapeDtypeStruct((levels, HEADS, piece, width), jnp.float32),
            jax.ShapeDtypeStruct(block, low_type),
        ],
        in_specs=[vmem] * 3,
        out_specs=[vmem] * 2,
        scratch_shapes=[
            pltpu.VMEM((2, HEADS, count, width), low_type),
            pltpu.VMEM((HEADS, count, width), low_type),
            pltpu.VMEM((HEADS, count, width), low_type),
            pltpu.VMEM((HEADS, count, width), jnp.float32),
            pltpu.VMEM((HEADS, levels, piece, width), low_type),
            pltpu.VMEM((levels, HEADS, piece, width), low_type),
            pltpu.VMEM((groups - 1, levels) + block, low_type),
            pltpu.VMEM((levels,) + block, low_type),
            pltpu.VMEM((levels - 1,) + block, low_type),
            pltpu.VMEM(block, low_type),
        ]
        + [dma(c) for c in counts for _ in range(2)],
        compiler_params=pltpu.CompilerParams(
            collective_id=10, has_side_effects=True, vmem_limit_bytes=56 * 2**20
        ),
        cost_estimate=cost(0, 200e6),
        name="finish",
    )(part, middle, grads)


BLOCK = 512
LOG2E = 1.4426950408889634


def dot(left_side, right_side, left_dim, right_dim):
    return lax.dot_general(
        left_side,
        right_side,
        (((left_dim,), (right_dim,)), ((), ())),
        preferred_element_type=jnp.float32,
    )


def attend_kernel(parts, first, q, *refs):
    keys, values = refs[:parts], refs[parts : 2 * parts]
    pos_q, start_q, pos_k, out, lse, top, total, acc = refs[2 * parts :]
    at = pl.program_id(0)
    blocks = pl.num_programs(0)
    rate = LOG2E * DH ** (-0.5)
    top[...] = jnp.full_like(top, -1e30)
    total[...] = jnp.zeros_like(total)
    acc[...] = jnp.zeros_like(acc)
    query = q[...]
    row_at, row_from = pos_q[0], start_q[0]

    for part in range(parts):

        def step(block, carry, k=keys[part], v=values[part], part=part):
            rows = pl.ds(pl.multiple_of(block * BLOCK, BLOCK), BLOCK)
            spot = pl.ds(pl.multiple_of((part * blocks + block) * BLOCK, BLOCK), BLOCK)
            scores = dot(k[rows, :], query, 1, 1)
            key_at = pos_k[spot, :]
            scores = jnp.where((key_at >= row_from) & (key_at <= row_at), scores, -1e30)
            old = top[...]
            new = jnp.maximum(old, jnp.max(scores, axis=0, keepdims=True))
            shrink = jnp.exp2((old - new) * rate)
            weight = jnp.exp2((scores - new) * rate)
            total[...] = total[...] * shrink + jnp.sum(weight, axis=0, keepdims=True)
            acc[...] = acc[...] * shrink + dot(v[rows, :], weight.astype(jnp.bfloat16), 0, 0)
            top[...] = new
            return carry

        begin = jnp.maximum(first[at] - part * blocks, 0)
        end = at + 1 if part == parts - 1 else blocks
        lax.fori_loop(begin, end, step, 0)
    out[...] = (acc[...] / total[...]).T
    lse[0] = top[...] * rate + jnp.log2(total[...])


def attend(first, queries, window, pos_q, start_q, pos_k):
    rows = queries.shape[0]
    parts = len(window)
    line = pl.BlockSpec((1, 1, BLOCK), lambda i, *_: (i, 0, 0))
    grid_spec = pltpu.PrefetchScalarGridSpec(
        num_scalar_prefetch=1,
        grid=(rows // BLOCK,),
        in_specs=[pl.BlockSpec((BLOCK, DH), lambda i, *_: (i, 0))]
        + [pl.BlockSpec((rows, DH), lambda i, *_: (0, 0))] * parts
        + [pl.BlockSpec((rows, DH), lambda i, *_: (0, 1))] * parts
        + [line, line, pl.BlockSpec((parts * rows, 1), lambda i, *_: (0, 0))],
        out_specs=[pl.BlockSpec((BLOCK, DH), lambda i, *_: (i, 0)), line],
        scratch_shapes=[
            pltpu.VMEM((1, BLOCK), jnp.float32),
            pltpu.VMEM((1, BLOCK), jnp.float32),
            pltpu.VMEM((DH, BLOCK), jnp.float32),
        ],
    )
    return pl.pallas_call(
        functools.partial(attend_kernel, parts),
        grid_spec=grid_spec,
        out_shape=[
            jax.ShapeDtypeStruct((rows, DH), jnp.float32),
            jax.ShapeDtypeStruct((rows // BLOCK, 1, BLOCK), jnp.float32),
        ],
        compiler_params=pltpu.CompilerParams(vmem_limit_bytes=48 * 2**20),
        cost_estimate=cost(2e10, 1e7),
        name="attend",
    )(first, queries, *window, *window, pos_q, start_q, pos_k)


def attend_back_kernel(parts, first, q, *refs):
    keys, values = refs[:parts], refs[parts : 2 * parts]
    grad, pos_q, start_q, lse, inner, pos_k, grad_q = refs[2 * parts : 2 * parts + 7]
    grads = refs[2 * parts + 7 : 3 * parts + 7]
    sum_k, sum_v, acc = refs[3 * parts + 7 :]
    at = pl.program_id(0)
    blocks = pl.num_programs(0)
    rate = LOG2E * DH ** (-0.5)
    scale = DH ** (-0.5)

    @pl.when(at == 0)
    def _():
        sum_k[...] = jnp.zeros_like(sum_k)
        sum_v[...] = jnp.zeros_like(sum_v)

    acc[...] = jnp.zeros_like(acc)
    query, grad_out = q[...], grad[...]
    row_at, row_from, row_lse, row_inner = pos_q[0], start_q[0], lse[0], inner[0]

    for part in range(parts):

        def step(block, carry, k=keys[part], v=values[part], part=part):
            rows = pl.ds(pl.multiple_of(block * BLOCK, BLOCK), BLOCK)
            spot = pl.ds(pl.multiple_of((part * blocks + block) * BLOCK, BLOCK), BLOCK)
            key, value = k[rows, :], v[rows, :]
            scores = dot(key, query, 1, 1)
            key_at = pos_k[spot, :]
            seen = (key_at >= row_from) & (key_at <= row_at)
            soft = jnp.where(seen, jnp.exp2(scores * rate - row_lse), 0.0)
            grad_soft = dot(value, grad_out, 1, 1)
            grad_scores = (soft * (grad_soft - row_inner)).astype(jnp.bfloat16)
            sum_v[spot, :] += dot(soft.astype(jnp.bfloat16), grad_out, 1, 0)
            sum_k[spot, :] += dot(grad_scores, query, 1, 0)
            acc[...] += dot(grad_scores, key, 0, 0)
            return carry

        begin = jnp.maximum(first[at] - part * blocks, 0)
        end = at + 1 if part == parts - 1 else blocks
        lax.fori_loop(begin, end, step, 0)
    grad_q[...] = (acc[...] * scale).astype(jnp.bfloat16)

    @pl.when(at == blocks - 1)
    def _():
        size = grads[0].shape[0]
        for part in range(parts):
            spot = slice(part * size, (part + 1) * size)
            grads[part][:, :DH] = (sum_k[spot, :] * scale).astype(grads[part].dtype)
            grads[part][:, DH:] = sum_v[spot, :].astype(grads[part].dtype)


def attend_back(first, queries, window, grads, pos_q, start_q, lse, inner, pos_k):
    rows = queries.shape[0]
    parts = len(window)
    block = pl.BlockSpec((BLOCK, DH), lambda i, *_: (i, 0))
    line = pl.BlockSpec((1, 1, BLOCK), lambda i, *_: (i, 0, 0))
    grid_spec = pltpu.PrefetchScalarGridSpec(
        num_scalar_prefetch=1,
        grid=(rows // BLOCK,),
        in_specs=[block]
        + [pl.BlockSpec((rows, DH), lambda i, *_: (0, 0))] * parts
        + [pl.BlockSpec((rows, DH), lambda i, *_: (0, 1))] * parts
        + [block, line, line, line, line]
        + [pl.BlockSpec((parts * rows, 1), lambda i, *_: (0, 0))],
        out_specs=[block] + [pl.BlockSpec((rows, 2 * DH), lambda i, *_: (0, 0))] * parts,
        scratch_shapes=[
            pltpu.VMEM((parts * rows, DH), jnp.float32),
            pltpu.VMEM((parts * rows, DH), jnp.float32),
            pltpu.VMEM((BLOCK, DH), jnp.float32),
        ],
    )
    kinds = [jnp.bfloat16] * (parts - 1) + [jnp.float32]
    return pl.pallas_call(
        functools.partial(attend_back_kernel, parts),
        grid_spec=grid_spec,
        out_shape=[jax.ShapeDtypeStruct((rows, DH), jnp.bfloat16)]
        + [jax.ShapeDtypeStruct((rows, 2 * DH), kind) for kind in kinds],
        compiler_params=pltpu.CompilerParams(vmem_limit_bytes=48 * 2**20),
        cost_estimate=cost(2e10, 1e7),
        name="attend_back",
    )(first, queries, *window, *window, grads, pos_q, start_q, lse, inner, pos_k)


def front_kernel(
    local, head, hidden, grads, w_in, w_out, gates, active, grad_pre, rows_out, acc
):
    groups, levels, depth, width = w_in.shape
    tile = hidden.shape[0]
    model = groups * depth
    acc[...] = jnp.zeros_like(acc)
    gate_grads = []
    for level in range(levels):
        pre_act = jnp.zeros((tile, width), jnp.float32)
        grad_active = jnp.zeros((tile, width), jnp.float32)
        for group in range(groups):
            part = slice(group * depth, (group + 1) * depth)
            pre_act += dot(hidden[:, part], w_in[group, level], 1, 0)
            grad_active += dot(grads[:, part], w_out[group, level], 1, 0)
        first = level * local
        gate = jnp.concatenate(
            [jnp.broadcast_to(gates[:, first + e : first + e + 1], (tile, FH)) for e in range(local)],
            axis=1,
        )
        sig = 1.0 / (1.0 + jnp.exp2(-LOG2E * pre_act))
        act_pre = pre_act * sig
        columns = slice(level * width, (level + 1) * width)
        active[:, columns] = (act_pre * gate).astype(jnp.bfloat16)
        product = grad_active * act_pre
        for e in range(local):
            gate_grads.append(
                jnp.sum(product[:, e * FH : (e + 1) * FH], axis=1, keepdims=True)
            )
        slope = sig * (1.0 + pre_act * (1.0 - sig))
        low_pre = (grad_active * gate * slope).astype(jnp.bfloat16)
        grad_pre[:, columns] = low_pre
        for group in range(groups):
            part = slice(group * depth, (group + 1) * depth)
            acc[:, part] += dot(low_pre, w_in[group, level], 1, 1)
    rows_out[:, :model] = acc[...].astype(jnp.bfloat16)
    spare = rows_out.shape[1] - model
    lane = lax.broadcasted_iota(jnp.int32, (tile, spare), 1) - head[0] * (levels * local)
    spread = jnp.zeros((tile, spare), jnp.float32)
    for e, column in enumerate(gate_grads):
        spread = jnp.where(lane == e, column, spread)
    rows_out[:, model:] = spread.astype(jnp.bfloat16)


def ffn_front(head, hidden, grads, w_in, w_out, gates, local):
    rows, wide = hidden.shape
    groups, levels, depth, width = w_in.shape
    tile = 512

    def by_row(columns):
        return pl.BlockSpec((tile, columns), lambda i, *_: (i, 0))

    whole = pl.BlockSpec(w_in.shape, lambda i, *_: (0, 0, 0, 0), pipeline_mode=pl.Buffered(1))
    grid_spec = pltpu.PrefetchScalarGridSpec(
        num_scalar_prefetch=1,
        grid=(rows // tile,),
        in_specs=[
            by_row(wide),
            by_row(groups * depth),
            whole,
            whole,
            by_row(gates.shape[1]),
        ],
        out_specs=[by_row(levels * width), by_row(levels * width), by_row(wide)],
        scratch_shapes=[pltpu.VMEM((tile, groups * depth), jnp.float32)],
    )
    hidden_units = jax.ShapeDtypeStruct((rows, levels * width), jnp.bfloat16)
    return pl.pallas_call(
        functools.partial(front_kernel, local),
        grid_spec=grid_spec,
        out_shape=[hidden_units, hidden_units, jax.ShapeDtypeStruct((rows, wide), jnp.bfloat16)],
        compiler_params=pltpu.CompilerParams(vmem_limit_bytes=58 * 2**20),
        cost_estimate=cost(6 * rows * groups * depth * levels * width, 3e7),
        name="ffn_front",
    )(head, hidden, grads, w_in, w_out, gates)


def rear_kernel(rows_in, hidden_units, weight_grads):
    groups, _, depth, _ = weight_grads.shape
    units = hidden_units[...]
    for group in range(groups):
        part = slice(group * depth, (group + 1) * depth)
        weight_grads[group, 0] = dot(rows_in[:, part], units, 0, 0).astype(jnp.bfloat16)


def normalized(rows, gain, bias):
    values = rows.astype(jnp.float32)
    centred = values - jnp.mean(values, axis=1, keepdims=True)
    inverse = lax.rsqrt(jnp.mean(centred * centred, axis=1, keepdims=True) + 1e-05)
    scaled = centred * inverse
    return scaled, inverse, (scaled * gain + bias).astype(jnp.bfloat16)


def project_kernel(
    levels, rows, w_value, w_query, w_key, routers, gain, bias, order, tables,
    query, key_value, projected, sigs, masks,
):
    count = rows.shape[0]
    piece = count // (levels * HEADS)
    _, _, normed = normalized(rows[...], gain[...], bias[...])
    query[...] = dot(normed, w_query[...], 1, 0).astype(jnp.bfloat16)
    key_value[:, :DH] = dot(normed, w_key[...], 1, 0).astype(jnp.bfloat16)
    sig = 1.0 / (1.0 + jnp.exp2(-LOG2E * dot(normed, routers[...], 1, 0)))
    sigs[...] = sig
    product = dot(rows[...], w_value[...], 1, 0)
    projected[...] = product
    at = lax.broadcasted_iota(jnp.int32, (count, count), 0)
    source = lax.rem(at // piece, levels) * HEADS + at // (piece * levels)
    here = (source * piece + lax.rem(at, piece) == order[0]).astype(jnp.bfloat16)
    lane = lax.broadcasted_iota(jnp.int32, (16, count), 0)
    table = tables[0]
    named = jnp.zeros((16, count), jnp.float32)
    for which in range(2):
        option = lane - which * VEXP
        for slot in range(2):
            pick = table[2 * which + slot : 2 * which + slot + 1, :]
            hit = (option == pick) & (option >= 0) & (option < VEXP)
            named = jnp.where(hit, 1.0, named)
    mask = dot(here, named.astype(jnp.bfloat16), 1, 1)
    masks[...] = mask
    value = jnp.zeros((count, DH), jnp.float32)
    for e in range(VEXP):
        gate = sig[:, e : e + 1] * mask[:, e : e + 1]
        value += gate * product[:, e * DH : (e + 1) * DH]
    key_value[:, DH:] = value.astype(jnp.bfloat16)


def project(rows, full, gain, bias, orders, tables, levels):
    total, width = rows.shape
    count = total // HEADS

    def by_row(columns):
        return pl.BlockSpec((count, columns), lambda i: (i, 0))

    def column(size, at):
        return pl.BlockSpec((width, size), lambda i: (0, at), pipeline_mode=pl.Buffered(1))

    line = pl.BlockSpec((1, width), lambda i: (0, 0))
    shapes = [(DH, jnp.bfloat16), (2 * DH, jnp.bfloat16), (VEXP * DH, jnp.float32)]
    shapes += [(128, jnp.float32), (16, jnp.float32)]
    return pl.pallas_call(
        functools.partial(project_kernel, levels),
        grid=(HEADS,),
        in_specs=[by_row(width), column(VEXP * DH, 0)]
        + [column(DH, 2 * VEXP + i) for i in range(3)]
        + [line, line]
        + [
            pl.BlockSpec((1, 1, count), lambda i: (i, 0, 0)),
            pl.BlockSpec((1,) + tables.shape[1:], lambda i: (i, 0, 0)),
        ],
        out_specs=[by_row(columns) for columns, _ in shapes],
        out_shape=[jax.ShapeDtypeStruct((total, columns), kind) for columns, kind in shapes],
        compiler_params=pltpu.CompilerParams(vmem_limit_bytes=48 * 2**20),
        cost_estimate=cost(2 * total * width * 1024, 2e7),
        name="project",
    )(rows, full, full, full, full, gain, bias, orders, tables)


def project_back_kernel(
    rows, grads, grad_query, out_logit, projected, sigs, masks,
    w_value, w_query, w_key, routers, gain, bias,
    grad_rows, weight_grads, acc, sums,
):
    at = pl.program_id(0)
    count = rows.shape[0]
    values = VEXP * DH

    @pl.when(at == 0)
    def _():
        acc[...] = jnp.zeros_like(acc)
        sums[...] = jnp.zeros_like(sums)

    scaled, inverse, normed = normalized(rows[...], gain[...], bias[...])
    grad_key = grads[:, :DH].astype(jnp.bfloat16)
    grad_value = grads[:, DH:]
    sig, mask = sigs[...], masks[...]
    lane = lax.broadcasted_iota(jnp.int32, (count, 128), 1)
    logits = out_logit[...].astype(jnp.float32)
    parts = []
    for e in range(VEXP):
        one, on = sig[:, e : e + 1], mask[:, e : e + 1]
        parts.append((one * on * grad_value).astype(jnp.bfloat16))
        inner = jnp.sum(grad_value * projected[:, e * DH : (e + 1) * DH], axis=1, keepdims=True)
        logits = jnp.where(lane == e, inner * one * (1.0 - one) * on, logits)
    grad_projected = jnp.concatenate(parts, axis=1)
    sides = jnp.concatenate([grad_query[...], grad_key, logits.astype(jnp.bfloat16)], axis=1)
    first = dot(sides[:, :DH], w_query[...], 1, 1)
    first += dot(sides[:, DH : 2 * DH], w_key[...], 1, 1)
    first += dot(sides[:, 2 * DH :], routers[...], 1, 1)
    sums[2 * VEXP : 2 * VEXP + 1, :] += jnp.sum(first * scaled, axis=0, keepdims=True)
    sums[2 * VEXP + 1 : 2 * VEXP + 2, :] += jnp.sum(first, axis=0, keepdims=True)
    inner_grad = first * gain[...]
    inner_grad = inverse * (
        inner_grad
        - jnp.mean(inner_grad, axis=1, keepdims=True)
        - scaled * jnp.mean(inner_grad * scaled, axis=1, keepdims=True)
    )
    grad_rows[...] = (inner_grad + dot(grad_projected, w_value[...], 1, 1)).astype(jnp.bfloat16)
    acc[:, :values] += dot(rows[...], grad_projected, 0, 0)
    acc[:, values:] += dot(normed, sides, 0, 0)

    @pl.when(at == pl.num_programs(0) - 1)
    def _():
        weight_grads[:, : values + 2 * DH] = acc[:, : values + 2 * DH].astype(jnp.bfloat16)
        last = acc[:, values + 2 * DH :] + sums[...].T
        weight_grads[:, values + 2 * DH :] = last.astype(jnp.bfloat16)


def project_back(rows, grads, grad_query, out_logit, projected, sigs, masks, full, gain, bias):
    total, width = rows.shape
    count = total // HEADS
    columns = VEXP * DH + 3 * DH

    def by_row(size):
        return pl.BlockSpec((count, size), lambda i: (i, 0))

    def column(size, at):
        return pl.BlockSpec((width, size), lambda i: (0, at), pipeline_mode=pl.Buffered(1))

    line = pl.BlockSpec((1, width), lambda i: (0, 0))
    return pl.pallas_call(
        project_back_kernel,
        grid=(HEADS,),
        in_specs=[by_row(width), by_row(2 * DH), by_row(DH), by_row(128), by_row(VEXP * DH)]
        + [by_row(128), by_row(16), column(VEXP * DH, 0)]
        + [column(DH, 2 * VEXP + i) for i in range(3)]
        + [line, line],
        out_specs=[by_row(width), pl.BlockSpec((width, columns), lambda i: (0, 0))],
        out_shape=[
            jax.ShapeDtypeStruct((total, width), jnp.bfloat16),
            jax.ShapeDtypeStruct((width, columns), jnp.bfloat16),
        ],
        scratch_shapes=[
            pltpu.VMEM((width, columns), jnp.float32),
            pltpu.VMEM((128, width), jnp.float32),
        ],
        compiler_params=pltpu.CompilerParams(vmem_limit_bytes=56 * 2**20),
        cost_estimate=cost(4 * total * width * 1024, 4e7),
        name="project_back",
    )(rows, grads, grad_query, out_logit, projected, sigs, masks, full, full, full, full, gain, bias)


def feed_kernel(rows_in, low_pre, active, w_out, weight_grads, feed, acc):
    groups, _, depth, _ = w_out.shape
    level = pl.program_id(0)
    units, act = low_pre[...], active[...]
    for group in range(groups):
        part = slice(group * depth, (group + 1) * depth)
        weight_grads[group, 0] = dot(rows_in[:, part], units, 0, 0).astype(jnp.bfloat16)
        fed = dot(act, w_out[group, 0], 1, 1)

        @pl.when(level == 0)
        def _():
            acc[:, part] = fed

        @pl.when(level > 0)
        def _():
            acc[:, part] += fed

    @pl.when(level == pl.num_programs(0) - 1)
    def _():
        feed[...] = acc[...].astype(jnp.bfloat16)


def whole_rows(rows, columns):
    return pl.BlockSpec((rows, columns), lambda i: (0, 0), pipeline_mode=pl.Buffered(1))


def ffn_feed(hidden, grad_pre, active, w_out):
    rows, wide = hidden.shape
    groups, levels, depth, width = w_out.shape
    by_level = pl.BlockSpec((rows, width), lambda i: (0, i))
    grads_spec = pl.BlockSpec((groups, 1, depth, width), lambda i: (0, i, 0, 0))
    return pl.pallas_call(
        feed_kernel,
        grid=(levels,),
        in_specs=[
            whole_rows(rows, wide),
            by_level,
            by_level,
            grads_spec,
        ],
        out_specs=[grads_spec, whole_rows(rows, groups * depth)],
        out_shape=[
            jax.ShapeDtypeStruct((groups, levels, depth, width), jnp.bfloat16),
            jax.ShapeDtypeStruct((rows, groups * depth), jnp.bfloat16),
        ],
        scratch_shapes=[pltpu.VMEM((rows, groups * depth), jnp.float32)],
        compiler_params=pltpu.CompilerParams(vmem_limit_bytes=58 * 2**20),
        cost_estimate=cost(6 * rows * groups * depth * levels * width, 3e7),
        name="ffn_feed",
    )(hidden, grad_pre, active, w_out)


def ffn_rear(rows_in, units, groups, levels):
    rows, wide = rows_in.shape
    width = units.shape[1] // levels
    depth = wide // groups
    return pl.pallas_call(
        rear_kernel,
        grid=(levels,),
        in_specs=[whole_rows(rows, wide), pl.BlockSpec((rows, width), lambda i: (0, i))],
        out_specs=pl.BlockSpec((groups, 1, depth, width), lambda i: (0, i, 0, 0)),
        out_shape=jax.ShapeDtypeStruct((groups, levels, depth, width), jnp.bfloat16),
        compiler_params=pltpu.CompilerParams(vmem_limit_bytes=58 * 2**20),
        cost_estimate=cost(4 * rows * groups * depth * levels * width, 3e7),
        name="ffn_rear",
    )(rows_in, units)


def chosen(routes, options):
    return jnp.sum(
        (routes[..., None] == jnp.arange(options, dtype=jnp.int32)).astype(jnp.float32), axis=-2
    )


def shift(value, axis, by):
    count = lax.axis_size(axis)
    pairs = [(i, i + by) for i in range(count) if 0 <= i + by < count]
    return lax.ppermute(value, axis, pairs)


def body(
    tokens_in,
    out_grad,
    deal_order,
    seq_lengths,
    value_routes,
    output_routes,
    ffn_routes,
    norm1_gain,
    norm1_bias,
    norm2_gain,
    norm2_bias,
    query_weight,
    key_weight,
    value_weight,
    output_weight,
    value_router,
    output_router,
    ffn_router,
    ffn_in,
    ffn_out,
):
    groups = lax.axis_size("group")
    levels = lax.axis_size("level")
    level = lax.axis_index("level")
    head = lax.axis_index("head")
    count, width = tokens_in.shape
    piece = count // (levels * HEADS)
    wrows = query_weight.shape[0]
    experts = ffn_router.shape[1]
    local_experts = ffn_in.shape[1] // FH

    small = jnp.concatenate(
        [
            ffn_router,
            norm1_gain[:, None],
            norm1_bias[:, None],
            norm2_gain[:, None],
            norm2_bias[:, None],
        ],
        axis=1,
    )
    shared = small.shape[1]
    pad = -(shared + 2 * VEXP) % 128
    packed = jnp.concatenate(
        [
            value_weight.reshape(wrows, HEADS, VEXP * DH),
            output_weight.reshape(wrows, HEADS, VEXP * DH),
            query_weight.reshape(wrows, HEADS, DH),
            key_weight.reshape(wrows, HEADS, DH),
            value_router.reshape(wrows, HEADS, VEXP),
            output_router.reshape(wrows, HEADS, VEXP),
            jnp.broadcast_to(small[:, None, :], (wrows, HEADS, shared)),
            jnp.zeros((wrows, HEADS, pad), jnp.bfloat16),
        ],
        axis=2,
    )
    cols = packed.shape[2]
    tables = jnp.concatenate(
        [value_routes.transpose(1, 2, 0), output_routes.transpose(1, 2, 0)], axis=1
    )
    picks = ffn_routes.reshape(levels, HEADS * piece, -1).transpose(0, 2, 1)
    arrived, full, tables, picks, orders = start(
        tokens_in.reshape(levels, HEADS, piece, width),
        packed.transpose(1, 0, 2),
        tables,
        picks,
        deal_order,
    )
    worker_in = arrived.reshape(HEADS * count, width)
    own_tokens = lax.dynamic_index_in_dim(arrived, head, 1, keepdims=False).reshape(count, width)
    full = full.reshape(width, cols)

    base = 2 * DH + 2 * VEXP * DH
    w_output = full[:, VEXP * DH : 2 * VEXP * DH]
    at = base + 2 * VEXP
    r_ffn = full[:, at : at + experts]
    gain_one, bias_one, gain_two, bias_two = (
        full[:, at + experts + i].astype(jnp.float32) for i in range(4)
    )
    gain_row, bias_row = gain_one[None], bias_one[None]
    orders = orders.reshape(levels, HEADS, count)
    own_order = lax.dynamic_index_in_dim(orders, level, 0, keepdims=False)[:, None, :]
    queries, key_value, projected, sigs, masks = project(
        worker_in, full, gain_row, bias_row, own_order, tables, levels
    )

    rows = HEADS * count
    reach = -(-LMAX // rows)
    window = [key_value]
    for _ in range(reach):
        window.insert(0, shift(window[0], "level", 1))
    own_grads = to_workers(after(out_grad, key_value))
    cotangent = level_gather(own_grads, 5, True)

    def gather_ffn(weight):
        whole = lax.all_gather(weight, ("group", "level"), axis=0)
        return whole.reshape((groups, levels) + weight.shape)

    w_in = gather_ffn(ffn_in)
    w_out = gather_ffn(after(ffn_out, window[0], cotangent))

    ramp = jnp.arange(count, dtype=jnp.int32)

    def arrival(values):
        lead, shape = values.shape[:-3], values.shape[-1:]
        four = values.reshape(lead + (HEADS, levels, HEADS, piece) + shape)
        return jnp.swapaxes(four, -4, -3).reshape(lead + (rows,) + shape)

    orders = after(orders, key_value)
    orders = jnp.concatenate([jnp.zeros((reach, HEADS, count), jnp.int32), orders], axis=0)
    orders = lax.dynamic_slice_in_dim(orders, level, reach + 1, 0)
    here = orders[:, :, None, :] == ramp[None, None, :, None]
    inverse = jnp.sum(here * ramp, axis=3)
    shard = (level - reach + jnp.arange(reach + 1, dtype=jnp.int32))[:, None] * HEADS
    shard = shard + jnp.arange(HEADS, dtype=jnp.int32)[None, :]
    pos_all = jnp.where(shard[:, :, None] < 0, -1, shard[:, :, None] * count + inverse)
    pos_all = arrival(pos_all[..., None]).reshape(-1)
    positions = pos_all[reach * rows :]
    own_routes = picks.reshape(levels, -1, HEADS, piece).transpose(2, 0, 3, 1).reshape(count, -1)

    seq_ends = jnp.cumsum(seq_lengths[0])

    def starts_of(places):
        return jnp.max(jnp.where(seq_ends <= places[:, None], seq_ends, 0), axis=1)

    starts = starts_of(positions)
    blocks = rows // BLOCK
    base_block = (level - reach) * blocks
    first_block = starts_of(level * rows + jnp.arange(blocks, dtype=jnp.int32) * BLOCK) // BLOCK
    first_block = jnp.maximum(first_block - base_block, 0)

    def lines(values):
        return values.reshape(blocks, 1, BLOCK)

    attended, log_total = attend(
        first_block,
        queries,
        window,
        lines(positions),
        lines(starts),
        pos_all[:, None],
    )

    out_sig = sigs[:, VEXP : 2 * VEXP]
    out_mask = masks[:, VEXP : 2 * VEXP]
    out_gate = out_sig * out_mask
    mixed = low((out_gate[..., None] * attended[:, None, :]).reshape(rows, VEXP * DH))
    branch = low(level_scatter(low(transposed(mixed, w_output)), 2))
    middle = own_tokens.astype(jnp.float32) + branch.astype(jnp.float32)

    normed_mid, scaled_two, inverse_two = layer_norm(middle, gain_two, bias_two)
    normed_two = low(normed_mid)
    ffn_sig = jax.nn.sigmoid(matmul(normed_two, r_ffn))
    member = chosen(own_routes, experts)
    shares = (ffn_sig * member).reshape(count, levels, HEADS, local_experts)
    shares = jnp.swapaxes(shares, 1, 2).reshape(count, experts)
    spare = -experts % 128
    extended = jnp.concatenate([middle, shares], axis=1)
    hidden = level_gather(jnp.pad(low(extended), ((0, 0), (0, spare))), 3, True)
    mine = levels * local_experts
    gates = lax.dynamic_slice_in_dim(hidden, width + head * mine, mine, 1).astype(jnp.float32)
    active, grad_pre, grad_rows = ffn_front(
        head[None], hidden, cotangent, w_in, w_out, gates, local_experts
    )
    summed, beyond = pair_scatter(grad_rows, 4, True)
    came = to_far(beyond)
    grad_in, feed = ffn_feed(after(hidden, beyond), grad_pre, active, w_out)
    came, feed = lax.optimization_barrier((came, feed))
    summed = summed + came.astype(jnp.float32)

    gate_grads = summed[:, width : width + experts].reshape(count, HEADS, levels, local_experts)
    gate_grads = jnp.swapaxes(gate_grads, 1, 2).reshape(count, experts)
    grad_logit = low(gate_grads * ffn_sig * (1.0 - ffn_sig) * member)
    grad_second = transposed(grad_logit, r_ffn)
    grad_r_ffn = contract_rows(normed_two, grad_logit)
    grad_gain_two = jnp.sum(grad_second * scaled_two, axis=0)
    grad_bias_two = jnp.sum(grad_second, axis=0)
    grad_middle = (
        own_grads.astype(jnp.float32)
        + summed[:, :width]
        + norm_back(grad_second, gain_two, scaled_two, inverse_two)
    )

    own_branch = low(grad_middle)
    came = to_far(own_branch)
    grad_out = ffn_rear(after(cotangent, own_branch), active, groups, levels)
    came, grad_out = lax.optimization_barrier((came, grad_out))
    grad_branch = pair_gather(own_branch, came, 7)

    def sum_over_rows(grad):
        return lax.psum_scatter(grad, ("group", "level"), scatter_dimension=0)

    ffn_in_grad = sum_over_rows(grad_in.reshape((groups * levels,) + grad_in.shape[2:]))
    grad_mixed = matmul(grad_branch, w_output).reshape(rows, VEXP, DH)
    grad_out_gate = jnp.sum(grad_mixed * attended[:, None, :], axis=-1)
    grad_attended = low(jnp.sum(grad_mixed * out_gate[..., None], axis=1))
    grad_out_logit = low(grad_out_gate * out_sig * (1.0 - out_sig) * out_mask)
    row_inner = jnp.sum(grad_attended.astype(jnp.float32) * attended, axis=-1)
    grad_queries, *grad_window = attend_back(
        first_block,
        queries,
        window,
        grad_attended,
        lines(positions),
        lines(starts),
        log_total,
        lines(row_inner),
        pos_all[:, None],
    )
    came = shift(grad_window[0], "level", -1)
    fed, beyond = pair_scatter(after(feed, grad_queries), 6, True)
    grad_w_output = contract_rows(after(grad_branch, fed), mixed)
    early = jnp.concatenate(
        [
            low(grad_w_output),
            low(grad_r_ffn),
            low(grad_gain_two)[:, None],
            low(grad_bias_two)[:, None],
            jnp.zeros((width, -(experts + 2) % 128), jnp.bfloat16),
        ],
        axis=1,
    )
    for i in range(1, reach + 1):
        if i < reach:
            came, fed = lax.optimization_barrier((came, fed))
        else:
            came, early = lax.optimization_barrier((came, early))
        grad_both = grad_window[i].astype(jnp.float32) + came.astype(jnp.float32)
        if i < reach:
            grad_keys_sent = low(grad_both)
            came = shift(grad_keys_sent, "level", -1)
    fed_far = to_far(beyond)
    ffn_out_grad = sum_over_rows(grad_out.reshape((groups * levels,) + grad_out.shape[2:]))
    early = early.reshape(groups * levels, HEADS * wrows, -1)
    early, ffn_in_grad = lax.optimization_barrier((early, ffn_in_grad))
    early = sum_over_rows(early)
    grad_inputs, late = project_back(
        worker_in,
        grad_both,
        grad_queries,
        jnp.pad(grad_out_logit, ((0, 0), (VEXP, 128 - 2 * VEXP))),
        projected,
        sigs,
        masks,
        full,
        gain_row,
        bias_row,
    )

    fed_far, grad_inputs = lax.optimization_barrier((fed_far, grad_inputs))
    layer_out = to_home(low(middle + fed + fed_far.astype(jnp.float32)))

    input_grad, owned = finish(
        grad_inputs.reshape(HEADS, HEADS, levels * piece, width),
        grad_middle.reshape(HEADS, levels * piece, width),
        late.reshape(groups, levels, HEADS, wrows, -1),
    )
    owned = owned.astype(jnp.float32)
    early = lax.all_to_all(
        early.reshape(HEADS, wrows, -1), "head", split_axis=0, concat_axis=0, tiled=True
    ).astype(jnp.float32)

    def columns(part, first, size):
        return part[:, :, first : first + size].transpose(1, 0, 2).reshape(wrows, HEADS * size)

    values = VEXP * DH
    misc = values + 2 * DH
    common = jnp.sum(early[:, :, values:], axis=0)
    norms = jnp.sum(owned[:, :, misc + 2 * VEXP :], axis=0)
    return (
        layer_out,
        input_grad.reshape(count, width),
        norms[:, 0],
        norms[:, 1],
        common[:, experts],
        common[:, experts + 1],
        columns(owned, values, DH),
        columns(owned, values + DH, DH),
        columns(owned, 0, values),
        columns(early, 0, values),
        columns(owned, misc, VEXP),
        columns(owned, misc + VEXP, VEXP),
        common[:, :experts],
        ffn_in_grad.astype(jnp.float32),
        ffn_out_grad.astype(jnp.float32),
    )


def solution(mesh):
    groups, shards = mesh.devices.shape
    fine = Mesh(mesh.devices.reshape(groups, shards // HEADS, HEADS), TOK)
    two, one, three = P(TOK, None), P(TOK), P(TOK, None, None)
    ffn = P("group", ("level", "head"))
    return jax.shard_map(
        body,
        mesh=fine,
        in_specs=(two, two, two, P("group", None), three, three, two, one, one, one, one)
        + (two,) * 7
        + (ffn, ffn),
        out_specs=(two, two, one, one, one, one) + (two,) * 7 + (ffn, ffn),
        check_vma=False,
    )
```

```python
import functools

import jax
import jax.numpy as jnp
from jax import lax
from jax.experimental import pallas as pl
from jax.experimental.pallas import tpu as pltpu
from jax.sharding import Mesh, PartitionSpec as P

HEADS = 4
DH = 128
VEXP = 5
FH = 128
LMAX = 4096

TOK = ("group", "level", "head")


def matmul(left_side, right_side):
    return jnp.dot(left_side, right_side, preferred_element_type=jnp.float32)


def transposed(left_side, right_side):
    return lax.dot_general(
        left_side, right_side, (((1,), (1,)), ((), ())), preferred_element_type=jnp.float32
    )


def contract_rows(left_side, right_side):
    return lax.dot_general(
        left_side, right_side, (((0,), (0,)), ((), ())), preferred_element_type=jnp.float32
    )


def low(value):
    return value.astype(jnp.bfloat16)


def layer_norm(inputs, gain_vec, bias_vec):
    centred = inputs - jnp.mean(inputs, axis=-1, keepdims=True)
    inverse = lax.rsqrt(jnp.mean(centred * centred, axis=-1, keepdims=True) + 1e-05)
    scaled = centred * inverse
    return (scaled * gain_vec + bias_vec, scaled, inverse)


def norm_back(grad_normed, gain_vec, scaled, inverse):
    inner_grad = grad_normed * gain_vec
    return inverse * (
        inner_grad
        - jnp.mean(inner_grad, axis=-1, keepdims=True)
        - scaled * jnp.mean(inner_grad * scaled, axis=-1, keepdims=True)
    )


def to_home(rows):
    levels = lax.axis_size("level")
    count = rows.shape[0]
    out = rows.reshape(HEADS, levels, count // levels // HEADS, -1).transpose(1, 0, 2, 3)
    back = lax.all_to_all(
        out.reshape(levels, count // levels, -1), "level", split_axis=0, concat_axis=0, tiled=True
    )
    return back.reshape(count, -1)


MESH = pl.DeviceIdType.MESH


def partners(head):
    near = head + 1 - 2 * lax.rem(head, 2)
    far = lax.rem(head + 2, HEADS)
    return near, far


def greet(near, far):
    barrier = pltpu.get_barrier_semaphore()
    for peer in (near, far):
        pl.semaphore_signal(barrier, inc=1, device_id={"head": peer}, device_id_type=MESH)
    pl.semaphore_wait(barrier, 2)


def remote(src, dst, send, recv, peer):
    return pltpu.make_async_remote_copy(
        src_ref=src,
        dst_ref=dst,
        send_sem=send,
        recv_sem=recv,
        device_id={"head": peer},
        device_id_type=MESH,
    )


def cost(flops, moved):
    return pl.CostEstimate(flops=int(flops), bytes_accessed=int(moved), transcendentals=0)


def gather_kernel(
    by_source, own, out, local_sem, near_send, near_recv, far_send, far_recv, pass_send, pass_recv
):
    head = lax.axis_index("head")
    near, far = partners(head)
    greet(near, far)

    def spot(i, source):
        return out.at[source, i] if by_source else out.at[i, source]

    pieces = range(HEADS)
    to_far = [remote(own.at[i], spot(i, head), far_send.at[i], far_recv.at[i], far) for i in pieces]
    to_near = [
        remote(own.at[i], spot(i, head), near_send.at[i], near_recv.at[i], near) for i in pieces
    ]
    passed = [
        remote(spot(i, far), spot(i, far), pass_send.at[i], pass_recv.at[i], near) for i in pieces
    ]
    kept = [pltpu.make_async_copy(own.at[i], spot(i, head), local_sem.at[i]) for i in pieces]
    for copy in to_far + to_near + kept:
        copy.start()
    for i in pieces:
        to_far[i].wait_recv()
        passed[i].start()
    for i in pieces:
        to_near[i].wait_recv()
        passed[i].wait_recv()
        kept[i].wait()
        to_far[i].wait_send()
        to_near[i].wait_send()
        passed[i].wait_send()


def level_gather(rows, collective_id, by_source=False):
    count, width = rows.shape
    whole = pl.pallas_call(
        functools.partial(gather_kernel, by_source),
        out_shape=jax.ShapeDtypeStruct((HEADS, HEADS, count // HEADS, width), rows.dtype),
        in_specs=[pl.BlockSpec(memory_space=pltpu.VMEM)],
        out_specs=pl.BlockSpec(memory_space=pl.ANY),
        scratch_shapes=[pltpu.SemaphoreType.DMA((HEADS,))] * 7,
        compiler_params=pltpu.CompilerParams(collective_id=collective_id, has_side_effects=True),
        cost_estimate=cost(0, 90e6),
        name="level_gather",
    )(rows.reshape(HEADS, count // HEADS, width))
    return whole.reshape(HEADS * count, width)


def scatter_kernel(
    by_source, part, out, near_buf, send_buf, far_buf, near_send, near_recv, far_send, far_recv
):
    head = lax.axis_index("head")
    near, far = partners(head)
    greet(near, far)
    across = HEADS - 1 - head
    pieces = range(HEADS)

    def spot(i, dest):
        return (dest, i) if by_source else (i, dest)

    def to_near(slot, i, dest):
        return remote(
            part.at[spot(i, dest)],
            near_buf.at[slot, i],
            near_send.at[slot, i],
            near_recv.at[slot, i],
            near,
        )

    first = [to_near(0, i, across) for i in pieces]
    second = [to_near(1, i, near) for i in pieces]
    onward = [
        remote(send_buf.at[i], far_buf.at[i], far_send.at[i], far_recv.at[i], far) for i in pieces
    ]
    for copy in first + second:
        copy.start()
    for i in pieces:
        first[i].wait_recv()
        both = part[spot(i, far)].astype(jnp.float32) + near_buf[0, i].astype(jnp.float32)
        send_buf[i] = both.astype(jnp.bfloat16)
        onward[i].start()
    for i in pieces:
        second[i].wait_recv()
        out[i] = part[spot(i, head)].astype(jnp.float32) + near_buf[1, i].astype(jnp.float32)
    for i in pieces:
        onward[i].wait_recv()
        out[i] = out[i] + far_buf[i].astype(jnp.float32)
    for i in pieces:
        first[i].wait_send()
        second[i].wait_send()
        onward[i].wait_send()


def level_scatter(rows, collective_id, by_source=False):
    total, width = rows.shape
    piece = total // (HEADS * HEADS)
    low_type = jnp.bfloat16
    mine = pl.pallas_call(
        functools.partial(scatter_kernel, by_source),
        out_shape=jax.ShapeDtypeStruct((HEADS, piece, width), jnp.float32),
        in_specs=[pl.BlockSpec(memory_space=pltpu.VMEM)],
        out_specs=pl.BlockSpec(memory_space=pltpu.VMEM),
        scratch_shapes=[
            pltpu.VMEM((2, HEADS, piece, width), low_type),
            pltpu.VMEM((HEADS, piece, width), low_type),
            pltpu.VMEM((HEADS, piece, width), low_type),
            pltpu.SemaphoreType.DMA((2, HEADS)),
            pltpu.SemaphoreType.DMA((2, HEADS)),
            pltpu.SemaphoreType.DMA((HEADS,)),
            pltpu.SemaphoreType.DMA((HEADS,)),
        ],
        compiler_params=pltpu.CompilerParams(
            collective_id=collective_id, has_side_effects=True, vmem_limit_bytes=32 * 2**20
        ),
        cost_estimate=cost(0, 80e6),
        name="level_scatter",
    )(rows.reshape(HEADS, HEADS, piece, width))
    return mine.reshape(HEADS * piece, width)


def meet(near):
    barrier = pltpu.get_barrier_semaphore()
    pl.semaphore_signal(barrier, inc=1, device_id={"head": near}, device_id_type=MESH)
    pl.semaphore_wait(barrier, 1)


def pair_scatter_kernel(by_source, part, out, out_far, near_buf, send, recv):
    head = lax.axis_index("head")
    near, far = partners(head)
    meet(near)
    across = HEADS - 1 - head
    pieces = range(HEADS)

    def spot(i, dest):
        return (dest, i) if by_source else (i, dest)

    def to_near(slot, i, dest):
        return remote(
            part.at[spot(i, dest)], near_buf.at[slot, i], send.at[slot, i], recv.at[slot, i], near
        )

    first = [to_near(0, i, across) for i in pieces]
    second = [to_near(1, i, near) for i in pieces]
    for copy in first + second:
        copy.start()
    for i in pieces:
        first[i].wait_recv()
        both = part[spot(i, far)].astype(jnp.float32) + near_buf[0, i].astype(jnp.float32)
        out_far[i] = both.astype(jnp.bfloat16)
    for i in pieces:
        second[i].wait_recv()
        out[i] = part[spot(i, head)].astype(jnp.float32) + near_buf[1, i].astype(jnp.float32)
    for i in pieces:
        first[i].wait_send()
        second[i].wait_send()


def pair_scatter(rows, collective_id, by_source=False):
    total, width = rows.shape
    piece = total // (HEADS * HEADS)
    mine, other = pl.pallas_call(
        functools.partial(pair_scatter_kernel, by_source),
        out_shape=[
            jax.ShapeDtypeStruct((HEADS, piece, width), jnp.float32),
            jax.ShapeDtypeStruct((HEADS, piece, width), jnp.bfloat16),
        ],
        in_specs=[pl.BlockSpec(memory_space=pltpu.VMEM)],
        out_specs=[pl.BlockSpec(memory_space=pltpu.VMEM)] * 2,
        scratch_shapes=[
            pltpu.VMEM((2, HEADS, piece, width), jnp.bfloat16),
            pltpu.SemaphoreType.DMA((2, HEADS)),
            pltpu.SemaphoreType.DMA((2, HEADS)),
        ],
        compiler_params=pltpu.CompilerParams(
            collective_id=collective_id, has_side_effects=True, vmem_limit_bytes=32 * 2**20
        ),
        cost_estimate=cost(0, 25e6),
        name="pair_scatter",
    )(rows.reshape(HEADS, HEADS, piece, width))
    return mine.reshape(HEADS * piece, width), other.reshape(HEADS * piece, width)


def pair_gather_kernel(by_source, own, other, out, local_sem, send, recv):
    head = lax.axis_index("head")
    near, far = partners(head)
    meet(near)
    copies, kept = [], []
    for i in range(HEADS):
        for slot, (block, source) in enumerate(((own, head), (other, far))):
            place = out.at[source, i] if by_source else out.at[i, source]
            copies.append(
                remote(block.at[i], place, send.at[slot, i], recv.at[slot, i], near)
            )
            kept.append(pltpu.make_async_copy(block.at[i], place, local_sem.at[slot, i]))
    for copy in copies + kept:
        copy.start()
    for copy in copies + kept:
        copy.wait()


def pair_gather(own, other, collective_id, by_source=False):
    count, width = own.shape
    split = (HEADS, count // HEADS, width)
    whole = pl.pallas_call(
        functools.partial(pair_gather_kernel, by_source),
        out_shape=jax.ShapeDtypeStruct((HEADS,) + split, own.dtype),
        in_specs=[pl.BlockSpec(memory_space=pltpu.VMEM)] * 2,
        out_specs=pl.BlockSpec(memory_space=pl.ANY),
        scratch_shapes=[pltpu.SemaphoreType.DMA((2, HEADS))] * 3,
        compiler_params=pltpu.CompilerParams(collective_id=collective_id, has_side_effects=True),
        cost_estimate=cost(0, 25e6),
        name="pair_gather",
    )(own.reshape(split), other.reshape(split))
    return whole.reshape(HEADS * count, width)


def to_far(rows):
    return lax.ppermute(rows, "head", [(i, (i + 2) % HEADS) for i in range(HEADS)])


def after(value, *others):
    return lax.optimization_barrier((value,) + others)[0]


def ring(axis):
    me, size = lax.axis_index(axis), lax.axis_size(axis)
    ahead = [lax.rem(me + k, size) for k in range(1, size)]
    behind = [lax.rem(me + size - k, size) for k in range(1, size)]
    return me, ahead, behind


def reach_out(src, dst, send, recv, peer):
    return pltpu.make_async_remote_copy(
        src_ref=src, dst_ref=dst, send_sem=send, recv_sem=recv, device_id=peer, device_id_type=MESH
    )


def greet_all(peers):
    barrier = pltpu.get_barrier_semaphore()
    for peer in peers:
        pl.semaphore_signal(barrier, inc=1, device_id=peer, device_id_type=MESH)
    pl.semaphore_wait(barrier, len(peers))


def start_kernel(
    tokens, cotangents, weights, tables, picks, order,
    rows, grads, full, routes, chosen_rows, orders, own_sem, *sems
):
    sems = iter(sems)

    def pair():
        return next(sems), next(sems)

    group, groups_ahead, _ = ring("group")
    level, levels_ahead, levels_behind = ring("level")
    head = lax.axis_index("head")
    near, far = partners(head)
    mates = [near, far, HEADS - 1 - head]
    greet_all(
        [{"head": m} for m in mates]
        + [{"level": n} for n in levels_ahead]
        + [{"group": n} for n in groups_ahead]
    )
    started = []

    def send(src, dst, send_sem, recv_sem, peer):
        copy = reach_out(src, dst, send_sem, recv_sem, peer)
        copy.start()
        started.append(copy)
        return copy

    out_s, out_r = pair()
    pick_s, pick_r = pair()
    crossing, picking = [], []
    for k, to in enumerate(levels_ahead):
        peer = {"level": to}
        crossing.append(send(tokens.at[to], rows.at[:, head, level], out_s.at[k], out_r.at[k], peer))
    mate_s, mate_r = pair()
    table_s, table_r = pair()
    order_s, order_r = pair()
    to_mates, order_mates, table_mates = [], [], []
    for k, to in enumerate(mates):
        peer = {"head": to}
        to_mates.append(
            send(weights.at[to], full.at[group, level, head], mate_s.at[k], mate_r.at[k], peer)
        )
        order_mates.append(
            send(order, orders.at[level, head], order_s.at[k], order_r.at[k], peer)
        )
    own = [
        (tokens.at[level], rows.at[:, head, level]),
        (weights.at[head], full.at[group, level, head]),
        (tables.at[head], routes.at[head]),
        (picks.at[level], chosen_rows.at[level]),
        (order, orders.at[level, head]),
        (cotangents.at[level], grads.at[:, level]),
    ]
    own = [pltpu.make_async_copy(src, dst, own_sem.at[i]) for i, (src, dst) in enumerate(own)]
    for copy in own:
        copy.start()
    far_s, far_r = pair()
    near_s, near_r = pair()
    pass_s, pass_r = pair()
    to_far, to_near = [], []

    def share(k, src, source):
        place = rows.at[:, head, source]
        to_far.append(send(src, place, far_s.at[k], far_r.at[k], {"head": far}))
        to_near.append(send(src, place, near_s.at[k], near_r.at[k], {"head": near}))

    share(0, tokens.at[level], level)
    up_s, up_r = pair()
    down_s, down_r = pair()
    group_s, group_r = pair()
    orders_s, orders_r = pair()
    for copy in to_mates:
        copy.wait_recv()
    own[1].wait()
    last = len(levels_ahead)
    grouped, ordered = [], []

    def to_groups(j, source):
        for k, to in enumerate(groups_ahead):
            block = full.at[group, source]
            grouped.append(
                send(block, block, group_s.at[k, j], group_r.at[k, j], {"group": to})
            )

    def hop(k, step):
        send_sem, recv_sem = (up_s, up_r) if step > 0 else (down_s, down_r)
        block = full.at[group, lax.rem(level - step * k + last + 1, last + 1)]
        to = lax.rem(level + step + last + 1, last + 1)
        return reach_out(block, block, send_sem.at[k], recv_sem.at[k], {"level": to})

    def sends(k, step):
        return (level >= k) & (level < last) if step > 0 else (level <= last - k) & (level > 0)

    def receives(k, step):
        return level >= k + 1 if step > 0 else level <= last - k - 1

    def start_hop(k, step):
        @pl.when(sends(k, step))
        def _():
            hop(k, step).start()

    def wait_hop(k, step):
        @pl.when(receives(k, step))
        def _():
            hop(k, step).wait_recv()

    for step in (1, -1):
        start_hop(0, step)
    to_groups(0, level)
    for k, to in enumerate(mates):
        table_mates.append(
            send(tables.at[to], routes.at[head], table_s.at[k], table_r.at[k], {"head": to})
        )
    for k, to in enumerate(levels_ahead):
        picking.append(
            send(picks.at[to], chosen_rows.at[level], pick_s.at[k], pick_r.at[k], {"level": to})
        )
    grad_s, grad_r = pair()
    crossed = []
    for k, to in enumerate(levels_ahead):
        crossed.append(
            send(cotangents.at[to], grads.at[:, level], grad_s.at[k], grad_r.at[k], {"level": to})
        )
    for copy in order_mates:
        copy.wait_recv()
    own[4].wait()
    for k, to in enumerate(levels_ahead):
        block = orders.at[level]
        ordered.append(send(block, block, orders_s.at[k], orders_r.at[k], {"level": to}))
    for k, source in enumerate(levels_behind):
        crossing[k].wait_recv()
        share(k + 1, rows.at[:, head, source], source)
    for k in range(last):
        for step in (1, -1):
            wait_hop(k, step)
            if k + 1 < last:
                start_hop(k + 1, step)
    for k, source in enumerate(levels_behind):
        to_groups(k + 1, source)
    passed = []
    for k, source in enumerate([level] + levels_behind):
        to_far[k].wait_recv()
        place = rows.at[:, far, source]
        passed.append(send(place, place, pass_s.at[k], pass_r.at[k], {"head": near}))
    for copy in to_near + passed + grouped + table_mates + picking + ordered + crossed:
        copy.wait_recv()
    for copy in started:
        copy.wait_send()
    for k in range(last):
        for step in (1, -1):

            @pl.when(sends(k, step))
            def _(k=k, step=step):
                hop(k, step).wait_send()

    for i in (0, 2, 3, 5):
        own[i].wait()


def start(tokens, cotangents, weights, tables, picks, order):
    groups, levels = lax.axis_size("group"), lax.axis_size("level")
    _, _, piece, width = tokens.shape
    shapes = [
        jax.ShapeDtypeStruct((HEADS, HEADS, levels, piece, width), tokens.dtype),
        jax.ShapeDtypeStruct((HEADS, levels, piece, width), tokens.dtype),
        jax.ShapeDtypeStruct((groups, levels) + weights.shape, weights.dtype),
        jax.ShapeDtypeStruct(tables.shape, tables.dtype),
        jax.ShapeDtypeStruct(picks.shape, picks.dtype),
        jax.ShapeDtypeStruct((levels, HEADS) + order.shape, order.dtype),
    ]
    dma = pltpu.SemaphoreType.DMA
    others, mates = (levels - 1,), (HEADS - 1,)
    counts = [others] * 2 + [mates] * 3 + [(levels,)] * 3
    counts += [others, others, (groups - 1, levels), others, others]
    return pl.pallas_call(
        start_kernel,
        out_shape=shapes,
        in_specs=[pl.BlockSpec(memory_space=pltpu.VMEM)] * 6,
        out_specs=[pl.BlockSpec(memory_space=pl.ANY)] * 6,
        scratch_shapes=[dma((6,))] + [dma(c) for c in counts for _ in range(2)],
        compiler_params=pltpu.CompilerParams(collective_id=9, has_side_effects=True),
        cost_estimate=cost(0, 200e6),
        name="start",
    )(tokens, cotangents, weights, tables, picks, order)


def finish_kernel(count, *refs):
    refs = iter(refs)

    def take(n):
        return [next(refs) for _ in range(n)]

    part, middle = take(2)
    grads = take(count)
    (home_grad,) = take(1)
    owned = take(count)
    near_buf, send_buf, far_buf, total, back_buf, came_buf = take(6)
    group_buf, level_send, level_buf, head_send = (take(count) for _ in range(4))

    def pair():
        return next(refs), next(refs)

    group, groups_ahead, _ = ring("group")
    level, levels_ahead, levels_behind = ring("level")
    head = lax.axis_index("head")
    near, far = partners(head)
    across = HEADS - 1 - head
    mates = [near, far, across]
    greet_all(
        [{"head": m} for m in mates]
        + [{"level": n} for n in levels_ahead]
        + [{"group": n} for n in groups_ahead]
    )
    started = []

    def send(src, dst, send_sem, recv_sem, peer):
        copy = reach_out(src, dst, send_sem, recv_sem, peer)
        copy.start()
        started.append(copy)
        return copy

    pieces = range(HEADS)
    sets = range(count)
    near_s, near_r = pair()
    far_s, far_r = pair()
    back_s, back_r = pair()
    group_s, group_r = pair()
    level_s, level_r = pair()
    mate_s, mate_r = pair()
    first, second, onward = [], [], []
    for slot, (dest, copies) in enumerate(((across, first), (near, second))):
        for i in pieces:
            copies.append(
                send(
                    part.at[i, dest],
                    near_buf.at[slot, i],
                    near_s.at[slot, i],
                    near_r.at[slot, i],
                    {"head": near},
                )
            )
    order = levels_ahead + [level]
    grouped = {}
    for j, dest in enumerate(order):
        for p in sets:
            grouped[j, p] = [
                send(
                    grads[p].at[to, dest],
                    group_buf[p].at[k, j],
                    group_s.at[p, k, j],
                    group_r.at[p, k, j],
                    {"group": to},
                )
                for k, to in enumerate(groups_ahead)
            ]
    for i in pieces:
        first[i].wait_recv()
        both = part[i, far].astype(jnp.float32) + near_buf[0, i].astype(jnp.float32)
        send_buf[i] = both.astype(jnp.bfloat16)
        onward.append(send(send_buf.at[i], far_buf.at[i], far_s.at[i], far_r.at[i], {"head": far}))
    for i in pieces:
        second[i].wait_recv()
        both = part[i, head].astype(jnp.float32) + near_buf[1, i].astype(jnp.float32)
        total[i] = both + middle[i]
    leveled = {}
    for j, dest in enumerate(order):
        for p in sets:
            amount = grads[p][group, dest].astype(jnp.float32)
            for k, copy in enumerate(grouped[j, p]):
                copy.wait_recv()
                amount = amount + group_buf[p][k, j].astype(jnp.float32)
            level_send[p][j] = amount.astype(jnp.bfloat16)
            if j < len(levels_ahead):
                leveled[j, p] = send(
                    level_send[p].at[j],
                    level_buf[p].at[j],
                    level_s.at[p, j],
                    level_r.at[p, j],
                    {"level": dest},
                )
    for i in pieces:
        onward[i].wait_recv()
        both = total[i] + far_buf[i].astype(jnp.float32)
        back_buf[i] = both.astype(jnp.bfloat16).reshape(back_buf.shape[1:])
    backs = [
        send(back_buf.at[:, to], came_buf.at[level], back_s.at[k], back_r.at[k], {"level": to})
        for k, to in enumerate(levels_ahead)
    ]
    sharing = []
    for p in sets:
        amount = level_send[p][len(levels_ahead)].astype(jnp.float32)
        for j in range(len(levels_ahead)):
            leveled[j, p].wait_recv()
            amount = amount + level_buf[p][j].astype(jnp.float32)
        head_send[p][...] = amount.astype(jnp.bfloat16)
        sharing += [
            send(
                head_send[p].at[to],
                owned[p].at[head],
                mate_s.at[p, k],
                mate_r.at[p, k],
                {"head": to},
            )
            for k, to in enumerate(mates)
        ]
        owned[p][head] = head_send[p][head]
    home_grad[level] = back_buf[:, level].astype(jnp.float32)
    for k, source in enumerate(levels_behind):
        backs[k].wait_recv()
        home_grad[source] = came_buf[source].astype(jnp.float32)
    for copy in sharing:
        copy.wait_recv()
    for copy in started:
        copy.wait_send()


def finish(part, middle, *grads):
    groups, levels = lax.axis_size("group"), lax.axis_size("level")
    _, count, width = middle.shape
    piece = count // levels
    low_type = jnp.bfloat16
    blocks = [grad.shape[2:] for grad in grads]
    sets = len(grads)
    dma = pltpu.SemaphoreType.DMA
    counts = [(2, HEADS), (HEADS,), (levels - 1,)]
    counts += [(sets, groups - 1, levels), (sets, levels - 1), (sets, HEADS - 1)]
    vmem = pl.BlockSpec(memory_space=pltpu.VMEM)
    return pl.pallas_call(
        functools.partial(finish_kernel, sets),
        out_shape=[jax.ShapeDtypeStruct((levels, HEADS, piece, width), jnp.float32)]
        + [jax.ShapeDtypeStruct(block, low_type) for block in blocks],
        in_specs=[vmem] * (2 + sets),
        out_specs=[vmem] * (1 + sets),
        scratch_shapes=[
            pltpu.VMEM((2, HEADS, count, width), low_type),
            pltpu.VMEM((HEADS, count, width), low_type),
            pltpu.VMEM((HEADS, count, width), low_type),
            pltpu.VMEM((HEADS, count, width), jnp.float32),
            pltpu.VMEM((HEADS, levels, piece, width), low_type),
            pltpu.VMEM((levels, HEADS, piece, width), low_type),
        ]
        + [pltpu.VMEM((groups - 1, levels) + block, low_type) for block in blocks]
        + [pltpu.VMEM((levels,) + block, low_type) for block in blocks]
        + [pltpu.VMEM((levels - 1,) + block, low_type) for block in blocks]
        + [pltpu.VMEM(block, low_type) for block in blocks]
        + [dma(c) for c in counts for _ in range(2)],
        compiler_params=pltpu.CompilerParams(
            collective_id=10, has_side_effects=True, vmem_limit_bytes=56 * 2**20
        ),
        cost_estimate=cost(0, 200e6),
        name="finish",
    )(part, middle, *grads)


BLOCK = 512
LOG2E = 1.4426950408889634


def dot(left_side, right_side, left_dim, right_dim):
    return lax.dot_general(
        left_side,
        right_side,
        (((left_dim,), (right_dim,)), ((), ())),
        preferred_element_type=jnp.float32,
    )


def attend_kernel(parts, first, q, *refs):
    keys, values = refs[:parts], refs[parts : 2 * parts]
    pos_q, start_q, pos_k, out, lse, top, total, acc = refs[2 * parts :]
    at = pl.program_id(0)
    blocks = pl.num_programs(0)
    rate = LOG2E * DH ** (-0.5)
    top[...] = jnp.full_like(top, -1e30)
    total[...] = jnp.zeros_like(total)
    acc[...] = jnp.zeros_like(acc)
    query = q[...]
    row_at, row_from = pos_q[0], start_q[0]

    for part in range(parts):

        def step(block, carry, k=keys[part], v=values[part], part=part):
            rows = pl.ds(pl.multiple_of(block * BLOCK, BLOCK), BLOCK)
            spot = pl.ds(pl.multiple_of((part * blocks + block) * BLOCK, BLOCK), BLOCK)
            scores = dot(k[rows, :], query, 1, 1)
            key_at = pos_k[spot, :]
            scores = jnp.where((key_at >= row_from) & (key_at <= row_at), scores, -1e30)
            old = top[...]
            new = jnp.maximum(old, jnp.max(scores, axis=0, keepdims=True))
            shrink = jnp.exp2((old - new) * rate)
            weight = jnp.exp2((scores - new) * rate)
            total[...] = total[...] * shrink + jnp.sum(weight, axis=0, keepdims=True)
            acc[...] = acc[...] * shrink + dot(v[rows, :], weight.astype(jnp.bfloat16), 0, 0)
            top[...] = new
            return carry

        begin = jnp.maximum(first[at] - part * blocks, 0)
        end = at + 1 if part == parts - 1 else blocks
        lax.fori_loop(begin, end, step, 0)
    out[...] = (acc[...] / total[...]).T
    lse[0] = top[...] * rate + jnp.log2(total[...])


def attend(first, queries, window, pos_q, start_q, pos_k):
    rows = queries.shape[0]
    parts = len(window)
    line = pl.BlockSpec((1, 1, BLOCK), lambda i, *_: (i, 0, 0))
    grid_spec = pltpu.PrefetchScalarGridSpec(
        num_scalar_prefetch=1,
        grid=(rows // BLOCK,),
        in_specs=[pl.BlockSpec((BLOCK, DH), lambda i, *_: (i, 0))]
        + [pl.BlockSpec((rows, DH), lambda i, *_: (0, 0))] * parts
        + [pl.BlockSpec((rows, DH), lambda i, *_: (0, 1))] * parts
        + [line, line, pl.BlockSpec((parts * rows, 1), lambda i, *_: (0, 0))],
        out_specs=[pl.BlockSpec((BLOCK, DH), lambda i, *_: (i, 0)), line],
        scratch_shapes=[
            pltpu.VMEM((1, BLOCK), jnp.float32),
            pltpu.VMEM((1, BLOCK), jnp.float32),
            pltpu.VMEM((DH, BLOCK), jnp.float32),
        ],
    )
    return pl.pallas_call(
        functools.partial(attend_kernel, parts),
        grid_spec=grid_spec,
        out_shape=[
            jax.ShapeDtypeStruct((rows, DH), jnp.float32),
            jax.ShapeDtypeStruct((rows // BLOCK, 1, BLOCK), jnp.float32),
        ],
        compiler_params=pltpu.CompilerParams(vmem_limit_bytes=48 * 2**20),
        cost_estimate=cost(2e10, 1e7),
        name="attend",
    )(first, queries, *window, *window, pos_q, start_q, pos_k)


def attend_back_kernel(parts, first, q, *refs):
    keys, values = refs[:parts], refs[parts : 2 * parts]
    grad, pos_q, start_q, lse, inner, pos_k, grad_q = refs[2 * parts : 2 * parts + 7]
    grads = refs[2 * parts + 7 : 3 * parts + 7]
    sum_k, sum_v, acc = refs[3 * parts + 7 :]
    at = pl.program_id(0)
    blocks = pl.num_programs(0)
    rate = LOG2E * DH ** (-0.5)
    scale = DH ** (-0.5)

    @pl.when(at == 0)
    def _():
        sum_k[...] = jnp.zeros_like(sum_k)
        sum_v[...] = jnp.zeros_like(sum_v)

    acc[...] = jnp.zeros_like(acc)
    query, grad_out = q[...], grad[...]
    row_at, row_from, row_lse, row_inner = pos_q[0], start_q[0], lse[0], inner[0]

    for part in range(parts):

        def step(block, carry, k=keys[part], v=values[part], part=part):
            rows = pl.ds(pl.multiple_of(block * BLOCK, BLOCK), BLOCK)
            spot = pl.ds(pl.multiple_of((part * blocks + block) * BLOCK, BLOCK), BLOCK)
            key, value = k[rows, :], v[rows, :]
            scores = dot(key, query, 1, 1)
            key_at = pos_k[spot, :]
            seen = (key_at >= row_from) & (key_at <= row_at)
            soft = jnp.where(seen, jnp.exp2(scores * rate - row_lse), 0.0)
            grad_soft = dot(value, grad_out, 1, 1)
            grad_scores = (soft * (grad_soft - row_inner)).astype(jnp.bfloat16)
            sum_v[spot, :] += dot(soft.astype(jnp.bfloat16), grad_out, 1, 0)
            sum_k[spot, :] += dot(grad_scores, query, 1, 0)
            acc[...] += dot(grad_scores, key, 0, 0)
            return carry

        begin = jnp.maximum(first[at] - part * blocks, 0)
        end = at + 1 if part == parts - 1 else blocks
        lax.fori_loop(begin, end, step, 0)
    grad_q[...] = (acc[...] * scale).astype(jnp.bfloat16)

    @pl.when(at == blocks - 1)
    def _():
        size = grads[0].shape[0]
        for part in range(parts):
            spot = slice(part * size, (part + 1) * size)
            grads[part][:, :DH] = (sum_k[spot, :] * scale).astype(grads[part].dtype)
            grads[part][:, DH:] = sum_v[spot, :].astype(grads[part].dtype)


def attend_back(first, queries, window, grads, pos_q, start_q, lse, inner, pos_k):
    rows = queries.shape[0]
    parts = len(window)
    block = pl.BlockSpec((BLOCK, DH), lambda i, *_: (i, 0))
    line = pl.BlockSpec((1, 1, BLOCK), lambda i, *_: (i, 0, 0))
    grid_spec = pltpu.PrefetchScalarGridSpec(
        num_scalar_prefetch=1,
        grid=(rows // BLOCK,),
        in_specs=[block]
        + [pl.BlockSpec((rows, DH), lambda i, *_: (0, 0))] * parts
        + [pl.BlockSpec((rows, DH), lambda i, *_: (0, 1))] * parts
        + [block, line, line, line, line]
        + [pl.BlockSpec((parts * rows, 1), lambda i, *_: (0, 0))],
        out_specs=[block] + [pl.BlockSpec((rows, 2 * DH), lambda i, *_: (0, 0))] * parts,
        scratch_shapes=[
            pltpu.VMEM((parts * rows, DH), jnp.float32),
            pltpu.VMEM((parts * rows, DH), jnp.float32),
            pltpu.VMEM((BLOCK, DH), jnp.float32),
        ],
    )
    kinds = [jnp.bfloat16] * (parts - 1) + [jnp.float32]
    return pl.pallas_call(
        functools.partial(attend_back_kernel, parts),
        grid_spec=grid_spec,
        out_shape=[jax.ShapeDtypeStruct((rows, DH), jnp.bfloat16)]
        + [jax.ShapeDtypeStruct((rows, 2 * DH), kind) for kind in kinds],
        compiler_params=pltpu.CompilerParams(vmem_limit_bytes=48 * 2**20),
        cost_estimate=cost(2e10, 1e7),
        name="attend_back",
    )(first, queries, *window, *window, grads, pos_q, start_q, lse, inner, pos_k)


def front_kernel(
    local, head, hidden, grads, w_in, w_out, gates, active, grad_pre, rows_out, acc
):
    groups, levels, depth, width = w_in.shape
    tile = hidden.shape[0]
    model = groups * depth
    acc[...] = jnp.zeros_like(acc)
    gate_grads = []
    for level in range(levels):
        pre_act = jnp.zeros((tile, width), jnp.float32)
        grad_active = jnp.zeros((tile, width), jnp.float32)
        for group in range(groups):
            part = slice(group * depth, (group + 1) * depth)
            pre_act += dot(hidden[:, part], w_in[group, level], 1, 0)
            grad_active += dot(grads[:, part], w_out[group, level], 1, 0)
        first = level * local
        gate = jnp.concatenate(
            [jnp.broadcast_to(gates[:, first + e : first + e + 1], (tile, FH)) for e in range(local)],
            axis=1,
        )
        sig = 1.0 / (1.0 + jnp.exp2(-LOG2E * pre_act))
        act_pre = pre_act * sig
        columns = slice(level * width, (level + 1) * width)
        active[:, columns] = (act_pre * gate).astype(jnp.bfloat16)
        product = grad_active * act_pre
        for e in range(local):
            gate_grads.append(
                jnp.sum(product[:, e * FH : (e + 1) * FH], axis=1, keepdims=True)
            )
        slope = sig * (1.0 + pre_act * (1.0 - sig))
        low_pre = (grad_active * gate * slope).astype(jnp.bfloat16)
        grad_pre[:, columns] = low_pre
        for group in range(groups):
            part = slice(group * depth, (group + 1) * depth)
            acc[:, part] += dot(low_pre, w_in[group, level], 1, 1)
    rows_out[:, :model] = acc[...].astype(jnp.bfloat16)
    spare = rows_out.shape[1] - model
    lane = lax.broadcasted_iota(jnp.int32, (tile, spare), 1) - head[0] * (levels * local)
    spread = jnp.zeros((tile, spare), jnp.float32)
    for e, column in enumerate(gate_grads):
        spread = jnp.where(lane == e, column, spread)
    rows_out[:, model:] = spread.astype(jnp.bfloat16)


def ffn_front(head, hidden, grads, w_in, w_out, gates, local):
    rows, wide = hidden.shape
    groups, levels, depth, width = w_in.shape
    tile = 512

    def by_row(columns):
        return pl.BlockSpec((tile, columns), lambda i, *_: (i, 0))

    whole = pl.BlockSpec(w_in.shape, lambda i, *_: (0, 0, 0, 0), pipeline_mode=pl.Buffered(1))
    grid_spec = pltpu.PrefetchScalarGridSpec(
        num_scalar_prefetch=1,
        grid=(rows // tile,),
        in_specs=[
            by_row(wide),
            by_row(groups * depth),
            whole,
            whole,
            by_row(gates.shape[1]),
        ],
        out_specs=[by_row(levels * width), by_row(levels * width), by_row(wide)],
        scratch_shapes=[pltpu.VMEM((tile, groups * depth), jnp.float32)],
    )
    hidden_units = jax.ShapeDtypeStruct((rows, levels * width), jnp.bfloat16)
    return pl.pallas_call(
        functools.partial(front_kernel, local),
        grid_spec=grid_spec,
        out_shape=[hidden_units, hidden_units, jax.ShapeDtypeStruct((rows, wide), jnp.bfloat16)],
        compiler_params=pltpu.CompilerParams(vmem_limit_bytes=58 * 2**20),
        cost_estimate=cost(6 * rows * groups * depth * levels * width, 3e7),
        name="ffn_front",
    )(head, hidden, grads, w_in, w_out, gates)


def rear_kernel(rows_in, hidden_units, weight_grads):
    groups, _, depth, _ = weight_grads.shape
    units = hidden_units[...]
    for group in range(groups):
        part = slice(group * depth, (group + 1) * depth)
        weight_grads[group, 0] = dot(rows_in[:, part], units, 0, 0).astype(jnp.bfloat16)


def normalized(rows, gain, bias):
    values = rows.astype(jnp.float32)
    centred = values - jnp.mean(values, axis=1, keepdims=True)
    inverse = lax.rsqrt(jnp.mean(centred * centred, axis=1, keepdims=True) + 1e-05)
    scaled = centred * inverse
    return scaled, inverse, (scaled * gain + bias).astype(jnp.bfloat16)


def project_kernel(
    levels, rows, w_value, w_query, w_key, routers, gain, bias, order, tables,
    query, key_value, projected, sigs, masks,
):
    count = rows.shape[0]
    piece = count // (levels * HEADS)
    _, _, normed = normalized(rows[...], gain[...], bias[...])
    query[...] = dot(normed, w_query[...], 1, 0).astype(jnp.bfloat16)
    key_value[:, :DH] = dot(normed, w_key[...], 1, 0).astype(jnp.bfloat16)
    sig = 1.0 / (1.0 + jnp.exp2(-LOG2E * dot(normed, routers[...], 1, 0)))
    sigs[...] = sig
    product = dot(rows[...], w_value[...], 1, 0)
    projected[...] = product
    at = lax.broadcasted_iota(jnp.int32, (count, count), 0)
    source = lax.rem(at // piece, levels) * HEADS + at // (piece * levels)
    here = (source * piece + lax.rem(at, piece) == order[0]).astype(jnp.bfloat16)
    lane = lax.broadcasted_iota(jnp.int32, (16, count), 0)
    table = tables[0]
    named = jnp.zeros((16, count), jnp.float32)
    for which in range(2):
        option = lane - which * VEXP
        for slot in range(2):
            pick = table[2 * which + slot : 2 * which + slot + 1, :]
            hit = (option == pick) & (option >= 0) & (option < VEXP)
            named = jnp.where(hit, 1.0, named)
    mask = dot(here, named.astype(jnp.bfloat16), 1, 1)
    masks[...] = mask
    value = jnp.zeros((count, DH), jnp.float32)
    for e in range(VEXP):
        gate = sig[:, e : e + 1] * mask[:, e : e + 1]
        value += gate * product[:, e * DH : (e + 1) * DH]
    key_value[:, DH:] = value.astype(jnp.bfloat16)


def project(rows, full, gain, bias, orders, tables, levels):
    total, width = rows.shape
    count = total // HEADS

    def by_row(columns):
        return pl.BlockSpec((count, columns), lambda i: (i, 0))

    def column(size, at):
        return pl.BlockSpec((width, size), lambda i: (0, at), pipeline_mode=pl.Buffered(1))

    line = pl.BlockSpec((1, width), lambda i: (0, 0))
    shapes = [(DH, jnp.bfloat16), (2 * DH, jnp.bfloat16), (VEXP * DH, jnp.float32)]
    shapes += [(128, jnp.float32), (16, jnp.float32)]
    return pl.pallas_call(
        functools.partial(project_kernel, levels),
        grid=(HEADS,),
        in_specs=[by_row(width), column(VEXP * DH, 0)]
        + [column(DH, 2 * VEXP + i) for i in range(3)]
        + [line, line]
        + [
            pl.BlockSpec((1, 1, count), lambda i: (i, 0, 0)),
            pl.BlockSpec((1,) + tables.shape[1:], lambda i: (i, 0, 0)),
        ],
        out_specs=[by_row(columns) for columns, _ in shapes],
        out_shape=[jax.ShapeDtypeStruct((total, columns), kind) for columns, kind in shapes],
        compiler_params=pltpu.CompilerParams(vmem_limit_bytes=48 * 2**20),
        cost_estimate=cost(2 * total * width * 1024, 2e7),
        name="project",
    )(rows, full, full, full, full, gain, bias, orders, tables)


def project_back_kernel(
    rows, grads, grad_query, out_logit, projected, sigs, masks,
    w_value, w_query, w_key, routers, gain, bias,
    grad_rows, weight_grads, acc, sums,
):
    at = pl.program_id(0)
    count = rows.shape[0]
    values = VEXP * DH

    @pl.when(at == 0)
    def _():
        acc[...] = jnp.zeros_like(acc)
        sums[...] = jnp.zeros_like(sums)

    scaled, inverse, normed = normalized(rows[...], gain[...], bias[...])
    grad_key = grads[:, :DH].astype(jnp.bfloat16)
    grad_value = grads[:, DH:]
    sig, mask = sigs[...], masks[...]
    lane = lax.broadcasted_iota(jnp.int32, (count, 128), 1)
    logits = out_logit[...].astype(jnp.float32)
    parts = []
    for e in range(VEXP):
        one, on = sig[:, e : e + 1], mask[:, e : e + 1]
        parts.append((one * on * grad_value).astype(jnp.bfloat16))
        inner = jnp.sum(grad_value * projected[:, e * DH : (e + 1) * DH], axis=1, keepdims=True)
        logits = jnp.where(lane == e, inner * one * (1.0 - one) * on, logits)
    grad_projected = jnp.concatenate(parts, axis=1)
    sides = jnp.concatenate([grad_query[...], grad_key, logits.astype(jnp.bfloat16)], axis=1)
    first = dot(sides[:, :DH], w_query[...], 1, 1)
    first += dot(sides[:, DH : 2 * DH], w_key[...], 1, 1)
    first += dot(sides[:, 2 * DH :], routers[...], 1, 1)
    sums[2 * VEXP : 2 * VEXP + 1, :] += jnp.sum(first * scaled, axis=0, keepdims=True)
    sums[2 * VEXP + 1 : 2 * VEXP + 2, :] += jnp.sum(first, axis=0, keepdims=True)
    inner_grad = first * gain[...]
    inner_grad = inverse * (
        inner_grad
        - jnp.mean(inner_grad, axis=1, keepdims=True)
        - scaled * jnp.mean(inner_grad * scaled, axis=1, keepdims=True)
    )
    grad_rows[...] = (inner_grad + dot(grad_projected, w_value[...], 1, 1)).astype(jnp.bfloat16)
    acc[:, :values] += dot(rows[...], grad_projected, 0, 0)
    acc[:, values:] += dot(normed, sides, 0, 0)

    @pl.when(at == pl.num_programs(0) - 1)
    def _():
        weight_grads[:, : values + 2 * DH] = acc[:, : values + 2 * DH].astype(jnp.bfloat16)
        last = acc[:, values + 2 * DH :] + sums[...].T
        weight_grads[:, values + 2 * DH :] = last.astype(jnp.bfloat16)


def project_back(rows, grads, grad_query, out_logit, projected, sigs, masks, full, gain, bias):
    total, width = rows.shape
    count = total // HEADS
    columns = VEXP * DH + 3 * DH

    def by_row(size):
        return pl.BlockSpec((count, size), lambda i: (i, 0))

    def column(size, at):
        return pl.BlockSpec((width, size), lambda i: (0, at), pipeline_mode=pl.Buffered(1))

    line = pl.BlockSpec((1, width), lambda i: (0, 0))
    return pl.pallas_call(
        project_back_kernel,
        grid=(HEADS,),
        in_specs=[by_row(width), by_row(2 * DH), by_row(DH), by_row(128), by_row(VEXP * DH)]
        + [by_row(128), by_row(16), column(VEXP * DH, 0)]
        + [column(DH, 2 * VEXP + i) for i in range(3)]
        + [line, line],
        out_specs=[by_row(width), pl.BlockSpec((width, columns), lambda i: (0, 0))],
        out_shape=[
            jax.ShapeDtypeStruct((total, width), jnp.bfloat16),
            jax.ShapeDtypeStruct((width, columns), jnp.bfloat16),
        ],
        scratch_shapes=[
            pltpu.VMEM((width, columns), jnp.float32),
            pltpu.VMEM((128, width), jnp.float32),
        ],
        compiler_params=pltpu.CompilerParams(vmem_limit_bytes=56 * 2**20),
        cost_estimate=cost(4 * total * width * 1024, 4e7),
        name="project_back",
    )(rows, grads, grad_query, out_logit, projected, sigs, masks, full, full, full, full, gain, bias)


def feed_kernel(rows_in, low_pre, active, w_out, weight_grads, feed, acc):
    groups, _, depth, _ = w_out.shape
    level = pl.program_id(0)
    units, act = low_pre[...], active[...]
    for group in range(groups):
        part = slice(group * depth, (group + 1) * depth)
        weight_grads[group, 0] = dot(rows_in[:, part], units, 0, 0).astype(jnp.bfloat16)
        fed = dot(act, w_out[group, 0], 1, 1)

        @pl.when(level == 0)
        def _():
            acc[:, part] = fed

        @pl.when(level > 0)
        def _():
            acc[:, part] += fed

    @pl.when(level == pl.num_programs(0) - 1)
    def _():
        feed[...] = acc[...].astype(jnp.bfloat16)


def whole_rows(rows, columns):
    return pl.BlockSpec((rows, columns), lambda i: (0, 0), pipeline_mode=pl.Buffered(1))


def ffn_feed(hidden, grad_pre, active, w_out):
    rows, wide = hidden.shape
    groups, levels, depth, width = w_out.shape
    by_level = pl.BlockSpec((rows, width), lambda i: (0, i))
    grads_spec = pl.BlockSpec((groups, 1, depth, width), lambda i: (0, i, 0, 0))
    return pl.pallas_call(
        feed_kernel,
        grid=(levels,),
        in_specs=[
            whole_rows(rows, wide),
            by_level,
            by_level,
            grads_spec,
        ],
        out_specs=[grads_spec, whole_rows(rows, groups * depth)],
        out_shape=[
            jax.ShapeDtypeStruct((groups, levels, depth, width), jnp.bfloat16),
            jax.ShapeDtypeStruct((rows, groups * depth), jnp.bfloat16),
        ],
        scratch_shapes=[pltpu.VMEM((rows, groups * depth), jnp.float32)],
        compiler_params=pltpu.CompilerParams(vmem_limit_bytes=58 * 2**20),
        cost_estimate=cost(6 * rows * groups * depth * levels * width, 3e7),
        name="ffn_feed",
    )(hidden, grad_pre, active, w_out)


def ffn_rear(rows_in, units, groups, levels):
    rows, wide = rows_in.shape
    width = units.shape[1] // levels
    depth = wide // groups
    return pl.pallas_call(
        rear_kernel,
        grid=(levels,),
        in_specs=[whole_rows(rows, wide), pl.BlockSpec((rows, width), lambda i: (0, i))],
        out_specs=pl.BlockSpec((groups, 1, depth, width), lambda i: (0, i, 0, 0)),
        out_shape=jax.ShapeDtypeStruct((groups, levels, depth, width), jnp.bfloat16),
        compiler_params=pltpu.CompilerParams(vmem_limit_bytes=58 * 2**20),
        cost_estimate=cost(4 * rows * groups * depth * levels * width, 3e7),
        name="ffn_rear",
    )(rows_in, units)


def chosen(routes, options):
    return jnp.sum(
        (routes[..., None] == jnp.arange(options, dtype=jnp.int32)).astype(jnp.float32), axis=-2
    )


def shift(value, axis, by):
    count = lax.axis_size(axis)
    pairs = [(i, i + by) for i in range(count) if 0 <= i + by < count]
    return lax.ppermute(value, axis, pairs)


def body(
    tokens_in,
    out_grad,
    deal_order,
    seq_lengths,
    value_routes,
    output_routes,
    ffn_routes,
    norm1_gain,
    norm1_bias,
    norm2_gain,
    norm2_bias,
    query_weight,
    key_weight,
    value_weight,
    output_weight,
    value_router,
    output_router,
    ffn_router,
    ffn_in,
    ffn_out,
):
    groups = lax.axis_size("group")
    levels = lax.axis_size("level")
    level = lax.axis_index("level")
    head = lax.axis_index("head")
    count, width = tokens_in.shape
    piece = count // (levels * HEADS)
    wrows = query_weight.shape[0]
    experts = ffn_router.shape[1]
    local_experts = ffn_in.shape[1] // FH

    small = jnp.concatenate(
        [
            ffn_router,
            norm1_gain[:, None],
            norm1_bias[:, None],
            norm2_gain[:, None],
            norm2_bias[:, None],
        ],
        axis=1,
    )
    shared = small.shape[1]
    pad = -(shared + 2 * VEXP) % 128
    packed = jnp.concatenate(
        [
            value_weight.reshape(wrows, HEADS, VEXP * DH),
            output_weight.reshape(wrows, HEADS, VEXP * DH),
            query_weight.reshape(wrows, HEADS, DH),
            key_weight.reshape(wrows, HEADS, DH),
            value_router.reshape(wrows, HEADS, VEXP),
            output_router.reshape(wrows, HEADS, VEXP),
            jnp.broadcast_to(small[:, None, :], (wrows, HEADS, shared)),
            jnp.zeros((wrows, HEADS, pad), jnp.bfloat16),
        ],
        axis=2,
    )
    cols = packed.shape[2]
    tables = jnp.concatenate(
        [value_routes.transpose(1, 2, 0), output_routes.transpose(1, 2, 0)], axis=1
    )
    picks = ffn_routes.reshape(levels, HEADS * piece, -1).transpose(0, 2, 1)
    arrived, own_grads, full, tables, picks, orders = start(
        tokens_in.reshape(levels, HEADS, piece, width),
        out_grad.reshape(levels, HEADS, piece, width),
        packed.transpose(1, 0, 2),
        tables,
        picks,
        deal_order,
    )
    worker_in = arrived.reshape(HEADS * count, width)
    own_tokens = lax.dynamic_index_in_dim(arrived, head, 1, keepdims=False).reshape(count, width)
    full = full.reshape(width, cols)

    base = 2 * DH + 2 * VEXP * DH
    w_output = full[:, VEXP * DH : 2 * VEXP * DH]
    at = base + 2 * VEXP
    r_ffn = full[:, at : at + experts]
    gain_one, bias_one, gain_two, bias_two = (
        full[:, at + experts + i].astype(jnp.float32) for i in range(4)
    )
    gain_row, bias_row = gain_one[None], bias_one[None]
    orders = orders.reshape(levels, HEADS, count)
    own_order = lax.dynamic_index_in_dim(orders, level, 0, keepdims=False)[:, None, :]
    queries, key_value, projected, sigs, masks = project(
        worker_in, full, gain_row, bias_row, own_order, tables, levels
    )

    rows = HEADS * count
    reach = -(-LMAX // rows)
    window = [key_value]
    own_grads = own_grads.reshape(count, width)
    cotangent = level_gather(own_grads, 5, True)
    for i in range(reach):
        came = shift(window[0], "level", 1)
        if i == 0:
            came, cotangent = lax.optimization_barrier((came, cotangent))
        window.insert(0, came)

    def gather_ffn(weight):
        whole = lax.all_gather(weight, ("group", "level"), axis=0)
        return whole.reshape((groups, levels) + weight.shape)

    w_in = gather_ffn(ffn_in)
    w_out = gather_ffn(ffn_out)

    ramp = jnp.arange(count, dtype=jnp.int32)

    def arrival(values):
        lead, shape = values.shape[:-3], values.shape[-1:]
        four = values.reshape(lead + (HEADS, levels, HEADS, piece) + shape)
        return jnp.swapaxes(four, -4, -3).reshape(lead + (rows,) + shape)

    orders = after(orders, key_value)
    orders = jnp.concatenate([jnp.zeros((reach, HEADS, count), jnp.int32), orders], axis=0)
    orders = lax.dynamic_slice_in_dim(orders, level, reach + 1, 0)
    here = orders[:, :, None, :] == ramp[None, None, :, None]
    inverse = jnp.sum(here * ramp, axis=3)
    shard = (level - reach + jnp.arange(reach + 1, dtype=jnp.int32))[:, None] * HEADS
    shard = shard + jnp.arange(HEADS, dtype=jnp.int32)[None, :]
    pos_all = jnp.where(shard[:, :, None] < 0, -1, shard[:, :, None] * count + inverse)
    pos_all = arrival(pos_all[..., None]).reshape(-1)
    positions = pos_all[reach * rows :]
    own_routes = picks.reshape(levels, -1, HEADS, piece).transpose(2, 0, 3, 1).reshape(count, -1)

    seq_ends = jnp.cumsum(seq_lengths[0])

    def starts_of(places):
        return jnp.max(jnp.where(seq_ends <= places[:, None], seq_ends, 0), axis=1)

    starts = starts_of(positions)
    blocks = rows // BLOCK
    base_block = (level - reach) * blocks
    first_block = starts_of(level * rows + jnp.arange(blocks, dtype=jnp.int32) * BLOCK) // BLOCK
    first_block = jnp.maximum(first_block - base_block, 0)

    def lines(values):
        return values.reshape(blocks, 1, BLOCK)

    attended, log_total = attend(
        first_block,
        queries,
        window,
        lines(positions),
        lines(starts),
        pos_all[:, None],
    )

    out_sig = sigs[:, VEXP : 2 * VEXP]
    out_mask = masks[:, VEXP : 2 * VEXP]
    out_gate = out_sig * out_mask
    mixed = low((out_gate[..., None] * attended[:, None, :]).reshape(rows, VEXP * DH))
    branch = low(level_scatter(low(transposed(mixed, w_output)), 2))
    middle = own_tokens.astype(jnp.float32) + branch.astype(jnp.float32)

    normed_mid, scaled_two, inverse_two = layer_norm(middle, gain_two, bias_two)
    normed_two = low(normed_mid)
    ffn_sig = jax.nn.sigmoid(matmul(normed_two, r_ffn))
    member = chosen(own_routes, experts)
    shares = (ffn_sig * member).reshape(count, levels, HEADS, local_experts)
    shares = jnp.swapaxes(shares, 1, 2).reshape(count, experts)
    spare = -experts % 128
    extended = jnp.concatenate([middle, shares], axis=1)
    hidden = level_gather(jnp.pad(low(extended), ((0, 0), (0, spare))), 3, True)
    mine = levels * local_experts
    gates = lax.dynamic_slice_in_dim(hidden, width + head * mine, mine, 1).astype(jnp.float32)
    active, grad_pre, grad_rows = ffn_front(
        head[None], hidden, cotangent, w_in, w_out, gates, local_experts
    )
    summed, beyond = pair_scatter(grad_rows, 4, True)
    came = to_far(beyond)
    grad_in, feed = ffn_feed(after(hidden, beyond), grad_pre, active, w_out)
    came, feed, grad_in = lax.optimization_barrier((came, feed, grad_in))
    summed = summed + came.astype(jnp.float32)

    gate_grads = summed[:, width : width + experts].reshape(count, HEADS, levels, local_experts)
    gate_grads = jnp.swapaxes(gate_grads, 1, 2).reshape(count, experts)
    grad_logit = low(gate_grads * ffn_sig * (1.0 - ffn_sig) * member)
    grad_second = transposed(grad_logit, r_ffn)
    grad_r_ffn = contract_rows(normed_two, grad_logit)
    grad_gain_two = jnp.sum(grad_second * scaled_two, axis=0)
    grad_bias_two = jnp.sum(grad_second, axis=0)
    grad_middle = (
        own_grads.astype(jnp.float32)
        + summed[:, :width]
        + norm_back(grad_second, gain_two, scaled_two, inverse_two)
    )

    own_branch = low(grad_middle)
    came = to_far(own_branch)
    grad_out = ffn_rear(after(cotangent, own_branch), active, groups, levels)
    came, grad_out = lax.optimization_barrier((came, grad_out))
    grad_branch = pair_gather(own_branch, came, 7)

    def sum_over_rows(grad):
        return lax.psum_scatter(grad, ("group", "level"), scatter_dimension=0)

    ffn_in_grad = sum_over_rows(grad_in.reshape((groups * levels,) + grad_in.shape[2:]))
    grad_mixed = matmul(grad_branch, w_output).reshape(rows, VEXP, DH)
    grad_out_gate = jnp.sum(grad_mixed * attended[:, None, :], axis=-1)
    grad_attended = low(jnp.sum(grad_mixed * out_gate[..., None], axis=1))
    grad_out_logit = low(grad_out_gate * out_sig * (1.0 - out_sig) * out_mask)
    row_inner = jnp.sum(grad_attended.astype(jnp.float32) * attended, axis=-1)
    grad_queries, *grad_window = attend_back(
        first_block,
        queries,
        window,
        grad_attended,
        lines(positions),
        lines(starts),
        log_total,
        lines(row_inner),
        pos_all[:, None],
    )
    came = shift(grad_window[0], "level", -1)
    fed, beyond = pair_scatter(after(feed, grad_queries), 6, True)
    grad_w_output = contract_rows(after(grad_branch, fed), mixed)
    early = jnp.concatenate(
        [
            low(grad_w_output),
            low(grad_r_ffn),
            low(grad_gain_two)[:, None],
            low(grad_bias_two)[:, None],
            jnp.zeros((width, -(experts + 2) % 128), jnp.bfloat16),
        ],
        axis=1,
    )
    for i in range(1, reach + 1):
        if i < reach:
            came, fed = lax.optimization_barrier((came, fed))
        else:
            came, early = lax.optimization_barrier((came, early))
        grad_both = grad_window[i].astype(jnp.float32) + came.astype(jnp.float32)
        if i < reach:
            grad_keys_sent = low(grad_both)
            came = shift(grad_keys_sent, "level", -1)
    fed_far = to_far(beyond)
    ffn_out_grad = sum_over_rows(grad_out.reshape((groups * levels,) + grad_out.shape[2:]))
    grad_inputs, late = project_back(
        worker_in,
        grad_both,
        grad_queries,
        jnp.pad(grad_out_logit, ((0, 0), (VEXP, 128 - 2 * VEXP))),
        projected,
        sigs,
        masks,
        full,
        gain_row,
        bias_row,
    )

    fed_far, grad_inputs = lax.optimization_barrier((fed_far, grad_inputs))
    layer_out = to_home(low(middle + fed + fed_far.astype(jnp.float32)))

    input_grad, owned, early = finish(
        grad_inputs.reshape(HEADS, HEADS, levels * piece, width),
        grad_middle.reshape(HEADS, levels * piece, width),
        late.reshape(groups, levels, HEADS, wrows, -1),
        early.reshape(groups, levels, HEADS, wrows, -1),
    )
    owned, early = owned.astype(jnp.float32), early.astype(jnp.float32)

    def columns(part, first, size):
        return part[:, :, first : first + size].transpose(1, 0, 2).reshape(wrows, HEADS * size)

    values = VEXP * DH
    misc = values + 2 * DH
    common = jnp.sum(early[:, :, values:], axis=0)
    norms = jnp.sum(owned[:, :, misc + 2 * VEXP :], axis=0)
    return (
        layer_out,
        input_grad.reshape(count, width),
        norms[:, 0],
        norms[:, 1],
        common[:, experts],
        common[:, experts + 1],
        columns(owned, values, DH),
        columns(owned, values + DH, DH),
        columns(owned, 0, values),
        columns(early, 0, values),
        columns(owned, misc, VEXP),
        columns(owned, misc + VEXP, VEXP),
        common[:, :experts],
        ffn_in_grad.astype(jnp.float32),
        ffn_out_grad.astype(jnp.float32),
    )


def solution(mesh):
    groups, shards = mesh.devices.shape
    fine = Mesh(mesh.devices.reshape(groups, shards // HEADS, HEADS), TOK)
    two, one, three = P(TOK, None), P(TOK), P(TOK, None, None)
    ffn = P("group", ("level", "head"))
    return jax.shard_map(
        body,
        mesh=fine,
        in_specs=(two, two, two, P("group", None), three, three, two, one, one, one, one)
        + (two,) * 7
        + (ffn, ffn),
        out_specs=(two, two, one, one, one, one) + (two,) * 7 + (ffn, ffn),
        check_vma=False,
    )
```

```python
import functools

import jax
import jax.numpy as jnp
from jax import lax
from jax.experimental import pallas as pl
from jax.experimental.pallas import tpu as pltpu
from jax.sharding import Mesh, PartitionSpec as P

HEADS = 4
DH = 128
VEXP = 5
FH = 128
LMAX = 4096

TOK = ("group", "level", "head")


def matmul(left_side, right_side):
    return jnp.dot(left_side, right_side, preferred_element_type=jnp.float32)


def transposed(left_side, right_side):
    return lax.dot_general(
        left_side, right_side, (((1,), (1,)), ((), ())), preferred_element_type=jnp.float32
    )


def contract_rows(left_side, right_side):
    return lax.dot_general(
        left_side, right_side, (((0,), (0,)), ((), ())), preferred_element_type=jnp.float32
    )


def low(value):
    return value.astype(jnp.bfloat16)


def layer_norm(inputs, gain_vec, bias_vec):
    centred = inputs - jnp.mean(inputs, axis=-1, keepdims=True)
    inverse = lax.rsqrt(jnp.mean(centred * centred, axis=-1, keepdims=True) + 1e-05)
    scaled = centred * inverse
    return (scaled * gain_vec + bias_vec, scaled, inverse)


def norm_back(grad_normed, gain_vec, scaled, inverse):
    inner_grad = grad_normed * gain_vec
    return inverse * (
        inner_grad
        - jnp.mean(inner_grad, axis=-1, keepdims=True)
        - scaled * jnp.mean(inner_grad * scaled, axis=-1, keepdims=True)
    )


def to_home(rows):
    levels = lax.axis_size("level")
    count = rows.shape[0]
    out = rows.reshape(HEADS, levels, count // levels // HEADS, -1).transpose(1, 0, 2, 3)
    back = lax.all_to_all(
        out.reshape(levels, count // levels, -1), "level", split_axis=0, concat_axis=0, tiled=True
    )
    return back.reshape(count, -1)


MESH = pl.DeviceIdType.MESH


def partners(head):
    near = head + 1 - 2 * lax.rem(head, 2)
    far = lax.rem(head + 2, HEADS)
    return near, far


def greet(near, far):
    barrier = pltpu.get_barrier_semaphore()
    for peer in (near, far):
        pl.semaphore_signal(barrier, inc=1, device_id={"head": peer}, device_id_type=MESH)
    pl.semaphore_wait(barrier, 2)


def remote(src, dst, send, recv, peer):
    return pltpu.make_async_remote_copy(
        src_ref=src,
        dst_ref=dst,
        send_sem=send,
        recv_sem=recv,
        device_id={"head": peer},
        device_id_type=MESH,
    )


def cost(flops, moved):
    return pl.CostEstimate(flops=int(flops), bytes_accessed=int(moved), transcendentals=0)


def gather_kernel(
    by_source, own, out, local_sem, near_send, near_recv, far_send, far_recv, pass_send, pass_recv
):
    head = lax.axis_index("head")
    near, far = partners(head)
    greet(near, far)

    def spot(i, source):
        return out.at[source, i] if by_source else out.at[i, source]

    pieces = range(HEADS)
    to_far = [remote(own.at[i], spot(i, head), far_send.at[i], far_recv.at[i], far) for i in pieces]
    to_near = [
        remote(own.at[i], spot(i, head), near_send.at[i], near_recv.at[i], near) for i in pieces
    ]
    passed = [
        remote(spot(i, far), spot(i, far), pass_send.at[i], pass_recv.at[i], near) for i in pieces
    ]
    kept = [pltpu.make_async_copy(own.at[i], spot(i, head), local_sem.at[i]) for i in pieces]
    for copy in to_far + to_near + kept:
        copy.start()
    for i in pieces:
        to_far[i].wait_recv()
        passed[i].start()
    for i in pieces:
        to_near[i].wait_recv()
        passed[i].wait_recv()
        kept[i].wait()
        to_far[i].wait_send()
        to_near[i].wait_send()
        passed[i].wait_send()


def level_gather(rows, collective_id, by_source=False):
    count, width = rows.shape
    whole = pl.pallas_call(
        functools.partial(gather_kernel, by_source),
        out_shape=jax.ShapeDtypeStruct((HEADS, HEADS, count // HEADS, width), rows.dtype),
        in_specs=[pl.BlockSpec(memory_space=pltpu.VMEM)],
        out_specs=pl.BlockSpec(memory_space=pl.ANY),
        scratch_shapes=[pltpu.SemaphoreType.DMA((HEADS,))] * 7,
        compiler_params=pltpu.CompilerParams(collective_id=collective_id, has_side_effects=True),
        cost_estimate=cost(0, 90e6),
        name="level_gather",
    )(rows.reshape(HEADS, count // HEADS, width))
    return whole.reshape(HEADS * count, width)


def scatter_kernel(
    by_source, part, out, near_buf, send_buf, far_buf, near_send, near_recv, far_send, far_recv
):
    head = lax.axis_index("head")
    near, far = partners(head)
    greet(near, far)
    across = HEADS - 1 - head
    pieces = range(HEADS)

    def spot(i, dest):
        return (dest, i) if by_source else (i, dest)

    def to_near(slot, i, dest):
        return remote(
            part.at[spot(i, dest)],
            near_buf.at[slot, i],
            near_send.at[slot, i],
            near_recv.at[slot, i],
            near,
        )

    first = [to_near(0, i, across) for i in pieces]
    second = [to_near(1, i, near) for i in pieces]
    onward = [
        remote(send_buf.at[i], far_buf.at[i], far_send.at[i], far_recv.at[i], far) for i in pieces
    ]
    for copy in first + second:
        copy.start()
    for i in pieces:
        first[i].wait_recv()
        both = part[spot(i, far)].astype(jnp.float32) + near_buf[0, i].astype(jnp.float32)
        send_buf[i] = both.astype(jnp.bfloat16)
        onward[i].start()
    for i in pieces:
        second[i].wait_recv()
        out[i] = part[spot(i, head)].astype(jnp.float32) + near_buf[1, i].astype(jnp.float32)
    for i in pieces:
        onward[i].wait_recv()
        out[i] = out[i] + far_buf[i].astype(jnp.float32)
    for i in pieces:
        first[i].wait_send()
        second[i].wait_send()
        onward[i].wait_send()


def level_scatter(rows, collective_id, by_source=False):
    total, width = rows.shape
    piece = total // (HEADS * HEADS)
    low_type = jnp.bfloat16
    mine = pl.pallas_call(
        functools.partial(scatter_kernel, by_source),
        out_shape=jax.ShapeDtypeStruct((HEADS, piece, width), jnp.float32),
        in_specs=[pl.BlockSpec(memory_space=pltpu.VMEM)],
        out_specs=pl.BlockSpec(memory_space=pltpu.VMEM),
        scratch_shapes=[
            pltpu.VMEM((2, HEADS, piece, width), low_type),
            pltpu.VMEM((HEADS, piece, width), low_type),
            pltpu.VMEM((HEADS, piece, width), low_type),
            pltpu.SemaphoreType.DMA((2, HEADS)),
            pltpu.SemaphoreType.DMA((2, HEADS)),
            pltpu.SemaphoreType.DMA((HEADS,)),
            pltpu.SemaphoreType.DMA((HEADS,)),
        ],
        compiler_params=pltpu.CompilerParams(
            collective_id=collective_id, has_side_effects=True, vmem_limit_bytes=32 * 2**20
        ),
        cost_estimate=cost(0, 80e6),
        name="level_scatter",
    )(rows.reshape(HEADS, HEADS, piece, width))
    return mine.reshape(HEADS * piece, width)


def meet(near):
    barrier = pltpu.get_barrier_semaphore()
    pl.semaphore_signal(barrier, inc=1, device_id={"head": near}, device_id_type=MESH)
    pl.semaphore_wait(barrier, 1)


def pair_scatter_kernel(by_source, part, out, out_far, near_buf, send, recv):
    head = lax.axis_index("head")
    near, far = partners(head)
    meet(near)
    across = HEADS - 1 - head
    pieces = range(HEADS)

    def spot(i, dest):
        return (dest, i) if by_source else (i, dest)

    def to_near(slot, i, dest):
        return remote(
            part.at[spot(i, dest)], near_buf.at[slot, i], send.at[slot, i], recv.at[slot, i], near
        )

    first = [to_near(0, i, across) for i in pieces]
    second = [to_near(1, i, near) for i in pieces]
    for copy in first + second:
        copy.start()
    for i in pieces:
        first[i].wait_recv()
        both = part[spot(i, far)].astype(jnp.float32) + near_buf[0, i].astype(jnp.float32)
        out_far[i] = both.astype(jnp.bfloat16)
    for i in pieces:
        second[i].wait_recv()
        out[i] = part[spot(i, head)].astype(jnp.float32) + near_buf[1, i].astype(jnp.float32)
    for i in pieces:
        first[i].wait_send()
        second[i].wait_send()


def pair_scatter(rows, collective_id, by_source=False):
    total, width = rows.shape
    piece = total // (HEADS * HEADS)
    mine, other = pl.pallas_call(
        functools.partial(pair_scatter_kernel, by_source),
        out_shape=[
            jax.ShapeDtypeStruct((HEADS, piece, width), jnp.float32),
            jax.ShapeDtypeStruct((HEADS, piece, width), jnp.bfloat16),
        ],
        in_specs=[pl.BlockSpec(memory_space=pltpu.VMEM)],
        out_specs=[pl.BlockSpec(memory_space=pltpu.VMEM)] * 2,
        scratch_shapes=[
            pltpu.VMEM((2, HEADS, piece, width), jnp.bfloat16),
            pltpu.SemaphoreType.DMA((2, HEADS)),
            pltpu.SemaphoreType.DMA((2, HEADS)),
        ],
        compiler_params=pltpu.CompilerParams(
            collective_id=collective_id, has_side_effects=True, vmem_limit_bytes=32 * 2**20
        ),
        cost_estimate=cost(0, 25e6),
        name="pair_scatter",
    )(rows.reshape(HEADS, HEADS, piece, width))
    return mine.reshape(HEADS * piece, width), other.reshape(HEADS * piece, width)


def pair_gather_kernel(by_source, own, other, out, local_sem, send, recv):
    head = lax.axis_index("head")
    near, far = partners(head)
    meet(near)
    copies, kept = [], []
    for i in range(HEADS):
        for slot, (block, source) in enumerate(((own, head), (other, far))):
            place = out.at[source, i] if by_source else out.at[i, source]
            copies.append(
                remote(block.at[i], place, send.at[slot, i], recv.at[slot, i], near)
            )
            kept.append(pltpu.make_async_copy(block.at[i], place, local_sem.at[slot, i]))
    for copy in copies + kept:
        copy.start()
    for copy in copies + kept:
        copy.wait()


def pair_gather(own, other, collective_id, by_source=False):
    count, width = own.shape
    split = (HEADS, count // HEADS, width)
    whole = pl.pallas_call(
        functools.partial(pair_gather_kernel, by_source),
        out_shape=jax.ShapeDtypeStruct((HEADS,) + split, own.dtype),
        in_specs=[pl.BlockSpec(memory_space=pltpu.VMEM)] * 2,
        out_specs=pl.BlockSpec(memory_space=pl.ANY),
        scratch_shapes=[pltpu.SemaphoreType.DMA((2, HEADS))] * 3,
        compiler_params=pltpu.CompilerParams(collective_id=collective_id, has_side_effects=True),
        cost_estimate=cost(0, 25e6),
        name="pair_gather",
    )(own.reshape(split), other.reshape(split))
    return whole.reshape(HEADS * count, width)


def to_far(rows):
    return lax.ppermute(rows, "head", [(i, (i + 2) % HEADS) for i in range(HEADS)])


def after(value, *others):
    return lax.optimization_barrier((value,) + others)[0]


def ring(axis):
    me, size = lax.axis_index(axis), lax.axis_size(axis)
    ahead = [lax.rem(me + k, size) for k in range(1, size)]
    behind = [lax.rem(me + size - k, size) for k in range(1, size)]
    return me, ahead, behind


def reach_out(src, dst, send, recv, peer):
    return pltpu.make_async_remote_copy(
        src_ref=src, dst_ref=dst, send_sem=send, recv_sem=recv, device_id=peer, device_id_type=MESH
    )


def greet_all(peers):
    barrier = pltpu.get_barrier_semaphore()
    for peer in peers:
        pl.semaphore_signal(barrier, inc=1, device_id=peer, device_id_type=MESH)
    pl.semaphore_wait(barrier, len(peers))


def start_kernel(
    tokens, cotangents, weights, tables, picks, order,
    rows, grads, full, routes, chosen_rows, orders, own_sem, *sems
):
    sems = iter(sems)

    def pair():
        return next(sems), next(sems)

    group, groups_ahead, _ = ring("group")
    level, levels_ahead, levels_behind = ring("level")
    head = lax.axis_index("head")
    near, far = partners(head)
    mates = [near, far, HEADS - 1 - head]
    greet_all(
        [{"head": m} for m in mates]
        + [{"level": n} for n in levels_ahead]
        + [{"group": n} for n in groups_ahead]
    )
    started = []

    def send(src, dst, send_sem, recv_sem, peer):
        copy = reach_out(src, dst, send_sem, recv_sem, peer)
        copy.start()
        started.append(copy)
        return copy

    out_s, out_r = pair()
    pick_s, pick_r = pair()
    crossing, picking = [], []
    for k, to in enumerate(levels_ahead):
        peer = {"level": to}
        crossing.append(send(tokens.at[to], rows.at[:, head, level], out_s.at[k], out_r.at[k], peer))
    mate_s, mate_r = pair()
    table_s, table_r = pair()
    order_s, order_r = pair()
    to_mates, order_mates, table_mates = [], [], []
    for k, to in enumerate(mates):
        peer = {"head": to}
        to_mates.append(
            send(weights.at[to], full.at[group, level, head], mate_s.at[k], mate_r.at[k], peer)
        )
        order_mates.append(
            send(order, orders.at[level, head], order_s.at[k], order_r.at[k], peer)
        )
    own = [
        (tokens.at[level], rows.at[:, head, level]),
        (weights.at[head], full.at[group, level, head]),
        (tables.at[head], routes.at[head]),
        (picks.at[level], chosen_rows.at[level]),
        (order, orders.at[level, head]),
        (cotangents.at[level], grads.at[:, level]),
    ]
    own = [pltpu.make_async_copy(src, dst, own_sem.at[i]) for i, (src, dst) in enumerate(own)]
    for copy in own:
        copy.start()
    far_s, far_r = pair()
    near_s, near_r = pair()
    pass_s, pass_r = pair()
    to_far, to_near = [], []

    def share(k, src, source):
        place = rows.at[:, head, source]
        to_far.append(send(src, place, far_s.at[k], far_r.at[k], {"head": far}))
        to_near.append(send(src, place, near_s.at[k], near_r.at[k], {"head": near}))

    share(0, tokens.at[level], level)
    block_s, block_r = pair()
    group_s, group_r = pair()
    orders_s, orders_r = pair()
    for copy in to_mates:
        copy.wait_recv()
    own[1].wait()
    blocks, grouped, ordered = [], [], []

    def to_groups(j, source):
        for k, to in enumerate(groups_ahead):
            block = full.at[group, source]
            grouped.append(
                send(block, block, group_s.at[k, j], group_r.at[k, j], {"group": to})
            )

    for k, to in enumerate(levels_ahead):
        block = full.at[group, level]
        blocks.append(send(block, block, block_s.at[k], block_r.at[k], {"level": to}))
    to_groups(0, level)
    for k, to in enumerate(mates):
        table_mates.append(
            send(tables.at[to], routes.at[head], table_s.at[k], table_r.at[k], {"head": to})
        )
    for k, to in enumerate(levels_ahead):
        picking.append(
            send(picks.at[to], chosen_rows.at[level], pick_s.at[k], pick_r.at[k], {"level": to})
        )
    for copy in order_mates:
        copy.wait_recv()
    own[4].wait()
    for k, to in enumerate(levels_ahead):
        block = orders.at[level]
        ordered.append(send(block, block, orders_s.at[k], orders_r.at[k], {"level": to}))
    for k, source in enumerate(levels_behind):
        crossing[k].wait_recv()
        share(k + 1, rows.at[:, head, source], source)
    grad_s, grad_r = pair()
    crossed = []
    for k, to in enumerate(levels_ahead):
        crossed.append(
            send(cotangents.at[to], grads.at[:, level], grad_s.at[k], grad_r.at[k], {"level": to})
        )
    for k, source in enumerate(levels_behind):
        blocks[k].wait_recv()
        to_groups(k + 1, source)
    passed = []
    for k, source in enumerate([level] + levels_behind):
        to_far[k].wait_recv()
        place = rows.at[:, far, source]
        passed.append(send(place, place, pass_s.at[k], pass_r.at[k], {"head": near}))
    for copy in to_near + passed + grouped + table_mates + picking + ordered + crossed:
        copy.wait_recv()
    for copy in started:
        copy.wait_send()
    for i in (0, 2, 3, 5):
        own[i].wait()


def start(tokens, cotangents, weights, tables, picks, order):
    groups, levels = lax.axis_size("group"), lax.axis_size("level")
    _, _, piece, width = tokens.shape
    shapes = [
        jax.ShapeDtypeStruct((HEADS, HEADS, levels, piece, width), tokens.dtype),
        jax.ShapeDtypeStruct((HEADS, levels, piece, width), tokens.dtype),
        jax.ShapeDtypeStruct((groups, levels) + weights.shape, weights.dtype),
        jax.ShapeDtypeStruct(tables.shape, tables.dtype),
        jax.ShapeDtypeStruct(picks.shape, picks.dtype),
        jax.ShapeDtypeStruct((levels, HEADS) + order.shape, order.dtype),
    ]
    dma = pltpu.SemaphoreType.DMA
    others, mates = (levels - 1,), (HEADS - 1,)
    counts = [others] * 2 + [mates] * 3 + [(levels,)] * 3
    counts += [others, (groups - 1, levels), others, others]
    return pl.pallas_call(
        start_kernel,
        out_shape=shapes,
        in_specs=[pl.BlockSpec(memory_space=pltpu.VMEM)] * 6,
        out_specs=[pl.BlockSpec(memory_space=pl.ANY)] * 6,
        scratch_shapes=[dma((6,))] + [dma(c) for c in counts for _ in range(2)],
        compiler_params=pltpu.CompilerParams(collective_id=9, has_side_effects=True),
        cost_estimate=cost(0, 200e6),
        name="start",
    )(tokens, cotangents, weights, tables, picks, order)


def finish_kernel(count, *refs):
    refs = iter(refs)

    def take(n):
        return [next(refs) for _ in range(n)]

    part, middle = take(2)
    grads = take(count)
    (home_grad,) = take(1)
    owned = take(count)
    near_buf, send_buf, far_buf, total, back_buf, came_buf = take(6)
    group_buf, level_send, level_buf, head_send = (take(count) for _ in range(4))

    def pair():
        return next(refs), next(refs)

    group, groups_ahead, _ = ring("group")
    level, levels_ahead, levels_behind = ring("level")
    head = lax.axis_index("head")
    near, far = partners(head)
    across = HEADS - 1 - head
    mates = [near, far, across]
    greet_all(
        [{"head": m} for m in mates]
        + [{"level": n} for n in levels_ahead]
        + [{"group": n} for n in groups_ahead]
    )
    started = []

    def send(src, dst, send_sem, recv_sem, peer):
        copy = reach_out(src, dst, send_sem, recv_sem, peer)
        copy.start()
        started.append(copy)
        return copy

    pieces = range(HEADS)
    sets = range(count)
    near_s, near_r = pair()
    far_s, far_r = pair()
    back_s, back_r = pair()
    group_s, group_r = pair()
    level_s, level_r = pair()
    mate_s, mate_r = pair()
    first, second, onward = [], [], []
    for slot, (dest, copies) in enumerate(((across, first), (near, second))):
        for i in pieces:
            copies.append(
                send(
                    part.at[i, dest],
                    near_buf.at[slot, i],
                    near_s.at[slot, i],
                    near_r.at[slot, i],
                    {"head": near},
                )
            )
    order = levels_ahead + [level]
    grouped = {}
    for j, dest in enumerate(order):
        for p in sets:
            grouped[j, p] = [
                send(
                    grads[p].at[to, dest],
                    group_buf[p].at[k, j],
                    group_s.at[p, k, j],
                    group_r.at[p, k, j],
                    {"group": to},
                )
                for k, to in enumerate(groups_ahead)
            ]
    for i in pieces:
        first[i].wait_recv()
        both = part[i, far].astype(jnp.float32) + near_buf[0, i].astype(jnp.float32)
        send_buf[i] = both.astype(jnp.bfloat16)
        onward.append(send(send_buf.at[i], far_buf.at[i], far_s.at[i], far_r.at[i], {"head": far}))
    for i in pieces:
        second[i].wait_recv()
        both = part[i, head].astype(jnp.float32) + near_buf[1, i].astype(jnp.float32)
        total[i] = both + middle[i]
    leveled = {}
    for j, dest in enumerate(order):
        for p in sets:
            amount = grads[p][group, dest].astype(jnp.float32)
            for k, copy in enumerate(grouped[j, p]):
                copy.wait_recv()
                amount = amount + group_buf[p][k, j].astype(jnp.float32)
            level_send[p][j] = amount.astype(jnp.bfloat16)
            if j < len(levels_ahead):
                leveled[j, p] = send(
                    level_send[p].at[j],
                    level_buf[p].at[j],
                    level_s.at[p, j],
                    level_r.at[p, j],
                    {"level": dest},
                )
    for i in pieces:
        onward[i].wait_recv()
        both = total[i] + far_buf[i].astype(jnp.float32)
        back_buf[i] = both.astype(jnp.bfloat16).reshape(back_buf.shape[1:])
    backs = [
        send(back_buf.at[:, to], came_buf.at[level], back_s.at[k], back_r.at[k], {"level": to})
        for k, to in enumerate(levels_ahead)
    ]
    sharing = []
    for p in sets:
        amount = level_send[p][len(levels_ahead)].astype(jnp.float32)
        for j in range(len(levels_ahead)):
            leveled[j, p].wait_recv()
            amount = amount + level_buf[p][j].astype(jnp.float32)
        head_send[p][...] = amount.astype(jnp.bfloat16)
        sharing += [
            send(
                head_send[p].at[to],
                owned[p].at[head],
                mate_s.at[p, k],
                mate_r.at[p, k],
                {"head": to},
            )
            for k, to in enumerate(mates)
        ]
        owned[p][head] = head_send[p][head]
    home_grad[level] = back_buf[:, level].astype(jnp.float32)
    for k, source in enumerate(levels_behind):
        backs[k].wait_recv()
        home_grad[source] = came_buf[source].astype(jnp.float32)
    for copy in sharing:
        copy.wait_recv()
    for copy in started:
        copy.wait_send()


def finish(part, middle, *grads):
    groups, levels = lax.axis_size("group"), lax.axis_size("level")
    _, count, width = middle.shape
    piece = count // levels
    low_type = jnp.bfloat16
    blocks = [grad.shape[2:] for grad in grads]
    sets = len(grads)
    dma = pltpu.SemaphoreType.DMA
    counts = [(2, HEADS), (HEADS,), (levels - 1,)]
    counts += [(sets, groups - 1, levels), (sets, levels - 1), (sets, HEADS - 1)]
    vmem = pl.BlockSpec(memory_space=pltpu.VMEM)
    return pl.pallas_call(
        functools.partial(finish_kernel, sets),
        out_shape=[jax.ShapeDtypeStruct((levels, HEADS, piece, width), jnp.float32)]
        + [jax.ShapeDtypeStruct(block, low_type) for block in blocks],
        in_specs=[vmem] * (2 + sets),
        out_specs=[vmem] * (1 + sets),
        scratch_shapes=[
            pltpu.VMEM((2, HEADS, count, width), low_type),
            pltpu.VMEM((HEADS, count, width), low_type),
            pltpu.VMEM((HEADS, count, width), low_type),
            pltpu.VMEM((HEADS, count, width), jnp.float32),
            pltpu.VMEM((HEADS, levels, piece, width), low_type),
            pltpu.VMEM((levels, HEADS, piece, width), low_type),
        ]
        + [pltpu.VMEM((groups - 1, levels) + block, low_type) for block in blocks]
        + [pltpu.VMEM((levels,) + block, low_type) for block in blocks]
        + [pltpu.VMEM((levels - 1,) + block, low_type) for block in blocks]
        + [pltpu.VMEM(block, low_type) for block in blocks]
        + [dma(c) for c in counts for _ in range(2)],
        compiler_params=pltpu.CompilerParams(
            collective_id=10, has_side_effects=True, vmem_limit_bytes=56 * 2**20
        ),
        cost_estimate=cost(0, 200e6),
        name="finish",
    )(part, middle, *grads)


BLOCK = 512
LOG2E = 1.4426950408889634


def dot(left_side, right_side, left_dim, right_dim):
    return lax.dot_general(
        left_side,
        right_side,
        (((left_dim,), (right_dim,)), ((), ())),
        preferred_element_type=jnp.float32,
    )


def attend_kernel(parts, first, q, *refs):
    keys, values = refs[:parts], refs[parts : 2 * parts]
    pos_q, start_q, pos_k, out, lse, top, total, acc = refs[2 * parts :]
    at = pl.program_id(0)
    blocks = pl.num_programs(0)
    rate = LOG2E * DH ** (-0.5)
    top[...] = jnp.full_like(top, -1e30)
    total[...] = jnp.zeros_like(total)
    acc[...] = jnp.zeros_like(acc)
    query = q[...]
    row_at, row_from = pos_q[0], start_q[0]

    for part in range(parts):

        def step(block, carry, k=keys[part], v=values[part], part=part):
            rows = pl.ds(pl.multiple_of(block * BLOCK, BLOCK), BLOCK)
            spot = pl.ds(pl.multiple_of((part * blocks + block) * BLOCK, BLOCK), BLOCK)
            scores = dot(k[rows, :], query, 1, 1)
            key_at = pos_k[spot, :]
            scores = jnp.where((key_at >= row_from) & (key_at <= row_at), scores, -1e30)
            old = top[...]
            new = jnp.maximum(old, jnp.max(scores, axis=0, keepdims=True))
            shrink = jnp.exp2((old - new) * rate)
            weight = jnp.exp2((scores - new) * rate)
            total[...] = total[...] * shrink + jnp.sum(weight, axis=0, keepdims=True)
            acc[...] = acc[...] * shrink + dot(v[rows, :], weight.astype(jnp.bfloat16), 0, 0)
            top[...] = new
            return carry

        begin = jnp.maximum(first[at] - part * blocks, 0)
        end = at + 1 if part == parts - 1 else blocks
        lax.fori_loop(begin, end, step, 0)
    out[...] = (acc[...] / total[...]).T
    lse[0] = top[...] * rate + jnp.log2(total[...])


def attend(first, queries, window, pos_q, start_q, pos_k):
    rows = queries.shape[0]
    parts = len(window)
    line = pl.BlockSpec((1, 1, BLOCK), lambda i, *_: (i, 0, 0))
    grid_spec = pltpu.PrefetchScalarGridSpec(
        num_scalar_prefetch=1,
        grid=(rows // BLOCK,),
        in_specs=[pl.BlockSpec((BLOCK, DH), lambda i, *_: (i, 0))]
        + [pl.BlockSpec((rows, DH), lambda i, *_: (0, 0))] * parts
        + [pl.BlockSpec((rows, DH), lambda i, *_: (0, 1))] * parts
        + [line, line, pl.BlockSpec((parts * rows, 1), lambda i, *_: (0, 0))],
        out_specs=[pl.BlockSpec((BLOCK, DH), lambda i, *_: (i, 0)), line],
        scratch_shapes=[
            pltpu.VMEM((1, BLOCK), jnp.float32),
            pltpu.VMEM((1, BLOCK), jnp.float32),
            pltpu.VMEM((DH, BLOCK), jnp.float32),
        ],
    )
    return pl.pallas_call(
        functools.partial(attend_kernel, parts),
        grid_spec=grid_spec,
        out_shape=[
            jax.ShapeDtypeStruct((rows, DH), jnp.float32),
            jax.ShapeDtypeStruct((rows // BLOCK, 1, BLOCK), jnp.float32),
        ],
        compiler_params=pltpu.CompilerParams(vmem_limit_bytes=48 * 2**20),
        cost_estimate=cost(2e10, 1e7),
        name="attend",
    )(first, queries, *window, *window, pos_q, start_q, pos_k)


def attend_back_kernel(parts, first, q, *refs):
    keys, values = refs[:parts], refs[parts : 2 * parts]
    grad, pos_q, start_q, lse, inner, pos_k, grad_q = refs[2 * parts : 2 * parts + 7]
    grads = refs[2 * parts + 7 : 3 * parts + 7]
    sum_k, sum_v, acc = refs[3 * parts + 7 :]
    at = pl.program_id(0)
    blocks = pl.num_programs(0)
    rate = LOG2E * DH ** (-0.5)
    scale = DH ** (-0.5)

    @pl.when(at == 0)
    def _():
        sum_k[...] = jnp.zeros_like(sum_k)
        sum_v[...] = jnp.zeros_like(sum_v)

    acc[...] = jnp.zeros_like(acc)
    query, grad_out = q[...], grad[...]
    row_at, row_from, row_lse, row_inner = pos_q[0], start_q[0], lse[0], inner[0]

    for part in range(parts):

        def step(block, carry, k=keys[part], v=values[part], part=part):
            rows = pl.ds(pl.multiple_of(block * BLOCK, BLOCK), BLOCK)
            spot = pl.ds(pl.multiple_of((part * blocks + block) * BLOCK, BLOCK), BLOCK)
            key, value = k[rows, :], v[rows, :]
            scores = dot(key, query, 1, 1)
            key_at = pos_k[spot, :]
            seen = (key_at >= row_from) & (key_at <= row_at)
            soft = jnp.where(seen, jnp.exp2(scores * rate - row_lse), 0.0)
            grad_soft = dot(value, grad_out, 1, 1)
            grad_scores = (soft * (grad_soft - row_inner)).astype(jnp.bfloat16)
            sum_v[spot, :] += dot(soft.astype(jnp.bfloat16), grad_out, 1, 0)
            sum_k[spot, :] += dot(grad_scores, query, 1, 0)
            acc[...] += dot(grad_scores, key, 0, 0)
            return carry

        begin = jnp.maximum(first[at] - part * blocks, 0)
        end = at + 1 if part == parts - 1 else blocks
        lax.fori_loop(begin, end, step, 0)
    grad_q[...] = (acc[...] * scale).astype(jnp.bfloat16)

    @pl.when(at == blocks - 1)
    def _():
        size = grads[0].shape[0]
        for part in range(parts):
            spot = slice(part * size, (part + 1) * size)
            grads[part][:, :DH] = (sum_k[spot, :] * scale).astype(grads[part].dtype)
            grads[part][:, DH:] = sum_v[spot, :].astype(grads[part].dtype)


def attend_back(first, queries, window, grads, pos_q, start_q, lse, inner, pos_k):
    rows = queries.shape[0]
    parts = len(window)
    block = pl.BlockSpec((BLOCK, DH), lambda i, *_: (i, 0))
    line = pl.BlockSpec((1, 1, BLOCK), lambda i, *_: (i, 0, 0))
    grid_spec = pltpu.PrefetchScalarGridSpec(
        num_scalar_prefetch=1,
        grid=(rows // BLOCK,),
        in_specs=[block]
        + [pl.BlockSpec((rows, DH), lambda i, *_: (0, 0))] * parts
        + [pl.BlockSpec((rows, DH), lambda i, *_: (0, 1))] * parts
        + [block, line, line, line, line]
        + [pl.BlockSpec((parts * rows, 1), lambda i, *_: (0, 0))],
        out_specs=[block] + [pl.BlockSpec((rows, 2 * DH), lambda i, *_: (0, 0))] * parts,
        scratch_shapes=[
            pltpu.VMEM((parts * rows, DH), jnp.float32),
            pltpu.VMEM((parts * rows, DH), jnp.float32),
            pltpu.VMEM((BLOCK, DH), jnp.float32),
        ],
    )
    kinds = [jnp.bfloat16] * (parts - 1) + [jnp.float32]
    return pl.pallas_call(
        functools.partial(attend_back_kernel, parts),
        grid_spec=grid_spec,
        out_shape=[jax.ShapeDtypeStruct((rows, DH), jnp.bfloat16)]
        + [jax.ShapeDtypeStruct((rows, 2 * DH), kind) for kind in kinds],
        compiler_params=pltpu.CompilerParams(vmem_limit_bytes=48 * 2**20),
        cost_estimate=cost(2e10, 1e7),
        name="attend_back",
    )(first, queries, *window, *window, grads, pos_q, start_q, lse, inner, pos_k)


def columns_of(ref, group, groups, step, depth):
    at = lax.rem(group + step + groups, groups) * depth
    return ref.at[:, pl.ds(pl.multiple_of(at, 128), depth)]


def front_kernel(groups, local, place, hidden, grads, *refs):
    w_in, w_out = refs[:groups], refs[groups : 2 * groups]
    gates, active, grad_pre, rows_out, turned, acc = refs[2 * groups :]
    levels, depth, width = w_in[0].shape
    tile = hidden.shape[0]
    model = groups * depth
    parts = [slice(step * depth, (step + 1) * depth) for step in range(groups)]
    for step in range(groups):
        turned[0, :, parts[step]] = columns_of(hidden, place[1], groups, -step, depth)[...]
        turned[1, :, parts[step]] = columns_of(grads, place[1], groups, -step, depth)[...]
    gate_grads = []
    for level in range(levels):
        pre_act = jnp.zeros((tile, width), jnp.float32)
        grad_active = jnp.zeros((tile, width), jnp.float32)
        for step in range(groups):
            pre_act += dot(turned[0, :, parts[step]], w_in[step][level], 1, 0)
            grad_active += dot(turned[1, :, parts[step]], w_out[step][level], 1, 0)
        first = level * local
        gate = jnp.concatenate(
            [jnp.broadcast_to(gates[:, first + e : first + e + 1], (tile, FH)) for e in range(local)],
            axis=1,
        )
        sig = 1.0 / (1.0 + jnp.exp2(-LOG2E * pre_act))
        act_pre = pre_act * sig
        columns = slice(level * width, (level + 1) * width)
        active[:, columns] = (act_pre * gate).astype(jnp.bfloat16)
        product = grad_active * act_pre
        for e in range(local):
            gate_grads.append(
                jnp.sum(product[:, e * FH : (e + 1) * FH], axis=1, keepdims=True)
            )
        slope = sig * (1.0 + pre_act * (1.0 - sig))
        low_pre = (grad_active * gate * slope).astype(jnp.bfloat16)
        grad_pre[:, columns] = low_pre
        for step in range(groups):
            back = dot(low_pre, w_in[step][level], 1, 1)
            acc[:, parts[step]] = back if level == 0 else acc[:, parts[step]] + back
    for step in range(groups):
        columns_of(rows_out, place[1], groups, -step, depth)[...] = acc[:, parts[step]].astype(
            jnp.bfloat16
        )
    spare = rows_out.shape[1] - model
    lane = lax.broadcasted_iota(jnp.int32, (tile, spare), 1) - place[0] * (levels * local)
    spread = jnp.zeros((tile, spare), jnp.float32)
    for e, column in enumerate(gate_grads):
        spread = jnp.where(lane == e, column, spread)
    rows_out[:, model:] = spread.astype(jnp.bfloat16)


def ffn_front(place, hidden, grads, w_in, w_out, gates, local):
    rows, wide = hidden.shape
    groups = len(w_in)
    levels, depth, width = w_in[0].shape
    tile = 512

    def by_row(columns):
        return pl.BlockSpec((tile, columns), lambda i, *_: (i, 0))

    whole = pl.BlockSpec(w_in[0].shape, lambda i, *_: (0, 0, 0), pipeline_mode=pl.Buffered(1))
    grid_spec = pltpu.PrefetchScalarGridSpec(
        num_scalar_prefetch=1,
        grid=(rows // tile,),
        in_specs=[by_row(wide), by_row(groups * depth)]
        + [whole] * (2 * groups)
        + [by_row(gates.shape[1])],
        out_specs=[by_row(levels * width), by_row(levels * width), by_row(wide)],
        scratch_shapes=[
            pltpu.VMEM((2, tile, groups * depth), jnp.bfloat16),
            pltpu.VMEM((tile, groups * depth), jnp.float32),
        ],
    )
    hidden_units = jax.ShapeDtypeStruct((rows, levels * width), jnp.bfloat16)
    return pl.pallas_call(
        functools.partial(front_kernel, groups, local),
        grid_spec=grid_spec,
        out_shape=[hidden_units, hidden_units, jax.ShapeDtypeStruct((rows, wide), jnp.bfloat16)],
        compiler_params=pltpu.CompilerParams(vmem_limit_bytes=58 * 2**20),
        cost_estimate=cost(6 * rows * groups * depth * levels * width, 3e7),
        name="ffn_front",
    )(place, hidden, grads, *w_in, *w_out, gates)


def rear_kernel(groups, place, rows_in, hidden_units, *weight_grads):
    _, depth, _ = weight_grads[0].shape
    units = hidden_units[...]
    for step in range(groups):
        part = columns_of(rows_in, place[1], groups, step, depth)
        weight_grads[step][0] = dot(part[...], units, 0, 0).astype(jnp.bfloat16)


def feed_kernel(groups, place, active, *refs):
    weights = refs[:groups]
    feed, acc = refs[groups:]
    _, depth, _ = weights[0].shape
    level = pl.program_id(0)
    act = active[...]
    for step in range(groups):
        fed = dot(act, weights[step][0], 1, 1)
        part = slice(step * depth, (step + 1) * depth)

        @pl.when(level == 0)
        def _():
            acc[:, part] = fed

        @pl.when(level > 0)
        def _():
            acc[:, part] += fed

    @pl.when(level == pl.num_programs(0) - 1)
    def _():
        for step in range(groups):
            part = slice(step * depth, (step + 1) * depth)
            columns_of(feed, place[1], groups, -step, depth)[...] = acc[:, part].astype(
                jnp.bfloat16
            )


def whole_rows(rows, columns):
    return pl.BlockSpec((rows, columns), lambda i, *_: (0, 0), pipeline_mode=pl.Buffered(1))


def ffn_feed(place, active, weights):
    rows = active.shape[0]
    groups = len(weights)
    levels, depth, width = weights[0].shape
    return pl.pallas_call(
        functools.partial(feed_kernel, groups),
        grid_spec=pltpu.PrefetchScalarGridSpec(
            num_scalar_prefetch=1,
            grid=(levels,),
            in_specs=[pl.BlockSpec((rows, width), lambda i, *_: (0, i))]
            + [pl.BlockSpec((1, depth, width), lambda i, *_: (i, 0, 0))] * groups,
            out_specs=whole_rows(rows, groups * depth),
            scratch_shapes=[pltpu.VMEM((rows, groups * depth), jnp.float32)],
        ),
        out_shape=jax.ShapeDtypeStruct((rows, groups * depth), jnp.bfloat16),
        compiler_params=pltpu.CompilerParams(vmem_limit_bytes=58 * 2**20),
        cost_estimate=cost(2 * rows * groups * depth * levels * width, 3e7),
        name="ffn_feed",
    )(place, active, *weights)


def ffn_rear(place, rows_in, units, model, groups, levels):
    rows, wide = rows_in.shape
    width = units.shape[1] // levels
    depth = model // groups
    return pl.pallas_call(
        functools.partial(rear_kernel, groups),
        grid_spec=pltpu.PrefetchScalarGridSpec(
            num_scalar_prefetch=1,
            grid=(levels,),
            in_specs=[
                whole_rows(rows, wide),
                pl.BlockSpec((rows, width), lambda i, *_: (0, i)),
            ],
            out_specs=[pl.BlockSpec((1, depth, width), lambda i, *_: (i, 0, 0))] * groups,
        ),
        out_shape=[jax.ShapeDtypeStruct((levels, depth, width), jnp.bfloat16)] * groups,
        compiler_params=pltpu.CompilerParams(vmem_limit_bytes=58 * 2**20),
        cost_estimate=cost(2 * rows * groups * depth * levels * width, 3e7),
        name="ffn_rear",
    )(place, rows_in, units)


def turn(value, axis, by):
    size = lax.axis_size(axis)
    return lax.ppermute(value, axis, [(i, (i + by) % size) for i in range(size)])


def normalized(rows, gain, bias):
    values = rows.astype(jnp.float32)
    centred = values - jnp.mean(values, axis=1, keepdims=True)
    inverse = lax.rsqrt(jnp.mean(centred * centred, axis=1, keepdims=True) + 1e-05)
    scaled = centred * inverse
    return scaled, inverse, (scaled * gain + bias).astype(jnp.bfloat16)


def project_kernel(
    levels, rows, w_value, w_query, w_key, routers, gain, bias, order, tables,
    query, key_value, projected, sigs, masks,
):
    count = rows.shape[0]
    piece = count // (levels * HEADS)
    _, _, normed = normalized(rows[...], gain[...], bias[...])
    query[...] = dot(normed, w_query[...], 1, 0).astype(jnp.bfloat16)
    key_value[:, :DH] = dot(normed, w_key[...], 1, 0).astype(jnp.bfloat16)
    sig = 1.0 / (1.0 + jnp.exp2(-LOG2E * dot(normed, routers[...], 1, 0)))
    sigs[...] = sig
    product = dot(rows[...], w_value[...], 1, 0)
    projected[...] = product
    at = lax.broadcasted_iota(jnp.int32, (count, count), 0)
    source = lax.rem(at // piece, levels) * HEADS + at // (piece * levels)
    here = (source * piece + lax.rem(at, piece) == order[0]).astype(jnp.bfloat16)
    lane = lax.broadcasted_iota(jnp.int32, (16, count), 0)
    table = tables[0]
    named = jnp.zeros((16, count), jnp.float32)
    for which in range(2):
        option = lane - which * VEXP
        for slot in range(2):
            pick = table[2 * which + slot : 2 * which + slot + 1, :]
            hit = (option == pick) & (option >= 0) & (option < VEXP)
            named = jnp.where(hit, 1.0, named)
    mask = dot(here, named.astype(jnp.bfloat16), 1, 1)
    masks[...] = mask
    value = jnp.zeros((count, DH), jnp.float32)
    for e in range(VEXP):
        gate = sig[:, e : e + 1] * mask[:, e : e + 1]
        value += gate * product[:, e * DH : (e + 1) * DH]
    key_value[:, DH:] = value.astype(jnp.bfloat16)


def project(rows, full, gain, bias, orders, tables, levels):
    total, width = rows.shape
    count = total // HEADS

    def by_row(columns):
        return pl.BlockSpec((count, columns), lambda i: (i, 0))

    def column(size, at):
        return pl.BlockSpec((width, size), lambda i: (0, at), pipeline_mode=pl.Buffered(1))

    line = pl.BlockSpec((1, width), lambda i: (0, 0))
    shapes = [(DH, jnp.bfloat16), (2 * DH, jnp.bfloat16), (VEXP * DH, jnp.float32)]
    shapes += [(128, jnp.float32), (16, jnp.float32)]
    return pl.pallas_call(
        functools.partial(project_kernel, levels),
        grid=(HEADS,),
        in_specs=[by_row(width), column(VEXP * DH, 0)]
        + [column(DH, 2 * VEXP + i) for i in range(3)]
        + [line, line]
        + [
            pl.BlockSpec((1, 1, count), lambda i: (i, 0, 0)),
            pl.BlockSpec((1,) + tables.shape[1:], lambda i: (i, 0, 0)),
        ],
        out_specs=[by_row(columns) for columns, _ in shapes],
        out_shape=[jax.ShapeDtypeStruct((total, columns), kind) for columns, kind in shapes],
        compiler_params=pltpu.CompilerParams(vmem_limit_bytes=48 * 2**20),
        cost_estimate=cost(2 * total * width * 1024, 2e7),
        name="project",
    )(rows, full, full, full, full, gain, bias, orders, tables)


def project_back_kernel(
    rows, grads, grad_query, out_logit, projected, sigs, masks,
    w_value, w_query, w_key, routers, gain, bias,
    grad_rows, weight_grads, acc, sums,
):
    at = pl.program_id(0)
    count = rows.shape[0]
    values = VEXP * DH

    @pl.when(at == 0)
    def _():
        acc[...] = jnp.zeros_like(acc)
        sums[...] = jnp.zeros_like(sums)

    scaled, inverse, normed = normalized(rows[...], gain[...], bias[...])
    grad_key = grads[:, :DH].astype(jnp.bfloat16)
    grad_value = grads[:, DH:]
    sig, mask = sigs[...], masks[...]
    lane = lax.broadcasted_iota(jnp.int32, (count, 128), 1)
    logits = out_logit[...].astype(jnp.float32)
    parts = []
    for e in range(VEXP):
        one, on = sig[:, e : e + 1], mask[:, e : e + 1]
        parts.append((one * on * grad_value).astype(jnp.bfloat16))
        inner = jnp.sum(grad_value * projected[:, e * DH : (e + 1) * DH], axis=1, keepdims=True)
        logits = jnp.where(lane == e, inner * one * (1.0 - one) * on, logits)
    grad_projected = jnp.concatenate(parts, axis=1)
    sides = jnp.concatenate([grad_query[...], grad_key, logits.astype(jnp.bfloat16)], axis=1)
    first = dot(sides[:, :DH], w_query[...], 1, 1)
    first += dot(sides[:, DH : 2 * DH], w_key[...], 1, 1)
    first += dot(sides[:, 2 * DH :], routers[...], 1, 1)
    sums[2 * VEXP : 2 * VEXP + 1, :] += jnp.sum(first * scaled, axis=0, keepdims=True)
    sums[2 * VEXP + 1 : 2 * VEXP + 2, :] += jnp.sum(first, axis=0, keepdims=True)
    inner_grad = first * gain[...]
    inner_grad = inverse * (
        inner_grad
        - jnp.mean(inner_grad, axis=1, keepdims=True)
        - scaled * jnp.mean(inner_grad * scaled, axis=1, keepdims=True)
    )
    grad_rows[...] = (inner_grad + dot(grad_projected, w_value[...], 1, 1)).astype(jnp.bfloat16)
    acc[:, :values] += dot(rows[...], grad_projected, 0, 0)
    acc[:, values:] += dot(normed, sides, 0, 0)

    @pl.when(at == pl.num_programs(0) - 1)
    def _():
        weight_grads[:, : values + 2 * DH] = acc[:, : values + 2 * DH].astype(jnp.bfloat16)
        last = acc[:, values + 2 * DH :] + sums[...].T
        weight_grads[:, values + 2 * DH :] = last.astype(jnp.bfloat16)


def project_back(rows, grads, grad_query, out_logit, projected, sigs, masks, full, gain, bias):
    total, width = rows.shape
    count = total // HEADS
    columns = VEXP * DH + 3 * DH

    def by_row(size):
        return pl.BlockSpec((count, size), lambda i: (i, 0))

    def column(size, at):
        return pl.BlockSpec((width, size), lambda i: (0, at), pipeline_mode=pl.Buffered(1))

    line = pl.BlockSpec((1, width), lambda i: (0, 0))
    return pl.pallas_call(
        project_back_kernel,
        grid=(HEADS,),
        in_specs=[by_row(width), by_row(2 * DH), by_row(DH), by_row(128), by_row(VEXP * DH)]
        + [by_row(128), by_row(16), column(VEXP * DH, 0)]
        + [column(DH, 2 * VEXP + i) for i in range(3)]
        + [line, line],
        out_specs=[by_row(width), pl.BlockSpec((width, columns), lambda i: (0, 0))],
        out_shape=[
            jax.ShapeDtypeStruct((total, width), jnp.bfloat16),
            jax.ShapeDtypeStruct((width, columns), jnp.bfloat16),
        ],
        scratch_shapes=[
            pltpu.VMEM((width, columns), jnp.float32),
            pltpu.VMEM((128, width), jnp.float32),
        ],
        compiler_params=pltpu.CompilerParams(vmem_limit_bytes=56 * 2**20),
        cost_estimate=cost(4 * total * width * 1024, 4e7),
        name="project_back",
    )(rows, grads, grad_query, out_logit, projected, sigs, masks, full, full, full, full, gain, bias)


def chosen(routes, options):
    return jnp.sum(
        (routes[..., None] == jnp.arange(options, dtype=jnp.int32)).astype(jnp.float32), axis=-2
    )


def shift(value, axis, by):
    count = lax.axis_size(axis)
    pairs = [(i, i + by) for i in range(count) if 0 <= i + by < count]
    return lax.ppermute(value, axis, pairs)


def body(
    tokens_in,
    out_grad,
    deal_order,
    seq_lengths,
    value_routes,
    output_routes,
    ffn_routes,
    norm1_gain,
    norm1_bias,
    norm2_gain,
    norm2_bias,
    query_weight,
    key_weight,
    value_weight,
    output_weight,
    value_router,
    output_router,
    ffn_router,
    ffn_in,
    ffn_out,
):
    groups = lax.axis_size("group")
    levels = lax.axis_size("level")
    level = lax.axis_index("level")
    head = lax.axis_index("head")
    count, width = tokens_in.shape
    piece = count // (levels * HEADS)
    wrows = query_weight.shape[0]
    experts = ffn_router.shape[1]
    local_experts = ffn_in.shape[1] // FH

    small = jnp.concatenate(
        [
            ffn_router,
            norm1_gain[:, None],
            norm1_bias[:, None],
            norm2_gain[:, None],
            norm2_bias[:, None],
        ],
        axis=1,
    )
    shared = small.shape[1]
    pad = -(shared + 2 * VEXP) % 128
    packed = jnp.concatenate(
        [
            value_weight.reshape(wrows, HEADS, VEXP * DH),
            output_weight.reshape(wrows, HEADS, VEXP * DH),
            query_weight.reshape(wrows, HEADS, DH),
            key_weight.reshape(wrows, HEADS, DH),
            value_router.reshape(wrows, HEADS, VEXP),
            output_router.reshape(wrows, HEADS, VEXP),
            jnp.broadcast_to(small[:, None, :], (wrows, HEADS, shared)),
            jnp.zeros((wrows, HEADS, pad), jnp.bfloat16),
        ],
        axis=2,
    )
    cols = packed.shape[2]
    tables = jnp.concatenate(
        [value_routes.transpose(1, 2, 0), output_routes.transpose(1, 2, 0)], axis=1
    )
    picks = ffn_routes.reshape(levels, HEADS * piece, -1).transpose(0, 2, 1)
    arrived, own_grads, full, tables, picks, orders = start(
        tokens_in.reshape(levels, HEADS, piece, width),
        out_grad.reshape(levels, HEADS, piece, width),
        packed.transpose(1, 0, 2),
        tables,
        picks,
        deal_order,
    )
    worker_in = arrived.reshape(HEADS * count, width)
    own_tokens = lax.dynamic_index_in_dim(arrived, head, 1, keepdims=False).reshape(count, width)
    in_rows = [turn(ffn_in, "group", k) for k in range(1, groups)]
    full, in_rows = lax.optimization_barrier((full.reshape(width, cols), in_rows))

    base = 2 * DH + 2 * VEXP * DH
    w_output = full[:, VEXP * DH : 2 * VEXP * DH]
    at = base + 2 * VEXP
    r_ffn = full[:, at : at + experts]
    gain_one, bias_one, gain_two, bias_two = (
        full[:, at + experts + i].astype(jnp.float32) for i in range(4)
    )
    gain_row, bias_row = gain_one[None], bias_one[None]
    orders = orders.reshape(levels, HEADS, count)
    own_order = lax.dynamic_index_in_dim(orders, level, 0, keepdims=False)[:, None, :]
    queries, key_value, projected, sigs, masks = project(
        worker_in, full, gain_row, bias_row, own_order, tables, levels
    )

    rows = HEADS * count
    reach = -(-LMAX // rows)

    ramp = jnp.arange(count, dtype=jnp.int32)

    def arrival(values):
        lead, shape = values.shape[:-3], values.shape[-1:]
        four = values.reshape(lead + (HEADS, levels, HEADS, piece) + shape)
        return jnp.swapaxes(four, -4, -3).reshape(lead + (rows,) + shape)

    orders = jnp.concatenate([jnp.zeros((reach, HEADS, count), jnp.int32), orders], axis=0)
    orders = lax.dynamic_slice_in_dim(orders, level, reach + 1, 0)
    here = orders[:, :, None, :] == ramp[None, None, :, None]
    inverse = jnp.sum(here * ramp, axis=3)
    shard = (level - reach + jnp.arange(reach + 1, dtype=jnp.int32))[:, None] * HEADS
    shard = shard + jnp.arange(HEADS, dtype=jnp.int32)[None, :]
    pos_all = jnp.where(shard[:, :, None] < 0, -1, shard[:, :, None] * count + inverse)
    pos_all = arrival(pos_all[..., None]).reshape(-1)
    positions = pos_all[reach * rows :]
    seq_ends = jnp.cumsum(seq_lengths[0])

    def starts_of(places):
        return jnp.max(jnp.where(seq_ends <= places[:, None], seq_ends, 0), axis=1)

    starts = starts_of(positions)
    blocks = rows // BLOCK
    base_block = (level - reach) * blocks
    first_block = starts_of(level * rows + jnp.arange(blocks, dtype=jnp.int32) * BLOCK) // BLOCK
    first_block = jnp.maximum(first_block - base_block, 0)

    window = [key_value]
    own_grads = own_grads.reshape(count, width)
    for i in range(reach):
        came = shift(window[0], "level", 1)
        if i == 0:
            came, own_grads, pos_all, starts, ffn_out, in_rows = lax.optimization_barrier(
                (came, own_grads, pos_all, starts, ffn_out, [ffn_in] + in_rows)
            )
            cotangent = level_gather(own_grads, 5, True)
        if i == reach - 1:
            came, cotangent = lax.optimization_barrier((came, cotangent))
        window.insert(0, came)
    place = jnp.stack([head, lax.axis_index("group")])
    out_here = lax.all_gather(ffn_out, "level", axis=0)
    w_in = [lax.all_gather(part, "level", axis=0) for part in in_rows]

    own_routes = picks.reshape(levels, -1, HEADS, piece).transpose(2, 0, 3, 1).reshape(count, -1)


    def lines(values):
        return values.reshape(blocks, 1, BLOCK)

    attended, log_total = attend(
        first_block,
        queries,
        window,
        lines(positions),
        lines(starts),
        pos_all[:, None],
    )

    out_sig = sigs[:, VEXP : 2 * VEXP]
    out_mask = masks[:, VEXP : 2 * VEXP]
    out_gate = out_sig * out_mask
    mixed = low((out_gate[..., None] * attended[:, None, :]).reshape(rows, VEXP * DH))
    branch = low(level_scatter(low(transposed(mixed, w_output)), 2))
    branch, out_here = lax.optimization_barrier((branch, out_here))
    w_out = [out_here] + [turn(out_here, "group", k) for k in range(1, groups)]
    middle = own_tokens.astype(jnp.float32) + branch.astype(jnp.float32)

    normed_mid, scaled_two, inverse_two = layer_norm(middle, gain_two, bias_two)
    normed_two = low(normed_mid)
    ffn_sig = jax.nn.sigmoid(matmul(normed_two, r_ffn))
    member = chosen(own_routes, experts)
    shares = (ffn_sig * member).reshape(count, levels, HEADS, local_experts)
    shares = jnp.swapaxes(shares, 1, 2).reshape(count, experts)
    spare = -experts % 128
    extended = jnp.concatenate([middle, shares], axis=1)
    hidden = level_gather(jnp.pad(low(extended), ((0, 0), (0, spare))), 3, True)
    mine = levels * local_experts
    gates = lax.dynamic_slice_in_dim(hidden, width + head * mine, mine, 1).astype(jnp.float32)
    active, grad_pre, grad_rows = ffn_front(
        place, hidden, cotangent, w_in, w_out, gates, local_experts
    )
    summed, beyond = pair_scatter(grad_rows, 4, True)
    came = to_far(beyond)
    grad_in = ffn_rear(place, hidden, grad_pre, width, groups, levels)
    in_came = [turn(grad_in[k], "group", k) for k in range(1, groups)]
    grad_out = ffn_rear(place, cotangent, active, width, groups, levels)
    out_came = [turn(grad_out[k], "group", k) for k in range(1, groups)]
    came, grad_in, grad_out = lax.optimization_barrier((came, grad_in, grad_out))
    summed = summed + came.astype(jnp.float32)

    gate_grads = summed[:, width : width + experts].reshape(count, HEADS, levels, local_experts)
    gate_grads = jnp.swapaxes(gate_grads, 1, 2).reshape(count, experts)
    grad_logit = low(gate_grads * ffn_sig * (1.0 - ffn_sig) * member)
    grad_second = transposed(grad_logit, r_ffn)
    grad_r_ffn = contract_rows(normed_two, grad_logit)
    grad_gain_two = jnp.sum(grad_second * scaled_two, axis=0)
    grad_bias_two = jnp.sum(grad_second, axis=0)
    grad_middle = (
        own_grads.astype(jnp.float32)
        + summed[:, :width]
        + norm_back(grad_second, gain_two, scaled_two, inverse_two)
    )

    own_branch = low(grad_middle)
    came = to_far(own_branch)
    feed = ffn_feed(place, active, w_out)
    came, feed = lax.optimization_barrier((came, feed))
    grad_branch = pair_gather(own_branch, came, 7)

    def sum_over_rows(own, others):
        total = own[0].astype(jnp.float32)
        for other in others:
            total = total + other.astype(jnp.float32)
        return lax.psum_scatter(low(total), "level", scatter_dimension=0)

    grad_branch, in_came = lax.optimization_barrier((grad_branch, in_came))
    ffn_in_grad = sum_over_rows(grad_in, in_came)
    grad_mixed = matmul(grad_branch, w_output).reshape(rows, VEXP, DH)
    grad_out_gate = jnp.sum(grad_mixed * attended[:, None, :], axis=-1)
    grad_attended = low(jnp.sum(grad_mixed * out_gate[..., None], axis=1))
    grad_out_logit = low(grad_out_gate * out_sig * (1.0 - out_sig) * out_mask)
    row_inner = jnp.sum(grad_attended.astype(jnp.float32) * attended, axis=-1)
    grad_queries, *grad_window = attend_back(
        first_block,
        queries,
        window,
        grad_attended,
        lines(positions),
        lines(starts),
        log_total,
        lines(row_inner),
        pos_all[:, None],
    )
    came = shift(grad_window[0], "level", -1)
    grad_queries, out_came = lax.optimization_barrier((grad_queries, out_came))
    ffn_out_grad = sum_over_rows(grad_out, out_came)
    fed, beyond = pair_scatter(feed, 6, True)
    grad_w_output = contract_rows(grad_branch, mixed)
    early = jnp.concatenate(
        [
            low(grad_w_output),
            low(grad_r_ffn),
            low(grad_gain_two)[:, None],
            low(grad_bias_two)[:, None],
            jnp.zeros((width, -(experts + 2) % 128), jnp.bfloat16),
        ],
        axis=1,
    )
    for i in range(1, reach + 1):
        if i < reach:
            came, fed = lax.optimization_barrier((came, fed))
        else:
            came, early = lax.optimization_barrier((came, early))
        grad_both = grad_window[i].astype(jnp.float32) + came.astype(jnp.float32)
        if i < reach:
            grad_keys_sent = low(grad_both)
            came = shift(grad_keys_sent, "level", -1)
    fed_far = to_far(beyond)
    grad_inputs, late = project_back(
        worker_in,
        grad_both,
        grad_queries,
        jnp.pad(grad_out_logit, ((0, 0), (VEXP, 128 - 2 * VEXP))),
        projected,
        sigs,
        masks,
        full,
        gain_row,
        bias_row,
    )

    fed_far, grad_inputs = lax.optimization_barrier((fed_far, grad_inputs))
    layer_out = to_home(low(middle + fed + fed_far.astype(jnp.float32)))

    input_grad, owned, early = finish(
        grad_inputs.reshape(HEADS, HEADS, levels * piece, width),
        grad_middle.reshape(HEADS, levels * piece, width),
        late.reshape(groups, levels, HEADS, wrows, -1),
        early.reshape(groups, levels, HEADS, wrows, -1),
    )
    owned, early = owned.astype(jnp.float32), early.astype(jnp.float32)

    def columns(part, first, size):
        return part[:, :, first : first + size].transpose(1, 0, 2).reshape(wrows, HEADS * size)

    values = VEXP * DH
    misc = values + 2 * DH
    common = jnp.sum(early[:, :, values:], axis=0)
    norms = jnp.sum(owned[:, :, misc + 2 * VEXP :], axis=0)
    return (
        layer_out,
        input_grad.reshape(count, width),
        norms[:, 0],
        norms[:, 1],
        common[:, experts],
        common[:, experts + 1],
        columns(owned, values, DH),
        columns(owned, values + DH, DH),
        columns(owned, 0, values),
        columns(early, 0, values),
        columns(owned, misc, VEXP),
        columns(owned, misc + VEXP, VEXP),
        common[:, :experts],
        ffn_in_grad.astype(jnp.float32),
        ffn_out_grad.astype(jnp.float32),
    )


def solution(mesh):
    groups, shards = mesh.devices.shape
    fine = Mesh(mesh.devices.reshape(groups, shards // HEADS, HEADS), TOK)
    two, one, three = P(TOK, None), P(TOK), P(TOK, None, None)
    ffn = P("group", ("level", "head"))
    return jax.shard_map(
        body,
        mesh=fine,
        in_specs=(two, two, two, P("group", None), three, three, two, one, one, one, one)
        + (two,) * 7
        + (ffn, ffn),
        out_specs=(two, two, one, one, one, one) + (two,) * 7 + (ffn, ffn),
        check_vma=False,
    )
```

```python
import functools

import jax
import jax.numpy as jnp
from jax import lax
from jax.experimental import pallas as pl
from jax.experimental.pallas import tpu as pltpu
from jax.sharding import Mesh, PartitionSpec as P

HEADS = 4
DH = 128
VEXP = 5
FH = 128
LMAX = 4096

TOK = ("group", "level", "head")


def transposed(left_side, right_side):
    return lax.dot_general(
        left_side, right_side, (((1,), (1,)), ((), ())), preferred_element_type=jnp.float32
    )


def low(value):
    return value.astype(jnp.bfloat16)


def to_home(rows):
    levels = lax.axis_size("level")
    count = rows.shape[0]
    out = rows.reshape(HEADS, levels, count // levels // HEADS, -1).transpose(1, 0, 2, 3)
    back = lax.all_to_all(
        out.reshape(levels, count // levels, -1), "level", split_axis=0, concat_axis=0, tiled=True
    )
    return back.reshape(count, -1)


MESH = pl.DeviceIdType.MESH


def partners(head):
    near = head + 1 - 2 * lax.rem(head, 2)
    far = lax.rem(head + 2, HEADS)
    return near, far


def greet(near, far):
    barrier = pltpu.get_barrier_semaphore()
    for peer in (near, far):
        pl.semaphore_signal(barrier, inc=1, device_id={"head": peer}, device_id_type=MESH)
    pl.semaphore_wait(barrier, 2)


def remote(src, dst, send, recv, peer):
    return pltpu.make_async_remote_copy(
        src_ref=src,
        dst_ref=dst,
        send_sem=send,
        recv_sem=recv,
        device_id={"head": peer},
        device_id_type=MESH,
    )


def cost(flops, moved):
    return pl.CostEstimate(flops=int(flops), bytes_accessed=int(moved), transcendentals=0)


def gather_kernel(
    by_source, own, out, local_sem, near_send, near_recv, far_send, far_recv, pass_send, pass_recv
):
    head = lax.axis_index("head")
    near, far = partners(head)
    greet(near, far)

    def spot(i, source):
        return out.at[source, i] if by_source else out.at[i, source]

    pieces = range(HEADS)
    to_far = [remote(own.at[i], spot(i, head), far_send.at[i], far_recv.at[i], far) for i in pieces]
    to_near = [
        remote(own.at[i], spot(i, head), near_send.at[i], near_recv.at[i], near) for i in pieces
    ]
    passed = [
        remote(spot(i, far), spot(i, far), pass_send.at[i], pass_recv.at[i], near) for i in pieces
    ]
    kept = [pltpu.make_async_copy(own.at[i], spot(i, head), local_sem.at[i]) for i in pieces]
    for copy in to_far + to_near + kept:
        copy.start()
    for i in pieces:
        to_far[i].wait_recv()
        passed[i].start()
    for i in pieces:
        to_near[i].wait_recv()
        passed[i].wait_recv()
        kept[i].wait()
        to_far[i].wait_send()
        to_near[i].wait_send()
        passed[i].wait_send()


def level_gather(rows, collective_id, by_source=False):
    count, width = rows.shape
    whole = pl.pallas_call(
        functools.partial(gather_kernel, by_source),
        out_shape=jax.ShapeDtypeStruct((HEADS, HEADS, count // HEADS, width), rows.dtype),
        in_specs=[pl.BlockSpec(memory_space=pltpu.VMEM)],
        out_specs=pl.BlockSpec(memory_space=pl.ANY),
        scratch_shapes=[pltpu.SemaphoreType.DMA((HEADS,))] * 7,
        compiler_params=pltpu.CompilerParams(collective_id=collective_id, has_side_effects=True),
        cost_estimate=cost(0, 90e6),
        name="level_gather",
    )(rows.reshape(HEADS, count // HEADS, width))
    return whole.reshape(HEADS * count, width)


def scatter_kernel(
    by_source, part, out, near_buf, send_buf, far_buf, near_send, near_recv, far_send, far_recv
):
    head = lax.axis_index("head")
    near, far = partners(head)
    greet(near, far)
    across = HEADS - 1 - head
    pieces = range(HEADS)

    def spot(i, dest):
        return (dest, i) if by_source else (i, dest)

    def to_near(slot, i, dest):
        return remote(
            part.at[spot(i, dest)],
            near_buf.at[slot, i],
            near_send.at[slot, i],
            near_recv.at[slot, i],
            near,
        )

    first = [to_near(0, i, across) for i in pieces]
    second = [to_near(1, i, near) for i in pieces]
    onward = [
        remote(send_buf.at[i], far_buf.at[i], far_send.at[i], far_recv.at[i], far) for i in pieces
    ]
    for copy in first + second:
        copy.start()
    for i in pieces:
        first[i].wait_recv()
        both = part[spot(i, far)].astype(jnp.float32) + near_buf[0, i].astype(jnp.float32)
        send_buf[i] = both.astype(jnp.bfloat16)
        onward[i].start()
    for i in pieces:
        second[i].wait_recv()
        out[i] = part[spot(i, head)].astype(jnp.float32) + near_buf[1, i].astype(jnp.float32)
    for i in pieces:
        onward[i].wait_recv()
        out[i] = out[i] + far_buf[i].astype(jnp.float32)
    for i in pieces:
        first[i].wait_send()
        second[i].wait_send()
        onward[i].wait_send()


def level_scatter(rows, collective_id, by_source=False):
    total, width = rows.shape
    piece = total // (HEADS * HEADS)
    low_type = jnp.bfloat16
    mine = pl.pallas_call(
        functools.partial(scatter_kernel, by_source),
        out_shape=jax.ShapeDtypeStruct((HEADS, piece, width), jnp.float32),
        in_specs=[pl.BlockSpec(memory_space=pltpu.VMEM)],
        out_specs=pl.BlockSpec(memory_space=pltpu.VMEM),
        scratch_shapes=[
            pltpu.VMEM((2, HEADS, piece, width), low_type),
            pltpu.VMEM((HEADS, piece, width), low_type),
            pltpu.VMEM((HEADS, piece, width), low_type),
            pltpu.SemaphoreType.DMA((2, HEADS)),
            pltpu.SemaphoreType.DMA((2, HEADS)),
            pltpu.SemaphoreType.DMA((HEADS,)),
            pltpu.SemaphoreType.DMA((HEADS,)),
        ],
        compiler_params=pltpu.CompilerParams(
            collective_id=collective_id, has_side_effects=True, vmem_limit_bytes=32 * 2**20
        ),
        cost_estimate=cost(0, 80e6),
        name="level_scatter",
    )(rows.reshape(HEADS, HEADS, piece, width))
    return mine.reshape(HEADS * piece, width)


def meet(near):
    barrier = pltpu.get_barrier_semaphore()
    pl.semaphore_signal(barrier, inc=1, device_id={"head": near}, device_id_type=MESH)
    pl.semaphore_wait(barrier, 1)


def pair_scatter_kernel(by_source, part, out, out_far, near_buf, send, recv):
    head = lax.axis_index("head")
    near, far = partners(head)
    meet(near)
    across = HEADS - 1 - head
    pieces = range(HEADS)

    def spot(i, dest):
        return (dest, i) if by_source else (i, dest)

    def to_near(slot, i, dest):
        return remote(
            part.at[spot(i, dest)], near_buf.at[slot, i], send.at[slot, i], recv.at[slot, i], near
        )

    first = [to_near(0, i, across) for i in pieces]
    second = [to_near(1, i, near) for i in pieces]
    for copy in first + second:
        copy.start()
    for i in pieces:
        first[i].wait_recv()
        both = part[spot(i, far)].astype(jnp.float32) + near_buf[0, i].astype(jnp.float32)
        out_far[i] = both.astype(jnp.bfloat16)
    for i in pieces:
        second[i].wait_recv()
        out[i] = part[spot(i, head)].astype(jnp.float32) + near_buf[1, i].astype(jnp.float32)
    for i in pieces:
        first[i].wait_send()
        second[i].wait_send()


def pair_scatter(rows, collective_id, by_source=False):
    total, width = rows.shape
    piece = total // (HEADS * HEADS)
    mine, other = pl.pallas_call(
        functools.partial(pair_scatter_kernel, by_source),
        out_shape=[
            jax.ShapeDtypeStruct((HEADS, piece, width), jnp.float32),
            jax.ShapeDtypeStruct((HEADS, piece, width), jnp.bfloat16),
        ],
        in_specs=[pl.BlockSpec(memory_space=pltpu.VMEM)],
        out_specs=[pl.BlockSpec(memory_space=pltpu.VMEM)] * 2,
        scratch_shapes=[
            pltpu.VMEM((2, HEADS, piece, width), jnp.bfloat16),
            pltpu.SemaphoreType.DMA((2, HEADS)),
            pltpu.SemaphoreType.DMA((2, HEADS)),
        ],
        compiler_params=pltpu.CompilerParams(
            collective_id=collective_id, has_side_effects=True, vmem_limit_bytes=32 * 2**20
        ),
        cost_estimate=cost(0, 25e6),
        name="pair_scatter",
    )(rows.reshape(HEADS, HEADS, piece, width))
    return mine.reshape(HEADS * piece, width), other.reshape(HEADS * piece, width)


def pair_gather_kernel(by_source, own, other, out, local_sem, send, recv):
    head = lax.axis_index("head")
    near, far = partners(head)
    meet(near)
    copies, kept = [], []
    for i in range(HEADS):
        for slot, (block, source) in enumerate(((own, head), (other, far))):
            place = out.at[source, i] if by_source else out.at[i, source]
            copies.append(
                remote(block.at[i], place, send.at[slot, i], recv.at[slot, i], near)
            )
            kept.append(pltpu.make_async_copy(block.at[i], place, local_sem.at[slot, i]))
    for copy in copies + kept:
        copy.start()
    for copy in copies + kept:
        copy.wait()


def pair_gather(own, other, collective_id, by_source=False):
    count, width = own.shape
    split = (HEADS, count // HEADS, width)
    whole = pl.pallas_call(
        functools.partial(pair_gather_kernel, by_source),
        out_shape=jax.ShapeDtypeStruct((HEADS,) + split, own.dtype),
        in_specs=[pl.BlockSpec(memory_space=pltpu.VMEM)] * 2,
        out_specs=pl.BlockSpec(memory_space=pl.ANY),
        scratch_shapes=[pltpu.SemaphoreType.DMA((2, HEADS))] * 3,
        compiler_params=pltpu.CompilerParams(collective_id=collective_id, has_side_effects=True),
        cost_estimate=cost(0, 25e6),
        name="pair_gather",
    )(own.reshape(split), other.reshape(split))
    return whole.reshape(HEADS * count, width)


def to_far(rows):
    return lax.ppermute(rows, "head", [(i, (i + 2) % HEADS) for i in range(HEADS)])


def ring(axis):
    me, size = lax.axis_index(axis), lax.axis_size(axis)
    ahead = [lax.rem(me + k, size) for k in range(1, size)]
    behind = [lax.rem(me + size - k, size) for k in range(1, size)]
    return me, ahead, behind


def reach_out(src, dst, send, recv, peer):
    return pltpu.make_async_remote_copy(
        src_ref=src, dst_ref=dst, send_sem=send, recv_sem=recv, device_id=peer, device_id_type=MESH
    )


def greet_all(peers):
    barrier = pltpu.get_barrier_semaphore()
    for peer in peers:
        pl.semaphore_signal(barrier, inc=1, device_id=peer, device_id_type=MESH)
    pl.semaphore_wait(barrier, len(peers))


def start_kernel(
    tokens, cotangents, value, output, query, key, extra, tables, picks, order,
    rows, grads, full, routes, chosen_rows, orders, weights, own_sem, *sems
):
    sems = iter(sems)

    def pair():
        return next(sems), next(sems)

    group, groups_ahead, _ = ring("group")
    level, levels_ahead, levels_behind = ring("level")
    head = lax.axis_index("head")
    near, far = partners(head)
    mates = [near, far, HEADS - 1 - head]
    for to in range(HEADS):
        at = 0
        for part in (value, output, query, key):
            size = part.shape[1] // HEADS
            weights[to, :, at : at + size] = part[:, to * size : (to + 1) * size]
            at += size
        weights[to, :, at:] = extra[to]
    greet_all(
        [{"head": m} for m in mates]
        + [{"level": n} for n in levels_ahead]
        + [{"group": n} for n in groups_ahead]
    )
    started = []

    def send(src, dst, send_sem, recv_sem, peer):
        copy = reach_out(src, dst, send_sem, recv_sem, peer)
        copy.start()
        started.append(copy)
        return copy

    out_s, out_r = pair()
    pick_s, pick_r = pair()
    crossing, picking = [], []
    for k, to in enumerate(levels_ahead):
        peer = {"level": to}
        crossing.append(send(tokens.at[to], rows.at[:, head, level], out_s.at[k], out_r.at[k], peer))
    mate_s, mate_r = pair()
    table_s, table_r = pair()
    order_s, order_r = pair()
    to_mates, order_mates, table_mates = [], [], []
    for k, to in enumerate(mates):
        peer = {"head": to}
        to_mates.append(
            send(weights.at[to], full.at[group, level, head], mate_s.at[k], mate_r.at[k], peer)
        )
        order_mates.append(
            send(order, orders.at[level, head], order_s.at[k], order_r.at[k], peer)
        )
    own = [
        (tokens.at[level], rows.at[:, head, level]),
        (weights.at[head], full.at[group, level, head]),
        (tables.at[head], routes.at[head]),
        (picks.at[level], chosen_rows.at[level]),
        (order, orders.at[level, head]),
        (cotangents.at[level], grads.at[:, level]),
    ]
    own = [pltpu.make_async_copy(src, dst, own_sem.at[i]) for i, (src, dst) in enumerate(own)]
    for copy in own:
        copy.start()
    far_s, far_r = pair()
    near_s, near_r = pair()
    pass_s, pass_r = pair()
    to_far, to_near = [], []

    def share(k, src, source):
        place = rows.at[:, head, source]
        to_far.append(send(src, place, far_s.at[k], far_r.at[k], {"head": far}))
        to_near.append(send(src, place, near_s.at[k], near_r.at[k], {"head": near}))

    share(0, tokens.at[level], level)
    block_s, block_r = pair()
    group_s, group_r = pair()
    orders_s, orders_r = pair()
    for copy in to_mates:
        copy.wait_recv()
    own[1].wait()
    blocks, grouped, ordered = [], [], []

    def to_groups(j, source):
        for k, to in enumerate(groups_ahead):
            block = full.at[group, source]
            grouped.append(
                send(block, block, group_s.at[k, j], group_r.at[k, j], {"group": to})
            )

    for k, to in enumerate(levels_ahead):
        block = full.at[group, level]
        blocks.append(send(block, block, block_s.at[k], block_r.at[k], {"level": to}))
    to_groups(0, level)
    for k, to in enumerate(mates):
        table_mates.append(
            send(tables.at[to], routes.at[head], table_s.at[k], table_r.at[k], {"head": to})
        )
    for k, to in enumerate(levels_ahead):
        picking.append(
            send(picks.at[to], chosen_rows.at[level], pick_s.at[k], pick_r.at[k], {"level": to})
        )
    for copy in order_mates:
        copy.wait_recv()
    own[4].wait()
    for k, to in enumerate(levels_ahead):
        block = orders.at[level]
        ordered.append(send(block, block, orders_s.at[k], orders_r.at[k], {"level": to}))
    for k, source in enumerate(levels_behind):
        crossing[k].wait_recv()
        share(k + 1, rows.at[:, head, source], source)
    grad_s, grad_r = pair()
    crossed = []
    for k, to in enumerate(levels_ahead):
        crossed.append(
            send(cotangents.at[to], grads.at[:, level], grad_s.at[k], grad_r.at[k], {"level": to})
        )
    for k, source in enumerate(levels_behind):
        blocks[k].wait_recv()
        to_groups(k + 1, source)
    passed = []
    for k, source in enumerate([level] + levels_behind):
        to_far[k].wait_recv()
        place = rows.at[:, far, source]
        passed.append(send(place, place, pass_s.at[k], pass_r.at[k], {"head": near}))
    for copy in to_near + passed + grouped + table_mates + picking + ordered + crossed:
        copy.wait_recv()
    for copy in started:
        copy.wait_send()
    for i in (0, 2, 3, 5):
        own[i].wait()


def start(tokens, cotangents, weights, extra, tables, picks, order):
    groups, levels = lax.axis_size("group"), lax.axis_size("level")
    _, _, piece, width = tokens.shape
    columns = sum(part.shape[1] for part in weights) // HEADS + extra.shape[2]
    block = extra.shape[:2] + (columns,)
    shapes = [
        jax.ShapeDtypeStruct((HEADS, HEADS, levels, piece, width), tokens.dtype),
        jax.ShapeDtypeStruct((HEADS, levels, piece, width), tokens.dtype),
        jax.ShapeDtypeStruct((groups, levels) + block, extra.dtype),
        jax.ShapeDtypeStruct(tables.shape, tables.dtype),
        jax.ShapeDtypeStruct(picks.shape, picks.dtype),
        jax.ShapeDtypeStruct((levels, HEADS) + order.shape, order.dtype),
    ]
    dma = pltpu.SemaphoreType.DMA
    others, mates = (levels - 1,), (HEADS - 1,)
    counts = [others] * 2 + [mates] * 3 + [(levels,)] * 3
    counts += [others, (groups - 1, levels), others, others]
    return pl.pallas_call(
        start_kernel,
        out_shape=shapes,
        in_specs=[pl.BlockSpec(memory_space=pltpu.VMEM)] * 10,
        out_specs=[pl.BlockSpec(memory_space=pl.ANY)] * 6,
        scratch_shapes=[pltpu.VMEM(block, extra.dtype), dma((6,))] + [dma(c) for c in counts for _ in range(2)],
        compiler_params=pltpu.CompilerParams(collective_id=9, has_side_effects=True),
        cost_estimate=cost(0, 200e6),
        name="start",
    )(tokens, cotangents, *weights, extra, tables, picks, order)


def finish_kernel(layout, *refs):
    refs = iter(refs)
    count = len(layout)

    def take(n):
        return [next(refs) for _ in range(n)]

    part, middle = take(2)
    grads = take(count)
    (home_grad,) = take(1)
    results = [take(len(pieces)) for pieces in layout]
    near_buf, send_buf, far_buf, total, back_buf, came_buf = take(6)
    group_buf, level_send, level_buf, head_send, owned = (take(count) for _ in range(5))

    def pair():
        return next(refs), next(refs)

    group, groups_ahead, _ = ring("group")
    level, levels_ahead, levels_behind = ring("level")
    head = lax.axis_index("head")
    near, far = partners(head)
    across = HEADS - 1 - head
    mates = [near, far, across]
    greet_all(
        [{"head": m} for m in mates]
        + [{"level": n} for n in levels_ahead]
        + [{"group": n} for n in groups_ahead]
    )
    started = []

    def send(src, dst, send_sem, recv_sem, peer):
        copy = reach_out(src, dst, send_sem, recv_sem, peer)
        copy.start()
        started.append(copy)
        return copy

    pieces = range(HEADS)
    sets = range(count)
    near_s, near_r = pair()
    far_s, far_r = pair()
    back_s, back_r = pair()
    group_s, group_r = pair()
    level_s, level_r = pair()
    mate_s, mate_r = pair()
    first, second, onward = [], [], []
    for slot, (dest, copies) in enumerate(((across, first), (near, second))):
        for i in pieces:
            copies.append(
                send(
                    part.at[i, dest],
                    near_buf.at[slot, i],
                    near_s.at[slot, i],
                    near_r.at[slot, i],
                    {"head": near},
                )
            )
    order = levels_ahead + [level]
    grouped = {}
    for j, dest in enumerate(order):
        for p in sets:
            grouped[j, p] = [
                send(
                    grads[p].at[to, dest],
                    group_buf[p].at[k, j],
                    group_s.at[p, k, j],
                    group_r.at[p, k, j],
                    {"group": to},
                )
                for k, to in enumerate(groups_ahead)
            ]
    for i in pieces:
        first[i].wait_recv()
        both = part[i, far].astype(jnp.float32) + near_buf[0, i].astype(jnp.float32)
        send_buf[i] = both.astype(jnp.bfloat16)
        onward.append(send(send_buf.at[i], far_buf.at[i], far_s.at[i], far_r.at[i], {"head": far}))
    for i in pieces:
        second[i].wait_recv()
        both = part[i, head].astype(jnp.float32) + near_buf[1, i].astype(jnp.float32)
        total[i] = both + middle[i]
    leveled = {}
    for j, dest in enumerate(order):
        for p in sets:
            amount = grads[p][group, dest].astype(jnp.float32)
            for k, copy in enumerate(grouped[j, p]):
                copy.wait_recv()
                amount = amount + group_buf[p][k, j].astype(jnp.float32)
            level_send[p][j] = amount.astype(jnp.bfloat16)
            if j < len(levels_ahead):
                leveled[j, p] = send(
                    level_send[p].at[j],
                    level_buf[p].at[j],
                    level_s.at[p, j],
                    level_r.at[p, j],
                    {"level": dest},
                )
    for i in pieces:
        onward[i].wait_recv()
        both = total[i] + far_buf[i].astype(jnp.float32)
        back_buf[i] = both.astype(jnp.bfloat16).reshape(back_buf.shape[1:])
    backs = [
        send(back_buf.at[:, to], came_buf.at[level], back_s.at[k], back_r.at[k], {"level": to})
        for k, to in enumerate(levels_ahead)
    ]
    sharing = []
    for p in sets:
        amount = level_send[p][len(levels_ahead)].astype(jnp.float32)
        for j in range(len(levels_ahead)):
            leveled[j, p].wait_recv()
            amount = amount + level_buf[p][j].astype(jnp.float32)
        head_send[p][...] = amount.astype(jnp.bfloat16)
        sharing += [
            send(
                head_send[p].at[to],
                owned[p].at[head],
                mate_s.at[p, k],
                mate_r.at[p, k],
                {"head": to},
            )
            for k, to in enumerate(mates)
        ]
        owned[p][head] = head_send[p][head]
    home_grad[level] = back_buf[:, level].astype(jnp.float32)
    for k, source in enumerate(levels_behind):
        backs[k].wait_recv()
        home_grad[source] = came_buf[source].astype(jnp.float32)
    for copy in sharing:
        copy.wait_recv()
    for p in sets:
        for out, (first_column, size, joined) in zip(results[p], layout[p]):
            for h in range(HEADS):
                value = owned[p][h, :, first_column : first_column + size].astype(jnp.float32)
                if joined:
                    out[:, h * size : (h + 1) * size] = value
                else:
                    out[h] = value
    for copy in started:
        copy.wait_send()


def finish(layout, part, middle, *grads):
    groups, levels = lax.axis_size("group"), lax.axis_size("level")
    _, count, width = middle.shape
    piece = count // levels
    low_type = jnp.bfloat16
    blocks = [grad.shape[2:] for grad in grads]
    sets = len(grads)
    dma = pltpu.SemaphoreType.DMA
    counts = [(2, HEADS), (HEADS,), (levels - 1,)]
    counts += [(sets, groups - 1, levels), (sets, levels - 1), (sets, HEADS - 1)]
    vmem = pl.BlockSpec(memory_space=pltpu.VMEM)
    shapes = []
    for pieces in layout:
        for _, size, joined in pieces:
            shape = (blocks[0][1], HEADS * size) if joined else (HEADS, blocks[0][1], size)
            shapes.append(jax.ShapeDtypeStruct(shape, jnp.float32))
    return pl.pallas_call(
        functools.partial(finish_kernel, layout),
        out_shape=[jax.ShapeDtypeStruct((levels, HEADS, piece, width), jnp.float32)] + shapes,
        in_specs=[vmem] * (2 + sets),
        out_specs=[vmem] * (1 + len(shapes)),
        scratch_shapes=[
            pltpu.VMEM((2, HEADS, count, width), low_type),
            pltpu.VMEM((HEADS, count, width), low_type),
            pltpu.VMEM((HEADS, count, width), low_type),
            pltpu.VMEM((HEADS, count, width), jnp.float32),
            pltpu.VMEM((HEADS, levels, piece, width), low_type),
            pltpu.VMEM((levels, HEADS, piece, width), low_type),
        ]
        + [pltpu.VMEM((groups - 1, levels) + block, low_type) for block in blocks]
        + [pltpu.VMEM((levels,) + block, low_type) for block in blocks]
        + [pltpu.VMEM((levels - 1,) + block, low_type) for block in blocks]
        + [pltpu.VMEM(block, low_type) for block in blocks] * 2
        + [dma(c) for c in counts for _ in range(2)],
        compiler_params=pltpu.CompilerParams(
            collective_id=10, has_side_effects=True, vmem_limit_bytes=56 * 2**20
        ),
        cost_estimate=cost(0, 200e6),
        name="finish",
    )(part, middle, *grads)


BLOCK = 512
LOG2E = 1.4426950408889634


def dot(left_side, right_side, left_dim, right_dim):
    return lax.dot_general(
        left_side,
        right_side,
        (((left_dim,), (right_dim,)), ((), ())),
        preferred_element_type=jnp.float32,
    )


def attend_kernel(parts, first, q, *refs):
    keys, values = refs[:parts], refs[parts : 2 * parts]
    pos_q, start_q, pos_k, out, lse, top, total, acc = refs[2 * parts :]
    at = pl.program_id(0)
    blocks = pl.num_programs(0)
    rate = LOG2E * DH ** (-0.5)
    top[...] = jnp.full_like(top, -1e30)
    total[...] = jnp.zeros_like(total)
    acc[...] = jnp.zeros_like(acc)
    query = q[...]
    row_at, row_from = pos_q[0], start_q[0]

    for part in range(parts):

        def step(block, carry, k=keys[part], v=values[part], part=part):
            rows = pl.ds(pl.multiple_of(block * BLOCK, BLOCK), BLOCK)
            spot = pl.ds(pl.multiple_of((part * blocks + block) * BLOCK, BLOCK), BLOCK)
            scores = dot(k[rows, :], query, 1, 1)
            key_at = pos_k[spot, :]
            scores = jnp.where((key_at >= row_from) & (key_at <= row_at), scores, -1e30)
            old = top[...]
            new = jnp.maximum(old, jnp.max(scores, axis=0, keepdims=True))
            shrink = jnp.exp2((old - new) * rate)
            weight = jnp.exp2((scores - new) * rate)
            total[...] = total[...] * shrink + jnp.sum(weight, axis=0, keepdims=True)
            acc[...] = acc[...] * shrink + dot(v[rows, :], weight.astype(jnp.bfloat16), 0, 0)
            top[...] = new
            return carry

        begin = jnp.maximum(first[at] - part * blocks, 0)
        end = at + 1 if part == parts - 1 else blocks
        lax.fori_loop(begin, end, step, 0)
    out[...] = (acc[...] / total[...]).T
    lse[0] = top[...] * rate + jnp.log2(total[...])


def attend(first, queries, window, pos_q, start_q, pos_k):
    rows = queries.shape[0]
    parts = len(window)
    line = pl.BlockSpec((1, 1, BLOCK), lambda i, *_: (i, 0, 0))
    grid_spec = pltpu.PrefetchScalarGridSpec(
        num_scalar_prefetch=1,
        grid=(rows // BLOCK,),
        in_specs=[pl.BlockSpec((BLOCK, DH), lambda i, *_: (i, 0))]
        + [pl.BlockSpec((rows, DH), lambda i, *_: (0, 0))] * parts
        + [pl.BlockSpec((rows, DH), lambda i, *_: (0, 1))] * parts
        + [line, line, pl.BlockSpec((parts * rows, 1), lambda i, *_: (0, 0))],
        out_specs=[pl.BlockSpec((BLOCK, DH), lambda i, *_: (i, 0)), line],
        scratch_shapes=[
            pltpu.VMEM((1, BLOCK), jnp.float32),
            pltpu.VMEM((1, BLOCK), jnp.float32),
            pltpu.VMEM((DH, BLOCK), jnp.float32),
        ],
    )
    return pl.pallas_call(
        functools.partial(attend_kernel, parts),
        grid_spec=grid_spec,
        out_shape=[
            jax.ShapeDtypeStruct((rows, DH), jnp.float32),
            jax.ShapeDtypeStruct((rows // BLOCK, 1, BLOCK), jnp.float32),
        ],
        compiler_params=pltpu.CompilerParams(vmem_limit_bytes=48 * 2**20),
        cost_estimate=cost(2e10, 1e7),
        name="attend",
    )(first, queries, *window, *window, pos_q, start_q, pos_k)


def attend_back_kernel(parts, first, q, *refs):
    keys, values = refs[:parts], refs[parts : 2 * parts]
    grad, pos_q, start_q, lse, inner, pos_k, grad_q = refs[2 * parts : 2 * parts + 7]
    grads = refs[2 * parts + 7 : 3 * parts + 7]
    sum_k, sum_v, acc = refs[3 * parts + 7 :]
    at = pl.program_id(0)
    blocks = pl.num_programs(0)
    rate = LOG2E * DH ** (-0.5)
    scale = DH ** (-0.5)

    @pl.when(at == 0)
    def _():
        sum_k[...] = jnp.zeros_like(sum_k)
        sum_v[...] = jnp.zeros_like(sum_v)

    acc[...] = jnp.zeros_like(acc)
    query, grad_out = q[...], grad[...]
    row_at, row_from, row_lse, row_inner = pos_q[0], start_q[0], lse[0], inner[0]

    for part in range(parts):

        def step(block, carry, k=keys[part], v=values[part], part=part):
            rows = pl.ds(pl.multiple_of(block * BLOCK, BLOCK), BLOCK)
            spot = pl.ds(pl.multiple_of((part * blocks + block) * BLOCK, BLOCK), BLOCK)
            key, value = k[rows, :], v[rows, :]
            scores = dot(key, query, 1, 1)
            key_at = pos_k[spot, :]
            seen = (key_at >= row_from) & (key_at <= row_at)
            soft = jnp.where(seen, jnp.exp2(scores * rate - row_lse), 0.0)
            grad_soft = dot(value, grad_out, 1, 1)
            grad_scores = (soft * (grad_soft - row_inner)).astype(jnp.bfloat16)
            sum_v[spot, :] += dot(soft.astype(jnp.bfloat16), grad_out, 1, 0)
            sum_k[spot, :] += dot(grad_scores, query, 1, 0)
            acc[...] += dot(grad_scores, key, 0, 0)
            return carry

        begin = jnp.maximum(first[at] - part * blocks, 0)
        end = at + 1 if part == parts - 1 else blocks
        lax.fori_loop(begin, end, step, 0)
    grad_q[...] = (acc[...] * scale).astype(jnp.bfloat16)

    @pl.when(at == blocks - 1)
    def _():
        size = grads[0].shape[0]
        for part in range(parts):
            spot = slice(part * size, (part + 1) * size)
            grads[part][:, :DH] = (sum_k[spot, :] * scale).astype(grads[part].dtype)
            grads[part][:, DH:] = sum_v[spot, :].astype(grads[part].dtype)


def attend_back(first, queries, window, grads, pos_q, start_q, lse, inner, pos_k):
    rows = queries.shape[0]
    parts = len(window)
    block = pl.BlockSpec((BLOCK, DH), lambda i, *_: (i, 0))
    line = pl.BlockSpec((1, 1, BLOCK), lambda i, *_: (i, 0, 0))
    grid_spec = pltpu.PrefetchScalarGridSpec(
        num_scalar_prefetch=1,
        grid=(rows // BLOCK,),
        in_specs=[block]
        + [pl.BlockSpec((rows, DH), lambda i, *_: (0, 0))] * parts
        + [pl.BlockSpec((rows, DH), lambda i, *_: (0, 1))] * parts
        + [block, line, line, line, line]
        + [pl.BlockSpec((parts * rows, 1), lambda i, *_: (0, 0))],
        out_specs=[block] + [pl.BlockSpec((rows, 2 * DH), lambda i, *_: (0, 0))] * parts,
        scratch_shapes=[
            pltpu.VMEM((parts * rows, DH), jnp.float32),
            pltpu.VMEM((parts * rows, DH), jnp.float32),
            pltpu.VMEM((BLOCK, DH), jnp.float32),
        ],
    )
    kinds = [jnp.bfloat16] * (parts - 1) + [jnp.float32]
    return pl.pallas_call(
        functools.partial(attend_back_kernel, parts),
        grid_spec=grid_spec,
        out_shape=[jax.ShapeDtypeStruct((rows, DH), jnp.bfloat16)]
        + [jax.ShapeDtypeStruct((rows, 2 * DH), kind) for kind in kinds],
        compiler_params=pltpu.CompilerParams(vmem_limit_bytes=48 * 2**20),
        cost_estimate=cost(2e10, 1e7),
        name="attend_back",
    )(first, queries, *window, *window, grads, pos_q, start_q, lse, inner, pos_k)


def columns_of(ref, group, groups, step, depth):
    at = lax.rem(group + step + groups, groups) * depth
    return ref.at[:, pl.ds(pl.multiple_of(at, 128), depth)]


def front_kernel(groups, local, place, hidden, grads, *refs):
    w_in, w_out = refs[:groups], refs[groups : 2 * groups]
    gates, active, grad_pre, rows_out, turned, acc = refs[2 * groups :]
    levels, depth, width = w_in[0].shape
    tile = hidden.shape[0]
    model = groups * depth
    parts = [slice(step * depth, (step + 1) * depth) for step in range(groups)]
    for step in range(groups):
        turned[0, :, parts[step]] = columns_of(hidden, place[1], groups, -step, depth)[...]
        turned[1, :, parts[step]] = columns_of(grads, place[1], groups, -step, depth)[...]
    gate_grads = []
    for level in range(levels):
        pre_act = jnp.zeros((tile, width), jnp.float32)
        grad_active = jnp.zeros((tile, width), jnp.float32)
        for step in range(groups):
            pre_act += dot(turned[0, :, parts[step]], w_in[step][level], 1, 0)
            grad_active += dot(turned[1, :, parts[step]], w_out[step][level], 1, 0)
        first = level * local
        gate = jnp.concatenate(
            [jnp.broadcast_to(gates[:, first + e : first + e + 1], (tile, FH)) for e in range(local)],
            axis=1,
        )
        sig = 1.0 / (1.0 + jnp.exp2(-LOG2E * pre_act))
        act_pre = pre_act * sig
        columns = slice(level * width, (level + 1) * width)
        active[:, columns] = (act_pre * gate).astype(jnp.bfloat16)
        product = grad_active * act_pre
        for e in range(local):
            gate_grads.append(
                jnp.sum(product[:, e * FH : (e + 1) * FH], axis=1, keepdims=True)
            )
        slope = sig * (1.0 + pre_act * (1.0 - sig))
        low_pre = (grad_active * gate * slope).astype(jnp.bfloat16)
        grad_pre[:, columns] = low_pre
        for step in range(groups):
            back = dot(low_pre, w_in[step][level], 1, 1)
            acc[:, parts[step]] = back if level == 0 else acc[:, parts[step]] + back
    for step in range(groups):
        columns_of(rows_out, place[1], groups, -step, depth)[...] = acc[:, parts[step]].astype(
            jnp.bfloat16
        )
    spare = rows_out.shape[1] - model
    lane = lax.broadcasted_iota(jnp.int32, (tile, spare), 1) - place[0] * (levels * local)
    spread = jnp.zeros((tile, spare), jnp.float32)
    for e, column in enumerate(gate_grads):
        spread = jnp.where(lane == e, column, spread)
    rows_out[:, model:] = spread.astype(jnp.bfloat16)


def ffn_front(place, hidden, grads, w_in, w_out, gates, local):
    rows, wide = hidden.shape
    groups = len(w_in)
    levels, depth, width = w_in[0].shape
    tile = 512

    def by_row(columns):
        return pl.BlockSpec((tile, columns), lambda i, *_: (i, 0))

    whole = pl.BlockSpec(w_in[0].shape, lambda i, *_: (0, 0, 0), pipeline_mode=pl.Buffered(1))
    grid_spec = pltpu.PrefetchScalarGridSpec(
        num_scalar_prefetch=1,
        grid=(rows // tile,),
        in_specs=[by_row(wide), by_row(groups * depth)]
        + [whole] * (2 * groups)
        + [by_row(gates.shape[1])],
        out_specs=[by_row(levels * width), by_row(levels * width), by_row(wide)],
        scratch_shapes=[
            pltpu.VMEM((2, tile, groups * depth), jnp.bfloat16),
            pltpu.VMEM((tile, groups * depth), jnp.float32),
        ],
    )
    hidden_units = jax.ShapeDtypeStruct((rows, levels * width), jnp.bfloat16)
    return pl.pallas_call(
        functools.partial(front_kernel, groups, local),
        grid_spec=grid_spec,
        out_shape=[hidden_units, hidden_units, jax.ShapeDtypeStruct((rows, wide), jnp.bfloat16)],
        compiler_params=pltpu.CompilerParams(vmem_limit_bytes=58 * 2**20),
        cost_estimate=cost(6 * rows * groups * depth * levels * width, 3e7),
        name="ffn_front",
    )(place, hidden, grads, *w_in, *w_out, gates)


def rear_kernel(groups, place, rows_in, hidden_units, *weight_grads):
    _, depth, _ = weight_grads[0].shape
    units = hidden_units[...]
    for step in range(groups):
        part = columns_of(rows_in, place[1], groups, step, depth)
        weight_grads[step][0] = dot(part[...], units, 0, 0).astype(jnp.bfloat16)


def feed_kernel(groups, place, active, *refs):
    weights = refs[:groups]
    feed, acc = refs[groups:]
    _, depth, _ = weights[0].shape
    level = pl.program_id(0)
    act = active[...]
    for step in range(groups):
        fed = dot(act, weights[step][0], 1, 1)
        part = slice(step * depth, (step + 1) * depth)

        @pl.when(level == 0)
        def _():
            acc[:, part] = fed

        @pl.when(level > 0)
        def _():
            acc[:, part] += fed

    @pl.when(level == pl.num_programs(0) - 1)
    def _():
        for step in range(groups):
            part = slice(step * depth, (step + 1) * depth)
            columns_of(feed, place[1], groups, -step, depth)[...] = acc[:, part].astype(
                jnp.bfloat16
            )


def whole_rows(rows, columns):
    return pl.BlockSpec((rows, columns), lambda i, *_: (0, 0), pipeline_mode=pl.Buffered(1))


def ffn_feed(place, active, weights):
    rows = active.shape[0]
    groups = len(weights)
    levels, depth, width = weights[0].shape
    return pl.pallas_call(
        functools.partial(feed_kernel, groups),
        grid_spec=pltpu.PrefetchScalarGridSpec(
            num_scalar_prefetch=1,
            grid=(levels,),
            in_specs=[pl.BlockSpec((rows, width), lambda i, *_: (0, i))]
            + [pl.BlockSpec((1, depth, width), lambda i, *_: (i, 0, 0))] * groups,
            out_specs=whole_rows(rows, groups * depth),
            scratch_shapes=[pltpu.VMEM((rows, groups * depth), jnp.float32)],
        ),
        out_shape=jax.ShapeDtypeStruct((rows, groups * depth), jnp.bfloat16),
        compiler_params=pltpu.CompilerParams(vmem_limit_bytes=58 * 2**20),
        cost_estimate=cost(2 * rows * groups * depth * levels * width, 3e7),
        name="ffn_feed",
    )(place, active, *weights)


def ffn_rear(place, rows_in, units, model, groups, levels):
    rows, wide = rows_in.shape
    width = units.shape[1] // levels
    depth = model // groups
    return pl.pallas_call(
        functools.partial(rear_kernel, groups),
        grid_spec=pltpu.PrefetchScalarGridSpec(
            num_scalar_prefetch=1,
            grid=(levels,),
            in_specs=[
                whole_rows(rows, wide),
                pl.BlockSpec((rows, width), lambda i, *_: (0, i)),
            ],
            out_specs=[pl.BlockSpec((1, depth, width), lambda i, *_: (i, 0, 0))] * groups,
        ),
        out_shape=[jax.ShapeDtypeStruct((levels, depth, width), jnp.bfloat16)] * groups,
        compiler_params=pltpu.CompilerParams(vmem_limit_bytes=58 * 2**20),
        cost_estimate=cost(2 * rows * groups * depth * levels * width, 3e7),
        name="ffn_rear",
    )(place, rows_in, units)


def named_by(routes, count):
    lane = lax.broadcasted_iota(jnp.int32, (routes.shape[0], count), 1)
    member = jnp.zeros(lane.shape, jnp.float32)
    for slot in range(routes.shape[1]):
        member = jnp.where(lane == routes[:, slot : slot + 1], 1.0, member)
    return member


def middle_kernel(rows, branch, routes, router, gain, bias, middle, extended, sig_out):
    experts = router.shape[1]
    width = rows.shape[1]
    rounded = branch[...].astype(jnp.bfloat16).astype(jnp.float32)
    value = rows[...].astype(jnp.float32) + rounded
    middle[...] = value
    _, _, normed = normalized(value, gain[...], bias[...])
    sig = 1.0 / (1.0 + jnp.exp2(-LOG2E * dot(normed, router[...], 1, 0)))
    sig_out[...] = sig
    extended[:, :width] = value.astype(jnp.bfloat16)
    gates = (sig * named_by(routes[...], experts)).astype(jnp.bfloat16)
    spare = extended.shape[1] - width - experts
    if spare:
        gates = jnp.concatenate([gates, jnp.zeros((gates.shape[0], spare), gates.dtype)], axis=1)
    extended[:, width:] = gates


def enter_ffn(rows, branch, routes, router, gain, bias):
    count, width = rows.shape
    experts = router.shape[1]
    wide = width + experts + -experts % 128
    return pl.pallas_call(
        middle_kernel,
        out_shape=[
            jax.ShapeDtypeStruct((count, width), jnp.float32),
            jax.ShapeDtypeStruct((count, wide), jnp.bfloat16),
            jax.ShapeDtypeStruct((count, experts), jnp.float32),
        ],
        compiler_params=pltpu.CompilerParams(vmem_limit_bytes=40 * 2**20),
        cost_estimate=cost(1e9, 1e7),
        name="middle",
    )(rows, branch, routes, router, gain, bias)


def leave_kernel(
    middle, own, came, cotangent, sigs, routes, router, gain, bias, grad_out, low_out, weight_grads
):
    experts = router.shape[1]
    count, width = middle.shape
    scaled, inverse, normed = normalized(middle[...], gain[...], bias[...])
    total = own[...] + came[...].astype(jnp.float32)
    sig = sigs[...]
    member = named_by(routes[...], experts)
    gate_grads = total[:, width : width + experts]
    logit = (gate_grads * sig * (1.0 - sig) * member).astype(jnp.bfloat16)
    second = dot(logit, router[...], 1, 1)
    inner_grad = second * gain[...]
    inner_grad = inverse * (
        inner_grad
        - jnp.mean(inner_grad, axis=1, keepdims=True)
        - scaled * jnp.mean(inner_grad * scaled, axis=1, keepdims=True)
    )
    grad = cotangent[...].astype(jnp.float32) + total[:, :width] + inner_grad
    grad_out[...] = grad
    low_out[...] = grad.astype(jnp.bfloat16)
    spare = weight_grads.shape[1] - experts
    sums = [
        jnp.sum(second * scaled, axis=0, keepdims=True),
        jnp.sum(second, axis=0, keepdims=True),
        jnp.zeros((126, width), jnp.float32),
    ]
    side = jnp.concatenate(sums, axis=0).T[:, :spare]
    both = jnp.concatenate([dot(normed, logit, 0, 0), side], axis=1)
    weight_grads[...] = both.astype(jnp.bfloat16)


def leave_ffn(middle, own, came, cotangent, sigs, routes, router, gain, bias):
    count, width = middle.shape
    experts = router.shape[1]
    columns = experts + 2 + -(experts + 2) % 128
    return pl.pallas_call(
        leave_kernel,
        out_shape=[
            jax.ShapeDtypeStruct((count, width), jnp.float32),
            jax.ShapeDtypeStruct((count, width), jnp.bfloat16),
            jax.ShapeDtypeStruct((width, columns), jnp.bfloat16),
        ],
        compiler_params=pltpu.CompilerParams(vmem_limit_bytes=48 * 2**20),
        cost_estimate=cost(1e9, 1e7),
        name="leave_ffn",
    )(middle, own, came, cotangent, sigs, routes, router, gain, bias)


def branch_back_kernel(
    grads, w_output, attended, sigs, masks, grad_attended, inner, out_logit, weight_grads, acc
):
    at = pl.program_id(0)
    count = grads.shape[0]
    sig, mask, values = sigs[...], masks[...], attended[...]
    mixed_grad = dot(grads[...], w_output[...], 1, 0)
    lane = lax.broadcasted_iota(jnp.int32, (count, 128), 1)
    logits = jnp.zeros((count, 128), jnp.float32)
    total = jnp.zeros((count, DH), jnp.float32)
    parts = []
    for e in range(VEXP):
        k = VEXP + e
        one, on = sig[:, k : k + 1], mask[:, k : k + 1]
        part = mixed_grad[:, e * DH : (e + 1) * DH]
        total += part * (one * on)
        gate_grad = jnp.sum(part * values, axis=1, keepdims=True)
        logits = jnp.where(lane == k, gate_grad * one * (1.0 - one) * on, logits)
        parts.append((one * on * values).astype(jnp.bfloat16))
    out_logit[...] = logits.astype(jnp.bfloat16)
    rounded = total.astype(jnp.bfloat16)
    grad_attended[...] = rounded
    product = rounded.astype(jnp.float32) * values
    inner[0] = jnp.sum(product.T, axis=0, keepdims=True)
    amount = dot(grads[...], jnp.concatenate(parts, axis=1), 0, 0)

    @pl.when(at == 0)
    def _():
        acc[...] = amount

    @pl.when(at > 0)
    def _():
        acc[...] += amount

    @pl.when(at == pl.num_programs(0) - 1)
    def _():
        weight_grads[...] = acc[...].astype(jnp.bfloat16)


def branch_back(grads, full, attended, sigs, masks):
    rows, width = grads.shape
    values = VEXP * DH

    def by_row(size):
        return pl.BlockSpec((BLOCK, size), lambda i: (i, 0))

    return pl.pallas_call(
        branch_back_kernel,
        grid=(rows // BLOCK,),
        in_specs=[
            by_row(width),
            pl.BlockSpec((width, values), lambda i: (0, 1), pipeline_mode=pl.Buffered(1)),
            by_row(DH),
            by_row(128),
            by_row(16),
        ],
        out_specs=[
            by_row(DH),
            pl.BlockSpec((1, 1, BLOCK), lambda i: (i, 0, 0)),
            by_row(128),
            pl.BlockSpec((width, values), lambda i: (0, 0)),
        ],
        out_shape=[
            jax.ShapeDtypeStruct((rows, DH), jnp.bfloat16),
            jax.ShapeDtypeStruct((rows // BLOCK, 1, BLOCK), jnp.float32),
            jax.ShapeDtypeStruct((rows, 128), jnp.bfloat16),
            jax.ShapeDtypeStruct((width, values), jnp.bfloat16),
        ],
        scratch_shapes=[pltpu.VMEM((width, values), jnp.float32)],
        compiler_params=pltpu.CompilerParams(vmem_limit_bytes=48 * 2**20),
        cost_estimate=cost(4 * rows * width * values, 2e7),
        name="branch_back",
    )(grads, full, attended, sigs, masks)


def turn(value, axis, by):
    size = lax.axis_size(axis)
    return lax.ppermute(value, axis, [(i, (i + by) % size) for i in range(size)])


def normalized(rows, gain, bias):
    values = rows.astype(jnp.float32)
    centred = values - jnp.mean(values, axis=1, keepdims=True)
    inverse = lax.rsqrt(jnp.mean(centred * centred, axis=1, keepdims=True) + 1e-05)
    scaled = centred * inverse
    return scaled, inverse, (scaled * gain + bias).astype(jnp.bfloat16)


def project_kernel(
    levels, rows, w_value, w_query, w_key, routers, gain, bias, order, tables,
    query, key_value, projected, sigs, masks,
):
    count = rows.shape[0]
    piece = count // (levels * HEADS)
    _, _, normed = normalized(rows[...], gain[...], bias[...])
    query[...] = dot(normed, w_query[...], 1, 0).astype(jnp.bfloat16)
    key_value[:, :DH] = dot(normed, w_key[...], 1, 0).astype(jnp.bfloat16)
    sig = 1.0 / (1.0 + jnp.exp2(-LOG2E * dot(normed, routers[...], 1, 0)))
    sigs[...] = sig
    product = dot(rows[...], w_value[...], 1, 0)
    projected[...] = product
    at = lax.broadcasted_iota(jnp.int32, (count, count), 0)
    source = lax.rem(at // piece, levels) * HEADS + at // (piece * levels)
    here = (source * piece + lax.rem(at, piece) == order[0]).astype(jnp.bfloat16)
    lane = lax.broadcasted_iota(jnp.int32, (16, count), 0)
    table = tables[0]
    named = jnp.zeros((16, count), jnp.float32)
    for which in range(2):
        option = lane - which * VEXP
        for slot in range(2):
            pick = table[2 * which + slot : 2 * which + slot + 1, :]
            hit = (option == pick) & (option >= 0) & (option < VEXP)
            named = jnp.where(hit, 1.0, named)
    mask = dot(here, named.astype(jnp.bfloat16), 1, 1)
    masks[...] = mask
    value = jnp.zeros((count, DH), jnp.float32)
    for e in range(VEXP):
        gate = sig[:, e : e + 1] * mask[:, e : e + 1]
        value += gate * product[:, e * DH : (e + 1) * DH]
    key_value[:, DH:] = value.astype(jnp.bfloat16)


def project(rows, full, gain, bias, orders, tables, levels):
    total, width = rows.shape
    count = total // HEADS

    def by_row(columns):
        return pl.BlockSpec((count, columns), lambda i: (i, 0))

    def column(size, at):
        return pl.BlockSpec((width, size), lambda i: (0, at), pipeline_mode=pl.Buffered(1))

    line = pl.BlockSpec((1, width), lambda i: (0, 0))
    shapes = [(DH, jnp.bfloat16), (2 * DH, jnp.bfloat16), (VEXP * DH, jnp.float32)]
    shapes += [(128, jnp.float32), (16, jnp.float32)]
    return pl.pallas_call(
        functools.partial(project_kernel, levels),
        grid=(HEADS,),
        in_specs=[by_row(width), column(VEXP * DH, 0)]
        + [column(DH, 2 * VEXP + i) for i in range(3)]
        + [line, line]
        + [
            pl.BlockSpec((1, 1, count), lambda i: (i, 0, 0)),
            pl.BlockSpec((1,) + tables.shape[1:], lambda i: (i, 0, 0)),
        ],
        out_specs=[by_row(columns) for columns, _ in shapes],
        out_shape=[jax.ShapeDtypeStruct((total, columns), kind) for columns, kind in shapes],
        compiler_params=pltpu.CompilerParams(vmem_limit_bytes=48 * 2**20),
        cost_estimate=cost(2 * total * width * 1024, 2e7),
        name="project",
    )(rows, full, full, full, full, gain, bias, orders, tables)


def project_back_kernel(
    rows, grads, grad_query, out_logit, projected, sigs, masks,
    w_value, w_query, w_key, routers, gain, bias,
    grad_rows, weight_grads, acc, sums,
):
    at = pl.program_id(0)
    count = rows.shape[0]
    values = VEXP * DH

    @pl.when(at == 0)
    def _():
        acc[...] = jnp.zeros_like(acc)
        sums[...] = jnp.zeros_like(sums)

    scaled, inverse, normed = normalized(rows[...], gain[...], bias[...])
    grad_key = grads[:, :DH].astype(jnp.bfloat16)
    grad_value = grads[:, DH:]
    sig, mask = sigs[...], masks[...]
    lane = lax.broadcasted_iota(jnp.int32, (count, 128), 1)
    logits = out_logit[...].astype(jnp.float32)
    parts = []
    for e in range(VEXP):
        one, on = sig[:, e : e + 1], mask[:, e : e + 1]
        parts.append((one * on * grad_value).astype(jnp.bfloat16))
        inner = jnp.sum(grad_value * projected[:, e * DH : (e + 1) * DH], axis=1, keepdims=True)
        logits = jnp.where(lane == e, inner * one * (1.0 - one) * on, logits)
    grad_projected = jnp.concatenate(parts, axis=1)
    sides = jnp.concatenate([grad_query[...], grad_key, logits.astype(jnp.bfloat16)], axis=1)
    first = dot(sides[:, :DH], w_query[...], 1, 1)
    first += dot(sides[:, DH : 2 * DH], w_key[...], 1, 1)
    first += dot(sides[:, 2 * DH :], routers[...], 1, 1)
    sums[2 * VEXP : 2 * VEXP + 1, :] += jnp.sum(first * scaled, axis=0, keepdims=True)
    sums[2 * VEXP + 1 : 2 * VEXP + 2, :] += jnp.sum(first, axis=0, keepdims=True)
    inner_grad = first * gain[...]
    inner_grad = inverse * (
        inner_grad
        - jnp.mean(inner_grad, axis=1, keepdims=True)
        - scaled * jnp.mean(inner_grad * scaled, axis=1, keepdims=True)
    )
    grad_rows[...] = (inner_grad + dot(grad_projected, w_value[...], 1, 1)).astype(jnp.bfloat16)
    acc[:, :values] += dot(rows[...], grad_projected, 0, 0)
    acc[:, values:] += dot(normed, sides, 0, 0)

    @pl.when(at == pl.num_programs(0) - 1)
    def _():
        weight_grads[:, : values + 2 * DH] = acc[:, : values + 2 * DH].astype(jnp.bfloat16)
        last = acc[:, values + 2 * DH :] + sums[...].T
        weight_grads[:, values + 2 * DH :] = last.astype(jnp.bfloat16)


def project_back(rows, grads, grad_query, out_logit, projected, sigs, masks, full, gain, bias):
    total, width = rows.shape
    count = total // HEADS
    columns = VEXP * DH + 3 * DH

    def by_row(size):
        return pl.BlockSpec((count, size), lambda i: (i, 0))

    def column(size, at):
        return pl.BlockSpec((width, size), lambda i: (0, at), pipeline_mode=pl.Buffered(1))

    line = pl.BlockSpec((1, width), lambda i: (0, 0))
    return pl.pallas_call(
        project_back_kernel,
        grid=(HEADS,),
        in_specs=[by_row(width), by_row(2 * DH), by_row(DH), by_row(128), by_row(VEXP * DH)]
        + [by_row(128), by_row(16), column(VEXP * DH, 0)]
        + [column(DH, 2 * VEXP + i) for i in range(3)]
        + [line, line],
        out_specs=[by_row(width), pl.BlockSpec((width, columns), lambda i: (0, 0))],
        out_shape=[
            jax.ShapeDtypeStruct((total, width), jnp.bfloat16),
            jax.ShapeDtypeStruct((width, columns), jnp.bfloat16),
        ],
        scratch_shapes=[
            pltpu.VMEM((width, columns), jnp.float32),
            pltpu.VMEM((128, width), jnp.float32),
        ],
        compiler_params=pltpu.CompilerParams(vmem_limit_bytes=56 * 2**20),
        cost_estimate=cost(4 * total * width * 1024, 4e7),
        name="project_back",
    )(rows, grads, grad_query, out_logit, projected, sigs, masks, full, full, full, full, gain, bias)


def shift(value, axis, by):
    count = lax.axis_size(axis)
    pairs = [(i, i + by) for i in range(count) if 0 <= i + by < count]
    return lax.ppermute(value, axis, pairs)


def body(
    tokens_in,
    out_grad,
    deal_order,
    seq_lengths,
    value_routes,
    output_routes,
    ffn_routes,
    norm1_gain,
    norm1_bias,
    norm2_gain,
    norm2_bias,
    query_weight,
    key_weight,
    value_weight,
    output_weight,
    value_router,
    output_router,
    ffn_router,
    ffn_in,
    ffn_out,
):
    groups = lax.axis_size("group")
    levels = lax.axis_size("level")
    level = lax.axis_index("level")
    head = lax.axis_index("head")
    count, width = tokens_in.shape
    piece = count // (levels * HEADS)
    wrows = query_weight.shape[0]
    experts = ffn_router.shape[1]
    local_experts = ffn_in.shape[1] // FH

    small = jnp.concatenate(
        [
            ffn_router,
            norm1_gain[:, None],
            norm1_bias[:, None],
            norm2_gain[:, None],
            norm2_bias[:, None],
        ],
        axis=1,
    )
    shared = small.shape[1]
    pad = -(shared + 2 * VEXP) % 128
    extra = jnp.concatenate(
        [
            value_router.reshape(wrows, HEADS, VEXP),
            output_router.reshape(wrows, HEADS, VEXP),
            jnp.broadcast_to(small[:, None, :], (wrows, HEADS, shared)),
            jnp.zeros((wrows, HEADS, pad), jnp.bfloat16),
        ],
        axis=2,
    )
    cols = 2 * DH + 2 * VEXP * DH + extra.shape[2]
    tables = jnp.concatenate(
        [value_routes.transpose(1, 2, 0), output_routes.transpose(1, 2, 0)], axis=1
    )
    picks = ffn_routes.reshape(levels, HEADS * piece, -1).transpose(0, 2, 1)
    arrived, own_grads, full, tables, picks, orders = start(
        tokens_in.reshape(levels, HEADS, piece, width),
        out_grad.reshape(levels, HEADS, piece, width),
        [value_weight, output_weight, query_weight, key_weight],
        extra.transpose(1, 0, 2),
        tables,
        picks,
        deal_order,
    )
    worker_in = arrived.reshape(HEADS * count, width)
    own_tokens = lax.dynamic_index_in_dim(arrived, head, 1, keepdims=False).reshape(count, width)
    in_rows = [turn(ffn_in, "group", k) for k in range(1, groups)]
    full, in_rows, ffn_out = lax.optimization_barrier(
        (full.reshape(width, cols), in_rows, ffn_out)
    )

    base = 2 * DH + 2 * VEXP * DH
    w_output = full[:, VEXP * DH : 2 * VEXP * DH]
    at = base + 2 * VEXP
    def relabelled(expert):
        share = expert // local_experts
        return (share % HEADS * levels + share // HEADS) * local_experts + expert % local_experts

    labels = jnp.arange(experts, dtype=jnp.int32)
    moved = low(relabelled(labels)[:, None] == labels[None, :])
    r_ffn = low(
        jnp.dot(full[:, at : at + experts], moved, preferred_element_type=jnp.float32)
    )
    gain_one, bias_one, gain_two, bias_two = (
        full[:, at + experts + i].astype(jnp.float32) for i in range(4)
    )
    gain_row, bias_row = gain_one[None], bias_one[None]
    orders = orders.reshape(levels, HEADS, count)
    own_order = lax.dynamic_index_in_dim(orders, level, 0, keepdims=False)[:, None, :]
    queries, key_value, projected, sigs, masks = project(
        worker_in, full, gain_row, bias_row, own_order, tables, levels
    )

    rows = HEADS * count
    reach = -(-LMAX // rows)

    ramp = jnp.arange(count, dtype=jnp.int32)

    def arrival(values):
        lead, shape = values.shape[:-3], values.shape[-1:]
        four = values.reshape(lead + (HEADS, levels, HEADS, piece) + shape)
        return jnp.swapaxes(four, -4, -3).reshape(lead + (rows,) + shape)

    orders = jnp.concatenate([jnp.zeros((reach, HEADS, count), jnp.int32), orders], axis=0)
    orders = lax.dynamic_slice_in_dim(orders, level, reach + 1, 0)
    here = orders[:, :, None, :] == ramp[None, None, :, None]
    inverse = jnp.sum(here * ramp, axis=3)
    shard = (level - reach + jnp.arange(reach + 1, dtype=jnp.int32))[:, None] * HEADS
    shard = shard + jnp.arange(HEADS, dtype=jnp.int32)[None, :]
    pos_all = jnp.where(shard[:, :, None] < 0, -1, shard[:, :, None] * count + inverse)
    pos_all = arrival(pos_all[..., None]).reshape(-1)
    positions = pos_all[reach * rows :]
    seq_ends = jnp.cumsum(seq_lengths[0])

    def starts_of(places):
        return jnp.max(jnp.where(seq_ends <= places[:, None], seq_ends, 0), axis=1)

    starts = starts_of(positions)
    blocks = rows // BLOCK
    base_block = (level - reach) * blocks
    first_block = starts_of(level * rows + jnp.arange(blocks, dtype=jnp.int32) * BLOCK) // BLOCK
    first_block = jnp.maximum(first_block - base_block, 0)

    own_routes = picks.reshape(levels, -1, HEADS, piece).transpose(2, 0, 3, 1).reshape(count, -1)
    own_routes = relabelled(own_routes)
    ffn_side = (own_routes, r_ffn, gain_two[None], bias_two[None], own_tokens)

    window = [key_value]
    own_grads = own_grads.reshape(count, width)
    for i in range(reach):
        came = shift(window[0], "level", 1)
        if i == 0:
            came, own_grads, pos_all, starts, in_rows = lax.optimization_barrier(
                (came, own_grads, pos_all, starts, [ffn_in] + in_rows)
            )
            cotangent = level_gather(own_grads, 5, True)
        if i == reach - 1:
            came, cotangent, ffn_side = lax.optimization_barrier((came, cotangent, ffn_side))
        window.insert(0, came)
    place = jnp.stack([head, lax.axis_index("group")])
    out_here = lax.all_gather(ffn_out, "level", axis=0)
    w_in = [lax.all_gather(part, "level", axis=0) for part in in_rows]


    def lines(values):
        return values.reshape(blocks, 1, BLOCK)

    attended, log_total = attend(
        first_block,
        queries,
        window,
        lines(positions),
        lines(starts),
        pos_all[:, None],
    )

    out_sig = sigs[:, VEXP : 2 * VEXP]
    out_mask = masks[:, VEXP : 2 * VEXP]
    out_gate = out_sig * out_mask
    mixed = low((out_gate[..., None] * attended[:, None, :]).reshape(rows, VEXP * DH))
    branch = level_scatter(low(transposed(mixed, w_output)), 2)
    branch, out_here = lax.optimization_barrier((branch, out_here))
    w_out = [out_here] + [turn(out_here, "group", k) for k in range(1, groups)]

    own_routes, r_ffn, gain_two, bias_two, own_tokens = ffn_side
    middle, extended, ffn_sig = enter_ffn(own_tokens, branch, own_routes, r_ffn, gain_two, bias_two)
    hidden = level_gather(extended, 3, True)
    mine = levels * local_experts
    gates = lax.dynamic_slice_in_dim(hidden, width + head * mine, mine, 1).astype(jnp.float32)
    active, grad_pre, grad_rows = ffn_front(
        place, hidden, cotangent, w_in, w_out, gates, local_experts
    )
    summed, beyond = pair_scatter(grad_rows, 4, True)
    came = to_far(beyond)
    grad_in = ffn_rear(place, hidden, grad_pre, width, groups, levels)
    in_came = [turn(grad_in[k], "group", k) for k in range(1, groups)]
    grad_out = ffn_rear(place, cotangent, active, width, groups, levels)
    out_came = [turn(grad_out[k], "group", k) for k in range(1, groups)]
    came, grad_in, grad_out = lax.optimization_barrier((came, grad_in, grad_out))
    grad_middle, own_branch, early = leave_ffn(
        middle, summed, came, own_grads, ffn_sig, own_routes, r_ffn, gain_two, bias_two
    )
    came = to_far(own_branch)
    feed = ffn_feed(place, active, w_out)
    came, feed = lax.optimization_barrier((came, feed))
    grad_branch = pair_gather(own_branch, came, 7)

    def sum_over_rows(own, others):
        total = own[0].astype(jnp.float32)
        for other in others:
            total = total + other.astype(jnp.float32)
        return lax.psum_scatter(low(total), "level", scatter_dimension=0)

    grad_branch, in_came = lax.optimization_barrier((grad_branch, in_came))
    ffn_in_grad = sum_over_rows(grad_in, in_came)
    grad_attended, row_inner, grad_out_logit, grad_w_output = branch_back(
        grad_branch, full, attended, sigs, masks
    )
    grad_queries, *grad_window = attend_back(
        first_block,
        queries,
        window,
        grad_attended,
        lines(positions),
        lines(starts),
        log_total,
        row_inner,
        pos_all[:, None],
    )
    came = shift(grad_window[0], "level", -1)
    grad_queries, out_came = lax.optimization_barrier((grad_queries, out_came))
    ffn_out_grad = sum_over_rows(grad_out, out_came)
    fed, beyond = pair_scatter(feed, 6, True)
    for i in range(1, reach + 1):
        if i < reach:
            came, fed = lax.optimization_barrier((came, fed))
        grad_both = grad_window[i].astype(jnp.float32) + came.astype(jnp.float32)
        if i < reach:
            grad_keys_sent = low(grad_both)
            came = shift(grad_keys_sent, "level", -1)
    fed_far = to_far(beyond)
    grad_inputs, late = project_back(
        worker_in,
        grad_both,
        grad_queries,
        grad_out_logit,
        projected,
        sigs,
        masks,
        full,
        gain_row,
        bias_row,
    )

    fed_far, grad_inputs = lax.optimization_barrier((fed_far, grad_inputs))
    layer_out = to_home(low(middle + fed + fed_far.astype(jnp.float32)))

    values = VEXP * DH
    layout = (
        ((0, values, True), (values, DH, True), (values + DH, DH, True), (values + 2 * DH, DH, False)),
        ((0, values, True),),
        ((0, early.shape[1], False),),
    )

    def by_owner(grads):
        return grads.reshape(groups, levels, HEADS, wrows, -1)

    input_grad, grad_value, grad_query, grad_key, sides, grad_output, common = finish(
        layout,
        grad_inputs.reshape(HEADS, HEADS, levels * piece, width),
        grad_middle.reshape(HEADS, levels * piece, width),
        by_owner(late),
        by_owner(grad_w_output),
        by_owner(early),
    )
    norms = jnp.sum(sides[:, :, 2 * VEXP : 2 * VEXP + 2], axis=0)
    common = jnp.sum(common[:, :, : experts + 2], axis=0)
    router_grad = common[:, :experts].reshape(wrows, HEADS, levels, local_experts)

    def side(first):
        return sides[:, :, first : first + VEXP].transpose(1, 0, 2).reshape(wrows, HEADS * VEXP)

    return (
        layer_out,
        input_grad.reshape(count, width),
        norms[:, 0],
        norms[:, 1],
        common[:, experts],
        common[:, experts + 1],
        grad_query,
        grad_key,
        grad_value,
        grad_output,
        side(0),
        side(VEXP),
        jnp.swapaxes(router_grad, 1, 2).reshape(wrows, experts),
        ffn_in_grad.astype(jnp.float32),
        ffn_out_grad.astype(jnp.float32),
    )


def solution(mesh):
    groups, shards = mesh.devices.shape
    fine = Mesh(mesh.devices.reshape(groups, shards // HEADS, HEADS), TOK)
    two, one, three = P(TOK, None), P(TOK), P(TOK, None, None)
    ffn = P("group", ("level", "head"))
    return jax.shard_map(
        body,
        mesh=fine,
        in_specs=(two, two, two, P("group", None), three, three, two, one, one, one, one)
        + (two,) * 7
        + (ffn, ffn),
        out_specs=(two, two, one, one, one, one) + (two,) * 7 + (ffn, ffn),
        check_vma=False,
    )
```

```python
import functools

import jax
import jax.numpy as jnp
from jax import lax
from jax.experimental import pallas as pl
from jax.experimental.pallas import tpu as pltpu
from jax.sharding import Mesh, PartitionSpec as P

HEADS = 4
DH = 128
VEXP = 5
FH = 128
LMAX = 4096

TOK = ("group", "level", "head")


def transposed(left_side, right_side):
    return lax.dot_general(
        left_side, right_side, (((1,), (1,)), ((), ())), preferred_element_type=jnp.float32
    )


def low(value):
    return value.astype(jnp.bfloat16)


def to_home(rows):
    levels = lax.axis_size("level")
    count = rows.shape[0]
    out = rows.reshape(HEADS, levels, count // levels // HEADS, -1).transpose(1, 0, 2, 3)
    back = lax.all_to_all(
        out.reshape(levels, count // levels, -1), "level", split_axis=0, concat_axis=0, tiled=True
    )
    return back.reshape(count, -1)


MESH = pl.DeviceIdType.MESH


def partners(head):
    near = head + 1 - 2 * lax.rem(head, 2)
    far = lax.rem(head + 2, HEADS)
    return near, far


def greet(near, far):
    barrier = pltpu.get_barrier_semaphore()
    for peer in (near, far):
        pl.semaphore_signal(barrier, inc=1, device_id={"head": peer}, device_id_type=MESH)
    pl.semaphore_wait(barrier, 2)


def remote(src, dst, send, recv, peer):
    return pltpu.make_async_remote_copy(
        src_ref=src,
        dst_ref=dst,
        send_sem=send,
        recv_sem=recv,
        device_id={"head": peer},
        device_id_type=MESH,
    )


def cost(flops, moved):
    return pl.CostEstimate(flops=int(flops), bytes_accessed=int(moved), transcendentals=0)


def gather_kernel(
    by_source, own, out, local_sem, near_send, near_recv, far_send, far_recv, pass_send, pass_recv
):
    head = lax.axis_index("head")
    near, far = partners(head)
    greet(near, far)

    def spot(i, source):
        return out.at[source, i] if by_source else out.at[i, source]

    pieces = range(HEADS)
    to_far = [remote(own.at[i], spot(i, head), far_send.at[i], far_recv.at[i], far) for i in pieces]
    to_near = [
        remote(own.at[i], spot(i, head), near_send.at[i], near_recv.at[i], near) for i in pieces
    ]
    passed = [
        remote(spot(i, far), spot(i, far), pass_send.at[i], pass_recv.at[i], near) for i in pieces
    ]
    kept = [pltpu.make_async_copy(own.at[i], spot(i, head), local_sem.at[i]) for i in pieces]
    for copy in to_far + to_near + kept:
        copy.start()
    for i in pieces:
        to_far[i].wait_recv()
        passed[i].start()
    for i in pieces:
        to_near[i].wait_recv()
        passed[i].wait_recv()
        kept[i].wait()
        to_far[i].wait_send()
        to_near[i].wait_send()
        passed[i].wait_send()


def level_gather(rows, collective_id, by_source=False):
    count, width = rows.shape
    whole = pl.pallas_call(
        functools.partial(gather_kernel, by_source),
        out_shape=jax.ShapeDtypeStruct((HEADS, HEADS, count // HEADS, width), rows.dtype),
        in_specs=[pl.BlockSpec(memory_space=pltpu.VMEM)],
        out_specs=pl.BlockSpec(memory_space=pl.ANY),
        scratch_shapes=[pltpu.SemaphoreType.DMA((HEADS,))] * 7,
        compiler_params=pltpu.CompilerParams(collective_id=collective_id, has_side_effects=True),
        cost_estimate=cost(0, 90e6),
        name="level_gather",
    )(rows.reshape(HEADS, count // HEADS, width))
    return whole.reshape(HEADS * count, width)


def scatter_kernel(
    by_source, part, out, near_buf, send_buf, far_buf, near_send, near_recv, far_send, far_recv
):
    head = lax.axis_index("head")
    near, far = partners(head)
    greet(near, far)
    across = HEADS - 1 - head
    pieces = range(HEADS)

    def spot(i, dest):
        return (dest, i) if by_source else (i, dest)

    def to_near(slot, i, dest):
        return remote(
            part.at[spot(i, dest)],
            near_buf.at[slot, i],
            near_send.at[slot, i],
            near_recv.at[slot, i],
            near,
        )

    first = [to_near(0, i, across) for i in pieces]
    second = [to_near(1, i, near) for i in pieces]
    onward = [
        remote(send_buf.at[i], far_buf.at[i], far_send.at[i], far_recv.at[i], far) for i in pieces
    ]
    for copy in first + second:
        copy.start()
    for i in pieces:
        first[i].wait_recv()
        both = part[spot(i, far)].astype(jnp.float32) + near_buf[0, i].astype(jnp.float32)
        send_buf[i] = both.astype(jnp.bfloat16)
        onward[i].start()
    for i in pieces:
        second[i].wait_recv()
        out[i] = part[spot(i, head)].astype(jnp.float32) + near_buf[1, i].astype(jnp.float32)
    for i in pieces:
        onward[i].wait_recv()
        out[i] = out[i] + far_buf[i].astype(jnp.float32)
    for i in pieces:
        first[i].wait_send()
        second[i].wait_send()
        onward[i].wait_send()


def level_scatter(rows, collective_id, by_source=False):
    total, width = rows.shape
    piece = total // (HEADS * HEADS)
    low_type = jnp.bfloat16
    mine = pl.pallas_call(
        functools.partial(scatter_kernel, by_source),
        out_shape=jax.ShapeDtypeStruct((HEADS, piece, width), jnp.float32),
        in_specs=[pl.BlockSpec(memory_space=pltpu.VMEM)],
        out_specs=pl.BlockSpec(memory_space=pltpu.VMEM),
        scratch_shapes=[
            pltpu.VMEM((2, HEADS, piece, width), low_type),
            pltpu.VMEM((HEADS, piece, width), low_type),
            pltpu.VMEM((HEADS, piece, width), low_type),
            pltpu.SemaphoreType.DMA((2, HEADS)),
            pltpu.SemaphoreType.DMA((2, HEADS)),
            pltpu.SemaphoreType.DMA((HEADS,)),
            pltpu.SemaphoreType.DMA((HEADS,)),
        ],
        compiler_params=pltpu.CompilerParams(
            collective_id=collective_id, has_side_effects=True, vmem_limit_bytes=32 * 2**20
        ),
        cost_estimate=cost(0, 80e6),
        name="level_scatter",
    )(rows.reshape(HEADS, HEADS, piece, width))
    return mine.reshape(HEADS * piece, width)


def meet(near):
    barrier = pltpu.get_barrier_semaphore()
    pl.semaphore_signal(barrier, inc=1, device_id={"head": near}, device_id_type=MESH)
    pl.semaphore_wait(barrier, 1)


def pair_scatter_kernel(by_source, part, out, out_far, near_buf, send, recv):
    head = lax.axis_index("head")
    near, far = partners(head)
    meet(near)
    across = HEADS - 1 - head
    pieces = range(HEADS)

    def spot(i, dest):
        return (dest, i) if by_source else (i, dest)

    def to_near(slot, i, dest):
        return remote(
            part.at[spot(i, dest)], near_buf.at[slot, i], send.at[slot, i], recv.at[slot, i], near
        )

    first = [to_near(0, i, across) for i in pieces]
    second = [to_near(1, i, near) for i in pieces]
    for copy in first + second:
        copy.start()
    for i in pieces:
        first[i].wait_recv()
        both = part[spot(i, far)].astype(jnp.float32) + near_buf[0, i].astype(jnp.float32)
        out_far[i] = both.astype(jnp.bfloat16)
    for i in pieces:
        second[i].wait_recv()
        out[i] = part[spot(i, head)].astype(jnp.float32) + near_buf[1, i].astype(jnp.float32)
    for i in pieces:
        first[i].wait_send()
        second[i].wait_send()


def pair_scatter(rows, collective_id, by_source=False):
    total, width = rows.shape
    piece = total // (HEADS * HEADS)
    mine, other = pl.pallas_call(
        functools.partial(pair_scatter_kernel, by_source),
        out_shape=[
            jax.ShapeDtypeStruct((HEADS, piece, width), jnp.float32),
            jax.ShapeDtypeStruct((HEADS, piece, width), jnp.bfloat16),
        ],
        in_specs=[pl.BlockSpec(memory_space=pltpu.VMEM)],
        out_specs=[pl.BlockSpec(memory_space=pltpu.VMEM)] * 2,
        scratch_shapes=[
            pltpu.VMEM((2, HEADS, piece, width), jnp.bfloat16),
            pltpu.SemaphoreType.DMA((2, HEADS)),
            pltpu.SemaphoreType.DMA((2, HEADS)),
        ],
        compiler_params=pltpu.CompilerParams(
            collective_id=collective_id, has_side_effects=True, vmem_limit_bytes=32 * 2**20
        ),
        cost_estimate=cost(0, 25e6),
        name="pair_scatter",
    )(rows.reshape(HEADS, HEADS, piece, width))
    return mine.reshape(HEADS * piece, width), other.reshape(HEADS * piece, width)


def pair_gather_kernel(by_source, own, other, out, local_sem, send, recv):
    head = lax.axis_index("head")
    near, far = partners(head)
    meet(near)
    copies, kept = [], []
    for i in range(HEADS):
        for slot, (block, source) in enumerate(((own, head), (other, far))):
            place = out.at[source, i] if by_source else out.at[i, source]
            copies.append(
                remote(block.at[i], place, send.at[slot, i], recv.at[slot, i], near)
            )
            kept.append(pltpu.make_async_copy(block.at[i], place, local_sem.at[slot, i]))
    for copy in copies + kept:
        copy.start()
    for copy in copies + kept:
        copy.wait()


def pair_gather(own, other, collective_id, by_source=False):
    count, width = own.shape
    split = (HEADS, count // HEADS, width)
    whole = pl.pallas_call(
        functools.partial(pair_gather_kernel, by_source),
        out_shape=jax.ShapeDtypeStruct((HEADS,) + split, own.dtype),
        in_specs=[pl.BlockSpec(memory_space=pltpu.VMEM)] * 2,
        out_specs=pl.BlockSpec(memory_space=pl.ANY),
        scratch_shapes=[pltpu.SemaphoreType.DMA((2, HEADS))] * 3,
        compiler_params=pltpu.CompilerParams(collective_id=collective_id, has_side_effects=True),
        cost_estimate=cost(0, 25e6),
        name="pair_gather",
    )(own.reshape(split), other.reshape(split))
    return whole.reshape(HEADS * count, width)


def to_far(rows):
    return lax.ppermute(rows, "head", [(i, (i + 2) % HEADS) for i in range(HEADS)])


def ring(axis):
    me, size = lax.axis_index(axis), lax.axis_size(axis)
    ahead = [lax.rem(me + k, size) for k in range(1, size)]
    behind = [lax.rem(me + size - k, size) for k in range(1, size)]
    return me, ahead, behind


def reach_out(src, dst, send, recv, peer):
    return pltpu.make_async_remote_copy(
        src_ref=src, dst_ref=dst, send_sem=send, recv_sem=recv, device_id=peer, device_id_type=MESH
    )


def greet_all(peers):
    barrier = pltpu.get_barrier_semaphore()
    for peer in peers:
        pl.semaphore_signal(barrier, inc=1, device_id=peer, device_id_type=MESH)
    pl.semaphore_wait(barrier, len(peers))


def start_kernel(
    tokens, cotangents, value, output, query, key, extra, tables, picks, order,
    rows, grads, full, routes, chosen_rows, orders, weights, own_sem, *sems
):
    sems = iter(sems)

    def pair():
        return next(sems), next(sems)

    group, groups_ahead, _ = ring("group")
    level, levels_ahead, levels_behind = ring("level")
    head = lax.axis_index("head")
    near, far = partners(head)
    mates = [near, far, HEADS - 1 - head]
    for to in range(HEADS):
        at = 0
        for part in (value, output, query, key):
            size = part.shape[1] // HEADS
            weights[to, :, at : at + size] = part[:, to * size : (to + 1) * size]
            at += size
        weights[to, :, at:] = extra[to]
    greet_all(
        [{"head": m} for m in mates]
        + [{"level": n} for n in levels_ahead]
        + [{"group": n} for n in groups_ahead]
    )
    started = []

    def send(src, dst, send_sem, recv_sem, peer):
        copy = reach_out(src, dst, send_sem, recv_sem, peer)
        copy.start()
        started.append(copy)
        return copy

    out_s, out_r = pair()
    pick_s, pick_r = pair()
    crossing, picking = [], []
    for k, to in enumerate(levels_ahead):
        peer = {"level": to}
        crossing.append(send(tokens.at[to], rows.at[:, head, level], out_s.at[k], out_r.at[k], peer))
    mate_s, mate_r = pair()
    table_s, table_r = pair()
    order_s, order_r = pair()
    to_mates, order_mates, table_mates = [], [], []
    for k, to in enumerate(mates):
        peer = {"head": to}
        to_mates.append(
            send(weights.at[to], full.at[group, level, head], mate_s.at[k], mate_r.at[k], peer)
        )
        order_mates.append(
            send(order, orders.at[level, head], order_s.at[k], order_r.at[k], peer)
        )
    own = [
        (tokens.at[level], rows.at[:, head, level]),
        (weights.at[head], full.at[group, level, head]),
        (tables.at[head], routes.at[head]),
        (picks.at[level], chosen_rows.at[level]),
        (order, orders.at[level, head]),
        (cotangents.at[level], grads.at[:, level]),
    ]
    own = [pltpu.make_async_copy(src, dst, own_sem.at[i]) for i, (src, dst) in enumerate(own)]
    for copy in own:
        copy.start()
    far_s, far_r = pair()
    near_s, near_r = pair()
    pass_s, pass_r = pair()
    to_far, to_near = [], []

    def share(k, src, source):
        place = rows.at[:, head, source]
        to_far.append(send(src, place, far_s.at[k], far_r.at[k], {"head": far}))
        to_near.append(send(src, place, near_s.at[k], near_r.at[k], {"head": near}))

    share(0, tokens.at[level], level)
    block_s, block_r = pair()
    group_s, group_r = pair()
    orders_s, orders_r = pair()
    for copy in to_mates:
        copy.wait_recv()
    own[1].wait()
    blocks, grouped, ordered = [], [], []

    def to_groups(j, source):
        for k, to in enumerate(groups_ahead):
            block = full.at[group, source]
            grouped.append(
                send(block, block, group_s.at[k, j], group_r.at[k, j], {"group": to})
            )

    for k, to in enumerate(levels_ahead):
        block = full.at[group, level]
        blocks.append(send(block, block, block_s.at[k], block_r.at[k], {"level": to}))
    to_groups(0, level)
    for k, to in enumerate(mates):
        table_mates.append(
            send(tables.at[to], routes.at[head], table_s.at[k], table_r.at[k], {"head": to})
        )
    for k, to in enumerate(levels_ahead):
        picking.append(
            send(picks.at[to], chosen_rows.at[level], pick_s.at[k], pick_r.at[k], {"level": to})
        )
    for copy in order_mates:
        copy.wait_recv()
    own[4].wait()
    for k, to in enumerate(levels_ahead):
        block = orders.at[level]
        ordered.append(send(block, block, orders_s.at[k], orders_r.at[k], {"level": to}))
    for k, source in enumerate(levels_behind):
        crossing[k].wait_recv()
        share(k + 1, rows.at[:, head, source], source)
    grad_s, grad_r = pair()
    crossed = []
    for k, to in enumerate(levels_ahead):
        crossed.append(
            send(cotangents.at[to], grads.at[:, level], grad_s.at[k], grad_r.at[k], {"level": to})
        )
    for k, source in enumerate(levels_behind):
        blocks[k].wait_recv()
        to_groups(k + 1, source)
    passed = []
    for k, source in enumerate([level] + levels_behind):
        to_far[k].wait_recv()
        place = rows.at[:, far, source]
        passed.append(send(place, place, pass_s.at[k], pass_r.at[k], {"head": near}))
    for copy in to_near + passed + grouped + table_mates + picking + ordered + crossed:
        copy.wait_recv()
    for copy in started:
        copy.wait_send()
    for i in (0, 2, 3, 5):
        own[i].wait()


def start(tokens, cotangents, weights, extra, tables, picks, order):
    groups, levels = lax.axis_size("group"), lax.axis_size("level")
    _, _, piece, width = tokens.shape
    columns = sum(part.shape[1] for part in weights) // HEADS + extra.shape[2]
    block = extra.shape[:2] + (columns,)
    shapes = [
        jax.ShapeDtypeStruct((HEADS, HEADS, levels, piece, width), tokens.dtype),
        jax.ShapeDtypeStruct((HEADS, levels, piece, width), tokens.dtype),
        jax.ShapeDtypeStruct((groups, levels) + block, extra.dtype),
        jax.ShapeDtypeStruct(tables.shape, tables.dtype),
        jax.ShapeDtypeStruct(picks.shape, picks.dtype),
        jax.ShapeDtypeStruct((levels, HEADS) + order.shape, order.dtype),
    ]
    dma = pltpu.SemaphoreType.DMA
    others, mates = (levels - 1,), (HEADS - 1,)
    counts = [others] * 2 + [mates] * 3 + [(levels,)] * 3
    counts += [others, (groups - 1, levels), others, others]
    return pl.pallas_call(
        start_kernel,
        out_shape=shapes,
        in_specs=[pl.BlockSpec(memory_space=pltpu.VMEM)] * 10,
        out_specs=[pl.BlockSpec(memory_space=pl.ANY)] * 6,
        scratch_shapes=[pltpu.VMEM(block, extra.dtype), dma((6,))] + [dma(c) for c in counts for _ in range(2)],
        compiler_params=pltpu.CompilerParams(collective_id=9, has_side_effects=True),
        cost_estimate=cost(0, 200e6),
        name="start",
    )(tokens, cotangents, *weights, extra, tables, picks, order)


def finish_kernel(layout, *refs):
    refs = iter(refs)
    count = len(layout)

    def take(n):
        return [next(refs) for _ in range(n)]

    part, middle = take(2)
    grads = take(count)
    (home_grad,) = take(1)
    results = [take(len(pieces)) for pieces in layout]
    near_buf, send_buf, far_buf, total, back_buf, came_buf = take(6)
    group_buf, level_send, level_buf, head_send, owned = (take(count) for _ in range(5))

    def pair():
        return next(refs), next(refs)

    group, groups_ahead, _ = ring("group")
    level, levels_ahead, levels_behind = ring("level")
    head = lax.axis_index("head")
    near, far = partners(head)
    across = HEADS - 1 - head
    mates = [near, far, across]
    greet_all(
        [{"head": m} for m in mates]
        + [{"level": n} for n in levels_ahead]
        + [{"group": n} for n in groups_ahead]
    )
    started = []

    def send(src, dst, send_sem, recv_sem, peer):
        copy = reach_out(src, dst, send_sem, recv_sem, peer)
        copy.start()
        started.append(copy)
        return copy

    pieces = range(HEADS)
    sets = range(count)
    near_s, near_r = pair()
    far_s, far_r = pair()
    back_s, back_r = pair()
    group_s, group_r = pair()
    level_s, level_r = pair()
    mate_s, mate_r = pair()
    first, second, onward = [], [], []
    for slot, (dest, copies) in enumerate(((across, first), (near, second))):
        for i in pieces:
            copies.append(
                send(
                    part.at[i, dest],
                    near_buf.at[slot, i],
                    near_s.at[slot, i],
                    near_r.at[slot, i],
                    {"head": near},
                )
            )
    order = levels_ahead + [level]
    grouped = {}
    for j, dest in enumerate(order):
        for p in sets:
            grouped[j, p] = [
                send(
                    grads[p].at[to, dest],
                    group_buf[p].at[k, j],
                    group_s.at[p, k, j],
                    group_r.at[p, k, j],
                    {"group": to},
                )
                for k, to in enumerate(groups_ahead)
            ]
    for i in pieces:
        first[i].wait_recv()
        both = part[i, far].astype(jnp.float32) + near_buf[0, i].astype(jnp.float32)
        send_buf[i] = both.astype(jnp.bfloat16)
        onward.append(send(send_buf.at[i], far_buf.at[i], far_s.at[i], far_r.at[i], {"head": far}))
    for i in pieces:
        second[i].wait_recv()
        both = part[i, head].astype(jnp.float32) + near_buf[1, i].astype(jnp.float32)
        total[i] = both + middle[i]
    leveled = {}
    for j, dest in enumerate(order):
        for p in sets:
            amount = grads[p][group, dest].astype(jnp.float32)
            for k, copy in enumerate(grouped[j, p]):
                copy.wait_recv()
                amount = amount + group_buf[p][k, j].astype(jnp.float32)
            level_send[p][j] = amount.astype(jnp.bfloat16)
            if j < len(levels_ahead):
                leveled[j, p] = send(
                    level_send[p].at[j],
                    level_buf[p].at[j],
                    level_s.at[p, j],
                    level_r.at[p, j],
                    {"level": dest},
                )
    for i in pieces:
        onward[i].wait_recv()
        both = total[i] + far_buf[i].astype(jnp.float32)
        back_buf[i] = both.astype(jnp.bfloat16).reshape(back_buf.shape[1:])
    backs = [
        send(back_buf.at[:, to], came_buf.at[level], back_s.at[k], back_r.at[k], {"level": to})
        for k, to in enumerate(levels_ahead)
    ]
    sharing = []
    for p in sets:
        amount = level_send[p][len(levels_ahead)].astype(jnp.float32)
        for j in range(len(levels_ahead)):
            leveled[j, p].wait_recv()
            amount = amount + level_buf[p][j].astype(jnp.float32)
        head_send[p][...] = amount.astype(jnp.bfloat16)
        sharing += [
            send(
                head_send[p].at[to],
                owned[p].at[head],
                mate_s.at[p, k],
                mate_r.at[p, k],
                {"head": to},
            )
            for k, to in enumerate(mates)
        ]
        owned[p][head] = head_send[p][head]
    home_grad[level] = back_buf[:, level].astype(jnp.float32)
    for k, source in enumerate(levels_behind):
        backs[k].wait_recv()
        home_grad[source] = came_buf[source].astype(jnp.float32)
    for copy in sharing:
        copy.wait_recv()
    for p in sets:
        for out, (first_column, size, joined) in zip(results[p], layout[p]):
            for h in range(HEADS):
                value = owned[p][h, :, first_column : first_column + size].astype(jnp.float32)
                if joined:
                    out[:, h * size : (h + 1) * size] = value
                else:
                    out[h] = value
    for copy in started:
        copy.wait_send()


def finish(layout, part, middle, *grads):
    groups, levels = lax.axis_size("group"), lax.axis_size("level")
    _, count, width = middle.shape
    piece = count // levels
    low_type = jnp.bfloat16
    blocks = [grad.shape[2:] for grad in grads]
    sets = len(grads)
    dma = pltpu.SemaphoreType.DMA
    counts = [(2, HEADS), (HEADS,), (levels - 1,)]
    counts += [(sets, groups - 1, levels), (sets, levels - 1), (sets, HEADS - 1)]
    vmem = pl.BlockSpec(memory_space=pltpu.VMEM)
    shapes = []
    for pieces in layout:
        for _, size, joined in pieces:
            shape = (blocks[0][1], HEADS * size) if joined else (HEADS, blocks[0][1], size)
            shapes.append(jax.ShapeDtypeStruct(shape, jnp.float32))
    return pl.pallas_call(
        functools.partial(finish_kernel, layout),
        out_shape=[jax.ShapeDtypeStruct((levels, HEADS, piece, width), jnp.float32)] + shapes,
        in_specs=[vmem] * (2 + sets),
        out_specs=[vmem] * (1 + len(shapes)),
        scratch_shapes=[
            pltpu.VMEM((2, HEADS, count, width), low_type),
            pltpu.VMEM((HEADS, count, width), low_type),
            pltpu.VMEM((HEADS, count, width), low_type),
            pltpu.VMEM((HEADS, count, width), jnp.float32),
            pltpu.VMEM((HEADS, levels, piece, width), low_type),
            pltpu.VMEM((levels, HEADS, piece, width), low_type),
        ]
        + [pltpu.VMEM((groups - 1, levels) + block, low_type) for block in blocks]
        + [pltpu.VMEM((levels,) + block, low_type) for block in blocks]
        + [pltpu.VMEM((levels - 1,) + block, low_type) for block in blocks]
        + [pltpu.VMEM(block, low_type) for block in blocks] * 2
        + [dma(c) for c in counts for _ in range(2)],
        compiler_params=pltpu.CompilerParams(
            collective_id=10, has_side_effects=True, vmem_limit_bytes=56 * 2**20
        ),
        cost_estimate=cost(0, 200e6),
        name="finish",
    )(part, middle, *grads)


BLOCK = 512
LOG2E = 1.4426950408889634


def dot(left_side, right_side, left_dim, right_dim):
    return lax.dot_general(
        left_side,
        right_side,
        (((left_dim,), (right_dim,)), ((), ())),
        preferred_element_type=jnp.float32,
    )


def attend_kernel(parts, first, q, *refs):
    keys, values = refs[:parts], refs[parts : 2 * parts]
    pos_q, start_q, pos_k, out, lse, top, total, acc = refs[2 * parts :]
    at = pl.program_id(0)
    blocks = pl.num_programs(0)
    rate = LOG2E * DH ** (-0.5)
    top[...] = jnp.full_like(top, -1e30)
    total[...] = jnp.zeros_like(total)
    acc[...] = jnp.zeros_like(acc)
    query = q[...]
    row_at, row_from = pos_q[0], start_q[0]

    for part in range(parts):

        def step(block, carry, k=keys[part], v=values[part], part=part):
            rows = pl.ds(pl.multiple_of(block * BLOCK, BLOCK), BLOCK)
            spot = pl.ds(pl.multiple_of((part * blocks + block) * BLOCK, BLOCK), BLOCK)
            scores = dot(k[rows, :], query, 1, 1)
            key_at = pos_k[spot, :]
            scores = jnp.where((key_at >= row_from) & (key_at <= row_at), scores, -1e30)
            old = top[...]
            new = jnp.maximum(old, jnp.max(scores, axis=0, keepdims=True))
            shrink = jnp.exp2((old - new) * rate)
            weight = jnp.exp2((scores - new) * rate)
            total[...] = total[...] * shrink + jnp.sum(weight, axis=0, keepdims=True)
            acc[...] = acc[...] * shrink + dot(v[rows, :], weight.astype(jnp.bfloat16), 0, 0)
            top[...] = new
            return carry

        begin = jnp.maximum(first[at] - part * blocks, 0)
        end = at + 1 if part == parts - 1 else blocks
        lax.fori_loop(begin, end, step, 0)
    out[...] = (acc[...] / total[...]).T
    lse[0] = top[...] * rate + jnp.log2(total[...])


def attend(first, queries, window, pos_q, start_q, pos_k):
    rows = queries.shape[0]
    parts = len(window)
    line = pl.BlockSpec((1, 1, BLOCK), lambda i, *_: (i, 0, 0))
    grid_spec = pltpu.PrefetchScalarGridSpec(
        num_scalar_prefetch=1,
        grid=(rows // BLOCK,),
        in_specs=[pl.BlockSpec((BLOCK, DH), lambda i, *_: (i, 0))]
        + [pl.BlockSpec((rows, DH), lambda i, *_: (0, 0))] * parts
        + [pl.BlockSpec((rows, DH), lambda i, *_: (0, 1))] * parts
        + [line, line, pl.BlockSpec((parts * rows, 1), lambda i, *_: (0, 0))],
        out_specs=[pl.BlockSpec((BLOCK, DH), lambda i, *_: (i, 0)), line],
        scratch_shapes=[
            pltpu.VMEM((1, BLOCK), jnp.float32),
            pltpu.VMEM((1, BLOCK), jnp.float32),
            pltpu.VMEM((DH, BLOCK), jnp.float32),
        ],
    )
    return pl.pallas_call(
        functools.partial(attend_kernel, parts),
        grid_spec=grid_spec,
        out_shape=[
            jax.ShapeDtypeStruct((rows, DH), jnp.float32),
            jax.ShapeDtypeStruct((rows // BLOCK, 1, BLOCK), jnp.float32),
        ],
        compiler_params=pltpu.CompilerParams(vmem_limit_bytes=48 * 2**20),
        cost_estimate=cost(2e10, 1e7),
        name="attend",
    )(first, queries, *window, *window, pos_q, start_q, pos_k)


def attend_back_kernel(parts, first, q, *refs):
    keys, values = refs[:parts], refs[parts : 2 * parts]
    grad, pos_q, start_q, lse, inner, pos_k, grad_q = refs[2 * parts : 2 * parts + 7]
    grads = refs[2 * parts + 7 : 3 * parts + 7]
    sum_k, sum_v, acc = refs[3 * parts + 7 :]
    at = pl.program_id(0)
    blocks = pl.num_programs(0)
    rate = LOG2E * DH ** (-0.5)
    scale = DH ** (-0.5)

    @pl.when(at == 0)
    def _():
        sum_k[...] = jnp.zeros_like(sum_k)
        sum_v[...] = jnp.zeros_like(sum_v)

    acc[...] = jnp.zeros_like(acc)
    query, grad_out = q[...], grad[...]
    row_at, row_from, row_lse, row_inner = pos_q[0], start_q[0], lse[0], inner[0]

    for part in range(parts):

        def step(block, carry, k=keys[part], v=values[part], part=part):
            rows = pl.ds(pl.multiple_of(block * BLOCK, BLOCK), BLOCK)
            spot = pl.ds(pl.multiple_of((part * blocks + block) * BLOCK, BLOCK), BLOCK)
            key, value = k[rows, :], v[rows, :]
            scores = dot(key, query, 1, 1)
            key_at = pos_k[spot, :]
            seen = (key_at >= row_from) & (key_at <= row_at)
            soft = jnp.where(seen, jnp.exp2(scores * rate - row_lse), 0.0)
            grad_soft = dot(value, grad_out, 1, 1)
            grad_scores = (soft * (grad_soft - row_inner)).astype(jnp.bfloat16)
            sum_v[spot, :] += dot(soft.astype(jnp.bfloat16), grad_out, 1, 0)
            sum_k[spot, :] += dot(grad_scores, query, 1, 0)
            acc[...] += dot(grad_scores, key, 0, 0)
            return carry

        begin = jnp.maximum(first[at] - part * blocks, 0)
        end = at + 1 if part == parts - 1 else blocks
        lax.fori_loop(begin, end, step, 0)
    grad_q[...] = (acc[...] * scale).astype(jnp.bfloat16)

    @pl.when(at == blocks - 1)
    def _():
        size = grads[0].shape[0]
        for part in range(parts):
            spot = slice(part * size, (part + 1) * size)
            grads[part][:, :DH] = (sum_k[spot, :] * scale).astype(grads[part].dtype)
            grads[part][:, DH:] = sum_v[spot, :].astype(grads[part].dtype)


def attend_back(first, queries, window, grads, pos_q, start_q, lse, inner, pos_k):
    rows = queries.shape[0]
    parts = len(window)
    block = pl.BlockSpec((BLOCK, DH), lambda i, *_: (i, 0))
    line = pl.BlockSpec((1, 1, BLOCK), lambda i, *_: (i, 0, 0))
    grid_spec = pltpu.PrefetchScalarGridSpec(
        num_scalar_prefetch=1,
        grid=(rows // BLOCK,),
        in_specs=[block]
        + [pl.BlockSpec((rows, DH), lambda i, *_: (0, 0))] * parts
        + [pl.BlockSpec((rows, DH), lambda i, *_: (0, 1))] * parts
        + [block, line, line, line, line]
        + [pl.BlockSpec((parts * rows, 1), lambda i, *_: (0, 0))],
        out_specs=[block] + [pl.BlockSpec((rows, 2 * DH), lambda i, *_: (0, 0))] * parts,
        scratch_shapes=[
            pltpu.VMEM((parts * rows, DH), jnp.float32),
            pltpu.VMEM((parts * rows, DH), jnp.float32),
            pltpu.VMEM((BLOCK, DH), jnp.float32),
        ],
    )
    kinds = [jnp.bfloat16] * (parts - 1) + [jnp.float32]
    return pl.pallas_call(
        functools.partial(attend_back_kernel, parts),
        grid_spec=grid_spec,
        out_shape=[jax.ShapeDtypeStruct((rows, DH), jnp.bfloat16)]
        + [jax.ShapeDtypeStruct((rows, 2 * DH), kind) for kind in kinds],
        compiler_params=pltpu.CompilerParams(vmem_limit_bytes=48 * 2**20),
        cost_estimate=cost(2e10, 1e7),
        name="attend_back",
    )(first, queries, *window, *window, grads, pos_q, start_q, lse, inner, pos_k)


def columns_of(ref, group, groups, step, depth):
    at = lax.rem(group + step + groups, groups) * depth
    return ref.at[:, pl.ds(pl.multiple_of(at, 128), depth)]


def front_kernel(groups, local, place, hidden, grads, *refs):
    w_in, w_out = refs[:groups], refs[groups : 2 * groups]
    gates, active, grad_pre, rows_out, turned, acc = refs[2 * groups :]
    levels, depth, width = w_in[0].shape
    tile = hidden.shape[0]
    model = groups * depth
    parts = [slice(step * depth, (step + 1) * depth) for step in range(groups)]
    for step in range(groups):
        turned[0, :, parts[step]] = columns_of(hidden, place[1], groups, -step, depth)[...]
        turned[1, :, parts[step]] = columns_of(grads, place[1], groups, -step, depth)[...]
    gate_grads = []
    for level in range(levels):
        pre_act = jnp.zeros((tile, width), jnp.float32)
        grad_active = jnp.zeros((tile, width), jnp.float32)
        for step in range(groups):
            pre_act += dot(turned[0, :, parts[step]], w_in[step][level], 1, 0)
            grad_active += dot(turned[1, :, parts[step]], w_out[step][level], 1, 0)
        first = level * local
        gate = jnp.concatenate(
            [jnp.broadcast_to(gates[:, first + e : first + e + 1], (tile, FH)) for e in range(local)],
            axis=1,
        )
        sig = 1.0 / (1.0 + jnp.exp2(-LOG2E * pre_act))
        act_pre = pre_act * sig
        columns = slice(level * width, (level + 1) * width)
        active[:, columns] = (act_pre * gate).astype(jnp.bfloat16)
        product = grad_active * act_pre
        for e in range(local):
            gate_grads.append(
                jnp.sum(product[:, e * FH : (e + 1) * FH], axis=1, keepdims=True)
            )
        slope = sig * (1.0 + pre_act * (1.0 - sig))
        low_pre = (grad_active * gate * slope).astype(jnp.bfloat16)
        grad_pre[:, columns] = low_pre
        for step in range(groups):
            back = dot(low_pre, w_in[step][level], 1, 1)
            acc[:, parts[step]] = back if level == 0 else acc[:, parts[step]] + back
    for step in range(groups):
        columns_of(rows_out, place[1], groups, -step, depth)[...] = acc[:, parts[step]].astype(
            jnp.bfloat16
        )
    spare = rows_out.shape[1] - model
    lane = lax.broadcasted_iota(jnp.int32, (tile, spare), 1) - place[0] * (levels * local)
    spread = jnp.zeros((tile, spare), jnp.float32)
    for e, column in enumerate(gate_grads):
        spread = jnp.where(lane == e, column, spread)
    rows_out[:, model:] = spread.astype(jnp.bfloat16)


def ffn_front(place, hidden, grads, w_in, w_out, gates, local):
    rows, wide = hidden.shape
    groups = len(w_in)
    levels, depth, width = w_in[0].shape
    tile = 512

    def by_row(columns):
        return pl.BlockSpec((tile, columns), lambda i, *_: (i, 0))

    whole = pl.BlockSpec(w_in[0].shape, lambda i, *_: (0, 0, 0), pipeline_mode=pl.Buffered(1))
    grid_spec = pltpu.PrefetchScalarGridSpec(
        num_scalar_prefetch=1,
        grid=(rows // tile,),
        in_specs=[by_row(wide), by_row(groups * depth)]
        + [whole] * (2 * groups)
        + [by_row(gates.shape[1])],
        out_specs=[by_row(levels * width), by_row(levels * width), by_row(wide)],
        scratch_shapes=[
            pltpu.VMEM((2, tile, groups * depth), jnp.bfloat16),
            pltpu.VMEM((tile, groups * depth), jnp.float32),
        ],
    )
    hidden_units = jax.ShapeDtypeStruct((rows, levels * width), jnp.bfloat16)
    return pl.pallas_call(
        functools.partial(front_kernel, groups, local),
        grid_spec=grid_spec,
        out_shape=[hidden_units, hidden_units, jax.ShapeDtypeStruct((rows, wide), jnp.bfloat16)],
        compiler_params=pltpu.CompilerParams(vmem_limit_bytes=58 * 2**20),
        cost_estimate=cost(6 * rows * groups * depth * levels * width, 3e7),
        name="ffn_front",
    )(place, hidden, grads, *w_in, *w_out, gates)


def rear_kernel(groups, place, rows_in, hidden_units, *weight_grads):
    _, depth, _ = weight_grads[0].shape
    units = hidden_units[...]
    for step in range(groups):
        part = columns_of(rows_in, place[1], groups, step, depth)
        weight_grads[step][0] = dot(part[...], units, 0, 0).astype(jnp.bfloat16)


def feed_kernel(groups, place, active, *refs):
    weights = refs[:groups]
    feed, acc = refs[groups:]
    _, depth, _ = weights[0].shape
    level = pl.program_id(0)
    act = active[...]
    for step in range(groups):
        fed = dot(act, weights[step][0], 1, 1)
        part = slice(step * depth, (step + 1) * depth)

        @pl.when(level == 0)
        def _():
            acc[:, part] = fed

        @pl.when(level > 0)
        def _():
            acc[:, part] += fed

    @pl.when(level == pl.num_programs(0) - 1)
    def _():
        for step in range(groups):
            part = slice(step * depth, (step + 1) * depth)
            columns_of(feed, place[1], groups, -step, depth)[...] = acc[:, part].astype(
                jnp.bfloat16
            )


def whole_rows(rows, columns):
    return pl.BlockSpec((rows, columns), lambda i, *_: (0, 0), pipeline_mode=pl.Buffered(1))


def ffn_feed(place, active, weights):
    rows = active.shape[0]
    groups = len(weights)
    levels, depth, width = weights[0].shape
    return pl.pallas_call(
        functools.partial(feed_kernel, groups),
        grid_spec=pltpu.PrefetchScalarGridSpec(
            num_scalar_prefetch=1,
            grid=(levels,),
            in_specs=[pl.BlockSpec((rows, width), lambda i, *_: (0, i))]
            + [pl.BlockSpec((1, depth, width), lambda i, *_: (i, 0, 0))] * groups,
            out_specs=whole_rows(rows, groups * depth),
            scratch_shapes=[pltpu.VMEM((rows, groups * depth), jnp.float32)],
        ),
        out_shape=jax.ShapeDtypeStruct((rows, groups * depth), jnp.bfloat16),
        compiler_params=pltpu.CompilerParams(vmem_limit_bytes=58 * 2**20),
        cost_estimate=cost(2 * rows * groups * depth * levels * width, 3e7),
        name="ffn_feed",
    )(place, active, *weights)


def ffn_rear(place, rows_in, units, model, groups, levels):
    rows, wide = rows_in.shape
    width = units.shape[1] // levels
    depth = model // groups
    return pl.pallas_call(
        functools.partial(rear_kernel, groups),
        grid_spec=pltpu.PrefetchScalarGridSpec(
            num_scalar_prefetch=1,
            grid=(levels,),
            in_specs=[
                whole_rows(rows, wide),
                pl.BlockSpec((rows, width), lambda i, *_: (0, i)),
            ],
            out_specs=[pl.BlockSpec((1, depth, width), lambda i, *_: (i, 0, 0))] * groups,
        ),
        out_shape=[jax.ShapeDtypeStruct((levels, depth, width), jnp.bfloat16)] * groups,
        compiler_params=pltpu.CompilerParams(vmem_limit_bytes=58 * 2**20),
        cost_estimate=cost(2 * rows * groups * depth * levels * width, 3e7),
        name="ffn_rear",
    )(place, rows_in, units)


def named_by(routes, count):
    lane = lax.broadcasted_iota(jnp.int32, (routes.shape[0], count), 1)
    member = jnp.zeros(lane.shape, jnp.float32)
    for slot in range(routes.shape[1]):
        member = jnp.where(lane == routes[:, slot : slot + 1], 1.0, member)
    return member


def middle_kernel(rows, branch, routes, router, gain, bias, middle, extended, sig_out):
    experts = router.shape[1]
    width = rows.shape[1]
    rounded = branch[...].astype(jnp.bfloat16).astype(jnp.float32)
    value = rows[...].astype(jnp.float32) + rounded
    middle[...] = value
    _, _, normed = normalized(value, gain[...], bias[...])
    sig = 1.0 / (1.0 + jnp.exp2(-LOG2E * dot(normed, router[...], 1, 0)))
    sig_out[...] = sig
    extended[:, :width] = value.astype(jnp.bfloat16)
    gates = (sig * named_by(routes[...], experts)).astype(jnp.bfloat16)
    spare = extended.shape[1] - width - experts
    if spare:
        gates = jnp.concatenate([gates, jnp.zeros((gates.shape[0], spare), gates.dtype)], axis=1)
    extended[:, width:] = gates


def enter_ffn(rows, branch, routes, router, gain, bias):
    count, width = rows.shape
    experts = router.shape[1]
    wide = width + experts + -experts % 128
    return pl.pallas_call(
        middle_kernel,
        out_shape=[
            jax.ShapeDtypeStruct((count, width), jnp.float32),
            jax.ShapeDtypeStruct((count, wide), jnp.bfloat16),
            jax.ShapeDtypeStruct((count, experts), jnp.float32),
        ],
        compiler_params=pltpu.CompilerParams(vmem_limit_bytes=40 * 2**20),
        cost_estimate=cost(1e9, 1e7),
        name="middle",
    )(rows, branch, routes, router, gain, bias)


def leave_kernel(
    middle, own, came, cotangent, sigs, routes, router, gain, bias, grad_out, low_out, weight_grads
):
    experts = router.shape[1]
    count, width = middle.shape
    scaled, inverse, normed = normalized(middle[...], gain[...], bias[...])
    total = own[...] + came[...].astype(jnp.float32)
    sig = sigs[...]
    member = named_by(routes[...], experts)
    gate_grads = total[:, width : width + experts]
    logit = (gate_grads * sig * (1.0 - sig) * member).astype(jnp.bfloat16)
    second = dot(logit, router[...], 1, 1)
    inner_grad = second * gain[...]
    inner_grad = inverse * (
        inner_grad
        - jnp.mean(inner_grad, axis=1, keepdims=True)
        - scaled * jnp.mean(inner_grad * scaled, axis=1, keepdims=True)
    )
    grad = cotangent[...].astype(jnp.float32) + total[:, :width] + inner_grad
    grad_out[...] = grad
    low_out[...] = grad.astype(jnp.bfloat16)
    spare = weight_grads.shape[1] - experts
    sums = [
        jnp.sum(second * scaled, axis=0, keepdims=True),
        jnp.sum(second, axis=0, keepdims=True),
        jnp.zeros((126, width), jnp.float32),
    ]
    side = jnp.concatenate(sums, axis=0).T[:, :spare]
    both = jnp.concatenate([dot(normed, logit, 0, 0), side], axis=1)
    weight_grads[...] = both.astype(jnp.bfloat16)


def leave_ffn(middle, own, came, cotangent, sigs, routes, router, gain, bias):
    count, width = middle.shape
    experts = router.shape[1]
    columns = experts + 2 + -(experts + 2) % 128
    return pl.pallas_call(
        leave_kernel,
        out_shape=[
            jax.ShapeDtypeStruct((count, width), jnp.float32),
            jax.ShapeDtypeStruct((count, width), jnp.bfloat16),
            jax.ShapeDtypeStruct((width, columns), jnp.bfloat16),
        ],
        compiler_params=pltpu.CompilerParams(vmem_limit_bytes=48 * 2**20),
        cost_estimate=cost(1e9, 1e7),
        name="leave_ffn",
    )(middle, own, came, cotangent, sigs, routes, router, gain, bias)


def branch_back_kernel(
    grads, w_output, attended, sigs, masks, grad_attended, inner, out_logit, weight_grads, acc
):
    at = pl.program_id(0)
    count = grads.shape[0]
    sig, mask, values = sigs[...], masks[...], attended[...]
    mixed_grad = dot(grads[...], w_output[...], 1, 0)
    lane = lax.broadcasted_iota(jnp.int32, (count, 128), 1)
    logits = jnp.zeros((count, 128), jnp.float32)
    total = jnp.zeros((count, DH), jnp.float32)
    parts = []
    for e in range(VEXP):
        k = VEXP + e
        one, on = sig[:, k : k + 1], mask[:, k : k + 1]
        part = mixed_grad[:, e * DH : (e + 1) * DH]
        total += part * (one * on)
        gate_grad = jnp.sum(part * values, axis=1, keepdims=True)
        logits = jnp.where(lane == k, gate_grad * one * (1.0 - one) * on, logits)
        parts.append((one * on * values).astype(jnp.bfloat16))
    out_logit[...] = logits.astype(jnp.bfloat16)
    rounded = total.astype(jnp.bfloat16)
    grad_attended[...] = rounded
    product = rounded.astype(jnp.float32) * values
    inner[0] = jnp.sum(product.T, axis=0, keepdims=True)
    amount = dot(grads[...], jnp.concatenate(parts, axis=1), 0, 0)

    @pl.when(at == 0)
    def _():
        acc[...] = amount

    @pl.when(at > 0)
    def _():
        acc[...] += amount

    @pl.when(at == pl.num_programs(0) - 1)
    def _():
        weight_grads[...] = acc[...].astype(jnp.bfloat16)


def branch_back(grads, full, attended, sigs, masks):
    rows, width = grads.shape
    values = VEXP * DH

    def by_row(size):
        return pl.BlockSpec((BLOCK, size), lambda i: (i, 0))

    return pl.pallas_call(
        branch_back_kernel,
        grid=(rows // BLOCK,),
        in_specs=[
            by_row(width),
            pl.BlockSpec((width, values), lambda i: (0, 1), pipeline_mode=pl.Buffered(1)),
            by_row(DH),
            by_row(128),
            by_row(16),
        ],
        out_specs=[
            by_row(DH),
            pl.BlockSpec((1, 1, BLOCK), lambda i: (i, 0, 0)),
            by_row(128),
            pl.BlockSpec((width, values), lambda i: (0, 0)),
        ],
        out_shape=[
            jax.ShapeDtypeStruct((rows, DH), jnp.bfloat16),
            jax.ShapeDtypeStruct((rows // BLOCK, 1, BLOCK), jnp.float32),
            jax.ShapeDtypeStruct((rows, 128), jnp.bfloat16),
            jax.ShapeDtypeStruct((width, values), jnp.bfloat16),
        ],
        scratch_shapes=[pltpu.VMEM((width, values), jnp.float32)],
        compiler_params=pltpu.CompilerParams(vmem_limit_bytes=48 * 2**20),
        cost_estimate=cost(4 * rows * width * values, 2e7),
        name="branch_back",
    )(grads, full, attended, sigs, masks)


def turn(value, axis, by):
    size = lax.axis_size(axis)
    return lax.ppermute(value, axis, [(i, (i + by) % size) for i in range(size)])


def normalized(rows, gain, bias):
    values = rows.astype(jnp.float32)
    centred = values - jnp.mean(values, axis=1, keepdims=True)
    inverse = lax.rsqrt(jnp.mean(centred * centred, axis=1, keepdims=True) + 1e-05)
    scaled = centred * inverse
    return scaled, inverse, (scaled * gain + bias).astype(jnp.bfloat16)


def project_kernel(
    levels, rows, w_value, w_query, w_key, routers, gain, bias, order, tables,
    query, key_value, projected, sigs, masks,
):
    count = rows.shape[0]
    piece = count // (levels * HEADS)
    _, _, normed = normalized(rows[...], gain[...], bias[...])
    query[...] = dot(normed, w_query[...], 1, 0).astype(jnp.bfloat16)
    key_value[:, :DH] = dot(normed, w_key[...], 1, 0).astype(jnp.bfloat16)
    sig = 1.0 / (1.0 + jnp.exp2(-LOG2E * dot(normed, routers[...], 1, 0)))
    sigs[...] = sig
    product = dot(rows[...], w_value[...], 1, 0)
    projected[...] = product
    at = lax.broadcasted_iota(jnp.int32, (count, count), 0)
    source = lax.rem(at // piece, levels) * HEADS + at // (piece * levels)
    here = (source * piece + lax.rem(at, piece) == order[0]).astype(jnp.bfloat16)
    lane = lax.broadcasted_iota(jnp.int32, (16, count), 0)
    table = tables[0]
    named = jnp.zeros((16, count), jnp.float32)
    for which in range(2):
        option = lane - which * VEXP
        for slot in range(2):
            pick = table[2 * which + slot : 2 * which + slot + 1, :]
            hit = (option == pick) & (option >= 0) & (option < VEXP)
            named = jnp.where(hit, 1.0, named)
    mask = dot(here, named.astype(jnp.bfloat16), 1, 1)
    masks[...] = mask
    value = jnp.zeros((count, DH), jnp.float32)
    for e in range(VEXP):
        gate = sig[:, e : e + 1] * mask[:, e : e + 1]
        value += gate * product[:, e * DH : (e + 1) * DH]
    key_value[:, DH:] = value.astype(jnp.bfloat16)


def project(rows, full, gain, bias, orders, tables, levels):
    total, width = rows.shape
    count = total // HEADS

    def by_row(columns):
        return pl.BlockSpec((count, columns), lambda i: (i, 0))

    def column(size, at):
        return pl.BlockSpec((width, size), lambda i: (0, at), pipeline_mode=pl.Buffered(1))

    line = pl.BlockSpec((1, width), lambda i: (0, 0))
    shapes = [(DH, jnp.bfloat16), (2 * DH, jnp.bfloat16), (VEXP * DH, jnp.float32)]
    shapes += [(128, jnp.float32), (16, jnp.float32)]
    return pl.pallas_call(
        functools.partial(project_kernel, levels),
        grid=(HEADS,),
        in_specs=[by_row(width), column(VEXP * DH, 0)]
        + [column(DH, 2 * VEXP + i) for i in range(3)]
        + [line, line]
        + [
            pl.BlockSpec((1, 1, count), lambda i: (i, 0, 0)),
            pl.BlockSpec((1,) + tables.shape[1:], lambda i: (i, 0, 0)),
        ],
        out_specs=[by_row(columns) for columns, _ in shapes],
        out_shape=[jax.ShapeDtypeStruct((total, columns), kind) for columns, kind in shapes],
        compiler_params=pltpu.CompilerParams(vmem_limit_bytes=48 * 2**20),
        cost_estimate=cost(2 * total * width * 1024, 2e7),
        name="project",
    )(rows, full, full, full, full, gain, bias, orders, tables)


def project_back_kernel(
    rows, grads, grad_query, out_logit, projected, sigs, masks,
    w_value, w_query, w_key, routers, gain, bias,
    grad_rows, weight_grads, acc, sums,
):
    at = pl.program_id(0)
    count = rows.shape[0]
    values = VEXP * DH

    @pl.when(at == 0)
    def _():
        acc[...] = jnp.zeros_like(acc)
        sums[...] = jnp.zeros_like(sums)

    scaled, inverse, normed = normalized(rows[...], gain[...], bias[...])
    grad_key = grads[:, :DH].astype(jnp.bfloat16)
    grad_value = grads[:, DH:]
    sig, mask = sigs[...], masks[...]
    lane = lax.broadcasted_iota(jnp.int32, (count, 128), 1)
    logits = out_logit[...].astype(jnp.float32)
    parts = []
    for e in range(VEXP):
        one, on = sig[:, e : e + 1], mask[:, e : e + 1]
        parts.append((one * on * grad_value).astype(jnp.bfloat16))
        inner = jnp.sum(grad_value * projected[:, e * DH : (e + 1) * DH], axis=1, keepdims=True)
        logits = jnp.where(lane == e, inner * one * (1.0 - one) * on, logits)
    grad_projected = jnp.concatenate(parts, axis=1)
    sides = jnp.concatenate([grad_query[...], grad_key, logits.astype(jnp.bfloat16)], axis=1)
    first = dot(sides[:, :DH], w_query[...], 1, 1)
    first += dot(sides[:, DH : 2 * DH], w_key[...], 1, 1)
    first += dot(sides[:, 2 * DH :], routers[...], 1, 1)
    sums[2 * VEXP : 2 * VEXP + 1, :] += jnp.sum(first * scaled, axis=0, keepdims=True)
    sums[2 * VEXP + 1 : 2 * VEXP + 2, :] += jnp.sum(first, axis=0, keepdims=True)
    inner_grad = first * gain[...]
    inner_grad = inverse * (
        inner_grad
        - jnp.mean(inner_grad, axis=1, keepdims=True)
        - scaled * jnp.mean(inner_grad * scaled, axis=1, keepdims=True)
    )
    grad_rows[...] = (inner_grad + dot(grad_projected, w_value[...], 1, 1)).astype(jnp.bfloat16)
    acc[:, :values] += dot(rows[...], grad_projected, 0, 0)
    acc[:, values:] += dot(normed, sides, 0, 0)

    @pl.when(at == pl.num_programs(0) - 1)
    def _():
        weight_grads[:, : values + 2 * DH] = acc[:, : values + 2 * DH].astype(jnp.bfloat16)
        last = acc[:, values + 2 * DH :] + sums[...].T
        weight_grads[:, values + 2 * DH :] = last.astype(jnp.bfloat16)


def project_back(rows, grads, grad_query, out_logit, projected, sigs, masks, full, gain, bias):
    total, width = rows.shape
    count = total // HEADS
    columns = VEXP * DH + 3 * DH

    def by_row(size):
        return pl.BlockSpec((count, size), lambda i: (i, 0))

    def column(size, at):
        return pl.BlockSpec((width, size), lambda i: (0, at), pipeline_mode=pl.Buffered(1))

    line = pl.BlockSpec((1, width), lambda i: (0, 0))
    return pl.pallas_call(
        project_back_kernel,
        grid=(HEADS,),
        in_specs=[by_row(width), by_row(2 * DH), by_row(DH), by_row(128), by_row(VEXP * DH)]
        + [by_row(128), by_row(16), column(VEXP * DH, 0)]
        + [column(DH, 2 * VEXP + i) for i in range(3)]
        + [line, line],
        out_specs=[by_row(width), pl.BlockSpec((width, columns), lambda i: (0, 0))],
        out_shape=[
            jax.ShapeDtypeStruct((total, width), jnp.bfloat16),
            jax.ShapeDtypeStruct((width, columns), jnp.bfloat16),
        ],
        scratch_shapes=[
            pltpu.VMEM((width, columns), jnp.float32),
            pltpu.VMEM((128, width), jnp.float32),
        ],
        compiler_params=pltpu.CompilerParams(vmem_limit_bytes=56 * 2**20),
        cost_estimate=cost(4 * total * width * 1024, 4e7),
        name="project_back",
    )(rows, grads, grad_query, out_logit, projected, sigs, masks, full, full, full, full, gain, bias)


def shift(value, axis, by):
    count = lax.axis_size(axis)
    pairs = [(i, i + by) for i in range(count) if 0 <= i + by < count]
    return lax.ppermute(value, axis, pairs)


def body(
    tokens_in,
    out_grad,
    deal_order,
    seq_lengths,
    value_routes,
    output_routes,
    ffn_routes,
    norm1_gain,
    norm1_bias,
    norm2_gain,
    norm2_bias,
    query_weight,
    key_weight,
    value_weight,
    output_weight,
    value_router,
    output_router,
    ffn_router,
    ffn_in,
    ffn_out,
):
    groups = lax.axis_size("group")
    levels = lax.axis_size("level")
    level = lax.axis_index("level")
    head = lax.axis_index("head")
    count, width = tokens_in.shape
    piece = count // (levels * HEADS)
    wrows = query_weight.shape[0]
    experts = ffn_router.shape[1]
    local_experts = ffn_in.shape[1] // FH

    small = jnp.concatenate(
        [
            ffn_router,
            norm1_gain[:, None],
            norm1_bias[:, None],
            norm2_gain[:, None],
            norm2_bias[:, None],
        ],
        axis=1,
    )
    shared = small.shape[1]
    pad = -(shared + 2 * VEXP) % 128
    extra = jnp.concatenate(
        [
            value_router.reshape(wrows, HEADS, VEXP),
            output_router.reshape(wrows, HEADS, VEXP),
            jnp.broadcast_to(small[:, None, :], (wrows, HEADS, shared)),
            jnp.zeros((wrows, HEADS, pad), jnp.bfloat16),
        ],
        axis=2,
    )
    cols = 2 * DH + 2 * VEXP * DH + extra.shape[2]
    tables = jnp.concatenate(
        [value_routes.transpose(1, 2, 0), output_routes.transpose(1, 2, 0)], axis=1
    )
    picks = ffn_routes.reshape(levels, HEADS * piece, -1).transpose(0, 2, 1)
    arrived, own_grads, full, tables, picks, orders = start(
        tokens_in.reshape(levels, HEADS, piece, width),
        out_grad.reshape(levels, HEADS, piece, width),
        [value_weight, output_weight, query_weight, key_weight],
        extra.transpose(1, 0, 2),
        tables,
        picks,
        deal_order,
    )
    worker_in = arrived.reshape(HEADS * count, width)
    own_tokens = lax.dynamic_index_in_dim(arrived, head, 1, keepdims=False).reshape(count, width)
    in_rows = [turn(ffn_in, "group", k) for k in range(1, groups)]
    full, in_rows = lax.optimization_barrier((full.reshape(width, cols), in_rows))

    base = 2 * DH + 2 * VEXP * DH
    w_output = full[:, VEXP * DH : 2 * VEXP * DH]
    at = base + 2 * VEXP
    def relabelled(expert):
        share = expert // local_experts
        return (share % HEADS * levels + share // HEADS) * local_experts + expert % local_experts

    labels = jnp.arange(experts, dtype=jnp.int32)
    moved = low(relabelled(labels)[:, None] == labels[None, :])
    r_ffn = low(
        jnp.dot(full[:, at : at + experts], moved, preferred_element_type=jnp.float32)
    )
    gain_one, bias_one, gain_two, bias_two = (
        full[:, at + experts + i].astype(jnp.float32) for i in range(4)
    )
    gain_row, bias_row = gain_one[None], bias_one[None]
    orders = orders.reshape(levels, HEADS, count)
    own_order = lax.dynamic_index_in_dim(orders, level, 0, keepdims=False)[:, None, :]
    queries, key_value, projected, sigs, masks = project(
        worker_in, full, gain_row, bias_row, own_order, tables, levels
    )

    rows = HEADS * count
    reach = -(-LMAX // rows)

    ramp = jnp.arange(count, dtype=jnp.int32)

    def arrival(values):
        lead, shape = values.shape[:-3], values.shape[-1:]
        four = values.reshape(lead + (HEADS, levels, HEADS, piece) + shape)
        return jnp.swapaxes(four, -4, -3).reshape(lead + (rows,) + shape)

    orders = jnp.concatenate([jnp.zeros((reach, HEADS, count), jnp.int32), orders], axis=0)
    orders = lax.dynamic_slice_in_dim(orders, level, reach + 1, 0)
    here = orders[:, :, None, :] == ramp[None, None, :, None]
    inverse = jnp.sum(here * ramp, axis=3)
    shard = (level - reach + jnp.arange(reach + 1, dtype=jnp.int32))[:, None] * HEADS
    shard = shard + jnp.arange(HEADS, dtype=jnp.int32)[None, :]
    pos_all = jnp.where(shard[:, :, None] < 0, -1, shard[:, :, None] * count + inverse)
    pos_all = arrival(pos_all[..., None]).reshape(-1)
    positions = pos_all[reach * rows :]
    seq_ends = jnp.cumsum(seq_lengths[0])

    def starts_of(places):
        return jnp.max(jnp.where(seq_ends <= places[:, None], seq_ends, 0), axis=1)

    starts = starts_of(positions)
    blocks = rows // BLOCK
    base_block = (level - reach) * blocks
    first_block = starts_of(level * rows + jnp.arange(blocks, dtype=jnp.int32) * BLOCK) // BLOCK
    first_block = jnp.maximum(first_block - base_block, 0)

    own_routes = picks.reshape(levels, -1, HEADS, piece).transpose(2, 0, 3, 1).reshape(count, -1)
    own_routes = relabelled(own_routes)
    ffn_side = (own_routes, r_ffn, gain_two[None], bias_two[None], own_tokens)

    window = [key_value]
    own_grads = own_grads.reshape(count, width)
    for i in range(reach):
        came = shift(window[0], "level", 1)
        if i == 0:
            came, own_grads, pos_all, starts, ffn_out, in_rows = lax.optimization_barrier(
                (came, own_grads, pos_all, starts, ffn_out, [ffn_in] + in_rows)
            )
            cotangent = level_gather(own_grads, 5, True)
        if i == reach - 1:
            came, cotangent, ffn_side = lax.optimization_barrier((came, cotangent, ffn_side))
        window.insert(0, came)
    place = jnp.stack([head, lax.axis_index("group")])
    out_here = lax.all_gather(ffn_out, "level", axis=0)
    w_in = [lax.all_gather(part, "level", axis=0) for part in in_rows]


    def lines(values):
        return values.reshape(blocks, 1, BLOCK)

    attended, log_total = attend(
        first_block,
        queries,
        window,
        lines(positions),
        lines(starts),
        pos_all[:, None],
    )

    out_sig = sigs[:, VEXP : 2 * VEXP]
    out_mask = masks[:, VEXP : 2 * VEXP]
    out_gate = out_sig * out_mask
    mixed = low((out_gate[..., None] * attended[:, None, :]).reshape(rows, VEXP * DH))
    branch = level_scatter(low(transposed(mixed, w_output)), 2)
    branch, out_here = lax.optimization_barrier((branch, out_here))
    w_out = [out_here] + [turn(out_here, "group", k) for k in range(1, groups)]

    own_routes, r_ffn, gain_two, bias_two, own_tokens = ffn_side
    middle, extended, ffn_sig = enter_ffn(own_tokens, branch, own_routes, r_ffn, gain_two, bias_two)
    hidden = level_gather(extended, 3, True)
    mine = levels * local_experts
    gates = lax.dynamic_slice_in_dim(hidden, width + head * mine, mine, 1).astype(jnp.float32)
    active, grad_pre, grad_rows = ffn_front(
        place, hidden, cotangent, w_in, w_out, gates, local_experts
    )
    summed, beyond = pair_scatter(grad_rows, 4, True)
    came = to_far(beyond)
    grad_in = ffn_rear(place, hidden, grad_pre, width, groups, levels)
    in_came = [turn(grad_in[k], "group", k) for k in range(1, groups)]
    grad_out = ffn_rear(place, cotangent, active, width, groups, levels)
    out_came = [turn(grad_out[k], "group", k) for k in range(1, groups)]
    came, grad_in, grad_out = lax.optimization_barrier((came, grad_in, grad_out))
    grad_middle, own_branch, early = leave_ffn(
        middle, summed, came, own_grads, ffn_sig, own_routes, r_ffn, gain_two, bias_two
    )
    came = to_far(own_branch)
    feed = ffn_feed(place, active, w_out)
    came, feed = lax.optimization_barrier((came, feed))
    grad_branch = pair_gather(own_branch, came, 7)

    def sum_of(own, others):
        total = own[0].astype(jnp.float32)
        for other in others:
            total = total + other.astype(jnp.float32)
        return low(total)

    def over_levels(total):
        return lax.psum_scatter(total, "level", scatter_dimension=0)

    grad_branch, in_total = lax.optimization_barrier((grad_branch, sum_of(grad_in, in_came)))
    ffn_in_grad = over_levels(in_total)
    grad_attended, row_inner, grad_out_logit, grad_w_output = branch_back(
        grad_branch, full, attended, sigs, masks
    )
    grad_queries, *grad_window = attend_back(
        first_block,
        queries,
        window,
        grad_attended,
        lines(positions),
        lines(starts),
        log_total,
        row_inner,
        pos_all[:, None],
    )
    came = shift(grad_window[0], "level", -1)
    fed, beyond = pair_scatter(feed, 6, True)
    for i in range(1, reach + 1):
        if i < reach:
            came, fed = lax.optimization_barrier((came, fed))
        grad_both = grad_window[i].astype(jnp.float32) + came.astype(jnp.float32)
        if i < reach:
            grad_keys_sent = low(grad_both)
            came = shift(grad_keys_sent, "level", -1)
    grad_both, out_came = lax.optimization_barrier((grad_both, out_came))
    ffn_out_grad = over_levels(sum_of(grad_out, out_came))
    fed_far = to_far(beyond)
    grad_inputs, late = project_back(
        worker_in,
        grad_both,
        grad_queries,
        grad_out_logit,
        projected,
        sigs,
        masks,
        full,
        gain_row,
        bias_row,
    )

    fed_far, grad_inputs = lax.optimization_barrier((fed_far, grad_inputs))
    layer_out = to_home(low(middle + fed + fed_far.astype(jnp.float32)))

    values = VEXP * DH
    layout = (
        ((0, values, True), (values, DH, True), (values + DH, DH, True), (values + 2 * DH, DH, False)),
        ((0, values, True),),
        ((0, early.shape[1], False),),
    )

    def by_owner(grads):
        return grads.reshape(groups, levels, HEADS, wrows, -1)

    input_grad, grad_value, grad_query, grad_key, sides, grad_output, common = finish(
        layout,
        grad_inputs.reshape(HEADS, HEADS, levels * piece, width),
        grad_middle.reshape(HEADS, levels * piece, width),
        by_owner(late),
        by_owner(grad_w_output),
        by_owner(early),
    )
    norms = jnp.sum(sides[:, :, 2 * VEXP : 2 * VEXP + 2], axis=0)
    common = jnp.sum(common[:, :, : experts + 2], axis=0)
    router_grad = common[:, :experts].reshape(wrows, HEADS, levels, local_experts)

    def side(first):
        return sides[:, :, first : first + VEXP].transpose(1, 0, 2).reshape(wrows, HEADS * VEXP)

    return (
        layer_out,
        input_grad.reshape(count, width),
        norms[:, 0],
        norms[:, 1],
        common[:, experts],
        common[:, experts + 1],
        grad_query,
        grad_key,
        grad_value,
        grad_output,
        side(0),
        side(VEXP),
        jnp.swapaxes(router_grad, 1, 2).reshape(wrows, experts),
        ffn_in_grad.astype(jnp.float32),
        ffn_out_grad.astype(jnp.float32),
    )


def solution(mesh):
    groups, shards = mesh.devices.shape
    fine = Mesh(mesh.devices.reshape(groups, shards // HEADS, HEADS), TOK)
    two, one, three = P(TOK, None), P(TOK), P(TOK, None, None)
    ffn = P("group", ("level", "head"))
    return jax.shard_map(
        body,
        mesh=fine,
        in_specs=(two, two, two, P("group", None), three, three, two, one, one, one, one)
        + (two,) * 7
        + (ffn, ffn),
        out_specs=(two, two, one, one, one, one) + (two,) * 7 + (ffn, ffn),
        check_vma=False,
    )
```

```python
import functools

import jax
import jax.numpy as jnp
from jax import lax
from jax.experimental import pallas as pl
from jax.experimental.pallas import tpu as pltpu
from jax.sharding import Mesh, PartitionSpec as P

HEADS = 4
DH = 128
VEXP = 5
FH = 128
LMAX = 4096

TOK = ("group", "level", "head")


def transposed(left_side, right_side):
    return lax.dot_general(
        left_side, right_side, (((1,), (1,)), ((), ())), preferred_element_type=jnp.float32
    )


def low(value):
    return value.astype(jnp.bfloat16)


def to_home(rows):
    levels = lax.axis_size("level")
    count = rows.shape[0]
    out = rows.reshape(HEADS, levels, count // levels // HEADS, -1).transpose(1, 0, 2, 3)
    back = lax.all_to_all(
        out.reshape(levels, count // levels, -1), "level", split_axis=0, concat_axis=0, tiled=True
    )
    return back.reshape(count, -1)


MESH = pl.DeviceIdType.MESH


def partners(head):
    near = head + 1 - 2 * lax.rem(head, 2)
    far = lax.rem(head + 2, HEADS)
    return near, far


def greet(near, far):
    barrier = pltpu.get_barrier_semaphore()
    for peer in (near, far):
        pl.semaphore_signal(barrier, inc=1, device_id={"head": peer}, device_id_type=MESH)
    pl.semaphore_wait(barrier, 2)


def remote(src, dst, send, recv, peer):
    return pltpu.make_async_remote_copy(
        src_ref=src,
        dst_ref=dst,
        send_sem=send,
        recv_sem=recv,
        device_id={"head": peer},
        device_id_type=MESH,
    )


def cost(flops, moved):
    return pl.CostEstimate(flops=int(flops), bytes_accessed=int(moved), transcendentals=0)


def gather_kernel(
    by_source, own, out, local_sem, near_send, near_recv, far_send, far_recv, pass_send, pass_recv
):
    head = lax.axis_index("head")
    near, far = partners(head)
    greet(near, far)

    def spot(i, source):
        return out.at[source, i] if by_source else out.at[i, source]

    pieces = range(HEADS)
    to_far = [remote(own.at[i], spot(i, head), far_send.at[i], far_recv.at[i], far) for i in pieces]
    to_near = [
        remote(own.at[i], spot(i, head), near_send.at[i], near_recv.at[i], near) for i in pieces
    ]
    passed = [
        remote(spot(i, far), spot(i, far), pass_send.at[i], pass_recv.at[i], near) for i in pieces
    ]
    kept = [pltpu.make_async_copy(own.at[i], spot(i, head), local_sem.at[i]) for i in pieces]
    for copy in to_far + to_near + kept:
        copy.start()
    for i in pieces:
        to_far[i].wait_recv()
        passed[i].start()
    for i in pieces:
        to_near[i].wait_recv()
        passed[i].wait_recv()
        kept[i].wait()
        to_far[i].wait_send()
        to_near[i].wait_send()
        passed[i].wait_send()


def level_gather(rows, collective_id, by_source=False):
    count, width = rows.shape
    whole = pl.pallas_call(
        functools.partial(gather_kernel, by_source),
        out_shape=jax.ShapeDtypeStruct((HEADS, HEADS, count // HEADS, width), rows.dtype),
        in_specs=[pl.BlockSpec(memory_space=pltpu.VMEM)],
        out_specs=pl.BlockSpec(memory_space=pl.ANY),
        scratch_shapes=[pltpu.SemaphoreType.DMA((HEADS,))] * 7,
        compiler_params=pltpu.CompilerParams(collective_id=collective_id, has_side_effects=True),
        cost_estimate=cost(0, 90e6),
        name="level_gather",
    )(rows.reshape(HEADS, count // HEADS, width))
    return whole.reshape(HEADS * count, width)


def scatter_kernel(
    by_source, part, out, near_buf, send_buf, far_buf, near_send, near_recv, far_send, far_recv
):
    head = lax.axis_index("head")
    near, far = partners(head)
    greet(near, far)
    across = HEADS - 1 - head
    pieces = range(HEADS)

    def spot(i, dest):
        return (dest, i) if by_source else (i, dest)

    def to_near(slot, i, dest):
        return remote(
            part.at[spot(i, dest)],
            near_buf.at[slot, i],
            near_send.at[slot, i],
            near_recv.at[slot, i],
            near,
        )

    first = [to_near(0, i, across) for i in pieces]
    second = [to_near(1, i, near) for i in pieces]
    onward = [
        remote(send_buf.at[i], far_buf.at[i], far_send.at[i], far_recv.at[i], far) for i in pieces
    ]
    for copy in first + second:
        copy.start()
    for i in pieces:
        first[i].wait_recv()
        both = part[spot(i, far)].astype(jnp.float32) + near_buf[0, i].astype(jnp.float32)
        send_buf[i] = both.astype(jnp.bfloat16)
        onward[i].start()
    for i in pieces:
        second[i].wait_recv()
        out[i] = part[spot(i, head)].astype(jnp.float32) + near_buf[1, i].astype(jnp.float32)
    for i in pieces:
        onward[i].wait_recv()
        out[i] = out[i] + far_buf[i].astype(jnp.float32)
    for i in pieces:
        first[i].wait_send()
        second[i].wait_send()
        onward[i].wait_send()


def level_scatter(rows, collective_id, by_source=False):
    total, width = rows.shape
    piece = total // (HEADS * HEADS)
    low_type = jnp.bfloat16
    mine = pl.pallas_call(
        functools.partial(scatter_kernel, by_source),
        out_shape=jax.ShapeDtypeStruct((HEADS, piece, width), jnp.float32),
        in_specs=[pl.BlockSpec(memory_space=pltpu.VMEM)],
        out_specs=pl.BlockSpec(memory_space=pltpu.VMEM),
        scratch_shapes=[
            pltpu.VMEM((2, HEADS, piece, width), low_type),
            pltpu.VMEM((HEADS, piece, width), low_type),
            pltpu.VMEM((HEADS, piece, width), low_type),
            pltpu.SemaphoreType.DMA((2, HEADS)),
            pltpu.SemaphoreType.DMA((2, HEADS)),
            pltpu.SemaphoreType.DMA((HEADS,)),
            pltpu.SemaphoreType.DMA((HEADS,)),
        ],
        compiler_params=pltpu.CompilerParams(
            collective_id=collective_id, has_side_effects=True, vmem_limit_bytes=32 * 2**20
        ),
        cost_estimate=cost(0, 80e6),
        name="level_scatter",
    )(rows.reshape(HEADS, HEADS, piece, width))
    return mine.reshape(HEADS * piece, width)


def meet(near):
    barrier = pltpu.get_barrier_semaphore()
    pl.semaphore_signal(barrier, inc=1, device_id={"head": near}, device_id_type=MESH)
    pl.semaphore_wait(barrier, 1)


def pair_scatter_kernel(by_source, part, out, out_far, near_buf, send, recv):
    head = lax.axis_index("head")
    near, far = partners(head)
    meet(near)
    across = HEADS - 1 - head
    pieces = range(HEADS)

    def spot(i, dest):
        return (dest, i) if by_source else (i, dest)

    def to_near(slot, i, dest):
        return remote(
            part.at[spot(i, dest)], near_buf.at[slot, i], send.at[slot, i], recv.at[slot, i], near
        )

    first = [to_near(0, i, across) for i in pieces]
    second = [to_near(1, i, near) for i in pieces]
    for copy in first + second:
        copy.start()
    for i in pieces:
        first[i].wait_recv()
        both = part[spot(i, far)].astype(jnp.float32) + near_buf[0, i].astype(jnp.float32)
        out_far[i] = both.astype(jnp.bfloat16)
    for i in pieces:
        second[i].wait_recv()
        out[i] = part[spot(i, head)].astype(jnp.float32) + near_buf[1, i].astype(jnp.float32)
    for i in pieces:
        first[i].wait_send()
        second[i].wait_send()


def pair_scatter(rows, collective_id, by_source=False):
    total, width = rows.shape
    piece = total // (HEADS * HEADS)
    mine, other = pl.pallas_call(
        functools.partial(pair_scatter_kernel, by_source),
        out_shape=[
            jax.ShapeDtypeStruct((HEADS, piece, width), jnp.float32),
            jax.ShapeDtypeStruct((HEADS, piece, width), jnp.bfloat16),
        ],
        in_specs=[pl.BlockSpec(memory_space=pltpu.VMEM)],
        out_specs=[pl.BlockSpec(memory_space=pltpu.VMEM)] * 2,
        scratch_shapes=[
            pltpu.VMEM((2, HEADS, piece, width), jnp.bfloat16),
            pltpu.SemaphoreType.DMA((2, HEADS)),
            pltpu.SemaphoreType.DMA((2, HEADS)),
        ],
        compiler_params=pltpu.CompilerParams(
            collective_id=collective_id, has_side_effects=True, vmem_limit_bytes=32 * 2**20
        ),
        cost_estimate=cost(0, 25e6),
        name="pair_scatter",
    )(rows.reshape(HEADS, HEADS, piece, width))
    return mine.reshape(HEADS * piece, width), other.reshape(HEADS * piece, width)


def pair_gather_kernel(by_source, own, other, out, local_sem, send, recv):
    head = lax.axis_index("head")
    near, far = partners(head)
    meet(near)
    copies, kept = [], []
    for i in range(HEADS):
        for slot, (block, source) in enumerate(((own, head), (other, far))):
            place = out.at[source, i] if by_source else out.at[i, source]
            copies.append(
                remote(block.at[i], place, send.at[slot, i], recv.at[slot, i], near)
            )
            kept.append(pltpu.make_async_copy(block.at[i], place, local_sem.at[slot, i]))
    for copy in copies + kept:
        copy.start()
    for copy in copies + kept:
        copy.wait()


def pair_gather(own, other, collective_id, by_source=False):
    count, width = own.shape
    split = (HEADS, count // HEADS, width)
    whole = pl.pallas_call(
        functools.partial(pair_gather_kernel, by_source),
        out_shape=jax.ShapeDtypeStruct((HEADS,) + split, own.dtype),
        in_specs=[pl.BlockSpec(memory_space=pltpu.VMEM)] * 2,
        out_specs=pl.BlockSpec(memory_space=pl.ANY),
        scratch_shapes=[pltpu.SemaphoreType.DMA((2, HEADS))] * 3,
        compiler_params=pltpu.CompilerParams(collective_id=collective_id, has_side_effects=True),
        cost_estimate=cost(0, 25e6),
        name="pair_gather",
    )(own.reshape(split), other.reshape(split))
    return whole.reshape(HEADS * count, width)


def to_far(rows):
    return lax.ppermute(rows, "head", [(i, (i + 2) % HEADS) for i in range(HEADS)])


def ring(axis):
    me, size = lax.axis_index(axis), lax.axis_size(axis)
    ahead = [lax.rem(me + k, size) for k in range(1, size)]
    behind = [lax.rem(me + size - k, size) for k in range(1, size)]
    return me, ahead, behind


def reach_out(src, dst, send, recv, peer):
    return pltpu.make_async_remote_copy(
        src_ref=src, dst_ref=dst, send_sem=send, recv_sem=recv, device_id=peer, device_id_type=MESH
    )


def greet_all(peers):
    barrier = pltpu.get_barrier_semaphore()
    for peer in peers:
        pl.semaphore_signal(barrier, inc=1, device_id=peer, device_id_type=MESH)
    pl.semaphore_wait(barrier, len(peers))


def start_kernel(
    tokens, cotangents, value, output, query, key, extra, tables, picks, order,
    rows, grads, full, routes, chosen_rows, orders, weights, own_sem, *sems
):
    sems = iter(sems)

    def pair():
        return next(sems), next(sems)

    group, groups_ahead, _ = ring("group")
    level, levels_ahead, levels_behind = ring("level")
    head = lax.axis_index("head")
    near, far = partners(head)
    mates = [near, far, HEADS - 1 - head]
    for to in range(HEADS):
        at = 0
        for part in (value, output, query, key):
            size = part.shape[1] // HEADS
            weights[to, :, at : at + size] = part[:, to * size : (to + 1) * size]
            at += size
        weights[to, :, at:] = extra[to]
    greet_all(
        [{"head": m} for m in mates]
        + [{"level": n} for n in levels_ahead]
        + [{"group": n} for n in groups_ahead]
    )
    started = []

    def send(src, dst, send_sem, recv_sem, peer):
        copy = reach_out(src, dst, send_sem, recv_sem, peer)
        copy.start()
        started.append(copy)
        return copy

    out_s, out_r = pair()
    pick_s, pick_r = pair()
    crossing, picking = [], []
    for k, to in enumerate(levels_ahead):
        peer = {"level": to}
        crossing.append(send(tokens.at[to], rows.at[:, head, level], out_s.at[k], out_r.at[k], peer))
    mate_s, mate_r = pair()
    table_s, table_r = pair()
    order_s, order_r = pair()
    to_mates, order_mates, table_mates = [], [], []
    for k, to in enumerate(mates):
        peer = {"head": to}
        to_mates.append(
            send(weights.at[to], full.at[group, level, head], mate_s.at[k], mate_r.at[k], peer)
        )
        order_mates.append(
            send(order, orders.at[level, head], order_s.at[k], order_r.at[k], peer)
        )
    own = [
        (tokens.at[level], rows.at[:, head, level]),
        (weights.at[head], full.at[group, level, head]),
        (tables.at[head], routes.at[head]),
        (picks.at[level], chosen_rows.at[level]),
        (order, orders.at[level, head]),
        (cotangents.at[level], grads.at[:, level]),
    ]
    own = [pltpu.make_async_copy(src, dst, own_sem.at[i]) for i, (src, dst) in enumerate(own)]
    for copy in own:
        copy.start()
    far_s, far_r = pair()
    near_s, near_r = pair()
    pass_s, pass_r = pair()
    to_far, to_near = [], []

    def share(k, src, source):
        place = rows.at[:, head, source]
        to_far.append(send(src, place, far_s.at[k], far_r.at[k], {"head": far}))
        to_near.append(send(src, place, near_s.at[k], near_r.at[k], {"head": near}))

    share(0, tokens.at[level], level)
    block_s, block_r = pair()
    group_s, group_r = pair()
    orders_s, orders_r = pair()
    for copy in to_mates:
        copy.wait_recv()
    own[1].wait()
    blocks, grouped, ordered = [], [], []

    def to_groups(j, source):
        for k, to in enumerate(groups_ahead):
            block = full.at[group, source]
            grouped.append(
                send(block, block, group_s.at[k, j], group_r.at[k, j], {"group": to})
            )

    for k, to in enumerate(levels_ahead):
        block = full.at[group, level]
        blocks.append(send(block, block, block_s.at[k], block_r.at[k], {"level": to}))
    to_groups(0, level)
    for k, to in enumerate(mates):
        table_mates.append(
            send(tables.at[to], routes.at[head], table_s.at[k], table_r.at[k], {"head": to})
        )
    for k, to in enumerate(levels_ahead):
        picking.append(
            send(picks.at[to], chosen_rows.at[level], pick_s.at[k], pick_r.at[k], {"level": to})
        )
    for copy in order_mates:
        copy.wait_recv()
    own[4].wait()
    for k, to in enumerate(levels_ahead):
        block = orders.at[level]
        ordered.append(send(block, block, orders_s.at[k], orders_r.at[k], {"level": to}))
    for k, source in enumerate(levels_behind):
        crossing[k].wait_recv()
        share(k + 1, rows.at[:, head, source], source)
    grad_s, grad_r = pair()
    crossed = []
    for k, to in enumerate(levels_ahead):
        crossed.append(
            send(cotangents.at[to], grads.at[:, level], grad_s.at[k], grad_r.at[k], {"level": to})
        )
    for k, source in enumerate(levels_behind):
        blocks[k].wait_recv()
        to_groups(k + 1, source)
    passed = []
    for k, source in enumerate([level] + levels_behind):
        to_far[k].wait_recv()
        place = rows.at[:, far, source]
        passed.append(send(place, place, pass_s.at[k], pass_r.at[k], {"head": near}))
    for copy in to_near + passed + grouped + table_mates + picking + ordered + crossed:
        copy.wait_recv()
    for copy in started:
        copy.wait_send()
    for i in (0, 2, 3, 5):
        own[i].wait()


def start(tokens, cotangents, weights, extra, tables, picks, order):
    groups, levels = lax.axis_size("group"), lax.axis_size("level")
    _, _, piece, width = tokens.shape
    columns = sum(part.shape[1] for part in weights) // HEADS + extra.shape[2]
    block = extra.shape[:2] + (columns,)
    shapes = [
        jax.ShapeDtypeStruct((HEADS, HEADS, levels, piece, width), tokens.dtype),
        jax.ShapeDtypeStruct((HEADS, levels, piece, width), tokens.dtype),
        jax.ShapeDtypeStruct((groups, levels) + block, extra.dtype),
        jax.ShapeDtypeStruct(tables.shape, tables.dtype),
        jax.ShapeDtypeStruct(picks.shape, picks.dtype),
        jax.ShapeDtypeStruct((levels, HEADS) + order.shape, order.dtype),
    ]
    dma = pltpu.SemaphoreType.DMA
    others, mates = (levels - 1,), (HEADS - 1,)
    counts = [others] * 2 + [mates] * 3 + [(levels,)] * 3
    counts += [others, (groups - 1, levels), others, others]
    return pl.pallas_call(
        start_kernel,
        out_shape=shapes,
        in_specs=[pl.BlockSpec(memory_space=pltpu.VMEM)] * 10,
        out_specs=[pl.BlockSpec(memory_space=pl.ANY)] * 6,
        scratch_shapes=[pltpu.VMEM(block, extra.dtype), dma((6,))] + [dma(c) for c in counts for _ in range(2)],
        compiler_params=pltpu.CompilerParams(collective_id=9, has_side_effects=True),
        cost_estimate=cost(0, 200e6),
        name="start",
    )(tokens, cotangents, *weights, extra, tables, picks, order)


def finish_kernel(layout, *refs):
    refs = iter(refs)
    count = len(layout)

    def take(n):
        return [next(refs) for _ in range(n)]

    part, middle = take(2)
    grads = take(count)
    (home_grad,) = take(1)
    results = [take(len(pieces)) for pieces in layout]
    near_buf, send_buf, far_buf, total, back_buf, came_buf = take(6)
    group_buf, level_send, level_buf, head_send, owned = (take(count) for _ in range(5))

    def pair():
        return next(refs), next(refs)

    group, groups_ahead, _ = ring("group")
    level, levels_ahead, levels_behind = ring("level")
    head = lax.axis_index("head")
    near, far = partners(head)
    across = HEADS - 1 - head
    mates = [near, far, across]
    greet_all(
        [{"head": m} for m in mates]
        + [{"level": n} for n in levels_ahead]
        + [{"group": n} for n in groups_ahead]
    )
    started = []

    def send(src, dst, send_sem, recv_sem, peer):
        copy = reach_out(src, dst, send_sem, recv_sem, peer)
        copy.start()
        started.append(copy)
        return copy

    pieces = range(HEADS)
    sets = range(count)
    near_s, near_r = pair()
    far_s, far_r = pair()
    back_s, back_r = pair()
    group_s, group_r = pair()
    level_s, level_r = pair()
    mate_s, mate_r = pair()
    first, second, onward = [], [], []
    for slot, (dest, copies) in enumerate(((across, first), (near, second))):
        for i in pieces:
            copies.append(
                send(
                    part.at[i, dest],
                    near_buf.at[slot, i],
                    near_s.at[slot, i],
                    near_r.at[slot, i],
                    {"head": near},
                )
            )
    order = levels_ahead + [level]
    grouped = {}
    for j, dest in enumerate(order):
        for p in sets:
            grouped[j, p] = [
                send(
                    grads[p].at[to, dest],
                    group_buf[p].at[k, j],
                    group_s.at[p, k, j],
                    group_r.at[p, k, j],
                    {"group": to},
                )
                for k, to in enumerate(groups_ahead)
            ]
    for i in pieces:
        first[i].wait_recv()
        both = part[i, far].astype(jnp.float32) + near_buf[0, i].astype(jnp.float32)
        send_buf[i] = both.astype(jnp.bfloat16)
        onward.append(send(send_buf.at[i], far_buf.at[i], far_s.at[i], far_r.at[i], {"head": far}))
    for i in pieces:
        second[i].wait_recv()
        both = part[i, head].astype(jnp.float32) + near_buf[1, i].astype(jnp.float32)
        total[i] = both + middle[i]
    leveled = {}
    for j, dest in enumerate(order):
        for p in sets:
            amount = grads[p][group, dest].astype(jnp.float32)
            for k, copy in enumerate(grouped[j, p]):
                copy.wait_recv()
                amount = amount + group_buf[p][k, j].astype(jnp.float32)
            level_send[p][j] = amount.astype(jnp.bfloat16)
            if j < len(levels_ahead):
                leveled[j, p] = send(
                    level_send[p].at[j],
                    level_buf[p].at[j],
                    level_s.at[p, j],
                    level_r.at[p, j],
                    {"level": dest},
                )
    for i in pieces:
        onward[i].wait_recv()
        both = total[i] + far_buf[i].astype(jnp.float32)
        back_buf[i] = both.astype(jnp.bfloat16).reshape(back_buf.shape[1:])
    backs = [
        send(back_buf.at[:, to], came_buf.at[level], back_s.at[k], back_r.at[k], {"level": to})
        for k, to in enumerate(levels_ahead)
    ]
    sharing = []
    for p in sets:
        amount = level_send[p][len(levels_ahead)].astype(jnp.float32)
        for j in range(len(levels_ahead)):
            leveled[j, p].wait_recv()
            amount = amount + level_buf[p][j].astype(jnp.float32)
        head_send[p][...] = amount.astype(jnp.bfloat16)
        sharing += [
            send(
                head_send[p].at[to],
                owned[p].at[head],
                mate_s.at[p, k],
                mate_r.at[p, k],
                {"head": to},
            )
            for k, to in enumerate(mates)
        ]
        owned[p][head] = head_send[p][head]
    home_grad[level] = back_buf[:, level].astype(jnp.float32)
    for k, source in enumerate(levels_behind):
        backs[k].wait_recv()
        home_grad[source] = came_buf[source].astype(jnp.float32)
    for copy in sharing:
        copy.wait_recv()
    for p in sets:
        for out, (first_column, size, joined) in zip(results[p], layout[p]):
            for h in range(HEADS):
                value = owned[p][h, :, first_column : first_column + size].astype(jnp.float32)
                if joined:
                    out[:, h * size : (h + 1) * size] = value
                else:
                    out[h] = value
    for copy in started:
        copy.wait_send()


def finish(layout, part, middle, *grads):
    groups, levels = lax.axis_size("group"), lax.axis_size("level")
    _, count, width = middle.shape
    piece = count // levels
    low_type = jnp.bfloat16
    blocks = [grad.shape[2:] for grad in grads]
    sets = len(grads)
    dma = pltpu.SemaphoreType.DMA
    counts = [(2, HEADS), (HEADS,), (levels - 1,)]
    counts += [(sets, groups - 1, levels), (sets, levels - 1), (sets, HEADS - 1)]
    vmem = pl.BlockSpec(memory_space=pltpu.VMEM)
    shapes = []
    for pieces in layout:
        for _, size, joined in pieces:
            shape = (blocks[0][1], HEADS * size) if joined else (HEADS, blocks[0][1], size)
            shapes.append(jax.ShapeDtypeStruct(shape, jnp.float32))
    return pl.pallas_call(
        functools.partial(finish_kernel, layout),
        out_shape=[jax.ShapeDtypeStruct((levels, HEADS, piece, width), jnp.float32)] + shapes,
        in_specs=[vmem] * (2 + sets),
        out_specs=[vmem] * (1 + len(shapes)),
        scratch_shapes=[
            pltpu.VMEM((2, HEADS, count, width), low_type),
            pltpu.VMEM((HEADS, count, width), low_type),
            pltpu.VMEM((HEADS, count, width), low_type),
            pltpu.VMEM((HEADS, count, width), jnp.float32),
            pltpu.VMEM((HEADS, levels, piece, width), low_type),
            pltpu.VMEM((levels, HEADS, piece, width), low_type),
        ]
        + [pltpu.VMEM((groups - 1, levels) + block, low_type) for block in blocks]
        + [pltpu.VMEM((levels,) + block, low_type) for block in blocks]
        + [pltpu.VMEM((levels - 1,) + block, low_type) for block in blocks]
        + [pltpu.VMEM(block, low_type) for block in blocks] * 2
        + [dma(c) for c in counts for _ in range(2)],
        compiler_params=pltpu.CompilerParams(
            collective_id=10, has_side_effects=True, vmem_limit_bytes=56 * 2**20
        ),
        cost_estimate=cost(0, 200e6),
        name="finish",
    )(part, middle, *grads)


BLOCK = 512
LOG2E = 1.4426950408889634


def dot(left_side, right_side, left_dim, right_dim):
    return lax.dot_general(
        left_side,
        right_side,
        (((left_dim,), (right_dim,)), ((), ())),
        preferred_element_type=jnp.float32,
    )


def attend_kernel(parts, first, q, *refs):
    keys, values = refs[:parts], refs[parts : 2 * parts]
    pos_q, start_q, pos_k, out, lse, top, total, acc = refs[2 * parts :]
    at = pl.program_id(0)
    blocks = pl.num_programs(0)
    rate = LOG2E * DH ** (-0.5)
    top[...] = jnp.full_like(top, -1e30)
    total[...] = jnp.zeros_like(total)
    acc[...] = jnp.zeros_like(acc)
    query = q[...]
    row_at, row_from = pos_q[0], start_q[0]

    for part in range(parts):

        def step(block, carry, k=keys[part], v=values[part], part=part):
            rows = pl.ds(pl.multiple_of(block * BLOCK, BLOCK), BLOCK)
            spot = pl.ds(pl.multiple_of((part * blocks + block) * BLOCK, BLOCK), BLOCK)
            scores = dot(k[rows, :], query, 1, 1)
            key_at = pos_k[spot, :]
            scores = jnp.where((key_at >= row_from) & (key_at <= row_at), scores, -1e30)
            old = top[...]
            new = jnp.maximum(old, jnp.max(scores, axis=0, keepdims=True))
            shrink = jnp.exp2((old - new) * rate)
            weight = jnp.exp2((scores - new) * rate)
            total[...] = total[...] * shrink + jnp.sum(weight, axis=0, keepdims=True)
            acc[...] = acc[...] * shrink + dot(v[rows, :], weight.astype(jnp.bfloat16), 0, 0)
            top[...] = new
            return carry

        begin = jnp.maximum(first[at] - part * blocks, 0)
        end = at + 1 if part == parts - 1 else blocks
        lax.fori_loop(begin, end, step, 0)
    out[...] = (acc[...] / total[...]).T
    lse[0] = top[...] * rate + jnp.log2(total[...])


def attend(first, queries, window, pos_q, start_q, pos_k):
    rows = queries.shape[0]
    parts = len(window)
    line = pl.BlockSpec((1, 1, BLOCK), lambda i, *_: (i, 0, 0))
    grid_spec = pltpu.PrefetchScalarGridSpec(
        num_scalar_prefetch=1,
        grid=(rows // BLOCK,),
        in_specs=[pl.BlockSpec((BLOCK, DH), lambda i, *_: (i, 0))]
        + [pl.BlockSpec((rows, DH), lambda i, *_: (0, 0))] * parts
        + [pl.BlockSpec((rows, DH), lambda i, *_: (0, 1))] * parts
        + [line, line, pl.BlockSpec((parts * rows, 1), lambda i, *_: (0, 0))],
        out_specs=[pl.BlockSpec((BLOCK, DH), lambda i, *_: (i, 0)), line],
        scratch_shapes=[
            pltpu.VMEM((1, BLOCK), jnp.float32),
            pltpu.VMEM((1, BLOCK), jnp.float32),
            pltpu.VMEM((DH, BLOCK), jnp.float32),
        ],
    )
    return pl.pallas_call(
        functools.partial(attend_kernel, parts),
        grid_spec=grid_spec,
        out_shape=[
            jax.ShapeDtypeStruct((rows, DH), jnp.float32),
            jax.ShapeDtypeStruct((rows // BLOCK, 1, BLOCK), jnp.float32),
        ],
        compiler_params=pltpu.CompilerParams(vmem_limit_bytes=48 * 2**20),
        cost_estimate=cost(2e10, 1e7),
        name="attend",
    )(first, queries, *window, *window, pos_q, start_q, pos_k)


def attend_back_kernel(parts, first, q, *refs):
    keys, values = refs[:parts], refs[parts : 2 * parts]
    grad, pos_q, start_q, lse, inner, pos_k, grad_q = refs[2 * parts : 2 * parts + 7]
    grads = refs[2 * parts + 7 : 3 * parts + 7]
    sum_k, sum_v, acc = refs[3 * parts + 7 :]
    at = pl.program_id(0)
    blocks = pl.num_programs(0)
    rate = LOG2E * DH ** (-0.5)
    scale = DH ** (-0.5)

    @pl.when(at == 0)
    def _():
        sum_k[...] = jnp.zeros_like(sum_k)
        sum_v[...] = jnp.zeros_like(sum_v)

    acc[...] = jnp.zeros_like(acc)
    query, grad_out = q[...], grad[...]
    row_at, row_from, row_lse, row_inner = pos_q[0], start_q[0], lse[0], inner[0]

    for part in range(parts):

        def step(block, carry, k=keys[part], v=values[part], part=part):
            rows = pl.ds(pl.multiple_of(block * BLOCK, BLOCK), BLOCK)
            spot = pl.ds(pl.multiple_of((part * blocks + block) * BLOCK, BLOCK), BLOCK)
            key, value = k[rows, :], v[rows, :]
            scores = dot(key, query, 1, 1)
            key_at = pos_k[spot, :]
            seen = (key_at >= row_from) & (key_at <= row_at)
            soft = jnp.where(seen, jnp.exp2(scores * rate - row_lse), 0.0)
            grad_soft = dot(value, grad_out, 1, 1)
            grad_scores = (soft * (grad_soft - row_inner)).astype(jnp.bfloat16)
            sum_v[spot, :] += dot(soft.astype(jnp.bfloat16), grad_out, 1, 0)
            sum_k[spot, :] += dot(grad_scores, query, 1, 0)
            acc[...] += dot(grad_scores, key, 0, 0)
            return carry

        begin = jnp.maximum(first[at] - part * blocks, 0)
        end = at + 1 if part == parts - 1 else blocks
        lax.fori_loop(begin, end, step, 0)
    grad_q[...] = (acc[...] * scale).astype(jnp.bfloat16)

    @pl.when(at == blocks - 1)
    def _():
        size = grads[0].shape[0]
        for part in range(parts):
            spot = slice(part * size, (part + 1) * size)
            grads[part][:, :DH] = (sum_k[spot, :] * scale).astype(grads[part].dtype)
            grads[part][:, DH:] = sum_v[spot, :].astype(grads[part].dtype)


def attend_back(first, queries, window, grads, pos_q, start_q, lse, inner, pos_k):
    rows = queries.shape[0]
    parts = len(window)
    block = pl.BlockSpec((BLOCK, DH), lambda i, *_: (i, 0))
    line = pl.BlockSpec((1, 1, BLOCK), lambda i, *_: (i, 0, 0))
    grid_spec = pltpu.PrefetchScalarGridSpec(
        num_scalar_prefetch=1,
        grid=(rows // BLOCK,),
        in_specs=[block]
        + [pl.BlockSpec((rows, DH), lambda i, *_: (0, 0))] * parts
        + [pl.BlockSpec((rows, DH), lambda i, *_: (0, 1))] * parts
        + [block, line, line, line, line]
        + [pl.BlockSpec((parts * rows, 1), lambda i, *_: (0, 0))],
        out_specs=[block] + [pl.BlockSpec((rows, 2 * DH), lambda i, *_: (0, 0))] * parts,
        scratch_shapes=[
            pltpu.VMEM((parts * rows, DH), jnp.float32),
            pltpu.VMEM((parts * rows, DH), jnp.float32),
            pltpu.VMEM((BLOCK, DH), jnp.float32),
        ],
    )
    kinds = [jnp.bfloat16] * (parts - 1) + [jnp.float32]
    return pl.pallas_call(
        functools.partial(attend_back_kernel, parts),
        grid_spec=grid_spec,
        out_shape=[jax.ShapeDtypeStruct((rows, DH), jnp.bfloat16)]
        + [jax.ShapeDtypeStruct((rows, 2 * DH), kind) for kind in kinds],
        compiler_params=pltpu.CompilerParams(vmem_limit_bytes=48 * 2**20),
        cost_estimate=cost(2e10, 1e7),
        name="attend_back",
    )(first, queries, *window, *window, grads, pos_q, start_q, lse, inner, pos_k)


def columns_of(ref, group, groups, step, depth):
    at = lax.rem(group + step + groups, groups) * depth
    return ref.at[:, pl.ds(pl.multiple_of(at, 128), depth)]


def front_kernel(groups, local, place, hidden, grads, *refs):
    w_in, w_out = refs[0], refs[1 : groups + 1]
    gates, active, grad_pre, rows_out, turned, acc = refs[groups + 1 :]
    levels, _, depth, width = w_in.shape
    tile = hidden.shape[0]
    model = groups * depth
    parts = [slice(step * depth, (step + 1) * depth) for step in range(groups)]
    for step in range(groups):
        turned[0, :, parts[step]] = columns_of(hidden, place[1], groups, -step, depth)[...]
        turned[1, :, parts[step]] = columns_of(grads, place[1], groups, -step, depth)[...]
    gate_grads = []
    for level in range(levels):
        pre_act = jnp.zeros((tile, width), jnp.float32)
        grad_active = jnp.zeros((tile, width), jnp.float32)
        for step in range(groups):
            pre_act += dot(turned[0, :, parts[step]], w_in[level, step], 1, 0)
            grad_active += dot(turned[1, :, parts[step]], w_out[step][level], 1, 0)
        first = level * local
        gate = jnp.concatenate(
            [jnp.broadcast_to(gates[:, first + e : first + e + 1], (tile, FH)) for e in range(local)],
            axis=1,
        )
        sig = 1.0 / (1.0 + jnp.exp2(-LOG2E * pre_act))
        act_pre = pre_act * sig
        columns = slice(level * width, (level + 1) * width)
        active[:, columns] = (act_pre * gate).astype(jnp.bfloat16)
        product = grad_active * act_pre
        for e in range(local):
            gate_grads.append(
                jnp.sum(product[:, e * FH : (e + 1) * FH], axis=1, keepdims=True)
            )
        slope = sig * (1.0 + pre_act * (1.0 - sig))
        low_pre = (grad_active * gate * slope).astype(jnp.bfloat16)
        grad_pre[:, columns] = low_pre
        for step in range(groups):
            back = dot(low_pre, w_in[level, step], 1, 1)
            acc[:, parts[step]] = back if level == 0 else acc[:, parts[step]] + back
    for step in range(groups):
        columns_of(rows_out, place[1], groups, -step, depth)[...] = acc[:, parts[step]].astype(
            jnp.bfloat16
        )
    spare = rows_out.shape[1] - model
    lane = lax.broadcasted_iota(jnp.int32, (tile, spare), 1) - place[0] * (levels * local)
    spread = jnp.zeros((tile, spare), jnp.float32)
    for e, column in enumerate(gate_grads):
        spread = jnp.where(lane == e, column, spread)
    rows_out[:, model:] = spread.astype(jnp.bfloat16)


def ffn_front(place, hidden, grads, w_in, w_out, gates, local):
    rows, wide = hidden.shape
    levels, groups, depth, width = w_in.shape
    tile = 512

    def by_row(columns):
        return pl.BlockSpec((tile, columns), lambda i, *_: (i, 0))

    once = pl.Buffered(1)
    whole = pl.BlockSpec(w_out[0].shape, lambda i, *_: (0, 0, 0), pipeline_mode=once)
    stacked = pl.BlockSpec(w_in.shape, lambda i, *_: (0, 0, 0, 0), pipeline_mode=once)
    grid_spec = pltpu.PrefetchScalarGridSpec(
        num_scalar_prefetch=1,
        grid=(rows // tile,),
        in_specs=[by_row(wide), by_row(groups * depth)]
        + [stacked]
        + [whole] * groups
        + [by_row(gates.shape[1])],
        out_specs=[by_row(levels * width), by_row(levels * width), by_row(wide)],
        scratch_shapes=[
            pltpu.VMEM((2, tile, groups * depth), jnp.bfloat16),
            pltpu.VMEM((tile, groups * depth), jnp.float32),
        ],
    )
    hidden_units = jax.ShapeDtypeStruct((rows, levels * width), jnp.bfloat16)
    return pl.pallas_call(
        functools.partial(front_kernel, groups, local),
        grid_spec=grid_spec,
        out_shape=[hidden_units, hidden_units, jax.ShapeDtypeStruct((rows, wide), jnp.bfloat16)],
        compiler_params=pltpu.CompilerParams(vmem_limit_bytes=58 * 2**20),
        cost_estimate=cost(6 * rows * groups * depth * levels * width, 3e7),
        name="ffn_front",
    )(place, hidden, grads, w_in, *w_out, gates)


def rear_kernel(groups, place, rows_in, hidden_units, *weight_grads):
    _, depth, _ = weight_grads[0].shape
    units = hidden_units[...]
    for step in range(groups):
        part = columns_of(rows_in, place[1], groups, step, depth)
        weight_grads[step][0] = dot(part[...], units, 0, 0).astype(jnp.bfloat16)


def feed_kernel(groups, place, active, *refs):
    weights = refs[:groups]
    feed, acc = refs[groups:]
    _, depth, _ = weights[0].shape
    level = pl.program_id(0)
    act = active[...]
    for step in range(groups):
        fed = dot(act, weights[step][0], 1, 1)
        part = slice(step * depth, (step + 1) * depth)

        @pl.when(level == 0)
        def _():
            acc[:, part] = fed

        @pl.when(level > 0)
        def _():
            acc[:, part] += fed

    @pl.when(level == pl.num_programs(0) - 1)
    def _():
        for step in range(groups):
            part = slice(step * depth, (step + 1) * depth)
            columns_of(feed, place[1], groups, -step, depth)[...] = acc[:, part].astype(
                jnp.bfloat16
            )


def whole_rows(rows, columns):
    return pl.BlockSpec((rows, columns), lambda i, *_: (0, 0), pipeline_mode=pl.Buffered(1))


def ffn_feed(place, active, weights):
    rows = active.shape[0]
    groups = len(weights)
    levels, depth, width = weights[0].shape
    return pl.pallas_call(
        functools.partial(feed_kernel, groups),
        grid_spec=pltpu.PrefetchScalarGridSpec(
            num_scalar_prefetch=1,
            grid=(levels,),
            in_specs=[pl.BlockSpec((rows, width), lambda i, *_: (0, i))]
            + [pl.BlockSpec((1, depth, width), lambda i, *_: (i, 0, 0))] * groups,
            out_specs=whole_rows(rows, groups * depth),
            scratch_shapes=[pltpu.VMEM((rows, groups * depth), jnp.float32)],
        ),
        out_shape=jax.ShapeDtypeStruct((rows, groups * depth), jnp.bfloat16),
        compiler_params=pltpu.CompilerParams(vmem_limit_bytes=58 * 2**20),
        cost_estimate=cost(2 * rows * groups * depth * levels * width, 3e7),
        name="ffn_feed",
    )(place, active, *weights)


def ffn_rear(place, rows_in, units, model, groups, levels):
    rows, wide = rows_in.shape
    width = units.shape[1] // levels
    depth = model // groups
    return pl.pallas_call(
        functools.partial(rear_kernel, groups),
        grid_spec=pltpu.PrefetchScalarGridSpec(
            num_scalar_prefetch=1,
            grid=(levels,),
            in_specs=[
                whole_rows(rows, wide),
                pl.BlockSpec((rows, width), lambda i, *_: (0, i)),
            ],
            out_specs=[pl.BlockSpec((1, depth, width), lambda i, *_: (i, 0, 0))] * groups,
        ),
        out_shape=[jax.ShapeDtypeStruct((levels, depth, width), jnp.bfloat16)] * groups,
        compiler_params=pltpu.CompilerParams(vmem_limit_bytes=58 * 2**20),
        cost_estimate=cost(2 * rows * groups * depth * levels * width, 3e7),
        name="ffn_rear",
    )(place, rows_in, units)


def named_by(routes, count):
    lane = lax.broadcasted_iota(jnp.int32, (routes.shape[0], count), 1)
    member = jnp.zeros(lane.shape, jnp.float32)
    for slot in range(routes.shape[1]):
        member = jnp.where(lane == routes[:, slot : slot + 1], 1.0, member)
    return member


def middle_kernel(rows, branch, routes, router, gain, bias, middle, extended, sig_out):
    experts = router.shape[1]
    width = rows.shape[1]
    rounded = branch[...].astype(jnp.bfloat16).astype(jnp.float32)
    value = rows[...].astype(jnp.float32) + rounded
    middle[...] = value
    _, _, normed = normalized(value, gain[...], bias[...])
    sig = 1.0 / (1.0 + jnp.exp2(-LOG2E * dot(normed, router[...], 1, 0)))
    sig_out[...] = sig
    extended[:, :width] = value.astype(jnp.bfloat16)
    gates = (sig * named_by(routes[...], experts)).astype(jnp.bfloat16)
    spare = extended.shape[1] - width - experts
    if spare:
        gates = jnp.concatenate([gates, jnp.zeros((gates.shape[0], spare), gates.dtype)], axis=1)
    extended[:, width:] = gates


def enter_ffn(rows, branch, routes, router, gain, bias):
    count, width = rows.shape
    experts = router.shape[1]
    wide = width + experts + -experts % 128
    return pl.pallas_call(
        middle_kernel,
        out_shape=[
            jax.ShapeDtypeStruct((count, width), jnp.float32),
            jax.ShapeDtypeStruct((count, wide), jnp.bfloat16),
            jax.ShapeDtypeStruct((count, experts), jnp.float32),
        ],
        compiler_params=pltpu.CompilerParams(vmem_limit_bytes=40 * 2**20),
        cost_estimate=cost(1e9, 1e7),
        name="middle",
    )(rows, branch, routes, router, gain, bias)


def leave_kernel(
    middle, own, came, cotangent, sigs, routes, router, gain, bias, grad_out, low_out, weight_grads
):
    experts = router.shape[1]
    count, width = middle.shape
    scaled, inverse, normed = normalized(middle[...], gain[...], bias[...])
    total = own[...] + came[...].astype(jnp.float32)
    sig = sigs[...]
    member = named_by(routes[...], experts)
    gate_grads = total[:, width : width + experts]
    logit = (gate_grads * sig * (1.0 - sig) * member).astype(jnp.bfloat16)
    second = dot(logit, router[...], 1, 1)
    inner_grad = second * gain[...]
    inner_grad = inverse * (
        inner_grad
        - jnp.mean(inner_grad, axis=1, keepdims=True)
        - scaled * jnp.mean(inner_grad * scaled, axis=1, keepdims=True)
    )
    grad = cotangent[...].astype(jnp.float32) + total[:, :width] + inner_grad
    grad_out[...] = grad
    low_out[...] = grad.astype(jnp.bfloat16)
    spare = weight_grads.shape[1] - experts
    sums = [
        jnp.sum(second * scaled, axis=0, keepdims=True),
        jnp.sum(second, axis=0, keepdims=True),
        jnp.zeros((126, width), jnp.float32),
    ]
    side = jnp.concatenate(sums, axis=0).T[:, :spare]
    both = jnp.concatenate([dot(normed, logit, 0, 0), side], axis=1)
    weight_grads[...] = both.astype(jnp.bfloat16)


def leave_ffn(middle, own, came, cotangent, sigs, routes, router, gain, bias):
    count, width = middle.shape
    experts = router.shape[1]
    columns = experts + 2 + -(experts + 2) % 128
    return pl.pallas_call(
        leave_kernel,
        out_shape=[
            jax.ShapeDtypeStruct((count, width), jnp.float32),
            jax.ShapeDtypeStruct((count, width), jnp.bfloat16),
            jax.ShapeDtypeStruct((width, columns), jnp.bfloat16),
        ],
        compiler_params=pltpu.CompilerParams(vmem_limit_bytes=48 * 2**20),
        cost_estimate=cost(1e9, 1e7),
        name="leave_ffn",
    )(middle, own, came, cotangent, sigs, routes, router, gain, bias)


def branch_back_kernel(
    grads, w_output, attended, sigs, masks, grad_attended, inner, out_logit, weight_grads, acc
):
    at = pl.program_id(0)
    count = grads.shape[0]
    sig, mask, values = sigs[...], masks[...], attended[...]
    mixed_grad = dot(grads[...], w_output[...], 1, 0)
    lane = lax.broadcasted_iota(jnp.int32, (count, 128), 1)
    logits = jnp.zeros((count, 128), jnp.float32)
    total = jnp.zeros((count, DH), jnp.float32)
    parts = []
    for e in range(VEXP):
        k = VEXP + e
        one, on = sig[:, k : k + 1], mask[:, k : k + 1]
        part = mixed_grad[:, e * DH : (e + 1) * DH]
        total += part * (one * on)
        gate_grad = jnp.sum(part * values, axis=1, keepdims=True)
        logits = jnp.where(lane == k, gate_grad * one * (1.0 - one) * on, logits)
        parts.append((one * on * values).astype(jnp.bfloat16))
    out_logit[...] = logits.astype(jnp.bfloat16)
    rounded = total.astype(jnp.bfloat16)
    grad_attended[...] = rounded
    product = rounded.astype(jnp.float32) * values
    inner[0] = jnp.sum(product.T, axis=0, keepdims=True)
    amount = dot(grads[...], jnp.concatenate(parts, axis=1), 0, 0)

    @pl.when(at == 0)
    def _():
        acc[...] = amount

    @pl.when(at > 0)
    def _():
        acc[...] += amount

    @pl.when(at == pl.num_programs(0) - 1)
    def _():
        weight_grads[...] = acc[...].astype(jnp.bfloat16)


def branch_back(grads, full, attended, sigs, masks):
    rows, width = grads.shape
    values = VEXP * DH

    def by_row(size):
        return pl.BlockSpec((BLOCK, size), lambda i: (i, 0))

    return pl.pallas_call(
        branch_back_kernel,
        grid=(rows // BLOCK,),
        in_specs=[
            by_row(width),
            pl.BlockSpec((width, values), lambda i: (0, 1), pipeline_mode=pl.Buffered(1)),
            by_row(DH),
            by_row(128),
            by_row(16),
        ],
        out_specs=[
            by_row(DH),
            pl.BlockSpec((1, 1, BLOCK), lambda i: (i, 0, 0)),
            by_row(128),
            pl.BlockSpec((width, values), lambda i: (0, 0)),
        ],
        out_shape=[
            jax.ShapeDtypeStruct((rows, DH), jnp.bfloat16),
            jax.ShapeDtypeStruct((rows // BLOCK, 1, BLOCK), jnp.float32),
            jax.ShapeDtypeStruct((rows, 128), jnp.bfloat16),
            jax.ShapeDtypeStruct((width, values), jnp.bfloat16),
        ],
        scratch_shapes=[pltpu.VMEM((width, values), jnp.float32)],
        compiler_params=pltpu.CompilerParams(vmem_limit_bytes=48 * 2**20),
        cost_estimate=cost(4 * rows * width * values, 2e7),
        name="branch_back",
    )(grads, full, attended, sigs, masks)


def turn(value, axis, by):
    size = lax.axis_size(axis)
    return lax.ppermute(value, axis, [(i, (i + by) % size) for i in range(size)])


def normalized(rows, gain, bias):
    values = rows.astype(jnp.float32)
    centred = values - jnp.mean(values, axis=1, keepdims=True)
    inverse = lax.rsqrt(jnp.mean(centred * centred, axis=1, keepdims=True) + 1e-05)
    scaled = centred * inverse
    return scaled, inverse, (scaled * gain + bias).astype(jnp.bfloat16)


def project_kernel(
    levels, rows, w_value, w_query, w_key, routers, gain, bias, order, tables,
    query, key_value, projected, sigs, masks,
):
    count = rows.shape[0]
    piece = count // (levels * HEADS)
    _, _, normed = normalized(rows[...], gain[...], bias[...])
    query[...] = dot(normed, w_query[...], 1, 0).astype(jnp.bfloat16)
    key_value[:, :DH] = dot(normed, w_key[...], 1, 0).astype(jnp.bfloat16)
    sig = 1.0 / (1.0 + jnp.exp2(-LOG2E * dot(normed, routers[...], 1, 0)))
    sigs[...] = sig
    product = dot(rows[...], w_value[...], 1, 0)
    projected[...] = product
    at = lax.broadcasted_iota(jnp.int32, (count, count), 0)
    source = lax.rem(at // piece, levels) * HEADS + at // (piece * levels)
    here = (source * piece + lax.rem(at, piece) == order[0]).astype(jnp.bfloat16)
    lane = lax.broadcasted_iota(jnp.int32, (16, count), 0)
    table = tables[0]
    named = jnp.zeros((16, count), jnp.float32)
    for which in range(2):
        option = lane - which * VEXP
        for slot in range(2):
            pick = table[2 * which + slot : 2 * which + slot + 1, :]
            hit = (option == pick) & (option >= 0) & (option < VEXP)
            named = jnp.where(hit, 1.0, named)
    mask = dot(here, named.astype(jnp.bfloat16), 1, 1)
    masks[...] = mask
    value = jnp.zeros((count, DH), jnp.float32)
    for e in range(VEXP):
        gate = sig[:, e : e + 1] * mask[:, e : e + 1]
        value += gate * product[:, e * DH : (e + 1) * DH]
    key_value[:, DH:] = value.astype(jnp.bfloat16)


def project(rows, full, gain, bias, orders, tables, levels):
    total, width = rows.shape
    count = total // HEADS

    def by_row(columns):
        return pl.BlockSpec((count, columns), lambda i: (i, 0))

    def column(size, at):
        return pl.BlockSpec((width, size), lambda i: (0, at), pipeline_mode=pl.Buffered(1))

    line = pl.BlockSpec((1, width), lambda i: (0, 0))
    shapes = [(DH, jnp.bfloat16), (2 * DH, jnp.bfloat16), (VEXP * DH, jnp.float32)]
    shapes += [(128, jnp.float32), (16, jnp.float32)]
    return pl.pallas_call(
        functools.partial(project_kernel, levels),
        grid=(HEADS,),
        in_specs=[by_row(width), column(VEXP * DH, 0)]
        + [column(DH, 2 * VEXP + i) for i in range(3)]
        + [line, line]
        + [
            pl.BlockSpec((1, 1, count), lambda i: (i, 0, 0)),
            pl.BlockSpec((1,) + tables.shape[1:], lambda i: (i, 0, 0)),
        ],
        out_specs=[by_row(columns) for columns, _ in shapes],
        out_shape=[jax.ShapeDtypeStruct((total, columns), kind) for columns, kind in shapes],
        compiler_params=pltpu.CompilerParams(vmem_limit_bytes=48 * 2**20),
        cost_estimate=cost(2 * total * width * 1024, 2e7),
        name="project",
    )(rows, full, full, full, full, gain, bias, orders, tables)


def project_back_kernel(
    rows, grads, grad_query, out_logit, projected, sigs, masks,
    w_value, w_query, w_key, routers, gain, bias,
    grad_rows, weight_grads, acc, sums,
):
    at = pl.program_id(0)
    count = rows.shape[0]
    values = VEXP * DH

    @pl.when(at == 0)
    def _():
        acc[...] = jnp.zeros_like(acc)
        sums[...] = jnp.zeros_like(sums)

    scaled, inverse, normed = normalized(rows[...], gain[...], bias[...])
    grad_key = grads[:, :DH].astype(jnp.bfloat16)
    grad_value = grads[:, DH:]
    sig, mask = sigs[...], masks[...]
    lane = lax.broadcasted_iota(jnp.int32, (count, 128), 1)
    logits = out_logit[...].astype(jnp.float32)
    parts = []
    for e in range(VEXP):
        one, on = sig[:, e : e + 1], mask[:, e : e + 1]
        parts.append((one * on * grad_value).astype(jnp.bfloat16))
        inner = jnp.sum(grad_value * projected[:, e * DH : (e + 1) * DH], axis=1, keepdims=True)
        logits = jnp.where(lane == e, inner * one * (1.0 - one) * on, logits)
    grad_projected = jnp.concatenate(parts, axis=1)
    sides = jnp.concatenate([grad_query[...], grad_key, logits.astype(jnp.bfloat16)], axis=1)
    first = dot(sides[:, :DH], w_query[...], 1, 1)
    first += dot(sides[:, DH : 2 * DH], w_key[...], 1, 1)
    first += dot(sides[:, 2 * DH :], routers[...], 1, 1)
    sums[2 * VEXP : 2 * VEXP + 1, :] += jnp.sum(first * scaled, axis=0, keepdims=True)
    sums[2 * VEXP + 1 : 2 * VEXP + 2, :] += jnp.sum(first, axis=0, keepdims=True)
    inner_grad = first * gain[...]
    inner_grad = inverse * (
        inner_grad
        - jnp.mean(inner_grad, axis=1, keepdims=True)
        - scaled * jnp.mean(inner_grad * scaled, axis=1, keepdims=True)
    )
    grad_rows[...] = (inner_grad + dot(grad_projected, w_value[...], 1, 1)).astype(jnp.bfloat16)
    acc[:, :values] += dot(rows[...], grad_projected, 0, 0)
    acc[:, values:] += dot(normed, sides, 0, 0)

    @pl.when(at == pl.num_programs(0) - 1)
    def _():
        weight_grads[:, : values + 2 * DH] = acc[:, : values + 2 * DH].astype(jnp.bfloat16)
        last = acc[:, values + 2 * DH :] + sums[...].T
        weight_grads[:, values + 2 * DH :] = last.astype(jnp.bfloat16)


def project_back(rows, grads, grad_query, out_logit, projected, sigs, masks, full, gain, bias):
    total, width = rows.shape
    count = total // HEADS
    columns = VEXP * DH + 3 * DH

    def by_row(size):
        return pl.BlockSpec((count, size), lambda i: (i, 0))

    def column(size, at):
        return pl.BlockSpec((width, size), lambda i: (0, at), pipeline_mode=pl.Buffered(1))

    line = pl.BlockSpec((1, width), lambda i: (0, 0))
    return pl.pallas_call(
        project_back_kernel,
        grid=(HEADS,),
        in_specs=[by_row(width), by_row(2 * DH), by_row(DH), by_row(128), by_row(VEXP * DH)]
        + [by_row(128), by_row(16), column(VEXP * DH, 0)]
        + [column(DH, 2 * VEXP + i) for i in range(3)]
        + [line, line],
        out_specs=[by_row(width), pl.BlockSpec((width, columns), lambda i: (0, 0))],
        out_shape=[
            jax.ShapeDtypeStruct((total, width), jnp.bfloat16),
            jax.ShapeDtypeStruct((width, columns), jnp.bfloat16),
        ],
        scratch_shapes=[
            pltpu.VMEM((width, columns), jnp.float32),
            pltpu.VMEM((128, width), jnp.float32),
        ],
        compiler_params=pltpu.CompilerParams(vmem_limit_bytes=56 * 2**20),
        cost_estimate=cost(4 * total * width * 1024, 4e7),
        name="project_back",
    )(rows, grads, grad_query, out_logit, projected, sigs, masks, full, full, full, full, gain, bias)


def shift(value, axis, by):
    count = lax.axis_size(axis)
    pairs = [(i, i + by) for i in range(count) if 0 <= i + by < count]
    return lax.ppermute(value, axis, pairs)


def body(
    tokens_in,
    out_grad,
    deal_order,
    seq_lengths,
    value_routes,
    output_routes,
    ffn_routes,
    norm1_gain,
    norm1_bias,
    norm2_gain,
    norm2_bias,
    query_weight,
    key_weight,
    value_weight,
    output_weight,
    value_router,
    output_router,
    ffn_router,
    ffn_in,
    ffn_out,
):
    groups = lax.axis_size("group")
    levels = lax.axis_size("level")
    level = lax.axis_index("level")
    head = lax.axis_index("head")
    count, width = tokens_in.shape
    piece = count // (levels * HEADS)
    wrows = query_weight.shape[0]
    experts = ffn_router.shape[1]
    local_experts = ffn_in.shape[1] // FH

    small = jnp.concatenate(
        [
            ffn_router,
            norm1_gain[:, None],
            norm1_bias[:, None],
            norm2_gain[:, None],
            norm2_bias[:, None],
        ],
        axis=1,
    )
    shared = small.shape[1]
    pad = -(shared + 2 * VEXP) % 128
    extra = jnp.concatenate(
        [
            value_router.reshape(wrows, HEADS, VEXP),
            output_router.reshape(wrows, HEADS, VEXP),
            jnp.broadcast_to(small[:, None, :], (wrows, HEADS, shared)),
            jnp.zeros((wrows, HEADS, pad), jnp.bfloat16),
        ],
        axis=2,
    )
    cols = 2 * DH + 2 * VEXP * DH + extra.shape[2]
    tables = jnp.concatenate(
        [value_routes.transpose(1, 2, 0), output_routes.transpose(1, 2, 0)], axis=1
    )
    picks = ffn_routes.reshape(levels, HEADS * piece, -1).transpose(0, 2, 1)
    arrived, own_grads, full, tables, picks, orders = start(
        tokens_in.reshape(levels, HEADS, piece, width),
        out_grad.reshape(levels, HEADS, piece, width),
        [value_weight, output_weight, query_weight, key_weight],
        extra.transpose(1, 0, 2),
        tables,
        picks,
        deal_order,
    )
    worker_in = arrived.reshape(HEADS * count, width)
    own_tokens = lax.dynamic_index_in_dim(arrived, head, 1, keepdims=False).reshape(count, width)
    in_rows = [turn(ffn_in, "group", k) for k in range(1, groups)]
    full, in_rows = lax.optimization_barrier((full.reshape(width, cols), in_rows))

    base = 2 * DH + 2 * VEXP * DH
    w_output = full[:, VEXP * DH : 2 * VEXP * DH]
    at = base + 2 * VEXP
    def relabelled(expert):
        share = expert // local_experts
        return (share % HEADS * levels + share // HEADS) * local_experts + expert % local_experts

    labels = jnp.arange(experts, dtype=jnp.int32)
    moved = low(relabelled(labels)[:, None] == labels[None, :])
    r_ffn = low(
        jnp.dot(full[:, at : at + experts], moved, preferred_element_type=jnp.float32)
    )
    gain_one, bias_one, gain_two, bias_two = (
        full[:, at + experts + i].astype(jnp.float32) for i in range(4)
    )
    gain_row, bias_row = gain_one[None], bias_one[None]
    orders = orders.reshape(levels, HEADS, count)
    own_order = lax.dynamic_index_in_dim(orders, level, 0, keepdims=False)[:, None, :]
    queries, key_value, projected, sigs, masks = project(
        worker_in, full, gain_row, bias_row, own_order, tables, levels
    )

    rows = HEADS * count
    reach = -(-LMAX // rows)

    ramp = jnp.arange(count, dtype=jnp.int32)

    def arrival(values):
        lead, shape = values.shape[:-3], values.shape[-1:]
        four = values.reshape(lead + (HEADS, levels, HEADS, piece) + shape)
        return jnp.swapaxes(four, -4, -3).reshape(lead + (rows,) + shape)

    orders = jnp.concatenate([jnp.zeros((reach, HEADS, count), jnp.int32), orders], axis=0)
    orders = lax.dynamic_slice_in_dim(orders, level, reach + 1, 0)
    here = orders[:, :, None, :] == ramp[None, None, :, None]
    inverse = jnp.sum(here * ramp, axis=3)
    shard = (level - reach + jnp.arange(reach + 1, dtype=jnp.int32))[:, None] * HEADS
    shard = shard + jnp.arange(HEADS, dtype=jnp.int32)[None, :]
    pos_all = jnp.where(shard[:, :, None] < 0, -1, shard[:, :, None] * count + inverse)
    pos_all = arrival(pos_all[..., None]).reshape(-1)
    positions = pos_all[reach * rows :]
    seq_ends = jnp.cumsum(seq_lengths[0])

    def starts_of(places):
        return jnp.max(jnp.where(seq_ends <= places[:, None], seq_ends, 0), axis=1)

    starts = starts_of(positions)
    blocks = rows // BLOCK
    base_block = (level - reach) * blocks
    first_block = starts_of(level * rows + jnp.arange(blocks, dtype=jnp.int32) * BLOCK) // BLOCK
    first_block = jnp.maximum(first_block - base_block, 0)

    own_routes = picks.reshape(levels, -1, HEADS, piece).transpose(2, 0, 3, 1).reshape(count, -1)
    own_routes = relabelled(own_routes)
    ffn_side = (own_routes, r_ffn, gain_two[None], bias_two[None], own_tokens)

    window = [key_value]
    own_grads = own_grads.reshape(count, width)
    for i in range(reach):
        came = shift(window[0], "level", 1)
        if i == 0:
            came, own_grads, pos_all, starts, ffn_out, in_rows = lax.optimization_barrier(
                (came, own_grads, pos_all, starts, ffn_out, [ffn_in] + in_rows)
            )
            cotangent = level_gather(own_grads, 5, True)
        if i == reach - 1:
            came, cotangent, ffn_side = lax.optimization_barrier((came, cotangent, ffn_side))
        window.insert(0, came)
    place = jnp.stack([head, lax.axis_index("group")])
    out_here = lax.all_gather(ffn_out, "level", axis=0)
    w_in = lax.all_gather(jnp.stack(in_rows), "level", axis=0)


    def lines(values):
        return values.reshape(blocks, 1, BLOCK)

    attended, log_total = attend(
        first_block,
        queries,
        window,
        lines(positions),
        lines(starts),
        pos_all[:, None],
    )

    out_sig = sigs[:, VEXP : 2 * VEXP]
    out_mask = masks[:, VEXP : 2 * VEXP]
    out_gate = out_sig * out_mask
    attended, out_here = lax.optimization_barrier((attended, out_here))
    w_out = [out_here] + [turn(out_here, "group", k) for k in range(1, groups)]
    mixed = low((out_gate[..., None] * attended[:, None, :]).reshape(rows, VEXP * DH))
    branch = level_scatter(low(transposed(mixed, w_output)), 2)

    own_routes, r_ffn, gain_two, bias_two, own_tokens = ffn_side
    middle, extended, ffn_sig = enter_ffn(own_tokens, branch, own_routes, r_ffn, gain_two, bias_two)
    hidden = level_gather(extended, 3, True)
    mine = levels * local_experts
    gates = lax.dynamic_slice_in_dim(hidden, width + head * mine, mine, 1).astype(jnp.float32)
    active, grad_pre, grad_rows = ffn_front(
        place, hidden, cotangent, w_in, w_out, gates, local_experts
    )
    summed, beyond = pair_scatter(grad_rows, 4, True)
    beyond, hidden = lax.optimization_barrier((beyond, hidden))
    came = to_far(beyond)
    grad_in = ffn_rear(place, hidden, grad_pre, width, groups, levels)
    in_came = [turn(grad_in[k], "group", k) for k in range(1, groups)]
    grad_out = ffn_rear(place, cotangent, active, width, groups, levels)
    out_came = [turn(grad_out[k], "group", k) for k in range(1, groups)]
    came, grad_in, grad_out = lax.optimization_barrier((came, grad_in, grad_out))
    grad_middle, own_branch, early = leave_ffn(
        middle, summed, came, own_grads, ffn_sig, own_routes, r_ffn, gain_two, bias_two
    )
    came = to_far(own_branch)
    feed = ffn_feed(place, active, w_out)
    came, feed = lax.optimization_barrier((came, feed))
    grad_branch = pair_gather(own_branch, came, 7)

    def sum_of(own, others):
        total = own[0].astype(jnp.float32)
        for other in others:
            total = total + other.astype(jnp.float32)
        return low(total)

    def over_levels(total):
        return lax.psum_scatter(total, "level", scatter_dimension=0)

    grad_branch, in_came = lax.optimization_barrier((grad_branch, in_came))
    ffn_in_grad = over_levels(sum_of(grad_in, in_came))
    grad_attended, row_inner, grad_out_logit, grad_w_output = branch_back(
        grad_branch, full, attended, sigs, masks
    )
    grad_queries, *grad_window = attend_back(
        first_block,
        queries,
        window,
        grad_attended,
        lines(positions),
        lines(starts),
        log_total,
        row_inner,
        pos_all[:, None],
    )
    came = shift(grad_window[0], "level", -1)
    fed, beyond = pair_scatter(feed, 6, True)
    for i in range(1, reach + 1):
        if i < reach:
            came, fed = lax.optimization_barrier((came, fed))
        grad_both = grad_window[i].astype(jnp.float32) + came.astype(jnp.float32)
        if i < reach:
            grad_keys_sent = low(grad_both)
            came = shift(grad_keys_sent, "level", -1)
    grad_both, out_came = lax.optimization_barrier((grad_both, out_came))
    ffn_out_grad = over_levels(sum_of(grad_out, out_came))
    fed_far = to_far(beyond)
    grad_inputs, late = project_back(
        worker_in,
        grad_both,
        grad_queries,
        grad_out_logit,
        projected,
        sigs,
        masks,
        full,
        gain_row,
        bias_row,
    )

    fed_far, grad_inputs = lax.optimization_barrier((fed_far, grad_inputs))
    layer_out = to_home(low(middle + fed + fed_far.astype(jnp.float32)))

    values = VEXP * DH
    layout = (
        ((0, values, True), (values, DH, True), (values + DH, DH, True), (values + 2 * DH, DH, False)),
        ((0, values, True),),
        ((0, early.shape[1], False),),
    )

    def by_owner(grads):
        return grads.reshape(groups, levels, HEADS, wrows, -1)

    input_grad, grad_value, grad_query, grad_key, sides, grad_output, common = finish(
        layout,
        grad_inputs.reshape(HEADS, HEADS, levels * piece, width),
        grad_middle.reshape(HEADS, levels * piece, width),
        by_owner(late),
        by_owner(grad_w_output),
        by_owner(early),
    )
    norms = jnp.sum(sides[:, :, 2 * VEXP : 2 * VEXP + 2], axis=0)
    common = jnp.sum(common[:, :, : experts + 2], axis=0)
    router_grad = common[:, :experts].reshape(wrows, HEADS, levels, local_experts)

    def side(first):
        return sides[:, :, first : first + VEXP].transpose(1, 0, 2).reshape(wrows, HEADS * VEXP)

    return (
        layer_out,
        input_grad.reshape(count, width),
        norms[:, 0],
        norms[:, 1],
        common[:, experts],
        common[:, experts + 1],
        grad_query,
        grad_key,
        grad_value,
        grad_output,
        side(0),
        side(VEXP),
        jnp.swapaxes(router_grad, 1, 2).reshape(wrows, experts),
        ffn_in_grad.astype(jnp.float32),
        ffn_out_grad.astype(jnp.float32),
    )


def solution(mesh):
    groups, shards = mesh.devices.shape
    fine = Mesh(mesh.devices.reshape(groups, shards // HEADS, HEADS), TOK)
    two, one, three = P(TOK, None), P(TOK), P(TOK, None, None)
    ffn = P("group", ("level", "head"))
    return jax.shard_map(
        body,
        mesh=fine,
        in_specs=(two, two, two, P("group", None), three, three, two, one, one, one, one)
        + (two,) * 7
        + (ffn, ffn),
        out_specs=(two, two, one, one, one, one) + (two,) * 7 + (ffn, ffn),
        check_vma=False,
    )
```

```python
import functools

import jax
import jax.numpy as jnp
from jax import lax
from jax.experimental import pallas as pl
from jax.experimental.pallas import tpu as pltpu
from jax.sharding import Mesh, PartitionSpec as P

HEADS = 4
DH = 128
VEXP = 5
FH = 128
LMAX = 4096

TOK = ("group", "level", "head")


def transposed(left_side, right_side):
    return lax.dot_general(
        left_side, right_side, (((1,), (1,)), ((), ())), preferred_element_type=jnp.float32
    )


def low(value):
    return value.astype(jnp.bfloat16)


def to_home(rows):
    levels = lax.axis_size("level")
    count = rows.shape[0]
    out = rows.reshape(HEADS, levels, count // levels // HEADS, -1).transpose(1, 0, 2, 3)
    back = lax.all_to_all(
        out.reshape(levels, count // levels, -1), "level", split_axis=0, concat_axis=0, tiled=True
    )
    return back.reshape(count, -1)


MESH = pl.DeviceIdType.MESH


def partners(head):
    near = head + 1 - 2 * lax.rem(head, 2)
    far = lax.rem(head + 2, HEADS)
    return near, far


def greet(near, far):
    barrier = pltpu.get_barrier_semaphore()
    for peer in (near, far):
        pl.semaphore_signal(barrier, inc=1, device_id={"head": peer}, device_id_type=MESH)
    pl.semaphore_wait(barrier, 2)


def remote(src, dst, send, recv, peer):
    return pltpu.make_async_remote_copy(
        src_ref=src,
        dst_ref=dst,
        send_sem=send,
        recv_sem=recv,
        device_id={"head": peer},
        device_id_type=MESH,
    )


def cost(flops, moved):
    return pl.CostEstimate(flops=int(flops), bytes_accessed=int(moved), transcendentals=0)


def gather_kernel(
    by_source, own, out, local_sem, near_send, near_recv, far_send, far_recv, pass_send, pass_recv
):
    head = lax.axis_index("head")
    near, far = partners(head)
    greet(near, far)

    def spot(i, source):
        return out.at[source, i] if by_source else out.at[i, source]

    pieces = range(HEADS)
    to_far = [remote(own.at[i], spot(i, head), far_send.at[i], far_recv.at[i], far) for i in pieces]
    to_near = [
        remote(own.at[i], spot(i, head), near_send.at[i], near_recv.at[i], near) for i in pieces
    ]
    passed = [
        remote(spot(i, far), spot(i, far), pass_send.at[i], pass_recv.at[i], near) for i in pieces
    ]
    kept = [pltpu.make_async_copy(own.at[i], spot(i, head), local_sem.at[i]) for i in pieces]
    for copy in to_far + to_near + kept:
        copy.start()
    for i in pieces:
        to_far[i].wait_recv()
        passed[i].start()
    for i in pieces:
        to_near[i].wait_recv()
        passed[i].wait_recv()
        kept[i].wait()
        to_far[i].wait_send()
        to_near[i].wait_send()
        passed[i].wait_send()


def level_gather(rows, collective_id, by_source=False):
    count, width = rows.shape
    whole = pl.pallas_call(
        functools.partial(gather_kernel, by_source),
        out_shape=jax.ShapeDtypeStruct((HEADS, HEADS, count // HEADS, width), rows.dtype),
        in_specs=[pl.BlockSpec(memory_space=pltpu.VMEM)],
        out_specs=pl.BlockSpec(memory_space=pl.ANY),
        scratch_shapes=[pltpu.SemaphoreType.DMA((HEADS,))] * 7,
        compiler_params=pltpu.CompilerParams(collective_id=collective_id, has_side_effects=True),
        cost_estimate=cost(0, 90e6),
        name="level_gather",
    )(rows.reshape(HEADS, count // HEADS, width))
    return whole.reshape(HEADS * count, width)


def scatter_kernel(
    by_source, part, out, near_buf, send_buf, far_buf, near_send, near_recv, far_send, far_recv
):
    head = lax.axis_index("head")
    near, far = partners(head)
    greet(near, far)
    across = HEADS - 1 - head
    pieces = range(HEADS)

    def spot(i, dest):
        return (dest, i) if by_source else (i, dest)

    def to_near(slot, i, dest):
        return remote(
            part.at[spot(i, dest)],
            near_buf.at[slot, i],
            near_send.at[slot, i],
            near_recv.at[slot, i],
            near,
        )

    first = [to_near(0, i, across) for i in pieces]
    second = [to_near(1, i, near) for i in pieces]
    onward = [
        remote(send_buf.at[i], far_buf.at[i], far_send.at[i], far_recv.at[i], far) for i in pieces
    ]
    for copy in first + second:
        copy.start()
    for i in pieces:
        first[i].wait_recv()
        both = part[spot(i, far)].astype(jnp.float32) + near_buf[0, i].astype(jnp.float32)
        send_buf[i] = both.astype(jnp.bfloat16)
        onward[i].start()
    for i in pieces:
        second[i].wait_recv()
        out[i] = part[spot(i, head)].astype(jnp.float32) + near_buf[1, i].astype(jnp.float32)
    for i in pieces:
        onward[i].wait_recv()
        out[i] = out[i] + far_buf[i].astype(jnp.float32)
    for i in pieces:
        first[i].wait_send()
        second[i].wait_send()
        onward[i].wait_send()


def level_scatter(rows, collective_id, by_source=False):
    total, width = rows.shape
    piece = total // (HEADS * HEADS)
    low_type = jnp.bfloat16
    mine = pl.pallas_call(
        functools.partial(scatter_kernel, by_source),
        out_shape=jax.ShapeDtypeStruct((HEADS, piece, width), jnp.float32),
        in_specs=[pl.BlockSpec(memory_space=pltpu.VMEM)],
        out_specs=pl.BlockSpec(memory_space=pltpu.VMEM),
        scratch_shapes=[
            pltpu.VMEM((2, HEADS, piece, width), low_type),
            pltpu.VMEM((HEADS, piece, width), low_type),
            pltpu.VMEM((HEADS, piece, width), low_type),
            pltpu.SemaphoreType.DMA((2, HEADS)),
            pltpu.SemaphoreType.DMA((2, HEADS)),
            pltpu.SemaphoreType.DMA((HEADS,)),
            pltpu.SemaphoreType.DMA((HEADS,)),
        ],
        compiler_params=pltpu.CompilerParams(
            collective_id=collective_id, has_side_effects=True, vmem_limit_bytes=32 * 2**20
        ),
        cost_estimate=cost(0, 80e6),
        name="level_scatter",
    )(rows.reshape(HEADS, HEADS, piece, width))
    return mine.reshape(HEADS * piece, width)


def meet(near):
    barrier = pltpu.get_barrier_semaphore()
    pl.semaphore_signal(barrier, inc=1, device_id={"head": near}, device_id_type=MESH)
    pl.semaphore_wait(barrier, 1)


def pair_scatter_kernel(by_source, part, out, out_far, near_buf, send, recv):
    head = lax.axis_index("head")
    near, far = partners(head)
    meet(near)
    across = HEADS - 1 - head
    pieces = range(HEADS)

    def spot(i, dest):
        return (dest, i) if by_source else (i, dest)

    def to_near(slot, i, dest):
        return remote(
            part.at[spot(i, dest)], near_buf.at[slot, i], send.at[slot, i], recv.at[slot, i], near
        )

    first = [to_near(0, i, across) for i in pieces]
    second = [to_near(1, i, near) for i in pieces]
    for copy in first + second:
        copy.start()
    for i in pieces:
        first[i].wait_recv()
        both = part[spot(i, far)].astype(jnp.float32) + near_buf[0, i].astype(jnp.float32)
        out_far[i] = both.astype(jnp.bfloat16)
    for i in pieces:
        second[i].wait_recv()
        out[i] = part[spot(i, head)].astype(jnp.float32) + near_buf[1, i].astype(jnp.float32)
    for i in pieces:
        first[i].wait_send()
        second[i].wait_send()


def pair_scatter(rows, collective_id, by_source=False):
    total, width = rows.shape
    piece = total // (HEADS * HEADS)
    mine, other = pl.pallas_call(
        functools.partial(pair_scatter_kernel, by_source),
        out_shape=[
            jax.ShapeDtypeStruct((HEADS, piece, width), jnp.float32),
            jax.ShapeDtypeStruct((HEADS, piece, width), jnp.bfloat16),
        ],
        in_specs=[pl.BlockSpec(memory_space=pltpu.VMEM)],
        out_specs=[pl.BlockSpec(memory_space=pltpu.VMEM)] * 2,
        scratch_shapes=[
            pltpu.VMEM((2, HEADS, piece, width), jnp.bfloat16),
            pltpu.SemaphoreType.DMA((2, HEADS)),
            pltpu.SemaphoreType.DMA((2, HEADS)),
        ],
        compiler_params=pltpu.CompilerParams(
            collective_id=collective_id, has_side_effects=True, vmem_limit_bytes=32 * 2**20
        ),
        cost_estimate=cost(0, 25e6),
        name="pair_scatter",
    )(rows.reshape(HEADS, HEADS, piece, width))
    return mine.reshape(HEADS * piece, width), other.reshape(HEADS * piece, width)


def pair_gather_kernel(by_source, own, other, out, local_sem, send, recv):
    head = lax.axis_index("head")
    near, far = partners(head)
    meet(near)
    copies, kept = [], []
    for i in range(HEADS):
        for slot, (block, source) in enumerate(((own, head), (other, far))):
            place = out.at[source, i] if by_source else out.at[i, source]
            copies.append(
                remote(block.at[i], place, send.at[slot, i], recv.at[slot, i], near)
            )
            kept.append(pltpu.make_async_copy(block.at[i], place, local_sem.at[slot, i]))
    for copy in copies + kept:
        copy.start()
    for copy in copies + kept:
        copy.wait()


def pair_gather(own, other, collective_id, by_source=False):
    count, width = own.shape
    split = (HEADS, count // HEADS, width)
    whole = pl.pallas_call(
        functools.partial(pair_gather_kernel, by_source),
        out_shape=jax.ShapeDtypeStruct((HEADS,) + split, own.dtype),
        in_specs=[pl.BlockSpec(memory_space=pltpu.VMEM)] * 2,
        out_specs=pl.BlockSpec(memory_space=pl.ANY),
        scratch_shapes=[pltpu.SemaphoreType.DMA((2, HEADS))] * 3,
        compiler_params=pltpu.CompilerParams(collective_id=collective_id, has_side_effects=True),
        cost_estimate=cost(0, 25e6),
        name="pair_gather",
    )(own.reshape(split), other.reshape(split))
    return whole.reshape(HEADS * count, width)


def to_far(rows):
    return lax.ppermute(rows, "head", [(i, (i + 2) % HEADS) for i in range(HEADS)])


def ring(axis):
    me, size = lax.axis_index(axis), lax.axis_size(axis)
    ahead = [lax.rem(me + k, size) for k in range(1, size)]
    behind = [lax.rem(me + size - k, size) for k in range(1, size)]
    return me, ahead, behind


def reach_out(src, dst, send, recv, peer):
    return pltpu.make_async_remote_copy(
        src_ref=src, dst_ref=dst, send_sem=send, recv_sem=recv, device_id=peer, device_id_type=MESH
    )


def greet_all(peers):
    barrier = pltpu.get_barrier_semaphore()
    for peer in peers:
        pl.semaphore_signal(barrier, inc=1, device_id=peer, device_id_type=MESH)
    pl.semaphore_wait(barrier, len(peers))


def start_kernel(
    tokens, cotangents, value, output, query, key, extra, tables, picks, order,
    rows, grads, full, routes, chosen_rows, orders, weights, own_sem, *sems
):
    sems = iter(sems)

    def pair():
        return next(sems), next(sems)

    group, groups_ahead, _ = ring("group")
    level, levels_ahead, levels_behind = ring("level")
    head = lax.axis_index("head")
    near, far = partners(head)
    mates = [near, far, HEADS - 1 - head]
    for to in range(HEADS):
        at = 0
        for part in (value, output, query, key):
            size = part.shape[1] // HEADS
            weights[to, :, at : at + size] = part[:, to * size : (to + 1) * size]
            at += size
        weights[to, :, at:] = extra[to]
    greet_all(
        [{"head": m} for m in mates]
        + [{"level": n} for n in levels_ahead]
        + [{"group": n} for n in groups_ahead]
    )
    started = []

    def send(src, dst, send_sem, recv_sem, peer):
        copy = reach_out(src, dst, send_sem, recv_sem, peer)
        copy.start()
        started.append(copy)
        return copy

    out_s, out_r = pair()
    pick_s, pick_r = pair()
    crossing, picking = [], []
    for k, to in enumerate(levels_ahead):
        peer = {"level": to}
        crossing.append(send(tokens.at[to], rows.at[:, head, level], out_s.at[k], out_r.at[k], peer))
    mate_s, mate_r = pair()
    table_s, table_r = pair()
    order_s, order_r = pair()
    to_mates, order_mates, table_mates = [], [], []
    for k, to in enumerate(mates):
        peer = {"head": to}
        to_mates.append(
            send(weights.at[to], full.at[group, level, head], mate_s.at[k], mate_r.at[k], peer)
        )
        order_mates.append(
            send(order, orders.at[level, head], order_s.at[k], order_r.at[k], peer)
        )
    own = [
        (tokens.at[level], rows.at[:, head, level]),
        (weights.at[head], full.at[group, level, head]),
        (tables.at[head], routes.at[head]),
        (picks.at[level], chosen_rows.at[level]),
        (order, orders.at[level, head]),
        (cotangents.at[level], grads.at[:, level]),
    ]
    own = [pltpu.make_async_copy(src, dst, own_sem.at[i]) for i, (src, dst) in enumerate(own)]
    for copy in own:
        copy.start()
    far_s, far_r = pair()
    near_s, near_r = pair()
    pass_s, pass_r = pair()
    to_far, to_near = [], []

    def share(k, src, source):
        place = rows.at[:, head, source]
        to_far.append(send(src, place, far_s.at[k], far_r.at[k], {"head": far}))
        to_near.append(send(src, place, near_s.at[k], near_r.at[k], {"head": near}))

    share(0, tokens.at[level], level)
    block_s, block_r = pair()
    group_s, group_r = pair()
    orders_s, orders_r = pair()
    for copy in to_mates:
        copy.wait_recv()
    own[1].wait()
    blocks, grouped, ordered = [], [], []

    def to_groups(j, source):
        for k, to in enumerate(groups_ahead):
            block = full.at[group, source]
            grouped.append(
                send(block, block, group_s.at[k, j], group_r.at[k, j], {"group": to})
            )

    for k, to in enumerate(levels_ahead):
        block = full.at[group, level]
        blocks.append(send(block, block, block_s.at[k], block_r.at[k], {"level": to}))
    to_groups(0, level)
    for k, to in enumerate(mates):
        table_mates.append(
            send(tables.at[to], routes.at[head], table_s.at[k], table_r.at[k], {"head": to})
        )
    for k, to in enumerate(levels_ahead):
        picking.append(
            send(picks.at[to], chosen_rows.at[level], pick_s.at[k], pick_r.at[k], {"level": to})
        )
    for copy in order_mates:
        copy.wait_recv()
    own[4].wait()
    for k, to in enumerate(levels_ahead):
        block = orders.at[level]
        ordered.append(send(block, block, orders_s.at[k], orders_r.at[k], {"level": to}))
    for k, source in enumerate(levels_behind):
        crossing[k].wait_recv()
        share(k + 1, rows.at[:, head, source], source)
    grad_s, grad_r = pair()
    crossed = []
    for k, to in enumerate(levels_ahead):
        crossed.append(
            send(cotangents.at[to], grads.at[:, level], grad_s.at[k], grad_r.at[k], {"level": to})
        )
    for k, source in enumerate(levels_behind):
        blocks[k].wait_recv()
        to_groups(k + 1, source)
    passed = []
    for k, source in enumerate([level] + levels_behind):
        to_far[k].wait_recv()
        place = rows.at[:, far, source]
        passed.append(send(place, place, pass_s.at[k], pass_r.at[k], {"head": near}))
    for copy in to_near + passed + grouped + table_mates + picking + ordered + crossed:
        copy.wait_recv()
    for copy in started:
        copy.wait_send()
    for i in (0, 2, 3, 5):
        own[i].wait()


def start(tokens, cotangents, weights, extra, tables, picks, order):
    groups, levels = lax.axis_size("group"), lax.axis_size("level")
    _, _, piece, width = tokens.shape
    columns = sum(part.shape[1] for part in weights) // HEADS + extra.shape[2]
    block = extra.shape[:2] + (columns,)
    shapes = [
        jax.ShapeDtypeStruct((HEADS, HEADS, levels, piece, width), tokens.dtype),
        jax.ShapeDtypeStruct((HEADS, levels, piece, width), tokens.dtype),
        jax.ShapeDtypeStruct((groups, levels) + block, extra.dtype),
        jax.ShapeDtypeStruct(tables.shape, tables.dtype),
        jax.ShapeDtypeStruct(picks.shape, picks.dtype),
        jax.ShapeDtypeStruct((levels, HEADS) + order.shape, order.dtype),
    ]
    dma = pltpu.SemaphoreType.DMA
    others, mates = (levels - 1,), (HEADS - 1,)
    counts = [others] * 2 + [mates] * 3 + [(levels,)] * 3
    counts += [others, (groups - 1, levels), others, others]
    return pl.pallas_call(
        start_kernel,
        out_shape=shapes,
        in_specs=[pl.BlockSpec(memory_space=pltpu.VMEM)] * 10,
        out_specs=[pl.BlockSpec(memory_space=pl.ANY)] * 6,
        scratch_shapes=[pltpu.VMEM(block, extra.dtype), dma((6,))] + [dma(c) for c in counts for _ in range(2)],
        compiler_params=pltpu.CompilerParams(collective_id=9, has_side_effects=True),
        cost_estimate=cost(0, 200e6),
        name="start",
    )(tokens, cotangents, *weights, extra, tables, picks, order)


def finish_kernel(layout, *refs):
    refs = iter(refs)
    count = len(layout)

    def take(n):
        return [next(refs) for _ in range(n)]

    part, middle = take(2)
    grads = take(count)
    (home_grad,) = take(1)
    results = [take(len(pieces)) for pieces in layout]
    near_buf, send_buf, far_buf, total, back_buf, came_buf = take(6)
    group_buf, level_send, level_buf, head_send, owned = (take(count) for _ in range(5))

    def pair():
        return next(refs), next(refs)

    group, groups_ahead, _ = ring("group")
    level, levels_ahead, levels_behind = ring("level")
    head = lax.axis_index("head")
    near, far = partners(head)
    across = HEADS - 1 - head
    mates = [near, far, across]
    greet_all(
        [{"head": m} for m in mates]
        + [{"level": n} for n in levels_ahead]
        + [{"group": n} for n in groups_ahead]
    )
    started = []

    def send(src, dst, send_sem, recv_sem, peer):
        copy = reach_out(src, dst, send_sem, recv_sem, peer)
        copy.start()
        started.append(copy)
        return copy

    pieces = range(HEADS)
    sets = range(count)
    near_s, near_r = pair()
    far_s, far_r = pair()
    back_s, back_r = pair()
    group_s, group_r = pair()
    level_s, level_r = pair()
    mate_s, mate_r = pair()
    first, second, onward = [], [], []
    for slot, (dest, copies) in enumerate(((across, first), (near, second))):
        for i in pieces:
            copies.append(
                send(
                    part.at[i, dest],
                    near_buf.at[slot, i],
                    near_s.at[slot, i],
                    near_r.at[slot, i],
                    {"head": near},
                )
            )
    order = levels_ahead + [level]
    grouped = {}
    for j, dest in enumerate(order):
        for p in sets:
            grouped[j, p] = [
                send(
                    grads[p].at[to, dest],
                    group_buf[p].at[k, j],
                    group_s.at[p, k, j],
                    group_r.at[p, k, j],
                    {"group": to},
                )
                for k, to in enumerate(groups_ahead)
            ]
    for i in pieces:
        first[i].wait_recv()
        both = part[i, far].astype(jnp.float32) + near_buf[0, i].astype(jnp.float32)
        send_buf[i] = both.astype(jnp.bfloat16)
        onward.append(send(send_buf.at[i], far_buf.at[i], far_s.at[i], far_r.at[i], {"head": far}))
    for i in pieces:
        second[i].wait_recv()
        both = part[i, head].astype(jnp.float32) + near_buf[1, i].astype(jnp.float32)
        total[i] = both + middle[i]
    leveled = {}
    for j, dest in enumerate(order):
        for p in sets:
            amount = grads[p][group, dest].astype(jnp.float32)
            for k, copy in enumerate(grouped[j, p]):
                copy.wait_recv()
                amount = amount + group_buf[p][k, j].astype(jnp.float32)
            level_send[p][j] = amount.astype(jnp.bfloat16)
            if j < len(levels_ahead):
                leveled[j, p] = send(
                    level_send[p].at[j],
                    level_buf[p].at[j],
                    level_s.at[p, j],
                    level_r.at[p, j],
                    {"level": dest},
                )
    for i in pieces:
        onward[i].wait_recv()
        both = total[i] + far_buf[i].astype(jnp.float32)
        back_buf[i] = both.astype(jnp.bfloat16).reshape(back_buf.shape[1:])
    backs = [
        send(back_buf.at[:, to], came_buf.at[level], back_s.at[k], back_r.at[k], {"level": to})
        for k, to in enumerate(levels_ahead)
    ]
    sharing = []
    for p in sets:
        amount = level_send[p][len(levels_ahead)].astype(jnp.float32)
        for j in range(len(levels_ahead)):
            leveled[j, p].wait_recv()
            amount = amount + level_buf[p][j].astype(jnp.float32)
        head_send[p][...] = amount.astype(jnp.bfloat16)
        sharing += [
            send(
                head_send[p].at[to],
                owned[p].at[head],
                mate_s.at[p, k],
                mate_r.at[p, k],
                {"head": to},
            )
            for k, to in enumerate(mates)
        ]
        owned[p][head] = head_send[p][head]
    home_grad[level] = back_buf[:, level].astype(jnp.float32)
    for k, source in enumerate(levels_behind):
        backs[k].wait_recv()
        home_grad[source] = came_buf[source].astype(jnp.float32)
    for copy in sharing:
        copy.wait_recv()
    for p in sets:
        for out, (first_column, size, joined) in zip(results[p], layout[p]):
            for h in range(HEADS):
                value = owned[p][h, :, first_column : first_column + size].astype(jnp.float32)
                if joined:
                    out[:, h * size : (h + 1) * size] = value
                else:
                    out[h] = value
    for copy in started:
        copy.wait_send()


def finish(layout, part, middle, *grads):
    groups, levels = lax.axis_size("group"), lax.axis_size("level")
    _, count, width = middle.shape
    piece = count // levels
    low_type = jnp.bfloat16
    blocks = [grad.shape[2:] for grad in grads]
    sets = len(grads)
    dma = pltpu.SemaphoreType.DMA
    counts = [(2, HEADS), (HEADS,), (levels - 1,)]
    counts += [(sets, groups - 1, levels), (sets, levels - 1), (sets, HEADS - 1)]
    vmem = pl.BlockSpec(memory_space=pltpu.VMEM)
    shapes = []
    for pieces in layout:
        for _, size, joined in pieces:
            shape = (blocks[0][1], HEADS * size) if joined else (HEADS, blocks[0][1], size)
            shapes.append(jax.ShapeDtypeStruct(shape, jnp.float32))
    return pl.pallas_call(
        functools.partial(finish_kernel, layout),
        out_shape=[jax.ShapeDtypeStruct((levels, HEADS, piece, width), jnp.float32)] + shapes,
        in_specs=[vmem] * (2 + sets),
        out_specs=[vmem] * (1 + len(shapes)),
        scratch_shapes=[
            pltpu.VMEM((2, HEADS, count, width), low_type),
            pltpu.VMEM((HEADS, count, width), low_type),
            pltpu.VMEM((HEADS, count, width), low_type),
            pltpu.VMEM((HEADS, count, width), jnp.float32),
            pltpu.VMEM((HEADS, levels, piece, width), low_type),
            pltpu.VMEM((levels, HEADS, piece, width), low_type),
        ]
        + [pltpu.VMEM((groups - 1, levels) + block, low_type) for block in blocks]
        + [pltpu.VMEM((levels,) + block, low_type) for block in blocks]
        + [pltpu.VMEM((levels - 1,) + block, low_type) for block in blocks]
        + [pltpu.VMEM(block, low_type) for block in blocks] * 2
        + [dma(c) for c in counts for _ in range(2)],
        compiler_params=pltpu.CompilerParams(
            collective_id=10, has_side_effects=True, vmem_limit_bytes=56 * 2**20
        ),
        cost_estimate=cost(0, 200e6),
        name="finish",
    )(part, middle, *grads)


BLOCK = 512
LOG2E = 1.4426950408889634


def dot(left_side, right_side, left_dim, right_dim):
    return lax.dot_general(
        left_side,
        right_side,
        (((left_dim,), (right_dim,)), ((), ())),
        preferred_element_type=jnp.float32,
    )


def attend_kernel(parts, first, q, *refs):
    keys, values = refs[:parts], refs[parts : 2 * parts]
    pos_q, start_q, pos_k, out, lse, top, total, acc = refs[2 * parts :]
    at = pl.program_id(0)
    blocks = pl.num_programs(0)
    rate = LOG2E * DH ** (-0.5)
    top[...] = jnp.full_like(top, -1e30)
    total[...] = jnp.zeros_like(total)
    acc[...] = jnp.zeros_like(acc)
    query = q[...]
    row_at, row_from = pos_q[0], start_q[0]

    for part in range(parts):

        def step(block, carry, k=keys[part], v=values[part], part=part):
            rows = pl.ds(pl.multiple_of(block * BLOCK, BLOCK), BLOCK)
            spot = pl.ds(pl.multiple_of((part * blocks + block) * BLOCK, BLOCK), BLOCK)
            scores = dot(k[rows, :], query, 1, 1)
            key_at = pos_k[spot, :]
            scores = jnp.where((key_at >= row_from) & (key_at <= row_at), scores, -1e30)
            old = top[...]
            new = jnp.maximum(old, jnp.max(scores, axis=0, keepdims=True))
            shrink = jnp.exp2((old - new) * rate)
            weight = jnp.exp2((scores - new) * rate)
            total[...] = total[...] * shrink + jnp.sum(weight, axis=0, keepdims=True)
            acc[...] = acc[...] * shrink + dot(v[rows, :], weight.astype(jnp.bfloat16), 0, 0)
            top[...] = new
            return carry

        begin = jnp.maximum(first[at] - part * blocks, 0)
        end = at + 1 if part == parts - 1 else blocks
        lax.fori_loop(begin, end, step, 0)
    out[...] = (acc[...] / total[...]).T
    lse[0] = top[...] * rate + jnp.log2(total[...])


def attend(first, queries, window, pos_q, start_q, pos_k):
    rows = queries.shape[0]
    parts = len(window)
    line = pl.BlockSpec((1, 1, BLOCK), lambda i, *_: (i, 0, 0))
    grid_spec = pltpu.PrefetchScalarGridSpec(
        num_scalar_prefetch=1,
        grid=(rows // BLOCK,),
        in_specs=[pl.BlockSpec((BLOCK, DH), lambda i, *_: (i, 0))]
        + [pl.BlockSpec((rows, DH), lambda i, *_: (0, 0))] * parts
        + [pl.BlockSpec((rows, DH), lambda i, *_: (0, 1))] * parts
        + [line, line, pl.BlockSpec((parts * rows, 1), lambda i, *_: (0, 0))],
        out_specs=[pl.BlockSpec((BLOCK, DH), lambda i, *_: (i, 0)), line],
        scratch_shapes=[
            pltpu.VMEM((1, BLOCK), jnp.float32),
            pltpu.VMEM((1, BLOCK), jnp.float32),
            pltpu.VMEM((DH, BLOCK), jnp.float32),
        ],
    )
    return pl.pallas_call(
        functools.partial(attend_kernel, parts),
        grid_spec=grid_spec,
        out_shape=[
            jax.ShapeDtypeStruct((rows, DH), jnp.float32),
            jax.ShapeDtypeStruct((rows // BLOCK, 1, BLOCK), jnp.float32),
        ],
        compiler_params=pltpu.CompilerParams(vmem_limit_bytes=48 * 2**20),
        cost_estimate=cost(2e10, 1e7),
        name="attend",
    )(first, queries, *window, *window, pos_q, start_q, pos_k)


def attend_back_kernel(parts, first, q, *refs):
    keys, values = refs[:parts], refs[parts : 2 * parts]
    grad, pos_q, start_q, lse, inner, pos_k, grad_q = refs[2 * parts : 2 * parts + 7]
    grads = refs[2 * parts + 7 : 3 * parts + 7]
    sum_k, sum_v, acc = refs[3 * parts + 7 :]
    at = pl.program_id(0)
    blocks = pl.num_programs(0)
    rate = LOG2E * DH ** (-0.5)
    scale = DH ** (-0.5)

    @pl.when(at == 0)
    def _():
        sum_k[...] = jnp.zeros_like(sum_k)
        sum_v[...] = jnp.zeros_like(sum_v)

    acc[...] = jnp.zeros_like(acc)
    query, grad_out = q[...], grad[...]
    row_at, row_from, row_lse, row_inner = pos_q[0], start_q[0], lse[0], inner[0]

    for part in range(parts):

        def step(block, carry, k=keys[part], v=values[part], part=part):
            rows = pl.ds(pl.multiple_of(block * BLOCK, BLOCK), BLOCK)
            spot = pl.ds(pl.multiple_of((part * blocks + block) * BLOCK, BLOCK), BLOCK)
            key, value = k[rows, :], v[rows, :]
            scores = dot(key, query, 1, 1)
            key_at = pos_k[spot, :]
            seen = (key_at >= row_from) & (key_at <= row_at)
            soft = jnp.where(seen, jnp.exp2(scores * rate - row_lse), 0.0)
            grad_soft = dot(value, grad_out, 1, 1)
            grad_scores = (soft * (grad_soft - row_inner)).astype(jnp.bfloat16)
            sum_v[spot, :] += dot(soft.astype(jnp.bfloat16), grad_out, 1, 0)
            sum_k[spot, :] += dot(grad_scores, query, 1, 0)
            acc[...] += dot(grad_scores, key, 0, 0)
            return carry

        begin = jnp.maximum(first[at] - part * blocks, 0)
        end = at + 1 if part == parts - 1 else blocks
        lax.fori_loop(begin, end, step, 0)
    grad_q[...] = (acc[...] * scale).astype(jnp.bfloat16)

    @pl.when(at == blocks - 1)
    def _():
        size = grads[0].shape[0]
        for part in range(parts):
            spot = slice(part * size, (part + 1) * size)
            grads[part][:, :DH] = (sum_k[spot, :] * scale).astype(grads[part].dtype)
            grads[part][:, DH:] = sum_v[spot, :].astype(grads[part].dtype)


def attend_back(first, queries, window, grads, pos_q, start_q, lse, inner, pos_k):
    rows = queries.shape[0]
    parts = len(window)
    block = pl.BlockSpec((BLOCK, DH), lambda i, *_: (i, 0))
    line = pl.BlockSpec((1, 1, BLOCK), lambda i, *_: (i, 0, 0))
    grid_spec = pltpu.PrefetchScalarGridSpec(
        num_scalar_prefetch=1,
        grid=(rows // BLOCK,),
        in_specs=[block]
        + [pl.BlockSpec((rows, DH), lambda i, *_: (0, 0))] * parts
        + [pl.BlockSpec((rows, DH), lambda i, *_: (0, 1))] * parts
        + [block, line, line, line, line]
        + [pl.BlockSpec((parts * rows, 1), lambda i, *_: (0, 0))],
        out_specs=[block] + [pl.BlockSpec((rows, 2 * DH), lambda i, *_: (0, 0))] * parts,
        scratch_shapes=[
            pltpu.VMEM((parts * rows, DH), jnp.float32),
            pltpu.VMEM((parts * rows, DH), jnp.float32),
            pltpu.VMEM((BLOCK, DH), jnp.float32),
        ],
    )
    kinds = [jnp.bfloat16] * (parts - 1) + [jnp.float32]
    return pl.pallas_call(
        functools.partial(attend_back_kernel, parts),
        grid_spec=grid_spec,
        out_shape=[jax.ShapeDtypeStruct((rows, DH), jnp.bfloat16)]
        + [jax.ShapeDtypeStruct((rows, 2 * DH), kind) for kind in kinds],
        compiler_params=pltpu.CompilerParams(vmem_limit_bytes=48 * 2**20),
        cost_estimate=cost(2e9, 1e6),
        name="attend_back",
    )(first, queries, *window, *window, grads, pos_q, start_q, lse, inner, pos_k)


def columns_of(ref, group, groups, step, depth):
    at = lax.rem(group + step + groups, groups) * depth
    return ref.at[:, pl.ds(pl.multiple_of(at, 128), depth)]


def front_kernel(groups, local, place, hidden, grads, *refs):
    w_in, w_out = refs[0], refs[1 : groups + 1]
    gates, active, grad_pre, rows_out, turned, acc = refs[groups + 1 :]
    levels, _, depth, width = w_in.shape
    tile = hidden.shape[0]
    model = groups * depth
    parts = [slice(step * depth, (step + 1) * depth) for step in range(groups)]
    for step in range(groups):
        turned[0, :, parts[step]] = columns_of(hidden, place[1], groups, -step, depth)[...]
        turned[1, :, parts[step]] = columns_of(grads, place[1], groups, -step, depth)[...]
    gate_grads = []
    for level in range(levels):
        pre_act = jnp.zeros((tile, width), jnp.float32)
        grad_active = jnp.zeros((tile, width), jnp.float32)
        for step in range(groups):
            pre_act += dot(turned[0, :, parts[step]], w_in[level, step], 1, 0)
            grad_active += dot(turned[1, :, parts[step]], w_out[step][level], 1, 0)
        first = level * local
        gate = jnp.concatenate(
            [jnp.broadcast_to(gates[:, first + e : first + e + 1], (tile, FH)) for e in range(local)],
            axis=1,
        )
        sig = 1.0 / (1.0 + jnp.exp2(-LOG2E * pre_act))
        act_pre = pre_act * sig
        columns = slice(level * width, (level + 1) * width)
        active[:, columns] = (act_pre * gate).astype(jnp.bfloat16)
        product = grad_active * act_pre
        for e in range(local):
            gate_grads.append(
                jnp.sum(product[:, e * FH : (e + 1) * FH], axis=1, keepdims=True)
            )
        slope = sig * (1.0 + pre_act * (1.0 - sig))
        low_pre = (grad_active * gate * slope).astype(jnp.bfloat16)
        grad_pre[:, columns] = low_pre
        for step in range(groups):
            back = dot(low_pre, w_in[level, step], 1, 1)
            acc[:, parts[step]] = back if level == 0 else acc[:, parts[step]] + back
    for step in range(groups):
        columns_of(rows_out, place[1], groups, -step, depth)[...] = acc[:, parts[step]].astype(
            jnp.bfloat16
        )
    spare = rows_out.shape[1] - model
    lane = lax.broadcasted_iota(jnp.int32, (tile, spare), 1) - place[0] * (levels * local)
    spread = jnp.zeros((tile, spare), jnp.float32)
    for e, column in enumerate(gate_grads):
        spread = jnp.where(lane == e, column, spread)
    rows_out[:, model:] = spread.astype(jnp.bfloat16)


def ffn_front(place, hidden, grads, w_in, w_out, gates, local):
    rows, wide = hidden.shape
    levels, groups, depth, width = w_in.shape
    tile = 512

    def by_row(columns):
        return pl.BlockSpec((tile, columns), lambda i, *_: (i, 0))

    once = pl.Buffered(1)
    whole = pl.BlockSpec(w_out[0].shape, lambda i, *_: (0, 0, 0), pipeline_mode=once)
    stacked = pl.BlockSpec(w_in.shape, lambda i, *_: (0, 0, 0, 0), pipeline_mode=once)
    grid_spec = pltpu.PrefetchScalarGridSpec(
        num_scalar_prefetch=1,
        grid=(rows // tile,),
        in_specs=[by_row(wide), by_row(groups * depth)]
        + [stacked]
        + [whole] * groups
        + [by_row(gates.shape[1])],
        out_specs=[by_row(levels * width), by_row(levels * width), by_row(wide)],
        scratch_shapes=[
            pltpu.VMEM((2, tile, groups * depth), jnp.bfloat16),
            pltpu.VMEM((tile, groups * depth), jnp.float32),
        ],
    )
    hidden_units = jax.ShapeDtypeStruct((rows, levels * width), jnp.bfloat16)
    return pl.pallas_call(
        functools.partial(front_kernel, groups, local),
        grid_spec=grid_spec,
        out_shape=[hidden_units, hidden_units, jax.ShapeDtypeStruct((rows, wide), jnp.bfloat16)],
        compiler_params=pltpu.CompilerParams(vmem_limit_bytes=58 * 2**20),
        cost_estimate=cost(6 * rows * groups * depth * levels * width, 3e7),
        name="ffn_front",
    )(place, hidden, grads, w_in, *w_out, gates)


def rear_kernel(groups, place, rows_in, hidden_units, *weight_grads):
    _, depth, _ = weight_grads[0].shape
    units = hidden_units[...]
    for step in range(groups):
        part = columns_of(rows_in, place[1], groups, step, depth)
        weight_grads[step][0] = dot(part[...], units, 0, 0).astype(jnp.bfloat16)


def feed_kernel(groups, place, active, *refs):
    weights = refs[:groups]
    feed, acc = refs[groups:]
    _, depth, _ = weights[0].shape
    level = pl.program_id(0)
    act = active[...]
    for step in range(groups):
        fed = dot(act, weights[step][0], 1, 1)
        part = slice(step * depth, (step + 1) * depth)

        @pl.when(level == 0)
        def _():
            acc[:, part] = fed

        @pl.when(level > 0)
        def _():
            acc[:, part] += fed

    @pl.when(level == pl.num_programs(0) - 1)
    def _():
        for step in range(groups):
            part = slice(step * depth, (step + 1) * depth)
            columns_of(feed, place[1], groups, -step, depth)[...] = acc[:, part].astype(
                jnp.bfloat16
            )


def whole_rows(rows, columns):
    return pl.BlockSpec((rows, columns), lambda i, *_: (0, 0), pipeline_mode=pl.Buffered(1))


def ffn_feed(place, active, weights):
    rows = active.shape[0]
    groups = len(weights)
    levels, depth, width = weights[0].shape
    return pl.pallas_call(
        functools.partial(feed_kernel, groups),
        grid_spec=pltpu.PrefetchScalarGridSpec(
            num_scalar_prefetch=1,
            grid=(levels,),
            in_specs=[pl.BlockSpec((rows, width), lambda i, *_: (0, i))]
            + [pl.BlockSpec((1, depth, width), lambda i, *_: (i, 0, 0))] * groups,
            out_specs=whole_rows(rows, groups * depth),
            scratch_shapes=[pltpu.VMEM((rows, groups * depth), jnp.float32)],
        ),
        out_shape=jax.ShapeDtypeStruct((rows, groups * depth), jnp.bfloat16),
        compiler_params=pltpu.CompilerParams(vmem_limit_bytes=58 * 2**20),
        cost_estimate=cost(1e3, 1e3),
        name="ffn_feed",
    )(place, active, *weights)


def ffn_rear(place, rows_in, units, model, groups, levels):
    rows, wide = rows_in.shape
    width = units.shape[1] // levels
    depth = model // groups
    return pl.pallas_call(
        functools.partial(rear_kernel, groups),
        grid_spec=pltpu.PrefetchScalarGridSpec(
            num_scalar_prefetch=1,
            grid=(levels,),
            in_specs=[
                whole_rows(rows, wide),
                pl.BlockSpec((rows, width), lambda i, *_: (0, i)),
            ],
            out_specs=[pl.BlockSpec((1, depth, width), lambda i, *_: (i, 0, 0))] * groups,
        ),
        out_shape=[jax.ShapeDtypeStruct((levels, depth, width), jnp.bfloat16)] * groups,
        compiler_params=pltpu.CompilerParams(vmem_limit_bytes=58 * 2**20),
        cost_estimate=cost(1e3, 1e3),
        name="ffn_rear",
    )(place, rows_in, units)


def named_by(routes, count):
    lane = lax.broadcasted_iota(jnp.int32, (routes.shape[0], count), 1)
    member = jnp.zeros(lane.shape, jnp.float32)
    for slot in range(routes.shape[1]):
        member = jnp.where(lane == routes[:, slot : slot + 1], 1.0, member)
    return member


def middle_kernel(rows, branch, routes, router, gain, bias, middle, extended, sig_out):
    experts = router.shape[1]
    width = rows.shape[1]
    rounded = branch[...].astype(jnp.bfloat16).astype(jnp.float32)
    value = rows[...].astype(jnp.float32) + rounded
    middle[...] = value
    _, _, normed = normalized(value, gain[...], bias[...])
    sig = 1.0 / (1.0 + jnp.exp2(-LOG2E * dot(normed, router[...], 1, 0)))
    sig_out[...] = sig
    extended[:, :width] = value.astype(jnp.bfloat16)
    gates = (sig * named_by(routes[...], experts)).astype(jnp.bfloat16)
    spare = extended.shape[1] - width - experts
    if spare:
        gates = jnp.concatenate([gates, jnp.zeros((gates.shape[0], spare), gates.dtype)], axis=1)
    extended[:, width:] = gates


def enter_ffn(rows, branch, routes, router, gain, bias):
    count, width = rows.shape
    experts = router.shape[1]
    wide = width + experts + -experts % 128
    return pl.pallas_call(
        middle_kernel,
        out_shape=[
            jax.ShapeDtypeStruct((count, width), jnp.float32),
            jax.ShapeDtypeStruct((count, wide), jnp.bfloat16),
            jax.ShapeDtypeStruct((count, experts), jnp.float32),
        ],
        compiler_params=pltpu.CompilerParams(vmem_limit_bytes=40 * 2**20),
        cost_estimate=cost(1e9, 1e7),
        name="middle",
    )(rows, branch, routes, router, gain, bias)


def leave_kernel(
    middle, own, came, cotangent, sigs, routes, router, gain, bias, grad_out, low_out, weight_grads
):
    experts = router.shape[1]
    count, width = middle.shape
    scaled, inverse, normed = normalized(middle[...], gain[...], bias[...])
    total = own[...] + came[...].astype(jnp.float32)
    sig = sigs[...]
    member = named_by(routes[...], experts)
    gate_grads = total[:, width : width + experts]
    logit = (gate_grads * sig * (1.0 - sig) * member).astype(jnp.bfloat16)
    second = dot(logit, router[...], 1, 1)
    inner_grad = second * gain[...]
    inner_grad = inverse * (
        inner_grad
        - jnp.mean(inner_grad, axis=1, keepdims=True)
        - scaled * jnp.mean(inner_grad * scaled, axis=1, keepdims=True)
    )
    grad = cotangent[...].astype(jnp.float32) + total[:, :width] + inner_grad
    grad_out[...] = grad
    low_out[...] = grad.astype(jnp.bfloat16)
    spare = weight_grads.shape[1] - experts
    sums = [
        jnp.sum(second * scaled, axis=0, keepdims=True),
        jnp.sum(second, axis=0, keepdims=True),
        jnp.zeros((126, width), jnp.float32),
    ]
    side = jnp.concatenate(sums, axis=0).T[:, :spare]
    both = jnp.concatenate([dot(normed, logit, 0, 0), side], axis=1)
    weight_grads[...] = both.astype(jnp.bfloat16)


def leave_ffn(middle, own, came, cotangent, sigs, routes, router, gain, bias):
    count, width = middle.shape
    experts = router.shape[1]
    columns = experts + 2 + -(experts + 2) % 128
    return pl.pallas_call(
        leave_kernel,
        out_shape=[
            jax.ShapeDtypeStruct((count, width), jnp.float32),
            jax.ShapeDtypeStruct((count, width), jnp.bfloat16),
            jax.ShapeDtypeStruct((width, columns), jnp.bfloat16),
        ],
        compiler_params=pltpu.CompilerParams(vmem_limit_bytes=48 * 2**20),
        cost_estimate=cost(1e9, 1e7),
        name="leave_ffn",
    )(middle, own, came, cotangent, sigs, routes, router, gain, bias)


def branch_back_kernel(
    grads, w_output, attended, sigs, masks, grad_attended, inner, out_logit, weight_grads, acc
):
    at = pl.program_id(0)
    count = grads.shape[0]
    sig, mask, values = sigs[...], masks[...], attended[...]
    mixed_grad = dot(grads[...], w_output[...], 1, 0)
    lane = lax.broadcasted_iota(jnp.int32, (count, 128), 1)
    logits = jnp.zeros((count, 128), jnp.float32)
    total = jnp.zeros((count, DH), jnp.float32)
    parts = []
    for e in range(VEXP):
        k = VEXP + e
        one, on = sig[:, k : k + 1], mask[:, k : k + 1]
        part = mixed_grad[:, e * DH : (e + 1) * DH]
        total += part * (one * on)
        gate_grad = jnp.sum(part * values, axis=1, keepdims=True)
        logits = jnp.where(lane == k, gate_grad * one * (1.0 - one) * on, logits)
        parts.append((one * on * values).astype(jnp.bfloat16))
    out_logit[...] = logits.astype(jnp.bfloat16)
    rounded = total.astype(jnp.bfloat16)
    grad_attended[...] = rounded
    product = rounded.astype(jnp.float32) * values
    inner[0] = jnp.sum(product.T, axis=0, keepdims=True)
    amount = dot(grads[...], jnp.concatenate(parts, axis=1), 0, 0)

    @pl.when(at == 0)
    def _():
        acc[...] = amount

    @pl.when(at > 0)
    def _():
        acc[...] += amount

    @pl.when(at == pl.num_programs(0) - 1)
    def _():
        weight_grads[...] = acc[...].astype(jnp.bfloat16)


def branch_back(grads, full, attended, sigs, masks):
    rows, width = grads.shape
    values = VEXP * DH

    def by_row(size):
        return pl.BlockSpec((BLOCK, size), lambda i: (i, 0))

    return pl.pallas_call(
        branch_back_kernel,
        grid=(rows // BLOCK,),
        in_specs=[
            by_row(width),
            pl.BlockSpec((width, values), lambda i: (0, 1), pipeline_mode=pl.Buffered(1)),
            by_row(DH),
            by_row(128),
            by_row(16),
        ],
        out_specs=[
            by_row(DH),
            pl.BlockSpec((1, 1, BLOCK), lambda i: (i, 0, 0)),
            by_row(128),
            pl.BlockSpec((width, values), lambda i: (0, 0)),
        ],
        out_shape=[
            jax.ShapeDtypeStruct((rows, DH), jnp.bfloat16),
            jax.ShapeDtypeStruct((rows // BLOCK, 1, BLOCK), jnp.float32),
            jax.ShapeDtypeStruct((rows, 128), jnp.bfloat16),
            jax.ShapeDtypeStruct((width, values), jnp.bfloat16),
        ],
        scratch_shapes=[pltpu.VMEM((width, values), jnp.float32)],
        compiler_params=pltpu.CompilerParams(vmem_limit_bytes=48 * 2**20),
        cost_estimate=cost(1e8, 1e6),
        name="branch_back",
    )(grads, full, attended, sigs, masks)


def turn(value, axis, by):
    size = lax.axis_size(axis)
    return lax.ppermute(value, axis, [(i, (i + by) % size) for i in range(size)])


def normalized(rows, gain, bias):
    values = rows.astype(jnp.float32)
    centred = values - jnp.mean(values, axis=1, keepdims=True)
    inverse = lax.rsqrt(jnp.mean(centred * centred, axis=1, keepdims=True) + 1e-05)
    scaled = centred * inverse
    return scaled, inverse, (scaled * gain + bias).astype(jnp.bfloat16)


def project_kernel(
    levels, rows, w_value, w_query, w_key, routers, gain, bias, order, tables,
    query, key_value, projected, sigs, masks,
):
    count = rows.shape[0]
    piece = count // (levels * HEADS)
    _, _, normed = normalized(rows[...], gain[...], bias[...])
    query[...] = dot(normed, w_query[...], 1, 0).astype(jnp.bfloat16)
    key_value[:, :DH] = dot(normed, w_key[...], 1, 0).astype(jnp.bfloat16)
    sig = 1.0 / (1.0 + jnp.exp2(-LOG2E * dot(normed, routers[...], 1, 0)))
    sigs[...] = sig
    product = dot(rows[...], w_value[...], 1, 0)
    projected[...] = product
    at = lax.broadcasted_iota(jnp.int32, (count, count), 0)
    source = lax.rem(at // piece, levels) * HEADS + at // (piece * levels)
    here = (source * piece + lax.rem(at, piece) == order[0]).astype(jnp.bfloat16)
    lane = lax.broadcasted_iota(jnp.int32, (16, count), 0)
    table = tables[0]
    named = jnp.zeros((16, count), jnp.float32)
    for which in range(2):
        option = lane - which * VEXP
        for slot in range(2):
            pick = table[2 * which + slot : 2 * which + slot + 1, :]
            hit = (option == pick) & (option >= 0) & (option < VEXP)
            named = jnp.where(hit, 1.0, named)
    mask = dot(here, named.astype(jnp.bfloat16), 1, 1)
    masks[...] = mask
    value = jnp.zeros((count, DH), jnp.float32)
    for e in range(VEXP):
        gate = sig[:, e : e + 1] * mask[:, e : e + 1]
        value += gate * product[:, e * DH : (e + 1) * DH]
    key_value[:, DH:] = value.astype(jnp.bfloat16)


def project(rows, full, gain, bias, orders, tables, levels):
    total, width = rows.shape
    count = total // HEADS

    def by_row(columns):
        return pl.BlockSpec((count, columns), lambda i: (i, 0))

    def column(size, at):
        return pl.BlockSpec((width, size), lambda i: (0, at), pipeline_mode=pl.Buffered(1))

    line = pl.BlockSpec((1, width), lambda i: (0, 0))
    shapes = [(DH, jnp.bfloat16), (2 * DH, jnp.bfloat16), (VEXP * DH, jnp.float32)]
    shapes += [(128, jnp.float32), (16, jnp.float32)]
    return pl.pallas_call(
        functools.partial(project_kernel, levels),
        grid=(HEADS,),
        in_specs=[by_row(width), column(VEXP * DH, 0)]
        + [column(DH, 2 * VEXP + i) for i in range(3)]
        + [line, line]
        + [
            pl.BlockSpec((1, 1, count), lambda i: (i, 0, 0)),
            pl.BlockSpec((1,) + tables.shape[1:], lambda i: (i, 0, 0)),
        ],
        out_specs=[by_row(columns) for columns, _ in shapes],
        out_shape=[jax.ShapeDtypeStruct((total, columns), kind) for columns, kind in shapes],
        compiler_params=pltpu.CompilerParams(vmem_limit_bytes=48 * 2**20),
        cost_estimate=cost(2 * total * width * 1024, 2e7),
        name="project",
    )(rows, full, full, full, full, gain, bias, orders, tables)


def project_back_kernel(
    rows, grads, grad_query, out_logit, projected, sigs, masks,
    w_value, w_query, w_key, routers, gain, bias,
    grad_rows, weight_grads, acc, sums,
):
    at = pl.program_id(0)
    count = rows.shape[0]
    values = VEXP * DH

    @pl.when(at == 0)
    def _():
        acc[...] = jnp.zeros_like(acc)
        sums[...] = jnp.zeros_like(sums)

    scaled, inverse, normed = normalized(rows[...], gain[...], bias[...])
    grad_key = grads[:, :DH].astype(jnp.bfloat16)
    grad_value = grads[:, DH:]
    sig, mask = sigs[...], masks[...]
    lane = lax.broadcasted_iota(jnp.int32, (count, 128), 1)
    logits = out_logit[...].astype(jnp.float32)
    parts = []
    for e in range(VEXP):
        one, on = sig[:, e : e + 1], mask[:, e : e + 1]
        parts.append((one * on * grad_value).astype(jnp.bfloat16))
        inner = jnp.sum(grad_value * projected[:, e * DH : (e + 1) * DH], axis=1, keepdims=True)
        logits = jnp.where(lane == e, inner * one * (1.0 - one) * on, logits)
    grad_projected = jnp.concatenate(parts, axis=1)
    sides = jnp.concatenate([grad_query[...], grad_key, logits.astype(jnp.bfloat16)], axis=1)
    first = dot(sides[:, :DH], w_query[...], 1, 1)
    first += dot(sides[:, DH : 2 * DH], w_key[...], 1, 1)
    first += dot(sides[:, 2 * DH :], routers[...], 1, 1)
    sums[2 * VEXP : 2 * VEXP + 1, :] += jnp.sum(first * scaled, axis=0, keepdims=True)
    sums[2 * VEXP + 1 : 2 * VEXP + 2, :] += jnp.sum(first, axis=0, keepdims=True)
    inner_grad = first * gain[...]
    inner_grad = inverse * (
        inner_grad
        - jnp.mean(inner_grad, axis=1, keepdims=True)
        - scaled * jnp.mean(inner_grad * scaled, axis=1, keepdims=True)
    )
    grad_rows[...] = (inner_grad + dot(grad_projected, w_value[...], 1, 1)).astype(jnp.bfloat16)
    acc[:, :values] += dot(rows[...], grad_projected, 0, 0)
    acc[:, values:] += dot(normed, sides, 0, 0)

    @pl.when(at == pl.num_programs(0) - 1)
    def _():
        weight_grads[:, : values + 2 * DH] = acc[:, : values + 2 * DH].astype(jnp.bfloat16)
        last = acc[:, values + 2 * DH :] + sums[...].T
        weight_grads[:, values + 2 * DH :] = last.astype(jnp.bfloat16)


def project_back(rows, grads, grad_query, out_logit, projected, sigs, masks, full, gain, bias):
    total, width = rows.shape
    count = total // HEADS
    columns = VEXP * DH + 3 * DH

    def by_row(size):
        return pl.BlockSpec((count, size), lambda i: (i, 0))

    def column(size, at):
        return pl.BlockSpec((width, size), lambda i: (0, at), pipeline_mode=pl.Buffered(1))

    line = pl.BlockSpec((1, width), lambda i: (0, 0))
    return pl.pallas_call(
        project_back_kernel,
        grid=(HEADS,),
        in_specs=[by_row(width), by_row(2 * DH), by_row(DH), by_row(128), by_row(VEXP * DH)]
        + [by_row(128), by_row(16), column(VEXP * DH, 0)]
        + [column(DH, 2 * VEXP + i) for i in range(3)]
        + [line, line],
        out_specs=[by_row(width), pl.BlockSpec((width, columns), lambda i: (0, 0))],
        out_shape=[
            jax.ShapeDtypeStruct((total, width), jnp.bfloat16),
            jax.ShapeDtypeStruct((width, columns), jnp.bfloat16),
        ],
        scratch_shapes=[
            pltpu.VMEM((width, columns), jnp.float32),
            pltpu.VMEM((128, width), jnp.float32),
        ],
        compiler_params=pltpu.CompilerParams(vmem_limit_bytes=56 * 2**20),
        cost_estimate=cost(total * width * 512, 4e6),
        name="project_back",
    )(rows, grads, grad_query, out_logit, projected, sigs, masks, full, full, full, full, gain, bias)


def shift(value, axis, by):
    count = lax.axis_size(axis)
    pairs = [(i, i + by) for i in range(count) if 0 <= i + by < count]
    return lax.ppermute(value, axis, pairs)


def body(
    tokens_in,
    out_grad,
    deal_order,
    seq_lengths,
    value_routes,
    output_routes,
    ffn_routes,
    norm1_gain,
    norm1_bias,
    norm2_gain,
    norm2_bias,
    query_weight,
    key_weight,
    value_weight,
    output_weight,
    value_router,
    output_router,
    ffn_router,
    ffn_in,
    ffn_out,
):
    groups = lax.axis_size("group")
    levels = lax.axis_size("level")
    level = lax.axis_index("level")
    head = lax.axis_index("head")
    count, width = tokens_in.shape
    piece = count // (levels * HEADS)
    wrows = query_weight.shape[0]
    experts = ffn_router.shape[1]
    local_experts = ffn_in.shape[1] // FH

    small = jnp.concatenate(
        [
            ffn_router,
            norm1_gain[:, None],
            norm1_bias[:, None],
            norm2_gain[:, None],
            norm2_bias[:, None],
        ],
        axis=1,
    )
    shared = small.shape[1]
    pad = -(shared + 2 * VEXP) % 128
    extra = jnp.concatenate(
        [
            value_router.reshape(wrows, HEADS, VEXP),
            output_router.reshape(wrows, HEADS, VEXP),
            jnp.broadcast_to(small[:, None, :], (wrows, HEADS, shared)),
            jnp.zeros((wrows, HEADS, pad), jnp.bfloat16),
        ],
        axis=2,
    )
    cols = 2 * DH + 2 * VEXP * DH + extra.shape[2]
    tables = jnp.concatenate(
        [value_routes.transpose(1, 2, 0), output_routes.transpose(1, 2, 0)], axis=1
    )
    picks = ffn_routes.reshape(levels, HEADS * piece, -1).transpose(0, 2, 1)
    arrived, own_grads, full, tables, picks, orders = start(
        tokens_in.reshape(levels, HEADS, piece, width),
        out_grad.reshape(levels, HEADS, piece, width),
        [value_weight, output_weight, query_weight, key_weight],
        extra.transpose(1, 0, 2),
        tables,
        picks,
        deal_order,
    )
    worker_in = arrived.reshape(HEADS * count, width)
    own_tokens = lax.dynamic_index_in_dim(arrived, head, 1, keepdims=False).reshape(count, width)
    in_rows = [turn(ffn_in, "group", k) for k in range(1, groups)]
    full, in_rows = lax.optimization_barrier((full.reshape(width, cols), in_rows))

    base = 2 * DH + 2 * VEXP * DH
    w_output = full[:, VEXP * DH : 2 * VEXP * DH]
    at = base + 2 * VEXP
    def relabelled(expert):
        share = expert // local_experts
        return (share % HEADS * levels + share // HEADS) * local_experts + expert % local_experts

    labels = jnp.arange(experts, dtype=jnp.int32)
    moved = low(relabelled(labels)[:, None] == labels[None, :])
    r_ffn = low(
        jnp.dot(full[:, at : at + experts], moved, preferred_element_type=jnp.float32)
    )
    gain_one, bias_one, gain_two, bias_two = (
        full[:, at + experts + i].astype(jnp.float32) for i in range(4)
    )
    gain_row, bias_row = gain_one[None], bias_one[None]
    orders = orders.reshape(levels, HEADS, count)
    own_order = lax.dynamic_index_in_dim(orders, level, 0, keepdims=False)[:, None, :]
    queries, key_value, projected, sigs, masks = project(
        worker_in, full, gain_row, bias_row, own_order, tables, levels
    )

    rows = HEADS * count
    reach = -(-LMAX // rows)

    ramp = jnp.arange(count, dtype=jnp.int32)

    def arrival(values):
        lead, shape = values.shape[:-3], values.shape[-1:]
        four = values.reshape(lead + (HEADS, levels, HEADS, piece) + shape)
        return jnp.swapaxes(four, -4, -3).reshape(lead + (rows,) + shape)

    orders = jnp.concatenate([jnp.zeros((reach, HEADS, count), jnp.int32), orders], axis=0)
    orders = lax.dynamic_slice_in_dim(orders, level, reach + 1, 0)
    here = orders[:, :, None, :] == ramp[None, None, :, None]
    inverse = jnp.sum(here * ramp, axis=3)
    shard = (level - reach + jnp.arange(reach + 1, dtype=jnp.int32))[:, None] * HEADS
    shard = shard + jnp.arange(HEADS, dtype=jnp.int32)[None, :]
    pos_all = jnp.where(shard[:, :, None] < 0, -1, shard[:, :, None] * count + inverse)
    pos_all = arrival(pos_all[..., None]).reshape(-1)
    positions = pos_all[reach * rows :]
    seq_ends = jnp.cumsum(seq_lengths[0])

    def starts_of(places):
        return jnp.max(jnp.where(seq_ends <= places[:, None], seq_ends, 0), axis=1)

    starts = starts_of(positions)
    blocks = rows // BLOCK
    base_block = (level - reach) * blocks
    first_block = starts_of(level * rows + jnp.arange(blocks, dtype=jnp.int32) * BLOCK) // BLOCK
    first_block = jnp.maximum(first_block - base_block, 0)

    own_routes = picks.reshape(levels, -1, HEADS, piece).transpose(2, 0, 3, 1).reshape(count, -1)
    own_routes = relabelled(own_routes)
    ffn_side = (own_routes, r_ffn, gain_two[None], bias_two[None], own_tokens)

    window = [key_value]
    own_grads = own_grads.reshape(count, width)
    for i in range(reach):
        came = shift(window[0], "level", 1)
        if i == 0:
            came, own_grads, pos_all, starts, ffn_out, in_rows = lax.optimization_barrier(
                (came, own_grads, pos_all, starts, ffn_out, [ffn_in] + in_rows)
            )
            cotangent = level_gather(own_grads, 5, True)
        if i == reach - 1:
            came, cotangent, ffn_side = lax.optimization_barrier((came, cotangent, ffn_side))
        window.insert(0, came)
    place = jnp.stack([head, lax.axis_index("group")])
    out_here = lax.all_gather(ffn_out, "level", axis=0)
    w_in = lax.all_gather(jnp.stack(in_rows), "level", axis=0)


    def lines(values):
        return values.reshape(blocks, 1, BLOCK)

    attended, log_total = attend(
        first_block,
        queries,
        window,
        lines(positions),
        lines(starts),
        pos_all[:, None],
    )

    out_sig = sigs[:, VEXP : 2 * VEXP]
    out_mask = masks[:, VEXP : 2 * VEXP]
    out_gate = out_sig * out_mask
    attended, out_here = lax.optimization_barrier((attended, out_here))
    w_out = [out_here] + [turn(out_here, "group", k) for k in range(1, groups)]
    mixed = low((out_gate[..., None] * attended[:, None, :]).reshape(rows, VEXP * DH))
    branch = level_scatter(low(transposed(mixed, w_output)), 2)

    own_routes, r_ffn, gain_two, bias_two, own_tokens = ffn_side
    middle, extended, ffn_sig = enter_ffn(own_tokens, branch, own_routes, r_ffn, gain_two, bias_two)
    hidden = level_gather(extended, 3, True)
    mine = levels * local_experts
    gates = lax.dynamic_slice_in_dim(hidden, width + head * mine, mine, 1).astype(jnp.float32)
    active, grad_pre, grad_rows = ffn_front(
        place, hidden, cotangent, w_in, w_out, gates, local_experts
    )
    summed, beyond = pair_scatter(grad_rows, 4, True)
    beyond, hidden = lax.optimization_barrier((beyond, hidden))
    came = to_far(beyond)
    grad_in = ffn_rear(place, hidden, grad_pre, width, groups, levels)
    in_came = [turn(grad_in[k], "group", k) for k in range(1, groups)]
    grad_out = ffn_rear(place, cotangent, active, width, groups, levels)
    out_came = [turn(grad_out[k], "group", k) for k in range(1, groups)]
    came, grad_in, grad_out = lax.optimization_barrier((came, grad_in, grad_out))
    grad_middle, own_branch, early = leave_ffn(
        middle, summed, came, own_grads, ffn_sig, own_routes, r_ffn, gain_two, bias_two
    )
    came = to_far(own_branch)
    feed = ffn_feed(place, active, w_out)
    came, feed = lax.optimization_barrier((came, feed))
    grad_branch = pair_gather(own_branch, came, 7)

    def sum_of(own, others):
        total = own[0].astype(jnp.float32)
        for other in others:
            total = total + other.astype(jnp.float32)
        return low(total)

    def over_levels(total):
        return lax.psum_scatter(total, "level", scatter_dimension=0)

    grad_branch, in_came = lax.optimization_barrier((grad_branch, in_came))
    ffn_in_grad = over_levels(sum_of(grad_in, in_came))
    grad_attended, row_inner, grad_out_logit, grad_w_output = branch_back(
        grad_branch, full, attended, sigs, masks
    )
    grad_queries, *grad_window = attend_back(
        first_block,
        queries,
        window,
        grad_attended,
        lines(positions),
        lines(starts),
        log_total,
        row_inner,
        pos_all[:, None],
    )
    came = shift(grad_window[0], "level", -1)
    fed, beyond = pair_scatter(feed, 6, True)
    for i in range(1, reach + 1):
        if i < reach:
            came, fed = lax.optimization_barrier((came, fed))
        grad_both = grad_window[i].astype(jnp.float32) + came.astype(jnp.float32)
        if i < reach:
            grad_keys_sent = low(grad_both)
            came = shift(grad_keys_sent, "level", -1)
    grad_both, out_came = lax.optimization_barrier((grad_both, out_came))
    ffn_out_grad = over_levels(sum_of(grad_out, out_came))
    fed_far = to_far(beyond)
    grad_inputs, late = project_back(
        worker_in,
        grad_both,
        grad_queries,
        grad_out_logit,
        projected,
        sigs,
        masks,
        full,
        gain_row,
        bias_row,
    )

    fed_far, grad_inputs = lax.optimization_barrier((fed_far, grad_inputs))
    layer_out = to_home(low(middle + fed + fed_far.astype(jnp.float32)))

    values = VEXP * DH
    layout = (
        ((0, values, True), (values, DH, True), (values + DH, DH, True), (values + 2 * DH, DH, False)),
        ((0, values, True),),
        ((0, early.shape[1], False),),
    )

    def by_owner(grads):
        return grads.reshape(groups, levels, HEADS, wrows, -1)

    input_grad, grad_value, grad_query, grad_key, sides, grad_output, common = finish(
        layout,
        grad_inputs.reshape(HEADS, HEADS, levels * piece, width),
        grad_middle.reshape(HEADS, levels * piece, width),
        by_owner(late),
        by_owner(grad_w_output),
        by_owner(early),
    )
    norms = jnp.sum(sides[:, :, 2 * VEXP : 2 * VEXP + 2], axis=0)
    common = jnp.sum(common[:, :, : experts + 2], axis=0)
    router_grad = common[:, :experts].reshape(wrows, HEADS, levels, local_experts)

    def side(first):
        return sides[:, :, first : first + VEXP].transpose(1, 0, 2).reshape(wrows, HEADS * VEXP)

    return (
        layer_out,
        input_grad.reshape(count, width),
        norms[:, 0],
        norms[:, 1],
        common[:, experts],
        common[:, experts + 1],
        grad_query,
        grad_key,
        grad_value,
        grad_output,
        side(0),
        side(VEXP),
        jnp.swapaxes(router_grad, 1, 2).reshape(wrows, experts),
        ffn_in_grad.astype(jnp.float32),
        ffn_out_grad.astype(jnp.float32),
    )


def solution(mesh):
    groups, shards = mesh.devices.shape
    fine = Mesh(mesh.devices.reshape(groups, shards // HEADS, HEADS), TOK)
    two, one, three = P(TOK, None), P(TOK), P(TOK, None, None)
    ffn = P("group", ("level", "head"))
    return jax.shard_map(
        body,
        mesh=fine,
        in_specs=(two, two, two, P("group", None), three, three, two, one, one, one, one)
        + (two,) * 7
        + (ffn, ffn),
        out_specs=(two, two, one, one, one, one) + (two,) * 7 + (ffn, ffn),
        check_vma=False,
    )
```

```python
import functools

import jax
import jax.numpy as jnp
from jax import lax
from jax.experimental import pallas as pl
from jax.experimental.pallas import tpu as pltpu
from jax.sharding import Mesh, PartitionSpec as P

HEADS = 4
DH = 128
VEXP = 5
FH = 128
LMAX = 4096

TOK = ("group", "level", "head")


def transposed(left_side, right_side):
    return lax.dot_general(
        left_side, right_side, (((1,), (1,)), ((), ())), preferred_element_type=jnp.float32
    )


def low(value):
    return value.astype(jnp.bfloat16)


def to_home(rows):
    levels = lax.axis_size("level")
    count = rows.shape[0]
    out = rows.reshape(HEADS, levels, count // levels // HEADS, -1).transpose(1, 0, 2, 3)
    back = lax.all_to_all(
        out.reshape(levels, count // levels, -1), "level", split_axis=0, concat_axis=0, tiled=True
    )
    return back.reshape(count, -1)


MESH = pl.DeviceIdType.MESH


def partners(head):
    near = head + 1 - 2 * lax.rem(head, 2)
    far = lax.rem(head + 2, HEADS)
    return near, far


def greet(near, far):
    barrier = pltpu.get_barrier_semaphore()
    for peer in (near, far):
        pl.semaphore_signal(barrier, inc=1, device_id={"head": peer}, device_id_type=MESH)
    pl.semaphore_wait(barrier, 2)


def remote(src, dst, send, recv, peer):
    return pltpu.make_async_remote_copy(
        src_ref=src,
        dst_ref=dst,
        send_sem=send,
        recv_sem=recv,
        device_id={"head": peer},
        device_id_type=MESH,
    )


def cost(flops, moved):
    return pl.CostEstimate(flops=int(flops), bytes_accessed=int(moved), transcendentals=0)


def gather_kernel(
    by_source, own, out, local_sem, near_send, near_recv, far_send, far_recv, pass_send, pass_recv
):
    head = lax.axis_index("head")
    near, far = partners(head)
    greet(near, far)

    def spot(i, source):
        return out.at[source, i] if by_source else out.at[i, source]

    pieces = range(HEADS)
    to_far = [remote(own.at[i], spot(i, head), far_send.at[i], far_recv.at[i], far) for i in pieces]
    to_near = [
        remote(own.at[i], spot(i, head), near_send.at[i], near_recv.at[i], near) for i in pieces
    ]
    passed = [
        remote(spot(i, far), spot(i, far), pass_send.at[i], pass_recv.at[i], near) for i in pieces
    ]
    kept = [pltpu.make_async_copy(own.at[i], spot(i, head), local_sem.at[i]) for i in pieces]
    for copy in to_far + to_near + kept:
        copy.start()
    for i in pieces:
        to_far[i].wait_recv()
        passed[i].start()
    for i in pieces:
        to_near[i].wait_recv()
        passed[i].wait_recv()
        kept[i].wait()
        to_far[i].wait_send()
        to_near[i].wait_send()
        passed[i].wait_send()


def level_gather(rows, collective_id, by_source=False):
    count, width = rows.shape
    whole = pl.pallas_call(
        functools.partial(gather_kernel, by_source),
        out_shape=jax.ShapeDtypeStruct((HEADS, HEADS, count // HEADS, width), rows.dtype),
        in_specs=[pl.BlockSpec(memory_space=pltpu.VMEM)],
        out_specs=pl.BlockSpec(memory_space=pl.ANY),
        scratch_shapes=[pltpu.SemaphoreType.DMA((HEADS,))] * 7,
        compiler_params=pltpu.CompilerParams(collective_id=collective_id, has_side_effects=True),
        cost_estimate=cost(0, 90e6),
        name="level_gather",
    )(rows.reshape(HEADS, count // HEADS, width))
    return whole.reshape(HEADS * count, width)


def scatter_kernel(
    by_source, part, out, near_buf, send_buf, far_buf, near_send, near_recv, far_send, far_recv
):
    head = lax.axis_index("head")
    near, far = partners(head)
    greet(near, far)
    across = HEADS - 1 - head
    pieces = range(HEADS)

    def spot(i, dest):
        return (dest, i) if by_source else (i, dest)

    def to_near(slot, i, dest):
        return remote(
            part.at[spot(i, dest)],
            near_buf.at[slot, i],
            near_send.at[slot, i],
            near_recv.at[slot, i],
            near,
        )

    first = [to_near(0, i, across) for i in pieces]
    second = [to_near(1, i, near) for i in pieces]
    onward = [
        remote(send_buf.at[i], far_buf.at[i], far_send.at[i], far_recv.at[i], far) for i in pieces
    ]
    for copy in first + second:
        copy.start()
    for i in pieces:
        first[i].wait_recv()
        both = part[spot(i, far)].astype(jnp.float32) + near_buf[0, i].astype(jnp.float32)
        send_buf[i] = both.astype(jnp.bfloat16)
        onward[i].start()
    for i in pieces:
        second[i].wait_recv()
        out[i] = part[spot(i, head)].astype(jnp.float32) + near_buf[1, i].astype(jnp.float32)
    for i in pieces:
        onward[i].wait_recv()
        out[i] = out[i] + far_buf[i].astype(jnp.float32)
    for i in pieces:
        first[i].wait_send()
        second[i].wait_send()
        onward[i].wait_send()


def level_scatter(rows, collective_id, by_source=False):
    total, width = rows.shape
    piece = total // (HEADS * HEADS)
    low_type = jnp.bfloat16
    mine = pl.pallas_call(
        functools.partial(scatter_kernel, by_source),
        out_shape=jax.ShapeDtypeStruct((HEADS, piece, width), jnp.float32),
        in_specs=[pl.BlockSpec(memory_space=pltpu.VMEM)],
        out_specs=pl.BlockSpec(memory_space=pltpu.VMEM),
        scratch_shapes=[
            pltpu.VMEM((2, HEADS, piece, width), low_type),
            pltpu.VMEM((HEADS, piece, width), low_type),
            pltpu.VMEM((HEADS, piece, width), low_type),
            pltpu.SemaphoreType.DMA((2, HEADS)),
            pltpu.SemaphoreType.DMA((2, HEADS)),
            pltpu.SemaphoreType.DMA((HEADS,)),
            pltpu.SemaphoreType.DMA((HEADS,)),
        ],
        compiler_params=pltpu.CompilerParams(
            collective_id=collective_id, has_side_effects=True, vmem_limit_bytes=32 * 2**20
        ),
        cost_estimate=cost(0, 80e6),
        name="level_scatter",
    )(rows.reshape(HEADS, HEADS, piece, width))
    return mine.reshape(HEADS * piece, width)


def meet(near):
    barrier = pltpu.get_barrier_semaphore()
    pl.semaphore_signal(barrier, inc=1, device_id={"head": near}, device_id_type=MESH)
    pl.semaphore_wait(barrier, 1)


def pair_scatter_kernel(by_source, part, out, out_far, near_buf, send, recv):
    head = lax.axis_index("head")
    near, far = partners(head)
    meet(near)
    across = HEADS - 1 - head
    pieces = range(HEADS)

    def spot(i, dest):
        return (dest, i) if by_source else (i, dest)

    def to_near(slot, i, dest):
        return remote(
            part.at[spot(i, dest)], near_buf.at[slot, i], send.at[slot, i], recv.at[slot, i], near
        )

    first = [to_near(0, i, across) for i in pieces]
    second = [to_near(1, i, near) for i in pieces]
    for copy in first + second:
        copy.start()
    for i in pieces:
        first[i].wait_recv()
        both = part[spot(i, far)].astype(jnp.float32) + near_buf[0, i].astype(jnp.float32)
        out_far[i] = both.astype(jnp.bfloat16)
    for i in pieces:
        second[i].wait_recv()
        out[i] = part[spot(i, head)].astype(jnp.float32) + near_buf[1, i].astype(jnp.float32)
    for i in pieces:
        first[i].wait_send()
        second[i].wait_send()


def pair_scatter(rows, collective_id, by_source=False):
    total, width = rows.shape
    piece = total // (HEADS * HEADS)
    mine, other = pl.pallas_call(
        functools.partial(pair_scatter_kernel, by_source),
        out_shape=[
            jax.ShapeDtypeStruct((HEADS, piece, width), jnp.float32),
            jax.ShapeDtypeStruct((HEADS, piece, width), jnp.bfloat16),
        ],
        in_specs=[pl.BlockSpec(memory_space=pltpu.VMEM)],
        out_specs=[pl.BlockSpec(memory_space=pltpu.VMEM)] * 2,
        scratch_shapes=[
            pltpu.VMEM((2, HEADS, piece, width), jnp.bfloat16),
            pltpu.SemaphoreType.DMA((2, HEADS)),
            pltpu.SemaphoreType.DMA((2, HEADS)),
        ],
        compiler_params=pltpu.CompilerParams(
            collective_id=collective_id, has_side_effects=True, vmem_limit_bytes=32 * 2**20
        ),
        cost_estimate=cost(0, 25e6),
        name="pair_scatter",
    )(rows.reshape(HEADS, HEADS, piece, width))
    return mine.reshape(HEADS * piece, width), other.reshape(HEADS * piece, width)


def pair_gather_kernel(by_source, own, other, out, local_sem, send, recv):
    head = lax.axis_index("head")
    near, far = partners(head)
    meet(near)
    copies, kept = [], []
    for i in range(HEADS):
        for slot, (block, source) in enumerate(((own, head), (other, far))):
            place = out.at[source, i] if by_source else out.at[i, source]
            copies.append(
                remote(block.at[i], place, send.at[slot, i], recv.at[slot, i], near)
            )
            kept.append(pltpu.make_async_copy(block.at[i], place, local_sem.at[slot, i]))
    for copy in copies + kept:
        copy.start()
    for copy in copies + kept:
        copy.wait()


def pair_gather(own, other, collective_id, by_source=False):
    count, width = own.shape
    split = (HEADS, count // HEADS, width)
    whole = pl.pallas_call(
        functools.partial(pair_gather_kernel, by_source),
        out_shape=jax.ShapeDtypeStruct((HEADS,) + split, own.dtype),
        in_specs=[pl.BlockSpec(memory_space=pltpu.VMEM)] * 2,
        out_specs=pl.BlockSpec(memory_space=pl.ANY),
        scratch_shapes=[pltpu.SemaphoreType.DMA((2, HEADS))] * 3,
        compiler_params=pltpu.CompilerParams(collective_id=collective_id, has_side_effects=True),
        cost_estimate=cost(0, 25e6),
        name="pair_gather",
    )(own.reshape(split), other.reshape(split))
    return whole.reshape(HEADS * count, width)


def to_far(rows):
    return lax.ppermute(rows, "head", [(i, (i + 2) % HEADS) for i in range(HEADS)])


def ring(axis):
    me, size = lax.axis_index(axis), lax.axis_size(axis)
    ahead = [lax.rem(me + k, size) for k in range(1, size)]
    behind = [lax.rem(me + size - k, size) for k in range(1, size)]
    return me, ahead, behind


def reach_out(src, dst, send, recv, peer):
    return pltpu.make_async_remote_copy(
        src_ref=src, dst_ref=dst, send_sem=send, recv_sem=recv, device_id=peer, device_id_type=MESH
    )


def greet_all(peers):
    barrier = pltpu.get_barrier_semaphore()
    for peer in peers:
        pl.semaphore_signal(barrier, inc=1, device_id=peer, device_id_type=MESH)
    pl.semaphore_wait(barrier, len(peers))


def start_kernel(
    tokens, cotangents, value, output, query, key, extra, tables, picks, order,
    rows, grads, full, routes, chosen_rows, orders, weights, own_sem, *sems
):
    sems = iter(sems)

    def pair():
        return next(sems), next(sems)

    group, groups_ahead, _ = ring("group")
    level, levels_ahead, levels_behind = ring("level")
    head = lax.axis_index("head")
    near, far = partners(head)
    mates = [near, far, HEADS - 1 - head]
    for to in range(HEADS):
        at = 0
        for part in (value, output, query, key):
            size = part.shape[1] // HEADS
            weights[to, :, at : at + size] = part[:, to * size : (to + 1) * size]
            at += size
        weights[to, :, at:] = extra[to]
    greet_all(
        [{"head": m} for m in mates]
        + [{"level": n} for n in levels_ahead]
        + [{"group": n} for n in groups_ahead]
    )
    started = []

    def send(src, dst, send_sem, recv_sem, peer):
        copy = reach_out(src, dst, send_sem, recv_sem, peer)
        copy.start()
        started.append(copy)
        return copy

    out_s, out_r = pair()
    pick_s, pick_r = pair()
    crossing, picking = [], []
    for k, to in enumerate(levels_ahead):
        peer = {"level": to}
        crossing.append(send(tokens.at[to], rows.at[:, head, level], out_s.at[k], out_r.at[k], peer))
    mate_s, mate_r = pair()
    table_s, table_r = pair()
    order_s, order_r = pair()
    to_mates, order_mates, table_mates = [], [], []
    for k, to in enumerate(mates):
        peer = {"head": to}
        to_mates.append(
            send(weights.at[to], full.at[group, level, head], mate_s.at[k], mate_r.at[k], peer)
        )
        order_mates.append(
            send(order, orders.at[level, head], order_s.at[k], order_r.at[k], peer)
        )
    own = [
        (tokens.at[level], rows.at[:, head, level]),
        (weights.at[head], full.at[group, level, head]),
        (tables.at[head], routes.at[head]),
        (picks.at[level], chosen_rows.at[level]),
        (order, orders.at[level, head]),
        (cotangents.at[level], grads.at[:, level]),
    ]
    own = [pltpu.make_async_copy(src, dst, own_sem.at[i]) for i, (src, dst) in enumerate(own)]
    for copy in own:
        copy.start()
    far_s, far_r = pair()
    near_s, near_r = pair()
    pass_s, pass_r = pair()
    to_far, to_near = [], []

    def share(k, src, source):
        place = rows.at[:, head, source]
        to_far.append(send(src, place, far_s.at[k], far_r.at[k], {"head": far}))
        to_near.append(send(src, place, near_s.at[k], near_r.at[k], {"head": near}))

    share(0, tokens.at[level], level)
    block_s, block_r = pair()
    group_s, group_r = pair()
    orders_s, orders_r = pair()
    for copy in to_mates:
        copy.wait_recv()
    own[1].wait()
    blocks, grouped, ordered = [], [], []

    def to_groups(j, source):
        for k, to in enumerate(groups_ahead):
            block = full.at[group, source]
            grouped.append(
                send(block, block, group_s.at[k, j], group_r.at[k, j], {"group": to})
            )

    for k, to in enumerate(levels_ahead):
        block = full.at[group, level]
        blocks.append(send(block, block, block_s.at[k], block_r.at[k], {"level": to}))
    to_groups(0, level)
    for k, to in enumerate(mates):
        table_mates.append(
            send(tables.at[to], routes.at[head], table_s.at[k], table_r.at[k], {"head": to})
        )
    for k, to in enumerate(levels_ahead):
        picking.append(
            send(picks.at[to], chosen_rows.at[level], pick_s.at[k], pick_r.at[k], {"level": to})
        )
    for copy in order_mates:
        copy.wait_recv()
    own[4].wait()
    for k, to in enumerate(levels_ahead):
        block = orders.at[level]
        ordered.append(send(block, block, orders_s.at[k], orders_r.at[k], {"level": to}))
    for k, source in enumerate(levels_behind):
        crossing[k].wait_recv()
        share(k + 1, rows.at[:, head, source], source)
    grad_s, grad_r = pair()
    crossed = []
    for k, to in enumerate(levels_ahead):
        crossed.append(
            send(cotangents.at[to], grads.at[:, level], grad_s.at[k], grad_r.at[k], {"level": to})
        )
    for k, source in enumerate(levels_behind):
        blocks[k].wait_recv()
        to_groups(k + 1, source)
    passed = []
    for k, source in enumerate([level] + levels_behind):
        to_far[k].wait_recv()
        place = rows.at[:, far, source]
        passed.append(send(place, place, pass_s.at[k], pass_r.at[k], {"head": near}))
    for copy in to_near + passed + grouped + table_mates + picking + ordered + crossed:
        copy.wait_recv()
    for copy in started:
        copy.wait_send()
    for i in (0, 2, 3, 5):
        own[i].wait()


def start(tokens, cotangents, weights, extra, tables, picks, order):
    groups, levels = lax.axis_size("group"), lax.axis_size("level")
    _, _, piece, width = tokens.shape
    columns = sum(part.shape[1] for part in weights) // HEADS + extra.shape[2]
    block = extra.shape[:2] + (columns,)
    shapes = [
        jax.ShapeDtypeStruct((HEADS, HEADS, levels, piece, width), tokens.dtype),
        jax.ShapeDtypeStruct((HEADS, levels, piece, width), tokens.dtype),
        jax.ShapeDtypeStruct((groups, levels) + block, extra.dtype),
        jax.ShapeDtypeStruct(tables.shape, tables.dtype),
        jax.ShapeDtypeStruct(picks.shape, picks.dtype),
        jax.ShapeDtypeStruct((levels, HEADS) + order.shape, order.dtype),
    ]
    dma = pltpu.SemaphoreType.DMA
    others, mates = (levels - 1,), (HEADS - 1,)
    counts = [others] * 2 + [mates] * 3 + [(levels,)] * 3
    counts += [others, (groups - 1, levels), others, others]
    return pl.pallas_call(
        start_kernel,
        out_shape=shapes,
        in_specs=[pl.BlockSpec(memory_space=pltpu.VMEM)] * 10,
        out_specs=[pl.BlockSpec(memory_space=pl.ANY)] * 6,
        scratch_shapes=[pltpu.VMEM(block, extra.dtype), dma((6,))] + [dma(c) for c in counts for _ in range(2)],
        compiler_params=pltpu.CompilerParams(collective_id=9, has_side_effects=True),
        cost_estimate=cost(0, 200e6),
        name="start",
    )(tokens, cotangents, *weights, extra, tables, picks, order)


def finish_kernel(layout, *refs):
    refs = iter(refs)
    count = len(layout)

    def take(n):
        return [next(refs) for _ in range(n)]

    part, middle = take(2)
    grads = take(count)
    (home_grad,) = take(1)
    results = [take(len(pieces)) for pieces in layout]
    near_buf, send_buf, far_buf, total, back_buf, came_buf = take(6)
    group_buf, level_send, level_buf, head_send, owned = (take(count) for _ in range(5))

    def pair():
        return next(refs), next(refs)

    group, groups_ahead, _ = ring("group")
    level, levels_ahead, levels_behind = ring("level")
    head = lax.axis_index("head")
    near, far = partners(head)
    across = HEADS - 1 - head
    mates = [near, far, across]
    greet_all(
        [{"head": m} for m in mates]
        + [{"level": n} for n in levels_ahead]
        + [{"group": n} for n in groups_ahead]
    )
    started = []

    def send(src, dst, send_sem, recv_sem, peer):
        copy = reach_out(src, dst, send_sem, recv_sem, peer)
        copy.start()
        started.append(copy)
        return copy

    pieces = range(HEADS)
    sets = range(count)
    near_s, near_r = pair()
    far_s, far_r = pair()
    back_s, back_r = pair()
    group_s, group_r = pair()
    level_s, level_r = pair()
    mate_s, mate_r = pair()
    first, second, onward = [], [], []
    for slot, (dest, copies) in enumerate(((across, first), (near, second))):
        for i in pieces:
            copies.append(
                send(
                    part.at[i, dest],
                    near_buf.at[slot, i],
                    near_s.at[slot, i],
                    near_r.at[slot, i],
                    {"head": near},
                )
            )
    order = levels_ahead + [level]
    grouped = {}
    for j, dest in enumerate(order):
        for p in sets:
            grouped[j, p] = [
                send(
                    grads[p].at[to, dest],
                    group_buf[p].at[k, j],
                    group_s.at[p, k, j],
                    group_r.at[p, k, j],
                    {"group": to},
                )
                for k, to in enumerate(groups_ahead)
            ]
    for i in pieces:
        first[i].wait_recv()
        both = part[i, far].astype(jnp.float32) + near_buf[0, i].astype(jnp.float32)
        send_buf[i] = both.astype(jnp.bfloat16)
        onward.append(send(send_buf.at[i], far_buf.at[i], far_s.at[i], far_r.at[i], {"head": far}))
    for i in pieces:
        second[i].wait_recv()
        both = part[i, head].astype(jnp.float32) + near_buf[1, i].astype(jnp.float32)
        total[i] = both + middle[i]
    leveled = {}
    for j, dest in enumerate(order):
        for p in sets:
            amount = grads[p][group, dest].astype(jnp.float32)
            for k, copy in enumerate(grouped[j, p]):
                copy.wait_recv()
                amount = amount + group_buf[p][k, j].astype(jnp.float32)
            level_send[p][j] = amount.astype(jnp.bfloat16)
            if j < len(levels_ahead):
                leveled[j, p] = send(
                    level_send[p].at[j],
                    level_buf[p].at[j],
                    level_s.at[p, j],
                    level_r.at[p, j],
                    {"level": dest},
                )
    for i in pieces:
        onward[i].wait_recv()
        both = total[i] + far_buf[i].astype(jnp.float32)
        back_buf[i] = both.astype(jnp.bfloat16).reshape(back_buf.shape[1:])
    backs = [
        send(back_buf.at[:, to], came_buf.at[level], back_s.at[k], back_r.at[k], {"level": to})
        for k, to in enumerate(levels_ahead)
    ]
    sharing = []
    for p in sets:
        amount = level_send[p][len(levels_ahead)].astype(jnp.float32)
        for j in range(len(levels_ahead)):
            leveled[j, p].wait_recv()
            amount = amount + level_buf[p][j].astype(jnp.float32)
        head_send[p][...] = amount.astype(jnp.bfloat16)
        sharing += [
            send(
                head_send[p].at[to],
                owned[p].at[head],
                mate_s.at[p, k],
                mate_r.at[p, k],
                {"head": to},
            )
            for k, to in enumerate(mates)
        ]
        owned[p][head] = head_send[p][head]
    home_grad[level] = back_buf[:, level].astype(jnp.float32)
    for k, source in enumerate(levels_behind):
        backs[k].wait_recv()
        home_grad[source] = came_buf[source].astype(jnp.float32)
    for copy in sharing:
        copy.wait_recv()
    for p in sets:
        for out, (first_column, size, joined) in zip(results[p], layout[p]):
            for h in range(HEADS):
                value = owned[p][h, :, first_column : first_column + size].astype(jnp.float32)
                if joined:
                    out[:, h * size : (h + 1) * size] = value
                else:
                    out[h] = value
    for copy in started:
        copy.wait_send()


def finish(layout, part, middle, *grads):
    groups, levels = lax.axis_size("group"), lax.axis_size("level")
    _, count, width = middle.shape
    piece = count // levels
    low_type = jnp.bfloat16
    blocks = [grad.shape[2:] for grad in grads]
    sets = len(grads)
    dma = pltpu.SemaphoreType.DMA
    counts = [(2, HEADS), (HEADS,), (levels - 1,)]
    counts += [(sets, groups - 1, levels), (sets, levels - 1), (sets, HEADS - 1)]
    vmem = pl.BlockSpec(memory_space=pltpu.VMEM)
    shapes = []
    for pieces in layout:
        for _, size, joined in pieces:
            shape = (blocks[0][1], HEADS * size) if joined else (HEADS, blocks[0][1], size)
            shapes.append(jax.ShapeDtypeStruct(shape, jnp.float32))
    return pl.pallas_call(
        functools.partial(finish_kernel, layout),
        out_shape=[jax.ShapeDtypeStruct((levels, HEADS, piece, width), jnp.float32)] + shapes,
        in_specs=[vmem] * (2 + sets),
        out_specs=[vmem] * (1 + len(shapes)),
        scratch_shapes=[
            pltpu.VMEM((2, HEADS, count, width), low_type),
            pltpu.VMEM((HEADS, count, width), low_type),
            pltpu.VMEM((HEADS, count, width), low_type),
            pltpu.VMEM((HEADS, count, width), jnp.float32),
            pltpu.VMEM((HEADS, levels, piece, width), low_type),
            pltpu.VMEM((levels, HEADS, piece, width), low_type),
        ]
        + [pltpu.VMEM((groups - 1, levels) + block, low_type) for block in blocks]
        + [pltpu.VMEM((levels,) + block, low_type) for block in blocks]
        + [pltpu.VMEM((levels - 1,) + block, low_type) for block in blocks]
        + [pltpu.VMEM(block, low_type) for block in blocks] * 2
        + [dma(c) for c in counts for _ in range(2)],
        compiler_params=pltpu.CompilerParams(
            collective_id=10, has_side_effects=True, vmem_limit_bytes=56 * 2**20
        ),
        cost_estimate=cost(0, 200e6),
        name="finish",
    )(part, middle, *grads)


BLOCK = 512
LOG2E = 1.4426950408889634


def dot(left_side, right_side, left_dim, right_dim):
    return lax.dot_general(
        left_side,
        right_side,
        (((left_dim,), (right_dim,)), ((), ())),
        preferred_element_type=jnp.float32,
    )


def attend_kernel(parts, first, q, *refs):
    keys, values = refs[:parts], refs[parts : 2 * parts]
    pos_q, start_q, pos_k, out, lse, top, total, acc = refs[2 * parts :]
    at = pl.program_id(0)
    blocks = pl.num_programs(0)
    rate = LOG2E * DH ** (-0.5)
    top[...] = jnp.full_like(top, -1e30)
    total[...] = jnp.zeros_like(total)
    acc[...] = jnp.zeros_like(acc)
    query = q[...]
    row_at, row_from = pos_q[0], start_q[0]

    for part in range(parts):

        def step(block, carry, k=keys[part], v=values[part], part=part):
            rows = pl.ds(pl.multiple_of(block * BLOCK, BLOCK), BLOCK)
            spot = pl.ds(pl.multiple_of((part * blocks + block) * BLOCK, BLOCK), BLOCK)
            scores = dot(k[rows, :], query, 1, 1)
            key_at = pos_k[spot, :]
            scores = jnp.where((key_at >= row_from) & (key_at <= row_at), scores, -1e30)
            old = top[...]
            new = jnp.maximum(old, jnp.max(scores, axis=0, keepdims=True))
            shrink = jnp.exp2((old - new) * rate)
            weight = jnp.exp2((scores - new) * rate)
            total[...] = total[...] * shrink + jnp.sum(weight, axis=0, keepdims=True)
            acc[...] = acc[...] * shrink + dot(v[rows, :], weight.astype(jnp.bfloat16), 0, 0)
            top[...] = new
            return carry

        begin = jnp.maximum(first[at] - part * blocks, 0)
        end = at + 1 if part == parts - 1 else blocks
        lax.fori_loop(begin, end, step, 0)
    out[...] = (acc[...] / total[...]).T
    lse[0] = top[...] * rate + jnp.log2(total[...])


def attend(first, queries, window, pos_q, start_q, pos_k):
    rows = queries.shape[0]
    parts = len(window)
    line = pl.BlockSpec((1, 1, BLOCK), lambda i, *_: (i, 0, 0))
    grid_spec = pltpu.PrefetchScalarGridSpec(
        num_scalar_prefetch=1,
        grid=(rows // BLOCK,),
        in_specs=[pl.BlockSpec((BLOCK, DH), lambda i, *_: (i, 0))]
        + [pl.BlockSpec((rows, DH), lambda i, *_: (0, 0))] * parts
        + [pl.BlockSpec((rows, DH), lambda i, *_: (0, 1))] * parts
        + [line, line, pl.BlockSpec((parts * rows, 1), lambda i, *_: (0, 0))],
        out_specs=[pl.BlockSpec((BLOCK, DH), lambda i, *_: (i, 0)), line],
        scratch_shapes=[
            pltpu.VMEM((1, BLOCK), jnp.float32),
            pltpu.VMEM((1, BLOCK), jnp.float32),
            pltpu.VMEM((DH, BLOCK), jnp.float32),
        ],
    )
    return pl.pallas_call(
        functools.partial(attend_kernel, parts),
        grid_spec=grid_spec,
        out_shape=[
            jax.ShapeDtypeStruct((rows, DH), jnp.float32),
            jax.ShapeDtypeStruct((rows // BLOCK, 1, BLOCK), jnp.float32),
        ],
        compiler_params=pltpu.CompilerParams(vmem_limit_bytes=48 * 2**20),
        cost_estimate=cost(2e10, 1e7),
        name="attend",
    )(first, queries, *window, *window, pos_q, start_q, pos_k)


def attend_back_kernel(parts, first, q, *refs):
    keys, values = refs[:parts], refs[parts : 2 * parts]
    grad, pos_q, start_q, lse, inner, pos_k, grad_q = refs[2 * parts : 2 * parts + 7]
    grads = refs[2 * parts + 7 : 3 * parts + 7]
    sum_k, sum_v, acc = refs[3 * parts + 7 :]
    at = pl.program_id(0)
    blocks = pl.num_programs(0)
    rate = LOG2E * DH ** (-0.5)
    scale = DH ** (-0.5)

    @pl.when(at == 0)
    def _():
        sum_k[...] = jnp.zeros_like(sum_k)
        sum_v[...] = jnp.zeros_like(sum_v)

    acc[...] = jnp.zeros_like(acc)
    query, grad_out = q[...], grad[...]
    row_at, row_from, row_lse, row_inner = pos_q[0], start_q[0], lse[0], inner[0]

    for part in range(parts):

        def step(block, carry, k=keys[part], v=values[part], part=part):
            rows = pl.ds(pl.multiple_of(block * BLOCK, BLOCK), BLOCK)
            spot = pl.ds(pl.multiple_of((part * blocks + block) * BLOCK, BLOCK), BLOCK)
            key, value = k[rows, :], v[rows, :]
            scores = dot(key, query, 1, 1)
            key_at = pos_k[spot, :]
            seen = (key_at >= row_from) & (key_at <= row_at)
            soft = jnp.where(seen, jnp.exp2(scores * rate - row_lse), 0.0)
            grad_soft = dot(value, grad_out, 1, 1)
            grad_scores = (soft * (grad_soft - row_inner)).astype(jnp.bfloat16)
            sum_v[spot, :] += dot(soft.astype(jnp.bfloat16), grad_out, 1, 0)
            sum_k[spot, :] += dot(grad_scores, query, 1, 0)
            acc[...] += dot(grad_scores, key, 0, 0)
            return carry

        begin = jnp.maximum(first[at] - part * blocks, 0)
        end = at + 1 if part == parts - 1 else blocks
        lax.fori_loop(begin, end, step, 0)
    grad_q[...] = (acc[...] * scale).astype(jnp.bfloat16)

    @pl.when(at == blocks - 1)
    def _():
        size = grads[0].shape[0]
        for part in range(parts):
            spot = slice(part * size, (part + 1) * size)
            grads[part][:, :DH] = (sum_k[spot, :] * scale).astype(grads[part].dtype)
            grads[part][:, DH:] = sum_v[spot, :].astype(grads[part].dtype)


def attend_back(first, queries, window, grads, pos_q, start_q, lse, inner, pos_k):
    rows = queries.shape[0]
    parts = len(window)
    block = pl.BlockSpec((BLOCK, DH), lambda i, *_: (i, 0))
    line = pl.BlockSpec((1, 1, BLOCK), lambda i, *_: (i, 0, 0))
    grid_spec = pltpu.PrefetchScalarGridSpec(
        num_scalar_prefetch=1,
        grid=(rows // BLOCK,),
        in_specs=[block]
        + [pl.BlockSpec((rows, DH), lambda i, *_: (0, 0))] * parts
        + [pl.BlockSpec((rows, DH), lambda i, *_: (0, 1))] * parts
        + [block, line, line, line, line]
        + [pl.BlockSpec((parts * rows, 1), lambda i, *_: (0, 0))],
        out_specs=[block] + [pl.BlockSpec((rows, 2 * DH), lambda i, *_: (0, 0))] * parts,
        scratch_shapes=[
            pltpu.VMEM((parts * rows, DH), jnp.float32),
            pltpu.VMEM((parts * rows, DH), jnp.float32),
            pltpu.VMEM((BLOCK, DH), jnp.float32),
        ],
    )
    kinds = [jnp.bfloat16] * (parts - 1) + [jnp.float32]
    return pl.pallas_call(
        functools.partial(attend_back_kernel, parts),
        grid_spec=grid_spec,
        out_shape=[jax.ShapeDtypeStruct((rows, DH), jnp.bfloat16)]
        + [jax.ShapeDtypeStruct((rows, 2 * DH), kind) for kind in kinds],
        compiler_params=pltpu.CompilerParams(vmem_limit_bytes=48 * 2**20),
        cost_estimate=cost(2e9, 1e6),
        name="attend_back",
    )(first, queries, *window, *window, grads, pos_q, start_q, lse, inner, pos_k)


def columns_of(ref, group, groups, step, depth):
    at = lax.rem(group + step + groups, groups) * depth
    return ref.at[:, pl.ds(pl.multiple_of(at, 128), depth)]


def front_kernel(groups, local, place, hidden, grads, *refs):
    w_in, w_out = refs[0], refs[1 : groups + 1]
    gates, active, grad_pre, rows_out, turned, acc = refs[groups + 1 :]
    levels, _, depth, width = w_in.shape
    tile = hidden.shape[0]
    model = groups * depth
    parts = [slice(step * depth, (step + 1) * depth) for step in range(groups)]
    for step in range(groups):
        turned[0, :, parts[step]] = columns_of(hidden, place[1], groups, -step, depth)[...]
        turned[1, :, parts[step]] = columns_of(grads, place[1], groups, -step, depth)[...]
    gate_grads = []
    for level in range(levels):
        pre_act = jnp.zeros((tile, width), jnp.float32)
        grad_active = jnp.zeros((tile, width), jnp.float32)
        for step in range(groups):
            pre_act += dot(turned[0, :, parts[step]], w_in[level, step], 1, 0)
            grad_active += dot(turned[1, :, parts[step]], w_out[step][level], 1, 0)
        first = level * local
        gate = jnp.concatenate(
            [jnp.broadcast_to(gates[:, first + e : first + e + 1], (tile, FH)) for e in range(local)],
            axis=1,
        )
        sig = 1.0 / (1.0 + jnp.exp2(-LOG2E * pre_act))
        act_pre = pre_act * sig
        columns = slice(level * width, (level + 1) * width)
        active[:, columns] = (act_pre * gate).astype(jnp.bfloat16)
        product = grad_active * act_pre
        for e in range(local):
            gate_grads.append(
                jnp.sum(product[:, e * FH : (e + 1) * FH], axis=1, keepdims=True)
            )
        slope = sig * (1.0 + pre_act * (1.0 - sig))
        low_pre = (grad_active * gate * slope).astype(jnp.bfloat16)
        grad_pre[:, columns] = low_pre
        for step in range(groups):
            back = dot(low_pre, w_in[level, step], 1, 1)
            acc[:, parts[step]] = back if level == 0 else acc[:, parts[step]] + back
    for step in range(groups):
        columns_of(rows_out, place[1], groups, -step, depth)[...] = acc[:, parts[step]].astype(
            jnp.bfloat16
        )
    spare = rows_out.shape[1] - model
    lane = lax.broadcasted_iota(jnp.int32, (tile, spare), 1) - place[0] * (levels * local)
    spread = jnp.zeros((tile, spare), jnp.float32)
    for e, column in enumerate(gate_grads):
        spread = jnp.where(lane == e, column, spread)
    rows_out[:, model:] = spread.astype(jnp.bfloat16)


def ffn_front(place, hidden, grads, w_in, w_out, gates, local):
    rows, wide = hidden.shape
    levels, groups, depth, width = w_in.shape
    tile = 512

    def by_row(columns):
        return pl.BlockSpec((tile, columns), lambda i, *_: (i, 0))

    once = pl.Buffered(1)
    whole = pl.BlockSpec(w_out[0].shape, lambda i, *_: (0, 0, 0), pipeline_mode=once)
    stacked = pl.BlockSpec(w_in.shape, lambda i, *_: (0, 0, 0, 0), pipeline_mode=once)
    grid_spec = pltpu.PrefetchScalarGridSpec(
        num_scalar_prefetch=1,
        grid=(rows // tile,),
        in_specs=[by_row(wide), by_row(groups * depth)]
        + [stacked]
        + [whole] * groups
        + [by_row(gates.shape[1])],
        out_specs=[by_row(levels * width), by_row(levels * width), by_row(wide)],
        scratch_shapes=[
            pltpu.VMEM((2, tile, groups * depth), jnp.bfloat16),
            pltpu.VMEM((tile, groups * depth), jnp.float32),
        ],
    )
    hidden_units = jax.ShapeDtypeStruct((rows, levels * width), jnp.bfloat16)
    return pl.pallas_call(
        functools.partial(front_kernel, groups, local),
        grid_spec=grid_spec,
        out_shape=[hidden_units, hidden_units, jax.ShapeDtypeStruct((rows, wide), jnp.bfloat16)],
        compiler_params=pltpu.CompilerParams(vmem_limit_bytes=58 * 2**20),
        cost_estimate=cost(6 * rows * groups * depth * levels * width, 3e7),
        name="ffn_front",
    )(place, hidden, grads, w_in, *w_out, gates)


def rear_kernel(groups, place, rows_in, hidden_units, *weight_grads):
    _, depth, _ = weight_grads[0].shape
    units = hidden_units[...]
    for step in range(groups):
        part = columns_of(rows_in, place[1], groups, step, depth)
        weight_grads[step][0] = dot(part[...], units, 0, 0).astype(jnp.bfloat16)


def feed_kernel(groups, place, active, *refs):
    weights = refs[:groups]
    feed, acc = refs[groups:]
    _, depth, _ = weights[0].shape
    level = pl.program_id(0)
    act = active[...]
    for step in range(groups):
        fed = dot(act, weights[step][0], 1, 1)
        part = slice(step * depth, (step + 1) * depth)

        @pl.when(level == 0)
        def _():
            acc[:, part] = fed

        @pl.when(level > 0)
        def _():
            acc[:, part] += fed

    @pl.when(level == pl.num_programs(0) - 1)
    def _():
        for step in range(groups):
            part = slice(step * depth, (step + 1) * depth)
            columns_of(feed, place[1], groups, -step, depth)[...] = acc[:, part].astype(
                jnp.bfloat16
            )


def whole_rows(rows, columns):
    return pl.BlockSpec((rows, columns), lambda i, *_: (0, 0), pipeline_mode=pl.Buffered(1))


def ffn_feed(place, active, weights):
    rows = active.shape[0]
    groups = len(weights)
    levels, depth, width = weights[0].shape
    return pl.pallas_call(
        functools.partial(feed_kernel, groups),
        grid_spec=pltpu.PrefetchScalarGridSpec(
            num_scalar_prefetch=1,
            grid=(levels,),
            in_specs=[pl.BlockSpec((rows, width), lambda i, *_: (0, i))]
            + [pl.BlockSpec((1, depth, width), lambda i, *_: (i, 0, 0))] * groups,
            out_specs=whole_rows(rows, groups * depth),
            scratch_shapes=[pltpu.VMEM((rows, groups * depth), jnp.float32)],
        ),
        out_shape=jax.ShapeDtypeStruct((rows, groups * depth), jnp.bfloat16),
        compiler_params=pltpu.CompilerParams(vmem_limit_bytes=58 * 2**20),
        cost_estimate=cost(1e3, 1e3),
        name="ffn_feed",
    )(place, active, *weights)


def ffn_rear(place, rows_in, units, model, groups, levels):
    rows, wide = rows_in.shape
    width = units.shape[1] // levels
    depth = model // groups
    return pl.pallas_call(
        functools.partial(rear_kernel, groups),
        grid_spec=pltpu.PrefetchScalarGridSpec(
            num_scalar_prefetch=1,
            grid=(levels,),
            in_specs=[
                whole_rows(rows, wide),
                pl.BlockSpec((rows, width), lambda i, *_: (0, i)),
            ],
            out_specs=[pl.BlockSpec((1, depth, width), lambda i, *_: (i, 0, 0))] * groups,
        ),
        out_shape=[jax.ShapeDtypeStruct((levels, depth, width), jnp.bfloat16)] * groups,
        compiler_params=pltpu.CompilerParams(vmem_limit_bytes=58 * 2**20),
        cost_estimate=cost(1e3, 1e3),
        name="ffn_rear",
    )(place, rows_in, units)


def named_by(routes, count):
    lane = lax.broadcasted_iota(jnp.int32, (routes.shape[0], count), 1)
    member = jnp.zeros(lane.shape, jnp.float32)
    for slot in range(routes.shape[1]):
        member = jnp.where(lane == routes[:, slot : slot + 1], 1.0, member)
    return member


def middle_kernel(rows, branch, routes, router, gain, bias, middle, extended, sig_out):
    experts = router.shape[1]
    width = rows.shape[1]
    rounded = branch[...].astype(jnp.bfloat16).astype(jnp.float32)
    value = rows[...].astype(jnp.float32) + rounded
    middle[...] = value
    _, _, normed = normalized(value, gain[...], bias[...])
    sig = 1.0 / (1.0 + jnp.exp2(-LOG2E * dot(normed, router[...], 1, 0)))
    sig_out[...] = sig
    extended[:, :width] = value.astype(jnp.bfloat16)
    gates = (sig * named_by(routes[...], experts)).astype(jnp.bfloat16)
    spare = extended.shape[1] - width - experts
    if spare:
        gates = jnp.concatenate([gates, jnp.zeros((gates.shape[0], spare), gates.dtype)], axis=1)
    extended[:, width:] = gates


def enter_ffn(rows, branch, routes, router, gain, bias):
    count, width = rows.shape
    experts = router.shape[1]
    wide = width + experts + -experts % 128
    return pl.pallas_call(
        middle_kernel,
        out_shape=[
            jax.ShapeDtypeStruct((count, width), jnp.float32),
            jax.ShapeDtypeStruct((count, wide), jnp.bfloat16),
            jax.ShapeDtypeStruct((count, experts), jnp.float32),
        ],
        compiler_params=pltpu.CompilerParams(vmem_limit_bytes=40 * 2**20),
        cost_estimate=cost(1e9, 1e7),
        name="middle",
    )(rows, branch, routes, router, gain, bias)


def leave_kernel(
    middle, own, came, cotangent, sigs, routes, router, gain, bias, grad_out, low_out, weight_grads
):
    experts = router.shape[1]
    count, width = middle.shape
    scaled, inverse, normed = normalized(middle[...], gain[...], bias[...])
    total = own[...] + came[...].astype(jnp.float32)
    sig = sigs[...]
    member = named_by(routes[...], experts)
    gate_grads = total[:, width : width + experts]
    logit = (gate_grads * sig * (1.0 - sig) * member).astype(jnp.bfloat16)
    second = dot(logit, router[...], 1, 1)
    inner_grad = second * gain[...]
    inner_grad = inverse * (
        inner_grad
        - jnp.mean(inner_grad, axis=1, keepdims=True)
        - scaled * jnp.mean(inner_grad * scaled, axis=1, keepdims=True)
    )
    grad = cotangent[...].astype(jnp.float32) + total[:, :width] + inner_grad
    grad_out[...] = grad
    low_out[...] = grad.astype(jnp.bfloat16)
    spare = weight_grads.shape[1] - experts
    sums = [
        jnp.sum(second * scaled, axis=0, keepdims=True),
        jnp.sum(second, axis=0, keepdims=True),
        jnp.zeros((126, width), jnp.float32),
    ]
    side = jnp.concatenate(sums, axis=0).T[:, :spare]
    both = jnp.concatenate([dot(normed, logit, 0, 0), side], axis=1)
    weight_grads[...] = both.astype(jnp.bfloat16)


def leave_ffn(middle, own, came, cotangent, sigs, routes, router, gain, bias):
    count, width = middle.shape
    experts = router.shape[1]
    columns = experts + 2 + -(experts + 2) % 128
    return pl.pallas_call(
        leave_kernel,
        out_shape=[
            jax.ShapeDtypeStruct((count, width), jnp.float32),
            jax.ShapeDtypeStruct((count, width), jnp.bfloat16),
            jax.ShapeDtypeStruct((width, columns), jnp.bfloat16),
        ],
        compiler_params=pltpu.CompilerParams(vmem_limit_bytes=48 * 2**20),
        cost_estimate=cost(1e9, 1e7),
        name="leave_ffn",
    )(middle, own, came, cotangent, sigs, routes, router, gain, bias)


def branch_back_kernel(
    grads, w_output, attended, sigs, masks, grad_attended, inner, out_logit, weight_grads, acc
):
    at = pl.program_id(0)
    count = grads.shape[0]
    sig, mask, values = sigs[...], masks[...], attended[...]
    mixed_grad = dot(grads[...], w_output[...], 1, 0)
    lane = lax.broadcasted_iota(jnp.int32, (count, 128), 1)
    logits = jnp.zeros((count, 128), jnp.float32)
    total = jnp.zeros((count, DH), jnp.float32)
    parts = []
    for e in range(VEXP):
        k = VEXP + e
        one, on = sig[:, k : k + 1], mask[:, k : k + 1]
        part = mixed_grad[:, e * DH : (e + 1) * DH]
        total += part * (one * on)
        gate_grad = jnp.sum(part * values, axis=1, keepdims=True)
        logits = jnp.where(lane == k, gate_grad * one * (1.0 - one) * on, logits)
        parts.append((one * on * values).astype(jnp.bfloat16))
    out_logit[...] = logits.astype(jnp.bfloat16)
    rounded = total.astype(jnp.bfloat16)
    grad_attended[...] = rounded
    product = rounded.astype(jnp.float32) * values
    inner[0] = jnp.sum(product.T, axis=0, keepdims=True)
    amount = dot(grads[...], jnp.concatenate(parts, axis=1), 0, 0)

    @pl.when(at == 0)
    def _():
        acc[...] = amount

    @pl.when(at > 0)
    def _():
        acc[...] += amount

    @pl.when(at == pl.num_programs(0) - 1)
    def _():
        weight_grads[...] = acc[...].astype(jnp.bfloat16)


def branch_back(grads, full, attended, sigs, masks):
    rows, width = grads.shape
    values = VEXP * DH

    def by_row(size):
        return pl.BlockSpec((BLOCK, size), lambda i: (i, 0))

    return pl.pallas_call(
        branch_back_kernel,
        grid=(rows // BLOCK,),
        in_specs=[
            by_row(width),
            pl.BlockSpec((width, values), lambda i: (0, 1), pipeline_mode=pl.Buffered(1)),
            by_row(DH),
            by_row(128),
            by_row(16),
        ],
        out_specs=[
            by_row(DH),
            pl.BlockSpec((1, 1, BLOCK), lambda i: (i, 0, 0)),
            by_row(128),
            pl.BlockSpec((width, values), lambda i: (0, 0)),
        ],
        out_shape=[
            jax.ShapeDtypeStruct((rows, DH), jnp.bfloat16),
            jax.ShapeDtypeStruct((rows // BLOCK, 1, BLOCK), jnp.float32),
            jax.ShapeDtypeStruct((rows, 128), jnp.bfloat16),
            jax.ShapeDtypeStruct((width, values), jnp.bfloat16),
        ],
        scratch_shapes=[pltpu.VMEM((width, values), jnp.float32)],
        compiler_params=pltpu.CompilerParams(vmem_limit_bytes=48 * 2**20),
        cost_estimate=cost(1e8, 1e6),
        name="branch_back",
    )(grads, full, attended, sigs, masks)


def turn(value, axis, by):
    size = lax.axis_size(axis)
    return lax.ppermute(value, axis, [(i, (i + by) % size) for i in range(size)])


def normalized(rows, gain, bias):
    values = rows.astype(jnp.float32)
    centred = values - jnp.mean(values, axis=1, keepdims=True)
    inverse = lax.rsqrt(jnp.mean(centred * centred, axis=1, keepdims=True) + 1e-05)
    scaled = centred * inverse
    return scaled, inverse, (scaled * gain + bias).astype(jnp.bfloat16)


def project_kernel(
    levels, rows, w_value, w_query, w_key, routers, gain, bias, order, tables,
    query, key_value, projected, sigs, masks,
):
    count = rows.shape[0]
    piece = count // (levels * HEADS)
    _, _, normed = normalized(rows[...], gain[...], bias[...])
    query[...] = dot(normed, w_query[...], 1, 0).astype(jnp.bfloat16)
    key_value[:, :DH] = dot(normed, w_key[...], 1, 0).astype(jnp.bfloat16)
    sig = 1.0 / (1.0 + jnp.exp2(-LOG2E * dot(normed, routers[...], 1, 0)))
    sigs[...] = sig
    product = dot(rows[...], w_value[...], 1, 0)
    projected[...] = product
    at = lax.broadcasted_iota(jnp.int32, (count, count), 0)
    source = lax.rem(at // piece, levels) * HEADS + at // (piece * levels)
    here = (source * piece + lax.rem(at, piece) == order[0]).astype(jnp.bfloat16)
    lane = lax.broadcasted_iota(jnp.int32, (16, count), 0)
    table = tables[0]
    named = jnp.zeros((16, count), jnp.float32)
    for which in range(2):
        option = lane - which * VEXP
        for slot in range(2):
            pick = table[2 * which + slot : 2 * which + slot + 1, :]
            hit = (option == pick) & (option >= 0) & (option < VEXP)
            named = jnp.where(hit, 1.0, named)
    mask = dot(here, named.astype(jnp.bfloat16), 1, 1)
    masks[...] = mask
    value = jnp.zeros((count, DH), jnp.float32)
    for e in range(VEXP):
        gate = sig[:, e : e + 1] * mask[:, e : e + 1]
        value += gate * product[:, e * DH : (e + 1) * DH]
    key_value[:, DH:] = value.astype(jnp.bfloat16)


def project(rows, full, gain, bias, orders, tables, levels):
    total, width = rows.shape
    count = total // HEADS

    def by_row(columns):
        return pl.BlockSpec((count, columns), lambda i: (i, 0))

    def column(size, at):
        return pl.BlockSpec((width, size), lambda i: (0, at), pipeline_mode=pl.Buffered(1))

    line = pl.BlockSpec((1, width), lambda i: (0, 0))
    shapes = [(DH, jnp.bfloat16), (2 * DH, jnp.bfloat16), (VEXP * DH, jnp.float32)]
    shapes += [(128, jnp.float32), (16, jnp.float32)]
    return pl.pallas_call(
        functools.partial(project_kernel, levels),
        grid=(HEADS,),
        in_specs=[by_row(width), column(VEXP * DH, 0)]
        + [column(DH, 2 * VEXP + i) for i in range(3)]
        + [line, line]
        + [
            pl.BlockSpec((1, 1, count), lambda i: (i, 0, 0)),
            pl.BlockSpec((1,) + tables.shape[1:], lambda i: (i, 0, 0)),
        ],
        out_specs=[by_row(columns) for columns, _ in shapes],
        out_shape=[jax.ShapeDtypeStruct((total, columns), kind) for columns, kind in shapes],
        compiler_params=pltpu.CompilerParams(vmem_limit_bytes=48 * 2**20),
        cost_estimate=cost(2 * total * width * 1024, 2e7),
        name="project",
    )(rows, full, full, full, full, gain, bias, orders, tables)


def project_back_kernel(
    rows, grads, grad_query, out_logit, projected, sigs, masks,
    w_value, w_query, w_key, routers, gain, bias,
    grad_rows, weight_grads, acc, sums,
):
    at = pl.program_id(0)
    count = rows.shape[0]
    values = VEXP * DH

    @pl.when(at == 0)
    def _():
        acc[...] = jnp.zeros_like(acc)
        sums[...] = jnp.zeros_like(sums)

    scaled, inverse, normed = normalized(rows[...], gain[...], bias[...])
    grad_key = grads[:, :DH].astype(jnp.bfloat16)
    grad_value = grads[:, DH:]
    sig, mask = sigs[...], masks[...]
    lane = lax.broadcasted_iota(jnp.int32, (count, 128), 1)
    logits = out_logit[...].astype(jnp.float32)
    parts = []
    for e in range(VEXP):
        one, on = sig[:, e : e + 1], mask[:, e : e + 1]
        parts.append((one * on * grad_value).astype(jnp.bfloat16))
        inner = jnp.sum(grad_value * projected[:, e * DH : (e + 1) * DH], axis=1, keepdims=True)
        logits = jnp.where(lane == e, inner * one * (1.0 - one) * on, logits)
    grad_projected = jnp.concatenate(parts, axis=1)
    sides = jnp.concatenate([grad_query[...], grad_key, logits.astype(jnp.bfloat16)], axis=1)
    first = dot(sides[:, :DH], w_query[...], 1, 1)
    first += dot(sides[:, DH : 2 * DH], w_key[...], 1, 1)
    first += dot(sides[:, 2 * DH :], routers[...], 1, 1)
    sums[2 * VEXP : 2 * VEXP + 1, :] += jnp.sum(first * scaled, axis=0, keepdims=True)
    sums[2 * VEXP + 1 : 2 * VEXP + 2, :] += jnp.sum(first, axis=0, keepdims=True)
    inner_grad = first * gain[...]
    inner_grad = inverse * (
        inner_grad
        - jnp.mean(inner_grad, axis=1, keepdims=True)
        - scaled * jnp.mean(inner_grad * scaled, axis=1, keepdims=True)
    )
    grad_rows[...] = (inner_grad + dot(grad_projected, w_value[...], 1, 1)).astype(jnp.bfloat16)
    acc[:, :values] += dot(rows[...], grad_projected, 0, 0)
    acc[:, values:] += dot(normed, sides, 0, 0)

    @pl.when(at == pl.num_programs(0) - 1)
    def _():
        weight_grads[:, : values + 2 * DH] = acc[:, : values + 2 * DH].astype(jnp.bfloat16)
        last = acc[:, values + 2 * DH :] + sums[...].T
        weight_grads[:, values + 2 * DH :] = last.astype(jnp.bfloat16)


def project_back(rows, grads, grad_query, out_logit, projected, sigs, masks, full, gain, bias):
    total, width = rows.shape
    count = total // HEADS
    columns = VEXP * DH + 3 * DH

    def by_row(size):
        return pl.BlockSpec((count, size), lambda i: (i, 0))

    def column(size, at):
        return pl.BlockSpec((width, size), lambda i: (0, at), pipeline_mode=pl.Buffered(1))

    line = pl.BlockSpec((1, width), lambda i: (0, 0))
    return pl.pallas_call(
        project_back_kernel,
        grid=(HEADS,),
        in_specs=[by_row(width), by_row(2 * DH), by_row(DH), by_row(128), by_row(VEXP * DH)]
        + [by_row(128), by_row(16), column(VEXP * DH, 0)]
        + [column(DH, 2 * VEXP + i) for i in range(3)]
        + [line, line],
        out_specs=[by_row(width), pl.BlockSpec((width, columns), lambda i: (0, 0))],
        out_shape=[
            jax.ShapeDtypeStruct((total, width), jnp.bfloat16),
            jax.ShapeDtypeStruct((width, columns), jnp.bfloat16),
        ],
        scratch_shapes=[
            pltpu.VMEM((width, columns), jnp.float32),
            pltpu.VMEM((128, width), jnp.float32),
        ],
        compiler_params=pltpu.CompilerParams(vmem_limit_bytes=56 * 2**20),
        cost_estimate=cost(1e3, 1e3),
        name="project_back",
    )(rows, grads, grad_query, out_logit, projected, sigs, masks, full, full, full, full, gain, bias)


def shift(value, axis, by):
    count = lax.axis_size(axis)
    pairs = [(i, i + by) for i in range(count) if 0 <= i + by < count]
    return lax.ppermute(value, axis, pairs)


def body(
    tokens_in,
    out_grad,
    deal_order,
    seq_lengths,
    value_routes,
    output_routes,
    ffn_routes,
    norm1_gain,
    norm1_bias,
    norm2_gain,
    norm2_bias,
    query_weight,
    key_weight,
    value_weight,
    output_weight,
    value_router,
    output_router,
    ffn_router,
    ffn_in,
    ffn_out,
):
    groups = lax.axis_size("group")
    levels = lax.axis_size("level")
    level = lax.axis_index("level")
    head = lax.axis_index("head")
    count, width = tokens_in.shape
    piece = count // (levels * HEADS)
    wrows = query_weight.shape[0]
    experts = ffn_router.shape[1]
    local_experts = ffn_in.shape[1] // FH

    small = jnp.concatenate(
        [
            ffn_router,
            norm1_gain[:, None],
            norm1_bias[:, None],
            norm2_gain[:, None],
            norm2_bias[:, None],
        ],
        axis=1,
    )
    shared = small.shape[1]
    pad = -(shared + 2 * VEXP) % 128
    extra = jnp.concatenate(
        [
            value_router.reshape(wrows, HEADS, VEXP),
            output_router.reshape(wrows, HEADS, VEXP),
            jnp.broadcast_to(small[:, None, :], (wrows, HEADS, shared)),
            jnp.zeros((wrows, HEADS, pad), jnp.bfloat16),
        ],
        axis=2,
    )
    cols = 2 * DH + 2 * VEXP * DH + extra.shape[2]
    tables = jnp.concatenate(
        [value_routes.transpose(1, 2, 0), output_routes.transpose(1, 2, 0)], axis=1
    )
    picks = ffn_routes.reshape(levels, HEADS * piece, -1).transpose(0, 2, 1)
    arrived, own_grads, full, tables, picks, orders = start(
        tokens_in.reshape(levels, HEADS, piece, width),
        out_grad.reshape(levels, HEADS, piece, width),
        [value_weight, output_weight, query_weight, key_weight],
        extra.transpose(1, 0, 2),
        tables,
        picks,
        deal_order,
    )
    worker_in = arrived.reshape(HEADS * count, width)
    own_tokens = lax.dynamic_index_in_dim(arrived, head, 1, keepdims=False).reshape(count, width)
    in_rows = [turn(ffn_in, "group", k) for k in range(1, groups)]
    full, in_rows = lax.optimization_barrier((full.reshape(width, cols), in_rows))

    base = 2 * DH + 2 * VEXP * DH
    w_output = full[:, VEXP * DH : 2 * VEXP * DH]
    at = base + 2 * VEXP
    def relabelled(expert):
        share = expert // local_experts
        return (share % HEADS * levels + share // HEADS) * local_experts + expert % local_experts

    labels = jnp.arange(experts, dtype=jnp.int32)
    moved = low(relabelled(labels)[:, None] == labels[None, :])
    r_ffn = low(
        jnp.dot(full[:, at : at + experts], moved, preferred_element_type=jnp.float32)
    )
    gain_one, bias_one, gain_two, bias_two = (
        full[:, at + experts + i].astype(jnp.float32) for i in range(4)
    )
    gain_row, bias_row = gain_one[None], bias_one[None]
    orders = orders.reshape(levels, HEADS, count)
    own_order = lax.dynamic_index_in_dim(orders, level, 0, keepdims=False)[:, None, :]
    queries, key_value, projected, sigs, masks = project(
        worker_in, full, gain_row, bias_row, own_order, tables, levels
    )

    rows = HEADS * count
    reach = -(-LMAX // rows)

    ramp = jnp.arange(count, dtype=jnp.int32)

    def arrival(values):
        lead, shape = values.shape[:-3], values.shape[-1:]
        four = values.reshape(lead + (HEADS, levels, HEADS, piece) + shape)
        return jnp.swapaxes(four, -4, -3).reshape(lead + (rows,) + shape)

    orders = jnp.concatenate([jnp.zeros((reach, HEADS, count), jnp.int32), orders], axis=0)
    orders = lax.dynamic_slice_in_dim(orders, level, reach + 1, 0)
    here = orders[:, :, None, :] == ramp[None, None, :, None]
    inverse = jnp.sum(here * ramp, axis=3)
    shard = (level - reach + jnp.arange(reach + 1, dtype=jnp.int32))[:, None] * HEADS
    shard = shard + jnp.arange(HEADS, dtype=jnp.int32)[None, :]
    pos_all = jnp.where(shard[:, :, None] < 0, -1, shard[:, :, None] * count + inverse)
    pos_all = arrival(pos_all[..., None]).reshape(-1)
    positions = pos_all[reach * rows :]
    seq_ends = jnp.cumsum(seq_lengths[0])

    def starts_of(places):
        return jnp.max(jnp.where(seq_ends <= places[:, None], seq_ends, 0), axis=1)

    starts = starts_of(positions)
    blocks = rows // BLOCK
    base_block = (level - reach) * blocks
    first_block = starts_of(level * rows + jnp.arange(blocks, dtype=jnp.int32) * BLOCK) // BLOCK
    first_block = jnp.maximum(first_block - base_block, 0)

    own_routes = picks.reshape(levels, -1, HEADS, piece).transpose(2, 0, 3, 1).reshape(count, -1)
    own_routes = relabelled(own_routes)
    ffn_side = (own_routes, r_ffn, gain_two[None], bias_two[None], own_tokens)

    window = [key_value]
    own_grads = own_grads.reshape(count, width)
    for i in range(reach):
        came = shift(window[0], "level", 1)
        if i == 0:
            came, own_grads, pos_all, starts, ffn_out, in_rows = lax.optimization_barrier(
                (came, own_grads, pos_all, starts, ffn_out, [ffn_in] + in_rows)
            )
            cotangent = level_gather(own_grads, 5, True)
        if i == reach - 1:
            came, cotangent, ffn_side = lax.optimization_barrier((came, cotangent, ffn_side))
        window.insert(0, came)
    place = jnp.stack([head, lax.axis_index("group")])
    out_here = lax.all_gather(ffn_out, "level", axis=0)
    w_in = lax.all_gather(jnp.stack(in_rows), "level", axis=0)


    def lines(values):
        return values.reshape(blocks, 1, BLOCK)

    attended, log_total = attend(
        first_block,
        queries,
        window,
        lines(positions),
        lines(starts),
        pos_all[:, None],
    )

    out_sig = sigs[:, VEXP : 2 * VEXP]
    out_mask = masks[:, VEXP : 2 * VEXP]
    out_gate = out_sig * out_mask
    attended, out_here = lax.optimization_barrier((attended, out_here))
    w_out = [out_here] + [turn(out_here, "group", k) for k in range(1, groups)]
    mixed = low((out_gate[..., None] * attended[:, None, :]).reshape(rows, VEXP * DH))
    branch = level_scatter(low(transposed(mixed, w_output)), 2)

    own_routes, r_ffn, gain_two, bias_two, own_tokens = ffn_side
    middle, extended, ffn_sig = enter_ffn(own_tokens, branch, own_routes, r_ffn, gain_two, bias_two)
    hidden = level_gather(extended, 3, True)
    mine = levels * local_experts
    gates = lax.dynamic_slice_in_dim(hidden, width + head * mine, mine, 1).astype(jnp.float32)
    active, grad_pre, grad_rows = ffn_front(
        place, hidden, cotangent, w_in, w_out, gates, local_experts
    )
    summed, beyond = pair_scatter(grad_rows, 4, True)
    beyond, hidden = lax.optimization_barrier((beyond, hidden))
    came = to_far(beyond)
    grad_in = ffn_rear(place, hidden, grad_pre, width, groups, levels)
    in_came = [turn(grad_in[k], "group", k) for k in range(1, groups)]
    grad_out = ffn_rear(place, cotangent, active, width, groups, levels)
    out_came = [turn(grad_out[k], "group", k) for k in range(1, groups)]
    came, grad_in, grad_out = lax.optimization_barrier((came, grad_in, grad_out))
    grad_middle, own_branch, early = leave_ffn(
        middle, summed, came, own_grads, ffn_sig, own_routes, r_ffn, gain_two, bias_two
    )
    came = to_far(own_branch)
    feed = ffn_feed(place, active, w_out)
    came, feed = lax.optimization_barrier((came, feed))
    grad_branch = pair_gather(own_branch, came, 7)

    def sum_of(own, others):
        total = own[0].astype(jnp.float32)
        for other in others:
            total = total + other.astype(jnp.float32)
        return low(total)

    def over_levels(total):
        return lax.psum_scatter(total, "level", scatter_dimension=0)

    grad_branch, in_came = lax.optimization_barrier((grad_branch, in_came))
    ffn_in_grad = over_levels(sum_of(grad_in, in_came))
    grad_attended, row_inner, grad_out_logit, grad_w_output = branch_back(
        grad_branch, full, attended, sigs, masks
    )
    grad_queries, *grad_window = attend_back(
        first_block,
        queries,
        window,
        grad_attended,
        lines(positions),
        lines(starts),
        log_total,
        row_inner,
        pos_all[:, None],
    )
    came = shift(grad_window[0], "level", -1)
    fed, beyond = pair_scatter(feed, 6, True)
    fed_far = to_far(beyond)
    for i in range(1, reach + 1):
        if i < reach:
            came, fed = lax.optimization_barrier((came, fed))
        else:
            layer_out = to_home(low(middle + fed + fed_far.astype(jnp.float32)))
            came, layer_out = lax.optimization_barrier((came, layer_out))
        grad_both = grad_window[i].astype(jnp.float32) + came.astype(jnp.float32)
        if i < reach:
            grad_keys_sent = low(grad_both)
            came = shift(grad_keys_sent, "level", -1)
    grad_both, out_came = lax.optimization_barrier((grad_both, out_came))
    ffn_out_grad = over_levels(sum_of(grad_out, out_came))
    grad_inputs, late = project_back(
        worker_in,
        grad_both,
        grad_queries,
        grad_out_logit,
        projected,
        sigs,
        masks,
        full,
        gain_row,
        bias_row,
    )


    values = VEXP * DH
    layout = (
        ((0, values, True), (values, DH, True), (values + DH, DH, True), (values + 2 * DH, DH, False)),
        ((0, values, True),),
        ((0, early.shape[1], False),),
    )

    def by_owner(grads):
        return grads.reshape(groups, levels, HEADS, wrows, -1)

    input_grad, grad_value, grad_query, grad_key, sides, grad_output, common = finish(
        layout,
        grad_inputs.reshape(HEADS, HEADS, levels * piece, width),
        grad_middle.reshape(HEADS, levels * piece, width),
        by_owner(late),
        by_owner(grad_w_output),
        by_owner(early),
    )
    norms = jnp.sum(sides[:, :, 2 * VEXP : 2 * VEXP + 2], axis=0)
    common = jnp.sum(common[:, :, : experts + 2], axis=0)
    router_grad = common[:, :experts].reshape(wrows, HEADS, levels, local_experts)

    def side(first):
        return sides[:, :, first : first + VEXP].transpose(1, 0, 2).reshape(wrows, HEADS * VEXP)

    return (
        layer_out,
        input_grad.reshape(count, width),
        norms[:, 0],
        norms[:, 1],
        common[:, experts],
        common[:, experts + 1],
        grad_query,
        grad_key,
        grad_value,
        grad_output,
        side(0),
        side(VEXP),
        jnp.swapaxes(router_grad, 1, 2).reshape(wrows, experts),
        ffn_in_grad.astype(jnp.float32),
        ffn_out_grad.astype(jnp.float32),
    )


def solution(mesh):
    groups, shards = mesh.devices.shape
    fine = Mesh(mesh.devices.reshape(groups, shards // HEADS, HEADS), TOK)
    two, one, three = P(TOK, None), P(TOK), P(TOK, None, None)
    ffn = P("group", ("level", "head"))
    return jax.shard_map(
        body,
        mesh=fine,
        in_specs=(two, two, two, P("group", None), three, three, two, one, one, one, one)
        + (two,) * 7
        + (ffn, ffn),
        out_specs=(two, two, one, one, one, one) + (two,) * 7 + (ffn, ffn),
        check_vma=False,
    )
```

```python
import functools

import jax
import jax.numpy as jnp
from jax import lax
from jax.experimental import pallas as pl
from jax.experimental.pallas import tpu as pltpu
from jax.sharding import Mesh, PartitionSpec as P

HEADS = 4
DH = 128
VEXP = 5
FH = 128
LMAX = 4096

TOK = ("group", "level", "head")


def transposed(left_side, right_side):
    return lax.dot_general(
        left_side, right_side, (((1,), (1,)), ((), ())), preferred_element_type=jnp.float32
    )


def low(value):
    return value.astype(jnp.bfloat16)


def to_home(rows):
    levels = lax.axis_size("level")
    count = rows.shape[0]
    out = rows.reshape(HEADS, levels, count // levels // HEADS, -1).transpose(1, 0, 2, 3)
    back = lax.all_to_all(
        out.reshape(levels, count // levels, -1), "level", split_axis=0, concat_axis=0, tiled=True
    )
    return back.reshape(count, -1)


MESH = pl.DeviceIdType.MESH


def partners(head):
    near = head + 1 - 2 * lax.rem(head, 2)
    far = lax.rem(head + 2, HEADS)
    return near, far


def greet(near, far):
    barrier = pltpu.get_barrier_semaphore()
    for peer in (near, far):
        pl.semaphore_signal(barrier, inc=1, device_id={"head": peer}, device_id_type=MESH)
    pl.semaphore_wait(barrier, 2)


def remote(src, dst, send, recv, peer):
    return pltpu.make_async_remote_copy(
        src_ref=src,
        dst_ref=dst,
        send_sem=send,
        recv_sem=recv,
        device_id={"head": peer},
        device_id_type=MESH,
    )


def cost(flops, moved):
    return pl.CostEstimate(flops=int(flops), bytes_accessed=int(moved), transcendentals=0)


def gather_kernel(
    by_source, own, out, local_sem, near_send, near_recv, far_send, far_recv, pass_send, pass_recv
):
    head = lax.axis_index("head")
    near, far = partners(head)
    greet(near, far)

    def spot(i, source):
        return out.at[source, i] if by_source else out.at[i, source]

    pieces = range(HEADS)
    to_far = [remote(own.at[i], spot(i, head), far_send.at[i], far_recv.at[i], far) for i in pieces]
    to_near = [
        remote(own.at[i], spot(i, head), near_send.at[i], near_recv.at[i], near) for i in pieces
    ]
    passed = [
        remote(spot(i, far), spot(i, far), pass_send.at[i], pass_recv.at[i], near) for i in pieces
    ]
    kept = [pltpu.make_async_copy(own.at[i], spot(i, head), local_sem.at[i]) for i in pieces]
    for copy in to_far + to_near + kept:
        copy.start()
    for i in pieces:
        to_far[i].wait_recv()
        passed[i].start()
    for i in pieces:
        to_near[i].wait_recv()
        passed[i].wait_recv()
        kept[i].wait()
        to_far[i].wait_send()
        to_near[i].wait_send()
        passed[i].wait_send()


def level_gather(rows, collective_id, by_source=False):
    count, width = rows.shape
    whole = pl.pallas_call(
        functools.partial(gather_kernel, by_source),
        out_shape=jax.ShapeDtypeStruct((HEADS, HEADS, count // HEADS, width), rows.dtype),
        in_specs=[pl.BlockSpec(memory_space=pltpu.VMEM)],
        out_specs=pl.BlockSpec(memory_space=pl.ANY),
        scratch_shapes=[pltpu.SemaphoreType.DMA((HEADS,))] * 7,
        compiler_params=pltpu.CompilerParams(collective_id=collective_id, has_side_effects=True),
        cost_estimate=cost(0, 90e6),
        name="level_gather",
    )(rows.reshape(HEADS, count // HEADS, width))
    return whole.reshape(HEADS * count, width)


def scatter_kernel(
    by_source, part, out, near_buf, send_buf, far_buf, near_send, near_recv, far_send, far_recv
):
    head = lax.axis_index("head")
    near, far = partners(head)
    greet(near, far)
    across = HEADS - 1 - head
    pieces = range(HEADS)

    def spot(i, dest):
        return (dest, i) if by_source else (i, dest)

    def to_near(slot, i, dest):
        return remote(
            part.at[spot(i, dest)],
            near_buf.at[slot, i],
            near_send.at[slot, i],
            near_recv.at[slot, i],
            near,
        )

    first = [to_near(0, i, across) for i in pieces]
    second = [to_near(1, i, near) for i in pieces]
    onward = [
        remote(send_buf.at[i], far_buf.at[i], far_send.at[i], far_recv.at[i], far) for i in pieces
    ]
    for copy in first + second:
        copy.start()
    for i in pieces:
        first[i].wait_recv()
        both = part[spot(i, far)].astype(jnp.float32) + near_buf[0, i].astype(jnp.float32)
        send_buf[i] = both.astype(jnp.bfloat16)
        onward[i].start()
    for i in pieces:
        second[i].wait_recv()
        out[i] = part[spot(i, head)].astype(jnp.float32) + near_buf[1, i].astype(jnp.float32)
    for i in pieces:
        onward[i].wait_recv()
        out[i] = out[i] + far_buf[i].astype(jnp.float32)
    for i in pieces:
        first[i].wait_send()
        second[i].wait_send()
        onward[i].wait_send()


def level_scatter(rows, collective_id, by_source=False):
    total, width = rows.shape
    piece = total // (HEADS * HEADS)
    low_type = jnp.bfloat16
    mine = pl.pallas_call(
        functools.partial(scatter_kernel, by_source),
        out_shape=jax.ShapeDtypeStruct((HEADS, piece, width), jnp.float32),
        in_specs=[pl.BlockSpec(memory_space=pltpu.VMEM)],
        out_specs=pl.BlockSpec(memory_space=pltpu.VMEM),
        scratch_shapes=[
            pltpu.VMEM((2, HEADS, piece, width), low_type),
            pltpu.VMEM((HEADS, piece, width), low_type),
            pltpu.VMEM((HEADS, piece, width), low_type),
            pltpu.SemaphoreType.DMA((2, HEADS)),
            pltpu.SemaphoreType.DMA((2, HEADS)),
            pltpu.SemaphoreType.DMA((HEADS,)),
            pltpu.SemaphoreType.DMA((HEADS,)),
        ],
        compiler_params=pltpu.CompilerParams(
            collective_id=collective_id, has_side_effects=True, vmem_limit_bytes=32 * 2**20
        ),
        cost_estimate=cost(0, 80e6),
        name="level_scatter",
    )(rows.reshape(HEADS, HEADS, piece, width))
    return mine.reshape(HEADS * piece, width)


def meet(near):
    barrier = pltpu.get_barrier_semaphore()
    pl.semaphore_signal(barrier, inc=1, device_id={"head": near}, device_id_type=MESH)
    pl.semaphore_wait(barrier, 1)


def pair_scatter_kernel(by_source, part, out, out_far, near_buf, send, recv):
    head = lax.axis_index("head")
    near, far = partners(head)
    meet(near)
    across = HEADS - 1 - head
    pieces = range(HEADS)

    def spot(i, dest):
        return (dest, i) if by_source else (i, dest)

    def to_near(slot, i, dest):
        return remote(
            part.at[spot(i, dest)], near_buf.at[slot, i], send.at[slot, i], recv.at[slot, i], near
        )

    first = [to_near(0, i, across) for i in pieces]
    second = [to_near(1, i, near) for i in pieces]
    for copy in first + second:
        copy.start()
    for i in pieces:
        first[i].wait_recv()
        both = part[spot(i, far)].astype(jnp.float32) + near_buf[0, i].astype(jnp.float32)
        out_far[i] = both.astype(jnp.bfloat16)
    for i in pieces:
        second[i].wait_recv()
        out[i] = part[spot(i, head)].astype(jnp.float32) + near_buf[1, i].astype(jnp.float32)
    for i in pieces:
        first[i].wait_send()
        second[i].wait_send()


def pair_scatter(rows, collective_id, by_source=False):
    total, width = rows.shape
    piece = total // (HEADS * HEADS)
    mine, other = pl.pallas_call(
        functools.partial(pair_scatter_kernel, by_source),
        out_shape=[
            jax.ShapeDtypeStruct((HEADS, piece, width), jnp.float32),
            jax.ShapeDtypeStruct((HEADS, piece, width), jnp.bfloat16),
        ],
        in_specs=[pl.BlockSpec(memory_space=pltpu.VMEM)],
        out_specs=[pl.BlockSpec(memory_space=pltpu.VMEM)] * 2,
        scratch_shapes=[
            pltpu.VMEM((2, HEADS, piece, width), jnp.bfloat16),
            pltpu.SemaphoreType.DMA((2, HEADS)),
            pltpu.SemaphoreType.DMA((2, HEADS)),
        ],
        compiler_params=pltpu.CompilerParams(
            collective_id=collective_id, has_side_effects=True, vmem_limit_bytes=32 * 2**20
        ),
        cost_estimate=cost(0, 25e6),
        name="pair_scatter",
    )(rows.reshape(HEADS, HEADS, piece, width))
    return mine.reshape(HEADS * piece, width), other.reshape(HEADS * piece, width)


def pair_gather_kernel(by_source, own, other, out, local_sem, send, recv):
    head = lax.axis_index("head")
    near, far = partners(head)
    meet(near)
    copies, kept = [], []
    for i in range(HEADS):
        for slot, (block, source) in enumerate(((own, head), (other, far))):
            place = out.at[source, i] if by_source else out.at[i, source]
            copies.append(
                remote(block.at[i], place, send.at[slot, i], recv.at[slot, i], near)
            )
            kept.append(pltpu.make_async_copy(block.at[i], place, local_sem.at[slot, i]))
    for copy in copies + kept:
        copy.start()
    for copy in copies + kept:
        copy.wait()


def pair_gather(own, other, collective_id, by_source=False):
    count, width = own.shape
    split = (HEADS, count // HEADS, width)
    whole = pl.pallas_call(
        functools.partial(pair_gather_kernel, by_source),
        out_shape=jax.ShapeDtypeStruct((HEADS,) + split, own.dtype),
        in_specs=[pl.BlockSpec(memory_space=pltpu.VMEM)] * 2,
        out_specs=pl.BlockSpec(memory_space=pl.ANY),
        scratch_shapes=[pltpu.SemaphoreType.DMA((2, HEADS))] * 3,
        compiler_params=pltpu.CompilerParams(collective_id=collective_id, has_side_effects=True),
        cost_estimate=cost(0, 25e6),
        name="pair_gather",
    )(own.reshape(split), other.reshape(split))
    return whole.reshape(HEADS * count, width)


def to_far(rows):
    return lax.ppermute(rows, "head", [(i, (i + 2) % HEADS) for i in range(HEADS)])


def ring(axis):
    me, size = lax.axis_index(axis), lax.axis_size(axis)
    ahead = [lax.rem(me + k, size) for k in range(1, size)]
    behind = [lax.rem(me + size - k, size) for k in range(1, size)]
    return me, ahead, behind


def reach_out(src, dst, send, recv, peer):
    return pltpu.make_async_remote_copy(
        src_ref=src, dst_ref=dst, send_sem=send, recv_sem=recv, device_id=peer, device_id_type=MESH
    )


def greet_all(peers):
    barrier = pltpu.get_barrier_semaphore()
    for peer in peers:
        pl.semaphore_signal(barrier, inc=1, device_id=peer, device_id_type=MESH)
    pl.semaphore_wait(barrier, len(peers))


def start_kernel(
    tokens, cotangents, value, output, query, key, extra, tables, picks, order,
    rows, grads, full, routes, chosen_rows, orders, weights, own_sem, *sems
):
    sems = iter(sems)

    def pair():
        return next(sems), next(sems)

    group, groups_ahead, _ = ring("group")
    level, levels_ahead, levels_behind = ring("level")
    head = lax.axis_index("head")
    near, far = partners(head)
    mates = [near, far, HEADS - 1 - head]
    for to in range(HEADS):
        at = 0
        for part in (value, output, query, key):
            size = part.shape[1] // HEADS
            weights[to, :, at : at + size] = part[:, to * size : (to + 1) * size]
            at += size
        weights[to, :, at:] = extra[to]
    greet_all(
        [{"head": m} for m in mates]
        + [{"level": n} for n in levels_ahead]
        + [{"group": n} for n in groups_ahead]
    )
    started = []

    def send(src, dst, send_sem, recv_sem, peer):
        copy = reach_out(src, dst, send_sem, recv_sem, peer)
        copy.start()
        started.append(copy)
        return copy

    out_s, out_r = pair()
    pick_s, pick_r = pair()
    crossing, picking = [], []
    for k, to in enumerate(levels_ahead):
        peer = {"level": to}
        crossing.append(send(tokens.at[to], rows.at[:, head, level], out_s.at[k], out_r.at[k], peer))
    mate_s, mate_r = pair()
    table_s, table_r = pair()
    order_s, order_r = pair()
    to_mates, order_mates, table_mates = [], [], []
    for k, to in enumerate(mates):
        peer = {"head": to}
        to_mates.append(
            send(weights.at[to], full.at[group, level, head], mate_s.at[k], mate_r.at[k], peer)
        )
        order_mates.append(
            send(order, orders.at[level, head], order_s.at[k], order_r.at[k], peer)
        )
    own = [
        (tokens.at[level], rows.at[:, head, level]),
        (weights.at[head], full.at[group, level, head]),
        (tables.at[head], routes.at[head]),
        (picks.at[level], chosen_rows.at[level]),
        (order, orders.at[level, head]),
        (cotangents.at[level], grads.at[:, level]),
    ]
    own = [pltpu.make_async_copy(src, dst, own_sem.at[i]) for i, (src, dst) in enumerate(own)]
    for copy in own:
        copy.start()
    far_s, far_r = pair()
    near_s, near_r = pair()
    pass_s, pass_r = pair()
    to_far, to_near = [], []

    def share(k, src, source):
        place = rows.at[:, head, source]
        to_far.append(send(src, place, far_s.at[k], far_r.at[k], {"head": far}))
        to_near.append(send(src, place, near_s.at[k], near_r.at[k], {"head": near}))

    share(0, tokens.at[level], level)
    block_s, block_r = pair()
    group_s, group_r = pair()
    orders_s, orders_r = pair()
    for copy in to_mates:
        copy.wait_recv()
    own[1].wait()
    blocks, grouped, ordered = [], [], []

    def to_groups(j, source):
        for k, to in enumerate(groups_ahead):
            block = full.at[group, source]
            grouped.append(
                send(block, block, group_s.at[k, j], group_r.at[k, j], {"group": to})
            )

    for k, to in enumerate(levels_ahead):
        block = full.at[group, level]
        blocks.append(send(block, block, block_s.at[k], block_r.at[k], {"level": to}))
    to_groups(0, level)
    for k, to in enumerate(mates):
        table_mates.append(
            send(tables.at[to], routes.at[head], table_s.at[k], table_r.at[k], {"head": to})
        )
    for k, to in enumerate(levels_ahead):
        picking.append(
            send(picks.at[to], chosen_rows.at[level], pick_s.at[k], pick_r.at[k], {"level": to})
        )
    for copy in order_mates:
        copy.wait_recv()
    own[4].wait()
    for k, to in enumerate(levels_ahead):
        block = orders.at[level]
        ordered.append(send(block, block, orders_s.at[k], orders_r.at[k], {"level": to}))
    for k, source in enumerate(levels_behind):
        crossing[k].wait_recv()
        share(k + 1, rows.at[:, head, source], source)
    grad_s, grad_r = pair()
    crossed = []
    for k, to in enumerate(levels_ahead):
        crossed.append(
            send(cotangents.at[to], grads.at[:, level], grad_s.at[k], grad_r.at[k], {"level": to})
        )
    for k, source in enumerate(levels_behind):
        blocks[k].wait_recv()
        to_groups(k + 1, source)
    passed = []
    for k, source in enumerate([level] + levels_behind):
        to_far[k].wait_recv()
        place = rows.at[:, far, source]
        passed.append(send(place, place, pass_s.at[k], pass_r.at[k], {"head": near}))
    for copy in to_near + passed + grouped + table_mates + picking + ordered + crossed:
        copy.wait_recv()
    for copy in started:
        copy.wait_send()
    for i in (0, 2, 3, 5):
        own[i].wait()


def start(tokens, cotangents, weights, extra, tables, picks, order):
    groups, levels = lax.axis_size("group"), lax.axis_size("level")
    _, _, piece, width = tokens.shape
    columns = sum(part.shape[1] for part in weights) // HEADS + extra.shape[2]
    block = extra.shape[:2] + (columns,)
    shapes = [
        jax.ShapeDtypeStruct((HEADS, HEADS, levels, piece, width), tokens.dtype),
        jax.ShapeDtypeStruct((HEADS, levels, piece, width), tokens.dtype),
        jax.ShapeDtypeStruct((groups, levels) + block, extra.dtype),
        jax.ShapeDtypeStruct(tables.shape, tables.dtype),
        jax.ShapeDtypeStruct(picks.shape, picks.dtype),
        jax.ShapeDtypeStruct((levels, HEADS) + order.shape, order.dtype),
    ]
    dma = pltpu.SemaphoreType.DMA
    others, mates = (levels - 1,), (HEADS - 1,)
    counts = [others] * 2 + [mates] * 3 + [(levels,)] * 3
    counts += [others, (groups - 1, levels), others, others]
    return pl.pallas_call(
        start_kernel,
        out_shape=shapes,
        in_specs=[pl.BlockSpec(memory_space=pltpu.VMEM)] * 10,
        out_specs=[pl.BlockSpec(memory_space=pl.ANY)] * 6,
        scratch_shapes=[pltpu.VMEM(block, extra.dtype), dma((6,))] + [dma(c) for c in counts for _ in range(2)],
        compiler_params=pltpu.CompilerParams(collective_id=9, has_side_effects=True),
        cost_estimate=cost(0, 200e6),
        name="start",
    )(tokens, cotangents, *weights, extra, tables, picks, order)


def finish_kernel(layout, *refs):
    refs = iter(refs)
    count = len(layout)

    def take(n):
        return [next(refs) for _ in range(n)]

    part, middle = take(2)
    grads = take(count)
    (home_grad,) = take(1)
    results = [take(len(pieces)) for pieces in layout]
    near_buf, send_buf, far_buf, total, back_buf, came_buf = take(6)
    group_buf, level_send, level_buf, head_send, owned = (take(count) for _ in range(5))

    def pair():
        return next(refs), next(refs)

    group, groups_ahead, _ = ring("group")
    level, levels_ahead, levels_behind = ring("level")
    head = lax.axis_index("head")
    near, far = partners(head)
    across = HEADS - 1 - head
    mates = [near, far, across]
    greet_all(
        [{"head": m} for m in mates]
        + [{"level": n} for n in levels_ahead]
        + [{"group": n} for n in groups_ahead]
    )
    started = []

    def send(src, dst, send_sem, recv_sem, peer):
        copy = reach_out(src, dst, send_sem, recv_sem, peer)
        copy.start()
        started.append(copy)
        return copy

    pieces = range(HEADS)
    sets = range(count)
    near_s, near_r = pair()
    far_s, far_r = pair()
    back_s, back_r = pair()
    group_s, group_r = pair()
    level_s, level_r = pair()
    mate_s, mate_r = pair()
    first, second, onward = [], [], []
    for slot, (dest, copies) in enumerate(((across, first), (near, second))):
        for i in pieces:
            copies.append(
                send(
                    part.at[i, dest],
                    near_buf.at[slot, i],
                    near_s.at[slot, i],
                    near_r.at[slot, i],
                    {"head": near},
                )
            )
    order = levels_ahead + [level]
    grouped = {}
    for j, dest in enumerate(order):
        for p in sets:
            grouped[j, p] = [
                send(
                    grads[p].at[to, dest],
                    group_buf[p].at[k, j],
                    group_s.at[p, k, j],
                    group_r.at[p, k, j],
                    {"group": to},
                )
                for k, to in enumerate(groups_ahead)
            ]
    for i in pieces:
        first[i].wait_recv()
        both = part[i, far].astype(jnp.float32) + near_buf[0, i].astype(jnp.float32)
        send_buf[i] = both.astype(jnp.bfloat16)
        onward.append(send(send_buf.at[i], far_buf.at[i], far_s.at[i], far_r.at[i], {"head": far}))
    for i in pieces:
        second[i].wait_recv()
        both = part[i, head].astype(jnp.float32) + near_buf[1, i].astype(jnp.float32)
        total[i] = both + middle[i]
    leveled = {}
    for j, dest in enumerate(order):
        for p in sets:
            amount = grads[p][group, dest].astype(jnp.float32)
            for k, copy in enumerate(grouped[j, p]):
                copy.wait_recv()
                amount = amount + group_buf[p][k, j].astype(jnp.float32)
            level_send[p][j] = amount.astype(jnp.bfloat16)
            if j < len(levels_ahead):
                leveled[j, p] = send(
                    level_send[p].at[j],
                    level_buf[p].at[j],
                    level_s.at[p, j],
                    level_r.at[p, j],
                    {"level": dest},
                )
    for i in pieces:
        onward[i].wait_recv()
        both = total[i] + far_buf[i].astype(jnp.float32)
        back_buf[i] = both.astype(jnp.bfloat16).reshape(back_buf.shape[1:])
    backs = [
        send(back_buf.at[:, to], came_buf.at[level], back_s.at[k], back_r.at[k], {"level": to})
        for k, to in enumerate(levels_ahead)
    ]
    sharing = []
    for p in sets:
        amount = level_send[p][len(levels_ahead)].astype(jnp.float32)
        for j in range(len(levels_ahead)):
            leveled[j, p].wait_recv()
            amount = amount + level_buf[p][j].astype(jnp.float32)
        head_send[p][...] = amount.astype(jnp.bfloat16)
        sharing += [
            send(
                head_send[p].at[to],
                owned[p].at[head],
                mate_s.at[p, k],
                mate_r.at[p, k],
                {"head": to},
            )
            for k, to in enumerate(mates)
        ]
        owned[p][head] = head_send[p][head]
    home_grad[level] = back_buf[:, level].astype(jnp.float32)
    for k, source in enumerate(levels_behind):
        backs[k].wait_recv()
        home_grad[source] = came_buf[source].astype(jnp.float32)
    for copy in sharing:
        copy.wait_recv()
    for p in sets:
        for out, (first_column, size, joined) in zip(results[p], layout[p]):
            for h in range(HEADS):
                value = owned[p][h, :, first_column : first_column + size].astype(jnp.float32)
                if joined:
                    out[:, h * size : (h + 1) * size] = value
                else:
                    out[h] = value
    for copy in started:
        copy.wait_send()


def finish(layout, part, middle, *grads):
    groups, levels = lax.axis_size("group"), lax.axis_size("level")
    _, count, width = middle.shape
    piece = count // levels
    low_type = jnp.bfloat16
    blocks = [grad.shape[2:] for grad in grads]
    sets = len(grads)
    dma = pltpu.SemaphoreType.DMA
    counts = [(2, HEADS), (HEADS,), (levels - 1,)]
    counts += [(sets, groups - 1, levels), (sets, levels - 1), (sets, HEADS - 1)]
    vmem = pl.BlockSpec(memory_space=pltpu.VMEM)
    shapes = []
    for pieces in layout:
        for _, size, joined in pieces:
            shape = (blocks[0][1], HEADS * size) if joined else (HEADS, blocks[0][1], size)
            shapes.append(jax.ShapeDtypeStruct(shape, jnp.float32))
    return pl.pallas_call(
        functools.partial(finish_kernel, layout),
        out_shape=[jax.ShapeDtypeStruct((levels, HEADS, piece, width), jnp.float32)] + shapes,
        in_specs=[vmem] * (2 + sets),
        out_specs=[vmem] * (1 + len(shapes)),
        scratch_shapes=[
            pltpu.VMEM((2, HEADS, count, width), low_type),
            pltpu.VMEM((HEADS, count, width), low_type),
            pltpu.VMEM((HEADS, count, width), low_type),
            pltpu.VMEM((HEADS, count, width), jnp.float32),
            pltpu.VMEM((HEADS, levels, piece, width), low_type),
            pltpu.VMEM((levels, HEADS, piece, width), low_type),
        ]
        + [pltpu.VMEM((groups - 1, levels) + block, low_type) for block in blocks]
        + [pltpu.VMEM((levels,) + block, low_type) for block in blocks]
        + [pltpu.VMEM((levels - 1,) + block, low_type) for block in blocks]
        + [pltpu.VMEM(block, low_type) for block in blocks] * 2
        + [dma(c) for c in counts for _ in range(2)],
        compiler_params=pltpu.CompilerParams(
            collective_id=10, has_side_effects=True, vmem_limit_bytes=56 * 2**20
        ),
        cost_estimate=cost(0, 200e6),
        name="finish",
    )(part, middle, *grads)


BLOCK = 512
LOG2E = 1.4426950408889634


def dot(left_side, right_side, left_dim, right_dim):
    return lax.dot_general(
        left_side,
        right_side,
        (((left_dim,), (right_dim,)), ((), ())),
        preferred_element_type=jnp.float32,
    )


def run_blocks(step, part, parts, blocks, at, first, clear):
    def local(block):
        return jnp.clip(block - part * blocks, 0, blocks)

    own = (parts - 1) * blocks + at
    begin, middle, end = local(first), local(jnp.clip(clear, first, own)), local(own)
    lax.fori_loop(begin, middle, functools.partial(step, True), 0)
    lax.fori_loop(middle, end, functools.partial(step, False), 0)
    if part == parts - 1:
        step(True, at, 0)


def attend_kernel(parts, first, clear, q, *refs):
    keys, values = refs[:parts], refs[parts : 2 * parts]
    pos_q, start_q, pos_k, out, lse, top, total, acc = refs[2 * parts :]
    at = pl.program_id(0)
    blocks = pl.num_programs(0)
    rate = LOG2E * DH ** (-0.5)
    top[...] = jnp.full_like(top, -1e30)
    total[...] = jnp.zeros_like(total)
    acc[...] = jnp.zeros_like(acc)
    query = q[...]
    row_at, row_from = pos_q[0], start_q[0]

    for part in range(parts):

        def step(masked, block, carry, k=keys[part], v=values[part], part=part):
            rows = pl.ds(pl.multiple_of(block * BLOCK, BLOCK), BLOCK)
            spot = pl.ds(pl.multiple_of((part * blocks + block) * BLOCK, BLOCK), BLOCK)
            scores = dot(k[rows, :], query, 1, 1)
            if masked:
                key_at = pos_k[spot, :]
                scores = jnp.where((key_at >= row_from) & (key_at <= row_at), scores, -1e30)
            old = top[...]
            new = jnp.maximum(old, jnp.max(scores, axis=0, keepdims=True))
            shrink = jnp.exp2((old - new) * rate)
            weight = jnp.exp2((scores - new) * rate)
            total[...] = total[...] * shrink + jnp.sum(weight, axis=0, keepdims=True)
            acc[...] = acc[...] * shrink + dot(v[rows, :], weight.astype(jnp.bfloat16), 0, 0)
            top[...] = new
            return carry

        run_blocks(step, part, parts, blocks, at, first[at], clear[at])
    out[...] = (acc[...] / total[...]).T
    lse[0] = top[...] * rate + jnp.log2(total[...])


def attend(first, clear, queries, window, pos_q, start_q, pos_k):
    rows = queries.shape[0]
    parts = len(window)
    line = pl.BlockSpec((1, 1, BLOCK), lambda i, *_: (i, 0, 0))
    grid_spec = pltpu.PrefetchScalarGridSpec(
        num_scalar_prefetch=2,
        grid=(rows // BLOCK,),
        in_specs=[pl.BlockSpec((BLOCK, DH), lambda i, *_: (i, 0))]
        + [pl.BlockSpec((rows, DH), lambda i, *_: (0, 0))] * parts
        + [pl.BlockSpec((rows, DH), lambda i, *_: (0, 1))] * parts
        + [line, line, pl.BlockSpec((parts * rows, 1), lambda i, *_: (0, 0))],
        out_specs=[pl.BlockSpec((BLOCK, DH), lambda i, *_: (i, 0)), line],
        scratch_shapes=[
            pltpu.VMEM((1, BLOCK), jnp.float32),
            pltpu.VMEM((1, BLOCK), jnp.float32),
            pltpu.VMEM((DH, BLOCK), jnp.float32),
        ],
    )
    return pl.pallas_call(
        functools.partial(attend_kernel, parts),
        grid_spec=grid_spec,
        out_shape=[
            jax.ShapeDtypeStruct((rows, DH), jnp.float32),
            jax.ShapeDtypeStruct((rows // BLOCK, 1, BLOCK), jnp.float32),
        ],
        compiler_params=pltpu.CompilerParams(vmem_limit_bytes=48 * 2**20),
        cost_estimate=cost(2e10, 1e7),
        name="attend",
    )(first, clear, queries, *window, *window, pos_q, start_q, pos_k)


def attend_back_kernel(parts, first, clear, q, *refs):
    keys, values = refs[:parts], refs[parts : 2 * parts]
    grad, pos_q, start_q, lse, inner, pos_k, grad_q = refs[2 * parts : 2 * parts + 7]
    grads = refs[2 * parts + 7 : 3 * parts + 7]
    sum_k, sum_v, acc = refs[3 * parts + 7 :]
    at = pl.program_id(0)
    blocks = pl.num_programs(0)
    rate = LOG2E * DH ** (-0.5)
    scale = DH ** (-0.5)

    @pl.when(at == 0)
    def _():
        sum_k[...] = jnp.zeros_like(sum_k)
        sum_v[...] = jnp.zeros_like(sum_v)

    acc[...] = jnp.zeros_like(acc)
    query, grad_out = q[...], grad[...]
    row_at, row_from, row_lse, row_inner = pos_q[0], start_q[0], lse[0], inner[0]

    for part in range(parts):

        def step(masked, block, carry, k=keys[part], v=values[part], part=part):
            rows = pl.ds(pl.multiple_of(block * BLOCK, BLOCK), BLOCK)
            spot = pl.ds(pl.multiple_of((part * blocks + block) * BLOCK, BLOCK), BLOCK)
            key, value = k[rows, :], v[rows, :]
            scores = dot(key, query, 1, 1)
            soft = jnp.exp2(scores * rate - row_lse)
            if masked:
                key_at = pos_k[spot, :]
                soft = jnp.where((key_at >= row_from) & (key_at <= row_at), soft, 0.0)
            grad_soft = dot(value, grad_out, 1, 1)
            grad_scores = (soft * (grad_soft - row_inner)).astype(jnp.bfloat16)
            sum_v[spot, :] += dot(soft.astype(jnp.bfloat16), grad_out, 1, 0)
            sum_k[spot, :] += dot(grad_scores, query, 1, 0)
            acc[...] += dot(grad_scores, key, 0, 0)
            return carry

        run_blocks(step, part, parts, blocks, at, first[at], clear[at])
    grad_q[...] = (acc[...] * scale).astype(jnp.bfloat16)

    @pl.when(at == blocks - 1)
    def _():
        size = grads[0].shape[0]
        for part in range(parts):
            spot = slice(part * size, (part + 1) * size)
            grads[part][:, :DH] = (sum_k[spot, :] * scale).astype(grads[part].dtype)
            grads[part][:, DH:] = sum_v[spot, :].astype(grads[part].dtype)


def attend_back(first, clear, queries, window, grads, pos_q, start_q, lse, inner, pos_k):
    rows = queries.shape[0]
    parts = len(window)
    block = pl.BlockSpec((BLOCK, DH), lambda i, *_: (i, 0))
    line = pl.BlockSpec((1, 1, BLOCK), lambda i, *_: (i, 0, 0))
    grid_spec = pltpu.PrefetchScalarGridSpec(
        num_scalar_prefetch=2,
        grid=(rows // BLOCK,),
        in_specs=[block]
        + [pl.BlockSpec((rows, DH), lambda i, *_: (0, 0))] * parts
        + [pl.BlockSpec((rows, DH), lambda i, *_: (0, 1))] * parts
        + [block, line, line, line, line]
        + [pl.BlockSpec((parts * rows, 1), lambda i, *_: (0, 0))],
        out_specs=[block] + [pl.BlockSpec((rows, 2 * DH), lambda i, *_: (0, 0))] * parts,
        scratch_shapes=[
            pltpu.VMEM((parts * rows, DH), jnp.float32),
            pltpu.VMEM((parts * rows, DH), jnp.float32),
            pltpu.VMEM((BLOCK, DH), jnp.float32),
        ],
    )
    kinds = [jnp.bfloat16] * (parts - 1) + [jnp.float32]
    return pl.pallas_call(
        functools.partial(attend_back_kernel, parts),
        grid_spec=grid_spec,
        out_shape=[jax.ShapeDtypeStruct((rows, DH), jnp.bfloat16)]
        + [jax.ShapeDtypeStruct((rows, 2 * DH), kind) for kind in kinds],
        compiler_params=pltpu.CompilerParams(vmem_limit_bytes=48 * 2**20),
        cost_estimate=cost(2e9, 1e6),
        name="attend_back",
    )(first, clear, queries, *window, *window, grads, pos_q, start_q, lse, inner, pos_k)


def columns_of(ref, group, groups, step, depth):
    at = lax.rem(group + step + groups, groups) * depth
    return ref.at[:, pl.ds(pl.multiple_of(at, 128), depth)]


def front_kernel(groups, local, place, hidden, grads, *refs):
    w_in, w_out = refs[0], refs[1 : groups + 1]
    gates, active, grad_pre, rows_out, turned, acc = refs[groups + 1 :]
    levels, _, depth, width = w_in.shape
    tile = hidden.shape[0]
    model = groups * depth
    parts = [slice(step * depth, (step + 1) * depth) for step in range(groups)]
    for step in range(groups):
        turned[0, :, parts[step]] = columns_of(hidden, place[1], groups, -step, depth)[...]
        turned[1, :, parts[step]] = columns_of(grads, place[1], groups, -step, depth)[...]
    gate_grads = []
    for level in range(levels):
        pre_act = jnp.zeros((tile, width), jnp.float32)
        grad_active = jnp.zeros((tile, width), jnp.float32)
        for step in range(groups):
            pre_act += dot(turned[0, :, parts[step]], w_in[level, step], 1, 0)
            grad_active += dot(turned[1, :, parts[step]], w_out[step][level], 1, 0)
        first = level * local
        gate = jnp.concatenate(
            [jnp.broadcast_to(gates[:, first + e : first + e + 1], (tile, FH)) for e in range(local)],
            axis=1,
        )
        sig = 1.0 / (1.0 + jnp.exp2(-LOG2E * pre_act))
        act_pre = pre_act * sig
        columns = slice(level * width, (level + 1) * width)
        active[:, columns] = (act_pre * gate).astype(jnp.bfloat16)
        product = grad_active * act_pre
        for e in range(local):
            gate_grads.append(
                jnp.sum(product[:, e * FH : (e + 1) * FH], axis=1, keepdims=True)
            )
        slope = sig * (1.0 + pre_act * (1.0 - sig))
        low_pre = (grad_active * gate * slope).astype(jnp.bfloat16)
        grad_pre[:, columns] = low_pre
        for step in range(groups):
            back = dot(low_pre, w_in[level, step], 1, 1)
            acc[:, parts[step]] = back if level == 0 else acc[:, parts[step]] + back
    for step in range(groups):
        columns_of(rows_out, place[1], groups, -step, depth)[...] = acc[:, parts[step]].astype(
            jnp.bfloat16
        )
    spare = rows_out.shape[1] - model
    lane = lax.broadcasted_iota(jnp.int32, (tile, spare), 1) - place[0] * (levels * local)
    spread = jnp.zeros((tile, spare), jnp.float32)
    for e, column in enumerate(gate_grads):
        spread = jnp.where(lane == e, column, spread)
    rows_out[:, model:] = spread.astype(jnp.bfloat16)


def ffn_front(place, hidden, grads, w_in, w_out, gates, local):
    rows, wide = hidden.shape
    levels, groups, depth, width = w_in.shape
    tile = 512

    def by_row(columns):
        return pl.BlockSpec((tile, columns), lambda i, *_: (i, 0))

    once = pl.Buffered(1)
    whole = pl.BlockSpec(w_out[0].shape, lambda i, *_: (0, 0, 0), pipeline_mode=once)
    stacked = pl.BlockSpec(w_in.shape, lambda i, *_: (0, 0, 0, 0), pipeline_mode=once)
    grid_spec = pltpu.PrefetchScalarGridSpec(
        num_scalar_prefetch=1,
        grid=(rows // tile,),
        in_specs=[by_row(wide), by_row(groups * depth)]
        + [stacked]
        + [whole] * groups
        + [by_row(gates.shape[1])],
        out_specs=[by_row(levels * width), by_row(levels * width), by_row(wide)],
        scratch_shapes=[
            pltpu.VMEM((2, tile, groups * depth), jnp.bfloat16),
            pltpu.VMEM((tile, groups * depth), jnp.float32),
        ],
    )
    hidden_units = jax.ShapeDtypeStruct((rows, levels * width), jnp.bfloat16)
    return pl.pallas_call(
        functools.partial(front_kernel, groups, local),
        grid_spec=grid_spec,
        out_shape=[hidden_units, hidden_units, jax.ShapeDtypeStruct((rows, wide), jnp.bfloat16)],
        compiler_params=pltpu.CompilerParams(vmem_limit_bytes=58 * 2**20),
        cost_estimate=cost(6 * rows * groups * depth * levels * width, 3e7),
        name="ffn_front",
    )(place, hidden, grads, w_in, *w_out, gates)


def rear_kernel(groups, place, rows_in, hidden_units, *weight_grads):
    _, depth, _ = weight_grads[0].shape
    units = hidden_units[...]
    for step in range(groups):
        part = columns_of(rows_in, place[1], groups, step, depth)
        weight_grads[step][0] = dot(part[...], units, 0, 0).astype(jnp.bfloat16)


def feed_kernel(groups, place, active, *refs):
    weights = refs[:groups]
    feed, acc = refs[groups:]
    _, depth, _ = weights[0].shape
    level = pl.program_id(0)
    act = active[...]
    for step in range(groups):
        fed = dot(act, weights[step][0], 1, 1)
        part = slice(step * depth, (step + 1) * depth)

        @pl.when(level == 0)
        def _():
            acc[:, part] = fed

        @pl.when(level > 0)
        def _():
            acc[:, part] += fed

    @pl.when(level == pl.num_programs(0) - 1)
    def _():
        for step in range(groups):
            part = slice(step * depth, (step + 1) * depth)
            columns_of(feed, place[1], groups, -step, depth)[...] = acc[:, part].astype(
                jnp.bfloat16
            )


def whole_rows(rows, columns):
    return pl.BlockSpec((rows, columns), lambda i, *_: (0, 0), pipeline_mode=pl.Buffered(1))


def ffn_feed(place, active, weights):
    rows = active.shape[0]
    groups = len(weights)
    levels, depth, width = weights[0].shape
    return pl.pallas_call(
        functools.partial(feed_kernel, groups),
        grid_spec=pltpu.PrefetchScalarGridSpec(
            num_scalar_prefetch=1,
            grid=(levels,),
            in_specs=[pl.BlockSpec((rows, width), lambda i, *_: (0, i))]
            + [pl.BlockSpec((1, depth, width), lambda i, *_: (i, 0, 0))] * groups,
            out_specs=whole_rows(rows, groups * depth),
            scratch_shapes=[pltpu.VMEM((rows, groups * depth), jnp.float32)],
        ),
        out_shape=jax.ShapeDtypeStruct((rows, groups * depth), jnp.bfloat16),
        compiler_params=pltpu.CompilerParams(vmem_limit_bytes=58 * 2**20),
        cost_estimate=cost(1e3, 1e3),
        name="ffn_feed",
    )(place, active, *weights)


def ffn_rear(place, rows_in, units, model, groups, levels):
    rows, wide = rows_in.shape
    width = units.shape[1] // levels
    depth = model // groups
    return pl.pallas_call(
        functools.partial(rear_kernel, groups),
        grid_spec=pltpu.PrefetchScalarGridSpec(
            num_scalar_prefetch=1,
            grid=(levels,),
            in_specs=[
                whole_rows(rows, wide),
                pl.BlockSpec((rows, width), lambda i, *_: (0, i)),
            ],
            out_specs=[pl.BlockSpec((1, depth, width), lambda i, *_: (i, 0, 0))] * groups,
        ),
        out_shape=[jax.ShapeDtypeStruct((levels, depth, width), jnp.bfloat16)] * groups,
        compiler_params=pltpu.CompilerParams(vmem_limit_bytes=58 * 2**20),
        cost_estimate=cost(1e3, 1e3),
        name="ffn_rear",
    )(place, rows_in, units)


def named_by(routes, count):
    lane = lax.broadcasted_iota(jnp.int32, (routes.shape[0], count), 1)
    member = jnp.zeros(lane.shape, jnp.float32)
    for slot in range(routes.shape[1]):
        member = jnp.where(lane == routes[:, slot : slot + 1], 1.0, member)
    return member


def middle_kernel(rows, branch, routes, router, gain, bias, middle, extended, sig_out):
    experts = router.shape[1]
    width = rows.shape[1]
    rounded = branch[...].astype(jnp.bfloat16).astype(jnp.float32)
    value = rows[...].astype(jnp.float32) + rounded
    middle[...] = value
    _, _, normed = normalized(value, gain[...], bias[...])
    sig = 1.0 / (1.0 + jnp.exp2(-LOG2E * dot(normed, router[...], 1, 0)))
    sig_out[...] = sig
    extended[:, :width] = value.astype(jnp.bfloat16)
    gates = (sig * named_by(routes[...], experts)).astype(jnp.bfloat16)
    spare = extended.shape[1] - width - experts
    if spare:
        gates = jnp.concatenate([gates, jnp.zeros((gates.shape[0], spare), gates.dtype)], axis=1)
    extended[:, width:] = gates


def enter_ffn(rows, branch, routes, router, gain, bias):
    count, width = rows.shape
    experts = router.shape[1]
    wide = width + experts + -experts % 128
    return pl.pallas_call(
        middle_kernel,
        out_shape=[
            jax.ShapeDtypeStruct((count, width), jnp.float32),
            jax.ShapeDtypeStruct((count, wide), jnp.bfloat16),
            jax.ShapeDtypeStruct((count, experts), jnp.float32),
        ],
        compiler_params=pltpu.CompilerParams(vmem_limit_bytes=40 * 2**20),
        cost_estimate=cost(1e9, 1e7),
        name="middle",
    )(rows, branch, routes, router, gain, bias)


def leave_kernel(
    middle, own, came, cotangent, sigs, routes, router, gain, bias, grad_out, low_out, weight_grads
):
    experts = router.shape[1]
    count, width = middle.shape
    scaled, inverse, normed = normalized(middle[...], gain[...], bias[...])
    total = own[...] + came[...].astype(jnp.float32)
    sig = sigs[...]
    member = named_by(routes[...], experts)
    gate_grads = total[:, width : width + experts]
    logit = (gate_grads * sig * (1.0 - sig) * member).astype(jnp.bfloat16)
    second = dot(logit, router[...], 1, 1)
    inner_grad = second * gain[...]
    inner_grad = inverse * (
        inner_grad
        - jnp.mean(inner_grad, axis=1, keepdims=True)
        - scaled * jnp.mean(inner_grad * scaled, axis=1, keepdims=True)
    )
    grad = cotangent[...].astype(jnp.float32) + total[:, :width] + inner_grad
    grad_out[...] = grad
    low_out[...] = grad.astype(jnp.bfloat16)
    spare = weight_grads.shape[1] - experts
    sums = [
        jnp.sum(second * scaled, axis=0, keepdims=True),
        jnp.sum(second, axis=0, keepdims=True),
        jnp.zeros((126, width), jnp.float32),
    ]
    side = jnp.concatenate(sums, axis=0).T[:, :spare]
    both = jnp.concatenate([dot(normed, logit, 0, 0), side], axis=1)
    weight_grads[...] = both.astype(jnp.bfloat16)


def leave_ffn(middle, own, came, cotangent, sigs, routes, router, gain, bias):
    count, width = middle.shape
    experts = router.shape[1]
    columns = experts + 2 + -(experts + 2) % 128
    return pl.pallas_call(
        leave_kernel,
        out_shape=[
            jax.ShapeDtypeStruct((count, width), jnp.float32),
            jax.ShapeDtypeStruct((count, width), jnp.bfloat16),
            jax.ShapeDtypeStruct((width, columns), jnp.bfloat16),
        ],
        compiler_params=pltpu.CompilerParams(vmem_limit_bytes=48 * 2**20),
        cost_estimate=cost(1e9, 1e7),
        name="leave_ffn",
    )(middle, own, came, cotangent, sigs, routes, router, gain, bias)


def branch_back_kernel(
    grads, w_output, attended, sigs, masks, grad_attended, inner, out_logit, weight_grads, acc
):
    at = pl.program_id(0)
    count = grads.shape[0]
    sig, mask, values = sigs[...], masks[...], attended[...]
    mixed_grad = dot(grads[...], w_output[...], 1, 0)
    lane = lax.broadcasted_iota(jnp.int32, (count, 128), 1)
    logits = jnp.zeros((count, 128), jnp.float32)
    total = jnp.zeros((count, DH), jnp.float32)
    parts = []
    for e in range(VEXP):
        k = VEXP + e
        one, on = sig[:, k : k + 1], mask[:, k : k + 1]
        part = mixed_grad[:, e * DH : (e + 1) * DH]
        total += part * (one * on)
        gate_grad = jnp.sum(part * values, axis=1, keepdims=True)
        logits = jnp.where(lane == k, gate_grad * one * (1.0 - one) * on, logits)
        parts.append((one * on * values).astype(jnp.bfloat16))
    out_logit[...] = logits.astype(jnp.bfloat16)
    rounded = total.astype(jnp.bfloat16)
    grad_attended[...] = rounded
    product = rounded.astype(jnp.float32) * values
    inner[0] = jnp.sum(product.T, axis=0, keepdims=True)
    amount = dot(grads[...], jnp.concatenate(parts, axis=1), 0, 0)

    @pl.when(at == 0)
    def _():
        acc[...] = amount

    @pl.when(at > 0)
    def _():
        acc[...] += amount

    @pl.when(at == pl.num_programs(0) - 1)
    def _():
        weight_grads[...] = acc[...].astype(jnp.bfloat16)


def branch_back(grads, full, attended, sigs, masks):
    rows, width = grads.shape
    values = VEXP * DH

    def by_row(size):
        return pl.BlockSpec((BLOCK, size), lambda i: (i, 0))

    return pl.pallas_call(
        branch_back_kernel,
        grid=(rows // BLOCK,),
        in_specs=[
            by_row(width),
            pl.BlockSpec((width, values), lambda i: (0, 1), pipeline_mode=pl.Buffered(1)),
            by_row(DH),
            by_row(128),
            by_row(16),
        ],
        out_specs=[
            by_row(DH),
            pl.BlockSpec((1, 1, BLOCK), lambda i: (i, 0, 0)),
            by_row(128),
            pl.BlockSpec((width, values), lambda i: (0, 0)),
        ],
        out_shape=[
            jax.ShapeDtypeStruct((rows, DH), jnp.bfloat16),
            jax.ShapeDtypeStruct((rows // BLOCK, 1, BLOCK), jnp.float32),
            jax.ShapeDtypeStruct((rows, 128), jnp.bfloat16),
            jax.ShapeDtypeStruct((width, values), jnp.bfloat16),
        ],
        scratch_shapes=[pltpu.VMEM((width, values), jnp.float32)],
        compiler_params=pltpu.CompilerParams(vmem_limit_bytes=48 * 2**20),
        cost_estimate=cost(1e8, 1e6),
        name="branch_back",
    )(grads, full, attended, sigs, masks)


def turn(value, axis, by):
    size = lax.axis_size(axis)
    return lax.ppermute(value, axis, [(i, (i + by) % size) for i in range(size)])


def normalized(rows, gain, bias):
    values = rows.astype(jnp.float32)
    centred = values - jnp.mean(values, axis=1, keepdims=True)
    inverse = lax.rsqrt(jnp.mean(centred * centred, axis=1, keepdims=True) + 1e-05)
    scaled = centred * inverse
    return scaled, inverse, (scaled * gain + bias).astype(jnp.bfloat16)


def project_kernel(
    levels, rows, w_value, w_query, w_key, routers, gain, bias, order, tables,
    query, key_value, projected, sigs, masks,
):
    count = rows.shape[0]
    piece = count // (levels * HEADS)
    _, _, normed = normalized(rows[...], gain[...], bias[...])
    query[...] = dot(normed, w_query[...], 1, 0).astype(jnp.bfloat16)
    key_value[:, :DH] = dot(normed, w_key[...], 1, 0).astype(jnp.bfloat16)
    sig = 1.0 / (1.0 + jnp.exp2(-LOG2E * dot(normed, routers[...], 1, 0)))
    sigs[...] = sig
    product = dot(rows[...], w_value[...], 1, 0)
    projected[...] = product
    at = lax.broadcasted_iota(jnp.int32, (count, count), 0)
    source = lax.rem(at // piece, levels) * HEADS + at // (piece * levels)
    here = (source * piece + lax.rem(at, piece) == order[0]).astype(jnp.bfloat16)
    lane = lax.broadcasted_iota(jnp.int32, (16, count), 0)
    table = tables[0]
    named = jnp.zeros((16, count), jnp.float32)
    for which in range(2):
        option = lane - which * VEXP
        for slot in range(2):
            pick = table[2 * which + slot : 2 * which + slot + 1, :]
            hit = (option == pick) & (option >= 0) & (option < VEXP)
            named = jnp.where(hit, 1.0, named)
    mask = dot(here, named.astype(jnp.bfloat16), 1, 1)
    masks[...] = mask
    value = jnp.zeros((count, DH), jnp.float32)
    for e in range(VEXP):
        gate = sig[:, e : e + 1] * mask[:, e : e + 1]
        value += gate * product[:, e * DH : (e + 1) * DH]
    key_value[:, DH:] = value.astype(jnp.bfloat16)


def project(rows, full, gain, bias, orders, tables, levels):
    total, width = rows.shape
    count = total // HEADS

    def by_row(columns):
        return pl.BlockSpec((count, columns), lambda i: (i, 0))

    def column(size, at):
        return pl.BlockSpec((width, size), lambda i: (0, at), pipeline_mode=pl.Buffered(1))

    line = pl.BlockSpec((1, width), lambda i: (0, 0))
    shapes = [(DH, jnp.bfloat16), (2 * DH, jnp.bfloat16), (VEXP * DH, jnp.float32)]
    shapes += [(128, jnp.float32), (16, jnp.float32)]
    return pl.pallas_call(
        functools.partial(project_kernel, levels),
        grid=(HEADS,),
        in_specs=[by_row(width), column(VEXP * DH, 0)]
        + [column(DH, 2 * VEXP + i) for i in range(3)]
        + [line, line]
        + [
            pl.BlockSpec((1, 1, count), lambda i: (i, 0, 0)),
            pl.BlockSpec((1,) + tables.shape[1:], lambda i: (i, 0, 0)),
        ],
        out_specs=[by_row(columns) for columns, _ in shapes],
        out_shape=[jax.ShapeDtypeStruct((total, columns), kind) for columns, kind in shapes],
        compiler_params=pltpu.CompilerParams(vmem_limit_bytes=48 * 2**20),
        cost_estimate=cost(2 * total * width * 1024, 2e7),
        name="project",
    )(rows, full, full, full, full, gain, bias, orders, tables)


def project_back_kernel(
    rows, grads, grad_query, out_logit, projected, sigs, masks,
    w_value, w_query, w_key, routers, gain, bias,
    grad_rows, weight_grads, acc, sums,
):
    at = pl.program_id(0)
    count = rows.shape[0]
    values = VEXP * DH

    @pl.when(at == 0)
    def _():
        acc[...] = jnp.zeros_like(acc)
        sums[...] = jnp.zeros_like(sums)

    scaled, inverse, normed = normalized(rows[...], gain[...], bias[...])
    grad_key = grads[:, :DH].astype(jnp.bfloat16)
    grad_value = grads[:, DH:]
    sig, mask = sigs[...], masks[...]
    lane = lax.broadcasted_iota(jnp.int32, (count, 128), 1)
    logits = out_logit[...].astype(jnp.float32)
    parts = []
    for e in range(VEXP):
        one, on = sig[:, e : e + 1], mask[:, e : e + 1]
        parts.append((one * on * grad_value).astype(jnp.bfloat16))
        inner = jnp.sum(grad_value * projected[:, e * DH : (e + 1) * DH], axis=1, keepdims=True)
        logits = jnp.where(lane == e, inner * one * (1.0 - one) * on, logits)
    grad_projected = jnp.concatenate(parts, axis=1)
    sides = jnp.concatenate([grad_query[...], grad_key, logits.astype(jnp.bfloat16)], axis=1)
    first = dot(sides[:, :DH], w_query[...], 1, 1)
    first += dot(sides[:, DH : 2 * DH], w_key[...], 1, 1)
    first += dot(sides[:, 2 * DH :], routers[...], 1, 1)
    sums[2 * VEXP : 2 * VEXP + 1, :] += jnp.sum(first * scaled, axis=0, keepdims=True)
    sums[2 * VEXP + 1 : 2 * VEXP + 2, :] += jnp.sum(first, axis=0, keepdims=True)
    inner_grad = first * gain[...]
    inner_grad = inverse * (
        inner_grad
        - jnp.mean(inner_grad, axis=1, keepdims=True)
        - scaled * jnp.mean(inner_grad * scaled, axis=1, keepdims=True)
    )
    grad_rows[...] = (inner_grad + dot(grad_projected, w_value[...], 1, 1)).astype(jnp.bfloat16)
    acc[:, :values] += dot(rows[...], grad_projected, 0, 0)
    acc[:, values:] += dot(normed, sides, 0, 0)

    @pl.when(at == pl.num_programs(0) - 1)
    def _():
        weight_grads[:, : values + 2 * DH] = acc[:, : values + 2 * DH].astype(jnp.bfloat16)
        last = acc[:, values + 2 * DH :] + sums[...].T
        weight_grads[:, values + 2 * DH :] = last.astype(jnp.bfloat16)


def project_back(rows, grads, grad_query, out_logit, projected, sigs, masks, full, gain, bias):
    total, width = rows.shape
    count = total // HEADS
    columns = VEXP * DH + 3 * DH

    def by_row(size):
        return pl.BlockSpec((count, size), lambda i: (i, 0))

    def column(size, at):
        return pl.BlockSpec((width, size), lambda i: (0, at), pipeline_mode=pl.Buffered(1))

    line = pl.BlockSpec((1, width), lambda i: (0, 0))
    return pl.pallas_call(
        project_back_kernel,
        grid=(HEADS,),
        in_specs=[by_row(width), by_row(2 * DH), by_row(DH), by_row(128), by_row(VEXP * DH)]
        + [by_row(128), by_row(16), column(VEXP * DH, 0)]
        + [column(DH, 2 * VEXP + i) for i in range(3)]
        + [line, line],
        out_specs=[by_row(width), pl.BlockSpec((width, columns), lambda i: (0, 0))],
        out_shape=[
            jax.ShapeDtypeStruct((total, width), jnp.bfloat16),
            jax.ShapeDtypeStruct((width, columns), jnp.bfloat16),
        ],
        scratch_shapes=[
            pltpu.VMEM((width, columns), jnp.float32),
            pltpu.VMEM((128, width), jnp.float32),
        ],
        compiler_params=pltpu.CompilerParams(vmem_limit_bytes=56 * 2**20),
        cost_estimate=cost(total * width * 512, 4e6),
        name="project_back",
    )(rows, grads, grad_query, out_logit, projected, sigs, masks, full, full, full, full, gain, bias)


def shift(value, axis, by):
    count = lax.axis_size(axis)
    pairs = [(i, i + by) for i in range(count) if 0 <= i + by < count]
    return lax.ppermute(value, axis, pairs)


def body(
    tokens_in,
    out_grad,
    deal_order,
    seq_lengths,
    value_routes,
    output_routes,
    ffn_routes,
    norm1_gain,
    norm1_bias,
    norm2_gain,
    norm2_bias,
    query_weight,
    key_weight,
    value_weight,
    output_weight,
    value_router,
    output_router,
    ffn_router,
    ffn_in,
    ffn_out,
):
    groups = lax.axis_size("group")
    levels = lax.axis_size("level")
    level = lax.axis_index("level")
    head = lax.axis_index("head")
    count, width = tokens_in.shape
    piece = count // (levels * HEADS)
    wrows = query_weight.shape[0]
    experts = ffn_router.shape[1]
    local_experts = ffn_in.shape[1] // FH

    small = jnp.concatenate(
        [
            ffn_router,
            norm1_gain[:, None],
            norm1_bias[:, None],
            norm2_gain[:, None],
            norm2_bias[:, None],
        ],
        axis=1,
    )
    shared = small.shape[1]
    pad = -(shared + 2 * VEXP) % 128
    extra = jnp.concatenate(
        [
            value_router.reshape(wrows, HEADS, VEXP),
            output_router.reshape(wrows, HEADS, VEXP),
            jnp.broadcast_to(small[:, None, :], (wrows, HEADS, shared)),
            jnp.zeros((wrows, HEADS, pad), jnp.bfloat16),
        ],
        axis=2,
    )
    cols = 2 * DH + 2 * VEXP * DH + extra.shape[2]
    tables = jnp.concatenate(
        [value_routes.transpose(1, 2, 0), output_routes.transpose(1, 2, 0)], axis=1
    )
    picks = ffn_routes.reshape(levels, HEADS * piece, -1).transpose(0, 2, 1)
    arrived, own_grads, full, tables, picks, orders = start(
        tokens_in.reshape(levels, HEADS, piece, width),
        out_grad.reshape(levels, HEADS, piece, width),
        [value_weight, output_weight, query_weight, key_weight],
        extra.transpose(1, 0, 2),
        tables,
        picks,
        deal_order,
    )
    worker_in = arrived.reshape(HEADS * count, width)
    own_tokens = lax.dynamic_index_in_dim(arrived, head, 1, keepdims=False).reshape(count, width)
    in_rows = [turn(ffn_in, "group", k) for k in range(1, groups)]
    full, in_rows = lax.optimization_barrier((full.reshape(width, cols), in_rows))

    base = 2 * DH + 2 * VEXP * DH
    w_output = full[:, VEXP * DH : 2 * VEXP * DH]
    at = base + 2 * VEXP
    def relabelled(expert):
        share = expert // local_experts
        return (share % HEADS * levels + share // HEADS) * local_experts + expert % local_experts

    labels = jnp.arange(experts, dtype=jnp.int32)
    moved = low(relabelled(labels)[:, None] == labels[None, :])
    r_ffn = low(
        jnp.dot(full[:, at : at + experts], moved, preferred_element_type=jnp.float32)
    )
    gain_one, bias_one, gain_two, bias_two = (
        full[:, at + experts + i].astype(jnp.float32) for i in range(4)
    )
    gain_row, bias_row = gain_one[None], bias_one[None]
    orders = orders.reshape(levels, HEADS, count)
    own_order = lax.dynamic_index_in_dim(orders, level, 0, keepdims=False)[:, None, :]
    queries, key_value, projected, sigs, masks = project(
        worker_in, full, gain_row, bias_row, own_order, tables, levels
    )

    rows = HEADS * count
    reach = -(-LMAX // rows)

    ramp = jnp.arange(count, dtype=jnp.int32)

    def arrival(values):
        lead, shape = values.shape[:-3], values.shape[-1:]
        four = values.reshape(lead + (HEADS, levels, HEADS, piece) + shape)
        return jnp.swapaxes(four, -4, -3).reshape(lead + (rows,) + shape)

    orders = jnp.concatenate([jnp.zeros((reach, HEADS, count), jnp.int32), orders], axis=0)
    orders = lax.dynamic_slice_in_dim(orders, level, reach + 1, 0)
    here = orders[:, :, None, :] == ramp[None, None, :, None]
    inverse = jnp.sum(here * ramp, axis=3)
    shard = (level - reach + jnp.arange(reach + 1, dtype=jnp.int32))[:, None] * HEADS
    shard = shard + jnp.arange(HEADS, dtype=jnp.int32)[None, :]
    pos_all = jnp.where(shard[:, :, None] < 0, -1, shard[:, :, None] * count + inverse)
    pos_all = arrival(pos_all[..., None]).reshape(-1)
    positions = pos_all[reach * rows :]
    seq_ends = jnp.cumsum(seq_lengths[0])

    def starts_of(places):
        return jnp.max(jnp.where(seq_ends <= places[:, None], seq_ends, 0), axis=1)

    starts = starts_of(positions)
    blocks = rows // BLOCK
    base_block = (level - reach) * blocks
    first_block = starts_of(level * rows + jnp.arange(blocks, dtype=jnp.int32) * BLOCK) // BLOCK
    first_block = jnp.maximum(first_block - base_block, 0)
    ends = level * rows + jnp.arange(1, blocks + 1, dtype=jnp.int32) * BLOCK - 1
    clear_block = (starts_of(ends) + BLOCK - 1) // BLOCK - base_block

    own_routes = picks.reshape(levels, -1, HEADS, piece).transpose(2, 0, 3, 1).reshape(count, -1)
    own_routes = relabelled(own_routes)
    ffn_side = (own_routes, r_ffn, gain_two[None], bias_two[None], own_tokens)

    window = [key_value]
    own_grads = own_grads.reshape(count, width)
    for i in range(reach):
        came = shift(window[0], "level", 1)
        if i == 0:
            came, own_grads, pos_all, starts, ffn_out, in_rows = lax.optimization_barrier(
                (came, own_grads, pos_all, starts, ffn_out, [ffn_in] + in_rows)
            )
            cotangent = level_gather(own_grads, 5, True)
        if i == reach - 1:
            came, cotangent, ffn_side = lax.optimization_barrier((came, cotangent, ffn_side))
        window.insert(0, came)
    place = jnp.stack([head, lax.axis_index("group")])
    out_here = lax.all_gather(ffn_out, "level", axis=0)
    w_in = lax.all_gather(jnp.stack(in_rows), "level", axis=0)


    def lines(values):
        return values.reshape(blocks, 1, BLOCK)

    attended, log_total = attend(
        first_block,
        clear_block,
        queries,
        window,
        lines(positions),
        lines(starts),
        pos_all[:, None],
    )

    out_sig = sigs[:, VEXP : 2 * VEXP]
    out_mask = masks[:, VEXP : 2 * VEXP]
    out_gate = out_sig * out_mask
    attended, out_here = lax.optimization_barrier((attended, out_here))
    w_out = [out_here] + [turn(out_here, "group", k) for k in range(1, groups)]
    mixed = low((out_gate[..., None] * attended[:, None, :]).reshape(rows, VEXP * DH))
    branch = level_scatter(low(transposed(mixed, w_output)), 2)

    own_routes, r_ffn, gain_two, bias_two, own_tokens = ffn_side
    middle, extended, ffn_sig = enter_ffn(own_tokens, branch, own_routes, r_ffn, gain_two, bias_two)
    hidden = level_gather(extended, 3, True)
    mine = levels * local_experts
    gates = lax.dynamic_slice_in_dim(hidden, width + head * mine, mine, 1).astype(jnp.float32)
    active, grad_pre, grad_rows = ffn_front(
        place, hidden, cotangent, w_in, w_out, gates, local_experts
    )
    summed, beyond = pair_scatter(grad_rows, 4, True)
    beyond, hidden = lax.optimization_barrier((beyond, hidden))
    came = to_far(beyond)
    grad_in = ffn_rear(place, hidden, grad_pre, width, groups, levels)
    in_came = [turn(grad_in[k], "group", k) for k in range(1, groups)]
    grad_out = ffn_rear(place, cotangent, active, width, groups, levels)
    out_came = [turn(grad_out[k], "group", k) for k in range(1, groups)]
    came, grad_in, grad_out = lax.optimization_barrier((came, grad_in, grad_out))
    grad_middle, own_branch, early = leave_ffn(
        middle, summed, came, own_grads, ffn_sig, own_routes, r_ffn, gain_two, bias_two
    )
    came = to_far(own_branch)
    feed = ffn_feed(place, active, w_out)
    came, feed = lax.optimization_barrier((came, feed))
    grad_branch = pair_gather(own_branch, came, 7)

    def sum_of(own, others):
        total = own[0].astype(jnp.float32)
        for other in others:
            total = total + other.astype(jnp.float32)
        return low(total)

    def over_levels(total):
        return lax.psum_scatter(total, "level", scatter_dimension=0)

    grad_branch, in_came = lax.optimization_barrier((grad_branch, in_came))
    ffn_in_grad = over_levels(sum_of(grad_in, in_came))
    grad_attended, row_inner, grad_out_logit, grad_w_output = branch_back(
        grad_branch, full, attended, sigs, masks
    )
    grad_queries, *grad_window = attend_back(
        first_block,
        clear_block,
        queries,
        window,
        grad_attended,
        lines(positions),
        lines(starts),
        log_total,
        row_inner,
        pos_all[:, None],
    )
    came = shift(grad_window[0], "level", -1)
    fed, beyond = pair_scatter(feed, 6, True)
    for i in range(1, reach + 1):
        if i < reach:
            came, fed = lax.optimization_barrier((came, fed))
        grad_both = grad_window[i].astype(jnp.float32) + came.astype(jnp.float32)
        if i < reach:
            grad_keys_sent = low(grad_both)
            came = shift(grad_keys_sent, "level", -1)
    grad_both, out_came = lax.optimization_barrier((grad_both, out_came))
    ffn_out_grad = over_levels(sum_of(grad_out, out_came))
    fed_far = to_far(beyond)
    grad_inputs, late = project_back(
        worker_in,
        grad_both,
        grad_queries,
        grad_out_logit,
        projected,
        sigs,
        masks,
        full,
        gain_row,
        bias_row,
    )

    fed_far, grad_inputs = lax.optimization_barrier((fed_far, grad_inputs))
    layer_out = to_home(low(middle + fed + fed_far.astype(jnp.float32)))

    values = VEXP * DH
    layout = (
        ((0, values, True), (values, DH, True), (values + DH, DH, True), (values + 2 * DH, DH, False)),
        ((0, values, True),),
        ((0, early.shape[1], False),),
    )

    def by_owner(grads):
        return grads.reshape(groups, levels, HEADS, wrows, -1)

    input_grad, grad_value, grad_query, grad_key, sides, grad_output, common = finish(
        layout,
        grad_inputs.reshape(HEADS, HEADS, levels * piece, width),
        grad_middle.reshape(HEADS, levels * piece, width),
        by_owner(late),
        by_owner(grad_w_output),
        by_owner(early),
    )
    norms = jnp.sum(sides[:, :, 2 * VEXP : 2 * VEXP + 2], axis=0)
    common = jnp.sum(common[:, :, : experts + 2], axis=0)
    router_grad = common[:, :experts].reshape(wrows, HEADS, levels, local_experts)

    def side(first):
        return sides[:, :, first : first + VEXP].transpose(1, 0, 2).reshape(wrows, HEADS * VEXP)

    return (
        layer_out,
        input_grad.reshape(count, width),
        norms[:, 0],
        norms[:, 1],
        common[:, experts],
        common[:, experts + 1],
        grad_query,
        grad_key,
        grad_value,
        grad_output,
        side(0),
        side(VEXP),
        jnp.swapaxes(router_grad, 1, 2).reshape(wrows, experts),
        ffn_in_grad.astype(jnp.float32),
        ffn_out_grad.astype(jnp.float32),
    )


def solution(mesh):
    groups, shards = mesh.devices.shape
    fine = Mesh(mesh.devices.reshape(groups, shards // HEADS, HEADS), TOK)
    two, one, three = P(TOK, None), P(TOK), P(TOK, None, None)
    ffn = P("group", ("level", "head"))
    return jax.shard_map(
        body,
        mesh=fine,
        in_specs=(two, two, two, P("group", None), three, three, two, one, one, one, one)
        + (two,) * 7
        + (ffn, ffn),
        out_specs=(two, two, one, one, one, one) + (two,) * 7 + (ffn, ffn),
        check_vma=False,
    )
```

```python
import functools

import jax
import jax.numpy as jnp
from jax import lax
from jax.experimental import pallas as pl
from jax.experimental.pallas import tpu as pltpu
from jax.sharding import Mesh, PartitionSpec as P

HEADS = 4
DH = 128
VEXP = 5
FH = 128
LMAX = 4096

TOK = ("group", "level", "head")


def transposed(left_side, right_side):
    return lax.dot_general(
        left_side, right_side, (((1,), (1,)), ((), ())), preferred_element_type=jnp.float32
    )


def low(value):
    return value.astype(jnp.bfloat16)


def to_home(rows):
    levels = lax.axis_size("level")
    count = rows.shape[0]
    out = rows.reshape(HEADS, levels, count // levels // HEADS, -1).transpose(1, 0, 2, 3)
    back = lax.all_to_all(
        out.reshape(levels, count // levels, -1), "level", split_axis=0, concat_axis=0, tiled=True
    )
    return back.reshape(count, -1)


MESH = pl.DeviceIdType.MESH


def partners(head):
    near = head + 1 - 2 * lax.rem(head, 2)
    far = lax.rem(head + 2, HEADS)
    return near, far


def greet(near, far):
    barrier = pltpu.get_barrier_semaphore()
    for peer in (near, far):
        pl.semaphore_signal(barrier, inc=1, device_id={"head": peer}, device_id_type=MESH)
    pl.semaphore_wait(barrier, 2)


def remote(src, dst, send, recv, peer):
    return pltpu.make_async_remote_copy(
        src_ref=src,
        dst_ref=dst,
        send_sem=send,
        recv_sem=recv,
        device_id={"head": peer},
        device_id_type=MESH,
    )


def cost(flops, moved):
    return pl.CostEstimate(flops=int(flops), bytes_accessed=int(moved), transcendentals=0)


def gather_kernel(
    by_source, own, out, local_sem, near_send, near_recv, far_send, far_recv, pass_send, pass_recv
):
    head = lax.axis_index("head")
    near, far = partners(head)
    greet(near, far)

    def spot(i, source):
        return out.at[source, i] if by_source else out.at[i, source]

    pieces = range(HEADS)
    to_far = [remote(own.at[i], spot(i, head), far_send.at[i], far_recv.at[i], far) for i in pieces]
    to_near = [
        remote(own.at[i], spot(i, head), near_send.at[i], near_recv.at[i], near) for i in pieces
    ]
    passed = [
        remote(spot(i, far), spot(i, far), pass_send.at[i], pass_recv.at[i], near) for i in pieces
    ]
    kept = [pltpu.make_async_copy(own.at[i], spot(i, head), local_sem.at[i]) for i in pieces]
    for copy in to_far + to_near + kept:
        copy.start()
    for i in pieces:
        to_far[i].wait_recv()
        passed[i].start()
    for i in pieces:
        to_near[i].wait_recv()
        passed[i].wait_recv()
        kept[i].wait()
        to_far[i].wait_send()
        to_near[i].wait_send()
        passed[i].wait_send()


def level_gather(rows, collective_id, by_source=False):
    count, width = rows.shape
    whole = pl.pallas_call(
        functools.partial(gather_kernel, by_source),
        out_shape=jax.ShapeDtypeStruct((HEADS, HEADS, count // HEADS, width), rows.dtype),
        in_specs=[pl.BlockSpec(memory_space=pltpu.VMEM)],
        out_specs=pl.BlockSpec(memory_space=pl.ANY),
        scratch_shapes=[pltpu.SemaphoreType.DMA((HEADS,))] * 7,
        compiler_params=pltpu.CompilerParams(collective_id=collective_id, has_side_effects=True),
        cost_estimate=cost(0, 90e6),
        name="level_gather",
    )(rows.reshape(HEADS, count // HEADS, width))
    return whole.reshape(HEADS * count, width)


def scatter_kernel(
    by_source, part, out, near_buf, send_buf, far_buf, near_send, near_recv, far_send, far_recv
):
    head = lax.axis_index("head")
    near, far = partners(head)
    greet(near, far)
    across = HEADS - 1 - head
    pieces = range(HEADS)

    def spot(i, dest):
        return (dest, i) if by_source else (i, dest)

    def to_near(slot, i, dest):
        return remote(
            part.at[spot(i, dest)],
            near_buf.at[slot, i],
            near_send.at[slot, i],
            near_recv.at[slot, i],
            near,
        )

    first = [to_near(0, i, across) for i in pieces]
    second = [to_near(1, i, near) for i in pieces]
    onward = [
        remote(send_buf.at[i], far_buf.at[i], far_send.at[i], far_recv.at[i], far) for i in pieces
    ]
    for copy in first + second:
        copy.start()
    for i in pieces:
        first[i].wait_recv()
        both = part[spot(i, far)].astype(jnp.float32) + near_buf[0, i].astype(jnp.float32)
        send_buf[i] = both.astype(jnp.bfloat16)
        onward[i].start()
    for i in pieces:
        second[i].wait_recv()
        out[i] = part[spot(i, head)].astype(jnp.float32) + near_buf[1, i].astype(jnp.float32)
    for i in pieces:
        onward[i].wait_recv()
        out[i] = out[i] + far_buf[i].astype(jnp.float32)
    for i in pieces:
        first[i].wait_send()
        second[i].wait_send()
        onward[i].wait_send()


def level_scatter(rows, collective_id, by_source=False):
    total, width = rows.shape
    piece = total // (HEADS * HEADS)
    low_type = jnp.bfloat16
    mine = pl.pallas_call(
        functools.partial(scatter_kernel, by_source),
        out_shape=jax.ShapeDtypeStruct((HEADS, piece, width), jnp.float32),
        in_specs=[pl.BlockSpec(memory_space=pltpu.VMEM)],
        out_specs=pl.BlockSpec(memory_space=pltpu.VMEM),
        scratch_shapes=[
            pltpu.VMEM((2, HEADS, piece, width), low_type),
            pltpu.VMEM((HEADS, piece, width), low_type),
            pltpu.VMEM((HEADS, piece, width), low_type),
            pltpu.SemaphoreType.DMA((2, HEADS)),
            pltpu.SemaphoreType.DMA((2, HEADS)),
            pltpu.SemaphoreType.DMA((HEADS,)),
            pltpu.SemaphoreType.DMA((HEADS,)),
        ],
        compiler_params=pltpu.CompilerParams(
            collective_id=collective_id, has_side_effects=True, vmem_limit_bytes=32 * 2**20
        ),
        cost_estimate=cost(0, 80e6),
        name="level_scatter",
    )(rows.reshape(HEADS, HEADS, piece, width))
    return mine.reshape(HEADS * piece, width)


def meet(near):
    barrier = pltpu.get_barrier_semaphore()
    pl.semaphore_signal(barrier, inc=1, device_id={"head": near}, device_id_type=MESH)
    pl.semaphore_wait(barrier, 1)


def pair_scatter_kernel(by_source, part, out, out_far, near_buf, send, recv):
    head = lax.axis_index("head")
    near, far = partners(head)
    meet(near)
    across = HEADS - 1 - head
    pieces = range(HEADS)

    def spot(i, dest):
        return (dest, i) if by_source else (i, dest)

    def to_near(slot, i, dest):
        return remote(
            part.at[spot(i, dest)], near_buf.at[slot, i], send.at[slot, i], recv.at[slot, i], near
        )

    first = [to_near(0, i, across) for i in pieces]
    second = [to_near(1, i, near) for i in pieces]
    for copy in first + second:
        copy.start()
    for i in pieces:
        first[i].wait_recv()
        both = part[spot(i, far)].astype(jnp.float32) + near_buf[0, i].astype(jnp.float32)
        out_far[i] = both.astype(jnp.bfloat16)
    for i in pieces:
        second[i].wait_recv()
        out[i] = part[spot(i, head)].astype(jnp.float32) + near_buf[1, i].astype(jnp.float32)
    for i in pieces:
        first[i].wait_send()
        second[i].wait_send()


def pair_scatter(rows, collective_id, by_source=False):
    total, width = rows.shape
    piece = total // (HEADS * HEADS)
    mine, other = pl.pallas_call(
        functools.partial(pair_scatter_kernel, by_source),
        out_shape=[
            jax.ShapeDtypeStruct((HEADS, piece, width), jnp.float32),
            jax.ShapeDtypeStruct((HEADS, piece, width), jnp.bfloat16),
        ],
        in_specs=[pl.BlockSpec(memory_space=pltpu.VMEM)],
        out_specs=[pl.BlockSpec(memory_space=pltpu.VMEM)] * 2,
        scratch_shapes=[
            pltpu.VMEM((2, HEADS, piece, width), jnp.bfloat16),
            pltpu.SemaphoreType.DMA((2, HEADS)),
            pltpu.SemaphoreType.DMA((2, HEADS)),
        ],
        compiler_params=pltpu.CompilerParams(
            collective_id=collective_id, has_side_effects=True, vmem_limit_bytes=32 * 2**20
        ),
        cost_estimate=cost(0, 25e6),
        name="pair_scatter",
    )(rows.reshape(HEADS, HEADS, piece, width))
    return mine.reshape(HEADS * piece, width), other.reshape(HEADS * piece, width)


def pair_gather_kernel(by_source, own, other, out, local_sem, send, recv):
    head = lax.axis_index("head")
    near, far = partners(head)
    meet(near)
    copies, kept = [], []
    for i in range(HEADS):
        for slot, (block, source) in enumerate(((own, head), (other, far))):
            place = out.at[source, i] if by_source else out.at[i, source]
            copies.append(
                remote(block.at[i], place, send.at[slot, i], recv.at[slot, i], near)
            )
            kept.append(pltpu.make_async_copy(block.at[i], place, local_sem.at[slot, i]))
    for copy in copies + kept:
        copy.start()
    for copy in copies + kept:
        copy.wait()


def pair_gather(own, other, collective_id, by_source=False):
    count, width = own.shape
    split = (HEADS, count // HEADS, width)
    whole = pl.pallas_call(
        functools.partial(pair_gather_kernel, by_source),
        out_shape=jax.ShapeDtypeStruct((HEADS,) + split, own.dtype),
        in_specs=[pl.BlockSpec(memory_space=pltpu.VMEM)] * 2,
        out_specs=pl.BlockSpec(memory_space=pl.ANY),
        scratch_shapes=[pltpu.SemaphoreType.DMA((2, HEADS))] * 3,
        compiler_params=pltpu.CompilerParams(collective_id=collective_id, has_side_effects=True),
        cost_estimate=cost(0, 25e6),
        name="pair_gather",
    )(own.reshape(split), other.reshape(split))
    return whole.reshape(HEADS * count, width)


def to_far(rows):
    return lax.ppermute(rows, "head", [(i, (i + 2) % HEADS) for i in range(HEADS)])


def ring(axis):
    me, size = lax.axis_index(axis), lax.axis_size(axis)
    ahead = [lax.rem(me + k, size) for k in range(1, size)]
    behind = [lax.rem(me + size - k, size) for k in range(1, size)]
    return me, ahead, behind


def reach_out(src, dst, send, recv, peer):
    return pltpu.make_async_remote_copy(
        src_ref=src, dst_ref=dst, send_sem=send, recv_sem=recv, device_id=peer, device_id_type=MESH
    )


def greet_all(peers):
    barrier = pltpu.get_barrier_semaphore()
    for peer in peers:
        pl.semaphore_signal(barrier, inc=1, device_id=peer, device_id_type=MESH)
    pl.semaphore_wait(barrier, len(peers))


def start_kernel(
    tokens, cotangents, value, output, query, key, extra, tables, picks, order,
    rows, grads, full, routes, chosen_rows, orders, weights, own_sem, *sems
):
    sems = iter(sems)

    def pair():
        return next(sems), next(sems)

    group, groups_ahead, _ = ring("group")
    level, levels_ahead, levels_behind = ring("level")
    head = lax.axis_index("head")
    near, far = partners(head)
    mates = [near, far, HEADS - 1 - head]
    for to in range(HEADS):
        at = 0
        for part in (value, output, query, key):
            size = part.shape[1] // HEADS
            weights[to, :, at : at + size] = part[:, to * size : (to + 1) * size]
            at += size
        weights[to, :, at:] = extra[to]
    greet_all(
        [{"head": m} for m in mates]
        + [{"level": n} for n in levels_ahead]
        + [{"group": n} for n in groups_ahead]
    )
    started = []

    def send(src, dst, send_sem, recv_sem, peer):
        copy = reach_out(src, dst, send_sem, recv_sem, peer)
        copy.start()
        started.append(copy)
        return copy

    out_s, out_r = pair()
    pick_s, pick_r = pair()
    crossing, picking = [], []
    for k, to in enumerate(levels_ahead):
        peer = {"level": to}
        crossing.append(send(tokens.at[to], rows.at[:, head, level], out_s.at[k], out_r.at[k], peer))
    mate_s, mate_r = pair()
    table_s, table_r = pair()
    order_s, order_r = pair()
    to_mates, order_mates, table_mates = [], [], []
    for k, to in enumerate(mates):
        peer = {"head": to}
        to_mates.append(
            send(weights.at[to], full.at[group, level, head], mate_s.at[k], mate_r.at[k], peer)
        )
        order_mates.append(
            send(order, orders.at[level, head], order_s.at[k], order_r.at[k], peer)
        )
    own = [
        (tokens.at[level], rows.at[:, head, level]),
        (weights.at[head], full.at[group, level, head]),
        (tables.at[head], routes.at[head]),
        (picks.at[level], chosen_rows.at[level]),
        (order, orders.at[level, head]),
        (cotangents.at[level], grads.at[:, level]),
    ]
    own = [pltpu.make_async_copy(src, dst, own_sem.at[i]) for i, (src, dst) in enumerate(own)]
    for copy in own:
        copy.start()
    far_s, far_r = pair()
    near_s, near_r = pair()
    pass_s, pass_r = pair()
    to_far, to_near = [], []

    def share(k, src, source):
        place = rows.at[:, head, source]
        to_far.append(send(src, place, far_s.at[k], far_r.at[k], {"head": far}))
        to_near.append(send(src, place, near_s.at[k], near_r.at[k], {"head": near}))

    share(0, tokens.at[level], level)
    up_s, up_r = pair()
    down_s, down_r = pair()
    group_s, group_r = pair()
    orders_s, orders_r = pair()
    for copy in to_mates:
        copy.wait_recv()
    own[1].wait()
    last = len(levels_ahead)
    ordered = []

    def to_groups(j):
        block = full.at[group, lax.rem(level - j + last + 1, last + 1)]
        return [
            reach_out(block, block, group_s.at[k, j], group_r.at[k, j], {"group": to})
            for k, to in enumerate(groups_ahead)
        ]

    def hop(k, step):
        send_sem, recv_sem = (up_s, up_r) if step > 0 else (down_s, down_r)
        block = full.at[group, lax.rem(level - step * k + last + 1, last + 1)]
        to = lax.rem(level + step + last + 1, last + 1)
        return reach_out(block, block, send_sem.at[k], recv_sem.at[k], {"level": to})

    def sends(k, step):
        return (level >= k) & (level < last) if step > 0 else (level <= last - k) & (level > 0)

    def receives(k, step):
        return level >= k + 1 if step > 0 else level <= last - k - 1

    def start_hop(k, step):
        @pl.when(sends(k, step))
        def _():
            hop(k, step).start()

    def wait_hop(k, step):
        @pl.when(receives(k, step))
        def _():
            hop(k, step).wait_recv()
            for copy in to_groups(k + 1 if step > 0 else last - k):
                copy.start()

    for step in (1, -1):
        start_hop(0, step)
    for copy in to_groups(0):
        copy.start()
    grouped = [copy for j in range(last + 1) for copy in to_groups(j)]
    for k, to in enumerate(mates):
        table_mates.append(
            send(tables.at[to], routes.at[head], table_s.at[k], table_r.at[k], {"head": to})
        )
    for k, to in enumerate(levels_ahead):
        picking.append(
            send(picks.at[to], chosen_rows.at[level], pick_s.at[k], pick_r.at[k], {"level": to})
        )
    for copy in order_mates:
        copy.wait_recv()
    own[4].wait()
    for k, to in enumerate(levels_ahead):
        block = orders.at[level]
        ordered.append(send(block, block, orders_s.at[k], orders_r.at[k], {"level": to}))
    def finish_hop(k):
        for step in (1, -1):
            wait_hop(k, step)
            if k + 1 < last:
                start_hop(k + 1, step)

    if last:
        finish_hop(0)
    for k, source in enumerate(levels_behind):
        crossing[k].wait_recv()
        share(k + 1, rows.at[:, head, source], source)
    grad_s, grad_r = pair()
    crossed = []
    for k, to in enumerate(levels_ahead):
        crossed.append(
            send(cotangents.at[to], grads.at[:, level], grad_s.at[k], grad_r.at[k], {"level": to})
        )
    for k in range(1, last):
        finish_hop(k)
    passed = []
    for k, source in enumerate([level] + levels_behind):
        to_far[k].wait_recv()
        place = rows.at[:, far, source]
        passed.append(send(place, place, pass_s.at[k], pass_r.at[k], {"head": near}))
    for copy in to_near + passed + grouped + table_mates + picking + ordered + crossed:
        copy.wait_recv()
    for copy in started + grouped:
        copy.wait_send()
    for k in range(last):
        for step in (1, -1):

            @pl.when(sends(k, step))
            def _(k=k, step=step):
                hop(k, step).wait_send()

    for i in (0, 2, 3, 5):
        own[i].wait()


def start(tokens, cotangents, weights, extra, tables, picks, order):
    groups, levels = lax.axis_size("group"), lax.axis_size("level")
    _, _, piece, width = tokens.shape
    columns = sum(part.shape[1] for part in weights) // HEADS + extra.shape[2]
    block = extra.shape[:2] + (columns,)
    shapes = [
        jax.ShapeDtypeStruct((HEADS, HEADS, levels, piece, width), tokens.dtype),
        jax.ShapeDtypeStruct((HEADS, levels, piece, width), tokens.dtype),
        jax.ShapeDtypeStruct((groups, levels) + block, extra.dtype),
        jax.ShapeDtypeStruct(tables.shape, tables.dtype),
        jax.ShapeDtypeStruct(picks.shape, picks.dtype),
        jax.ShapeDtypeStruct((levels, HEADS) + order.shape, order.dtype),
    ]
    dma = pltpu.SemaphoreType.DMA
    others, mates = (levels - 1,), (HEADS - 1,)
    counts = [others] * 2 + [mates] * 3 + [(levels,)] * 3
    counts += [others, others, (groups - 1, levels), others, others]
    return pl.pallas_call(
        start_kernel,
        out_shape=shapes,
        in_specs=[pl.BlockSpec(memory_space=pltpu.VMEM)] * 10,
        out_specs=[pl.BlockSpec(memory_space=pl.ANY)] * 6,
        scratch_shapes=[pltpu.VMEM(block, extra.dtype), dma((6,))] + [dma(c) for c in counts for _ in range(2)],
        compiler_params=pltpu.CompilerParams(collective_id=9, has_side_effects=True),
        cost_estimate=cost(0, 200e6),
        name="start",
    )(tokens, cotangents, *weights, extra, tables, picks, order)


def finish_kernel(layout, *refs):
    refs = iter(refs)
    count = len(layout)

    def take(n):
        return [next(refs) for _ in range(n)]

    part, middle = take(2)
    grads = take(count)
    (home_grad,) = take(1)
    results = [take(len(pieces)) for pieces in layout]
    near_buf, send_buf, far_buf, total, back_buf, came_buf = take(6)
    group_buf, level_send, level_buf, head_send, owned = (take(count) for _ in range(5))

    def pair():
        return next(refs), next(refs)

    group, groups_ahead, _ = ring("group")
    level, levels_ahead, levels_behind = ring("level")
    head = lax.axis_index("head")
    near, far = partners(head)
    across = HEADS - 1 - head
    mates = [near, far, across]
    greet_all(
        [{"head": m} for m in mates]
        + [{"level": n} for n in levels_ahead]
        + [{"group": n} for n in groups_ahead]
    )
    started = []

    def send(src, dst, send_sem, recv_sem, peer):
        copy = reach_out(src, dst, send_sem, recv_sem, peer)
        copy.start()
        started.append(copy)
        return copy

    pieces = range(HEADS)
    sets = range(count)
    near_s, near_r = pair()
    far_s, far_r = pair()
    back_s, back_r = pair()
    group_s, group_r = pair()
    level_s, level_r = pair()
    mate_s, mate_r = pair()
    first, second, onward = [], [], []
    for slot, (dest, copies) in enumerate(((across, first), (near, second))):
        for i in pieces:
            copies.append(
                send(
                    part.at[i, dest],
                    near_buf.at[slot, i],
                    near_s.at[slot, i],
                    near_r.at[slot, i],
                    {"head": near},
                )
            )
    order = levels_ahead + [level]
    grouped = {}
    for j, dest in enumerate(order):
        for p in sets:
            grouped[j, p] = [
                send(
                    grads[p].at[to, dest],
                    group_buf[p].at[k, j],
                    group_s.at[p, k, j],
                    group_r.at[p, k, j],
                    {"group": to},
                )
                for k, to in enumerate(groups_ahead)
            ]
    for i in pieces:
        first[i].wait_recv()
        both = part[i, far].astype(jnp.float32) + near_buf[0, i].astype(jnp.float32)
        send_buf[i] = both.astype(jnp.bfloat16)
        onward.append(send(send_buf.at[i], far_buf.at[i], far_s.at[i], far_r.at[i], {"head": far}))
    for i in pieces:
        second[i].wait_recv()
        both = part[i, head].astype(jnp.float32) + near_buf[1, i].astype(jnp.float32)
        total[i] = both + middle[i]
    leveled = {}
    for j, dest in enumerate(order):
        for p in sets:
            amount = grads[p][group, dest].astype(jnp.float32)
            for k, copy in enumerate(grouped[j, p]):
                copy.wait_recv()
                amount = amount + group_buf[p][k, j].astype(jnp.float32)
            level_send[p][j] = amount.astype(jnp.bfloat16)
            if j < len(levels_ahead):
                leveled[j, p] = send(
                    level_send[p].at[j],
                    level_buf[p].at[j],
                    level_s.at[p, j],
                    level_r.at[p, j],
                    {"level": dest},
                )
    for i in pieces:
        onward[i].wait_recv()
        both = total[i] + far_buf[i].astype(jnp.float32)
        back_buf[i] = both.astype(jnp.bfloat16).reshape(back_buf.shape[1:])
    backs = [
        send(back_buf.at[:, to], came_buf.at[level], back_s.at[k], back_r.at[k], {"level": to})
        for k, to in enumerate(levels_ahead)
    ]
    sharing = []
    for p in sets:
        amount = level_send[p][len(levels_ahead)].astype(jnp.float32)
        for j in range(len(levels_ahead)):
            leveled[j, p].wait_recv()
            amount = amount + level_buf[p][j].astype(jnp.float32)
        head_send[p][...] = amount.astype(jnp.bfloat16)
        sharing += [
            send(
                head_send[p].at[to],
                owned[p].at[head],
                mate_s.at[p, k],
                mate_r.at[p, k],
                {"head": to},
            )
            for k, to in enumerate(mates)
        ]
        owned[p][head] = head_send[p][head]
    home_grad[level] = back_buf[:, level].astype(jnp.float32)
    for k, source in enumerate(levels_behind):
        backs[k].wait_recv()
        home_grad[source] = came_buf[source].astype(jnp.float32)
    for copy in sharing:
        copy.wait_recv()
    for p in sets:
        for out, (first_column, size, joined) in zip(results[p], layout[p]):
            for h in range(HEADS):
                value = owned[p][h, :, first_column : first_column + size].astype(jnp.float32)
                if joined:
                    out[:, h * size : (h + 1) * size] = value
                else:
                    out[h] = value
    for copy in started:
        copy.wait_send()


def finish(layout, part, middle, *grads):
    groups, levels = lax.axis_size("group"), lax.axis_size("level")
    _, count, width = middle.shape
    piece = count // levels
    low_type = jnp.bfloat16
    blocks = [grad.shape[2:] for grad in grads]
    sets = len(grads)
    dma = pltpu.SemaphoreType.DMA
    counts = [(2, HEADS), (HEADS,), (levels - 1,)]
    counts += [(sets, groups - 1, levels), (sets, levels - 1), (sets, HEADS - 1)]
    vmem = pl.BlockSpec(memory_space=pltpu.VMEM)
    shapes = []
    for pieces in layout:
        for _, size, joined in pieces:
            shape = (blocks[0][1], HEADS * size) if joined else (HEADS, blocks[0][1], size)
            shapes.append(jax.ShapeDtypeStruct(shape, jnp.float32))
    return pl.pallas_call(
        functools.partial(finish_kernel, layout),
        out_shape=[jax.ShapeDtypeStruct((levels, HEADS, piece, width), jnp.float32)] + shapes,
        in_specs=[vmem] * (2 + sets),
        out_specs=[vmem] * (1 + len(shapes)),
        scratch_shapes=[
            pltpu.VMEM((2, HEADS, count, width), low_type),
            pltpu.VMEM((HEADS, count, width), low_type),
            pltpu.VMEM((HEADS, count, width), low_type),
            pltpu.VMEM((HEADS, count, width), jnp.float32),
            pltpu.VMEM((HEADS, levels, piece, width), low_type),
            pltpu.VMEM((levels, HEADS, piece, width), low_type),
        ]
        + [pltpu.VMEM((groups - 1, levels) + block, low_type) for block in blocks]
        + [pltpu.VMEM((levels,) + block, low_type) for block in blocks]
        + [pltpu.VMEM((levels - 1,) + block, low_type) for block in blocks]
        + [pltpu.VMEM(block, low_type) for block in blocks] * 2
        + [dma(c) for c in counts for _ in range(2)],
        compiler_params=pltpu.CompilerParams(
            collective_id=10, has_side_effects=True, vmem_limit_bytes=56 * 2**20
        ),
        cost_estimate=cost(0, 200e6),
        name="finish",
    )(part, middle, *grads)


BLOCK = 512
LOG2E = 1.4426950408889634


def dot(left_side, right_side, left_dim, right_dim):
    return lax.dot_general(
        left_side,
        right_side,
        (((left_dim,), (right_dim,)), ((), ())),
        preferred_element_type=jnp.float32,
    )


def run_blocks(step, part, parts, blocks, at, first, clear):
    def local(block):
        return jnp.clip(block - part * blocks, 0, blocks)

    own = (parts - 1) * blocks + at
    begin, middle, end = local(first), local(jnp.clip(clear, first, own)), local(own)
    lax.fori_loop(begin, middle, functools.partial(step, True), 0)
    lax.fori_loop(middle, end, functools.partial(step, False), 0)
    if part == parts - 1:
        step(True, at, 0)


def attend_kernel(parts, first, clear, q, *refs):
    keys, values = refs[:parts], refs[parts : 2 * parts]
    pos_q, start_q, pos_k, out, lse, top, total, acc = refs[2 * parts :]
    at = pl.program_id(0)
    blocks = pl.num_programs(0)
    rate = LOG2E * DH ** (-0.5)
    top[...] = jnp.full_like(top, -1e30)
    total[...] = jnp.zeros_like(total)
    acc[...] = jnp.zeros_like(acc)
    query = q[...]
    row_at, row_from = pos_q[0], start_q[0]

    for part in range(parts):

        def step(masked, block, carry, k=keys[part], v=values[part], part=part):
            rows = pl.ds(pl.multiple_of(block * BLOCK, BLOCK), BLOCK)
            spot = pl.ds(pl.multiple_of((part * blocks + block) * BLOCK, BLOCK), BLOCK)
            scores = dot(k[rows, :], query, 1, 1)
            if masked:
                key_at = pos_k[spot, :]
                scores = jnp.where((key_at >= row_from) & (key_at <= row_at), scores, -1e30)
            old = top[...]
            new = jnp.maximum(old, jnp.max(scores, axis=0, keepdims=True))
            shrink = jnp.exp2((old - new) * rate)
            weight = jnp.exp2((scores - new) * rate)
            total[...] = total[...] * shrink + jnp.sum(weight, axis=0, keepdims=True)
            acc[...] = acc[...] * shrink + dot(v[rows, :], weight.astype(jnp.bfloat16), 0, 0)
            top[...] = new
            return carry

        run_blocks(step, part, parts, blocks, at, first[at], clear[at])
    out[...] = (acc[...] / total[...]).T
    lse[0] = top[...] * rate + jnp.log2(total[...])


def attend(first, clear, queries, window, pos_q, start_q, pos_k):
    rows = queries.shape[0]
    parts = len(window)
    line = pl.BlockSpec((1, 1, BLOCK), lambda i, *_: (i, 0, 0))
    grid_spec = pltpu.PrefetchScalarGridSpec(
        num_scalar_prefetch=2,
        grid=(rows // BLOCK,),
        in_specs=[pl.BlockSpec((BLOCK, DH), lambda i, *_: (i, 0))]
        + [pl.BlockSpec((rows, DH), lambda i, *_: (0, 0))] * parts
        + [pl.BlockSpec((rows, DH), lambda i, *_: (0, 1))] * parts
        + [line, line, pl.BlockSpec((parts * rows, 1), lambda i, *_: (0, 0))],
        out_specs=[pl.BlockSpec((BLOCK, DH), lambda i, *_: (i, 0)), line],
        scratch_shapes=[
            pltpu.VMEM((1, BLOCK), jnp.float32),
            pltpu.VMEM((1, BLOCK), jnp.float32),
            pltpu.VMEM((DH, BLOCK), jnp.float32),
        ],
    )
    return pl.pallas_call(
        functools.partial(attend_kernel, parts),
        grid_spec=grid_spec,
        out_shape=[
            jax.ShapeDtypeStruct((rows, DH), jnp.float32),
            jax.ShapeDtypeStruct((rows // BLOCK, 1, BLOCK), jnp.float32),
        ],
        compiler_params=pltpu.CompilerParams(vmem_limit_bytes=48 * 2**20),
        cost_estimate=cost(2e10, 1e7),
        name="attend",
    )(first, clear, queries, *window, *window, pos_q, start_q, pos_k)


def attend_back_kernel(parts, first, clear, q, *refs):
    keys, values = refs[:parts], refs[parts : 2 * parts]
    grad, pos_q, start_q, lse, inner, pos_k, grad_q = refs[2 * parts : 2 * parts + 7]
    grads = refs[2 * parts + 7 : 3 * parts + 7]
    sum_k, sum_v, acc = refs[3 * parts + 7 :]
    at = pl.program_id(0)
    blocks = pl.num_programs(0)
    rate = LOG2E * DH ** (-0.5)
    scale = DH ** (-0.5)

    @pl.when(at == 0)
    def _():
        sum_k[...] = jnp.zeros_like(sum_k)
        sum_v[...] = jnp.zeros_like(sum_v)

    acc[...] = jnp.zeros_like(acc)
    query, grad_out = q[...], grad[...]
    row_at, row_from, row_lse, row_inner = pos_q[0], start_q[0], lse[0], inner[0]

    for part in range(parts):

        def step(masked, block, carry, k=keys[part], v=values[part], part=part):
            rows = pl.ds(pl.multiple_of(block * BLOCK, BLOCK), BLOCK)
            spot = pl.ds(pl.multiple_of((part * blocks + block) * BLOCK, BLOCK), BLOCK)
            key, value = k[rows, :], v[rows, :]
            scores = dot(key, query, 1, 1)
            soft = jnp.exp2(scores * rate - row_lse)
            if masked:
                key_at = pos_k[spot, :]
                soft = jnp.where((key_at >= row_from) & (key_at <= row_at), soft, 0.0)
            grad_soft = dot(value, grad_out, 1, 1)
            grad_scores = (soft * (grad_soft - row_inner)).astype(jnp.bfloat16)
            sum_v[spot, :] += dot(soft.astype(jnp.bfloat16), grad_out, 1, 0)
            sum_k[spot, :] += dot(grad_scores, query, 1, 0)
            acc[...] += dot(grad_scores, key, 0, 0)
            return carry

        run_blocks(step, part, parts, blocks, at, first[at], clear[at])
    grad_q[...] = (acc[...] * scale).astype(jnp.bfloat16)

    @pl.when(at == blocks - 1)
    def _():
        size = grads[0].shape[0]
        for part in range(parts):
            spot = slice(part * size, (part + 1) * size)
            grads[part][:, :DH] = (sum_k[spot, :] * scale).astype(grads[part].dtype)
            grads[part][:, DH:] = sum_v[spot, :].astype(grads[part].dtype)


def attend_back(first, clear, queries, window, grads, pos_q, start_q, lse, inner, pos_k):
    rows = queries.shape[0]
    parts = len(window)
    block = pl.BlockSpec((BLOCK, DH), lambda i, *_: (i, 0))
    line = pl.BlockSpec((1, 1, BLOCK), lambda i, *_: (i, 0, 0))
    grid_spec = pltpu.PrefetchScalarGridSpec(
        num_scalar_prefetch=2,
        grid=(rows // BLOCK,),
        in_specs=[block]
        + [pl.BlockSpec((rows, DH), lambda i, *_: (0, 0))] * parts
        + [pl.BlockSpec((rows, DH), lambda i, *_: (0, 1))] * parts
        + [block, line, line, line, line]
        + [pl.BlockSpec((parts * rows, 1), lambda i, *_: (0, 0))],
        out_specs=[block] + [pl.BlockSpec((rows, 2 * DH), lambda i, *_: (0, 0))] * parts,
        scratch_shapes=[
            pltpu.VMEM((parts * rows, DH), jnp.float32),
            pltpu.VMEM((parts * rows, DH), jnp.float32),
            pltpu.VMEM((BLOCK, DH), jnp.float32),
        ],
    )
    kinds = [jnp.bfloat16] * (parts - 1) + [jnp.float32]
    return pl.pallas_call(
        functools.partial(attend_back_kernel, parts),
        grid_spec=grid_spec,
        out_shape=[jax.ShapeDtypeStruct((rows, DH), jnp.bfloat16)]
        + [jax.ShapeDtypeStruct((rows, 2 * DH), kind) for kind in kinds],
        compiler_params=pltpu.CompilerParams(vmem_limit_bytes=48 * 2**20),
        cost_estimate=cost(2e9, 1e6),
        name="attend_back",
    )(first, clear, queries, *window, *window, grads, pos_q, start_q, lse, inner, pos_k)


def columns_of(ref, group, groups, step, depth):
    at = lax.rem(group + step + groups, groups) * depth
    return ref.at[:, pl.ds(pl.multiple_of(at, 128), depth)]


def front_kernel(groups, local, place, hidden, grads, *refs):
    w_in, w_out = refs[0], refs[1 : groups + 1]
    gates, active, grad_pre, rows_out, turned, acc = refs[groups + 1 :]
    levels, _, depth, width = w_in.shape
    tile = hidden.shape[0]
    model = groups * depth
    parts = [slice(step * depth, (step + 1) * depth) for step in range(groups)]
    for step in range(groups):
        turned[0, :, parts[step]] = columns_of(hidden, place[1], groups, -step, depth)[...]
        turned[1, :, parts[step]] = columns_of(grads, place[1], groups, -step, depth)[...]
    gate_grads = []
    for level in range(levels):
        pre_act = jnp.zeros((tile, width), jnp.float32)
        grad_active = jnp.zeros((tile, width), jnp.float32)
        for step in range(groups):
            pre_act += dot(turned[0, :, parts[step]], w_in[level, step], 1, 0)
            grad_active += dot(turned[1, :, parts[step]], w_out[step][level], 1, 0)
        first = level * local
        gate = jnp.concatenate(
            [jnp.broadcast_to(gates[:, first + e : first + e + 1], (tile, FH)) for e in range(local)],
            axis=1,
        )
        sig = 1.0 / (1.0 + jnp.exp2(-LOG2E * pre_act))
        act_pre = pre_act * sig
        columns = slice(level * width, (level + 1) * width)
        active[:, columns] = (act_pre * gate).astype(jnp.bfloat16)
        product = grad_active * act_pre
        for e in range(local):
            gate_grads.append(
                jnp.sum(product[:, e * FH : (e + 1) * FH], axis=1, keepdims=True)
            )
        slope = sig * (1.0 + pre_act * (1.0 - sig))
        low_pre = (grad_active * gate * slope).astype(jnp.bfloat16)
        grad_pre[:, columns] = low_pre
        for step in range(groups):
            back = dot(low_pre, w_in[level, step], 1, 1)
            acc[:, parts[step]] = back if level == 0 else acc[:, parts[step]] + back
    for step in range(groups):
        columns_of(rows_out, place[1], groups, -step, depth)[...] = acc[:, parts[step]].astype(
            jnp.bfloat16
        )
    spare = rows_out.shape[1] - model
    lane = lax.broadcasted_iota(jnp.int32, (tile, spare), 1) - place[0] * (levels * local)
    spread = jnp.zeros((tile, spare), jnp.float32)
    for e, column in enumerate(gate_grads):
        spread = jnp.where(lane == e, column, spread)
    rows_out[:, model:] = spread.astype(jnp.bfloat16)


def ffn_front(place, hidden, grads, w_in, w_out, gates, local):
    rows, wide = hidden.shape
    levels, groups, depth, width = w_in.shape
    tile = 512

    def by_row(columns):
        return pl.BlockSpec((tile, columns), lambda i, *_: (i, 0))

    once = pl.Buffered(1)
    whole = pl.BlockSpec(w_out[0].shape, lambda i, *_: (0, 0, 0), pipeline_mode=once)
    stacked = pl.BlockSpec(w_in.shape, lambda i, *_: (0, 0, 0, 0), pipeline_mode=once)
    grid_spec = pltpu.PrefetchScalarGridSpec(
        num_scalar_prefetch=1,
        grid=(rows // tile,),
        in_specs=[by_row(wide), by_row(groups * depth)]
        + [stacked]
        + [whole] * groups
        + [by_row(gates.shape[1])],
        out_specs=[by_row(levels * width), by_row(levels * width), by_row(wide)],
        scratch_shapes=[
            pltpu.VMEM((2, tile, groups * depth), jnp.bfloat16),
            pltpu.VMEM((tile, groups * depth), jnp.float32),
        ],
    )
    hidden_units = jax.ShapeDtypeStruct((rows, levels * width), jnp.bfloat16)
    return pl.pallas_call(
        functools.partial(front_kernel, groups, local),
        grid_spec=grid_spec,
        out_shape=[hidden_units, hidden_units, jax.ShapeDtypeStruct((rows, wide), jnp.bfloat16)],
        compiler_params=pltpu.CompilerParams(vmem_limit_bytes=58 * 2**20),
        cost_estimate=cost(6 * rows * groups * depth * levels * width, 3e7),
        name="ffn_front",
    )(place, hidden, grads, w_in, *w_out, gates)


def rear_kernel(groups, place, rows_in, hidden_units, *weight_grads):
    _, depth, _ = weight_grads[0].shape
    units = hidden_units[...]
    for step in range(groups):
        part = columns_of(rows_in, place[1], groups, step, depth)
        weight_grads[step][0] = dot(part[...], units, 0, 0).astype(jnp.bfloat16)


def feed_kernel(groups, place, active, *refs):
    weights = refs[:groups]
    feed, acc = refs[groups:]
    _, depth, _ = weights[0].shape
    level = pl.program_id(0)
    act = active[...]
    for step in range(groups):
        fed = dot(act, weights[step][0], 1, 1)
        part = slice(step * depth, (step + 1) * depth)

        @pl.when(level == 0)
        def _():
            acc[:, part] = fed

        @pl.when(level > 0)
        def _():
            acc[:, part] += fed

    @pl.when(level == pl.num_programs(0) - 1)
    def _():
        for step in range(groups):
            part = slice(step * depth, (step + 1) * depth)
            columns_of(feed, place[1], groups, -step, depth)[...] = acc[:, part].astype(
                jnp.bfloat16
            )


def whole_rows(rows, columns):
    return pl.BlockSpec((rows, columns), lambda i, *_: (0, 0), pipeline_mode=pl.Buffered(1))


def ffn_feed(place, active, weights):
    rows = active.shape[0]
    groups = len(weights)
    levels, depth, width = weights[0].shape
    return pl.pallas_call(
        functools.partial(feed_kernel, groups),
        grid_spec=pltpu.PrefetchScalarGridSpec(
            num_scalar_prefetch=1,
            grid=(levels,),
            in_specs=[pl.BlockSpec((rows, width), lambda i, *_: (0, i))]
            + [pl.BlockSpec((1, depth, width), lambda i, *_: (i, 0, 0))] * groups,
            out_specs=whole_rows(rows, groups * depth),
            scratch_shapes=[pltpu.VMEM((rows, groups * depth), jnp.float32)],
        ),
        out_shape=jax.ShapeDtypeStruct((rows, groups * depth), jnp.bfloat16),
        compiler_params=pltpu.CompilerParams(vmem_limit_bytes=58 * 2**20),
        cost_estimate=cost(1e3, 1e3),
        name="ffn_feed",
    )(place, active, *weights)


def ffn_rear(place, rows_in, units, model, groups, levels):
    rows, wide = rows_in.shape
    width = units.shape[1] // levels
    depth = model // groups
    return pl.pallas_call(
        functools.partial(rear_kernel, groups),
        grid_spec=pltpu.PrefetchScalarGridSpec(
            num_scalar_prefetch=1,
            grid=(levels,),
            in_specs=[
                whole_rows(rows, wide),
                pl.BlockSpec((rows, width), lambda i, *_: (0, i)),
            ],
            out_specs=[pl.BlockSpec((1, depth, width), lambda i, *_: (i, 0, 0))] * groups,
        ),
        out_shape=[jax.ShapeDtypeStruct((levels, depth, width), jnp.bfloat16)] * groups,
        compiler_params=pltpu.CompilerParams(vmem_limit_bytes=58 * 2**20),
        cost_estimate=cost(1e3, 1e3),
        name="ffn_rear",
    )(place, rows_in, units)


def named_by(routes, count):
    lane = lax.broadcasted_iota(jnp.int32, (routes.shape[0], count), 1)
    member = jnp.zeros(lane.shape, jnp.float32)
    for slot in range(routes.shape[1]):
        member = jnp.where(lane == routes[:, slot : slot + 1], 1.0, member)
    return member


def middle_kernel(rows, branch, routes, router, gain, bias, middle, extended, sig_out):
    experts = router.shape[1]
    width = rows.shape[1]
    rounded = branch[...].astype(jnp.bfloat16).astype(jnp.float32)
    value = rows[...].astype(jnp.float32) + rounded
    middle[...] = value
    _, _, normed = normalized(value, gain[...], bias[...])
    sig = 1.0 / (1.0 + jnp.exp2(-LOG2E * dot(normed, router[...], 1, 0)))
    sig_out[...] = sig
    extended[:, :width] = value.astype(jnp.bfloat16)
    gates = (sig * named_by(routes[...], experts)).astype(jnp.bfloat16)
    spare = extended.shape[1] - width - experts
    if spare:
        gates = jnp.concatenate([gates, jnp.zeros((gates.shape[0], spare), gates.dtype)], axis=1)
    extended[:, width:] = gates


def enter_ffn(rows, branch, routes, router, gain, bias):
    count, width = rows.shape
    experts = router.shape[1]
    wide = width + experts + -experts % 128
    return pl.pallas_call(
        middle_kernel,
        out_shape=[
            jax.ShapeDtypeStruct((count, width), jnp.float32),
            jax.ShapeDtypeStruct((count, wide), jnp.bfloat16),
            jax.ShapeDtypeStruct((count, experts), jnp.float32),
        ],
        compiler_params=pltpu.CompilerParams(vmem_limit_bytes=40 * 2**20),
        cost_estimate=cost(1e9, 1e7),
        name="middle",
    )(rows, branch, routes, router, gain, bias)


def leave_kernel(
    middle, own, came, cotangent, sigs, routes, router, gain, bias, grad_out, low_out, weight_grads
):
    experts = router.shape[1]
    count, width = middle.shape
    scaled, inverse, normed = normalized(middle[...], gain[...], bias[...])
    total = own[...] + came[...].astype(jnp.float32)
    sig = sigs[...]
    member = named_by(routes[...], experts)
    gate_grads = total[:, width : width + experts]
    logit = (gate_grads * sig * (1.0 - sig) * member).astype(jnp.bfloat16)
    second = dot(logit, router[...], 1, 1)
    inner_grad = second * gain[...]
    inner_grad = inverse * (
        inner_grad
        - jnp.mean(inner_grad, axis=1, keepdims=True)
        - scaled * jnp.mean(inner_grad * scaled, axis=1, keepdims=True)
    )
    grad = cotangent[...].astype(jnp.float32) + total[:, :width] + inner_grad
    grad_out[...] = grad
    low_out[...] = grad.astype(jnp.bfloat16)
    spare = weight_grads.shape[1] - experts
    sums = [
        jnp.sum(second * scaled, axis=0, keepdims=True),
        jnp.sum(second, axis=0, keepdims=True),
        jnp.zeros((126, width), jnp.float32),
    ]
    side = jnp.concatenate(sums, axis=0).T[:, :spare]
    both = jnp.concatenate([dot(normed, logit, 0, 0), side], axis=1)
    weight_grads[...] = both.astype(jnp.bfloat16)


def leave_ffn(middle, own, came, cotangent, sigs, routes, router, gain, bias):
    count, width = middle.shape
    experts = router.shape[1]
    columns = experts + 2 + -(experts + 2) % 128
    return pl.pallas_call(
        leave_kernel,
        out_shape=[
            jax.ShapeDtypeStruct((count, width), jnp.float32),
            jax.ShapeDtypeStruct((count, width), jnp.bfloat16),
            jax.ShapeDtypeStruct((width, columns), jnp.bfloat16),
        ],
        compiler_params=pltpu.CompilerParams(vmem_limit_bytes=48 * 2**20),
        cost_estimate=cost(1e9, 1e7),
        name="leave_ffn",
    )(middle, own, came, cotangent, sigs, routes, router, gain, bias)


def branch_back_kernel(
    grads, w_output, attended, sigs, masks, grad_attended, inner, out_logit, weight_grads, acc
):
    at = pl.program_id(0)
    count = grads.shape[0]
    sig, mask, values = sigs[...], masks[...], attended[...]
    mixed_grad = dot(grads[...], w_output[...], 1, 0)
    lane = lax.broadcasted_iota(jnp.int32, (count, 128), 1)
    logits = jnp.zeros((count, 128), jnp.float32)
    total = jnp.zeros((count, DH), jnp.float32)
    parts = []
    for e in range(VEXP):
        k = VEXP + e
        one, on = sig[:, k : k + 1], mask[:, k : k + 1]
        part = mixed_grad[:, e * DH : (e + 1) * DH]
        total += part * (one * on)
        gate_grad = jnp.sum(part * values, axis=1, keepdims=True)
        logits = jnp.where(lane == k, gate_grad * one * (1.0 - one) * on, logits)
        parts.append((one * on * values).astype(jnp.bfloat16))
    out_logit[...] = logits.astype(jnp.bfloat16)
    rounded = total.astype(jnp.bfloat16)
    grad_attended[...] = rounded
    product = rounded.astype(jnp.float32) * values
    inner[0] = jnp.sum(product.T, axis=0, keepdims=True)
    amount = dot(grads[...], jnp.concatenate(parts, axis=1), 0, 0)

    @pl.when(at == 0)
    def _():
        acc[...] = amount

    @pl.when(at > 0)
    def _():
        acc[...] += amount

    @pl.when(at == pl.num_programs(0) - 1)
    def _():
        weight_grads[...] = acc[...].astype(jnp.bfloat16)


def branch_back(grads, full, attended, sigs, masks):
    rows, width = grads.shape
    values = VEXP * DH

    def by_row(size):
        return pl.BlockSpec((BLOCK, size), lambda i: (i, 0))

    return pl.pallas_call(
        branch_back_kernel,
        grid=(rows // BLOCK,),
        in_specs=[
            by_row(width),
            pl.BlockSpec((width, values), lambda i: (0, 1), pipeline_mode=pl.Buffered(1)),
            by_row(DH),
            by_row(128),
            by_row(16),
        ],
        out_specs=[
            by_row(DH),
            pl.BlockSpec((1, 1, BLOCK), lambda i: (i, 0, 0)),
            by_row(128),
            pl.BlockSpec((width, values), lambda i: (0, 0)),
        ],
        out_shape=[
            jax.ShapeDtypeStruct((rows, DH), jnp.bfloat16),
            jax.ShapeDtypeStruct((rows // BLOCK, 1, BLOCK), jnp.float32),
            jax.ShapeDtypeStruct((rows, 128), jnp.bfloat16),
            jax.ShapeDtypeStruct((width, values), jnp.bfloat16),
        ],
        scratch_shapes=[pltpu.VMEM((width, values), jnp.float32)],
        compiler_params=pltpu.CompilerParams(vmem_limit_bytes=48 * 2**20),
        cost_estimate=cost(1e8, 1e6),
        name="branch_back",
    )(grads, full, attended, sigs, masks)


def turn(value, axis, by):
    size = lax.axis_size(axis)
    return lax.ppermute(value, axis, [(i, (i + by) % size) for i in range(size)])


def normalized(rows, gain, bias):
    values = rows.astype(jnp.float32)
    centred = values - jnp.mean(values, axis=1, keepdims=True)
    inverse = lax.rsqrt(jnp.mean(centred * centred, axis=1, keepdims=True) + 1e-05)
    scaled = centred * inverse
    return scaled, inverse, (scaled * gain + bias).astype(jnp.bfloat16)


def project_kernel(
    levels, rows, w_value, w_query, w_key, routers, gain, bias, order, tables,
    query, key_value, projected, sigs, masks,
):
    count = rows.shape[0]
    piece = count // (levels * HEADS)
    _, _, normed = normalized(rows[...], gain[...], bias[...])
    query[...] = dot(normed, w_query[...], 1, 0).astype(jnp.bfloat16)
    key_value[:, :DH] = dot(normed, w_key[...], 1, 0).astype(jnp.bfloat16)
    sig = 1.0 / (1.0 + jnp.exp2(-LOG2E * dot(normed, routers[...], 1, 0)))
    sigs[...] = sig
    product = dot(rows[...], w_value[...], 1, 0)
    projected[...] = product
    at = lax.broadcasted_iota(jnp.int32, (count, count), 0)
    source = lax.rem(at // piece, levels) * HEADS + at // (piece * levels)
    here = (source * piece + lax.rem(at, piece) == order[0]).astype(jnp.bfloat16)
    lane = lax.broadcasted_iota(jnp.int32, (16, count), 0)
    table = tables[0]
    named = jnp.zeros((16, count), jnp.float32)
    for which in range(2):
        option = lane - which * VEXP
        for slot in range(2):
            pick = table[2 * which + slot : 2 * which + slot + 1, :]
            hit = (option == pick) & (option >= 0) & (option < VEXP)
            named = jnp.where(hit, 1.0, named)
    mask = dot(here, named.astype(jnp.bfloat16), 1, 1)
    masks[...] = mask
    value = jnp.zeros((count, DH), jnp.float32)
    for e in range(VEXP):
        gate = sig[:, e : e + 1] * mask[:, e : e + 1]
        value += gate * product[:, e * DH : (e + 1) * DH]
    key_value[:, DH:] = value.astype(jnp.bfloat16)


def project(rows, full, gain, bias, orders, tables, levels):
    total, width = rows.shape
    count = total // HEADS

    def by_row(columns):
        return pl.BlockSpec((count, columns), lambda i: (i, 0))

    def column(size, at):
        return pl.BlockSpec((width, size), lambda i: (0, at), pipeline_mode=pl.Buffered(1))

    line = pl.BlockSpec((1, width), lambda i: (0, 0))
    shapes = [(DH, jnp.bfloat16), (2 * DH, jnp.bfloat16), (VEXP * DH, jnp.float32)]
    shapes += [(128, jnp.float32), (16, jnp.float32)]
    return pl.pallas_call(
        functools.partial(project_kernel, levels),
        grid=(HEADS,),
        in_specs=[by_row(width), column(VEXP * DH, 0)]
        + [column(DH, 2 * VEXP + i) for i in range(3)]
        + [line, line]
        + [
            pl.BlockSpec((1, 1, count), lambda i: (i, 0, 0)),
            pl.BlockSpec((1,) + tables.shape[1:], lambda i: (i, 0, 0)),
        ],
        out_specs=[by_row(columns) for columns, _ in shapes],
        out_shape=[jax.ShapeDtypeStruct((total, columns), kind) for columns, kind in shapes],
        compiler_params=pltpu.CompilerParams(vmem_limit_bytes=48 * 2**20),
        cost_estimate=cost(2 * total * width * 1024, 2e7),
        name="project",
    )(rows, full, full, full, full, gain, bias, orders, tables)


def project_back_kernel(
    rows, grads, grad_query, out_logit, projected, sigs, masks,
    w_value, w_query, w_key, routers, gain, bias,
    grad_rows, weight_grads, acc, sums,
):
    at = pl.program_id(0)
    count = rows.shape[0]
    values = VEXP * DH

    @pl.when(at == 0)
    def _():
        acc[...] = jnp.zeros_like(acc)
        sums[...] = jnp.zeros_like(sums)

    scaled, inverse, normed = normalized(rows[...], gain[...], bias[...])
    grad_key = grads[:, :DH].astype(jnp.bfloat16)
    grad_value = grads[:, DH:]
    sig, mask = sigs[...], masks[...]
    lane = lax.broadcasted_iota(jnp.int32, (count, 128), 1)
    logits = out_logit[...].astype(jnp.float32)
    parts = []
    for e in range(VEXP):
        one, on = sig[:, e : e + 1], mask[:, e : e + 1]
        parts.append((one * on * grad_value).astype(jnp.bfloat16))
        inner = jnp.sum(grad_value * projected[:, e * DH : (e + 1) * DH], axis=1, keepdims=True)
        logits = jnp.where(lane == e, inner * one * (1.0 - one) * on, logits)
    grad_projected = jnp.concatenate(parts, axis=1)
    sides = jnp.concatenate([grad_query[...], grad_key, logits.astype(jnp.bfloat16)], axis=1)
    first = dot(sides[:, :DH], w_query[...], 1, 1)
    first += dot(sides[:, DH : 2 * DH], w_key[...], 1, 1)
    first += dot(sides[:, 2 * DH :], routers[...], 1, 1)
    sums[2 * VEXP : 2 * VEXP + 1, :] += jnp.sum(first * scaled, axis=0, keepdims=True)
    sums[2 * VEXP + 1 : 2 * VEXP + 2, :] += jnp.sum(first, axis=0, keepdims=True)
    inner_grad = first * gain[...]
    inner_grad = inverse * (
        inner_grad
        - jnp.mean(inner_grad, axis=1, keepdims=True)
        - scaled * jnp.mean(inner_grad * scaled, axis=1, keepdims=True)
    )
    grad_rows[...] = (inner_grad + dot(grad_projected, w_value[...], 1, 1)).astype(jnp.bfloat16)
    acc[:, :values] += dot(rows[...], grad_projected, 0, 0)
    acc[:, values:] += dot(normed, sides, 0, 0)

    @pl.when(at == pl.num_programs(0) - 1)
    def _():
        weight_grads[:, : values + 2 * DH] = acc[:, : values + 2 * DH].astype(jnp.bfloat16)
        last = acc[:, values + 2 * DH :] + sums[...].T
        weight_grads[:, values + 2 * DH :] = last.astype(jnp.bfloat16)


def project_back(rows, grads, grad_query, out_logit, projected, sigs, masks, full, gain, bias):
    total, width = rows.shape
    count = total // HEADS
    columns = VEXP * DH + 3 * DH

    def by_row(size):
        return pl.BlockSpec((count, size), lambda i: (i, 0))

    def column(size, at):
        return pl.BlockSpec((width, size), lambda i: (0, at), pipeline_mode=pl.Buffered(1))

    line = pl.BlockSpec((1, width), lambda i: (0, 0))
    return pl.pallas_call(
        project_back_kernel,
        grid=(HEADS,),
        in_specs=[by_row(width), by_row(2 * DH), by_row(DH), by_row(128), by_row(VEXP * DH)]
        + [by_row(128), by_row(16), column(VEXP * DH, 0)]
        + [column(DH, 2 * VEXP + i) for i in range(3)]
        + [line, line],
        out_specs=[by_row(width), pl.BlockSpec((width, columns), lambda i: (0, 0))],
        out_shape=[
            jax.ShapeDtypeStruct((total, width), jnp.bfloat16),
            jax.ShapeDtypeStruct((width, columns), jnp.bfloat16),
        ],
        scratch_shapes=[
            pltpu.VMEM((width, columns), jnp.float32),
            pltpu.VMEM((128, width), jnp.float32),
        ],
        compiler_params=pltpu.CompilerParams(vmem_limit_bytes=56 * 2**20),
        cost_estimate=cost(total * width * 512, 4e6),
        name="project_back",
    )(rows, grads, grad_query, out_logit, projected, sigs, masks, full, full, full, full, gain, bias)


def shift(value, axis, by):
    count = lax.axis_size(axis)
    pairs = [(i, i + by) for i in range(count) if 0 <= i + by < count]
    return lax.ppermute(value, axis, pairs)


def body(
    tokens_in,
    out_grad,
    deal_order,
    seq_lengths,
    value_routes,
    output_routes,
    ffn_routes,
    norm1_gain,
    norm1_bias,
    norm2_gain,
    norm2_bias,
    query_weight,
    key_weight,
    value_weight,
    output_weight,
    value_router,
    output_router,
    ffn_router,
    ffn_in,
    ffn_out,
):
    groups = lax.axis_size("group")
    levels = lax.axis_size("level")
    level = lax.axis_index("level")
    head = lax.axis_index("head")
    count, width = tokens_in.shape
    piece = count // (levels * HEADS)
    wrows = query_weight.shape[0]
    experts = ffn_router.shape[1]
    local_experts = ffn_in.shape[1] // FH

    small = jnp.concatenate(
        [
            ffn_router,
            norm1_gain[:, None],
            norm1_bias[:, None],
            norm2_gain[:, None],
            norm2_bias[:, None],
        ],
        axis=1,
    )
    shared = small.shape[1]
    pad = -(shared + 2 * VEXP) % 128
    extra = jnp.concatenate(
        [
            value_router.reshape(wrows, HEADS, VEXP),
            output_router.reshape(wrows, HEADS, VEXP),
            jnp.broadcast_to(small[:, None, :], (wrows, HEADS, shared)),
            jnp.zeros((wrows, HEADS, pad), jnp.bfloat16),
        ],
        axis=2,
    )
    cols = 2 * DH + 2 * VEXP * DH + extra.shape[2]
    tables = jnp.concatenate(
        [value_routes.transpose(1, 2, 0), output_routes.transpose(1, 2, 0)], axis=1
    )
    picks = ffn_routes.reshape(levels, HEADS * piece, -1).transpose(0, 2, 1)
    arrived, own_grads, full, tables, picks, orders = start(
        tokens_in.reshape(levels, HEADS, piece, width),
        out_grad.reshape(levels, HEADS, piece, width),
        [value_weight, output_weight, query_weight, key_weight],
        extra.transpose(1, 0, 2),
        tables,
        picks,
        deal_order,
    )
    worker_in = arrived.reshape(HEADS * count, width)
    own_tokens = lax.dynamic_index_in_dim(arrived, head, 1, keepdims=False).reshape(count, width)
    in_rows = [turn(ffn_in, "group", k) for k in range(1, groups)]
    full, in_rows = lax.optimization_barrier((full.reshape(width, cols), in_rows))

    base = 2 * DH + 2 * VEXP * DH
    w_output = full[:, VEXP * DH : 2 * VEXP * DH]
    at = base + 2 * VEXP
    def relabelled(expert):
        share = expert // local_experts
        return (share % HEADS * levels + share // HEADS) * local_experts + expert % local_experts

    labels = jnp.arange(experts, dtype=jnp.int32)
    moved = low(relabelled(labels)[:, None] == labels[None, :])
    r_ffn = low(
        jnp.dot(full[:, at : at + experts], moved, preferred_element_type=jnp.float32)
    )
    gain_one, bias_one, gain_two, bias_two = (
        full[:, at + experts + i].astype(jnp.float32) for i in range(4)
    )
    gain_row, bias_row = gain_one[None], bias_one[None]
    orders = orders.reshape(levels, HEADS, count)
    own_order = lax.dynamic_index_in_dim(orders, level, 0, keepdims=False)[:, None, :]
    queries, key_value, projected, sigs, masks = project(
        worker_in, full, gain_row, bias_row, own_order, tables, levels
    )

    rows = HEADS * count
    reach = -(-LMAX // rows)

    ramp = jnp.arange(count, dtype=jnp.int32)

    def arrival(values):
        lead, shape = values.shape[:-3], values.shape[-1:]
        four = values.reshape(lead + (HEADS, levels, HEADS, piece) + shape)
        return jnp.swapaxes(four, -4, -3).reshape(lead + (rows,) + shape)

    orders = jnp.concatenate([jnp.zeros((reach, HEADS, count), jnp.int32), orders], axis=0)
    orders = lax.dynamic_slice_in_dim(orders, level, reach + 1, 0)
    here = orders[:, :, None, :] == ramp[None, None, :, None]
    inverse = jnp.sum(here * ramp, axis=3)
    shard = (level - reach + jnp.arange(reach + 1, dtype=jnp.int32))[:, None] * HEADS
    shard = shard + jnp.arange(HEADS, dtype=jnp.int32)[None, :]
    pos_all = jnp.where(shard[:, :, None] < 0, -1, shard[:, :, None] * count + inverse)
    pos_all = arrival(pos_all[..., None]).reshape(-1)
    positions = pos_all[reach * rows :]
    seq_ends = jnp.cumsum(seq_lengths[0])

    def starts_of(places):
        return jnp.max(jnp.where(seq_ends <= places[:, None], seq_ends, 0), axis=1)

    starts = starts_of(positions)
    blocks = rows // BLOCK
    base_block = (level - reach) * blocks
    first_block = starts_of(level * rows + jnp.arange(blocks, dtype=jnp.int32) * BLOCK) // BLOCK
    first_block = jnp.maximum(first_block - base_block, 0)
    ends = level * rows + jnp.arange(1, blocks + 1, dtype=jnp.int32) * BLOCK - 1
    clear_block = (starts_of(ends) + BLOCK - 1) // BLOCK - base_block

    own_routes = picks.reshape(levels, -1, HEADS, piece).transpose(2, 0, 3, 1).reshape(count, -1)
    own_routes = relabelled(own_routes)
    ffn_side = (own_routes, r_ffn, gain_two[None], bias_two[None], own_tokens)

    window = [key_value]
    own_grads = own_grads.reshape(count, width)
    for i in range(reach):
        came = shift(window[0], "level", 1)
        if i == 0:
            came, own_grads, pos_all, starts, ffn_out, in_rows = lax.optimization_barrier(
                (came, own_grads, pos_all, starts, ffn_out, [ffn_in] + in_rows)
            )
            cotangent = level_gather(own_grads, 5, True)
        if i == reach - 1:
            came, cotangent, ffn_side = lax.optimization_barrier((came, cotangent, ffn_side))
        window.insert(0, came)
    place = jnp.stack([head, lax.axis_index("group")])
    out_here = lax.all_gather(ffn_out, "level", axis=0)
    w_in = lax.all_gather(jnp.stack(in_rows), "level", axis=0)


    def lines(values):
        return values.reshape(blocks, 1, BLOCK)

    attended, log_total = attend(
        first_block,
        clear_block,
        queries,
        window,
        lines(positions),
        lines(starts),
        pos_all[:, None],
    )

    out_sig = sigs[:, VEXP : 2 * VEXP]
    out_mask = masks[:, VEXP : 2 * VEXP]
    out_gate = out_sig * out_mask
    attended, out_here = lax.optimization_barrier((attended, out_here))
    w_out = [out_here] + [turn(out_here, "group", k) for k in range(1, groups)]
    mixed = low((out_gate[..., None] * attended[:, None, :]).reshape(rows, VEXP * DH))
    branch = level_scatter(low(transposed(mixed, w_output)), 2)

    own_routes, r_ffn, gain_two, bias_two, own_tokens = ffn_side
    middle, extended, ffn_sig = enter_ffn(own_tokens, branch, own_routes, r_ffn, gain_two, bias_two)
    hidden = level_gather(extended, 3, True)
    mine = levels * local_experts
    gates = lax.dynamic_slice_in_dim(hidden, width + head * mine, mine, 1).astype(jnp.float32)
    active, grad_pre, grad_rows = ffn_front(
        place, hidden, cotangent, w_in, w_out, gates, local_experts
    )
    summed, beyond = pair_scatter(grad_rows, 4, True)
    beyond, hidden = lax.optimization_barrier((beyond, hidden))
    came = to_far(beyond)
    grad_in = ffn_rear(place, hidden, grad_pre, width, groups, levels)
    in_came = [turn(grad_in[k], "group", k) for k in range(1, groups)]
    grad_out = ffn_rear(place, cotangent, active, width, groups, levels)
    out_came = [turn(grad_out[k], "group", k) for k in range(1, groups)]
    came, grad_in, grad_out = lax.optimization_barrier((came, grad_in, grad_out))
    grad_middle, own_branch, early = leave_ffn(
        middle, summed, came, own_grads, ffn_sig, own_routes, r_ffn, gain_two, bias_two
    )
    came = to_far(own_branch)
    feed = ffn_feed(place, active, w_out)
    came, feed = lax.optimization_barrier((came, feed))
    grad_branch = pair_gather(own_branch, came, 7)

    def sum_of(own, others):
        total = own[0].astype(jnp.float32)
        for other in others:
            total = total + other.astype(jnp.float32)
        return low(total)

    def over_levels(total):
        return lax.psum_scatter(total, "level", scatter_dimension=0)

    grad_branch, in_came = lax.optimization_barrier((grad_branch, in_came))
    ffn_in_grad = over_levels(sum_of(grad_in, in_came))
    grad_attended, row_inner, grad_out_logit, grad_w_output = branch_back(
        grad_branch, full, attended, sigs, masks
    )
    grad_queries, *grad_window = attend_back(
        first_block,
        clear_block,
        queries,
        window,
        grad_attended,
        lines(positions),
        lines(starts),
        log_total,
        row_inner,
        pos_all[:, None],
    )
    came = shift(grad_window[0], "level", -1)
    fed, beyond = pair_scatter(feed, 6, True)
    for i in range(1, reach + 1):
        if i < reach:
            came, fed = lax.optimization_barrier((came, fed))
        grad_both = grad_window[i].astype(jnp.float32) + came.astype(jnp.float32)
        if i < reach:
            grad_keys_sent = low(grad_both)
            came = shift(grad_keys_sent, "level", -1)
    grad_both, out_came = lax.optimization_barrier((grad_both, out_came))
    ffn_out_grad = over_levels(sum_of(grad_out, out_came))
    fed_far = to_far(beyond)
    grad_inputs, late = project_back(
        worker_in,
        grad_both,
        grad_queries,
        grad_out_logit,
        projected,
        sigs,
        masks,
        full,
        gain_row,
        bias_row,
    )

    fed_far, grad_inputs = lax.optimization_barrier((fed_far, grad_inputs))
    layer_out = to_home(low(middle + fed + fed_far.astype(jnp.float32)))

    values = VEXP * DH
    layout = (
        ((0, values, True), (values, DH, True), (values + DH, DH, True), (values + 2 * DH, DH, False)),
        ((0, values, True),),
        ((0, early.shape[1], False),),
    )

    def by_owner(grads):
        return grads.reshape(groups, levels, HEADS, wrows, -1)

    input_grad, grad_value, grad_query, grad_key, sides, grad_output, common = finish(
        layout,
        grad_inputs.reshape(HEADS, HEADS, levels * piece, width),
        grad_middle.reshape(HEADS, levels * piece, width),
        by_owner(late),
        by_owner(grad_w_output),
        by_owner(early),
    )
    norms = jnp.sum(sides[:, :, 2 * VEXP : 2 * VEXP + 2], axis=0)
    common = jnp.sum(common[:, :, : experts + 2], axis=0)
    router_grad = common[:, :experts].reshape(wrows, HEADS, levels, local_experts)

    def side(first):
        return sides[:, :, first : first + VEXP].transpose(1, 0, 2).reshape(wrows, HEADS * VEXP)

    return (
        layer_out,
        input_grad.reshape(count, width),
        norms[:, 0],
        norms[:, 1],
        common[:, experts],
        common[:, experts + 1],
        grad_query,
        grad_key,
        grad_value,
        grad_output,
        side(0),
        side(VEXP),
        jnp.swapaxes(router_grad, 1, 2).reshape(wrows, experts),
        ffn_in_grad.astype(jnp.float32),
        ffn_out_grad.astype(jnp.float32),
    )


def solution(mesh):
    groups, shards = mesh.devices.shape
    fine = Mesh(mesh.devices.reshape(groups, shards // HEADS, HEADS), TOK)
    two, one, three = P(TOK, None), P(TOK), P(TOK, None, None)
    ffn = P("group", ("level", "head"))
    return jax.shard_map(
        body,
        mesh=fine,
        in_specs=(two, two, two, P("group", None), three, three, two, one, one, one, one)
        + (two,) * 7
        + (ffn, ffn),
        out_specs=(two, two, one, one, one, one) + (two,) * 7 + (ffn, ffn),
        check_vma=False,
    )
```

```python
import functools

import jax
import jax.numpy as jnp
from jax import lax
from jax.experimental import pallas as pl
from jax.experimental.pallas import tpu as pltpu
from jax.sharding import Mesh, PartitionSpec as P

HEADS = 4
DH = 128
VEXP = 5
FH = 128
LMAX = 4096

TOK = ("group", "level", "head")


def transposed(left_side, right_side):
    return lax.dot_general(
        left_side, right_side, (((1,), (1,)), ((), ())), preferred_element_type=jnp.float32
    )


def low(value):
    return value.astype(jnp.bfloat16)


def to_home(rows):
    levels = lax.axis_size("level")
    count = rows.shape[0]
    out = rows.reshape(HEADS, levels, count // levels // HEADS, -1).transpose(1, 0, 2, 3)
    back = lax.all_to_all(
        out.reshape(levels, count // levels, -1), "level", split_axis=0, concat_axis=0, tiled=True
    )
    return back.reshape(count, -1)


MESH = pl.DeviceIdType.MESH


def partners(head):
    near = head + 1 - 2 * lax.rem(head, 2)
    far = lax.rem(head + 2, HEADS)
    return near, far


def greet(near, far):
    barrier = pltpu.get_barrier_semaphore()
    for peer in (near, far):
        pl.semaphore_signal(barrier, inc=1, device_id={"head": peer}, device_id_type=MESH)
    pl.semaphore_wait(barrier, 2)


def remote(src, dst, send, recv, peer):
    return pltpu.make_async_remote_copy(
        src_ref=src,
        dst_ref=dst,
        send_sem=send,
        recv_sem=recv,
        device_id={"head": peer},
        device_id_type=MESH,
    )


def cost(flops, moved):
    return pl.CostEstimate(flops=int(flops), bytes_accessed=int(moved), transcendentals=0)


def gather_kernel(
    by_source, own, out, local_sem, near_send, near_recv, far_send, far_recv, pass_send, pass_recv
):
    head = lax.axis_index("head")
    near, far = partners(head)
    greet(near, far)

    def spot(i, source):
        return out.at[source, i] if by_source else out.at[i, source]

    pieces = range(HEADS)
    to_far = [remote(own.at[i], spot(i, head), far_send.at[i], far_recv.at[i], far) for i in pieces]
    to_near = [
        remote(own.at[i], spot(i, head), near_send.at[i], near_recv.at[i], near) for i in pieces
    ]
    passed = [
        remote(spot(i, far), spot(i, far), pass_send.at[i], pass_recv.at[i], near) for i in pieces
    ]
    kept = [pltpu.make_async_copy(own.at[i], spot(i, head), local_sem.at[i]) for i in pieces]
    for copy in to_far + to_near + kept:
        copy.start()
    for i in pieces:
        to_far[i].wait_recv()
        passed[i].start()
    for i in pieces:
        to_near[i].wait_recv()
        passed[i].wait_recv()
        kept[i].wait()
        to_far[i].wait_send()
        to_near[i].wait_send()
        passed[i].wait_send()


def level_gather(rows, collective_id, by_source=False):
    count, width = rows.shape
    whole = pl.pallas_call(
        functools.partial(gather_kernel, by_source),
        out_shape=jax.ShapeDtypeStruct((HEADS, HEADS, count // HEADS, width), rows.dtype),
        in_specs=[pl.BlockSpec(memory_space=pltpu.VMEM)],
        out_specs=pl.BlockSpec(memory_space=pl.ANY),
        scratch_shapes=[pltpu.SemaphoreType.DMA((HEADS,))] * 7,
        compiler_params=pltpu.CompilerParams(collective_id=collective_id, has_side_effects=True),
        cost_estimate=cost(0, 90e6),
        name="level_gather",
    )(rows.reshape(HEADS, count // HEADS, width))
    return whole.reshape(HEADS * count, width)


def scatter_kernel(
    by_source, part, out, near_buf, send_buf, far_buf, near_send, near_recv, far_send, far_recv
):
    head = lax.axis_index("head")
    near, far = partners(head)
    greet(near, far)
    across = HEADS - 1 - head
    pieces = range(HEADS)

    def spot(i, dest):
        return (dest, i) if by_source else (i, dest)

    def to_near(slot, i, dest):
        return remote(
            part.at[spot(i, dest)],
            near_buf.at[slot, i],
            near_send.at[slot, i],
            near_recv.at[slot, i],
            near,
        )

    first = [to_near(0, i, across) for i in pieces]
    second = [to_near(1, i, near) for i in pieces]
    onward = [
        remote(send_buf.at[i], far_buf.at[i], far_send.at[i], far_recv.at[i], far) for i in pieces
    ]
    for copy in first + second:
        copy.start()
    for i in pieces:
        first[i].wait_recv()
        both = part[spot(i, far)].astype(jnp.float32) + near_buf[0, i].astype(jnp.float32)
        send_buf[i] = both.astype(jnp.bfloat16)
        onward[i].start()
    for i in pieces:
        second[i].wait_recv()
        out[i] = part[spot(i, head)].astype(jnp.float32) + near_buf[1, i].astype(jnp.float32)
    for i in pieces:
        onward[i].wait_recv()
        out[i] = out[i] + far_buf[i].astype(jnp.float32)
    for i in pieces:
        first[i].wait_send()
        second[i].wait_send()
        onward[i].wait_send()


def level_scatter(rows, collective_id, by_source=False):
    total, width = rows.shape
    piece = total // (HEADS * HEADS)
    low_type = jnp.bfloat16
    mine = pl.pallas_call(
        functools.partial(scatter_kernel, by_source),
        out_shape=jax.ShapeDtypeStruct((HEADS, piece, width), jnp.float32),
        in_specs=[pl.BlockSpec(memory_space=pltpu.VMEM)],
        out_specs=pl.BlockSpec(memory_space=pltpu.VMEM),
        scratch_shapes=[
            pltpu.VMEM((2, HEADS, piece, width), low_type),
            pltpu.VMEM((HEADS, piece, width), low_type),
            pltpu.VMEM((HEADS, piece, width), low_type),
            pltpu.SemaphoreType.DMA((2, HEADS)),
            pltpu.SemaphoreType.DMA((2, HEADS)),
            pltpu.SemaphoreType.DMA((HEADS,)),
            pltpu.SemaphoreType.DMA((HEADS,)),
        ],
        compiler_params=pltpu.CompilerParams(
            collective_id=collective_id, has_side_effects=True, vmem_limit_bytes=32 * 2**20
        ),
        cost_estimate=cost(0, 80e6),
        name="level_scatter",
    )(rows.reshape(HEADS, HEADS, piece, width))
    return mine.reshape(HEADS * piece, width)


def meet(near):
    barrier = pltpu.get_barrier_semaphore()
    pl.semaphore_signal(barrier, inc=1, device_id={"head": near}, device_id_type=MESH)
    pl.semaphore_wait(barrier, 1)


def pair_scatter_kernel(by_source, part, out, out_far, near_buf, send, recv):
    head = lax.axis_index("head")
    near, far = partners(head)
    meet(near)
    across = HEADS - 1 - head
    pieces = range(HEADS)

    def spot(i, dest):
        return (dest, i) if by_source else (i, dest)

    def to_near(slot, i, dest):
        return remote(
            part.at[spot(i, dest)], near_buf.at[slot, i], send.at[slot, i], recv.at[slot, i], near
        )

    first = [to_near(0, i, across) for i in pieces]
    second = [to_near(1, i, near) for i in pieces]
    for copy in first + second:
        copy.start()
    for i in pieces:
        first[i].wait_recv()
        both = part[spot(i, far)].astype(jnp.float32) + near_buf[0, i].astype(jnp.float32)
        out_far[i] = both.astype(jnp.bfloat16)
    for i in pieces:
        second[i].wait_recv()
        out[i] = part[spot(i, head)].astype(jnp.float32) + near_buf[1, i].astype(jnp.float32)
    for i in pieces:
        first[i].wait_send()
        second[i].wait_send()


def pair_scatter(rows, collective_id, by_source=False):
    total, width = rows.shape
    piece = total // (HEADS * HEADS)
    mine, other = pl.pallas_call(
        functools.partial(pair_scatter_kernel, by_source),
        out_shape=[
            jax.ShapeDtypeStruct((HEADS, piece, width), jnp.float32),
            jax.ShapeDtypeStruct((HEADS, piece, width), jnp.bfloat16),
        ],
        in_specs=[pl.BlockSpec(memory_space=pltpu.VMEM)],
        out_specs=[pl.BlockSpec(memory_space=pltpu.VMEM)] * 2,
        scratch_shapes=[
            pltpu.VMEM((2, HEADS, piece, width), jnp.bfloat16),
            pltpu.SemaphoreType.DMA((2, HEADS)),
            pltpu.SemaphoreType.DMA((2, HEADS)),
        ],
        compiler_params=pltpu.CompilerParams(
            collective_id=collective_id, has_side_effects=True, vmem_limit_bytes=32 * 2**20
        ),
        cost_estimate=cost(0, 25e6),
        name="pair_scatter",
    )(rows.reshape(HEADS, HEADS, piece, width))
    return mine.reshape(HEADS * piece, width), other.reshape(HEADS * piece, width)


def pair_gather_kernel(by_source, own, other, out, local_sem, send, recv):
    head = lax.axis_index("head")
    near, far = partners(head)
    meet(near)
    copies, kept = [], []
    for i in range(HEADS):
        for slot, (block, source) in enumerate(((own, head), (other, far))):
            place = out.at[source, i] if by_source else out.at[i, source]
            copies.append(
                remote(block.at[i], place, send.at[slot, i], recv.at[slot, i], near)
            )
            kept.append(pltpu.make_async_copy(block.at[i], place, local_sem.at[slot, i]))
    for copy in copies + kept:
        copy.start()
    for copy in copies + kept:
        copy.wait()


def pair_gather(own, other, collective_id, by_source=False):
    count, width = own.shape
    split = (HEADS, count // HEADS, width)
    whole = pl.pallas_call(
        functools.partial(pair_gather_kernel, by_source),
        out_shape=jax.ShapeDtypeStruct((HEADS,) + split, own.dtype),
        in_specs=[pl.BlockSpec(memory_space=pltpu.VMEM)] * 2,
        out_specs=pl.BlockSpec(memory_space=pl.ANY),
        scratch_shapes=[pltpu.SemaphoreType.DMA((2, HEADS))] * 3,
        compiler_params=pltpu.CompilerParams(collective_id=collective_id, has_side_effects=True),
        cost_estimate=cost(0, 25e6),
        name="pair_gather",
    )(own.reshape(split), other.reshape(split))
    return whole.reshape(HEADS * count, width)


def to_far(rows):
    return lax.ppermute(rows, "head", [(i, (i + 2) % HEADS) for i in range(HEADS)])


def ring(axis):
    me, size = lax.axis_index(axis), lax.axis_size(axis)
    ahead = [lax.rem(me + k, size) for k in range(1, size)]
    behind = [lax.rem(me + size - k, size) for k in range(1, size)]
    return me, ahead, behind


def reach_out(src, dst, send, recv, peer):
    return pltpu.make_async_remote_copy(
        src_ref=src, dst_ref=dst, send_sem=send, recv_sem=recv, device_id=peer, device_id_type=MESH
    )


def greet_all(peers):
    barrier = pltpu.get_barrier_semaphore()
    for peer in peers:
        pl.semaphore_signal(barrier, inc=1, device_id=peer, device_id_type=MESH)
    pl.semaphore_wait(barrier, len(peers))


def start_kernel(
    tokens, cotangents, value, output, query, key, extra, tables, picks, order,
    rows, grads, full, routes, chosen_rows, orders, weights, own_sem, *sems
):
    sems = iter(sems)

    def pair():
        return next(sems), next(sems)

    group, groups_ahead, _ = ring("group")
    level, levels_ahead, levels_behind = ring("level")
    head = lax.axis_index("head")
    near, far = partners(head)
    mates = [near, far, HEADS - 1 - head]
    for to in range(HEADS):
        at = 0
        for part in (value, output, query, key):
            size = part.shape[1] // HEADS
            weights[to, :, at : at + size] = part[:, to * size : (to + 1) * size]
            at += size
        weights[to, :, at:] = extra[to]
    greet_all(
        [{"head": m} for m in mates]
        + [{"level": n} for n in levels_ahead]
        + [{"group": n} for n in groups_ahead]
    )
    started = []

    def send(src, dst, send_sem, recv_sem, peer):
        copy = reach_out(src, dst, send_sem, recv_sem, peer)
        copy.start()
        started.append(copy)
        return copy

    out_s, out_r = pair()
    pick_s, pick_r = pair()
    crossing, picking = [], []
    for k, to in enumerate(levels_ahead):
        peer = {"level": to}
        crossing.append(send(tokens.at[to], rows.at[:, head, level], out_s.at[k], out_r.at[k], peer))
    mate_s, mate_r = pair()
    table_s, table_r = pair()
    order_s, order_r = pair()
    to_mates, order_mates, table_mates = [], [], []
    for k, to in enumerate(mates):
        peer = {"head": to}
        to_mates.append(
            send(weights.at[to], full.at[group, level, head], mate_s.at[k], mate_r.at[k], peer)
        )
        order_mates.append(
            send(order, orders.at[level, head], order_s.at[k], order_r.at[k], peer)
        )
    own = [
        (tokens.at[level], rows.at[:, head, level]),
        (weights.at[head], full.at[group, level, head]),
        (tables.at[head], routes.at[head]),
        (picks.at[level], chosen_rows.at[level]),
        (order, orders.at[level, head]),
        (cotangents.at[level], grads.at[:, level]),
    ]
    own = [pltpu.make_async_copy(src, dst, own_sem.at[i]) for i, (src, dst) in enumerate(own)]
    for copy in own:
        copy.start()
    far_s, far_r = pair()
    near_s, near_r = pair()
    pass_s, pass_r = pair()
    to_far, to_near = [], []

    def share(k, src, source):
        place = rows.at[:, head, source]
        to_far.append(send(src, place, far_s.at[k], far_r.at[k], {"head": far}))
        to_near.append(send(src, place, near_s.at[k], near_r.at[k], {"head": near}))

    share(0, tokens.at[level], level)
    up_s, up_r = pair()
    down_s, down_r = pair()
    group_s, group_r = pair()
    orders_s, orders_r = pair()
    for copy in to_mates:
        copy.wait_recv()
    own[1].wait()
    last = len(levels_ahead)
    ordered = []

    def to_groups(j):
        block = full.at[group, lax.rem(level - j + last + 1, last + 1)]
        return [
            reach_out(block, block, group_s.at[k, j], group_r.at[k, j], {"group": to})
            for k, to in enumerate(groups_ahead)
        ]

    def hop(k, step):
        send_sem, recv_sem = (up_s, up_r) if step > 0 else (down_s, down_r)
        block = full.at[group, lax.rem(level - step * k + last + 1, last + 1)]
        to = lax.rem(level + step + last + 1, last + 1)
        return reach_out(block, block, send_sem.at[k], recv_sem.at[k], {"level": to})

    def sends(k, step):
        return (level >= k) & (level < last) if step > 0 else (level <= last - k) & (level > 0)

    def receives(k, step):
        return level >= k + 1 if step > 0 else level <= last - k - 1

    def start_hop(k, step):
        @pl.when(sends(k, step))
        def _():
            hop(k, step).start()

    def wait_hop(k, step):
        @pl.when(receives(k, step))
        def _():
            hop(k, step).wait_recv()
            for copy in to_groups(k + 1 if step > 0 else last - k):
                copy.start()

    for step in (1, -1):
        start_hop(0, step)
    for copy in to_groups(0):
        copy.start()
    grouped = [copy for j in range(last + 1) for copy in to_groups(j)]
    for k, to in enumerate(mates):
        table_mates.append(
            send(tables.at[to], routes.at[head], table_s.at[k], table_r.at[k], {"head": to})
        )
    for k, to in enumerate(levels_ahead):
        picking.append(
            send(picks.at[to], chosen_rows.at[level], pick_s.at[k], pick_r.at[k], {"level": to})
        )
    for copy in order_mates:
        copy.wait_recv()
    own[4].wait()
    for k, to in enumerate(levels_ahead):
        block = orders.at[level]
        ordered.append(send(block, block, orders_s.at[k], orders_r.at[k], {"level": to}))
    def finish_hop(k):
        for step in (1, -1):
            wait_hop(k, step)
            if k + 1 < last:
                start_hop(k + 1, step)

    if last:
        finish_hop(0)
    for k, source in enumerate(levels_behind):
        crossing[k].wait_recv()
        share(k + 1, rows.at[:, head, source], source)
    grad_s, grad_r = pair()
    crossed = []
    for k, to in enumerate(levels_ahead):
        crossed.append(
            send(cotangents.at[to], grads.at[:, level], grad_s.at[k], grad_r.at[k], {"level": to})
        )
    for k in range(1, last):
        finish_hop(k)
    passed = []
    for k, source in enumerate([level] + levels_behind):
        to_far[k].wait_recv()
        place = rows.at[:, far, source]
        passed.append(send(place, place, pass_s.at[k], pass_r.at[k], {"head": near}))
    for copy in to_near + passed + grouped + table_mates + picking + ordered + crossed:
        copy.wait_recv()
    for copy in started + grouped:
        copy.wait_send()
    for k in range(last):
        for step in (1, -1):

            @pl.when(sends(k, step))
            def _(k=k, step=step):
                hop(k, step).wait_send()

    for i in (0, 2, 3, 5):
        own[i].wait()


def start(tokens, cotangents, weights, extra, tables, picks, order):
    groups, levels = lax.axis_size("group"), lax.axis_size("level")
    _, _, piece, width = tokens.shape
    columns = sum(part.shape[1] for part in weights) // HEADS + extra.shape[2]
    block = extra.shape[:2] + (columns,)
    shapes = [
        jax.ShapeDtypeStruct((HEADS, HEADS, levels, piece, width), tokens.dtype),
        jax.ShapeDtypeStruct((HEADS, levels, piece, width), tokens.dtype),
        jax.ShapeDtypeStruct((groups, levels) + block, extra.dtype),
        jax.ShapeDtypeStruct(tables.shape, tables.dtype),
        jax.ShapeDtypeStruct(picks.shape, picks.dtype),
        jax.ShapeDtypeStruct((levels, HEADS) + order.shape, order.dtype),
    ]
    dma = pltpu.SemaphoreType.DMA
    others, mates = (levels - 1,), (HEADS - 1,)
    counts = [others] * 2 + [mates] * 3 + [(levels,)] * 3
    counts += [others, others, (groups - 1, levels), others, others]
    return pl.pallas_call(
        start_kernel,
        out_shape=shapes,
        in_specs=[pl.BlockSpec(memory_space=pltpu.VMEM)] * 10,
        out_specs=[pl.BlockSpec(memory_space=pl.ANY)] * 6,
        scratch_shapes=[pltpu.VMEM(block, extra.dtype), dma((6,))] + [dma(c) for c in counts for _ in range(2)],
        compiler_params=pltpu.CompilerParams(collective_id=9, has_side_effects=True),
        cost_estimate=cost(0, 200e6),
        name="start",
    )(tokens, cotangents, *weights, extra, tables, picks, order)


def finish_kernel(layout, *refs):
    refs = iter(refs)
    count = len(layout)

    def take(n):
        return [next(refs) for _ in range(n)]

    part, middle = take(2)
    grads = take(count)
    (home_grad,) = take(1)
    results = [take(len(pieces)) for pieces in layout]
    near_buf, send_buf, far_buf, total, back_buf, came_buf = take(6)
    group_buf, level_send, level_buf, head_send, owned = (take(count) for _ in range(5))

    def pair():
        return next(refs), next(refs)

    group, groups_ahead, _ = ring("group")
    level, levels_ahead, levels_behind = ring("level")
    head = lax.axis_index("head")
    near, far = partners(head)
    across = HEADS - 1 - head
    mates = [near, far, across]
    greet_all(
        [{"head": m} for m in mates]
        + [{"level": n} for n in levels_ahead]
        + [{"group": n} for n in groups_ahead]
    )
    started = []

    def send(src, dst, send_sem, recv_sem, peer):
        copy = reach_out(src, dst, send_sem, recv_sem, peer)
        copy.start()
        started.append(copy)
        return copy

    pieces = range(HEADS)
    sets = range(count)
    near_s, near_r = pair()
    far_s, far_r = pair()
    back_s, back_r = pair()
    group_s, group_r = pair()
    level_s, level_r = pair()
    mate_s, mate_r = pair()
    first, second, onward = [], [], []
    for slot, (dest, copies) in enumerate(((across, first), (near, second))):
        for i in pieces:
            copies.append(
                send(
                    part.at[i, dest],
                    near_buf.at[slot, i],
                    near_s.at[slot, i],
                    near_r.at[slot, i],
                    {"head": near},
                )
            )
    order = levels_ahead + [level]
    grouped = {}
    for j, dest in enumerate(order):
        for p in sets:
            grouped[j, p] = [
                send(
                    grads[p].at[to, dest],
                    group_buf[p].at[k, j],
                    group_s.at[p, k, j],
                    group_r.at[p, k, j],
                    {"group": to},
                )
                for k, to in enumerate(groups_ahead)
            ]
    for i in pieces:
        first[i].wait_recv()
        both = part[i, far].astype(jnp.float32) + near_buf[0, i].astype(jnp.float32)
        send_buf[i] = both.astype(jnp.bfloat16)
        onward.append(send(send_buf.at[i], far_buf.at[i], far_s.at[i], far_r.at[i], {"head": far}))
    for i in pieces:
        second[i].wait_recv()
        both = part[i, head].astype(jnp.float32) + near_buf[1, i].astype(jnp.float32)
        total[i] = both + middle[i]
    leveled = {}
    for j, dest in enumerate(order):
        for p in sets:
            amount = grads[p][group, dest].astype(jnp.float32)
            for k, copy in enumerate(grouped[j, p]):
                copy.wait_recv()
                amount = amount + group_buf[p][k, j].astype(jnp.float32)
            level_send[p][j] = amount.astype(jnp.bfloat16)
            if j < len(levels_ahead):
                leveled[j, p] = send(
                    level_send[p].at[j],
                    level_buf[p].at[j],
                    level_s.at[p, j],
                    level_r.at[p, j],
                    {"level": dest},
                )
    for i in pieces:
        onward[i].wait_recv()
        both = total[i] + far_buf[i].astype(jnp.float32)
        back_buf[i] = both.astype(jnp.bfloat16).reshape(back_buf.shape[1:])
    backs = [
        send(back_buf.at[:, to], came_buf.at[level], back_s.at[k], back_r.at[k], {"level": to})
        for k, to in enumerate(levels_ahead)
    ]
    sharing = []
    for p in sets:
        amount = level_send[p][len(levels_ahead)].astype(jnp.float32)
        for j in range(len(levels_ahead)):
            leveled[j, p].wait_recv()
            amount = amount + level_buf[p][j].astype(jnp.float32)
        head_send[p][...] = amount.astype(jnp.bfloat16)
        sharing += [
            send(
                head_send[p].at[to],
                owned[p].at[head],
                mate_s.at[p, k],
                mate_r.at[p, k],
                {"head": to},
            )
            for k, to in enumerate(mates)
        ]
        owned[p][head] = head_send[p][head]
    home_grad[level] = back_buf[:, level].astype(jnp.float32)
    for k, source in enumerate(levels_behind):
        backs[k].wait_recv()
        home_grad[source] = came_buf[source].astype(jnp.float32)
    for copy in sharing:
        copy.wait_recv()
    for p in sets:
        for out, (first_column, size, joined) in zip(results[p], layout[p]):
            for h in range(HEADS):
                value = owned[p][h, :, first_column : first_column + size].astype(jnp.float32)
                if joined:
                    out[:, h * size : (h + 1) * size] = value
                else:
                    out[h] = value
    for copy in started:
        copy.wait_send()


def finish(layout, part, middle, *grads):
    groups, levels = lax.axis_size("group"), lax.axis_size("level")
    _, count, width = middle.shape
    piece = count // levels
    low_type = jnp.bfloat16
    blocks = [grad.shape[2:] for grad in grads]
    sets = len(grads)
    dma = pltpu.SemaphoreType.DMA
    counts = [(2, HEADS), (HEADS,), (levels - 1,)]
    counts += [(sets, groups - 1, levels), (sets, levels - 1), (sets, HEADS - 1)]
    vmem = pl.BlockSpec(memory_space=pltpu.VMEM)
    shapes = []
    for pieces in layout:
        for _, size, joined in pieces:
            shape = (blocks[0][1], HEADS * size) if joined else (HEADS, blocks[0][1], size)
            shapes.append(jax.ShapeDtypeStruct(shape, jnp.float32))
    return pl.pallas_call(
        functools.partial(finish_kernel, layout),
        out_shape=[jax.ShapeDtypeStruct((levels, HEADS, piece, width), jnp.float32)] + shapes,
        in_specs=[vmem] * (2 + sets),
        out_specs=[vmem] * (1 + len(shapes)),
        scratch_shapes=[
            pltpu.VMEM((2, HEADS, count, width), low_type),
            pltpu.VMEM((HEADS, count, width), low_type),
            pltpu.VMEM((HEADS, count, width), low_type),
            pltpu.VMEM((HEADS, count, width), jnp.float32),
            pltpu.VMEM((HEADS, levels, piece, width), low_type),
            pltpu.VMEM((levels, HEADS, piece, width), low_type),
        ]
        + [pltpu.VMEM((groups - 1, levels) + block, low_type) for block in blocks]
        + [pltpu.VMEM((levels,) + block, low_type) for block in blocks]
        + [pltpu.VMEM((levels - 1,) + block, low_type) for block in blocks]
        + [pltpu.VMEM(block, low_type) for block in blocks] * 2
        + [dma(c) for c in counts for _ in range(2)],
        compiler_params=pltpu.CompilerParams(
            collective_id=10, has_side_effects=True, vmem_limit_bytes=56 * 2**20
        ),
        cost_estimate=cost(0, 200e6),
        name="finish",
    )(part, middle, *grads)


BLOCK = 512
LOG2E = 1.4426950408889634


def dot(left_side, right_side, left_dim, right_dim):
    return lax.dot_general(
        left_side,
        right_side,
        (((left_dim,), (right_dim,)), ((), ())),
        preferred_element_type=jnp.float32,
    )


def run_blocks(step, part, parts, blocks, at, first, clear):
    def local(block):
        return jnp.clip(block - part * blocks, 0, blocks)

    own = (parts - 1) * blocks + at
    begin, middle, end = local(first), local(jnp.clip(clear, first, own)), local(own)
    lax.fori_loop(begin, middle, functools.partial(step, True), 0)
    lax.fori_loop(middle, end, functools.partial(step, False), 0)
    if part == parts - 1:
        step(True, at, 0)


def attend_kernel(parts, first, clear, q, *refs):
    keys, values = refs[:parts], refs[parts : 2 * parts]
    pos_q, start_q, pos_k, out, lse, top, total, acc = refs[2 * parts :]
    at = pl.program_id(0)
    blocks = pl.num_programs(0)
    rate = LOG2E * DH ** (-0.5)
    top[...] = jnp.full_like(top, -1e30)
    total[...] = jnp.zeros_like(total)
    acc[...] = jnp.zeros_like(acc)
    query = q[...]
    row_at, row_from = pos_q[0], start_q[0]

    for part in range(parts):

        def step(masked, block, carry, k=keys[part], v=values[part], part=part):
            rows = pl.ds(pl.multiple_of(block * BLOCK, BLOCK), BLOCK)
            spot = pl.ds(pl.multiple_of((part * blocks + block) * BLOCK, BLOCK), BLOCK)
            scores = dot(k[rows, :], query, 1, 1)
            if masked:
                key_at = pos_k[spot, :]
                scores = jnp.where((key_at >= row_from) & (key_at <= row_at), scores, -1e30)
            old = top[...]
            new = jnp.maximum(old, jnp.max(scores, axis=0, keepdims=True))
            shrink = jnp.exp2((old - new) * rate)
            weight = jnp.exp2((scores - new) * rate)
            total[...] = total[...] * shrink + jnp.sum(weight, axis=0, keepdims=True)
            acc[...] = acc[...] * shrink + dot(v[rows, :], weight.astype(jnp.bfloat16), 0, 0)
            top[...] = new
            return carry

        run_blocks(step, part, parts, blocks, at, first[at], clear[at])
    out[...] = (acc[...] / total[...]).T
    lse[0] = top[...] * rate + jnp.log2(total[...])


def attend(first, clear, queries, window, pos_q, start_q, pos_k):
    rows = queries.shape[0]
    parts = len(window)
    line = pl.BlockSpec((1, 1, BLOCK), lambda i, *_: (i, 0, 0))
    grid_spec = pltpu.PrefetchScalarGridSpec(
        num_scalar_prefetch=2,
        grid=(rows // BLOCK,),
        in_specs=[pl.BlockSpec((BLOCK, DH), lambda i, *_: (i, 0))]
        + [pl.BlockSpec((rows, DH), lambda i, *_: (0, 0))] * parts
        + [pl.BlockSpec((rows, DH), lambda i, *_: (0, 1))] * parts
        + [line, line, pl.BlockSpec((parts * rows, 1), lambda i, *_: (0, 0))],
        out_specs=[pl.BlockSpec((BLOCK, DH), lambda i, *_: (i, 0)), line],
        scratch_shapes=[
            pltpu.VMEM((1, BLOCK), jnp.float32),
            pltpu.VMEM((1, BLOCK), jnp.float32),
            pltpu.VMEM((DH, BLOCK), jnp.float32),
        ],
    )
    return pl.pallas_call(
        functools.partial(attend_kernel, parts),
        grid_spec=grid_spec,
        out_shape=[
            jax.ShapeDtypeStruct((rows, DH), jnp.float32),
            jax.ShapeDtypeStruct((rows // BLOCK, 1, BLOCK), jnp.float32),
        ],
        compiler_params=pltpu.CompilerParams(vmem_limit_bytes=48 * 2**20),
        cost_estimate=cost(2e10, 1e7),
        name="attend",
    )(first, clear, queries, *window, *window, pos_q, start_q, pos_k)


def attend_back_kernel(parts, first, clear, q, *refs):
    keys, values = refs[:parts], refs[parts : 2 * parts]
    grad, pos_q, start_q, lse, inner, pos_k, grad_q = refs[2 * parts : 2 * parts + 7]
    grads = refs[2 * parts + 7 : 3 * parts + 7]
    sum_k, sum_v, acc = refs[3 * parts + 7 :]
    at = pl.program_id(0)
    blocks = pl.num_programs(0)
    rate = LOG2E * DH ** (-0.5)
    scale = DH ** (-0.5)

    @pl.when(at == 0)
    def _():
        sum_k[...] = jnp.zeros_like(sum_k)
        sum_v[...] = jnp.zeros_like(sum_v)

    acc[...] = jnp.zeros_like(acc)
    query, grad_out = q[...], grad[...]
    row_at, row_from, row_lse, row_inner = pos_q[0], start_q[0], lse[0], inner[0]

    for part in range(parts):

        def step(masked, block, carry, k=keys[part], v=values[part], part=part):
            rows = pl.ds(pl.multiple_of(block * BLOCK, BLOCK), BLOCK)
            spot = pl.ds(pl.multiple_of((part * blocks + block) * BLOCK, BLOCK), BLOCK)
            key, value = k[rows, :], v[rows, :]
            scores = dot(key, query, 1, 1)
            soft = jnp.exp2(scores * rate - row_lse)
            if masked:
                key_at = pos_k[spot, :]
                soft = jnp.where((key_at >= row_from) & (key_at <= row_at), soft, 0.0)
            grad_soft = dot(value, grad_out, 1, 1)
            grad_scores = (soft * (grad_soft - row_inner)).astype(jnp.bfloat16)
            sum_v[spot, :] += dot(soft.astype(jnp.bfloat16), grad_out, 1, 0)
            sum_k[spot, :] += dot(grad_scores, query, 1, 0)
            acc[...] += dot(grad_scores, key, 0, 0)
            return carry

        run_blocks(step, part, parts, blocks, at, first[at], clear[at])
    grad_q[...] = (acc[...] * scale).astype(jnp.bfloat16)

    @pl.when(at == blocks - 1)
    def _():
        size = grads[0].shape[0]
        for part in range(parts):
            spot = slice(part * size, (part + 1) * size)
            grads[part][:, :DH] = (sum_k[spot, :] * scale).astype(grads[part].dtype)
            grads[part][:, DH:] = sum_v[spot, :].astype(grads[part].dtype)


def attend_back(first, clear, queries, window, grads, pos_q, start_q, lse, inner, pos_k):
    rows = queries.shape[0]
    parts = len(window)
    block = pl.BlockSpec((BLOCK, DH), lambda i, *_: (i, 0))
    line = pl.BlockSpec((1, 1, BLOCK), lambda i, *_: (i, 0, 0))
    grid_spec = pltpu.PrefetchScalarGridSpec(
        num_scalar_prefetch=2,
        grid=(rows // BLOCK,),
        in_specs=[block]
        + [pl.BlockSpec((rows, DH), lambda i, *_: (0, 0))] * parts
        + [pl.BlockSpec((rows, DH), lambda i, *_: (0, 1))] * parts
        + [block, line, line, line, line]
        + [pl.BlockSpec((parts * rows, 1), lambda i, *_: (0, 0))],
        out_specs=[block] + [pl.BlockSpec((rows, 2 * DH), lambda i, *_: (0, 0))] * parts,
        scratch_shapes=[
            pltpu.VMEM((parts * rows, DH), jnp.float32),
            pltpu.VMEM((parts * rows, DH), jnp.float32),
            pltpu.VMEM((BLOCK, DH), jnp.float32),
        ],
    )
    kinds = [jnp.bfloat16] * (parts - 1) + [jnp.float32]
    return pl.pallas_call(
        functools.partial(attend_back_kernel, parts),
        grid_spec=grid_spec,
        out_shape=[jax.ShapeDtypeStruct((rows, DH), jnp.bfloat16)]
        + [jax.ShapeDtypeStruct((rows, 2 * DH), kind) for kind in kinds],
        compiler_params=pltpu.CompilerParams(vmem_limit_bytes=48 * 2**20),
        cost_estimate=cost(2e9, 1e6),
        name="attend_back",
    )(first, clear, queries, *window, *window, grads, pos_q, start_q, lse, inner, pos_k)


def columns_of(ref, group, groups, step, depth):
    at = lax.rem(group + step + groups, groups) * depth
    return ref.at[:, pl.ds(pl.multiple_of(at, 128), depth)]


def front_kernel(groups, local, place, hidden, grads, *refs):
    w_in, w_out = refs[0], refs[1 : groups + 1]
    gates, active, grad_pre, rows_out, turned, acc = refs[groups + 1 :]
    levels, _, depth, width = w_in.shape
    tile = hidden.shape[0]
    model = groups * depth
    parts = [slice(step * depth, (step + 1) * depth) for step in range(groups)]
    for step in range(groups):
        turned[0, :, parts[step]] = columns_of(hidden, place[1], groups, -step, depth)[...]
        turned[1, :, parts[step]] = columns_of(grads, place[1], groups, -step, depth)[...]
    gate_grads = []
    for level in range(levels):
        pre_act = jnp.zeros((tile, width), jnp.float32)
        grad_active = jnp.zeros((tile, width), jnp.float32)
        for step in range(groups):
            pre_act += dot(turned[0, :, parts[step]], w_in[level, step], 1, 0)
            grad_active += dot(turned[1, :, parts[step]], w_out[step][level], 1, 0)
        first = level * local
        gate = jnp.concatenate(
            [jnp.broadcast_to(gates[:, first + e : first + e + 1], (tile, FH)) for e in range(local)],
            axis=1,
        )
        sig = 1.0 / (1.0 + jnp.exp2(-LOG2E * pre_act))
        act_pre = pre_act * sig
        columns = slice(level * width, (level + 1) * width)
        active[:, columns] = (act_pre * gate).astype(jnp.bfloat16)
        product = grad_active * act_pre
        for e in range(local):
            gate_grads.append(
                jnp.sum(product[:, e * FH : (e + 1) * FH], axis=1, keepdims=True)
            )
        slope = sig * (1.0 + pre_act * (1.0 - sig))
        low_pre = (grad_active * gate * slope).astype(jnp.bfloat16)
        grad_pre[:, columns] = low_pre
        for step in range(groups):
            back = dot(low_pre, w_in[level, step], 1, 1)
            acc[:, parts[step]] = back if level == 0 else acc[:, parts[step]] + back
    for step in range(groups):
        columns_of(rows_out, place[1], groups, -step, depth)[...] = acc[:, parts[step]].astype(
            jnp.bfloat16
        )
    spare = rows_out.shape[1] - model
    lane = lax.broadcasted_iota(jnp.int32, (tile, spare), 1) - place[0] * (levels * local)
    spread = jnp.zeros((tile, spare), jnp.float32)
    for e, column in enumerate(gate_grads):
        spread = jnp.where(lane == e, column, spread)
    rows_out[:, model:] = spread.astype(jnp.bfloat16)


def ffn_front(place, hidden, grads, w_in, w_out, gates, local):
    rows, wide = hidden.shape
    levels, groups, depth, width = w_in.shape
    tile = 512

    def by_row(columns):
        return pl.BlockSpec((tile, columns), lambda i, *_: (i, 0))

    once = pl.Buffered(1)
    whole = pl.BlockSpec(w_out[0].shape, lambda i, *_: (0, 0, 0), pipeline_mode=once)
    stacked = pl.BlockSpec(w_in.shape, lambda i, *_: (0, 0, 0, 0), pipeline_mode=once)
    grid_spec = pltpu.PrefetchScalarGridSpec(
        num_scalar_prefetch=1,
        grid=(rows // tile,),
        in_specs=[by_row(wide), by_row(groups * depth)]
        + [stacked]
        + [whole] * groups
        + [by_row(gates.shape[1])],
        out_specs=[by_row(levels * width), by_row(levels * width), by_row(wide)],
        scratch_shapes=[
            pltpu.VMEM((2, tile, groups * depth), jnp.bfloat16),
            pltpu.VMEM((tile, groups * depth), jnp.float32),
        ],
    )
    hidden_units = jax.ShapeDtypeStruct((rows, levels * width), jnp.bfloat16)
    return pl.pallas_call(
        functools.partial(front_kernel, groups, local),
        grid_spec=grid_spec,
        out_shape=[hidden_units, hidden_units, jax.ShapeDtypeStruct((rows, wide), jnp.bfloat16)],
        compiler_params=pltpu.CompilerParams(vmem_limit_bytes=58 * 2**20),
        cost_estimate=cost(6 * rows * groups * depth * levels * width, 3e7),
        name="ffn_front",
    )(place, hidden, grads, w_in, *w_out, gates)


def rear_kernel(groups, place, rows_in, hidden_units, *weight_grads):
    _, depth, _ = weight_grads[0].shape
    units = hidden_units[...]
    for step in range(groups):
        part = columns_of(rows_in, place[1], groups, step, depth)
        weight_grads[step][0] = dot(part[...], units, 0, 0).astype(jnp.bfloat16)


def feed_kernel(groups, place, active, *refs):
    weights = refs[:groups]
    feed, acc = refs[groups:]
    _, depth, _ = weights[0].shape
    level = pl.program_id(0)
    act = active[...]
    for step in range(groups):
        fed = dot(act, weights[step][0], 1, 1)
        part = slice(step * depth, (step + 1) * depth)

        @pl.when(level == 0)
        def _():
            acc[:, part] = fed

        @pl.when(level > 0)
        def _():
            acc[:, part] += fed

    @pl.when(level == pl.num_programs(0) - 1)
    def _():
        for step in range(groups):
            part = slice(step * depth, (step + 1) * depth)
            columns_of(feed, place[1], groups, -step, depth)[...] = acc[:, part].astype(
                jnp.bfloat16
            )


def whole_rows(rows, columns):
    return pl.BlockSpec((rows, columns), lambda i, *_: (0, 0), pipeline_mode=pl.Buffered(1))


def ffn_feed(place, active, weights):
    rows = active.shape[0]
    groups = len(weights)
    levels, depth, width = weights[0].shape
    return pl.pallas_call(
        functools.partial(feed_kernel, groups),
        grid_spec=pltpu.PrefetchScalarGridSpec(
            num_scalar_prefetch=1,
            grid=(levels,),
            in_specs=[pl.BlockSpec((rows, width), lambda i, *_: (0, i))]
            + [pl.BlockSpec((1, depth, width), lambda i, *_: (i, 0, 0))] * groups,
            out_specs=whole_rows(rows, groups * depth),
            scratch_shapes=[pltpu.VMEM((rows, groups * depth), jnp.float32)],
        ),
        out_shape=jax.ShapeDtypeStruct((rows, groups * depth), jnp.bfloat16),
        compiler_params=pltpu.CompilerParams(vmem_limit_bytes=58 * 2**20),
        cost_estimate=cost(1e3, 1e3),
        name="ffn_feed",
    )(place, active, *weights)


def ffn_rear(place, rows_in, units, model, groups, levels):
    rows, wide = rows_in.shape
    width = units.shape[1] // levels
    depth = model // groups
    return pl.pallas_call(
        functools.partial(rear_kernel, groups),
        grid_spec=pltpu.PrefetchScalarGridSpec(
            num_scalar_prefetch=1,
            grid=(levels,),
            in_specs=[
                whole_rows(rows, wide),
                pl.BlockSpec((rows, width), lambda i, *_: (0, i)),
            ],
            out_specs=[pl.BlockSpec((1, depth, width), lambda i, *_: (i, 0, 0))] * groups,
        ),
        out_shape=[jax.ShapeDtypeStruct((levels, depth, width), jnp.bfloat16)] * groups,
        compiler_params=pltpu.CompilerParams(vmem_limit_bytes=58 * 2**20),
        cost_estimate=cost(1e3, 1e3),
        name="ffn_rear",
    )(place, rows_in, units)


def named_by(routes, count):
    lane = lax.broadcasted_iota(jnp.int32, (routes.shape[0], count), 1)
    member = jnp.zeros(lane.shape, jnp.float32)
    for slot in range(routes.shape[1]):
        member = jnp.where(lane == routes[:, slot : slot + 1], 1.0, member)
    return member


def middle_kernel(rows, branch, routes, router, gain, bias, middle, extended, sig_out):
    experts = router.shape[1]
    width = rows.shape[1]
    rounded = branch[...].astype(jnp.bfloat16).astype(jnp.float32)
    value = rows[...].astype(jnp.float32) + rounded
    middle[...] = value
    _, _, normed = normalized(value, gain[...], bias[...])
    sig = 1.0 / (1.0 + jnp.exp2(-LOG2E * dot(normed, router[...], 1, 0)))
    sig_out[...] = sig
    extended[:, :width] = value.astype(jnp.bfloat16)
    gates = (sig * named_by(routes[...], experts)).astype(jnp.bfloat16)
    spare = extended.shape[1] - width - experts
    if spare:
        gates = jnp.concatenate([gates, jnp.zeros((gates.shape[0], spare), gates.dtype)], axis=1)
    extended[:, width:] = gates


def enter_ffn(rows, branch, routes, router, gain, bias):
    count, width = rows.shape
    experts = router.shape[1]
    wide = width + experts + -experts % 128
    return pl.pallas_call(
        middle_kernel,
        out_shape=[
            jax.ShapeDtypeStruct((count, width), jnp.float32),
            jax.ShapeDtypeStruct((count, wide), jnp.bfloat16),
            jax.ShapeDtypeStruct((count, experts), jnp.float32),
        ],
        compiler_params=pltpu.CompilerParams(vmem_limit_bytes=40 * 2**20),
        cost_estimate=cost(1e9, 1e7),
        name="middle",
    )(rows, branch, routes, router, gain, bias)


def leave_kernel(
    middle, own, came, cotangent, sigs, routes, router, gain, bias, grad_out, low_out, weight_grads
):
    experts = router.shape[1]
    count, width = middle.shape
    scaled, inverse, normed = normalized(middle[...], gain[...], bias[...])
    total = own[...] + came[...].astype(jnp.float32)
    sig = sigs[...]
    member = named_by(routes[...], experts)
    gate_grads = total[:, width : width + experts]
    logit = (gate_grads * sig * (1.0 - sig) * member).astype(jnp.bfloat16)
    second = dot(logit, router[...], 1, 1)
    inner_grad = second * gain[...]
    inner_grad = inverse * (
        inner_grad
        - jnp.mean(inner_grad, axis=1, keepdims=True)
        - scaled * jnp.mean(inner_grad * scaled, axis=1, keepdims=True)
    )
    grad = cotangent[...].astype(jnp.float32) + total[:, :width] + inner_grad
    grad_out[...] = grad
    low_out[...] = grad.astype(jnp.bfloat16)
    spare = weight_grads.shape[1] - experts
    sums = [
        jnp.sum(second * scaled, axis=0, keepdims=True),
        jnp.sum(second, axis=0, keepdims=True),
        jnp.zeros((126, width), jnp.float32),
    ]
    side = jnp.concatenate(sums, axis=0).T[:, :spare]
    both = jnp.concatenate([dot(normed, logit, 0, 0), side], axis=1)
    weight_grads[...] = both.astype(jnp.bfloat16)


def leave_ffn(middle, own, came, cotangent, sigs, routes, router, gain, bias):
    count, width = middle.shape
    experts = router.shape[1]
    columns = experts + 2 + -(experts + 2) % 128
    return pl.pallas_call(
        leave_kernel,
        out_shape=[
            jax.ShapeDtypeStruct((count, width), jnp.float32),
            jax.ShapeDtypeStruct((count, width), jnp.bfloat16),
            jax.ShapeDtypeStruct((width, columns), jnp.bfloat16),
        ],
        compiler_params=pltpu.CompilerParams(vmem_limit_bytes=48 * 2**20),
        cost_estimate=cost(1e9, 1e7),
        name="leave_ffn",
    )(middle, own, came, cotangent, sigs, routes, router, gain, bias)


def branch_back_kernel(
    grads, w_output, attended, sigs, masks, grad_attended, inner, out_logit, weight_grads, acc
):
    at = pl.program_id(0)
    count = grads.shape[0]
    sig, mask, values = sigs[...], masks[...], attended[...]
    mixed_grad = dot(grads[...], w_output[...], 1, 0)
    lane = lax.broadcasted_iota(jnp.int32, (count, 128), 1)
    logits = jnp.zeros((count, 128), jnp.float32)
    total = jnp.zeros((count, DH), jnp.float32)
    parts = []
    for e in range(VEXP):
        k = VEXP + e
        one, on = sig[:, k : k + 1], mask[:, k : k + 1]
        part = mixed_grad[:, e * DH : (e + 1) * DH]
        total += part * (one * on)
        gate_grad = jnp.sum(part * values, axis=1, keepdims=True)
        logits = jnp.where(lane == k, gate_grad * one * (1.0 - one) * on, logits)
        parts.append((one * on * values).astype(jnp.bfloat16))
    out_logit[...] = logits.astype(jnp.bfloat16)
    rounded = total.astype(jnp.bfloat16)
    grad_attended[...] = rounded
    product = rounded.astype(jnp.float32) * values
    inner[0] = jnp.sum(product.T, axis=0, keepdims=True)
    amount = dot(grads[...], jnp.concatenate(parts, axis=1), 0, 0)

    @pl.when(at == 0)
    def _():
        acc[...] = amount

    @pl.when(at > 0)
    def _():
        acc[...] += amount

    @pl.when(at == pl.num_programs(0) - 1)
    def _():
        weight_grads[...] = acc[...].astype(jnp.bfloat16)


def branch_back(grads, full, attended, sigs, masks):
    rows, width = grads.shape
    values = VEXP * DH

    def by_row(size):
        return pl.BlockSpec((BLOCK, size), lambda i: (i, 0))

    return pl.pallas_call(
        branch_back_kernel,
        grid=(rows // BLOCK,),
        in_specs=[
            by_row(width),
            pl.BlockSpec((width, values), lambda i: (0, 1), pipeline_mode=pl.Buffered(1)),
            by_row(DH),
            by_row(128),
            by_row(16),
        ],
        out_specs=[
            by_row(DH),
            pl.BlockSpec((1, 1, BLOCK), lambda i: (i, 0, 0)),
            by_row(128),
            pl.BlockSpec((width, values), lambda i: (0, 0)),
        ],
        out_shape=[
            jax.ShapeDtypeStruct((rows, DH), jnp.bfloat16),
            jax.ShapeDtypeStruct((rows // BLOCK, 1, BLOCK), jnp.float32),
            jax.ShapeDtypeStruct((rows, 128), jnp.bfloat16),
            jax.ShapeDtypeStruct((width, values), jnp.bfloat16),
        ],
        scratch_shapes=[pltpu.VMEM((width, values), jnp.float32)],
        compiler_params=pltpu.CompilerParams(vmem_limit_bytes=48 * 2**20),
        cost_estimate=cost(1e8, 1e6),
        name="branch_back",
    )(grads, full, attended, sigs, masks)


def turn(value, axis, by):
    size = lax.axis_size(axis)
    return lax.ppermute(value, axis, [(i, (i + by) % size) for i in range(size)])


def normalized(rows, gain, bias):
    values = rows.astype(jnp.float32)
    centred = values - jnp.mean(values, axis=1, keepdims=True)
    inverse = lax.rsqrt(jnp.mean(centred * centred, axis=1, keepdims=True) + 1e-05)
    scaled = centred * inverse
    return scaled, inverse, (scaled * gain + bias).astype(jnp.bfloat16)


def project_kernel(
    levels, rows, w_value, w_query, w_key, routers, gain, bias, order, tables,
    query, key_value, projected, sigs, masks,
):
    count = rows.shape[0]
    piece = count // (levels * HEADS)
    _, _, normed = normalized(rows[...], gain[...], bias[...])
    query[...] = dot(normed, w_query[...], 1, 0).astype(jnp.bfloat16)
    key_value[:, :DH] = dot(normed, w_key[...], 1, 0).astype(jnp.bfloat16)
    sig = 1.0 / (1.0 + jnp.exp2(-LOG2E * dot(normed, routers[...], 1, 0)))
    sigs[...] = sig
    product = dot(rows[...], w_value[...], 1, 0)
    projected[...] = product
    at = lax.broadcasted_iota(jnp.int32, (count, count), 0)
    source = lax.rem(at // piece, levels) * HEADS + at // (piece * levels)
    here = (source * piece + lax.rem(at, piece) == order[0]).astype(jnp.bfloat16)
    lane = lax.broadcasted_iota(jnp.int32, (16, count), 0)
    table = tables[0]
    named = jnp.zeros((16, count), jnp.float32)
    for which in range(2):
        option = lane - which * VEXP
        for slot in range(2):
            pick = table[2 * which + slot : 2 * which + slot + 1, :]
            hit = (option == pick) & (option >= 0) & (option < VEXP)
            named = jnp.where(hit, 1.0, named)
    mask = dot(here, named.astype(jnp.bfloat16), 1, 1)
    masks[...] = mask
    value = jnp.zeros((count, DH), jnp.float32)
    for e in range(VEXP):
        gate = sig[:, e : e + 1] * mask[:, e : e + 1]
        value += gate * product[:, e * DH : (e + 1) * DH]
    key_value[:, DH:] = value.astype(jnp.bfloat16)


def project(rows, full, gain, bias, orders, tables, levels):
    total, width = rows.shape
    count = total // HEADS

    def by_row(columns):
        return pl.BlockSpec((count, columns), lambda i: (i, 0))

    def column(size, at):
        return pl.BlockSpec((width, size), lambda i: (0, at), pipeline_mode=pl.Buffered(1))

    line = pl.BlockSpec((1, width), lambda i: (0, 0))
    shapes = [(DH, jnp.bfloat16), (2 * DH, jnp.bfloat16), (VEXP * DH, jnp.float32)]
    shapes += [(128, jnp.float32), (16, jnp.float32)]
    return pl.pallas_call(
        functools.partial(project_kernel, levels),
        grid=(HEADS,),
        in_specs=[by_row(width), column(VEXP * DH, 0)]
        + [column(DH, 2 * VEXP + i) for i in range(3)]
        + [line, line]
        + [
            pl.BlockSpec((1, 1, count), lambda i: (i, 0, 0)),
            pl.BlockSpec((1,) + tables.shape[1:], lambda i: (i, 0, 0)),
        ],
        out_specs=[by_row(columns) for columns, _ in shapes],
        out_shape=[jax.ShapeDtypeStruct((total, columns), kind) for columns, kind in shapes],
        compiler_params=pltpu.CompilerParams(vmem_limit_bytes=48 * 2**20),
        cost_estimate=cost(2 * total * width * 1024, 2e7),
        name="project",
    )(rows, full, full, full, full, gain, bias, orders, tables)


def project_back_kernel(
    rows, grads, grad_query, out_logit, projected, sigs, masks,
    w_value, w_query, w_key, routers, gain, bias,
    grad_rows, weight_grads, acc, sums,
):
    at = pl.program_id(0)
    count = rows.shape[0]
    values = VEXP * DH

    @pl.when(at == 0)
    def _():
        acc[...] = jnp.zeros_like(acc)
        sums[...] = jnp.zeros_like(sums)

    scaled, inverse, normed = normalized(rows[...], gain[...], bias[...])
    grad_key = grads[:, :DH].astype(jnp.bfloat16)
    grad_value = grads[:, DH:]
    sig, mask = sigs[...], masks[...]
    lane = lax.broadcasted_iota(jnp.int32, (count, 128), 1)
    logits = out_logit[...].astype(jnp.float32)
    parts = []
    for e in range(VEXP):
        one, on = sig[:, e : e + 1], mask[:, e : e + 1]
        parts.append((one * on * grad_value).astype(jnp.bfloat16))
        inner = jnp.sum(grad_value * projected[:, e * DH : (e + 1) * DH], axis=1, keepdims=True)
        logits = jnp.where(lane == e, inner * one * (1.0 - one) * on, logits)
    grad_projected = jnp.concatenate(parts, axis=1)
    sides = jnp.concatenate([grad_query[...], grad_key, logits.astype(jnp.bfloat16)], axis=1)
    first = dot(sides[:, :DH], w_query[...], 1, 1)
    first += dot(sides[:, DH : 2 * DH], w_key[...], 1, 1)
    first += dot(sides[:, 2 * DH :], routers[...], 1, 1)
    sums[2 * VEXP : 2 * VEXP + 1, :] += jnp.sum(first * scaled, axis=0, keepdims=True)
    sums[2 * VEXP + 1 : 2 * VEXP + 2, :] += jnp.sum(first, axis=0, keepdims=True)
    inner_grad = first * gain[...]
    inner_grad = inverse * (
        inner_grad
        - jnp.mean(inner_grad, axis=1, keepdims=True)
        - scaled * jnp.mean(inner_grad * scaled, axis=1, keepdims=True)
    )
    grad_rows[...] = (inner_grad + dot(grad_projected, w_value[...], 1, 1)).astype(jnp.bfloat16)
    acc[:, :values] += dot(rows[...], grad_projected, 0, 0)
    acc[:, values:] += dot(normed, sides, 0, 0)

    @pl.when(at == pl.num_programs(0) - 1)
    def _():
        weight_grads[:, : values + 2 * DH] = acc[:, : values + 2 * DH].astype(jnp.bfloat16)
        last = acc[:, values + 2 * DH :] + sums[...].T
        weight_grads[:, values + 2 * DH :] = last.astype(jnp.bfloat16)


def project_back(rows, grads, grad_query, out_logit, projected, sigs, masks, full, gain, bias):
    total, width = rows.shape
    count = total // HEADS
    columns = VEXP * DH + 3 * DH

    def by_row(size):
        return pl.BlockSpec((count, size), lambda i: (i, 0))

    def column(size, at):
        return pl.BlockSpec((width, size), lambda i: (0, at), pipeline_mode=pl.Buffered(1))

    line = pl.BlockSpec((1, width), lambda i: (0, 0))
    return pl.pallas_call(
        project_back_kernel,
        grid=(HEADS,),
        in_specs=[by_row(width), by_row(2 * DH), by_row(DH), by_row(128), by_row(VEXP * DH)]
        + [by_row(128), by_row(16), column(VEXP * DH, 0)]
        + [column(DH, 2 * VEXP + i) for i in range(3)]
        + [line, line],
        out_specs=[by_row(width), pl.BlockSpec((width, columns), lambda i: (0, 0))],
        out_shape=[
            jax.ShapeDtypeStruct((total, width), jnp.bfloat16),
            jax.ShapeDtypeStruct((width, columns), jnp.bfloat16),
        ],
        scratch_shapes=[
            pltpu.VMEM((width, columns), jnp.float32),
            pltpu.VMEM((128, width), jnp.float32),
        ],
        compiler_params=pltpu.CompilerParams(vmem_limit_bytes=56 * 2**20),
        cost_estimate=cost(total * width * 512, 4e6),
        name="project_back",
    )(rows, grads, grad_query, out_logit, projected, sigs, masks, full, full, full, full, gain, bias)


def shift(value, axis, by):
    count = lax.axis_size(axis)
    pairs = [(i, i + by) for i in range(count) if 0 <= i + by < count]
    return lax.ppermute(value, axis, pairs)


def body(
    tokens_in,
    out_grad,
    deal_order,
    seq_lengths,
    value_routes,
    output_routes,
    ffn_routes,
    norm1_gain,
    norm1_bias,
    norm2_gain,
    norm2_bias,
    query_weight,
    key_weight,
    value_weight,
    output_weight,
    value_router,
    output_router,
    ffn_router,
    ffn_in,
    ffn_out,
):
    groups = lax.axis_size("group")
    levels = lax.axis_size("level")
    level = lax.axis_index("level")
    head = lax.axis_index("head")
    count, width = tokens_in.shape
    piece = count // (levels * HEADS)
    wrows = query_weight.shape[0]
    experts = ffn_router.shape[1]
    local_experts = ffn_in.shape[1] // FH

    small = jnp.concatenate(
        [
            ffn_router,
            norm1_gain[:, None],
            norm1_bias[:, None],
            norm2_gain[:, None],
            norm2_bias[:, None],
        ],
        axis=1,
    )
    shared = small.shape[1]
    pad = -(shared + 2 * VEXP) % 128
    extra = jnp.concatenate(
        [
            value_router.reshape(wrows, HEADS, VEXP),
            output_router.reshape(wrows, HEADS, VEXP),
            jnp.broadcast_to(small[:, None, :], (wrows, HEADS, shared)),
            jnp.zeros((wrows, HEADS, pad), jnp.bfloat16),
        ],
        axis=2,
    )
    cols = 2 * DH + 2 * VEXP * DH + extra.shape[2]
    tables = jnp.concatenate(
        [value_routes.transpose(1, 2, 0), output_routes.transpose(1, 2, 0)], axis=1
    )
    picks = ffn_routes.reshape(levels, HEADS * piece, -1).transpose(0, 2, 1)
    arrived, own_grads, full, tables, picks, orders = start(
        tokens_in.reshape(levels, HEADS, piece, width),
        out_grad.reshape(levels, HEADS, piece, width),
        [value_weight, output_weight, query_weight, key_weight],
        extra.transpose(1, 0, 2),
        tables,
        picks,
        deal_order,
    )
    worker_in = arrived.reshape(HEADS * count, width)
    own_tokens = lax.dynamic_index_in_dim(arrived, head, 1, keepdims=False).reshape(count, width)
    in_rows = [turn(ffn_in, "group", k) for k in range(1, groups)]
    full, in_rows = lax.optimization_barrier((full.reshape(width, cols), in_rows))

    base = 2 * DH + 2 * VEXP * DH
    w_output = full[:, VEXP * DH : 2 * VEXP * DH]
    at = base + 2 * VEXP
    def relabelled(expert):
        share = expert // local_experts
        return (share % HEADS * levels + share // HEADS) * local_experts + expert % local_experts

    labels = jnp.arange(experts, dtype=jnp.int32)
    moved = low(relabelled(labels)[:, None] == labels[None, :])
    r_ffn = low(
        jnp.dot(full[:, at : at + experts], moved, preferred_element_type=jnp.float32)
    )
    gain_one, bias_one, gain_two, bias_two = (
        full[:, at + experts + i].astype(jnp.float32) for i in range(4)
    )
    gain_row, bias_row = gain_one[None], bias_one[None]
    orders = orders.reshape(levels, HEADS, count)
    own_order = lax.dynamic_index_in_dim(orders, level, 0, keepdims=False)[:, None, :]
    queries, key_value, projected, sigs, masks = project(
        worker_in, full, gain_row, bias_row, own_order, tables, levels
    )

    rows = HEADS * count
    reach = -(-LMAX // rows)

    ramp = jnp.arange(count, dtype=jnp.int32)

    def arrival(values):
        lead, shape = values.shape[:-3], values.shape[-1:]
        four = values.reshape(lead + (HEADS, levels, HEADS, piece) + shape)
        return jnp.swapaxes(four, -4, -3).reshape(lead + (rows,) + shape)

    orders = jnp.concatenate([jnp.zeros((reach, HEADS, count), jnp.int32), orders], axis=0)
    orders = lax.dynamic_slice_in_dim(orders, level, reach + 1, 0)
    here = orders[:, :, None, :] == ramp[None, None, :, None]
    inverse = jnp.sum(here * ramp, axis=3)
    shard = (level - reach + jnp.arange(reach + 1, dtype=jnp.int32))[:, None] * HEADS
    shard = shard + jnp.arange(HEADS, dtype=jnp.int32)[None, :]
    pos_all = jnp.where(shard[:, :, None] < 0, -1, shard[:, :, None] * count + inverse)
    pos_all = arrival(pos_all[..., None]).reshape(-1)
    positions = pos_all[reach * rows :]
    seq_ends = jnp.cumsum(seq_lengths[0])

    def starts_of(places):
        return jnp.max(jnp.where(seq_ends <= places[:, None], seq_ends, 0), axis=1)

    starts = starts_of(positions)
    blocks = rows // BLOCK
    base_block = (level - reach) * blocks
    first_block = starts_of(level * rows + jnp.arange(blocks, dtype=jnp.int32) * BLOCK) // BLOCK
    first_block = jnp.maximum(first_block - base_block, 0)
    ends = level * rows + jnp.arange(1, blocks + 1, dtype=jnp.int32) * BLOCK - 1
    clear_block = (starts_of(ends) + BLOCK - 1) // BLOCK - base_block

    own_routes = picks.reshape(levels, -1, HEADS, piece).transpose(2, 0, 3, 1).reshape(count, -1)
    own_routes = relabelled(own_routes)
    ffn_side = (own_routes, r_ffn, gain_two[None], bias_two[None], own_tokens)

    window = [key_value]
    own_grads = own_grads.reshape(count, width)
    for i in range(reach):
        came = shift(window[0], "level", 1)
        if i == 0:
            came, own_grads, pos_all, starts, ffn_out = lax.optimization_barrier(
                (came, own_grads, pos_all, starts, ffn_out)
            )
            cotangent = level_gather(own_grads, 5, True)
        if i == reach - 1:
            came, cotangent, ffn_side, in_rows = lax.optimization_barrier(
                (came, cotangent, ffn_side, [ffn_in] + in_rows)
            )
        window.insert(0, came)
    place = jnp.stack([head, lax.axis_index("group")])
    out_here = lax.all_gather(ffn_out, "level", axis=0)
    w_in = lax.all_gather(jnp.stack(in_rows), "level", axis=0)


    def lines(values):
        return values.reshape(blocks, 1, BLOCK)

    attended, log_total = attend(
        first_block,
        clear_block,
        queries,
        window,
        lines(positions),
        lines(starts),
        pos_all[:, None],
    )

    out_sig = sigs[:, VEXP : 2 * VEXP]
    out_mask = masks[:, VEXP : 2 * VEXP]
    out_gate = out_sig * out_mask
    attended, out_here = lax.optimization_barrier((attended, out_here))
    w_out = [out_here] + [turn(out_here, "group", k) for k in range(1, groups)]
    mixed = low((out_gate[..., None] * attended[:, None, :]).reshape(rows, VEXP * DH))
    branch = level_scatter(low(transposed(mixed, w_output)), 2)

    own_routes, r_ffn, gain_two, bias_two, own_tokens = ffn_side
    middle, extended, ffn_sig = enter_ffn(own_tokens, branch, own_routes, r_ffn, gain_two, bias_two)
    hidden = level_gather(extended, 3, True)
    mine = levels * local_experts
    gates = lax.dynamic_slice_in_dim(hidden, width + head * mine, mine, 1).astype(jnp.float32)
    active, grad_pre, grad_rows = ffn_front(
        place, hidden, cotangent, w_in, w_out, gates, local_experts
    )
    summed, beyond = pair_scatter(grad_rows, 4, True)
    beyond, hidden = lax.optimization_barrier((beyond, hidden))
    came = to_far(beyond)
    grad_in = ffn_rear(place, hidden, grad_pre, width, groups, levels)
    in_came = [turn(grad_in[k], "group", k) for k in range(1, groups)]
    grad_out = ffn_rear(place, cotangent, active, width, groups, levels)
    out_came = [turn(grad_out[k], "group", k) for k in range(1, groups)]
    came, grad_in, grad_out = lax.optimization_barrier((came, grad_in, grad_out))
    grad_middle, own_branch, early = leave_ffn(
        middle, summed, came, own_grads, ffn_sig, own_routes, r_ffn, gain_two, bias_two
    )
    came = to_far(own_branch)
    feed = ffn_feed(place, active, w_out)
    came, feed = lax.optimization_barrier((came, feed))
    grad_branch = pair_gather(own_branch, came, 7)

    def sum_of(own, others):
        total = own[0].astype(jnp.float32)
        for other in others:
            total = total + other.astype(jnp.float32)
        return low(total)

    def over_levels(total):
        return lax.psum_scatter(total, "level", scatter_dimension=0)

    grad_branch, in_came = lax.optimization_barrier((grad_branch, in_came))
    ffn_in_grad = over_levels(sum_of(grad_in, in_came))
    grad_attended, row_inner, grad_out_logit, grad_w_output = branch_back(
        grad_branch, full, attended, sigs, masks
    )
    grad_queries, *grad_window = attend_back(
        first_block,
        clear_block,
        queries,
        window,
        grad_attended,
        lines(positions),
        lines(starts),
        log_total,
        row_inner,
        pos_all[:, None],
    )
    came = shift(grad_window[0], "level", -1)
    fed, beyond = pair_scatter(feed, 6, True)
    for i in range(1, reach + 1):
        if i < reach:
            came, fed = lax.optimization_barrier((came, fed))
        grad_both = grad_window[i].astype(jnp.float32) + came.astype(jnp.float32)
        if i < reach:
            grad_keys_sent = low(grad_both)
            came = shift(grad_keys_sent, "level", -1)
    grad_both, out_came = lax.optimization_barrier((grad_both, out_came))
    ffn_out_grad = over_levels(sum_of(grad_out, out_came))
    fed_far = to_far(beyond)
    grad_inputs, late = project_back(
        worker_in,
        grad_both,
        grad_queries,
        grad_out_logit,
        projected,
        sigs,
        masks,
        full,
        gain_row,
        bias_row,
    )

    fed_far, grad_inputs = lax.optimization_barrier((fed_far, grad_inputs))
    layer_out = to_home(low(middle + fed + fed_far.astype(jnp.float32)))

    values = VEXP * DH
    layout = (
        ((0, values, True), (values, DH, True), (values + DH, DH, True), (values + 2 * DH, DH, False)),
        ((0, values, True),),
        ((0, early.shape[1], False),),
    )

    def by_owner(grads):
        return grads.reshape(groups, levels, HEADS, wrows, -1)

    input_grad, grad_value, grad_query, grad_key, sides, grad_output, common = finish(
        layout,
        grad_inputs.reshape(HEADS, HEADS, levels * piece, width),
        grad_middle.reshape(HEADS, levels * piece, width),
        by_owner(late),
        by_owner(grad_w_output),
        by_owner(early),
    )
    norms = jnp.sum(sides[:, :, 2 * VEXP : 2 * VEXP + 2], axis=0)
    common = jnp.sum(common[:, :, : experts + 2], axis=0)
    router_grad = common[:, :experts].reshape(wrows, HEADS, levels, local_experts)

    def side(first):
        return sides[:, :, first : first + VEXP].transpose(1, 0, 2).reshape(wrows, HEADS * VEXP)

    return (
        layer_out,
        input_grad.reshape(count, width),
        norms[:, 0],
        norms[:, 1],
        common[:, experts],
        common[:, experts + 1],
        grad_query,
        grad_key,
        grad_value,
        grad_output,
        side(0),
        side(VEXP),
        jnp.swapaxes(router_grad, 1, 2).reshape(wrows, experts),
        ffn_in_grad.astype(jnp.float32),
        ffn_out_grad.astype(jnp.float32),
    )


def solution(mesh):
    groups, shards = mesh.devices.shape
    fine = Mesh(mesh.devices.reshape(groups, shards // HEADS, HEADS), TOK)
    two, one, three = P(TOK, None), P(TOK), P(TOK, None, None)
    ffn = P("group", ("level", "head"))
    return jax.shard_map(
        body,
        mesh=fine,
        in_specs=(two, two, two, P("group", None), three, three, two, one, one, one, one)
        + (two,) * 7
        + (ffn, ffn),
        out_specs=(two, two, one, one, one, one) + (two,) * 7 + (ffn, ffn),
        check_vma=False,
    )
```
